32 devices in a mesh: dp: 2 (over x), seq: 4 (over y, core), tensor: 4 (over z).
Axes of the slice: x: 2, y: 2, z: 4, core: 2. Of those that a mesh axis runs over, the one named last changes fastest.
Arguments:
- inputs: bfloat16 [4, 2048, 1024], P('dp', ('seq', 'tensor')), may hold values from -6 to 6
- seg_starts: int32 [4, 4], P('dp', 'seq'), may hold values from 0 to 256, as said below
- lengths: int32 [4], P('dp'), may hold values from 512 to 2048, as said below
- init_state: float32 [512, 1024], P('tensor'), may hold values from -6 to 6
- attn_gain: float32 [1024], replicated, may hold values from 0.5 to 1.5
- state_gain: float32 [1024], replicated, may hold values from 0.5 to 1.5
- mlp_gain: float32 [1024], replicated, may hold values from 0.5 to 1.5
- w_query: bfloat16 [1024, 1024], P(None, 'tensor'), may hold values from -0.1875 to 0.1875
- w_key: bfloat16 [1024, 1024], P(None, 'tensor'), may hold values from -0.1875 to 0.1875
- w_value: bfloat16 [1024, 1024], P(None, 'tensor'), may hold values from -0.1875 to 0.1875
- w_out: bfloat16 [1024, 1024], P('tensor'), may hold values from -4 to 4
- w_squery: bfloat16 [1024, 1024], P(None, 'tensor'), may hold values from -0.1875 to 0.1875
- w_sout: bfloat16 [1024, 1024], P('tensor'), may hold values from -4 to 4
- w_up: bfloat16 [1024, 4096], P(None, 'tensor'), may hold values from -0.1875 to 0.1875
- w_down: bfloat16 [4096, 1024], P('tensor'), may hold values from -0.125 to 0.125
- rel_bias: float32 [32, 8], P(None, 'tensor'), may hold values from -4 to 4
- gate_bias: float32 [1024], replicated, may hold values from -3 to 3
- out_cot: bfloat16 [4, 2048, 1024], P('dp', ('seq', 'tensor')), may hold values from -6 to 6
- state_cot: bfloat16 [4, 4, 512, 1024], P('dp', 'seq', 'tensor'), may hold values from -6 to 6
Outputs:
- tokens_out: bfloat16 [4, 2048, 1024], P('dp', ('seq', 'tensor'))
- states_out: float32 [4, 4, 512, 1024], P('dp', 'seq', 'tensor')
- inputs_grad: float32 [4, 2048, 1024], P('dp', ('seq', 'tensor'))
- state_grad: float32 [512, 1024], P('tensor')
- attn_gain_grad: float32 [1024], replicated
- state_gain_grad: float32 [1024], replicated
- mlp_gain_grad: float32 [1024], replicated
- query_grad: float32 [1024, 1024], P(None, 'tensor')
- key_grad: float32 [1024, 1024], P(None, 'tensor')
- value_grad: float32 [1024, 1024], P(None, 'tensor')
- out_grad: float32 [1024, 1024], P('tensor')
- squery_grad: float32 [1024, 1024], P(None, 'tensor')
- sout_grad: float32 [1024, 1024], P('tensor')
- up_grad: float32 [1024, 4096], P(None, 'tensor')
- down_grad: float32 [4096, 1024], P('tensor')
- bias_grad: float32 [32, 8], P(None, 'tensor')
- gate_grad: float32 [1024], replicated
The draws below stay inside these ranges and needn't reach their ends.
Inputs may be any that keep to these rules, and one draw needn't show every extreme that they name: `seg_starts`: each block's bidirectional segment starts at this offset inside the block and covers 256 tokens. `lengths`: tokens at or past a sequence's length are padding that no key may show.
All inputs are finite; a program needn't handle non-finite values.
Results may differ from the reference program's by a relative error of at most 0.025.
Values may be sent and summed in bfloat16 or wider, within the bound.
A program may use at most 192 MiB of HBM per device.

```python
import jax
import jax.numpy as jnp
from jax import lax

D = 1024
HEADS = 8
HEAD_DIM = 128
FF = 4096
STATES = 512
BLOCK = 512
SEG = 256
BUCKETS = 32
SEQS = 4
BLOCKS = 4
LENGTH = 2048


def draw_seg_starts(key, part):
    starts_flat = jax.random.randint(key, (SEQS * BLOCKS,), 0, BLOCK - SEG + 1)
    shuffled = jax.random.permutation(jax.random.fold_in(key, 11), SEQS * BLOCKS)
    starts_flat = starts_flat.at[shuffled[0]].set(0).at[shuffled[1]].set(BLOCK - SEG)
    return starts_flat.reshape(SEQS, BLOCKS).astype(jnp.int32)


def draw_lengths(key, part):
    length_list = jax.random.randint(key, (SEQS,), BLOCK, LENGTH + 1)
    shuffled = jax.random.permutation(jax.random.fold_in(key, 13), SEQS)
    length_list = length_list.at[shuffled[0]].set(LENGTH).at[shuffled[1]].set(BLOCK)
    return length_list.astype(jnp.int32)


def block_levels(key, shape, shards, low, high):
    def one(position, parts):
        steps = jax.random.uniform(jax.random.fold_in(jax.random.fold_in(key, 6), position), (parts,), jnp.float32, low / len(shards), high / len(shards))
        return jnp.repeat(jnp.exp(steps), shape[position] // parts).reshape((-1,) + (1,) * (len(shape) - position - 1))

    level = one(*shards[0])
    for cut in shards[1:]:
        level = level * one(*cut)
    return level


def normal_values(stream_key, extent, scale, limit, cuts=(), dtype=jnp.bfloat16):
    entries = jax.random.normal(stream_key, extent, jnp.float32) * scale
    if len(cuts) > 0:
        entries = block_levels(stream_key, extent, cuts, -0.22, 0.18) * entries
    return jnp.clip(entries, min=-limit, max=limit).astype(dtype)


def setup_inputs(seed: int = 0) -> dict:
    keys = jax.random.split(jax.random.key(seed), 20)
    return {
        "inputs": normal_values(keys[0], (SEQS, LENGTH, D), 1.0, 6.0, ((0, 2), (1, 16))),
        "seg_starts": draw_seg_starts(jax.random.fold_in(keys[19], 71), 0),
        "lengths": draw_lengths(jax.random.fold_in(keys[19], 71), 0),
        "init_state": normal_values(keys[3], (STATES, D), 1.0, 6.0, ((0, 4),), jnp.float32),
        "attn_gain": jnp.clip(1.0 + 0.1 * jax.random.normal(keys[4], (D,), jnp.float32), 0.5, 1.5),
        "state_gain": jnp.clip(1.0 + 0.1 * jax.random.normal(keys[5], (D,), jnp.float32), 0.5, 1.5),
        "mlp_gain": jnp.clip(1.0 + 0.1 * jax.random.normal(keys[6], (D,), jnp.float32), 0.5, 1.5),
        "w_query": normal_values(keys[7], (D, HEADS * HEAD_DIM), D ** -0.5, 0.1875, ((1, 4),)),
        "w_key": normal_values(keys[8], (D, HEADS * HEAD_DIM), D ** -0.5, 0.1875, ((1, 4),)),
        "w_value": normal_values(keys[9], (D, HEADS * HEAD_DIM), D ** -0.5, 0.1875, ((1, 4),)),
        "w_out": normal_values(keys[10], (HEADS * HEAD_DIM, D), (max(D // 512, 1)) ** -0.5, 4.0, ((0, 4),)),
        "w_squery": normal_values(keys[11], (D, HEADS * HEAD_DIM), D ** -0.5, 0.1875, ((1, 4),)),
        "w_sout": normal_values(keys[12], (HEADS * HEAD_DIM, D), (max(D // 512, 1)) ** -0.5, 4.0, ((0, 4),)),
        "w_up": normal_values(keys[13], (D, FF), D ** -0.5, 0.1875, ((1, 4),)),
        "w_down": normal_values(keys[14], (FF, D), (FF // 2) ** -0.5, 0.125, ((0, 4),)),
        "rel_bias": normal_values(keys[15], (BUCKETS, HEADS), 1.0, 4.0, ((1, 4),), jnp.float32),
        "gate_bias": jnp.clip(jax.random.uniform(keys[16], (D,), jnp.float32, -3.0, 3.0), -3.0, 3.0),
        "out_cot": normal_values(keys[17], (SEQS, LENGTH, D), 1.0, 6.0, ((0, 2), (1, 16))),
        "state_cot": normal_values(keys[18], (SEQS, BLOCKS, STATES, D), 1.0, 6.0, ((0, 2), (1, 4), (2, 4))),
    }


@jax.custom_vjp
def low(v):
    return lax.optimization_barrier(v.astype(jnp.bfloat16)).astype(jnp.float32)

@jax.custom_vjp
def low_back(v):
    return v

def low_keep(v):
    return (low(v), None)

def low_pass(kept, grad):
    return (grad,)

def back_keep(v):
    return (v, None)

def back_low(kept, grad):
    return (low(grad),)
low.defvjp(low_keep, low_pass)
low_back.defvjp(back_keep, back_low)
norm_eps = 1e-06
masked_score = -1e+30
bucket_edges = (12, 16, 23, 32, 46, 64, 91)

def bucket_of(relative):
    distance = jnp.abs(relative)
    far_bucket = 8 + sum(((distance >= boundary).astype(jnp.int32) for boundary in bucket_edges))
    near_far = jnp.where(distance < 8, distance, far_bucket)
    return (near_far + 16 * (relative > 0).astype(jnp.int32)).astype(jnp.int32)

def token_mask(seg_start, seq_length, block_index):
    positions = jnp.arange(BLOCK).astype(jnp.int32)
    offset = block_index * BLOCK
    prev_valid = (block_index > 0) & (offset - BLOCK + positions < seq_length)
    cur_valid = offset + positions < seq_length
    inside = (positions >= seg_start) & (positions < seg_start + SEG)
    prev_mask = (positions[None, :] > positions[:, None]) & prev_valid[None, :]
    cur_mask = ((positions[None, :] <= positions[:, None]) | inside[None, :] & inside[:, None]) & cur_valid[None, :]
    state_mask = jnp.ones((BLOCK, STATES), jnp.bool_)
    return jnp.concatenate([prev_mask, cur_mask, state_mask], axis=1)

def layer_norm(values, gain_vec):
    centered = values - lax.optimization_barrier(jnp.mean(values, axis=-1, keepdims=True))
    spread = lax.optimization_barrier(jnp.mean(centered * centered, axis=-1, keepdims=True))
    return centered * lax.rsqrt(spread + norm_eps) * gain_vec

def dot_high(left, right):
    return jnp.dot(left, right, precision=lax.Precision.HIGHEST, preferred_element_type=jnp.float32)

def attend_high(query_rows, key_all, value_all, bias_all, allowed):
    query_count = query_rows.shape[0]
    key_count = key_all.shape[0]
    query_heads = query_rows.reshape(query_count, HEADS, HEAD_DIM)
    key_heads = key_all.reshape(key_count, HEADS, HEAD_DIM)
    value_heads = value_all.reshape(key_count, HEADS, HEAD_DIM)
    scores = jnp.einsum('qhd,khd->hqk', query_heads, key_heads, precision=lax.Precision.HIGHEST, preferred_element_type=jnp.float32) * HEAD_DIM ** (-0.5) + bias_all
    scores = low_back(jnp.where(allowed[None], scores, masked_score))
    row_max = lax.optimization_barrier(jnp.max(scores, axis=-1, keepdims=True))
    exp_scores = jnp.exp(scores - row_max)
    weight_all = low(exp_scores / lax.optimization_barrier(jnp.sum(exp_scores, axis=-1, keepdims=True)))
    mixed_out = jnp.einsum('hqk,khd->qhd', weight_all, value_heads, precision=lax.Precision.HIGHEST, preferred_element_type=jnp.float32)
    return low(low_back(mixed_out.reshape(query_count, HEADS * HEAD_DIM)))

def run_sequence(weights, init_state, seq_inputs, seq_segs, seq_length):
    attn_gain, state_gain, mlp_gain, w_query, w_key, w_value, w_out, w_squery, w_sout, w_up, w_down, rel_bias, gate_bias = weights
    positions = jnp.arange(BLOCK).astype(jnp.int32)
    rel_table = bucket_of((jnp.arange(2 * BLOCK).astype(jnp.int32) - BLOCK)[None, :] - positions[:, None])
    token_bias = jnp.concatenate([jnp.transpose(rel_bias[rel_table], (2, 0, 1)), jnp.zeros((HEADS, BLOCK, STATES), jnp.float32)], axis=2)
    gate_value = jax.nn.sigmoid(gate_bias)

    def block_step(carry, block_in):
        state_now, key_prev, value_prev = carry
        block_rows, seg_start, block_index = block_in
        tokens_low = low(layer_norm(block_rows, attn_gain))
        query_tok = low(low_back(dot_high(tokens_low, w_query)))
        key_tok = low(low_back(dot_high(tokens_low, w_key)))
        value_tok = low(low_back(dot_high(tokens_low, w_value)))
        state_low = low(layer_norm(state_now, state_gain))
        query_st = low(low_back(dot_high(state_low, w_squery)))
        key_st = low(low_back(dot_high(state_low, w_key)))
        value_st = low(low_back(dot_high(state_low, w_value)))
        allowed_tok = token_mask(seg_start, seq_length, block_index)
        mixed_tok = attend_high(query_tok, jnp.concatenate([key_prev, key_tok, key_st], axis=0), jnp.concatenate([value_prev, value_tok, value_st], axis=0), token_bias, allowed_tok)
        hidden_in = block_rows + low_back(dot_high(mixed_tok, w_out))
        mid_low = low(layer_norm(hidden_in, mlp_gain))
        pre_act = low_back(dot_high(mid_low, w_up))
        hidden_low = low(jax.nn.gelu(pre_act))
        block_out = hidden_in + low_back(dot_high(hidden_low, w_down))
        valid_keys = block_index * BLOCK + positions < seq_length
        allowed_st = jnp.concatenate([jnp.broadcast_to(valid_keys[None, :], (STATES, BLOCK)), jnp.ones((STATES, STATES), jnp.bool_)], axis=1)
        mixed_st = attend_high(query_st, jnp.concatenate([key_tok, key_st], axis=0), jnp.concatenate([value_tok, value_st], axis=0), 0.0, allowed_st)
        update = low_back(dot_high(mixed_st, w_sout))
        state_next = gate_value * state_now + (1.0 - gate_value) * update
        return ((state_next, key_tok, value_tok), (block_out, state_next))
    zero_keys = jnp.zeros((BLOCK, HEADS * HEAD_DIM), jnp.float32)
    block_list = (seq_inputs.reshape(BLOCKS, BLOCK, D), seq_segs, jnp.arange(BLOCKS).astype(jnp.int32))
    _, (block_outs, state_list) = lax.scan(jax.checkpoint(block_step), (init_state, zero_keys, zero_keys), block_list)
    return (block_outs.reshape(LENGTH, D), state_list)

def reference(inputs, seg_starts, lengths, init_state, attn_gain, state_gain, mlp_gain, w_query, w_key, w_value, w_out, w_squery, w_sout, w_up, w_down, rel_bias, gate_bias, out_cot, state_cot):
    weights = (attn_gain, state_gain, mlp_gain, w_query.astype(jnp.float32), w_key.astype(jnp.float32), w_value.astype(jnp.float32), w_out.astype(jnp.float32), w_squery.astype(jnp.float32), w_sout.astype(jnp.float32), w_up.astype(jnp.float32), w_down.astype(jnp.float32), rel_bias, gate_bias)

    def forward(all_inputs, start_state, weights_in):

        def per_sequence(carry, seq_in):
            return (carry, run_sequence(weights_in, start_state, seq_in[0], seq_in[1], seq_in[2]))
        _, (token_rows, state_rows) = lax.scan(per_sequence, None, (all_inputs, seg_starts, lengths))
        return (token_rows, state_rows)
    (token_rows, state_rows), pullback = jax.vjp(forward, inputs.astype(jnp.float32), init_state, weights)
    inputs_grad, state_grad, weight_grads = pullback((out_cot.astype(jnp.float32), state_cot.astype(jnp.float32)))
    return (token_rows.astype(jnp.bfloat16), state_rows, inputs_grad, state_grad, weight_grads[0], weight_grads[1], weight_grads[2], weight_grads[3], weight_grads[4], weight_grads[5], weight_grads[6], weight_grads[7], weight_grads[8], weight_grads[9], weight_grads[10], weight_grads[11], weight_grads[12])
```

```python
import jax
import jax.numpy as jnp
from jax import lax
from jax.experimental import pallas as pl
from jax.experimental.pallas import tpu as pltpu
from jax.sharding import PartitionSpec as P

D = 1024
HEAD_DIM = 128
STATES = 512
BLOCK = 512
SEG = 256
BUCKETS = 32


norm_eps = 1e-06
masked_score = -1e30
bucket_edges = (12, 16, 23, 32, 46, 64, 91)


def passed_along(value, axis, steps):
    count = lax.axis_size(axis)
    leading, last = (max(0, -steps), min(count, count - steps))
    return lax.ppermute(value, axis, [(source, source + steps) for source in range(leading, last)])


def bucket_of(relative):
    distance = jnp.abs(relative)
    far_bucket = 8 + sum(((distance >= boundary).astype(jnp.int32) for boundary in bucket_edges))
    near_far = jnp.where(distance < 8, distance, far_bucket)
    return near_far + 16 * (relative > 0).astype(jnp.int32)


def token_mask(seg_start, seq_length, block_index):
    positions = jnp.arange(BLOCK)
    offset = block_index * BLOCK
    prev_valid = (block_index > 0) & (offset - BLOCK + positions < seq_length)
    cur_valid = offset + positions < seq_length
    inside = (positions >= seg_start) & (positions < seg_start + SEG)
    prev_mask = (positions[None, :] > positions[:, None]) & prev_valid[None, :]
    cur_mask = (
        (positions[None, :] <= positions[:, None]) | inside[None, :] & inside[:, None]
    ) & cur_valid[None, :]
    state_mask = jnp.ones((BLOCK, STATES), jnp.bool_)
    return jnp.concatenate([prev_mask, cur_mask, state_mask], axis=1)


def state_mask_of(valid_blk):
    batch_count = valid_blk.shape[0]
    block_part = jnp.broadcast_to(valid_blk[:, None, :], (batch_count, STATES, BLOCK))
    return jnp.concatenate([block_part, jnp.ones((batch_count, STATES, STATES), jnp.bool_)], axis=2)


def layer_norm(values, gain_vec):
    centered = values - jnp.mean(values, axis=-1, keepdims=True)
    spread = jnp.mean(centered * centered, axis=-1, keepdims=True)
    return centered * lax.rsqrt(spread + norm_eps) * gain_vec


def norm_back(values, gain_vec, grad_out):
    _, pullback = jax.vjp(layer_norm, values, gain_vec)
    return pullback(grad_out)


def gelu_back(pre_act, grad_out):
    _, pullback = jax.vjp(jax.nn.gelu, pre_act)
    return pullback(grad_out)[0]


def to_low(array_in):
    return array_in.astype(jnp.bfloat16)


def matmul(left, right):
    return jnp.einsum("...k,kn->...n", left, right, preferred_element_type=jnp.float32)


def matmul_t(left, right):
    return jnp.einsum("...n,kn->...k", left, right, preferred_element_type=jnp.float32)


def outer_sum(left, right):
    left_flat = left.reshape(-1, left.shape[-1])
    right_flat = right.reshape(-1, right.shape[-1])
    return lax.dot_general(
        left_flat, right_flat, (((0,), (0,)), ((), ())), preferred_element_type=jnp.float32
    )


def gather_rows(values):
    return lax.all_gather(values, "tensor", axis=1, tiled=True)


def sum_rows(terms):
    return lax.psum_scatter(
        terms.astype(jnp.bfloat16), "tensor", scatter_dimension=1, tiled=True
    ).astype(jnp.float32)


def pass_state(rows_now):
    return passed_along(rows_now.astype(jnp.bfloat16), "seq", 1).astype(rows_now.dtype)


def pass_back(grad_now):
    return passed_along(grad_now.astype(jnp.bfloat16), "seq", -1).astype(grad_now.dtype)


def split_heads(rows_in):
    return rows_in.reshape(rows_in.shape[0], rows_in.shape[1] // HEAD_DIM, HEAD_DIM)


def score_block(query_rows, key_all, bias_all, allowed):
    scores = (
        jnp.einsum(
            "qhd,khd->hqk",
            split_heads(query_rows),
            split_heads(key_all),
            preferred_element_type=jnp.float32,
        )
        * HEAD_DIM ** (-0.5)
        + bias_all
    )
    return jnp.where(allowed[None], scores, masked_score)


def attend_forward(query_rows, key_all, value_all, bias_all, allowed):
    scores = score_block(query_rows, key_all, bias_all, allowed)
    row_max = jnp.max(scores, axis=-1, keepdims=True)
    exp_scores = jnp.exp(scores - row_max)
    row_total = jnp.sum(exp_scores, axis=-1, keepdims=True)
    weight_all = to_low(exp_scores / row_total)
    mixed_out = jnp.einsum(
        "hqk,khd->qhd", weight_all, split_heads(value_all), preferred_element_type=jnp.float32
    )
    return (
        to_low(mixed_out.reshape(query_rows.shape[0], -1)),
        (row_max + jnp.log(row_total))[..., 0],
    )


def attend_back(query_rows, key_all, value_all, bias_all, allowed, log_total, grad_mixed):
    scores = score_block(query_rows, key_all, bias_all, allowed)
    weight_all = jnp.where(allowed[None], jnp.exp(scores - log_total[..., None]), 0.0)
    grad_heads = split_heads(grad_mixed)
    grad_weight = jnp.einsum(
        "qhd,khd->hqk", grad_heads, split_heads(value_all), preferred_element_type=jnp.float32
    )
    row_inner = jnp.sum(weight_all * grad_weight, axis=-1, keepdims=True)
    grad_scores = to_low(weight_all * (grad_weight - row_inner))
    grad_query = jnp.einsum(
        "hqk,khd->qhd", grad_scores, split_heads(key_all), preferred_element_type=jnp.float32
    ) * HEAD_DIM ** (-0.5)
    grad_keys = jnp.einsum(
        "hqk,qhd->khd", grad_scores, split_heads(query_rows), preferred_element_type=jnp.float32
    ) * HEAD_DIM ** (-0.5)
    grad_values = jnp.einsum(
        "hqk,qhd->khd", to_low(weight_all), grad_heads, preferred_element_type=jnp.float32
    )
    return (
        grad_query.reshape(query_rows.shape[0], -1),
        grad_keys.reshape(key_all.shape[0], -1),
        grad_values.reshape(key_all.shape[0], -1),
        grad_scores,
    )


def bias_lookup(rel_bias, rel_table):
    table_heads = jnp.zeros((rel_bias.shape[1],) + rel_table.shape, jnp.float32)
    for bucket_id in range(BUCKETS):
        table_heads = table_heads + jnp.where(
            rel_table[None] == bucket_id, rel_bias[bucket_id][:, None, None], 0.0
        )
    return table_heads


def bias_sums(score_grad, rel_table):
    grad_wide = score_grad.astype(jnp.float32)
    columns = []
    for bucket_id in range(BUCKETS):
        columns.append(
            jnp.sum(jnp.where(rel_table[None, None] == bucket_id, grad_wide, 0.0), axis=(0, 2, 3))
        )
    return jnp.stack(columns, axis=0)


def body(
    inputs,
    seg_starts,
    lengths,
    init_state,
    attn_gain,
    state_gain,
    mlp_gain,
    w_query,
    w_key,
    w_value,
    w_out,
    w_squery,
    w_sout,
    w_up,
    w_down,
    rel_bias,
    gate_bias,
    out_cot,
    state_cot,
):
    seq_count = inputs.shape[0]
    chain_length = lax.axis_size("seq")
    block_index = lax.axis_index("seq")
    is_first = block_index == 0
    width_local = w_query.shape[1]
    head_count = width_local // HEAD_DIM
    gate_value = jax.nn.sigmoid(gate_bias)
    positions = jnp.arange(BLOCK)
    inputs_wide = inputs.astype(jnp.float32)
    tokens_low = gather_rows(to_low(layer_norm(inputs_wide, attn_gain)))
    query_tok = to_low(matmul(tokens_low, w_query))
    key_tok = to_low(matmul(tokens_low, w_key))
    value_tok = to_low(matmul(tokens_low, w_value))
    key_prev, value_prev = passed_along((key_tok, value_tok), "seq", 1)
    valid_keys = (block_index * BLOCK + positions)[None, :] < lengths[:, None]
    batched_attend = jax.vmap(attend_forward, in_axes=(0, 0, 0, None, 0))
    batched_back = jax.vmap(attend_back, in_axes=(0, 0, 0, None, 0, 0, 0))

    def state_forward(state_rows, key_blk, value_blk, valid_blk):
        state_low = lax.all_gather(
            to_low(layer_norm(state_rows, state_gain)), "tensor", axis=1, tiled=True
        )
        query_st = to_low(matmul(state_low, w_squery))
        key_st = to_low(matmul(state_low, w_key))
        value_st = to_low(matmul(state_low, w_value))
        key_all = jnp.concatenate([key_blk, key_st], axis=1)
        value_all = jnp.concatenate([value_blk, value_st], axis=1)
        mixed_st, lse_st = batched_attend(
            query_st, key_all, value_all, 0.0, state_mask_of(valid_blk)
        )
        update = lax.psum_scatter(
            matmul(mixed_st, w_sout).astype(jnp.bfloat16), "tensor", scatter_dimension=1, tiled=True
        ).astype(jnp.float32)
        state_next = gate_value * state_rows + (1.0 - gate_value) * update
        return (state_next, (state_low, query_st, key_st, value_st, mixed_st, lse_st, update))

    def state_backward(
        grad_out, state_rows, kept_one, key_blk, value_blk, valid_blk, extra_key, extra_value
    ):
        state_low, query_st, key_st, value_st, mixed_st, lse_st, update = kept_one
        gate_part = (
            jnp.sum(grad_out * (state_rows - update), axis=(0, 1)) * gate_value * (1.0 - gate_value)
        )
        grad_update = lax.all_gather(
            to_low((1.0 - gate_value) * grad_out), "tensor", axis=1, tiled=True
        )
        grad_mixed_st = to_low(matmul_t(grad_update, w_sout))
        sout_part = outer_sum(mixed_st, grad_update)
        key_all = jnp.concatenate([key_blk, key_st], axis=1)
        value_all = jnp.concatenate([value_blk, value_st], axis=1)
        grad_query_st, grad_keys_st, grad_values_st, _ = batched_back(
            query_st, key_all, value_all, 0.0, state_mask_of(valid_blk), lse_st, grad_mixed_st
        )
        query_low = to_low(grad_query_st)
        key_low = to_low(grad_keys_st[:, BLOCK:] + extra_key)
        value_low = to_low(grad_values_st[:, BLOCK:] + extra_value)
        squery_part = outer_sum(state_low, query_low)
        key_part = outer_sum(state_low, key_low)
        value_part = outer_sum(state_low, value_low)
        terms = (
            matmul_t(query_low, w_squery) + matmul_t(key_low, w_key) + matmul_t(value_low, w_value)
        )
        grad_normed = lax.psum_scatter(
            terms.astype(jnp.bfloat16), "tensor", scatter_dimension=1, tiled=True
        ).astype(jnp.float32)
        grad_rows_norm, gain_part = norm_back(state_rows, state_gain, grad_normed)
        grad_in = gate_value * grad_out + grad_rows_norm
        block_grads = (grad_keys_st[:, :BLOCK], grad_values_st[:, :BLOCK])
        return (
            grad_in,
            block_grads,
            (squery_part, key_part, value_part, sout_part, gain_part, gate_part),
        )

    zeros_rows = jnp.zeros((seq_count,) + init_state.shape, jnp.float32)
    narrow_zero = jnp.zeros((seq_count, STATES, width_local), jnp.bfloat16)
    stored_start = (
        zeros_rows,
        zeros_rows,
        jnp.zeros((seq_count, STATES, D), jnp.bfloat16),
        narrow_zero,
        narrow_zero,
        narrow_zero,
        narrow_zero,
        jnp.zeros((seq_count, head_count, STATES), jnp.float32),
        zeros_rows,
    )

    def forward_turn(turn_index, carry):
        incoming, stored_now = carry
        order_index = turn_index - block_index
        is_live = (order_index >= 0) & (order_index < seq_count)
        picked = jnp.clip(order_index, 0, seq_count - 1)
        rows_now = jnp.where(is_first, init_state[None], incoming)
        key_one = lax.dynamic_slice_in_dim(key_tok, picked, 1, 0)
        value_one = lax.dynamic_slice_in_dim(value_tok, picked, 1, 0)
        valid_one = lax.dynamic_slice_in_dim(valid_keys, picked, 1, 0)
        rows_next, kept_one = state_forward(rows_now, key_one, value_one, valid_one)
        fresh = (rows_now, rows_next) + kept_one
        stored_now = tuple(
            (
                jnp.where(
                    is_live,
                    lax.dynamic_update_slice_in_dim(whole_array, fresh_part, picked, 0),
                    whole_array,
                )
                for whole_array, fresh_part in zip(stored_now, fresh)
            )
        )
        return (pass_state(rows_next), stored_now)

    incoming_start = jnp.zeros((1,) + init_state.shape, jnp.float32)
    _, stored_all = lax.fori_loop(
        0, chain_length + seq_count - 1, forward_turn, (incoming_start, stored_start)
    )
    state_in = stored_all[0]
    state_out = stored_all[1]
    kept = stored_all[2:]
    key_all_tok = jnp.concatenate([key_prev, key_tok, kept[2]], axis=1)
    value_all_tok = jnp.concatenate([value_prev, value_tok, kept[3]], axis=1)
    allowed_tok = jax.vmap(token_mask, in_axes=(0, 0, None))(seg_starts[:, 0], lengths, block_index)
    rel_table = bucket_of((jnp.arange(2 * BLOCK) - BLOCK)[None, :] - positions[:, None])
    full_bias = jnp.concatenate(
        [bias_lookup(rel_bias, rel_table), jnp.zeros((head_count, BLOCK, STATES), jnp.float32)],
        axis=2,
    )
    mixed_tok, lse_tok = batched_attend(
        query_tok, key_all_tok, value_all_tok, full_bias, allowed_tok
    )
    hidden_in = inputs_wide + sum_rows(matmul(mixed_tok, w_out))
    mid_low = gather_rows(to_low(layer_norm(hidden_in, mlp_gain)))
    pre_act = matmul(mid_low, w_up)
    hidden_low = to_low(jax.nn.gelu(pre_act))
    mlp_rows = sum_rows(matmul(hidden_low, w_down))
    tokens_out = (hidden_in + mlp_rows).astype(jnp.bfloat16)
    cot_wide = out_cot.astype(jnp.float32)
    cot_used = gather_rows(out_cot)
    grad_hidden_act = matmul_t(cot_used, w_down)
    down_grad = outer_sum(hidden_low, cot_used)
    grad_pre = to_low(gelu_back(pre_act, grad_hidden_act))
    up_grad = outer_sum(mid_low, grad_pre)
    grad_normed_mid = sum_rows(matmul_t(grad_pre, w_up))
    grad_mid_in, mlp_gain_grad = norm_back(hidden_in, mlp_gain, grad_normed_mid)
    grad_hidden = cot_wide + grad_mid_in
    grad_attn_low = gather_rows(to_low(grad_hidden))
    grad_mixed = to_low(matmul_t(grad_attn_low, w_out))
    out_grad = outer_sum(mixed_tok, grad_attn_low)
    grad_query_tok, grad_keys_tok, grad_values_tok, grad_scores = batched_back(
        query_tok, key_all_tok, value_all_tok, full_bias, allowed_tok, lse_tok, grad_mixed
    )
    bias_grad = bias_sums(grad_scores[..., : 2 * BLOCK], rel_table)
    grad_key_next, grad_value_next = (
        passed_along(grad_keys_tok[:, :BLOCK].astype(jnp.bfloat16), "seq", -1).astype(jnp.float32),
        passed_along(grad_values_tok[:, :BLOCK].astype(jnp.bfloat16), "seq", -1).astype(
            jnp.float32
        ),
    )
    grad_key_own = grad_keys_tok[:, BLOCK : 2 * BLOCK] + grad_key_next
    grad_value_own = grad_values_tok[:, BLOCK : 2 * BLOCK] + grad_value_next
    grad_key_st_tok = grad_keys_tok[:, 2 * BLOCK :]
    grad_value_st_tok = grad_values_tok[:, 2 * BLOCK :]
    cot_rows = state_cot[:, 0].astype(jnp.float32)
    wide_zero = jnp.zeros((seq_count, BLOCK, width_local), jnp.float32)
    stored_back = (zeros_rows, wide_zero, wide_zero)
    totals_start = (
        jnp.zeros((D, width_local), jnp.float32),
        jnp.zeros((D, width_local), jnp.float32),
        jnp.zeros((D, width_local), jnp.float32),
        jnp.zeros((width_local, D), jnp.float32),
        jnp.zeros((D,), jnp.float32),
        jnp.zeros((D,), jnp.float32),
    )

    def backward_turn(turn_index, carry):
        incoming, stored_now, totals_now = carry
        order_index = turn_index - (chain_length - 1 - block_index)
        is_live = (order_index >= 0) & (order_index < seq_count)
        picked = jnp.clip(order_index, 0, seq_count - 1)

        def slice_one(whole_array):
            return lax.dynamic_slice_in_dim(whole_array, picked, 1, 0)

        grad_out = slice_one(cot_rows) + incoming
        kept_one = tuple((slice_one(kept_array) for kept_array in kept))
        grad_in, block_one, parts_one = state_backward(
            grad_out,
            slice_one(state_in),
            kept_one,
            slice_one(key_tok),
            slice_one(value_tok),
            slice_one(valid_keys),
            slice_one(grad_key_st_tok),
            slice_one(grad_value_st_tok),
        )
        fresh = (grad_in,) + block_one
        stored_now = tuple(
            (
                jnp.where(
                    is_live,
                    lax.dynamic_update_slice_in_dim(whole_array, fresh_part, picked, 0),
                    whole_array,
                )
                for whole_array, fresh_part in zip(stored_now, fresh)
            )
        )
        totals_now = tuple(
            (
                total_now + jnp.where(is_live, part_now, 0.0)
                for total_now, part_now in zip(totals_now, parts_one)
            )
        )
        return (pass_back(grad_in), stored_now, totals_now)

    incoming_start = jnp.zeros((1,) + init_state.shape, jnp.float32)
    _, stored_done, weight_parts = lax.fori_loop(
        0, chain_length + seq_count - 1, backward_turn, (incoming_start, stored_back, totals_start)
    )
    grad_in_all, grad_key_blk, grad_value_blk = stored_done
    query_low = to_low(grad_query_tok)
    key_low = to_low(grad_key_own + grad_key_blk)
    value_low = to_low(grad_value_own + grad_value_blk)
    query_grad = outer_sum(tokens_low, query_low)
    key_grad = outer_sum(tokens_low, key_low) + weight_parts[1]
    value_grad = outer_sum(tokens_low, value_low) + weight_parts[2]
    grad_tokens = sum_rows(
        matmul_t(query_low, w_query) + matmul_t(key_low, w_key) + matmul_t(value_low, w_value)
    )
    grad_in_norm, attn_gain_grad = norm_back(inputs_wide, attn_gain, grad_tokens)
    inputs_grad = grad_hidden + grad_in_norm
    state_part = jnp.where(is_first, jnp.sum(grad_in_all, axis=0), 0.0)
    gains = lax.psum(
        jnp.stack([attn_gain_grad, weight_parts[4], mlp_gain_grad, weight_parts[5]]), "tensor"
    )
    totals = (
        lax.psum(query_grad.astype(jnp.bfloat16), ("dp", "seq")).astype(jnp.float32),
        lax.psum(key_grad.astype(jnp.bfloat16), ("dp", "seq")).astype(jnp.float32),
        lax.psum(value_grad.astype(jnp.bfloat16), ("dp", "seq")).astype(jnp.float32),
        lax.psum(out_grad.astype(jnp.bfloat16), ("dp", "seq")).astype(jnp.float32),
        lax.psum(weight_parts[0].astype(jnp.bfloat16), ("dp", "seq")).astype(jnp.float32),
        lax.psum(weight_parts[3].astype(jnp.bfloat16), ("dp", "seq")).astype(jnp.float32),
        lax.psum(up_grad.astype(jnp.bfloat16), ("dp", "seq")).astype(jnp.float32),
        lax.psum(down_grad.astype(jnp.bfloat16), ("dp", "seq")).astype(jnp.float32),
        lax.psum(bias_grad.astype(jnp.bfloat16), ("dp", "seq")).astype(jnp.float32),
        lax.psum(state_part.astype(jnp.bfloat16), ("dp", "seq")).astype(jnp.float32),
        lax.psum(gains.astype(jnp.bfloat16), ("dp", "seq")).astype(jnp.float32),
    )
    gain_total = totals[10]
    return (
        tokens_out,
        state_out[:, None],
        inputs_grad,
        totals[9],
        gain_total[0],
        gain_total[1],
        gain_total[2],
        totals[0],
        totals[1],
        totals[2],
        totals[3],
        totals[4],
        totals[5],
        totals[6],
        totals[7],
        totals[8],
        gain_total[3],
    )


def chosen_body(mesh):
    if mesh.shape["seq"] == 4 and mesh.shape["tensor"] == 4:
        return line_body
    return body


MESH_ID = pl.DeviceIdType.MESH
ROWS = 128
CHUNKS = BLOCK // ROWS
LINE = 8
SCALE = HEAD_DIM ** (-0.5)
VMEM_LIMIT = 60 * 1024 * 1024


def dot_nn(left, right):
    return lax.dot_general(left, right, (((1,), (0,)), ((), ())), preferred_element_type=jnp.float32)


def dot_nt(left, right):
    return lax.dot_general(left, right, (((1,), (1,)), ((), ())), preferred_element_type=jnp.float32)


def dot_tn(left, right):
    return lax.dot_general(left, right, (((0,), (0,)), ((), ())), preferred_element_type=jnp.float32)


def line_place():
    place = lax.axis_index("seq")
    half = lax.rem(place, 2)
    rank = lax.axis_index("tensor")
    return place, half, rank


def span(index, size):
    return pl.ds(pl.multiple_of(index * size, size), size)


def norm_parts(rows):
    centered = rows - jnp.mean(rows, axis=-1, keepdims=True)
    spread = jnp.mean(centered * centered, axis=-1, keepdims=True)
    return centered, lax.rsqrt(spread + norm_eps)


def token_masks(scal, block_id, first_row):
    length = scal[0]
    start = scal[1 + block_id]
    row = lax.broadcasted_iota(jnp.int32, (ROWS, BLOCK), 0) + first_row
    col = lax.broadcasted_iota(jnp.int32, (ROWS, BLOCK), 1)
    prev_limit = jnp.where(block_id > 0, length - (block_id - 1) * BLOCK, 0)
    prev_ok = (col > row) & (col < prev_limit)
    row_in = (row >= start) & (row < start + SEG)
    col_in = (col >= start) & (col < start + SEG)
    cur_ok = ((col <= row) | (row_in & col_in)) & (col < length - block_id * BLOCK)
    return prev_ok, cur_ok


def state_block_mask(scal, block_id):
    col = lax.broadcasted_iota(jnp.int32, (ROWS, BLOCK), 1)
    return col < scal[0] - block_id * BLOCK


def softmax_of(score_parts):
    top = jnp.max(score_parts[0], axis=-1, keepdims=True)
    for part in score_parts[1:]:
        top = jnp.maximum(top, jnp.max(part, axis=-1, keepdims=True))
    raised = [jnp.exp(part - top) for part in score_parts]
    total = jnp.sum(raised[0], axis=-1, keepdims=True)
    for part in raised[1:]:
        total = total + jnp.sum(part, axis=-1, keepdims=True)
    inverse = 1.0 / total
    return [to_low(part * inverse) for part in raised], top + jnp.log(total)


def token_scores(scal, qkv, qkvst, bias, block_id, chunk):
    rows = span(chunk, ROWS)
    prev_id = jnp.maximum(block_id - 1, 0)
    query = qkv[block_id, rows, 0:128]
    prev_ok, cur_ok = token_masks(scal, block_id, chunk * ROWS)
    prev = dot_nt(query, qkv[prev_id, :, 128:256]) * SCALE + bias[rows, 0:BLOCK]
    cur = dot_nt(query, qkv[block_id, :, 128:256]) * SCALE + bias[rows, BLOCK : 2 * BLOCK]
    stt = dot_nt(query, qkvst[block_id, :, 128:256]) * SCALE
    prev = jnp.where(prev_ok, prev, masked_score)
    cur = jnp.where(cur_ok, cur, masked_score)
    return query, (prev, cur, stt)


def state_scores(scal, qkv, qkvst, block_id, chunk):
    query = qkvst[block_id, span(chunk, ROWS), 0:128]
    tok = dot_nt(query, qkv[block_id, :, 128:256]) * SCALE
    tok = jnp.where(state_block_mask(scal, block_id), tok, masked_score)
    stt = dot_nt(query, qkvst[block_id, :, 128:256]) * SCALE
    return query, (tok, stt)


def forward_kernel(
    scal, qkv, start, w_state, w_sout, vecs, bias,
    o_out, lse_out, state_rows, state_low, qkvst, lse_st, os_rows,
    held, os_all, send_sem, pass_sem, recv_sem,
):
    place, half, rank = line_place()
    partner = place + 1 - 2 * half
    head = 2 * rank + half
    peers = [lax.rem(rank + step, 4) for step in (1, 2, 3)]
    barrier = pltpu.get_barrier_semaphore()
    for peer in peers:
        pl.semaphore_signal(
            barrier, inc=1, device_id={"seq": place, "tensor": peer}, device_id_type=MESH_ID
        )
    pl.semaphore_signal(
        barrier, inc=1, device_id={"seq": partner, "tensor": rank}, device_id_type=MESH_ID
    )
    held[...] = start[...].astype(jnp.float32)
    gain = vecs[0:1, :]
    gate = vecs[1:2, :]
    pl.semaphore_wait(barrier, 4)

    def carry_copy(block_id, which, sem, seq_to, rank_to):
        part = os_all.at[block_id, :, span(which, 128)]
        return pltpu.make_async_remote_copy(
            src_ref=part,
            dst_ref=part,
            send_sem=sem,
            recv_sem=recv_sem.at[block_id, which],
            device_id={"seq": seq_to, "tensor": rank_to},
            device_id_type=MESH_ID,
        )

    def one_block(block_id, _):
        def project(chunk, _):
            rows = span(chunk, ROWS)
            centered, scale = norm_parts(held[rows, :])
            low = to_low(centered * scale * gain)
            state_low[block_id, rows, :] = low
            qkvst[block_id, rows, :] = to_low(dot_nn(low, w_state[...]))
            return 0

        lax.fori_loop(0, CHUNKS, project, 0)

        def attend_state(chunk, _):
            rows = span(chunk, ROWS)
            _, parts = state_scores(scal, qkv, qkvst, block_id, chunk)
            (w_tok, w_stt), total = softmax_of(parts)
            mixed = dot_nn(w_tok, qkv[block_id, :, 256:384]) + dot_nn(
                w_stt, qkvst[block_id, :, 256:384]
            )
            os_all[block_id, rows, span(head, 128)] = to_low(mixed)
            lse_st[block_id, rows, :] = total
            return 0

        lax.fori_loop(0, CHUNKS, attend_state, 0)
        for slot, peer in enumerate(peers):
            carry_copy(block_id, head, send_sem.at[block_id, slot], place, peer).start()
        carry_copy(block_id, head, send_sem.at[block_id, 3], partner, rank).start()

        def attend_token(chunk, _):
            rows = span(chunk, ROWS)
            _, parts = token_scores(scal, qkv, qkvst, bias, block_id, chunk)
            weights, total = softmax_of(parts)
            prev_id = jnp.maximum(block_id - 1, 0)
            mixed = (
                dot_nn(weights[0], qkv[prev_id, :, 256:384])
                + dot_nn(weights[1], qkv[block_id, :, 256:384])
                + dot_nn(weights[2], qkvst[block_id, :, 256:384])
            )
            o_out[block_id, rows, :] = to_low(mixed)
            lse_out[block_id, rows, :] = total
            return 0

        lax.fori_loop(0, CHUNKS, attend_token, 0)
        for slot, peer in enumerate(peers):
            other = 2 * peer + half
            carry_copy(block_id, other, send_sem.at[block_id, slot], place, peer).wait_recv()
            carry_copy(block_id, other, pass_sem.at[block_id, slot], partner, rank).start()
        for other_rank in range(4):
            carry_copy(
                block_id, 2 * other_rank + 1 - half, send_sem.at[block_id, 3], partner, rank
            ).wait_recv()

        def update(chunk, _):
            rows = span(chunk, ROWS)
            change = dot_nn(os_all[block_id, rows, :], w_sout[...])
            held[rows, :] = gate * held[rows, :] + (1.0 - gate) * change
            return 0

        lax.fori_loop(0, CHUNKS, update, 0)
        state_rows[block_id] = held[span(rank, 128), :]
        os_rows[block_id] = os_all[block_id, span(head, 64), :]
        return 0

    lax.fori_loop(0, 4, one_block, 0)

    def drain(block_id, _):
        for slot, peer in enumerate(peers):
            carry_copy(block_id, head, send_sem.at[block_id, slot], place, peer).wait_send()
            other = 2 * peer + half
            carry_copy(block_id, other, pass_sem.at[block_id, slot], partner, rank).wait_send()
        carry_copy(block_id, head, send_sem.at[block_id, 3], partner, rank).wait_send()
        return 0

    lax.fori_loop(0, 4, drain, 0)


def vmem_specs(count):
    return [pl.BlockSpec(memory_space=pltpu.VMEM)] * count


def forward_chain(scal, qkv, start, w_state, w_sout, vecs, bias):
    low, wide = jnp.bfloat16, jnp.float32
    shapes = (
        ((4, BLOCK, 128), low),
        ((4, BLOCK, 1), wide),
        ((4, 128, D), wide),
        ((4, STATES, D), low),
        ((4, STATES, 384), low),
        ((4, STATES, 1), wide),
        ((4, 64, D), low),
    )
    return pl.pallas_call(
        forward_kernel,
        out_shape=[jax.ShapeDtypeStruct(*one) for one in shapes],
        in_specs=[pl.BlockSpec(memory_space=pltpu.SMEM)] + vmem_specs(6),
        out_specs=vmem_specs(7),
        scratch_shapes=[
            pltpu.VMEM((STATES, D), wide),
            pltpu.VMEM((4, STATES, D), low),
            pltpu.SemaphoreType.DMA((4, 4)),
            pltpu.SemaphoreType.DMA((4, 3)),
            pltpu.SemaphoreType.DMA((4, 8)),
        ],
        compiler_params=pltpu.CompilerParams(
            collective_id=1, has_side_effects=True, vmem_limit_bytes=VMEM_LIMIT
        ),
        cost_estimate=pl.CostEstimate(flops=20000000000, bytes_accessed=20000000, transcendentals=0),
        name="forward_chain",
    )(scal, qkv, start, w_state, w_sout, vecs, bias)


def backward_kernel(
    scal, qkv, d_o, lse_tok, qkvst, lse_st, states, cots, w_back, w_sout, vecs, bias,
    d_qkv, d_qkvst, du_rows, d_start, sums, dz_sum,
    key_acc, value_acc, st_key, st_value, dos_rows, dos_got, d_got, grad_in,
    send_sem, recv_sem,
):
    place, half, rank = line_place()
    head = 2 * rank + half
    peers = []
    for step in range(1, LINE):
        other = lax.rem(head + step, LINE)
        peers.append((other, place - half + lax.rem(other, 2), other // 2))
    barrier = pltpu.get_barrier_semaphore()
    for _, seq_to, rank_to in peers:
        pl.semaphore_signal(
            barrier, inc=1, device_id={"seq": seq_to, "tensor": rank_to}, device_id_type=MESH_ID
        )
    gain = vecs[0:1, :]
    gate = vecs[1:2, :]
    key_acc[...] = jnp.zeros_like(key_acc)
    value_acc[...] = jnp.zeros_like(value_acc)
    dz_sum[...] = jnp.zeros_like(dz_sum)
    sums[...] = jnp.zeros_like(sums)
    grad_in[...] = jnp.zeros_like(grad_in)

    def back_parts(parts, total, grad, values):
        weights = [jnp.exp(part - total) for part in parts]
        d_weights = [dot_nt(grad, value) for value in values]
        inner = jnp.sum(weights[0] * d_weights[0], axis=-1, keepdims=True)
        for one, other in zip(weights[1:], d_weights[1:]):
            inner = inner + jnp.sum(one * other, axis=-1, keepdims=True)
        d_scores = [to_low(one * (other - inner)) for one, other in zip(weights, d_weights)]
        return [to_low(one) for one in weights], d_scores

    def token_back(block_id):
        prev_id = jnp.maximum(block_id - 1, 0)
        st_key[...] = jnp.zeros_like(st_key)
        st_value[...] = jnp.zeros_like(st_value)

        def one_chunk(chunk, _):
            rows = span(chunk, ROWS)
            query, parts = token_scores(scal, qkv, qkvst, bias, block_id, chunk)
            grad = d_o[block_id, rows, :]
            keys = (qkv[prev_id, :, 128:256], qkv[block_id, :, 128:256], qkvst[block_id, :, 128:256])
            values = (
                qkv[prev_id, :, 256:384], qkv[block_id, :, 256:384], qkvst[block_id, :, 256:384]
            )
            weights, d_scores = back_parts(parts, lse_tok[block_id, rows, :], grad, values)
            d_query = dot_nn(d_scores[0], keys[0])
            d_query = d_query + dot_nn(d_scores[1], keys[1]) + dot_nn(d_scores[2], keys[2])
            d_qkv[block_id, rows, 0:128] = to_low(d_query * SCALE)
            key_acc[prev_id] += dot_tn(d_scores[0], query) * SCALE
            value_acc[prev_id] += dot_tn(weights[0], grad)
            key_acc[block_id] += dot_tn(d_scores[1], query) * SCALE
            value_acc[block_id] += dot_tn(weights[1], grad)
            st_key[...] += dot_tn(d_scores[2], query) * SCALE
            st_value[...] += dot_tn(weights[2], grad)
            dz_sum[rows, 0:BLOCK] += d_scores[0].astype(jnp.float32)
            dz_sum[rows, BLOCK : 2 * BLOCK] += d_scores[1].astype(jnp.float32)
            return 0

        lax.fori_loop(0, CHUNKS, one_chunk, 0)

    token_back(3)
    pl.semaphore_wait(barrier, LINE - 1)

    def mixed_copy(block_id, slot, sender, other, seq_to, rank_to):
        return pltpu.make_async_remote_copy(
            src_ref=dos_rows.at[block_id, :, span(other, 128)],
            dst_ref=dos_got.at[block_id, span(sender, 64), :],
            send_sem=send_sem.at[0, block_id, slot],
            recv_sem=recv_sem.at[0, block_id, sender],
            device_id={"seq": seq_to, "tensor": rank_to},
            device_id_type=MESH_ID,
        )

    def grads_copy(block_id, slot, sender, other, seq_to, rank_to):
        return pltpu.make_async_remote_copy(
            src_ref=d_qkvst.at[block_id, span(other, 64), :],
            dst_ref=d_got.at[block_id, sender],
            send_sem=send_sem.at[1, block_id, slot],
            recv_sem=recv_sem.at[1, block_id, sender],
            device_id={"seq": seq_to, "tensor": rank_to},
            device_id_type=MESH_ID,
        )

    def one_block(turn, _):
        block_id = 3 - turn
        grad_out = grad_in[...] + cots[block_id].astype(jnp.float32)
        sums[0:1, :] += jnp.sum(
            grad_out * (states[block_id] - states[block_id + 1]), axis=0, keepdims=True
        ) * gate
        change = to_low((1.0 - gate) * grad_out)
        du_rows[block_id] = change
        dos_rows[block_id] = to_low(dot_nt(change, w_sout[...]))
        for slot, (other, seq_to, rank_to) in enumerate(peers):
            mixed_copy(block_id, slot, head, other, seq_to, rank_to).start()
        dos_got[block_id, span(head, 64), :] = dos_rows[block_id, :, span(head, 128)]
        for slot, (other, seq_to, rank_to) in enumerate(peers):
            mixed_copy(block_id, slot, other, other, seq_to, rank_to).wait_recv()

        def one_chunk(chunk, _):
            rows = span(chunk, ROWS)
            query, parts = state_scores(scal, qkv, qkvst, block_id, chunk)
            grad = dos_got[block_id, rows, :]
            keys = (qkv[block_id, :, 128:256], qkvst[block_id, :, 128:256])
            values = (qkv[block_id, :, 256:384], qkvst[block_id, :, 256:384])
            weights, d_scores = back_parts(parts, lse_st[block_id, rows, :], grad, values)
            d_query = dot_nn(d_scores[0], keys[0]) + dot_nn(d_scores[1], keys[1])
            d_qkvst[block_id, rows, 0:128] = to_low(d_query * SCALE)
            key_acc[block_id] += dot_tn(d_scores[0], query) * SCALE
            value_acc[block_id] += dot_tn(weights[0], grad)
            st_key[...] += dot_tn(d_scores[1], query) * SCALE
            st_value[...] += dot_tn(weights[1], grad)
            return 0

        lax.fori_loop(0, CHUNKS, one_chunk, 0)
        d_qkvst[block_id, :, 128:256] = to_low(st_key[...])
        d_qkvst[block_id, :, 256:384] = to_low(st_value[...])
        for slot, (other, seq_to, rank_to) in enumerate(peers):
            grads_copy(block_id, slot, head, other, seq_to, rank_to).start()
        d_got[block_id, head] = d_qkvst[block_id, span(head, 64), :]

        @pl.when(turn < 3)
        def _():
            token_back(block_id - 1)

        d_qkv[block_id, :, 128:256] = to_low(key_acc[block_id])
        d_qkv[block_id, :, 256:384] = to_low(value_acc[block_id])
        for slot, (other, seq_to, rank_to) in enumerate(peers):
            grads_copy(block_id, slot, other, other, seq_to, rank_to).wait_recv()
        d_low = dot_nn(d_got[block_id, 0], w_back[0])
        for other in range(1, LINE):
            d_low = d_low + dot_nn(d_got[block_id, other], w_back[other])
        centered, scale = norm_parts(states[block_id])
        normed = centered * scale
        sums[1:2, :] += jnp.sum(d_low * normed, axis=0, keepdims=True)
        lifted = d_low * gain
        grad_in[...] = gate * grad_out + scale * (
            lifted
            - jnp.mean(lifted, axis=-1, keepdims=True)
            - normed * jnp.mean(lifted * normed, axis=-1, keepdims=True)
        )
        return 0

    lax.fori_loop(0, 4, one_block, 0)
    d_start[...] = grad_in[...]

    def drain(block_id, _):
        for slot, (other, seq_to, rank_to) in enumerate(peers):
            mixed_copy(block_id, slot, head, other, seq_to, rank_to).wait_send()
            grads_copy(block_id, slot, head, other, seq_to, rank_to).wait_send()
        return 0

    lax.fori_loop(0, 4, drain, 0)


def backward_chain(scal, qkv, d_o, lse_tok, qkvst, lse_st, states, cots, w_back, w_sout, vecs, bias):
    low, wide = jnp.bfloat16, jnp.float32
    shapes = (
        ((4, BLOCK, 384), low),
        ((4, STATES, 384), low),
        ((4, 64, D), low),
        ((64, D), wide),
        ((8, D), wide),
        ((BLOCK, 2 * BLOCK), wide),
    )
    return pl.pallas_call(
        backward_kernel,
        out_shape=[jax.ShapeDtypeStruct(*one) for one in shapes],
        in_specs=[pl.BlockSpec(memory_space=pltpu.SMEM)] + vmem_specs(11),
        out_specs=vmem_specs(6),
        scratch_shapes=[
            pltpu.VMEM((4, BLOCK, 128), wide),
            pltpu.VMEM((4, BLOCK, 128), wide),
            pltpu.VMEM((STATES, 128), wide),
            pltpu.VMEM((STATES, 128), wide),
            pltpu.VMEM((4, 64, D), low),
            pltpu.VMEM((4, STATES, 128), low),
            pltpu.VMEM((4, LINE, 64, 384), low),
            pltpu.VMEM((64, D), wide),
            pltpu.SemaphoreType.DMA((2, 4, LINE - 1)),
            pltpu.SemaphoreType.DMA((2, 4, LINE)),
        ],
        compiler_params=pltpu.CompilerParams(
            collective_id=2, has_side_effects=True, vmem_limit_bytes=VMEM_LIMIT
        ),
        cost_estimate=pl.CostEstimate(flops=40000000000, bytes_accessed=40000000, transcendentals=0),
        name="backward_chain",
    )(scal, qkv, d_o, lse_tok, qkvst, lse_st, states, cots, w_back, w_sout, vecs, bias)


WIDE = 2048


def bias_kernel(line, table):
    first = line[...]
    row = lax.broadcasted_iota(jnp.int32, (8, WIDE), 0)
    for step in (1, 2, 4):
        first = jnp.where(row // step % 2 == 1, pltpu.roll(first, step, 1), first)

    def one(group, _):
        table[span(group, 8), :] = pltpu.roll(first, 8 * group, 1)[:, 0 : 2 * BLOCK]
        return 0

    lax.fori_loop(0, BLOCK // 8, one, 0)


def bias_table(line):
    return pl.pallas_call(
        bias_kernel,
        out_shape=jax.ShapeDtypeStruct((BLOCK, 2 * BLOCK), jnp.float32),
        in_specs=vmem_specs(1),
        out_specs=pl.BlockSpec(memory_space=pltpu.VMEM),
        compiler_params=pltpu.CompilerParams(vmem_limit_bytes=VMEM_LIMIT),
        name="bias_table",
    )(line)


def diagonal_kernel(table, out, acc):
    acc[...] = jnp.zeros_like(acc)

    def one(group, _):
        rows = table[span(group, 8), :]
        wide = jnp.concatenate([rows, jnp.zeros((8, WIDE - 2 * BLOCK), jnp.float32)], axis=1)
        acc[...] += pltpu.roll(wide, lax.rem(WIDE - 8 * group, WIDE), 1)
        return 0

    lax.fori_loop(0, BLOCK // 8, one, 0)
    total = acc[...]
    row = lax.broadcasted_iota(jnp.int32, (8, WIDE), 0)
    for step in (1, 2, 4):
        total = jnp.where(row // step % 2 == 1, pltpu.roll(total, WIDE - step, 1), total)
    out[...] = jnp.broadcast_to(jnp.sum(total, axis=0, keepdims=True), (8, WIDE))


def diagonal_sums(table):
    return pl.pallas_call(
        diagonal_kernel,
        out_shape=jax.ShapeDtypeStruct((8, WIDE), jnp.float32),
        in_specs=vmem_specs(1),
        out_specs=pl.BlockSpec(memory_space=pltpu.VMEM),
        scratch_shapes=[pltpu.VMEM((8, WIDE), jnp.float32)],
        compiler_params=pltpu.CompilerParams(vmem_limit_bytes=VMEM_LIMIT),
        name="diagonal_sums",
    )(table)


def own_half(part, half, axis):
    empty = jnp.zeros_like(part)
    return jnp.where(
        half == 0,
        jnp.concatenate([part, empty], axis=axis),
        jnp.concatenate([empty, part], axis=axis),
    )


def swap_seq(value):
    return lax.all_to_all(value, "seq", 0, 0, tiled=False)


def line_body(
    inputs,
    seg_starts,
    lengths,
    init_state,
    attn_gain,
    state_gain,
    mlp_gain,
    w_query,
    w_key,
    w_value,
    w_out,
    w_squery,
    w_sout,
    w_up,
    w_down,
    rel_bias,
    gate_bias,
    out_cot,
    state_cot,
):
    low, wide = jnp.bfloat16, jnp.float32
    place = lax.axis_index("seq")
    half = lax.rem(place, 2)
    mine = place // 2
    head_of = lambda weight: lax.dynamic_slice_in_dim(weight, half * 128, 128, 1)
    gate_value = jax.nn.sigmoid(gate_bias)
    vecs = jnp.stack([state_gain, gate_value] + [jnp.zeros_like(gate_value)] * 6)
    offsets = lax.rem(jnp.arange(WIDE) + WIDE - BLOCK, WIDE)
    offsets = jnp.arange(WIDE) - BLOCK
    offsets = jnp.where(offsets >= WIDE - 2 * BLOCK, offsets - WIDE, offsets)
    bucket_ids = bucket_of(offsets)
    one_hot = (bucket_ids[:, None] == jnp.arange(BUCKETS)[None, :]).astype(wide)
    my_bias = jnp.where(half == 0, rel_bias[:, 0], rel_bias[:, 1])
    bias_line = jnp.sum(one_hot * my_bias[None, :], axis=1)
    bias = bias_table(jnp.broadcast_to(bias_line[None, :], (8, WIDE)))
    segs = lax.all_gather(seg_starts[:, 0], "seq", axis=1, tiled=False)
    scal = jnp.concatenate(
        [lax.dynamic_slice_in_dim(lengths, mine, 1, 0), lax.dynamic_slice_in_dim(segs, mine, 1, 0)[0]]
    )

    inputs_wide = inputs.astype(wide)
    tokens_low = gather_rows(to_low(layer_norm(inputs_wide, attn_gain)))
    w_qkv = jnp.stack(
        [w.reshape(D, 2, 128) for w in (w_query, w_key, w_value)], axis=2
    ).reshape(D, 2, 384)
    qkv_native = to_low(
        jnp.einsum("sqd,dhe->shqe", tokens_low, w_qkv, preferred_element_type=wide)
    )
    qkv = swap_seq(qkv_native.reshape(4, BLOCK, 384))
    start_all = lax.all_gather(to_low(init_state), "tensor", axis=0, tiled=True)
    w_sout_all = lax.all_gather(w_sout, "tensor", axis=0, tiled=True)
    w_state = jnp.concatenate([head_of(w_squery), head_of(w_key), head_of(w_value)], axis=1)
    mixed, lse_tok, state_rows, state_low, qkvst, lse_st, os_rows = forward_chain(
        scal, qkv, start_all, w_state, w_sout_all, vecs, bias
    )
    other_block = lax.rem(place + 2, 4)
    sent = lax.dynamic_slice_in_dim(state_rows, other_block, 1, 0)[0].astype(low)
    came = lax.ppermute(sent, "seq", [(source, (source + 2) % 4) for source in range(4)])
    kept = lax.dynamic_slice_in_dim(state_rows, place, 1, 0)[0]
    state_out = jnp.where(
        mine == 0, jnp.stack([kept, came.astype(wide)]), jnp.stack([came.astype(wide), kept])
    )

    mixed_native = swap_seq(mixed).reshape(2, 2, BLOCK, 128)
    w_out_heads = w_out.reshape(2, 128, D)
    hidden_in = inputs_wide + sum_rows(
        jnp.einsum("shqe,hed->sqd", mixed_native, w_out_heads, preferred_element_type=wide)
    )
    mid_low = gather_rows(to_low(layer_norm(hidden_in, mlp_gain)))
    pre_act = matmul(mid_low, w_up)
    hidden_low = to_low(jax.nn.gelu(pre_act))
    mlp_rows = sum_rows(matmul(hidden_low, w_down))
    tokens_out = (hidden_in + mlp_rows).astype(low)
    cot_wide = out_cot.astype(wide)
    cot_used = gather_rows(out_cot)
    grad_hidden_act = matmul_t(cot_used, w_down)
    down_grad = outer_sum(hidden_low, cot_used)
    grad_pre = to_low(gelu_back(pre_act, grad_hidden_act))
    up_grad = outer_sum(mid_low, grad_pre)
    grad_normed_mid = sum_rows(matmul_t(grad_pre, w_up))
    grad_mid_in, mlp_gain_grad = norm_back(hidden_in, mlp_gain, grad_normed_mid)
    grad_hidden = cot_wide + grad_mid_in
    grad_attn_low = gather_rows(to_low(grad_hidden))
    d_mixed_native = to_low(
        jnp.einsum("sqd,hed->shqe", grad_attn_low, w_out_heads, preferred_element_type=wide)
    )
    out_grad = jnp.einsum(
        "shqe,sqd->hed", mixed_native, grad_attn_low, preferred_element_type=wide
    ).reshape(256, D)
    d_mixed = swap_seq(d_mixed_native.reshape(4, BLOCK, 128))

    cots = swap_seq(state_cot.reshape(4, 64, D))
    w_back_own = jnp.concatenate(
        [w.T.reshape(2, 128, D) for w in (w_squery, w_key, w_value)], axis=1
    )
    w_back = lax.all_gather(w_back_own, "tensor", axis=0, tiled=True)
    start_half = lax.dynamic_slice_in_dim(to_low(init_state).astype(wide), half * 64, 64, 0)
    states = jnp.concatenate(
        [start_half[None], lax.dynamic_slice_in_dim(state_rows, half * 64, 64, 1)], axis=0
    )
    d_qkv, d_qkvst, du_rows, d_start, sums, dz_sum = backward_chain(
        scal, qkv, d_mixed, lse_tok, qkvst, lse_st, states, cots, w_back, w_sout_all, vecs, bias
    )
    diag = diagonal_sums(dz_sum)[0]
    bias_grad = own_half(
        jnp.sum(one_hot * diag[:, None], axis=0)[:, None], half, 1
    )
    d_native = swap_seq(d_qkv).reshape(2, 2, BLOCK, 384)
    grad_tokens = sum_rows(
        jnp.einsum("shqe,dhe->sqd", d_native, w_qkv, preferred_element_type=wide)
    )
    grad_in_norm, attn_gain_grad = norm_back(inputs_wide, attn_gain, grad_tokens)
    inputs_grad = grad_hidden + grad_in_norm
    tok_grads = jnp.einsum("sqd,shqe->dhe", tokens_low, d_native, preferred_element_type=wide)
    st_grads = outer_sum(state_low, d_qkvst)
    query_grad = tok_grads[:, :, 0:128].reshape(D, 256)
    key_grad = tok_grads[:, :, 128:256].reshape(D, 256) + own_half(st_grads[:, 128:256], half, 1)
    value_grad = tok_grads[:, :, 256:384].reshape(D, 256) + own_half(st_grads[:, 256:384], half, 1)
    squery_grad = own_half(st_grads[:, 0:128], half, 1)
    sout_part = lax.psum_scatter(
        outer_sum(os_rows, du_rows).astype(low), "tensor", scatter_dimension=0, tiled=True
    )
    state_part = own_half(d_start, half, 0)
    gains = lax.psum(jnp.stack([attn_gain_grad, sums[1], mlp_gain_grad, sums[0]]), "tensor")

    def total(part):
        return lax.psum(part.astype(low), ("dp", "seq")).astype(wide)

    gain_total = total(gains)
    return (
        tokens_out,
        state_out[:, None],
        inputs_grad,
        total(state_part),
        gain_total[0],
        gain_total[1],
        gain_total[2],
        total(query_grad),
        total(key_grad),
        total(value_grad),
        total(out_grad),
        total(squery_grad),
        total(sout_part),
        total(up_grad),
        total(down_grad),
        total(bias_grad),
        gain_total[3],
    )


def solution(mesh):
    return jax.shard_map(
        chosen_body(mesh),
        mesh=mesh,
        in_specs=(
            P("dp", ("seq", "tensor"), None),
            P("dp", "seq"),
            P("dp"),
            P("tensor", None),
            P(),
            P(),
            P(),
            P(None, "tensor"),
            P(None, "tensor"),
            P(None, "tensor"),
            P("tensor", None),
            P(None, "tensor"),
            P("tensor", None),
            P(None, "tensor"),
            P("tensor", None),
            P(None, "tensor"),
            P(),
            P("dp", ("seq", "tensor"), None),
            P("dp", "seq", "tensor", None),
        ),
        out_specs=(
            P("dp", ("seq", "tensor"), None),
            P("dp", "seq", "tensor", None),
            P("dp", ("seq", "tensor"), None),
            P("tensor", None),
            P(),
            P(),
            P(),
            P(None, "tensor"),
            P(None, "tensor"),
            P(None, "tensor"),
            P("tensor", None),
            P(None, "tensor"),
            P("tensor", None),
            P(None, "tensor"),
            P("tensor", None),
            P(None, "tensor"),
            P(),
        ),
        check_vma=False,
    )
```

```python
import jax
import jax.numpy as jnp
from jax import lax
from jax.experimental import pallas as pl
from jax.experimental.pallas import tpu as pltpu
from jax.sharding import PartitionSpec as P

D = 1024
HEAD_DIM = 128
STATES = 512
BLOCK = 512
SEG = 256
BUCKETS = 32


norm_eps = 1e-06
masked_score = -1e30
bucket_edges = (12, 16, 23, 32, 46, 64, 91)


def passed_along(value, axis, steps):
    count = lax.axis_size(axis)
    leading, last = (max(0, -steps), min(count, count - steps))
    return lax.ppermute(value, axis, [(source, source + steps) for source in range(leading, last)])


def bucket_of(relative):
    distance = jnp.abs(relative)
    far_bucket = 8 + sum(((distance >= boundary).astype(jnp.int32) for boundary in bucket_edges))
    near_far = jnp.where(distance < 8, distance, far_bucket)
    return near_far + 16 * (relative > 0).astype(jnp.int32)


def token_mask(seg_start, seq_length, block_index):
    positions = jnp.arange(BLOCK)
    offset = block_index * BLOCK
    prev_valid = (block_index > 0) & (offset - BLOCK + positions < seq_length)
    cur_valid = offset + positions < seq_length
    inside = (positions >= seg_start) & (positions < seg_start + SEG)
    prev_mask = (positions[None, :] > positions[:, None]) & prev_valid[None, :]
    cur_mask = (
        (positions[None, :] <= positions[:, None]) | inside[None, :] & inside[:, None]
    ) & cur_valid[None, :]
    state_mask = jnp.ones((BLOCK, STATES), jnp.bool_)
    return jnp.concatenate([prev_mask, cur_mask, state_mask], axis=1)


def state_mask_of(valid_blk):
    batch_count = valid_blk.shape[0]
    block_part = jnp.broadcast_to(valid_blk[:, None, :], (batch_count, STATES, BLOCK))
    return jnp.concatenate([block_part, jnp.ones((batch_count, STATES, STATES), jnp.bool_)], axis=2)


def layer_norm(values, gain_vec):
    centered = values - jnp.mean(values, axis=-1, keepdims=True)
    spread = jnp.mean(centered * centered, axis=-1, keepdims=True)
    return centered * lax.rsqrt(spread + norm_eps) * gain_vec


def norm_back(values, gain_vec, grad_out):
    _, pullback = jax.vjp(layer_norm, values, gain_vec)
    return pullback(grad_out)


def gelu_back(pre_act, grad_out):
    _, pullback = jax.vjp(jax.nn.gelu, pre_act)
    return pullback(grad_out)[0]


def to_low(array_in):
    return array_in.astype(jnp.bfloat16)


def matmul(left, right):
    return jnp.einsum("...k,kn->...n", left, right, preferred_element_type=jnp.float32)


def matmul_t(left, right):
    return jnp.einsum("...n,kn->...k", left, right, preferred_element_type=jnp.float32)


def outer_sum(left, right):
    left_flat = left.reshape(-1, left.shape[-1])
    right_flat = right.reshape(-1, right.shape[-1])
    return lax.dot_general(
        left_flat, right_flat, (((0,), (0,)), ((), ())), preferred_element_type=jnp.float32
    )


def gather_rows(values):
    return lax.all_gather(values, "tensor", axis=1, tiled=True)


def sum_rows(terms):
    return lax.psum_scatter(
        terms.astype(jnp.bfloat16), "tensor", scatter_dimension=1, tiled=True
    ).astype(jnp.float32)


def pass_state(rows_now):
    return passed_along(rows_now.astype(jnp.bfloat16), "seq", 1).astype(rows_now.dtype)


def pass_back(grad_now):
    return passed_along(grad_now.astype(jnp.bfloat16), "seq", -1).astype(grad_now.dtype)


def split_heads(rows_in):
    return rows_in.reshape(rows_in.shape[0], rows_in.shape[1] // HEAD_DIM, HEAD_DIM)


def score_block(query_rows, key_all, bias_all, allowed):
    scores = (
        jnp.einsum(
            "qhd,khd->hqk",
            split_heads(query_rows),
            split_heads(key_all),
            preferred_element_type=jnp.float32,
        )
        * HEAD_DIM ** (-0.5)
        + bias_all
    )
    return jnp.where(allowed[None], scores, masked_score)


def attend_forward(query_rows, key_all, value_all, bias_all, allowed):
    scores = score_block(query_rows, key_all, bias_all, allowed)
    row_max = jnp.max(scores, axis=-1, keepdims=True)
    exp_scores = jnp.exp(scores - row_max)
    row_total = jnp.sum(exp_scores, axis=-1, keepdims=True)
    weight_all = to_low(exp_scores / row_total)
    mixed_out = jnp.einsum(
        "hqk,khd->qhd", weight_all, split_heads(value_all), preferred_element_type=jnp.float32
    )
    return (
        to_low(mixed_out.reshape(query_rows.shape[0], -1)),
        (row_max + jnp.log(row_total))[..., 0],
    )


def attend_back(query_rows, key_all, value_all, bias_all, allowed, log_total, grad_mixed):
    scores = score_block(query_rows, key_all, bias_all, allowed)
    weight_all = jnp.where(allowed[None], jnp.exp(scores - log_total[..., None]), 0.0)
    grad_heads = split_heads(grad_mixed)
    grad_weight = jnp.einsum(
        "qhd,khd->hqk", grad_heads, split_heads(value_all), preferred_element_type=jnp.float32
    )
    row_inner = jnp.sum(weight_all * grad_weight, axis=-1, keepdims=True)
    grad_scores = to_low(weight_all * (grad_weight - row_inner))
    grad_query = jnp.einsum(
        "hqk,khd->qhd", grad_scores, split_heads(key_all), preferred_element_type=jnp.float32
    ) * HEAD_DIM ** (-0.5)
    grad_keys = jnp.einsum(
        "hqk,qhd->khd", grad_scores, split_heads(query_rows), preferred_element_type=jnp.float32
    ) * HEAD_DIM ** (-0.5)
    grad_values = jnp.einsum(
        "hqk,qhd->khd", to_low(weight_all), grad_heads, preferred_element_type=jnp.float32
    )
    return (
        grad_query.reshape(query_rows.shape[0], -1),
        grad_keys.reshape(key_all.shape[0], -1),
        grad_values.reshape(key_all.shape[0], -1),
        grad_scores,
    )


def bias_lookup(rel_bias, rel_table):
    table_heads = jnp.zeros((rel_bias.shape[1],) + rel_table.shape, jnp.float32)
    for bucket_id in range(BUCKETS):
        table_heads = table_heads + jnp.where(
            rel_table[None] == bucket_id, rel_bias[bucket_id][:, None, None], 0.0
        )
    return table_heads


def bias_sums(score_grad, rel_table):
    grad_wide = score_grad.astype(jnp.float32)
    columns = []
    for bucket_id in range(BUCKETS):
        columns.append(
            jnp.sum(jnp.where(rel_table[None, None] == bucket_id, grad_wide, 0.0), axis=(0, 2, 3))
        )
    return jnp.stack(columns, axis=0)


def body(
    inputs,
    seg_starts,
    lengths,
    init_state,
    attn_gain,
    state_gain,
    mlp_gain,
    w_query,
    w_key,
    w_value,
    w_out,
    w_squery,
    w_sout,
    w_up,
    w_down,
    rel_bias,
    gate_bias,
    out_cot,
    state_cot,
):
    seq_count = inputs.shape[0]
    chain_length = lax.axis_size("seq")
    block_index = lax.axis_index("seq")
    is_first = block_index == 0
    width_local = w_query.shape[1]
    head_count = width_local // HEAD_DIM
    gate_value = jax.nn.sigmoid(gate_bias)
    positions = jnp.arange(BLOCK)
    inputs_wide = inputs.astype(jnp.float32)
    tokens_low = gather_rows(to_low(layer_norm(inputs_wide, attn_gain)))
    query_tok = to_low(matmul(tokens_low, w_query))
    key_tok = to_low(matmul(tokens_low, w_key))
    value_tok = to_low(matmul(tokens_low, w_value))
    key_prev, value_prev = passed_along((key_tok, value_tok), "seq", 1)
    valid_keys = (block_index * BLOCK + positions)[None, :] < lengths[:, None]
    batched_attend = jax.vmap(attend_forward, in_axes=(0, 0, 0, None, 0))
    batched_back = jax.vmap(attend_back, in_axes=(0, 0, 0, None, 0, 0, 0))

    def state_forward(state_rows, key_blk, value_blk, valid_blk):
        state_low = lax.all_gather(
            to_low(layer_norm(state_rows, state_gain)), "tensor", axis=1, tiled=True
        )
        query_st = to_low(matmul(state_low, w_squery))
        key_st = to_low(matmul(state_low, w_key))
        value_st = to_low(matmul(state_low, w_value))
        key_all = jnp.concatenate([key_blk, key_st], axis=1)
        value_all = jnp.concatenate([value_blk, value_st], axis=1)
        mixed_st, lse_st = batched_attend(
            query_st, key_all, value_all, 0.0, state_mask_of(valid_blk)
        )
        update = lax.psum_scatter(
            matmul(mixed_st, w_sout).astype(jnp.bfloat16), "tensor", scatter_dimension=1, tiled=True
        ).astype(jnp.float32)
        state_next = gate_value * state_rows + (1.0 - gate_value) * update
        return (state_next, (state_low, query_st, key_st, value_st, mixed_st, lse_st, update))

    def state_backward(
        grad_out, state_rows, kept_one, key_blk, value_blk, valid_blk, extra_key, extra_value
    ):
        state_low, query_st, key_st, value_st, mixed_st, lse_st, update = kept_one
        gate_part = (
            jnp.sum(grad_out * (state_rows - update), axis=(0, 1)) * gate_value * (1.0 - gate_value)
        )
        grad_update = lax.all_gather(
            to_low((1.0 - gate_value) * grad_out), "tensor", axis=1, tiled=True
        )
        grad_mixed_st = to_low(matmul_t(grad_update, w_sout))
        sout_part = outer_sum(mixed_st, grad_update)
        key_all = jnp.concatenate([key_blk, key_st], axis=1)
        value_all = jnp.concatenate([value_blk, value_st], axis=1)
        grad_query_st, grad_keys_st, grad_values_st, _ = batched_back(
            query_st, key_all, value_all, 0.0, state_mask_of(valid_blk), lse_st, grad_mixed_st
        )
        query_low = to_low(grad_query_st)
        key_low = to_low(grad_keys_st[:, BLOCK:] + extra_key)
        value_low = to_low(grad_values_st[:, BLOCK:] + extra_value)
        squery_part = outer_sum(state_low, query_low)
        key_part = outer_sum(state_low, key_low)
        value_part = outer_sum(state_low, value_low)
        terms = (
            matmul_t(query_low, w_squery) + matmul_t(key_low, w_key) + matmul_t(value_low, w_value)
        )
        grad_normed = lax.psum_scatter(
            terms.astype(jnp.bfloat16), "tensor", scatter_dimension=1, tiled=True
        ).astype(jnp.float32)
        grad_rows_norm, gain_part = norm_back(state_rows, state_gain, grad_normed)
        grad_in = gate_value * grad_out + grad_rows_norm
        block_grads = (grad_keys_st[:, :BLOCK], grad_values_st[:, :BLOCK])
        return (
            grad_in,
            block_grads,
            (squery_part, key_part, value_part, sout_part, gain_part, gate_part),
        )

    zeros_rows = jnp.zeros((seq_count,) + init_state.shape, jnp.float32)
    narrow_zero = jnp.zeros((seq_count, STATES, width_local), jnp.bfloat16)
    stored_start = (
        zeros_rows,
        zeros_rows,
        jnp.zeros((seq_count, STATES, D), jnp.bfloat16),
        narrow_zero,
        narrow_zero,
        narrow_zero,
        narrow_zero,
        jnp.zeros((seq_count, head_count, STATES), jnp.float32),
        zeros_rows,
    )

    def forward_turn(turn_index, carry):
        incoming, stored_now = carry
        order_index = turn_index - block_index
        is_live = (order_index >= 0) & (order_index < seq_count)
        picked = jnp.clip(order_index, 0, seq_count - 1)
        rows_now = jnp.where(is_first, init_state[None], incoming)
        key_one = lax.dynamic_slice_in_dim(key_tok, picked, 1, 0)
        value_one = lax.dynamic_slice_in_dim(value_tok, picked, 1, 0)
        valid_one = lax.dynamic_slice_in_dim(valid_keys, picked, 1, 0)
        rows_next, kept_one = state_forward(rows_now, key_one, value_one, valid_one)
        fresh = (rows_now, rows_next) + kept_one
        stored_now = tuple(
            (
                jnp.where(
                    is_live,
                    lax.dynamic_update_slice_in_dim(whole_array, fresh_part, picked, 0),
                    whole_array,
                )
                for whole_array, fresh_part in zip(stored_now, fresh)
            )
        )
        return (pass_state(rows_next), stored_now)

    incoming_start = jnp.zeros((1,) + init_state.shape, jnp.float32)
    _, stored_all = lax.fori_loop(
        0, chain_length + seq_count - 1, forward_turn, (incoming_start, stored_start)
    )
    state_in = stored_all[0]
    state_out = stored_all[1]
    kept = stored_all[2:]
    key_all_tok = jnp.concatenate([key_prev, key_tok, kept[2]], axis=1)
    value_all_tok = jnp.concatenate([value_prev, value_tok, kept[3]], axis=1)
    allowed_tok = jax.vmap(token_mask, in_axes=(0, 0, None))(seg_starts[:, 0], lengths, block_index)
    rel_table = bucket_of((jnp.arange(2 * BLOCK) - BLOCK)[None, :] - positions[:, None])
    full_bias = jnp.concatenate(
        [bias_lookup(rel_bias, rel_table), jnp.zeros((head_count, BLOCK, STATES), jnp.float32)],
        axis=2,
    )
    mixed_tok, lse_tok = batched_attend(
        query_tok, key_all_tok, value_all_tok, full_bias, allowed_tok
    )
    hidden_in = inputs_wide + sum_rows(matmul(mixed_tok, w_out))
    mid_low = gather_rows(to_low(layer_norm(hidden_in, mlp_gain)))
    pre_act = matmul(mid_low, w_up)
    hidden_low = to_low(jax.nn.gelu(pre_act))
    mlp_rows = sum_rows(matmul(hidden_low, w_down))
    tokens_out = (hidden_in + mlp_rows).astype(jnp.bfloat16)
    cot_wide = out_cot.astype(jnp.float32)
    cot_used = gather_rows(out_cot)
    grad_hidden_act = matmul_t(cot_used, w_down)
    down_grad = outer_sum(hidden_low, cot_used)
    grad_pre = to_low(gelu_back(pre_act, grad_hidden_act))
    up_grad = outer_sum(mid_low, grad_pre)
    grad_normed_mid = sum_rows(matmul_t(grad_pre, w_up))
    grad_mid_in, mlp_gain_grad = norm_back(hidden_in, mlp_gain, grad_normed_mid)
    grad_hidden = cot_wide + grad_mid_in
    grad_attn_low = gather_rows(to_low(grad_hidden))
    grad_mixed = to_low(matmul_t(grad_attn_low, w_out))
    out_grad = outer_sum(mixed_tok, grad_attn_low)
    grad_query_tok, grad_keys_tok, grad_values_tok, grad_scores = batched_back(
        query_tok, key_all_tok, value_all_tok, full_bias, allowed_tok, lse_tok, grad_mixed
    )
    bias_grad = bias_sums(grad_scores[..., : 2 * BLOCK], rel_table)
    grad_key_next, grad_value_next = (
        passed_along(grad_keys_tok[:, :BLOCK].astype(jnp.bfloat16), "seq", -1).astype(jnp.float32),
        passed_along(grad_values_tok[:, :BLOCK].astype(jnp.bfloat16), "seq", -1).astype(
            jnp.float32
        ),
    )
    grad_key_own = grad_keys_tok[:, BLOCK : 2 * BLOCK] + grad_key_next
    grad_value_own = grad_values_tok[:, BLOCK : 2 * BLOCK] + grad_value_next
    grad_key_st_tok = grad_keys_tok[:, 2 * BLOCK :]
    grad_value_st_tok = grad_values_tok[:, 2 * BLOCK :]
    cot_rows = state_cot[:, 0].astype(jnp.float32)
    wide_zero = jnp.zeros((seq_count, BLOCK, width_local), jnp.float32)
    stored_back = (zeros_rows, wide_zero, wide_zero)
    totals_start = (
        jnp.zeros((D, width_local), jnp.float32),
        jnp.zeros((D, width_local), jnp.float32),
        jnp.zeros((D, width_local), jnp.float32),
        jnp.zeros((width_local, D), jnp.float32),
        jnp.zeros((D,), jnp.float32),
        jnp.zeros((D,), jnp.float32),
    )

    def backward_turn(turn_index, carry):
        incoming, stored_now, totals_now = carry
        order_index = turn_index - (chain_length - 1 - block_index)
        is_live = (order_index >= 0) & (order_index < seq_count)
        picked = jnp.clip(order_index, 0, seq_count - 1)

        def slice_one(whole_array):
            return lax.dynamic_slice_in_dim(whole_array, picked, 1, 0)

        grad_out = slice_one(cot_rows) + incoming
        kept_one = tuple((slice_one(kept_array) for kept_array in kept))
        grad_in, block_one, parts_one = state_backward(
            grad_out,
            slice_one(state_in),
            kept_one,
            slice_one(key_tok),
            slice_one(value_tok),
            slice_one(valid_keys),
            slice_one(grad_key_st_tok),
            slice_one(grad_value_st_tok),
        )
        fresh = (grad_in,) + block_one
        stored_now = tuple(
            (
                jnp.where(
                    is_live,
                    lax.dynamic_update_slice_in_dim(whole_array, fresh_part, picked, 0),
                    whole_array,
                )
                for whole_array, fresh_part in zip(stored_now, fresh)
            )
        )
        totals_now = tuple(
            (
                total_now + jnp.where(is_live, part_now, 0.0)
                for total_now, part_now in zip(totals_now, parts_one)
            )
        )
        return (pass_back(grad_in), stored_now, totals_now)

    incoming_start = jnp.zeros((1,) + init_state.shape, jnp.float32)
    _, stored_done, weight_parts = lax.fori_loop(
        0, chain_length + seq_count - 1, backward_turn, (incoming_start, stored_back, totals_start)
    )
    grad_in_all, grad_key_blk, grad_value_blk = stored_done
    query_low = to_low(grad_query_tok)
    key_low = to_low(grad_key_own + grad_key_blk)
    value_low = to_low(grad_value_own + grad_value_blk)
    query_grad = outer_sum(tokens_low, query_low)
    key_grad = outer_sum(tokens_low, key_low) + weight_parts[1]
    value_grad = outer_sum(tokens_low, value_low) + weight_parts[2]
    grad_tokens = sum_rows(
        matmul_t(query_low, w_query) + matmul_t(key_low, w_key) + matmul_t(value_low, w_value)
    )
    grad_in_norm, attn_gain_grad = norm_back(inputs_wide, attn_gain, grad_tokens)
    inputs_grad = grad_hidden + grad_in_norm
    state_part = jnp.where(is_first, jnp.sum(grad_in_all, axis=0), 0.0)
    gains = lax.psum(
        jnp.stack([attn_gain_grad, weight_parts[4], mlp_gain_grad, weight_parts[5]]), "tensor"
    )
    totals = (
        lax.psum(query_grad.astype(jnp.bfloat16), ("dp", "seq")).astype(jnp.float32),
        lax.psum(key_grad.astype(jnp.bfloat16), ("dp", "seq")).astype(jnp.float32),
        lax.psum(value_grad.astype(jnp.bfloat16), ("dp", "seq")).astype(jnp.float32),
        lax.psum(out_grad.astype(jnp.bfloat16), ("dp", "seq")).astype(jnp.float32),
        lax.psum(weight_parts[0].astype(jnp.bfloat16), ("dp", "seq")).astype(jnp.float32),
        lax.psum(weight_parts[3].astype(jnp.bfloat16), ("dp", "seq")).astype(jnp.float32),
        lax.psum(up_grad.astype(jnp.bfloat16), ("dp", "seq")).astype(jnp.float32),
        lax.psum(down_grad.astype(jnp.bfloat16), ("dp", "seq")).astype(jnp.float32),
        lax.psum(bias_grad.astype(jnp.bfloat16), ("dp", "seq")).astype(jnp.float32),
        lax.psum(state_part.astype(jnp.bfloat16), ("dp", "seq")).astype(jnp.float32),
        lax.psum(gains.astype(jnp.bfloat16), ("dp", "seq")).astype(jnp.float32),
    )
    gain_total = totals[10]
    return (
        tokens_out,
        state_out[:, None],
        inputs_grad,
        totals[9],
        gain_total[0],
        gain_total[1],
        gain_total[2],
        totals[0],
        totals[1],
        totals[2],
        totals[3],
        totals[4],
        totals[5],
        totals[6],
        totals[7],
        totals[8],
        gain_total[3],
    )


def chosen_body(mesh):
    if mesh.shape["seq"] == 4 and mesh.shape["tensor"] == 4:
        return line_body
    return body


MESH_ID = pl.DeviceIdType.MESH
ROWS = 128
CHUNKS = BLOCK // ROWS
LINE = 8
SCALE = HEAD_DIM ** (-0.5)
VMEM_LIMIT = 60 * 1024 * 1024


def dot_nn(left, right):
    return lax.dot_general(left, right, (((1,), (0,)), ((), ())), preferred_element_type=jnp.float32)


def dot_nt(left, right):
    return lax.dot_general(left, right, (((1,), (1,)), ((), ())), preferred_element_type=jnp.float32)


def dot_tn(left, right):
    return lax.dot_general(left, right, (((0,), (0,)), ((), ())), preferred_element_type=jnp.float32)


def line_place():
    place = lax.axis_index("seq")
    half = lax.rem(place, 2)
    rank = lax.axis_index("tensor")
    return place, half, rank


def span(index, size):
    return pl.ds(pl.multiple_of(index * size, size), size)


def norm_parts(rows):
    centered = rows - jnp.mean(rows, axis=-1, keepdims=True)
    spread = jnp.mean(centered * centered, axis=-1, keepdims=True)
    return centered, lax.rsqrt(spread + norm_eps)


def token_masks(scal, block_id, first_row):
    length = scal[0]
    start = scal[1 + block_id]
    row = lax.broadcasted_iota(jnp.int32, (ROWS, BLOCK), 0) + first_row
    col = lax.broadcasted_iota(jnp.int32, (ROWS, BLOCK), 1)
    prev_limit = jnp.where(block_id > 0, length - (block_id - 1) * BLOCK, 0)
    prev_ok = (col > row) & (col < prev_limit)
    row_in = (row >= start) & (row < start + SEG)
    col_in = (col >= start) & (col < start + SEG)
    cur_ok = ((col <= row) | (row_in & col_in)) & (col < length - block_id * BLOCK)
    return prev_ok, cur_ok


def state_block_mask(scal, block_id):
    col = lax.broadcasted_iota(jnp.int32, (ROWS, BLOCK), 1)
    return col < scal[0] - block_id * BLOCK


def softmax_of(score_parts):
    top = jnp.max(score_parts[0], axis=-1, keepdims=True)
    for part in score_parts[1:]:
        top = jnp.maximum(top, jnp.max(part, axis=-1, keepdims=True))
    raised = [jnp.exp(part - top) for part in score_parts]
    total = jnp.sum(raised[0], axis=-1, keepdims=True)
    for part in raised[1:]:
        total = total + jnp.sum(part, axis=-1, keepdims=True)
    inverse = 1.0 / total
    return [to_low(part * inverse) for part in raised], top + jnp.log(total)


def token_scores(scal, qkv, qkvst, bias, block_id, chunk):
    rows = span(chunk, ROWS)
    prev_id = jnp.maximum(block_id - 1, 0)
    query = qkv[block_id, rows, 0:128]
    prev_ok, cur_ok = token_masks(scal, block_id, chunk * ROWS)
    prev = dot_nt(query, qkv[prev_id, :, 128:256]) * SCALE + bias[rows, 0:BLOCK]
    cur = dot_nt(query, qkv[block_id, :, 128:256]) * SCALE + bias[rows, BLOCK : 2 * BLOCK]
    stt = dot_nt(query, qkvst[block_id, :, 128:256]) * SCALE
    prev = jnp.where(prev_ok, prev, masked_score)
    cur = jnp.where(cur_ok, cur, masked_score)
    return query, (prev, cur, stt)


def state_scores(scal, qkv, qkvst, block_id, chunk):
    query = qkvst[block_id, span(chunk, ROWS), 0:128]
    tok = dot_nt(query, qkv[block_id, :, 128:256]) * SCALE
    tok = jnp.where(state_block_mask(scal, block_id), tok, masked_score)
    stt = dot_nt(query, qkvst[block_id, :, 128:256]) * SCALE
    return query, (tok, stt)


def forward_kernel(
    scal, qkv, start, w_state, w_sout, vecs, bias,
    o_out, lse_out, state_rows, state_low, qkvst, lse_st, os_rows,
    held, os_all, send_sem, pass_sem, recv_sem,
):
    place, half, rank = line_place()
    partner = place + 1 - 2 * half
    head = 2 * rank + half
    peers = [lax.rem(rank + step, 4) for step in (1, 2, 3)]
    barrier = pltpu.get_barrier_semaphore()
    for peer in peers:
        pl.semaphore_signal(
            barrier, inc=1, device_id={"seq": place, "tensor": peer}, device_id_type=MESH_ID
        )
    pl.semaphore_signal(
        barrier, inc=1, device_id={"seq": partner, "tensor": rank}, device_id_type=MESH_ID
    )
    held[...] = start[...].astype(jnp.float32)
    gain = vecs[0:1, :]
    gate = vecs[1:2, :]
    pl.semaphore_wait(barrier, 4)

    def carry_copy(block_id, which, sem, seq_to, rank_to):
        part = os_all.at[block_id, :, span(which, 128)]
        return pltpu.make_async_remote_copy(
            src_ref=part,
            dst_ref=part,
            send_sem=sem,
            recv_sem=recv_sem.at[block_id, which],
            device_id={"seq": seq_to, "tensor": rank_to},
            device_id_type=MESH_ID,
        )

    def one_block(block_id, _):
        def project(chunk, _):
            rows = span(chunk, ROWS)
            centered, scale = norm_parts(held[rows, :])
            low = to_low(centered * scale * gain)
            state_low[block_id, rows, :] = low
            qkvst[block_id, rows, :] = to_low(dot_nn(low, w_state[...]))
            return 0

        lax.fori_loop(0, CHUNKS, project, 0)

        def attend_state(chunk, _):
            rows = span(chunk, ROWS)
            _, parts = state_scores(scal, qkv, qkvst, block_id, chunk)
            (w_tok, w_stt), total = softmax_of(parts)
            mixed = dot_nn(w_tok, qkv[block_id, :, 256:384]) + dot_nn(
                w_stt, qkvst[block_id, :, 256:384]
            )
            os_all[block_id, rows, span(head, 128)] = to_low(mixed)
            lse_st[block_id, rows, :] = total
            return 0

        lax.fori_loop(0, CHUNKS, attend_state, 0)
        for slot, peer in enumerate(peers):
            carry_copy(block_id, head, send_sem.at[block_id, slot], place, peer).start()
        carry_copy(block_id, head, send_sem.at[block_id, 3], partner, rank).start()

        def attend_token(chunk, _):
            rows = span(chunk, ROWS)
            _, parts = token_scores(scal, qkv, qkvst, bias, block_id, chunk)
            weights, total = softmax_of(parts)
            prev_id = jnp.maximum(block_id - 1, 0)
            mixed = (
                dot_nn(weights[0], qkv[prev_id, :, 256:384])
                + dot_nn(weights[1], qkv[block_id, :, 256:384])
                + dot_nn(weights[2], qkvst[block_id, :, 256:384])
            )
            o_out[block_id, rows, :] = to_low(mixed)
            lse_out[block_id, rows, :] = total
            return 0

        lax.fori_loop(0, CHUNKS, attend_token, 0)
        for slot, peer in enumerate(peers):
            other = 2 * peer + half
            carry_copy(block_id, other, send_sem.at[block_id, slot], place, peer).wait_recv()
            carry_copy(block_id, other, pass_sem.at[block_id, slot], partner, rank).start()
        for other_rank in range(4):
            carry_copy(
                block_id, 2 * other_rank + 1 - half, send_sem.at[block_id, 3], partner, rank
            ).wait_recv()

        def update(chunk, _):
            rows = span(chunk, ROWS)
            change = dot_nn(os_all[block_id, rows, :], w_sout[...])
            held[rows, :] = gate * held[rows, :] + (1.0 - gate) * change
            return 0

        lax.fori_loop(0, CHUNKS, update, 0)
        state_rows[block_id] = held[span(rank, 128), :]
        os_rows[block_id] = os_all[block_id, span(head, 64), :]
        return 0

    lax.fori_loop(0, 4, one_block, 0)

    def drain(block_id, _):
        for slot, peer in enumerate(peers):
            carry_copy(block_id, head, send_sem.at[block_id, slot], place, peer).wait_send()
            other = 2 * peer + half
            carry_copy(block_id, other, pass_sem.at[block_id, slot], partner, rank).wait_send()
        carry_copy(block_id, head, send_sem.at[block_id, 3], partner, rank).wait_send()
        return 0

    lax.fori_loop(0, 4, drain, 0)


def vmem_specs(count):
    return [pl.BlockSpec(memory_space=pltpu.VMEM)] * count


def forward_chain(scal, qkv, start, w_state, w_sout, vecs, bias):
    low, wide = jnp.bfloat16, jnp.float32
    shapes = (
        ((4, BLOCK, 128), low),
        ((4, BLOCK, 1), wide),
        ((4, 128, D), wide),
        ((4, STATES, D), low),
        ((4, STATES, 384), low),
        ((4, STATES, 1), wide),
        ((4, 64, D), low),
    )
    return pl.pallas_call(
        forward_kernel,
        out_shape=[jax.ShapeDtypeStruct(*one) for one in shapes],
        in_specs=[pl.BlockSpec(memory_space=pltpu.SMEM)] + vmem_specs(6),
        out_specs=vmem_specs(7),
        scratch_shapes=[
            pltpu.VMEM((STATES, D), wide),
            pltpu.VMEM((4, STATES, D), low),
            pltpu.SemaphoreType.DMA((4, 4)),
            pltpu.SemaphoreType.DMA((4, 3)),
            pltpu.SemaphoreType.DMA((4, 8)),
        ],
        compiler_params=pltpu.CompilerParams(
            collective_id=1, has_side_effects=True, vmem_limit_bytes=VMEM_LIMIT
        ),
        cost_estimate=pl.CostEstimate(flops=20000000000, bytes_accessed=20000000, transcendentals=0),
        name="forward_chain",
    )(scal, qkv, start, w_state, w_sout, vecs, bias)


def backward_kernel(
    scal, qkv, d_o, lse_tok, qkvst, lse_st, states, cots, w_back, w_sout, vecs, bias,
    d_qkv, d_qkvst, du_rows, d_start, sums, dz_sum,
    key_acc, value_acc, st_key, st_value, dos_rows, dos_got, d_got, grad_in,
    send_sem, recv_sem,
):
    place, half, rank = line_place()
    head = 2 * rank + half
    peers = []
    for step in range(1, LINE):
        other = lax.rem(head + step, LINE)
        peers.append((other, place - half + lax.rem(other, 2), other // 2))
    barrier = pltpu.get_barrier_semaphore()
    for _, seq_to, rank_to in peers:
        pl.semaphore_signal(
            barrier, inc=1, device_id={"seq": seq_to, "tensor": rank_to}, device_id_type=MESH_ID
        )
    gain = vecs[0:1, :]
    gate = vecs[1:2, :]
    key_acc[...] = jnp.zeros_like(key_acc)
    value_acc[...] = jnp.zeros_like(value_acc)
    dz_sum[...] = jnp.zeros_like(dz_sum)
    sums[...] = jnp.zeros_like(sums)
    grad_in[...] = jnp.zeros_like(grad_in)

    def back_parts(parts, total, grad, values):
        weights = [jnp.exp(part - total) for part in parts]
        d_weights = [dot_nt(grad, value) for value in values]
        inner = jnp.sum(weights[0] * d_weights[0], axis=-1, keepdims=True)
        for one, other in zip(weights[1:], d_weights[1:]):
            inner = inner + jnp.sum(one * other, axis=-1, keepdims=True)
        d_scores = [to_low(one * (other - inner)) for one, other in zip(weights, d_weights)]
        return [to_low(one) for one in weights], d_scores

    def token_back(block_id):
        prev_id = jnp.maximum(block_id - 1, 0)
        st_key[...] = jnp.zeros_like(st_key)
        st_value[...] = jnp.zeros_like(st_value)

        def one_chunk(chunk, _):
            rows = span(chunk, ROWS)
            query, parts = token_scores(scal, qkv, qkvst, bias, block_id, chunk)
            grad = d_o[block_id, rows, :]
            keys = (qkv[prev_id, :, 128:256], qkv[block_id, :, 128:256], qkvst[block_id, :, 128:256])
            values = (
                qkv[prev_id, :, 256:384], qkv[block_id, :, 256:384], qkvst[block_id, :, 256:384]
            )
            weights, d_scores = back_parts(parts, lse_tok[block_id, rows, :], grad, values)
            d_query = dot_nn(d_scores[0], keys[0])
            d_query = d_query + dot_nn(d_scores[1], keys[1]) + dot_nn(d_scores[2], keys[2])
            d_qkv[block_id, rows, 0:128] = to_low(d_query * SCALE)
            key_acc[prev_id] += dot_tn(d_scores[0], query) * SCALE
            value_acc[prev_id] += dot_tn(weights[0], grad)
            key_acc[block_id] += dot_tn(d_scores[1], query) * SCALE
            value_acc[block_id] += dot_tn(weights[1], grad)
            st_key[...] += dot_tn(d_scores[2], query) * SCALE
            st_value[...] += dot_tn(weights[2], grad)
            dz_sum[rows, 0:BLOCK] += d_scores[0].astype(jnp.float32)
            dz_sum[rows, BLOCK : 2 * BLOCK] += d_scores[1].astype(jnp.float32)
            return 0

        lax.fori_loop(0, CHUNKS, one_chunk, 0)

    token_back(3)
    pl.semaphore_wait(barrier, LINE - 1)

    def mixed_copy(block_id, slot, sender, other, seq_to, rank_to):
        return pltpu.make_async_remote_copy(
            src_ref=dos_rows.at[block_id, :, span(other, 128)],
            dst_ref=dos_got.at[block_id, span(sender, 64), :],
            send_sem=send_sem.at[0, block_id, slot],
            recv_sem=recv_sem.at[0, block_id, sender],
            device_id={"seq": seq_to, "tensor": rank_to},
            device_id_type=MESH_ID,
        )

    def grads_copy(block_id, slot, sender, other, seq_to, rank_to):
        return pltpu.make_async_remote_copy(
            src_ref=d_qkvst.at[block_id, span(other, 64), :],
            dst_ref=d_got.at[block_id, sender],
            send_sem=send_sem.at[1, block_id, slot],
            recv_sem=recv_sem.at[1, block_id, sender],
            device_id={"seq": seq_to, "tensor": rank_to},
            device_id_type=MESH_ID,
        )

    def one_block(turn, _):
        block_id = 3 - turn
        grad_out = grad_in[...] + cots[block_id].astype(jnp.float32)
        sums[0:1, :] += jnp.sum(
            grad_out * (states[block_id] - states[block_id + 1]), axis=0, keepdims=True
        ) * gate
        change = to_low((1.0 - gate) * grad_out)
        du_rows[block_id] = change
        dos_rows[block_id] = to_low(dot_nt(change, w_sout[...]))
        for slot, (other, seq_to, rank_to) in enumerate(peers):
            mixed_copy(block_id, slot, head, other, seq_to, rank_to).start()
        dos_got[block_id, span(head, 64), :] = dos_rows[block_id, :, span(head, 128)]
        for slot, (other, seq_to, rank_to) in enumerate(peers):
            mixed_copy(block_id, slot, other, other, seq_to, rank_to).wait_recv()

        def one_chunk(chunk, _):
            rows = span(chunk, ROWS)
            query, parts = state_scores(scal, qkv, qkvst, block_id, chunk)
            grad = dos_got[block_id, rows, :]
            keys = (qkv[block_id, :, 128:256], qkvst[block_id, :, 128:256])
            values = (qkv[block_id, :, 256:384], qkvst[block_id, :, 256:384])
            weights, d_scores = back_parts(parts, lse_st[block_id, rows, :], grad, values)
            d_query = dot_nn(d_scores[0], keys[0]) + dot_nn(d_scores[1], keys[1])
            d_qkvst[block_id, rows, 0:128] = to_low(d_query * SCALE)
            key_acc[block_id] += dot_tn(d_scores[0], query) * SCALE
            value_acc[block_id] += dot_tn(weights[0], grad)
            st_key[...] += dot_tn(d_scores[1], query) * SCALE
            st_value[...] += dot_tn(weights[1], grad)
            return 0

        lax.fori_loop(0, CHUNKS, one_chunk, 0)
        d_qkvst[block_id, :, 128:256] = to_low(st_key[...])
        d_qkvst[block_id, :, 256:384] = to_low(st_value[...])
        for slot, (other, seq_to, rank_to) in enumerate(peers):
            grads_copy(block_id, slot, head, other, seq_to, rank_to).start()
        d_got[block_id, head] = d_qkvst[block_id, span(head, 64), :]

        @pl.when(turn < 3)
        def _():
            token_back(block_id - 1)

        d_qkv[block_id, :, 128:256] = to_low(key_acc[block_id])
        d_qkv[block_id, :, 256:384] = to_low(value_acc[block_id])
        for slot, (other, seq_to, rank_to) in enumerate(peers):
            grads_copy(block_id, slot, other, other, seq_to, rank_to).wait_recv()
        d_low = dot_nn(d_got[block_id, 0], w_back[0])
        for other in range(1, LINE):
            d_low = d_low + dot_nn(d_got[block_id, other], w_back[other])
        centered, scale = norm_parts(states[block_id])
        normed = centered * scale
        sums[1:2, :] += jnp.sum(d_low * normed, axis=0, keepdims=True)
        lifted = d_low * gain
        grad_in[...] = gate * grad_out + scale * (
            lifted
            - jnp.mean(lifted, axis=-1, keepdims=True)
            - normed * jnp.mean(lifted * normed, axis=-1, keepdims=True)
        )
        return 0

    lax.fori_loop(0, 4, one_block, 0)
    d_start[...] = grad_in[...]

    def drain(block_id, _):
        for slot, (other, seq_to, rank_to) in enumerate(peers):
            mixed_copy(block_id, slot, head, other, seq_to, rank_to).wait_send()
            grads_copy(block_id, slot, head, other, seq_to, rank_to).wait_send()
        return 0

    lax.fori_loop(0, 4, drain, 0)


def backward_chain(scal, qkv, d_o, lse_tok, qkvst, lse_st, states, cots, w_back, w_sout, vecs, bias):
    low, wide = jnp.bfloat16, jnp.float32
    shapes = (
        ((4, BLOCK, 384), low),
        ((4, STATES, 384), low),
        ((4, 64, D), low),
        ((64, D), wide),
        ((8, D), wide),
        ((BLOCK, 2 * BLOCK), wide),
    )
    return pl.pallas_call(
        backward_kernel,
        out_shape=[jax.ShapeDtypeStruct(*one) for one in shapes],
        in_specs=[pl.BlockSpec(memory_space=pltpu.SMEM)] + vmem_specs(11),
        out_specs=vmem_specs(6),
        scratch_shapes=[
            pltpu.VMEM((4, BLOCK, 128), wide),
            pltpu.VMEM((4, BLOCK, 128), wide),
            pltpu.VMEM((STATES, 128), wide),
            pltpu.VMEM((STATES, 128), wide),
            pltpu.VMEM((4, 64, D), low),
            pltpu.VMEM((4, STATES, 128), low),
            pltpu.VMEM((4, LINE, 64, 384), low),
            pltpu.VMEM((64, D), wide),
            pltpu.SemaphoreType.DMA((2, 4, LINE - 1)),
            pltpu.SemaphoreType.DMA((2, 4, LINE)),
        ],
        compiler_params=pltpu.CompilerParams(
            collective_id=2, has_side_effects=True, vmem_limit_bytes=VMEM_LIMIT
        ),
        cost_estimate=pl.CostEstimate(flops=40000000000, bytes_accessed=40000000, transcendentals=0),
        name="backward_chain",
    )(scal, qkv, d_o, lse_tok, qkvst, lse_st, states, cots, w_back, w_sout, vecs, bias)


def plane_place():
    place, half, rank = line_place()
    side = lax.axis_index("dp")
    return side, place, half, rank


def plane_index(side, place):
    return 4 * side + place


def plane_gather(buf, rows, send_sem, recv_sem):
    side, place, half, rank = plane_place()
    across, beside = 1 - side, lax.rem(place + 2, 4)
    core = place + 1 - 2 * half
    me = plane_index(side, place)
    at_x, at_y = plane_index(across, place), plane_index(side, beside)
    at_d = plane_index(across, beside)
    to_x = {"dp": across}
    to_y = {"seq": beside}
    to_c = {"seq": core}
    size = rows // 2

    def piece(owner, part, slot, target):
        view = buf.at[owner, pl.ds(part * size, size), :]
        return pltpu.make_async_remote_copy(
            src_ref=view,
            dst_ref=view,
            send_sem=send_sem.at[slot],
            recv_sem=recv_sem.at[owner, part],
            device_id=target,
            device_id_type=MESH_ID,
        )

    sent = []

    def send(owner, part, target):
        one = piece(owner, part, len(sent), target)
        sent.append(one)
        one.start()

    def arrived(owner, part):
        piece(owner, part, 0, to_c).wait_recv()

    send(me, 0, to_x)
    send(me, 1, to_y)
    send(me, 1, to_x)
    send(me, 0, to_y)
    send(me, 0, to_c)
    send(me, 1, to_c)
    arrived(at_x, 0)
    send(at_x, 0, to_y)
    arrived(at_y, 1)
    send(at_y, 1, to_x)
    send(at_x, 0, to_c)
    send(at_y, 1, to_c)
    arrived(at_x, 1)
    send(at_x, 1, to_c)
    arrived(at_y, 0)
    send(at_y, 0, to_c)
    arrived(at_d, 0)
    send(at_d, 0, to_c)
    arrived(at_d, 1)
    send(at_d, 1, to_c)
    for owner in (
        plane_index(side, core),
        plane_index(across, core),
        plane_index(side, lax.rem(core + 2, 4)),
        plane_index(across, lax.rem(core + 2, 4)),
    ):
        arrived(owner, 0)
        arrived(owner, 1)
    for one in sent:
        one.wait_send()


def plane_scatter(part, core_got, near_got, far_got, total, rows, send_sem, recv_sem):
    side, place, half, rank = plane_place()
    across, beside = 1 - side, lax.rem(place + 2, 4)
    core = place + 1 - 2 * half
    me = plane_index(side, place)
    at_x, at_y = plane_index(across, place), plane_index(side, beside)
    at_d = plane_index(across, beside)
    size = rows // 2
    halves = (pl.ds(0, size), pl.ds(size, size))

    def moved(source, target_ref, slot, target):
        return pltpu.make_async_remote_copy(
            src_ref=source,
            dst_ref=target_ref,
            send_sem=send_sem.at[slot],
            recv_sem=recv_sem.at[slot],
            device_id=target,
            device_id_type=MESH_ID,
        )

    order = (at_d, at_x, at_y, me)
    swapped = (
        plane_index(across, lax.rem(core + 2, 4)),
        plane_index(across, core),
        plane_index(side, lax.rem(core + 2, 4)),
        plane_index(side, core),
    )
    first = [
        moved(part.at[owner], core_got.at[slot], slot, {"seq": core})
        for slot, owner in enumerate(swapped)
    ]
    for one in first:
        one.start()

    def add_into(owner, view, other):
        part[owner, view, :] = to_low(
            part[owner, view, :].astype(jnp.float32) + other.astype(jnp.float32)
        )

    near = [
        moved(part.at[at_d, halves[0], :], near_got.at[0], 4, {"dp": across}),
        moved(part.at[at_d, halves[1], :], near_got.at[1], 5, {"seq": beside}),
        moved(part.at[at_x, halves[0], :], near_got.at[2], 6, {"dp": across}),
        moved(part.at[at_y, halves[1], :], near_got.at[3], 7, {"seq": beside}),
    ]
    for slot, owner in enumerate(order):
        first[slot].wait_recv()
        for view in halves:
            add_into(owner, view, core_got[slot, view, :])
        if slot == 0:
            near[0].start()
            near[1].start()
        if slot == 1:
            near[2].start()
        if slot == 2:
            near[3].start()
    near[0].wait_recv()
    add_into(at_y, halves[0], near_got[0])
    far = [
        moved(part.at[at_y, halves[0], :], far_got.at[0], 8, {"seq": beside}),
        moved(part.at[at_x, halves[1], :], far_got.at[1], 9, {"dp": across}),
    ]
    far[0].start()
    near[1].wait_recv()
    add_into(at_x, halves[1], near_got[1])
    far[1].start()
    near[2].wait_recv()
    add_into(me, halves[0], near_got[2])
    near[3].wait_recv()
    add_into(me, halves[1], near_got[3])
    for slot, view in enumerate(halves):
        far[slot].wait_recv()
        total[view, :] = part[me, view, :].astype(jnp.float32) + far_got[slot].astype(jnp.float32)
    for one in first + near + far:
        one.wait_send()


def group_peers():
    place, half, rank = line_place()
    here = 4 * place + rank
    peers = []
    for step in range(1, 16):
        other = lax.rem(here + step, 16)
        peers.append((other, other // 4, lax.rem(other, 4)))
    return here, peers


def greet(peers):
    side = lax.axis_index("dp")
    barrier = pltpu.get_barrier_semaphore()
    for _, seq_to, rank_to in peers:
        pl.semaphore_signal(
            barrier, inc=1, device_id={"seq": seq_to, "tensor": rank_to}, device_id_type=MESH_ID
        )
    pl.semaphore_signal(barrier, inc=1, device_id={"dp": 1 - side}, device_id_type=MESH_ID)
    pl.semaphore_wait(barrier, len(peers) + 1)


def middle_forward_kernel(
    mixed, tokens, w_out, vecs,
    hidden, mixed_rows, mid_all,
    send_sem, recv_sem, ring_send, ring_recv,
):
    side, place, half, rank = plane_place()
    mine = place // 2
    head = 2 * rank + half
    here, peers = group_peers()
    greet(peers)

    def rows_copy(slot, sender, seq_from, rank_from, seq_to, rank_to):
        return pltpu.make_async_remote_copy(
            src_ref=mixed.at[seq_to, span(rank_to, 128), :],
            dst_ref=mixed_rows.at[
                seq_from // 2, :, span(2 * rank_from + lax.rem(seq_from, 2), 128)
            ],
            send_sem=send_sem.at[slot],
            recv_sem=recv_sem.at[sender],
            device_id={"seq": seq_to, "tensor": rank_to},
            device_id_type=MESH_ID,
        )

    for slot, (_, seq_to, rank_to) in enumerate(peers):
        rows_copy(slot, here, place, rank, seq_to, rank_to).start()
    mixed_rows[mine, :, span(head, 128)] = mixed[place, span(rank, 128), :]
    for slot, (other, seq_to, rank_to) in enumerate(peers):
        rows_copy(slot, other, seq_to, rank_to, seq_to, rank_to).wait_recv()
    me = plane_index(side, place)
    gain = vecs[2:3, :]

    def one(which, _):
        added = dot_nn(mixed_rows[which], w_out[...]) + tokens[which].astype(jnp.float32)
        hidden[which] = added
        centered, scale = norm_parts(added)
        mid_all[me, span(which, 128), :] = to_low(centered * scale * gain)
        return 0

    lax.fori_loop(0, 2, one, 0)
    plane_gather(mid_all, 256, ring_send, ring_recv)
    for slot, (_, seq_to, rank_to) in enumerate(peers):
        rows_copy(slot, here, place, rank, seq_to, rank_to).wait_send()


def middle_forward(mixed, tokens, w_out, vecs):
    low, wide = jnp.bfloat16, jnp.float32
    shapes = (((2, 128, D), wide), ((2, 128, D), low), ((8, 256, D), low))
    return pl.pallas_call(
        middle_forward_kernel,
        out_shape=[jax.ShapeDtypeStruct(*one) for one in shapes],
        in_specs=vmem_specs(4),
        out_specs=vmem_specs(3),
        scratch_shapes=[
            pltpu.SemaphoreType.DMA((15,)),
            pltpu.SemaphoreType.DMA((16,)),
            pltpu.SemaphoreType.DMA((16,)),
            pltpu.SemaphoreType.DMA((8, 2)),
        ],
        compiler_params=pltpu.CompilerParams(
            collective_id=3, has_side_effects=True, vmem_limit_bytes=VMEM_LIMIT
        ),
        cost_estimate=pl.CostEstimate(
            flops=30000000000, bytes_accessed=30000000, transcendentals=0
        ),
        name="middle_forward",
    )(mixed, tokens, w_out, vecs)


def middle_backward_kernel(
    part, hidden, cots, w_out, vecs,
    d_hidden, d_low, d_line, sums,
    work, core_got, near_got, far_got, total, d_rows,
    ring_send, ring_recv, send_sem, recv_sem,
):
    side, place, half, rank = plane_place()
    mine = place // 2
    head = 2 * rank + half
    here, peers = group_peers()

    def keep(owner, _):
        work[owner] = part[owner]
        return 0

    lax.fori_loop(0, 8, keep, 0)
    greet(peers)
    plane_scatter(work, core_got, near_got, far_got, total, 256, ring_send, ring_recv)
    gain = vecs[2:3, :]
    sums[...] = jnp.zeros_like(sums)

    def one(which, _):
        rows = span(which, 128)
        grad = total[rows, :]
        centered, scale = norm_parts(hidden[which])
        normed = centered * scale
        sums[0:1, :] += jnp.sum(grad * normed, axis=0, keepdims=True)
        lifted = grad * gain
        back = cots[which].astype(jnp.float32) + scale * (
            lifted
            - jnp.mean(lifted, axis=-1, keepdims=True)
            - normed * jnp.mean(lifted * normed, axis=-1, keepdims=True)
        )
        d_hidden[which] = back
        d_low[which] = to_low(back)
        d_rows[which] = to_low(dot_nt(to_low(back), w_out[...]))
        return 0

    lax.fori_loop(0, 2, one, 0)

    def line_copy(slot, sender, seq_from, rank_from, seq_to, rank_to):
        return pltpu.make_async_remote_copy(
            src_ref=d_rows.at[seq_to // 2, :, span(2 * rank_to + lax.rem(seq_to, 2), 128)],
            dst_ref=d_line.at[seq_from, span(rank_from, 128), :],
            send_sem=send_sem.at[slot],
            recv_sem=recv_sem.at[sender],
            device_id={"seq": seq_to, "tensor": rank_to},
            device_id_type=MESH_ID,
        )

    for slot, (_, seq_to, rank_to) in enumerate(peers):
        line_copy(slot, here, place, rank, seq_to, rank_to).start()
    d_line[place, span(rank, 128), :] = d_rows[mine, :, span(head, 128)]
    for slot, (other, seq_to, rank_to) in enumerate(peers):
        line_copy(slot, other, seq_to, rank_to, seq_to, rank_to).wait_recv()
    for slot, (_, seq_to, rank_to) in enumerate(peers):
        line_copy(slot, here, place, rank, seq_to, rank_to).wait_send()


def middle_backward(part, hidden, cots, w_out, vecs):
    low, wide = jnp.bfloat16, jnp.float32
    shapes = (((2, 128, D), wide), ((2, 128, D), low), ((4, BLOCK, 128), low), ((8, D), wide))
    return pl.pallas_call(
        middle_backward_kernel,
        out_shape=[jax.ShapeDtypeStruct(*one) for one in shapes],
        in_specs=vmem_specs(5),
        out_specs=vmem_specs(4),
        scratch_shapes=[
            pltpu.VMEM((8, 256, D), low),
            pltpu.VMEM((4, 256, D), low),
            pltpu.VMEM((4, 128, D), low),
            pltpu.VMEM((2, 128, D), low),
            pltpu.VMEM((256, D), wide),
            pltpu.VMEM((2, 128, D), low),
            pltpu.SemaphoreType.DMA((10,)),
            pltpu.SemaphoreType.DMA((10,)),
            pltpu.SemaphoreType.DMA((15,)),
            pltpu.SemaphoreType.DMA((16,)),
        ],
        compiler_params=pltpu.CompilerParams(
            collective_id=4, has_side_effects=True, vmem_limit_bytes=VMEM_LIMIT
        ),
        cost_estimate=pl.CostEstimate(
            flops=30000000000, bytes_accessed=30000000, transcendentals=0
        ),
        name="middle_backward",
    )(part, hidden, cots, w_out, vecs)


WIDE = 2048


def bias_kernel(line, table):
    first = line[...]
    row = lax.broadcasted_iota(jnp.int32, (8, WIDE), 0)
    for step in (1, 2, 4):
        first = jnp.where(row // step % 2 == 1, pltpu.roll(first, step, 1), first)

    def one(group, _):
        table[span(group, 8), :] = pltpu.roll(first, 8 * group, 1)[:, 0 : 2 * BLOCK]
        return 0

    lax.fori_loop(0, BLOCK // 8, one, 0)


def bias_table(line):
    return pl.pallas_call(
        bias_kernel,
        out_shape=jax.ShapeDtypeStruct((BLOCK, 2 * BLOCK), jnp.float32),
        in_specs=vmem_specs(1),
        out_specs=pl.BlockSpec(memory_space=pltpu.VMEM),
        compiler_params=pltpu.CompilerParams(vmem_limit_bytes=VMEM_LIMIT),
        name="bias_table",
    )(line)


def diagonal_kernel(table, out, acc):
    acc[...] = jnp.zeros_like(acc)

    def one(group, _):
        rows = table[span(group, 8), :]
        wide = jnp.concatenate([rows, jnp.zeros((8, WIDE - 2 * BLOCK), jnp.float32)], axis=1)
        acc[...] += pltpu.roll(wide, lax.rem(WIDE - 8 * group, WIDE), 1)
        return 0

    lax.fori_loop(0, BLOCK // 8, one, 0)
    total = acc[...]
    row = lax.broadcasted_iota(jnp.int32, (8, WIDE), 0)
    for step in (1, 2, 4):
        total = jnp.where(row // step % 2 == 1, pltpu.roll(total, WIDE - step, 1), total)
    out[...] = jnp.broadcast_to(jnp.sum(total, axis=0, keepdims=True), (8, WIDE))


def diagonal_sums(table):
    return pl.pallas_call(
        diagonal_kernel,
        out_shape=jax.ShapeDtypeStruct((8, WIDE), jnp.float32),
        in_specs=vmem_specs(1),
        out_specs=pl.BlockSpec(memory_space=pltpu.VMEM),
        scratch_shapes=[pltpu.VMEM((8, WIDE), jnp.float32)],
        compiler_params=pltpu.CompilerParams(vmem_limit_bytes=VMEM_LIMIT),
        name="diagonal_sums",
    )(table)


def own_half(part, half, axis):
    empty = jnp.zeros_like(part)
    return jnp.where(
        half == 0,
        jnp.concatenate([part, empty], axis=axis),
        jnp.concatenate([empty, part], axis=axis),
    )


def swap_seq(value):
    return lax.all_to_all(value, "seq", 0, 0, tiled=False)


def line_body(
    inputs,
    seg_starts,
    lengths,
    init_state,
    attn_gain,
    state_gain,
    mlp_gain,
    w_query,
    w_key,
    w_value,
    w_out,
    w_squery,
    w_sout,
    w_up,
    w_down,
    rel_bias,
    gate_bias,
    out_cot,
    state_cot,
):
    low, wide = jnp.bfloat16, jnp.float32
    place = lax.axis_index("seq")
    half = lax.rem(place, 2)
    mine = place // 2
    head_of = lambda weight: lax.dynamic_slice_in_dim(weight, half * 128, 128, 1)
    gate_value = jax.nn.sigmoid(gate_bias)
    vecs = jnp.stack([state_gain, gate_value, mlp_gain] + [jnp.zeros_like(gate_value)] * 5)
    offsets = jnp.arange(WIDE) - BLOCK
    offsets = jnp.where(offsets >= WIDE - 2 * BLOCK, offsets - WIDE, offsets)
    bucket_ids = bucket_of(offsets)
    one_hot = (bucket_ids[:, None] == jnp.arange(BUCKETS)[None, :]).astype(wide)
    my_bias = jnp.where(half == 0, rel_bias[:, 0], rel_bias[:, 1])
    bias_line = jnp.sum(one_hot * my_bias[None, :], axis=1)
    bias = bias_table(jnp.broadcast_to(bias_line[None, :], (8, WIDE)))
    segs = jnp.broadcast_to(jnp.repeat(seg_starts[:, 0], 2)[:, None, None], (4, 1, 128))
    segs = swap_seq(segs)[:, 0, 0]
    scal = jnp.concatenate([lax.dynamic_slice_in_dim(lengths, mine, 1, 0), segs])

    inputs_wide = inputs.astype(wide)
    tokens_low = gather_rows(to_low(layer_norm(inputs_wide, attn_gain)))
    w_qkv = jnp.stack(
        [w.reshape(D, 2, 128) for w in (w_query, w_key, w_value)], axis=2
    ).reshape(D, 2, 384)
    qkv_native = to_low(
        jnp.einsum("sqd,dhe->shqe", tokens_low, w_qkv, preferred_element_type=wide)
    )
    qkv = swap_seq(qkv_native.reshape(4, BLOCK, 384))
    start_all = lax.all_gather(to_low(init_state), "tensor", axis=0, tiled=True)
    w_sout_all = lax.all_gather(w_sout, "tensor", axis=0, tiled=True)
    plane = ("dp", "seq")
    spot = 4 * lax.axis_index("dp") + place
    ff_own = w_up.shape[1] // 8
    ff_slices = jnp.concatenate(
        [
            lax.dynamic_slice_in_dim(w_up, spot * ff_own, ff_own, 1).T,
            lax.dynamic_slice_in_dim(w_down, spot * ff_own, ff_own, 0),
        ],
        axis=0,
    )
    w_back_own = jnp.concatenate(
        [w.T.reshape(2, 128, D) for w in (w_squery, w_key, w_value)], axis=1
    )
    w_sout_all, w_out_own, ff_slices, cot_own, w_back_own = lax.optimization_barrier(
        (w_sout_all, w_out, ff_slices, out_cot, w_back_own)
    )
    w_out_all = lax.all_gather(w_out_own, "tensor", axis=0, tiled=True)
    ff_all = lax.all_gather(ff_slices, "tensor", axis=0, tiled=True).reshape(4, 2, ff_own, D)
    up_rows = ff_all[:, 0].reshape(4 * ff_own, D)
    down_rows = ff_all[:, 1].reshape(4 * ff_own, D)
    cot_used = lax.all_gather(cot_own.reshape(256, D), plane, axis=0, tiled=True)
    w_back = lax.all_gather(w_back_own, "tensor", axis=0, tiled=True)
    w_state = jnp.concatenate([head_of(w_squery), head_of(w_key), head_of(w_value)], axis=1)
    mixed, lse_tok, state_rows, state_low, qkvst, lse_st, os_rows = forward_chain(
        scal, qkv, start_all, w_state, w_sout_all, vecs, bias
    )
    other_block = lax.rem(place + 2, 4)
    sent = lax.dynamic_slice_in_dim(state_rows, other_block, 1, 0)[0].astype(low)
    came = lax.ppermute(sent, "seq", [(source, (source + 2) % 4) for source in range(4)])
    kept = lax.dynamic_slice_in_dim(state_rows, place, 1, 0)[0]
    state_out = jnp.where(
        mine == 0, jnp.stack([kept, came.astype(wide)]), jnp.stack([came.astype(wide), kept])
    )

    hidden_in, mixed_rows, mid_all = middle_forward(mixed, inputs, w_out_all, vecs)
    mid_low = mid_all.reshape(2048, D)
    pre_act = matmul_t(mid_low, up_rows)
    hidden_low = to_low(jax.nn.gelu(pre_act))
    mlp_part = to_low(matmul(hidden_low, down_rows))
    grad_hidden_act = matmul_t(cot_used, down_rows)
    grad_pre = to_low(gelu_back(pre_act, grad_hidden_act))
    d_mid_part = to_low(matmul(grad_pre, up_rows))
    grad_hidden, grad_low, d_mixed, mlp_sums = middle_backward(
        d_mid_part.reshape(8, 256, D), hidden_in, out_cot, w_out_all, vecs
    )
    mlp_rows = lax.psum_scatter(mlp_part, plane, scatter_dimension=0, tiled=True)
    tokens_out = (hidden_in + mlp_rows.reshape(2, 128, D).astype(wide)).astype(low)
    ff_grads = jnp.stack(
        [
            outer_sum(grad_pre, mid_low).astype(low).reshape(4, ff_own, D),
            outer_sum(hidden_low, cot_used).astype(low).reshape(4, ff_own, D),
        ],
        axis=1,
    )
    ff_sum = lax.psum_scatter(
        ff_grads.reshape(8 * ff_own, D), "tensor", scatter_dimension=0, tiled=True
    )
    ff_total = lax.all_gather(ff_sum, plane, axis=0, tiled=True).reshape(8, 2, ff_own, D)
    up_grad = ff_total[:, 0].reshape(8 * ff_own, D).T.astype(wide)
    down_grad = ff_total[:, 1].reshape(8 * ff_own, D).astype(wide)
    out_part = lax.psum_scatter(
        outer_sum(mixed_rows, grad_low).astype(low), "tensor", scatter_dimension=0, tiled=True
    )

    cots = swap_seq(state_cot.reshape(4, 64, D))
    start_half = lax.dynamic_slice_in_dim(to_low(init_state).astype(wide), half * 64, 64, 0)
    states = jnp.concatenate(
        [start_half[None], lax.dynamic_slice_in_dim(state_rows, half * 64, 64, 1)], axis=0
    )
    d_qkv, d_qkvst, du_rows, d_start, sums, dz_sum = backward_chain(
        scal, qkv, d_mixed, lse_tok, qkvst, lse_st, states, cots, w_back, w_sout_all, vecs, bias
    )
    diag = diagonal_sums(dz_sum)[0]
    bias_grad = own_half(
        jnp.sum(one_hot * diag[:, None], axis=0)[:, None], half, 1
    )
    d_native = swap_seq(d_qkv).reshape(2, 2, BLOCK, 384)
    grad_tokens = sum_rows(
        jnp.einsum("shqe,dhe->sqd", d_native, w_qkv, preferred_element_type=wide)
    )
    grad_in_norm, attn_gain_grad = norm_back(inputs_wide, attn_gain, grad_tokens)
    inputs_grad = grad_hidden + grad_in_norm
    tok_grads = jnp.einsum("sqd,shqe->dhe", tokens_low, d_native, preferred_element_type=wide)
    st_grads = outer_sum(state_low, d_qkvst)
    query_grad = tok_grads[:, :, 0:128].reshape(D, 256)
    key_grad = tok_grads[:, :, 128:256].reshape(D, 256) + own_half(st_grads[:, 128:256], half, 1)
    value_grad = tok_grads[:, :, 256:384].reshape(D, 256) + own_half(st_grads[:, 256:384], half, 1)
    squery_grad = own_half(st_grads[:, 0:128], half, 1)
    sout_part = lax.psum_scatter(
        outer_sum(os_rows, du_rows).astype(low), "tensor", scatter_dimension=0, tiled=True
    )
    state_part = own_half(d_start, half, 0)
    gains = lax.psum(jnp.stack([attn_gain_grad, sums[1], mlp_sums[0], sums[0]]), "tensor")

    def total(part):
        return lax.psum(part.astype(low), ("dp", "seq")).astype(wide)

    gain_total = total(gains)
    return (
        tokens_out,
        state_out[:, None],
        inputs_grad,
        total(state_part),
        gain_total[0],
        gain_total[1],
        gain_total[2],
        total(query_grad),
        total(key_grad),
        total(value_grad),
        total(out_part),
        total(squery_grad),
        total(sout_part),
        up_grad,
        down_grad,
        total(bias_grad),
        gain_total[3],
    )


def solution(mesh):
    return jax.shard_map(
        chosen_body(mesh),
        mesh=mesh,
        in_specs=(
            P("dp", ("seq", "tensor"), None),
            P("dp", "seq"),
            P("dp"),
            P("tensor", None),
            P(),
            P(),
            P(),
            P(None, "tensor"),
            P(None, "tensor"),
            P(None, "tensor"),
            P("tensor", None),
            P(None, "tensor"),
            P("tensor", None),
            P(None, "tensor"),
            P("tensor", None),
            P(None, "tensor"),
            P(),
            P("dp", ("seq", "tensor"), None),
            P("dp", "seq", "tensor", None),
        ),
        out_specs=(
            P("dp", ("seq", "tensor"), None),
            P("dp", "seq", "tensor", None),
            P("dp", ("seq", "tensor"), None),
            P("tensor", None),
            P(),
            P(),
            P(),
            P(None, "tensor"),
            P(None, "tensor"),
            P(None, "tensor"),
            P("tensor", None),
            P(None, "tensor"),
            P("tensor", None),
            P(None, "tensor"),
            P("tensor", None),
            P(None, "tensor"),
            P(),
        ),
        check_vma=False,
    )
```

```python
import jax
import jax.numpy as jnp
from jax import lax
from jax.experimental import pallas as pl
from jax.experimental.pallas import tpu as pltpu
from jax.sharding import PartitionSpec as P

D = 1024
HEAD_DIM = 128
STATES = 512
BLOCK = 512
SEG = 256
BUCKETS = 32


norm_eps = 1e-06
masked_score = -1e30
bucket_edges = (12, 16, 23, 32, 46, 64, 91)


def passed_along(value, axis, steps):
    count = lax.axis_size(axis)
    leading, last = (max(0, -steps), min(count, count - steps))
    return lax.ppermute(value, axis, [(source, source + steps) for source in range(leading, last)])


def bucket_of(relative):
    distance = jnp.abs(relative)
    far_bucket = 8 + sum(((distance >= boundary).astype(jnp.int32) for boundary in bucket_edges))
    near_far = jnp.where(distance < 8, distance, far_bucket)
    return near_far + 16 * (relative > 0).astype(jnp.int32)


def token_mask(seg_start, seq_length, block_index):
    positions = jnp.arange(BLOCK)
    offset = block_index * BLOCK
    prev_valid = (block_index > 0) & (offset - BLOCK + positions < seq_length)
    cur_valid = offset + positions < seq_length
    inside = (positions >= seg_start) & (positions < seg_start + SEG)
    prev_mask = (positions[None, :] > positions[:, None]) & prev_valid[None, :]
    cur_mask = (
        (positions[None, :] <= positions[:, None]) | inside[None, :] & inside[:, None]
    ) & cur_valid[None, :]
    state_mask = jnp.ones((BLOCK, STATES), jnp.bool_)
    return jnp.concatenate([prev_mask, cur_mask, state_mask], axis=1)


def state_mask_of(valid_blk):
    batch_count = valid_blk.shape[0]
    block_part = jnp.broadcast_to(valid_blk[:, None, :], (batch_count, STATES, BLOCK))
    return jnp.concatenate([block_part, jnp.ones((batch_count, STATES, STATES), jnp.bool_)], axis=2)


def layer_norm(values, gain_vec):
    centered = values - jnp.mean(values, axis=-1, keepdims=True)
    spread = jnp.mean(centered * centered, axis=-1, keepdims=True)
    return centered * lax.rsqrt(spread + norm_eps) * gain_vec


def norm_back(values, gain_vec, grad_out):
    _, pullback = jax.vjp(layer_norm, values, gain_vec)
    return pullback(grad_out)


def gelu_back(pre_act, grad_out):
    _, pullback = jax.vjp(jax.nn.gelu, pre_act)
    return pullback(grad_out)[0]


def to_low(array_in):
    return array_in.astype(jnp.bfloat16)


def matmul(left, right):
    return jnp.einsum("...k,kn->...n", left, right, preferred_element_type=jnp.float32)


def matmul_t(left, right):
    return jnp.einsum("...n,kn->...k", left, right, preferred_element_type=jnp.float32)


def outer_sum(left, right):
    left_flat = left.reshape(-1, left.shape[-1])
    right_flat = right.reshape(-1, right.shape[-1])
    return lax.dot_general(
        left_flat, right_flat, (((0,), (0,)), ((), ())), preferred_element_type=jnp.float32
    )


def gather_rows(values):
    return lax.all_gather(values, "tensor", axis=1, tiled=True)


def sum_rows(terms):
    return lax.psum_scatter(
        terms.astype(jnp.bfloat16), "tensor", scatter_dimension=1, tiled=True
    ).astype(jnp.float32)


def pass_state(rows_now):
    return passed_along(rows_now.astype(jnp.bfloat16), "seq", 1).astype(rows_now.dtype)


def pass_back(grad_now):
    return passed_along(grad_now.astype(jnp.bfloat16), "seq", -1).astype(grad_now.dtype)


def split_heads(rows_in):
    return rows_in.reshape(rows_in.shape[0], rows_in.shape[1] // HEAD_DIM, HEAD_DIM)


def score_block(query_rows, key_all, bias_all, allowed):
    scores = (
        jnp.einsum(
            "qhd,khd->hqk",
            split_heads(query_rows),
            split_heads(key_all),
            preferred_element_type=jnp.float32,
        )
        * HEAD_DIM ** (-0.5)
        + bias_all
    )
    return jnp.where(allowed[None], scores, masked_score)


def attend_forward(query_rows, key_all, value_all, bias_all, allowed):
    scores = score_block(query_rows, key_all, bias_all, allowed)
    row_max = jnp.max(scores, axis=-1, keepdims=True)
    exp_scores = jnp.exp(scores - row_max)
    row_total = jnp.sum(exp_scores, axis=-1, keepdims=True)
    weight_all = to_low(exp_scores / row_total)
    mixed_out = jnp.einsum(
        "hqk,khd->qhd", weight_all, split_heads(value_all), preferred_element_type=jnp.float32
    )
    return (
        to_low(mixed_out.reshape(query_rows.shape[0], -1)),
        (row_max + jnp.log(row_total))[..., 0],
    )


def attend_back(query_rows, key_all, value_all, bias_all, allowed, log_total, grad_mixed):
    scores = score_block(query_rows, key_all, bias_all, allowed)
    weight_all = jnp.where(allowed[None], jnp.exp(scores - log_total[..., None]), 0.0)
    grad_heads = split_heads(grad_mixed)
    grad_weight = jnp.einsum(
        "qhd,khd->hqk", grad_heads, split_heads(value_all), preferred_element_type=jnp.float32
    )
    row_inner = jnp.sum(weight_all * grad_weight, axis=-1, keepdims=True)
    grad_scores = to_low(weight_all * (grad_weight - row_inner))
    grad_query = jnp.einsum(
        "hqk,khd->qhd", grad_scores, split_heads(key_all), preferred_element_type=jnp.float32
    ) * HEAD_DIM ** (-0.5)
    grad_keys = jnp.einsum(
        "hqk,qhd->khd", grad_scores, split_heads(query_rows), preferred_element_type=jnp.float32
    ) * HEAD_DIM ** (-0.5)
    grad_values = jnp.einsum(
        "hqk,qhd->khd", to_low(weight_all), grad_heads, preferred_element_type=jnp.float32
    )
    return (
        grad_query.reshape(query_rows.shape[0], -1),
        grad_keys.reshape(key_all.shape[0], -1),
        grad_values.reshape(key_all.shape[0], -1),
        grad_scores,
    )


def bias_lookup(rel_bias, rel_table):
    table_heads = jnp.zeros((rel_bias.shape[1],) + rel_table.shape, jnp.float32)
    for bucket_id in range(BUCKETS):
        table_heads = table_heads + jnp.where(
            rel_table[None] == bucket_id, rel_bias[bucket_id][:, None, None], 0.0
        )
    return table_heads


def bias_sums(score_grad, rel_table):
    grad_wide = score_grad.astype(jnp.float32)
    columns = []
    for bucket_id in range(BUCKETS):
        columns.append(
            jnp.sum(jnp.where(rel_table[None, None] == bucket_id, grad_wide, 0.0), axis=(0, 2, 3))
        )
    return jnp.stack(columns, axis=0)


def body(
    inputs,
    seg_starts,
    lengths,
    init_state,
    attn_gain,
    state_gain,
    mlp_gain,
    w_query,
    w_key,
    w_value,
    w_out,
    w_squery,
    w_sout,
    w_up,
    w_down,
    rel_bias,
    gate_bias,
    out_cot,
    state_cot,
):
    seq_count = inputs.shape[0]
    chain_length = lax.axis_size("seq")
    block_index = lax.axis_index("seq")
    is_first = block_index == 0
    width_local = w_query.shape[1]
    head_count = width_local // HEAD_DIM
    gate_value = jax.nn.sigmoid(gate_bias)
    positions = jnp.arange(BLOCK)
    inputs_wide = inputs.astype(jnp.float32)
    tokens_low = gather_rows(to_low(layer_norm(inputs_wide, attn_gain)))
    query_tok = to_low(matmul(tokens_low, w_query))
    key_tok = to_low(matmul(tokens_low, w_key))
    value_tok = to_low(matmul(tokens_low, w_value))
    key_prev, value_prev = passed_along((key_tok, value_tok), "seq", 1)
    valid_keys = (block_index * BLOCK + positions)[None, :] < lengths[:, None]
    batched_attend = jax.vmap(attend_forward, in_axes=(0, 0, 0, None, 0))
    batched_back = jax.vmap(attend_back, in_axes=(0, 0, 0, None, 0, 0, 0))

    def state_forward(state_rows, key_blk, value_blk, valid_blk):
        state_low = lax.all_gather(
            to_low(layer_norm(state_rows, state_gain)), "tensor", axis=1, tiled=True
        )
        query_st = to_low(matmul(state_low, w_squery))
        key_st = to_low(matmul(state_low, w_key))
        value_st = to_low(matmul(state_low, w_value))
        key_all = jnp.concatenate([key_blk, key_st], axis=1)
        value_all = jnp.concatenate([value_blk, value_st], axis=1)
        mixed_st, lse_st = batched_attend(
            query_st, key_all, value_all, 0.0, state_mask_of(valid_blk)
        )
        update = lax.psum_scatter(
            matmul(mixed_st, w_sout).astype(jnp.bfloat16), "tensor", scatter_dimension=1, tiled=True
        ).astype(jnp.float32)
        state_next = gate_value * state_rows + (1.0 - gate_value) * update
        return (state_next, (state_low, query_st, key_st, value_st, mixed_st, lse_st, update))

    def state_backward(
        grad_out, state_rows, kept_one, key_blk, value_blk, valid_blk, extra_key, extra_value
    ):
        state_low, query_st, key_st, value_st, mixed_st, lse_st, update = kept_one
        gate_part = (
            jnp.sum(grad_out * (state_rows - update), axis=(0, 1)) * gate_value * (1.0 - gate_value)
        )
        grad_update = lax.all_gather(
            to_low((1.0 - gate_value) * grad_out), "tensor", axis=1, tiled=True
        )
        grad_mixed_st = to_low(matmul_t(grad_update, w_sout))
        sout_part = outer_sum(mixed_st, grad_update)
        key_all = jnp.concatenate([key_blk, key_st], axis=1)
        value_all = jnp.concatenate([value_blk, value_st], axis=1)
        grad_query_st, grad_keys_st, grad_values_st, _ = batched_back(
            query_st, key_all, value_all, 0.0, state_mask_of(valid_blk), lse_st, grad_mixed_st
        )
        query_low = to_low(grad_query_st)
        key_low = to_low(grad_keys_st[:, BLOCK:] + extra_key)
        value_low = to_low(grad_values_st[:, BLOCK:] + extra_value)
        squery_part = outer_sum(state_low, query_low)
        key_part = outer_sum(state_low, key_low)
        value_part = outer_sum(state_low, value_low)
        terms = (
            matmul_t(query_low, w_squery) + matmul_t(key_low, w_key) + matmul_t(value_low, w_value)
        )
        grad_normed = lax.psum_scatter(
            terms.astype(jnp.bfloat16), "tensor", scatter_dimension=1, tiled=True
        ).astype(jnp.float32)
        grad_rows_norm, gain_part = norm_back(state_rows, state_gain, grad_normed)
        grad_in = gate_value * grad_out + grad_rows_norm
        block_grads = (grad_keys_st[:, :BLOCK], grad_values_st[:, :BLOCK])
        return (
            grad_in,
            block_grads,
            (squery_part, key_part, value_part, sout_part, gain_part, gate_part),
        )

    zeros_rows = jnp.zeros((seq_count,) + init_state.shape, jnp.float32)
    narrow_zero = jnp.zeros((seq_count, STATES, width_local), jnp.bfloat16)
    stored_start = (
        zeros_rows,
        zeros_rows,
        jnp.zeros((seq_count, STATES, D), jnp.bfloat16),
        narrow_zero,
        narrow_zero,
        narrow_zero,
        narrow_zero,
        jnp.zeros((seq_count, head_count, STATES), jnp.float32),
        zeros_rows,
    )

    def forward_turn(turn_index, carry):
        incoming, stored_now = carry
        order_index = turn_index - block_index
        is_live = (order_index >= 0) & (order_index < seq_count)
        picked = jnp.clip(order_index, 0, seq_count - 1)
        rows_now = jnp.where(is_first, init_state[None], incoming)
        key_one = lax.dynamic_slice_in_dim(key_tok, picked, 1, 0)
        value_one = lax.dynamic_slice_in_dim(value_tok, picked, 1, 0)
        valid_one = lax.dynamic_slice_in_dim(valid_keys, picked, 1, 0)
        rows_next, kept_one = state_forward(rows_now, key_one, value_one, valid_one)
        fresh = (rows_now, rows_next) + kept_one
        stored_now = tuple(
            (
                jnp.where(
                    is_live,
                    lax.dynamic_update_slice_in_dim(whole_array, fresh_part, picked, 0),
                    whole_array,
                )
                for whole_array, fresh_part in zip(stored_now, fresh)
            )
        )
        return (pass_state(rows_next), stored_now)

    incoming_start = jnp.zeros((1,) + init_state.shape, jnp.float32)
    _, stored_all = lax.fori_loop(
        0, chain_length + seq_count - 1, forward_turn, (incoming_start, stored_start)
    )
    state_in = stored_all[0]
    state_out = stored_all[1]
    kept = stored_all[2:]
    key_all_tok = jnp.concatenate([key_prev, key_tok, kept[2]], axis=1)
    value_all_tok = jnp.concatenate([value_prev, value_tok, kept[3]], axis=1)
    allowed_tok = jax.vmap(token_mask, in_axes=(0, 0, None))(seg_starts[:, 0], lengths, block_index)
    rel_table = bucket_of((jnp.arange(2 * BLOCK) - BLOCK)[None, :] - positions[:, None])
    full_bias = jnp.concatenate(
        [bias_lookup(rel_bias, rel_table), jnp.zeros((head_count, BLOCK, STATES), jnp.float32)],
        axis=2,
    )
    mixed_tok, lse_tok = batched_attend(
        query_tok, key_all_tok, value_all_tok, full_bias, allowed_tok
    )
    hidden_in = inputs_wide + sum_rows(matmul(mixed_tok, w_out))
    mid_low = gather_rows(to_low(layer_norm(hidden_in, mlp_gain)))
    pre_act = matmul(mid_low, w_up)
    hidden_low = to_low(jax.nn.gelu(pre_act))
    mlp_rows = sum_rows(matmul(hidden_low, w_down))
    tokens_out = (hidden_in + mlp_rows).astype(jnp.bfloat16)
    cot_wide = out_cot.astype(jnp.float32)
    cot_used = gather_rows(out_cot)
    grad_hidden_act = matmul_t(cot_used, w_down)
    down_grad = outer_sum(hidden_low, cot_used)
    grad_pre = to_low(gelu_back(pre_act, grad_hidden_act))
    up_grad = outer_sum(mid_low, grad_pre)
    grad_normed_mid = sum_rows(matmul_t(grad_pre, w_up))
    grad_mid_in, mlp_gain_grad = norm_back(hidden_in, mlp_gain, grad_normed_mid)
    grad_hidden = cot_wide + grad_mid_in
    grad_attn_low = gather_rows(to_low(grad_hidden))
    grad_mixed = to_low(matmul_t(grad_attn_low, w_out))
    out_grad = outer_sum(mixed_tok, grad_attn_low)
    grad_query_tok, grad_keys_tok, grad_values_tok, grad_scores = batched_back(
        query_tok, key_all_tok, value_all_tok, full_bias, allowed_tok, lse_tok, grad_mixed
    )
    bias_grad = bias_sums(grad_scores[..., : 2 * BLOCK], rel_table)
    grad_key_next, grad_value_next = (
        passed_along(grad_keys_tok[:, :BLOCK].astype(jnp.bfloat16), "seq", -1).astype(jnp.float32),
        passed_along(grad_values_tok[:, :BLOCK].astype(jnp.bfloat16), "seq", -1).astype(
            jnp.float32
        ),
    )
    grad_key_own = grad_keys_tok[:, BLOCK : 2 * BLOCK] + grad_key_next
    grad_value_own = grad_values_tok[:, BLOCK : 2 * BLOCK] + grad_value_next
    grad_key_st_tok = grad_keys_tok[:, 2 * BLOCK :]
    grad_value_st_tok = grad_values_tok[:, 2 * BLOCK :]
    cot_rows = state_cot[:, 0].astype(jnp.float32)
    wide_zero = jnp.zeros((seq_count, BLOCK, width_local), jnp.float32)
    stored_back = (zeros_rows, wide_zero, wide_zero)
    totals_start = (
        jnp.zeros((D, width_local), jnp.float32),
        jnp.zeros((D, width_local), jnp.float32),
        jnp.zeros((D, width_local), jnp.float32),
        jnp.zeros((width_local, D), jnp.float32),
        jnp.zeros((D,), jnp.float32),
        jnp.zeros((D,), jnp.float32),
    )

    def backward_turn(turn_index, carry):
        incoming, stored_now, totals_now = carry
        order_index = turn_index - (chain_length - 1 - block_index)
        is_live = (order_index >= 0) & (order_index < seq_count)
        picked = jnp.clip(order_index, 0, seq_count - 1)

        def slice_one(whole_array):
            return lax.dynamic_slice_in_dim(whole_array, picked, 1, 0)

        grad_out = slice_one(cot_rows) + incoming
        kept_one = tuple((slice_one(kept_array) for kept_array in kept))
        grad_in, block_one, parts_one = state_backward(
            grad_out,
            slice_one(state_in),
            kept_one,
            slice_one(key_tok),
            slice_one(value_tok),
            slice_one(valid_keys),
            slice_one(grad_key_st_tok),
            slice_one(grad_value_st_tok),
        )
        fresh = (grad_in,) + block_one
        stored_now = tuple(
            (
                jnp.where(
                    is_live,
                    lax.dynamic_update_slice_in_dim(whole_array, fresh_part, picked, 0),
                    whole_array,
                )
                for whole_array, fresh_part in zip(stored_now, fresh)
            )
        )
        totals_now = tuple(
            (
                total_now + jnp.where(is_live, part_now, 0.0)
                for total_now, part_now in zip(totals_now, parts_one)
            )
        )
        return (pass_back(grad_in), stored_now, totals_now)

    incoming_start = jnp.zeros((1,) + init_state.shape, jnp.float32)
    _, stored_done, weight_parts = lax.fori_loop(
        0, chain_length + seq_count - 1, backward_turn, (incoming_start, stored_back, totals_start)
    )
    grad_in_all, grad_key_blk, grad_value_blk = stored_done
    query_low = to_low(grad_query_tok)
    key_low = to_low(grad_key_own + grad_key_blk)
    value_low = to_low(grad_value_own + grad_value_blk)
    query_grad = outer_sum(tokens_low, query_low)
    key_grad = outer_sum(tokens_low, key_low) + weight_parts[1]
    value_grad = outer_sum(tokens_low, value_low) + weight_parts[2]
    grad_tokens = sum_rows(
        matmul_t(query_low, w_query) + matmul_t(key_low, w_key) + matmul_t(value_low, w_value)
    )
    grad_in_norm, attn_gain_grad = norm_back(inputs_wide, attn_gain, grad_tokens)
    inputs_grad = grad_hidden + grad_in_norm
    state_part = jnp.where(is_first, jnp.sum(grad_in_all, axis=0), 0.0)
    gains = lax.psum(
        jnp.stack([attn_gain_grad, weight_parts[4], mlp_gain_grad, weight_parts[5]]), "tensor"
    )
    totals = (
        lax.psum(query_grad.astype(jnp.bfloat16), ("dp", "seq")).astype(jnp.float32),
        lax.psum(key_grad.astype(jnp.bfloat16), ("dp", "seq")).astype(jnp.float32),
        lax.psum(value_grad.astype(jnp.bfloat16), ("dp", "seq")).astype(jnp.float32),
        lax.psum(out_grad.astype(jnp.bfloat16), ("dp", "seq")).astype(jnp.float32),
        lax.psum(weight_parts[0].astype(jnp.bfloat16), ("dp", "seq")).astype(jnp.float32),
        lax.psum(weight_parts[3].astype(jnp.bfloat16), ("dp", "seq")).astype(jnp.float32),
        lax.psum(up_grad.astype(jnp.bfloat16), ("dp", "seq")).astype(jnp.float32),
        lax.psum(down_grad.astype(jnp.bfloat16), ("dp", "seq")).astype(jnp.float32),
        lax.psum(bias_grad.astype(jnp.bfloat16), ("dp", "seq")).astype(jnp.float32),
        lax.psum(state_part.astype(jnp.bfloat16), ("dp", "seq")).astype(jnp.float32),
        lax.psum(gains.astype(jnp.bfloat16), ("dp", "seq")).astype(jnp.float32),
    )
    gain_total = totals[10]
    return (
        tokens_out,
        state_out[:, None],
        inputs_grad,
        totals[9],
        gain_total[0],
        gain_total[1],
        gain_total[2],
        totals[0],
        totals[1],
        totals[2],
        totals[3],
        totals[4],
        totals[5],
        totals[6],
        totals[7],
        totals[8],
        gain_total[3],
    )


def chosen_body(mesh):
    if mesh.shape["seq"] == 4 and mesh.shape["tensor"] == 4:
        return line_body
    return body


MESH_ID = pl.DeviceIdType.MESH
ROWS = 128
CHUNKS = BLOCK // ROWS
LINE = 8
SCALE = HEAD_DIM ** (-0.5)
VMEM_LIMIT = 60 * 1024 * 1024


def dot_nn(left, right):
    return lax.dot_general(left, right, (((1,), (0,)), ((), ())), preferred_element_type=jnp.float32)


def dot_nt(left, right):
    return lax.dot_general(left, right, (((1,), (1,)), ((), ())), preferred_element_type=jnp.float32)


def dot_tn(left, right):
    return lax.dot_general(left, right, (((0,), (0,)), ((), ())), preferred_element_type=jnp.float32)


def line_place():
    place = lax.axis_index("seq")
    half = lax.rem(place, 2)
    rank = lax.axis_index("tensor")
    return place, half, rank


def span(index, size):
    return pl.ds(pl.multiple_of(index * size, size), size)


def norm_parts(rows):
    centered = rows - jnp.mean(rows, axis=-1, keepdims=True)
    spread = jnp.mean(centered * centered, axis=-1, keepdims=True)
    return centered, lax.rsqrt(spread + norm_eps)


def token_masks(scal, block_id, first_row):
    length = scal[0]
    start = scal[1 + block_id]
    row = lax.broadcasted_iota(jnp.int32, (ROWS, BLOCK), 0) + first_row
    col = lax.broadcasted_iota(jnp.int32, (ROWS, BLOCK), 1)
    prev_limit = jnp.where(block_id > 0, length - (block_id - 1) * BLOCK, 0)
    prev_ok = (col > row) & (col < prev_limit)
    row_in = (row >= start) & (row < start + SEG)
    col_in = (col >= start) & (col < start + SEG)
    cur_ok = ((col <= row) | (row_in & col_in)) & (col < length - block_id * BLOCK)
    return prev_ok, cur_ok


def state_block_mask(scal, block_id):
    col = lax.broadcasted_iota(jnp.int32, (ROWS, BLOCK), 1)
    return col < scal[0] - block_id * BLOCK


def softmax_of(score_parts):
    top = jnp.max(score_parts[0], axis=-1, keepdims=True)
    for part in score_parts[1:]:
        top = jnp.maximum(top, jnp.max(part, axis=-1, keepdims=True))
    raised = [jnp.exp(part - top) for part in score_parts]
    total = jnp.sum(raised[0], axis=-1, keepdims=True)
    for part in raised[1:]:
        total = total + jnp.sum(part, axis=-1, keepdims=True)
    inverse = 1.0 / total
    return [to_low(part * inverse) for part in raised], top + jnp.log(total)


def token_scores(scal, qkv, qkvst, bias, block_id, chunk):
    rows = span(chunk, ROWS)
    prev_id = jnp.maximum(block_id - 1, 0)
    query = qkv[block_id, rows, 0:128]
    prev_ok, cur_ok = token_masks(scal, block_id, chunk * ROWS)
    prev = dot_nt(query, qkv[prev_id, :, 128:256]) * SCALE + bias[rows, 0:BLOCK]
    cur = dot_nt(query, qkv[block_id, :, 128:256]) * SCALE + bias[rows, BLOCK : 2 * BLOCK]
    stt = dot_nt(query, qkvst[block_id, :, 128:256]) * SCALE
    prev = jnp.where(prev_ok, prev, masked_score)
    cur = jnp.where(cur_ok, cur, masked_score)
    return query, (prev, cur, stt)


def state_scores(scal, qkv, qkvst, block_id, chunk):
    query = qkvst[block_id, span(chunk, ROWS), 0:128]
    tok = dot_nt(query, qkv[block_id, :, 128:256]) * SCALE
    tok = jnp.where(state_block_mask(scal, block_id), tok, masked_score)
    stt = dot_nt(query, qkvst[block_id, :, 128:256]) * SCALE
    return query, (tok, stt)


def forward_kernel(
    scal, qkv, start, w_state, w_sout, vecs, bias,
    o_out, lse_out, state_rows, state_low, qkvst, lse_st, os_rows,
    held, os_all, send_sem, pass_sem, recv_sem,
):
    place, half, rank = line_place()
    partner = place + 1 - 2 * half
    head = 2 * rank + half
    peers = [lax.rem(rank + step, 4) for step in (1, 2, 3)]
    barrier = pltpu.get_barrier_semaphore()
    for peer in peers:
        pl.semaphore_signal(
            barrier, inc=1, device_id={"seq": place, "tensor": peer}, device_id_type=MESH_ID
        )
    pl.semaphore_signal(
        barrier, inc=1, device_id={"seq": partner, "tensor": rank}, device_id_type=MESH_ID
    )
    held[...] = start[...].astype(jnp.float32)
    gain = vecs[0:1, :]
    gate = vecs[1:2, :]
    pl.semaphore_wait(barrier, 4)

    def carry_copy(block_id, which, sem, seq_to, rank_to):
        part = os_all.at[block_id, :, span(which, 128)]
        return pltpu.make_async_remote_copy(
            src_ref=part,
            dst_ref=part,
            send_sem=sem,
            recv_sem=recv_sem.at[block_id, which],
            device_id={"seq": seq_to, "tensor": rank_to},
            device_id_type=MESH_ID,
        )

    def one_block(block_id, _):
        def project(chunk, _):
            rows = span(chunk, ROWS)
            centered, scale = norm_parts(held[rows, :])
            low = to_low(centered * scale * gain)
            state_low[block_id, rows, :] = low
            qkvst[block_id, rows, :] = to_low(dot_nn(low, w_state[...]))
            return 0

        lax.fori_loop(0, CHUNKS, project, 0)

        def attend_state(chunk, _):
            rows = span(chunk, ROWS)
            _, parts = state_scores(scal, qkv, qkvst, block_id, chunk)
            (w_tok, w_stt), total = softmax_of(parts)
            mixed = dot_nn(w_tok, qkv[block_id, :, 256:384]) + dot_nn(
                w_stt, qkvst[block_id, :, 256:384]
            )
            os_all[block_id, rows, span(head, 128)] = to_low(mixed)
            lse_st[block_id, rows, :] = total
            return 0

        lax.fori_loop(0, CHUNKS, attend_state, 0)
        for slot, peer in enumerate(peers):
            carry_copy(block_id, head, send_sem.at[block_id, slot], place, peer).start()
        carry_copy(block_id, head, send_sem.at[block_id, 3], partner, rank).start()

        def attend_token(chunk, _):
            rows = span(chunk, ROWS)
            _, parts = token_scores(scal, qkv, qkvst, bias, block_id, chunk)
            weights, total = softmax_of(parts)
            prev_id = jnp.maximum(block_id - 1, 0)
            mixed = (
                dot_nn(weights[0], qkv[prev_id, :, 256:384])
                + dot_nn(weights[1], qkv[block_id, :, 256:384])
                + dot_nn(weights[2], qkvst[block_id, :, 256:384])
            )
            o_out[block_id, rows, :] = to_low(mixed)
            lse_out[block_id, rows, :] = total
            return 0

        lax.fori_loop(0, CHUNKS, attend_token, 0)
        for slot, peer in enumerate(peers):
            other = 2 * peer + half
            carry_copy(block_id, other, send_sem.at[block_id, slot], place, peer).wait_recv()
            carry_copy(block_id, other, pass_sem.at[block_id, slot], partner, rank).start()
        for other_rank in range(4):
            carry_copy(
                block_id, 2 * other_rank + 1 - half, send_sem.at[block_id, 3], partner, rank
            ).wait_recv()

        def update(chunk, _):
            rows = span(chunk, ROWS)
            change = dot_nn(os_all[block_id, rows, :], w_sout[...])
            held[rows, :] = gate * held[rows, :] + (1.0 - gate) * change
            return 0

        lax.fori_loop(0, CHUNKS, update, 0)
        state_rows[block_id] = held[span(rank, 128), :]
        os_rows[block_id] = os_all[block_id, span(head, 64), :]
        return 0

    lax.fori_loop(0, 4, one_block, 0)

    def drain(block_id, _):
        for slot, peer in enumerate(peers):
            carry_copy(block_id, head, send_sem.at[block_id, slot], place, peer).wait_send()
            other = 2 * peer + half
            carry_copy(block_id, other, pass_sem.at[block_id, slot], partner, rank).wait_send()
        carry_copy(block_id, head, send_sem.at[block_id, 3], partner, rank).wait_send()
        return 0

    lax.fori_loop(0, 4, drain, 0)


def vmem_specs(count):
    return [pl.BlockSpec(memory_space=pltpu.VMEM)] * count


def forward_chain(scal, qkv, start, w_state, w_sout, vecs, bias):
    low, wide = jnp.bfloat16, jnp.float32
    shapes = (
        ((4, BLOCK, 128), low),
        ((4, BLOCK, 1), wide),
        ((4, 128, D), wide),
        ((4, STATES, D), low),
        ((4, STATES, 384), low),
        ((4, STATES, 1), wide),
        ((4, 64, D), low),
    )
    return pl.pallas_call(
        forward_kernel,
        out_shape=[jax.ShapeDtypeStruct(*one) for one in shapes],
        in_specs=[pl.BlockSpec(memory_space=pltpu.SMEM)] + vmem_specs(6),
        out_specs=vmem_specs(7),
        scratch_shapes=[
            pltpu.VMEM((STATES, D), wide),
            pltpu.VMEM((4, STATES, D), low),
            pltpu.SemaphoreType.DMA((4, 4)),
            pltpu.SemaphoreType.DMA((4, 3)),
            pltpu.SemaphoreType.DMA((4, 8)),
        ],
        compiler_params=pltpu.CompilerParams(
            collective_id=1, has_side_effects=True, vmem_limit_bytes=VMEM_LIMIT
        ),
        cost_estimate=pl.CostEstimate(flops=20000000000, bytes_accessed=20000000, transcendentals=0),
        name="forward_chain",
    )(scal, qkv, start, w_state, w_sout, vecs, bias)


def backward_kernel(
    scal, qkv, d_o, lse_tok, qkvst, lse_st, states, cots, w_back, w_sout, vecs, bias,
    d_qkv, d_qkvst, du_rows, d_start, sums, dz_sum,
    key_acc, value_acc, st_key, st_value, dos_rows, dos_got, d_got, grad_in,
    send_sem, recv_sem,
):
    place, half, rank = line_place()
    head = 2 * rank + half
    peers = []
    for step in range(1, LINE):
        other = lax.rem(head + step, LINE)
        peers.append((other, place - half + lax.rem(other, 2), other // 2))
    barrier = pltpu.get_barrier_semaphore()
    for _, seq_to, rank_to in peers:
        pl.semaphore_signal(
            barrier, inc=1, device_id={"seq": seq_to, "tensor": rank_to}, device_id_type=MESH_ID
        )
    gain = vecs[0:1, :]
    gate = vecs[1:2, :]
    key_acc[...] = jnp.zeros_like(key_acc)
    value_acc[...] = jnp.zeros_like(value_acc)
    dz_sum[...] = jnp.zeros_like(dz_sum)
    sums[...] = jnp.zeros_like(sums)
    grad_in[...] = jnp.zeros_like(grad_in)

    def back_parts(parts, total, grad, values):
        weights = [jnp.exp(part - total) for part in parts]
        d_weights = [dot_nt(grad, value) for value in values]
        inner = jnp.sum(weights[0] * d_weights[0], axis=-1, keepdims=True)
        for one, other in zip(weights[1:], d_weights[1:]):
            inner = inner + jnp.sum(one * other, axis=-1, keepdims=True)
        d_scores = [to_low(one * (other - inner)) for one, other in zip(weights, d_weights)]
        return [to_low(one) for one in weights], d_scores

    def token_back(block_id):
        prev_id = jnp.maximum(block_id - 1, 0)
        st_key[...] = jnp.zeros_like(st_key)
        st_value[...] = jnp.zeros_like(st_value)

        def one_chunk(chunk, _):
            rows = span(chunk, ROWS)
            query, parts = token_scores(scal, qkv, qkvst, bias, block_id, chunk)
            grad = d_o[block_id, rows, :]
            keys = (qkv[prev_id, :, 128:256], qkv[block_id, :, 128:256], qkvst[block_id, :, 128:256])
            values = (
                qkv[prev_id, :, 256:384], qkv[block_id, :, 256:384], qkvst[block_id, :, 256:384]
            )
            weights, d_scores = back_parts(parts, lse_tok[block_id, rows, :], grad, values)
            d_query = dot_nn(d_scores[0], keys[0])
            d_query = d_query + dot_nn(d_scores[1], keys[1]) + dot_nn(d_scores[2], keys[2])
            d_qkv[block_id, rows, 0:128] = to_low(d_query * SCALE)
            key_acc[prev_id] += dot_tn(d_scores[0], query) * SCALE
            value_acc[prev_id] += dot_tn(weights[0], grad)
            key_acc[block_id] += dot_tn(d_scores[1], query) * SCALE
            value_acc[block_id] += dot_tn(weights[1], grad)
            st_key[...] += dot_tn(d_scores[2], query) * SCALE
            st_value[...] += dot_tn(weights[2], grad)
            dz_sum[rows, 0:BLOCK] += d_scores[0].astype(jnp.float32)
            dz_sum[rows, BLOCK : 2 * BLOCK] += d_scores[1].astype(jnp.float32)
            return 0

        lax.fori_loop(0, CHUNKS, one_chunk, 0)

    token_back(3)
    pl.semaphore_wait(barrier, LINE - 1)

    def mixed_copy(block_id, slot, sender, other, seq_to, rank_to):
        return pltpu.make_async_remote_copy(
            src_ref=dos_rows.at[block_id, :, span(other, 128)],
            dst_ref=dos_got.at[block_id, span(sender, 64), :],
            send_sem=send_sem.at[0, block_id, slot],
            recv_sem=recv_sem.at[0, block_id, sender],
            device_id={"seq": seq_to, "tensor": rank_to},
            device_id_type=MESH_ID,
        )

    def grads_copy(block_id, slot, sender, other, seq_to, rank_to):
        return pltpu.make_async_remote_copy(
            src_ref=d_qkvst.at[block_id, span(other, 64), :],
            dst_ref=d_got.at[block_id, sender],
            send_sem=send_sem.at[1, block_id, slot],
            recv_sem=recv_sem.at[1, block_id, sender],
            device_id={"seq": seq_to, "tensor": rank_to},
            device_id_type=MESH_ID,
        )

    def one_block(turn, _):
        block_id = 3 - turn
        grad_out = grad_in[...] + cots[block_id].astype(jnp.float32)
        sums[0:1, :] += jnp.sum(
            grad_out * (states[block_id] - states[block_id + 1]), axis=0, keepdims=True
        ) * gate
        change = to_low((1.0 - gate) * grad_out)
        du_rows[block_id] = change
        dos_rows[block_id] = to_low(dot_nt(change, w_sout[...]))
        for slot, (other, seq_to, rank_to) in enumerate(peers):
            mixed_copy(block_id, slot, head, other, seq_to, rank_to).start()
        dos_got[block_id, span(head, 64), :] = dos_rows[block_id, :, span(head, 128)]
        for slot, (other, seq_to, rank_to) in enumerate(peers):
            mixed_copy(block_id, slot, other, other, seq_to, rank_to).wait_recv()

        def one_chunk(chunk, _):
            rows = span(chunk, ROWS)
            query, parts = state_scores(scal, qkv, qkvst, block_id, chunk)
            grad = dos_got[block_id, rows, :]
            keys = (qkv[block_id, :, 128:256], qkvst[block_id, :, 128:256])
            values = (qkv[block_id, :, 256:384], qkvst[block_id, :, 256:384])
            weights, d_scores = back_parts(parts, lse_st[block_id, rows, :], grad, values)
            d_query = dot_nn(d_scores[0], keys[0]) + dot_nn(d_scores[1], keys[1])
            d_qkvst[block_id, rows, 0:128] = to_low(d_query * SCALE)
            key_acc[block_id] += dot_tn(d_scores[0], query) * SCALE
            value_acc[block_id] += dot_tn(weights[0], grad)
            st_key[...] += dot_tn(d_scores[1], query) * SCALE
            st_value[...] += dot_tn(weights[1], grad)
            return 0

        lax.fori_loop(0, CHUNKS, one_chunk, 0)
        d_qkvst[block_id, :, 128:256] = to_low(st_key[...])
        d_qkvst[block_id, :, 256:384] = to_low(st_value[...])
        for slot, (other, seq_to, rank_to) in enumerate(peers):
            grads_copy(block_id, slot, head, other, seq_to, rank_to).start()
        d_got[block_id, head] = d_qkvst[block_id, span(head, 64), :]

        @pl.when(turn < 3)
        def _():
            token_back(block_id - 1)

        d_qkv[block_id, :, 128:256] = to_low(key_acc[block_id])
        d_qkv[block_id, :, 256:384] = to_low(value_acc[block_id])
        for slot, (other, seq_to, rank_to) in enumerate(peers):
            grads_copy(block_id, slot, other, other, seq_to, rank_to).wait_recv()
        d_low = dot_nn(d_got[block_id, 0], w_back[0])
        for other in range(1, LINE):
            d_low = d_low + dot_nn(d_got[block_id, other], w_back[other])
        centered, scale = norm_parts(states[block_id])
        normed = centered * scale
        sums[1:2, :] += jnp.sum(d_low * normed, axis=0, keepdims=True)
        lifted = d_low * gain
        grad_in[...] = gate * grad_out + scale * (
            lifted
            - jnp.mean(lifted, axis=-1, keepdims=True)
            - normed * jnp.mean(lifted * normed, axis=-1, keepdims=True)
        )
        return 0

    lax.fori_loop(0, 4, one_block, 0)
    d_start[...] = grad_in[...]

    def drain(block_id, _):
        for slot, (other, seq_to, rank_to) in enumerate(peers):
            mixed_copy(block_id, slot, head, other, seq_to, rank_to).wait_send()
            grads_copy(block_id, slot, head, other, seq_to, rank_to).wait_send()
        return 0

    lax.fori_loop(0, 4, drain, 0)


def backward_chain(scal, qkv, d_o, lse_tok, qkvst, lse_st, states, cots, w_back, w_sout, vecs, bias):
    low, wide = jnp.bfloat16, jnp.float32
    shapes = (
        ((4, BLOCK, 384), low),
        ((4, STATES, 384), low),
        ((4, 64, D), low),
        ((64, D), wide),
        ((8, D), wide),
        ((BLOCK, 2 * BLOCK), wide),
    )
    return pl.pallas_call(
        backward_kernel,
        out_shape=[jax.ShapeDtypeStruct(*one) for one in shapes],
        in_specs=[pl.BlockSpec(memory_space=pltpu.SMEM)] + vmem_specs(11),
        out_specs=vmem_specs(6),
        scratch_shapes=[
            pltpu.VMEM((4, BLOCK, 128), wide),
            pltpu.VMEM((4, BLOCK, 128), wide),
            pltpu.VMEM((STATES, 128), wide),
            pltpu.VMEM((STATES, 128), wide),
            pltpu.VMEM((4, 64, D), low),
            pltpu.VMEM((4, STATES, 128), low),
            pltpu.VMEM((4, LINE, 64, 384), low),
            pltpu.VMEM((64, D), wide),
            pltpu.SemaphoreType.DMA((2, 4, LINE - 1)),
            pltpu.SemaphoreType.DMA((2, 4, LINE)),
        ],
        compiler_params=pltpu.CompilerParams(
            collective_id=2, has_side_effects=True, vmem_limit_bytes=VMEM_LIMIT
        ),
        cost_estimate=pl.CostEstimate(flops=40000000000, bytes_accessed=40000000, transcendentals=0),
        name="backward_chain",
    )(scal, qkv, d_o, lse_tok, qkvst, lse_st, states, cots, w_back, w_sout, vecs, bias)


def plane_place():
    place, half, rank = line_place()
    side = lax.axis_index("dp")
    return side, place, half, rank


def plane_index(side, place):
    return 4 * side + place


def plane_gather(buf, rows, send_sem, recv_sem):
    side, place, half, rank = plane_place()
    across, beside = 1 - side, lax.rem(place + 2, 4)
    core = place + 1 - 2 * half
    me = plane_index(side, place)
    at_x, at_y = plane_index(across, place), plane_index(side, beside)
    at_d = plane_index(across, beside)
    to_x = {"dp": across}
    to_y = {"seq": beside}
    to_c = {"seq": core}
    size = rows // 2

    def piece(owner, part, slot, target):
        view = buf.at[owner, pl.ds(part * size, size), :]
        return pltpu.make_async_remote_copy(
            src_ref=view,
            dst_ref=view,
            send_sem=send_sem.at[slot],
            recv_sem=recv_sem.at[owner, part],
            device_id=target,
            device_id_type=MESH_ID,
        )

    sent = []

    def send(owner, part, target):
        one = piece(owner, part, len(sent), target)
        sent.append(one)
        one.start()

    def arrived(owner, part):
        piece(owner, part, 0, to_c).wait_recv()

    send(me, 0, to_x)
    send(me, 1, to_y)
    send(me, 1, to_x)
    send(me, 0, to_y)
    send(me, 0, to_c)
    send(me, 1, to_c)
    yield
    arrived(at_x, 0)
    send(at_x, 0, to_y)
    arrived(at_y, 1)
    send(at_y, 1, to_x)
    send(at_x, 0, to_c)
    send(at_y, 1, to_c)
    yield
    arrived(at_x, 1)
    send(at_x, 1, to_c)
    arrived(at_y, 0)
    send(at_y, 0, to_c)
    yield
    arrived(at_d, 0)
    send(at_d, 0, to_c)
    arrived(at_d, 1)
    send(at_d, 1, to_c)
    yield
    for owner in (
        plane_index(side, core),
        plane_index(across, core),
        plane_index(side, lax.rem(core + 2, 4)),
        plane_index(across, lax.rem(core + 2, 4)),
    ):
        arrived(owner, 0)
        arrived(owner, 1)
    for one in sent:
        one.wait_send()


def run_all(*steps):
    waiting = list(steps)
    while waiting:
        for one in list(waiting):
            try:
                next(one)
            except StopIteration:
                waiting.remove(one)


def plane_scatter(part, core_got, near_got, far_got, total, rows, send_sem, recv_sem):
    side, place, half, rank = plane_place()
    across, beside = 1 - side, lax.rem(place + 2, 4)
    core = place + 1 - 2 * half
    me = plane_index(side, place)
    at_x, at_y = plane_index(across, place), plane_index(side, beside)
    at_d = plane_index(across, beside)
    size = rows // 2
    halves = (pl.ds(0, size), pl.ds(size, size))

    def moved(source, target_ref, slot, target):
        return pltpu.make_async_remote_copy(
            src_ref=source,
            dst_ref=target_ref,
            send_sem=send_sem.at[slot],
            recv_sem=recv_sem.at[slot],
            device_id=target,
            device_id_type=MESH_ID,
        )

    order = (at_d, at_x, at_y, me)
    swapped = (
        plane_index(across, lax.rem(core + 2, 4)),
        plane_index(across, core),
        plane_index(side, lax.rem(core + 2, 4)),
        plane_index(side, core),
    )
    first = [
        moved(part.at[owner], core_got.at[slot], slot, {"seq": core})
        for slot, owner in enumerate(swapped)
    ]
    for one in first:
        one.start()

    def add_into(owner, view, other):
        part[owner, view, :] = to_low(
            part[owner, view, :].astype(jnp.float32) + other.astype(jnp.float32)
        )

    near = [
        moved(part.at[at_d, halves[0], :], near_got.at[0], 4, {"dp": across}),
        moved(part.at[at_d, halves[1], :], near_got.at[1], 5, {"seq": beside}),
        moved(part.at[at_x, halves[0], :], near_got.at[2], 6, {"dp": across}),
        moved(part.at[at_y, halves[1], :], near_got.at[3], 7, {"seq": beside}),
    ]
    for slot, owner in enumerate(order):
        first[slot].wait_recv()
        for view in halves:
            add_into(owner, view, core_got[slot, view, :])
        if slot == 0:
            near[0].start()
            near[1].start()
        if slot == 1:
            near[2].start()
        if slot == 2:
            near[3].start()
    yield
    near[0].wait_recv()
    add_into(at_y, halves[0], near_got[0])
    far = [
        moved(part.at[at_y, halves[0], :], far_got.at[0], 8, {"seq": beside}),
        moved(part.at[at_x, halves[1], :], far_got.at[1], 9, {"dp": across}),
    ]
    far[0].start()
    near[1].wait_recv()
    add_into(at_x, halves[1], near_got[1])
    far[1].start()
    yield
    near[2].wait_recv()
    add_into(me, halves[0], near_got[2])
    near[3].wait_recv()
    add_into(me, halves[1], near_got[3])
    yield
    for slot, view in enumerate(halves):
        far[slot].wait_recv()
        total[view, :] = part[me, view, :].astype(jnp.float32) + far_got[slot].astype(jnp.float32)
    for one in first + near + far:
        one.wait_send()


def group_peers():
    place, half, rank = line_place()
    here = 4 * place + rank
    peers = []
    for step in range(1, 16):
        other = lax.rem(here + step, 16)
        peers.append((other, other // 4, lax.rem(other, 4)))
    return here, peers


def greet(peers):
    side = lax.axis_index("dp")
    barrier = pltpu.get_barrier_semaphore()
    for _, seq_to, rank_to in peers:
        pl.semaphore_signal(
            barrier, inc=1, device_id={"seq": seq_to, "tensor": rank_to}, device_id_type=MESH_ID
        )
    pl.semaphore_signal(barrier, inc=1, device_id={"dp": 1 - side}, device_id_type=MESH_ID)
    pl.semaphore_wait(barrier, len(peers) + 1)


def middle_forward_kernel(
    mixed, tokens, w_out, vecs,
    hidden, mixed_rows, mid_all,
    send_sem, recv_sem, ring_send, ring_recv,
):
    side, place, half, rank = plane_place()
    mine = place // 2
    head = 2 * rank + half
    here, peers = group_peers()
    greet(peers)

    def rows_copy(slot, sender, seq_from, rank_from, seq_to, rank_to):
        return pltpu.make_async_remote_copy(
            src_ref=mixed.at[seq_to, span(rank_to, 128), :],
            dst_ref=mixed_rows.at[
                seq_from // 2, :, span(2 * rank_from + lax.rem(seq_from, 2), 128)
            ],
            send_sem=send_sem.at[slot],
            recv_sem=recv_sem.at[sender],
            device_id={"seq": seq_to, "tensor": rank_to},
            device_id_type=MESH_ID,
        )

    for slot, (_, seq_to, rank_to) in enumerate(peers):
        rows_copy(slot, here, place, rank, seq_to, rank_to).start()
    mixed_rows[mine, :, span(head, 128)] = mixed[place, span(rank, 128), :]
    for slot, (other, seq_to, rank_to) in enumerate(peers):
        rows_copy(slot, other, seq_to, rank_to, seq_to, rank_to).wait_recv()
    me = plane_index(side, place)
    gain = vecs[2:3, :]

    def one(which, _):
        added = dot_nn(mixed_rows[which], w_out[...]) + tokens[which].astype(jnp.float32)
        hidden[which] = added
        centered, scale = norm_parts(added)
        mid_all[me, span(which, 128), :] = to_low(centered * scale * gain)
        return 0

    lax.fori_loop(0, 2, one, 0)
    run_all(plane_gather(mid_all, 256, ring_send, ring_recv))
    for slot, (_, seq_to, rank_to) in enumerate(peers):
        rows_copy(slot, here, place, rank, seq_to, rank_to).wait_send()


def middle_forward(mixed, tokens, w_out, vecs):
    low, wide = jnp.bfloat16, jnp.float32
    shapes = (((2, 128, D), wide), ((2, 128, D), low), ((8, 256, D), low))
    return pl.pallas_call(
        middle_forward_kernel,
        out_shape=[jax.ShapeDtypeStruct(*one) for one in shapes],
        in_specs=vmem_specs(4),
        out_specs=vmem_specs(3),
        scratch_shapes=[
            pltpu.SemaphoreType.DMA((15,)),
            pltpu.SemaphoreType.DMA((16,)),
            pltpu.SemaphoreType.DMA((16,)),
            pltpu.SemaphoreType.DMA((8, 2)),
        ],
        compiler_params=pltpu.CompilerParams(
            collective_id=3, has_side_effects=True, vmem_limit_bytes=VMEM_LIMIT
        ),
        cost_estimate=pl.CostEstimate(
            flops=30000000000, bytes_accessed=30000000, transcendentals=0
        ),
        name="middle_forward",
    )(mixed, tokens, w_out, vecs)


def middle_backward_kernel(
    part, hidden, cots, w_out, vecs,
    d_hidden, d_low, d_line, sums,
    work, core_got, near_got, far_got, total, d_rows,
    ring_send, ring_recv, send_sem, recv_sem,
):
    side, place, half, rank = plane_place()
    mine = place // 2
    head = 2 * rank + half
    here, peers = group_peers()

    def keep(owner, _):
        work[owner] = part[owner]
        return 0

    lax.fori_loop(0, 8, keep, 0)
    greet(peers)
    run_all(plane_scatter(work, core_got, near_got, far_got, total, 256, ring_send, ring_recv))
    gain = vecs[2:3, :]
    sums[...] = jnp.zeros_like(sums)

    def one(which, _):
        rows = span(which, 128)
        grad = total[rows, :]
        centered, scale = norm_parts(hidden[which])
        normed = centered * scale
        sums[0:1, :] += jnp.sum(grad * normed, axis=0, keepdims=True)
        lifted = grad * gain
        back = cots[which].astype(jnp.float32) + scale * (
            lifted
            - jnp.mean(lifted, axis=-1, keepdims=True)
            - normed * jnp.mean(lifted * normed, axis=-1, keepdims=True)
        )
        d_hidden[which] = back
        d_low[which] = to_low(back)
        d_rows[which] = to_low(dot_nt(to_low(back), w_out[...]))
        return 0

    lax.fori_loop(0, 2, one, 0)

    def line_copy(slot, sender, seq_from, rank_from, seq_to, rank_to):
        return pltpu.make_async_remote_copy(
            src_ref=d_rows.at[seq_to // 2, :, span(2 * rank_to + lax.rem(seq_to, 2), 128)],
            dst_ref=d_line.at[seq_from, span(rank_from, 128), :],
            send_sem=send_sem.at[slot],
            recv_sem=recv_sem.at[sender],
            device_id={"seq": seq_to, "tensor": rank_to},
            device_id_type=MESH_ID,
        )

    for slot, (_, seq_to, rank_to) in enumerate(peers):
        line_copy(slot, here, place, rank, seq_to, rank_to).start()
    d_line[place, span(rank, 128), :] = d_rows[mine, :, span(head, 128)]
    for slot, (other, seq_to, rank_to) in enumerate(peers):
        line_copy(slot, other, seq_to, rank_to, seq_to, rank_to).wait_recv()
    for slot, (_, seq_to, rank_to) in enumerate(peers):
        line_copy(slot, here, place, rank, seq_to, rank_to).wait_send()


def middle_backward(part, hidden, cots, w_out, vecs):
    low, wide = jnp.bfloat16, jnp.float32
    shapes = (((2, 128, D), wide), ((2, 128, D), low), ((4, BLOCK, 128), low), ((8, D), wide))
    return pl.pallas_call(
        middle_backward_kernel,
        out_shape=[jax.ShapeDtypeStruct(*one) for one in shapes],
        in_specs=vmem_specs(5),
        out_specs=vmem_specs(4),
        scratch_shapes=[
            pltpu.VMEM((8, 256, D), low),
            pltpu.VMEM((4, 256, D), low),
            pltpu.VMEM((4, 128, D), low),
            pltpu.VMEM((2, 128, D), low),
            pltpu.VMEM((256, D), wide),
            pltpu.VMEM((2, 128, D), low),
            pltpu.SemaphoreType.DMA((10,)),
            pltpu.SemaphoreType.DMA((10,)),
            pltpu.SemaphoreType.DMA((15,)),
            pltpu.SemaphoreType.DMA((16,)),
        ],
        compiler_params=pltpu.CompilerParams(
            collective_id=4, has_side_effects=True, vmem_limit_bytes=VMEM_LIMIT
        ),
        cost_estimate=pl.CostEstimate(
            flops=30000000000, bytes_accessed=30000000, transcendentals=0
        ),
        name="middle_backward",
    )(part, hidden, cots, w_out, vecs)


WIDE = 2048


def opening_kernel(
    tokens, w_qkv, piece, vecs, line,
    rows_all, qkv, kept, table,
    stage, send_sem, core_sem, recv_sem, piece_send, piece_recv, ring_send, ring_recv,
):
    side, place, half, rank = plane_place()
    mine = place // 2
    core = place + 1 - 2 * half
    other = lax.rem(place + 2, 4)
    me = plane_index(side, place)
    extra = piece.shape[0]
    barrier = pltpu.get_barrier_semaphore()
    greeted = [{"tensor": lax.rem(rank + step, 4)} for step in (1, 2, 3)]
    greeted += [{"seq": core}, {"seq": other}, {"dp": 1 - side}]
    for target in greeted:
        pl.semaphore_signal(barrier, inc=1, device_id=target, device_id_type=MESH_ID)
    gain = vecs[3:4, :]

    def normed(which):
        centered, scale = norm_parts(tokens[which].astype(jnp.float32))
        return to_low(centered * scale * gain)

    def moved(block_id, origin, sem, target):
        view = rows_all.at[block_id, span(origin, 128), :]
        return pltpu.make_async_remote_copy(
            src_ref=view,
            dst_ref=view,
            send_sem=sem,
            recv_sem=recv_sem.at[block_id, origin],
            device_id=target,
            device_id_type=MESH_ID,
        )

    stage[...] = normed(1 - mine)
    kept[me, span(rank, extra), :] = piece[...]
    pl.semaphore_wait(barrier, 6)
    aside = pltpu.make_async_remote_copy(
        src_ref=stage,
        dst_ref=rows_all.at[place, span(rank, 128), :],
        send_sem=send_sem.at[0, 0, 3],
        recv_sem=recv_sem.at[place, rank],
        device_id={"seq": other},
        device_id_type=MESH_ID,
    )
    aside.start()
    rows_all[place, span(rank, 128), :] = normed(mine)
    right, left = {"tensor": lax.rem(rank + 1, 4)}, {"tensor": lax.rem(rank + 3, 4)}
    blocks = (place, other)

    def pass_on(which, distance):
        block_id = blocks[which]

        @pl.when((rank < 3) & (rank >= distance))
        def _():
            moved(block_id, jnp.maximum(rank - distance, 0), send_sem.at[which, distance, 0], right).start()

        @pl.when((rank > 0) & (rank + distance <= 3))
        def _():
            moved(block_id, jnp.minimum(rank + distance, 3), send_sem.at[which, distance, 1], left).start()

    def pass_done(which, distance):
        block_id = blocks[which]

        @pl.when((rank < 3) & (rank >= distance))
        def _():
            moved(block_id, jnp.maximum(rank - distance, 0), send_sem.at[which, distance, 0], right).wait_send()

        @pl.when((rank > 0) & (rank + distance <= 3))
        def _():
            moved(block_id, jnp.minimum(rank + distance, 3), send_sem.at[which, distance, 1], left).wait_send()

    def project(block_id, origin):
        view = span(origin, 128)
        qkv[block_id, view, :] = to_low(dot_nn(rows_all[block_id, view, :], w_qkv[...]))

    def rows_steps():
        pass_on(0, 0)
        moved(place, rank, core_sem.at[0, rank], {"seq": core}).start()
        project(place, rank)
        moved(other, rank, send_sem.at[0, 0, 3], {"seq": other}).wait_recv()
        pass_on(1, 0)
        moved(other, rank, core_sem.at[1, rank], {"seq": core}).start()
        project(other, rank)
        yield
        for distance in (1, 2, 3):
            for which in (0, 1):
                block_id = blocks[which]
                for way, ok, origin in (
                    (0, rank >= distance, jnp.maximum(rank - distance, 0)),
                    (1, rank + distance <= 3, jnp.minimum(rank + distance, 3)),
                ):

                    @pl.when(ok)
                    def _():
                        moved(block_id, origin, send_sem.at[which, distance, way], right).wait_recv()
                        if distance < 3:
                            if way == 0:

                                @pl.when(rank < 3)
                                def _():
                                    moved(
                                        block_id, origin, send_sem.at[which, distance, 0], right
                                    ).start()

                            else:

                                @pl.when(rank > 0)
                                def _():
                                    moved(
                                        block_id, origin, send_sem.at[which, distance, 1], left
                                    ).start()

                        moved(block_id, origin, core_sem.at[which, origin], {"seq": core}).start()
                        project(block_id, origin)

                yield
        for which, block_id in enumerate((core, lax.rem(core + 2, 4))):
            for origin in range(4):
                moved(block_id, origin, core_sem.at[which, origin], {"seq": core}).wait_recv()
                project(block_id, origin)
        for which in (0, 1):
            for distance in (0, 1, 2):
                pass_done(which, distance)
            for origin in range(4):
                moved(blocks[which], origin, core_sem.at[which, origin], {"seq": core}).wait_send()

    def piece_move(slot, origin, target):
        view = kept.at[me, span(origin, extra), :]
        return pltpu.make_async_remote_copy(
            src_ref=view,
            dst_ref=view,
            send_sem=piece_send.at[slot],
            recv_sem=piece_recv.at[origin],
            device_id=target,
            device_id_type=MESH_ID,
        )

    def piece_steps():
        for slot in range(3):
            piece_move(slot, rank, greeted[slot]).start()
        first = line[...]
        row = lax.broadcasted_iota(jnp.int32, (8, WIDE), 0)
        for step in (1, 2, 4):
            first = jnp.where(row // step % 2 == 1, pltpu.roll(first, step, 1), first)

        def one(group, _):
            table[span(group, 8), :] = pltpu.roll(first, 8 * group, 1)[:, 0 : 2 * BLOCK]
            return 0

        lax.fori_loop(0, BLOCK // 8, one, 0)
        yield
        for slot in range(3):
            piece_move(slot, lax.rem(rank + slot + 1, 4), greeted[slot]).wait_recv()
        for _ in plane_gather(kept, 4 * extra, ring_send, ring_recv):
            yield
        for slot in range(3):
            piece_move(slot, rank, greeted[slot]).wait_send()

    run_all(rows_steps(), piece_steps())
    aside.wait_send()


def opening(tokens, w_qkv, piece, vecs, line):
    low, wide = jnp.bfloat16, jnp.float32
    extra = piece.shape[0]
    shapes = (
        ((4, BLOCK, D), low),
        ((4, BLOCK, 384), low),
        ((8, 4 * extra, D), low),
        ((BLOCK, 2 * BLOCK), wide),
    )
    return pl.pallas_call(
        opening_kernel,
        out_shape=[jax.ShapeDtypeStruct(*one) for one in shapes],
        in_specs=vmem_specs(5),
        out_specs=vmem_specs(4),
        scratch_shapes=[
            pltpu.VMEM((128, D), low),
            pltpu.SemaphoreType.DMA((2, 4, 4)),
            pltpu.SemaphoreType.DMA((2, 4)),
            pltpu.SemaphoreType.DMA((4, 4)),
            pltpu.SemaphoreType.DMA((3,)),
            pltpu.SemaphoreType.DMA((4,)),
            pltpu.SemaphoreType.DMA((16,)),
            pltpu.SemaphoreType.DMA((8, 2)),
        ],
        compiler_params=pltpu.CompilerParams(
            collective_id=5, has_side_effects=True, vmem_limit_bytes=VMEM_LIMIT
        ),
        cost_estimate=pl.CostEstimate(
            flops=30000000000, bytes_accessed=30000000, transcendentals=0
        ),
        name="opening",
    )(tokens, w_qkv, piece, vecs, line)


def pair_sum(part, near_got, far_got, result, rows, send_sem, recv_sem):
    side, place, half, rank = plane_place()
    mine = place // 2
    across, beside = 1 - side, 1 - mine
    me = 2 * side + mine
    at_x, at_y, at_d = 2 * across + mine, 2 * side + beside, 2 * across + beside
    to_x, to_y = {"dp": across}, {"seq": lax.rem(place + 2, 4)}
    size = rows // 2
    views = (pl.ds(0, size), pl.ds(size, size))

    def moved(source, target_ref, slot, target):
        return pltpu.make_async_remote_copy(
            src_ref=source,
            dst_ref=target_ref,
            send_sem=send_sem.at[slot],
            recv_sem=recv_sem.at[slot],
            device_id=target,
            device_id_type=MESH_ID,
        )

    def add_into(owner, view, other):
        part[owner, view, :] = to_low(
            part[owner, view, :].astype(jnp.float32) + other.astype(jnp.float32)
        )

    near = [
        moved(part.at[at_d, views[0], :], near_got.at[0], 0, to_x),
        moved(part.at[at_d, views[1], :], near_got.at[1], 1, to_y),
        moved(part.at[at_x, views[0], :], near_got.at[2], 2, to_x),
        moved(part.at[at_y, views[1], :], near_got.at[3], 3, to_y),
    ]
    for one in near:
        one.start()
    yield
    near[0].wait_recv()
    add_into(at_y, views[0], near_got[0])
    far = [
        moved(part.at[at_y, views[0], :], far_got.at[0], 4, to_y),
        moved(part.at[at_x, views[1], :], far_got.at[1], 5, to_x),
    ]
    far[0].start()
    near[1].wait_recv()
    add_into(at_x, views[1], near_got[1])
    far[1].start()
    yield
    near[2].wait_recv()
    add_into(me, views[0], near_got[2])
    near[3].wait_recv()
    add_into(me, views[1], near_got[3])
    for slot, view in enumerate(views):
        far[slot].wait_recv()
        result[me, view, :] = to_low(
            part[me, view, :].astype(jnp.float32) + far_got[slot].astype(jnp.float32)
        )

    def given(owner, which, slot, target):
        view = result.at[owner, views[which], :]
        return moved(view, view, slot, target)

    own = [
        given(me, 0, 6, to_x),
        given(me, 1, 7, to_y),
        given(me, 1, 8, to_x),
        given(me, 0, 9, to_y),
    ]
    for one in own:
        one.start()
    yield
    given(at_x, 0, 6, to_x).wait_recv()
    last = [given(at_x, 0, 10, to_y), given(at_y, 1, 11, to_x)]
    last[0].start()
    given(at_y, 1, 7, to_y).wait_recv()
    last[1].start()
    yield
    given(at_x, 1, 8, to_x).wait_recv()
    given(at_y, 0, 9, to_y).wait_recv()
    given(at_d, 0, 10, to_y).wait_recv()
    given(at_d, 1, 11, to_x).wait_recv()
    for one in near + far + own + last:
        one.wait_send()


PAIR_ROWS = 640


def closing_kernel(
    d_qkv, w_qkv, tokens, d_hidden, vecs, rows_all, state_low, d_qkvst, os_rows, du_rows,
    d_start, dz_sum, spots, small, out_part,
    inputs_grad, pair_out, sout_out, small_out,
    leave, came, sums, got_r, got_l, final, cross, cross_got,
    pair_part, pair_near, pair_far,
    work, core_got, near_got, far_got, total, z_part, z_got,
    diag, small_z, small_p,
    line_send, line_recv, way_send, way_recv, pair_send, pair_recv, core_sem,
    ring_send, ring_recv, zs_send, zs_recv, gather_send, gather_recv, small_send, small_recv,
):
    side, place, half, rank = plane_place()
    mine = place // 2
    core = place + 1 - 2 * half
    other = lax.rem(place + 2, 4)
    me = plane_index(side, place)
    ranks = [lax.rem(rank + step, 4) for step in (1, 2, 3)]
    spots_of = [lax.rem(me + step, 8) for step in range(1, 8)]
    barrier = pltpu.get_barrier_semaphore()
    for target in ranks:
        pl.semaphore_signal(barrier, inc=1, device_id={"tensor": target}, device_id_type=MESH_ID)
    for target in spots_of:
        pl.semaphore_signal(
            barrier,
            inc=1,
            device_id={"dp": target // 4, "seq": lax.rem(target, 4)},
            device_id_type=MESH_ID,
        )
    gain = vecs[3:4, :]
    right, left = {"tensor": lax.rem(rank + 1, 4)}, {"tensor": lax.rem(rank + 3, 4)}

    def moved(source, target_ref, send, recv, target):
        return pltpu.make_async_remote_copy(
            src_ref=source,
            dst_ref=target_ref,
            send_sem=send,
            recv_sem=recv,
            device_id=target,
            device_id_type=MESH_ID,
        )

    def to_core(which):
        return moved(
            leave.at[which], came.at[which], line_send.at[which], line_recv.at[which], {"seq": core}
        )

    def crossing():
        return moved(cross, cross_got, line_send.at[2], line_recv.at[2], {"seq": other})

    def step_right(which, target):
        return moved(
            sums.at[which, target], got_r.at[which, target],
            way_send.at[which, target], way_recv.at[0, which, target], right,
        )

    def step_left(which, target):
        return moved(
            sums.at[which, target], got_l.at[which, target],
            way_send.at[which, target], way_recv.at[1, which, target], left,
        )

    def add_sum(which, target, got):
        sums[which, target] = to_low(
            sums[which, target].astype(jnp.float32) + got[which, target].astype(jnp.float32)
        )

    def line_steps():
        for which, block_id in enumerate((lax.rem(core + 2, 4), core)):

            def partner(chunk, _):
                rows = span(chunk, ROWS)
                leave[which, rows, :] = to_low(dot_nt(d_qkv[block_id, rows, :], w_qkv[...]))
                return 0

            lax.fori_loop(0, CHUNKS, partner, 0)
            if which == 0:
                pl.semaphore_wait(barrier, 10)
            to_core(which).start()
        for which, block_id in enumerate((other, place)):
            to_core(which).wait_recv()

            def own(chunk, _):
                rows = span(chunk, ROWS)
                sums[which, chunk] = to_low(
                    dot_nt(d_qkv[block_id, rows, :], w_qkv[...])
                    + came[which, rows, :].astype(jnp.float32)
                )
                return 0

            lax.fori_loop(0, CHUNKS, own, 0)
        for which in (0, 1):
            for to_right, to_left in ((3, 0), (2, 1), (1, 2)):

                @pl.when(rank < to_right)
                def _():
                    @pl.when(rank > 0)
                    def _():
                        step_right(which, to_right).wait_recv()
                        add_sum(which, to_right, got_r)

                    step_right(which, to_right).start()

                @pl.when(rank > to_left)
                def _():
                    @pl.when(rank < 3)
                    def _():
                        step_left(which, to_left).wait_recv()
                        add_sum(which, to_left, got_l)

                    step_left(which, to_left).start()

                yield
            final[which] = sums[which, rank].astype(jnp.float32)

            @pl.when(rank > 0)
            def _():
                step_right(which, rank).wait_recv()
                final[which] += got_r[which, rank].astype(jnp.float32)

            @pl.when(rank < 3)
            def _():
                step_left(which, rank).wait_recv()
                final[which] += got_l[which, rank].astype(jnp.float32)

            if which == 0:
                cross[...] = to_low(final[0])
                crossing().start()
            yield
        crossing().wait_recv()
        final[0] = cross_got[...].astype(jnp.float32)
        small_z[rank] = small[...]
        for which, row_set in ((1, mine), (0, 1 - mine)):
            grad = final[which]
            centered, scale = norm_parts(tokens[row_set].astype(jnp.float32))
            normed = centered * scale
            small_z[rank, 0:1, :] += jnp.sum(grad * normed, axis=0, keepdims=True)
            lifted = grad * gain
            inputs_grad[row_set] = d_hidden[row_set] + scale * (
                lifted
                - jnp.mean(lifted, axis=-1, keepdims=True)
                - normed * jnp.mean(lifted * normed, axis=-1, keepdims=True)
            )
        crossing().wait_send()
        for which in (0, 1):
            to_core(which).wait_send()
            for target in range(4):

                @pl.when(rank < target)
                def _():
                    step_right(which, target).wait_send()

                @pl.when(rank > target)
                def _():
                    step_left(which, target).wait_send()

    def pair_steps():
        for chunk in range(4):
            if chunk < 3:
                first = 128 * chunk

                def one(block_id, acc):
                    acc = acc + dot_tn(d_qkv[block_id, :, first : first + 128], rows_all[block_id])
                    if chunk > 0:
                        acc = acc + dot_tn(
                            d_qkvst[block_id, :, first : first + 128], state_low[block_id]
                        )
                    return acc

            else:

                def one(block_id, acc):
                    return acc + dot_tn(d_qkvst[block_id, :, 0:128], state_low[block_id])

            acc = lax.fori_loop(0, 4, one, jnp.zeros((128, D), jnp.float32))
            low = to_low(acc)
            first = 128 * chunk
            while first < 128 * (chunk + 1):
                owner, inside = first // 160, first % 160
                size = min(160 - inside, 128 * (chunk + 1) - first)
                begin = first - 128 * chunk
                pair_part[owner, inside : inside + size, :] = low[begin : begin + size, :]
                first += size
        pair_part[3, 32:96, :] = to_low(d_start[...])
        pair_part[3, 96:160, :] = jnp.zeros((64, D), jnp.bfloat16)
        for _ in pair_sum(
            pair_part, pair_near, pair_far, pair_out.at[half], 160, pair_send, pair_recv
        ):
            yield
        full = moved(
            pair_out.at[half], pair_out.at[half], core_sem.at[0], core_sem.at[1], {"seq": core}
        )
        full.start()
        yield
        moved(
            pair_out.at[1 - half], pair_out.at[1 - half], core_sem.at[0], core_sem.at[1],
            {"seq": core},
        ).wait_recv()
        full.wait_send()

    def sout_steps():
        for head in range(LINE):
            low = to_low(dot_tn(os_rows[:, 128 * head : 128 * head + 128], du_rows[...]))
            for piece in range(4):
                work[
                    4 * (head % 2) + piece, 32 * (head // 2) : 32 * (head // 2) + 32, :
                ] = low[32 * piece : 32 * piece + 32, :]
        for _ in plane_scatter(
            work, core_got, near_got, far_got, total, 128, ring_send, ring_recv
        ):
            yield
        z_part[:, 0:32, :] = to_low(total[...]).reshape(4, 32, D)
        z_part[:, 32:64, :] = out_part[...].reshape(4, 32, D)
        out = [
            moved(
                z_part.at[target], z_got.at[rank], zs_send.at[slot], zs_recv.at[rank],
                {"tensor": target},
            )
            for slot, target in enumerate(ranks)
        ]
        for one in out:
            one.start()
        z_got[rank] = z_part[rank]
        yield
        for slot, target in enumerate(ranks):
            moved(
                z_part.at[target], z_got.at[target], zs_send.at[slot], zs_recv.at[target],
                {"tensor": target},
            ).wait_recv()
        acc = z_got[0].astype(jnp.float32)
        for target in range(1, 4):
            acc = acc + z_got[target].astype(jnp.float32)
        sout_out[me] = to_low(acc)
        for _ in plane_gather(sout_out, 64, gather_send, gather_recv):
            yield
        for one in out:
            one.wait_send()

    def diag_steps():
        diag[...] = jnp.zeros_like(diag)
        for part in range(4):

            def one(group, _):
                rows = dz_sum[span(group, 8), :]
                wide = jnp.concatenate(
                    [rows, jnp.zeros((8, WIDE - 2 * BLOCK), jnp.float32)], axis=1
                )
                diag[...] += pltpu.roll(wide, lax.rem(WIDE - 8 * group, WIDE), 1)
                return 0

            lax.fori_loop(16 * part, 16 * part + 16, one, 0)
            yield
        total_line = diag[...]
        row = lax.broadcasted_iota(jnp.int32, (8, WIDE), 0)
        for step in (1, 2, 4):
            total_line = jnp.where(
                row // step % 2 == 1, pltpu.roll(total_line, WIDE - step, 1), total_line
            )
        line_sum = jnp.broadcast_to(jnp.sum(total_line, axis=0, keepdims=True), (8, WIDE))
        high = to_low(line_sum)
        rest = to_low(line_sum - high.astype(jnp.float32))
        diag[:, 0:256] = dot_nn(high, spots[...]) + dot_nn(rest, spots[...])

    run_all(line_steps(), pair_steps(), sout_steps(), diag_steps())
    small_z[rank, 4:5, 0:256] = diag[0:1, 0:256]

    def small_over_z(slot, sender, target):
        return moved(
            small_z.at[sender], small_z.at[sender], small_send.at[slot], small_recv.at[sender],
            {"tensor": target},
        )

    for slot, target in enumerate(ranks):
        small_over_z(slot, rank, target).start()
    for slot, target in enumerate(ranks):
        small_over_z(slot, target, target).wait_recv()
    small_p[me] = small_z[0] + small_z[1] + small_z[2] + small_z[3]

    def small_over_plane(slot, sender, target):
        return moved(
            small_p.at[sender], small_p.at[sender], small_send.at[3 + slot],
            small_recv.at[4 + sender],
            {"dp": target // 4, "seq": lax.rem(target, 4)},
        )

    for slot, target in enumerate(spots_of):
        small_over_plane(slot, me, target).start()
    for slot, target in enumerate(spots_of):
        small_over_plane(slot, target, target).wait_recv()
    acc = small_p[0]
    for target in range(1, 8):
        acc = acc + small_p[target]
    small_out[...] = acc
    for slot, target in enumerate(ranks):
        small_over_z(slot, rank, target).wait_send()
    for slot, target in enumerate(spots_of):
        small_over_plane(slot, me, target).wait_send()


def closing(
    d_qkv, w_qkv, tokens, d_hidden, vecs, rows_all, state_low, d_qkvst, os_rows, du_rows,
    d_start, dz_sum, spots, small, out_part,
):
    low, wide = jnp.bfloat16, jnp.float32
    shapes = (
        ((2, 128, D), wide),
        ((2, 4, PAIR_ROWS // 4, D), low),
        ((8, 64, D), low),
        ((8, D), wide),
    )
    dma = pltpu.SemaphoreType.DMA
    return pl.pallas_call(
        closing_kernel,
        out_shape=[jax.ShapeDtypeStruct(*one) for one in shapes],
        in_specs=vmem_specs(15),
        out_specs=vmem_specs(4),
        scratch_shapes=[
            pltpu.VMEM((2, BLOCK, D), low),
            pltpu.VMEM((2, BLOCK, D), low),
            pltpu.VMEM((2, 4, 128, D), low),
            pltpu.VMEM((2, 4, 128, D), low),
            pltpu.VMEM((2, 4, 128, D), low),
            pltpu.VMEM((2, 128, D), wide),
            pltpu.VMEM((128, D), low),
            pltpu.VMEM((128, D), low),
            pltpu.VMEM((4, PAIR_ROWS // 4, D), low),
            pltpu.VMEM((4, PAIR_ROWS // 8, D), low),
            pltpu.VMEM((2, PAIR_ROWS // 8, D), low),
            pltpu.VMEM((8, 128, D), low),
            pltpu.VMEM((4, 128, D), low),
            pltpu.VMEM((4, 64, D), low),
            pltpu.VMEM((2, 64, D), low),
            pltpu.VMEM((128, D), wide),
            pltpu.VMEM((4, 64, D), low),
            pltpu.VMEM((4, 64, D), low),
            pltpu.VMEM((8, WIDE), wide),
            pltpu.VMEM((4, 8, D), wide),
            pltpu.VMEM((8, 8, D), wide),
            dma((3,)), dma((3,)), dma((2, 4)), dma((2, 2, 4)), dma((12,)), dma((12,)), dma((2,)),
            dma((10,)), dma((10,)), dma((3,)), dma((4,)), dma((16,)), dma((8, 2)), dma((10,)),
            dma((12,)),
        ],
        compiler_params=pltpu.CompilerParams(
            collective_id=6, has_side_effects=True, vmem_limit_bytes=VMEM_LIMIT
        ),
        cost_estimate=pl.CostEstimate(
            flops=30000000000, bytes_accessed=30000000, transcendentals=0
        ),
        name="closing",
    )(
        d_qkv, w_qkv, tokens, d_hidden, vecs, rows_all, state_low, d_qkvst, os_rows, du_rows,
        d_start, dz_sum, spots, small, out_part,
    )


def swap_seq(value):
    return lax.all_to_all(value, "seq", 0, 0, tiled=False)


def line_body(
    inputs,
    seg_starts,
    lengths,
    init_state,
    attn_gain,
    state_gain,
    mlp_gain,
    w_query,
    w_key,
    w_value,
    w_out,
    w_squery,
    w_sout,
    w_up,
    w_down,
    rel_bias,
    gate_bias,
    out_cot,
    state_cot,
):
    low, wide = jnp.bfloat16, jnp.float32
    place = lax.axis_index("seq")
    half = lax.rem(place, 2)
    mine = place // 2
    plane = ("dp", "seq")
    spot = 4 * lax.axis_index("dp") + place
    head = 2 * lax.axis_index("tensor") + half
    head_of = lambda weight: lax.dynamic_slice_in_dim(weight, half * 128, 128, 1)
    gate_value = jax.nn.sigmoid(gate_bias)
    vecs = jnp.stack(
        [state_gain, gate_value, mlp_gain, attn_gain] + [jnp.zeros_like(gate_value)] * 4
    )
    offsets = jnp.arange(WIDE) - BLOCK
    offsets = jnp.where(offsets >= WIDE - 2 * BLOCK, offsets - WIDE, offsets)
    bucket_ids = bucket_of(offsets)
    one_hot = bucket_ids[:, None] == jnp.arange(BUCKETS)[None, :]
    my_bias = jnp.where(half == 0, rel_bias[:, 0], rel_bias[:, 1])
    bias_line = jnp.sum(jnp.where(one_hot, my_bias[None, :], 0.0), axis=1)
    lane = jnp.arange(LINE * BUCKETS)
    spots = (
        (bucket_ids[:, None] == lax.rem(lane, BUCKETS)[None, :]) & (lane // BUCKETS == head)[None, :]
    ).astype(low)
    segs = jnp.broadcast_to(jnp.repeat(seg_starts[:, 0], 2)[:, None, None], (4, 1, 128))
    segs = swap_seq(segs)[:, 0, 0]
    cots = swap_seq(state_cot.reshape(4, 64, D))
    cot_used = lax.all_gather(out_cot.reshape(256, D), plane, axis=0, tiled=True)

    w_qkv = jnp.concatenate([head_of(w_query), head_of(w_key), head_of(w_value)], axis=1)
    w_state = jnp.concatenate([head_of(w_squery), w_qkv[:, 128:]], axis=1)
    piece = jnp.concatenate(
        [
            lax.dynamic_slice_in_dim(w_sout, spot * 32, 32, 0),
            to_low(lax.dynamic_slice_in_dim(init_state, spot * 16, 16, 0)),
            lax.dynamic_slice_in_dim(w_out, spot * 32, 32, 0),
        ],
        axis=0,
    )
    rows_all, qkv, kept, bias = opening(
        inputs, w_qkv, piece, vecs, jnp.broadcast_to(bias_line[None, :], (8, WIDE))
    )
    kept = kept.reshape(8, 4, 80, D).transpose(1, 0, 2, 3)
    w_sout_all = kept[:, :, :32].reshape(D, D)
    start_all = kept[:, :, 32:48].reshape(STATES, D)
    w_out_all = kept[:, :, 48:].reshape(D, D)

    ff_own = w_up.shape[1] // 8
    piece_of = lambda weight: lax.dynamic_slice_in_dim(weight, spot * 32, 32, 1).T
    pieces = jnp.concatenate(
        [
            piece_of(w_squery),
            piece_of(w_key),
            piece_of(w_value),
            lax.dynamic_slice_in_dim(w_up, spot * ff_own, ff_own, 1).T,
            lax.dynamic_slice_in_dim(w_down, spot * ff_own, ff_own, 0),
        ],
        axis=0,
    )
    qkv, pieces, segs = lax.optimization_barrier((qkv, pieces, segs))
    scal = jnp.concatenate([lax.dynamic_slice_in_dim(lengths, mine, 1, 0), segs])
    spread = lax.all_gather(pieces, "tensor", axis=0, tiled=True).reshape(4, 96 + 2 * ff_own, D)
    up_rows = spread[:, 96 : 96 + ff_own].reshape(4 * ff_own, D)
    down_rows = spread[:, 96 + ff_own :].reshape(4 * ff_own, D)

    mixed, lse_tok, state_rows, state_low, qkvst, lse_st, os_rows = forward_chain(
        scal, qkv, start_all, w_state, w_sout_all, vecs, bias
    )
    other_block = lax.rem(place + 2, 4)
    sent = lax.dynamic_slice_in_dim(state_rows, other_block, 1, 0)[0].astype(low)
    came = lax.ppermute(sent, "seq", [(source, (source + 2) % 4) for source in range(4)])
    kept_rows = lax.dynamic_slice_in_dim(state_rows, place, 1, 0)[0]
    state_out = jnp.where(
        mine == 0,
        jnp.stack([kept_rows, came.astype(wide)]),
        jnp.stack([came.astype(wide), kept_rows]),
    )

    mixed, back_piece, cots = lax.optimization_barrier(
        (mixed, spread[:, 0:96].reshape(384, D), cots)
    )
    w_back = lax.all_gather(back_piece, plane, axis=0, tiled=True)
    hidden_in, mixed_rows, mid_all = middle_forward(mixed, inputs, w_out_all, vecs)
    mid_low = mid_all.reshape(2048, D)
    pre_act = matmul_t(mid_low, up_rows)
    hidden_low = to_low(jax.nn.gelu(pre_act))
    grad_hidden_act = matmul_t(cot_used, down_rows)
    grad_pre = to_low(gelu_back(pre_act, grad_hidden_act))
    d_mid_part = to_low(matmul(grad_pre, up_rows))
    d_mid_part, w_back = lax.optimization_barrier((d_mid_part, w_back))
    w_back = (
        w_back.reshape(2, 4, 4, 3, 32, D).transpose(2, 0, 3, 1, 4, 5).reshape(LINE, 384, D)
    )
    grad_hidden, grad_low, d_mixed, mlp_sums = middle_backward(
        d_mid_part.reshape(8, 256, D), hidden_in, out_cot, w_out_all, vecs
    )
    mlp_part = to_low(matmul(hidden_low, down_rows))
    ff_grads = jnp.stack(
        [
            outer_sum(grad_pre, mid_low).astype(low).reshape(4, ff_own, D),
            outer_sum(hidden_low, cot_used).astype(low).reshape(4, ff_own, D),
        ],
        axis=1,
    )
    out_part = outer_sum(mixed_rows, grad_low).astype(low)
    out_part = out_part.reshape(4, 8, 32, D).transpose(1, 0, 2, 3).reshape(D, D)
    d_mixed, mlp_part, ff_grads, out_part = lax.optimization_barrier(
        (d_mixed, mlp_part, ff_grads, out_part)
    )
    mlp_rows = lax.psum_scatter(mlp_part, plane, scatter_dimension=0, tiled=True)
    ff_sum = lax.psum_scatter(
        ff_grads.reshape(8 * ff_own, D), "tensor", scatter_dimension=0, tiled=True
    )
    out_part = lax.psum_scatter(out_part, plane, scatter_dimension=0, tiled=True)

    start_half = lax.dynamic_slice_in_dim(to_low(init_state).astype(wide), half * 64, 64, 0)
    states = jnp.concatenate(
        [start_half[None], lax.dynamic_slice_in_dim(state_rows, half * 64, 64, 1)], axis=0
    )
    d_qkv, d_qkvst, du_rows, d_start, sums, dz_sum = backward_chain(
        scal, qkv, d_mixed, lse_tok, qkvst, lse_st, states, cots, w_back, w_sout_all, vecs, bias
    )
    d_qkv, ff_sum, out_part = lax.optimization_barrier((d_qkv, ff_sum, out_part))
    tokens_out = (hidden_in + mlp_rows.reshape(2, 128, D).astype(wide)).astype(low)
    ff_total = lax.all_gather(ff_sum, plane, axis=0, tiled=True).reshape(8, 2, ff_own, D)
    up_grad = ff_total[:, 0].reshape(8 * ff_own, D).T.astype(wide)
    down_grad = ff_total[:, 1].reshape(8 * ff_own, D).astype(wide)
    small = jnp.concatenate(
        [jnp.zeros((1, D), wide), sums[1:2], mlp_sums[0:1], sums[0:1], jnp.zeros((4, D), wide)]
    )
    inputs_grad, pair, two_grads, small = closing(
        d_qkv, w_qkv, inputs, grad_hidden, vecs, rows_all, state_low, d_qkvst,
        os_rows.reshape(256, D), du_rows.reshape(256, D), d_start, dz_sum, spots, small, out_part,
    )
    pair = pair.reshape(2, PAIR_ROWS, D)
    out_grad = two_grads[:, 32:].reshape(256, D).astype(wide)
    sout_grad = two_grads[:, :32].reshape(256, D).astype(wide)

    def turned(first):
        return pair[:, first : first + 128].reshape(256, D).T.astype(wide)

    bias_grad = lax.dynamic_slice_in_dim(
        small[4, : LINE * BUCKETS].reshape(4, 2, BUCKETS), lax.axis_index("tensor"), 1, 0
    )[0].T
    return (
        tokens_out,
        state_out[:, None],
        inputs_grad,
        pair[:, 512:576].reshape(128, D).astype(wide),
        small[0],
        small[1],
        small[2],
        turned(0),
        turned(128),
        turned(256),
        out_grad,
        turned(384),
        sout_grad,
        up_grad,
        down_grad,
        bias_grad,
        small[3],
    )


def solution(mesh):
    return jax.shard_map(
        chosen_body(mesh),
        mesh=mesh,
        in_specs=(
            P("dp", ("seq", "tensor"), None),
            P("dp", "seq"),
            P("dp"),
            P("tensor", None),
            P(),
            P(),
            P(),
            P(None, "tensor"),
            P(None, "tensor"),
            P(None, "tensor"),
            P("tensor", None),
            P(None, "tensor"),
            P("tensor", None),
            P(None, "tensor"),
            P("tensor", None),
            P(None, "tensor"),
            P(),
            P("dp", ("seq", "tensor"), None),
            P("dp", "seq", "tensor", None),
        ),
        out_specs=(
            P("dp", ("seq", "tensor"), None),
            P("dp", "seq", "tensor", None),
            P("dp", ("seq", "tensor"), None),
            P("tensor", None),
            P(),
            P(),
            P(),
            P(None, "tensor"),
            P(None, "tensor"),
            P(None, "tensor"),
            P("tensor", None),
            P(None, "tensor"),
            P("tensor", None),
            P(None, "tensor"),
            P("tensor", None),
            P(None, "tensor"),
            P(),
        ),
        check_vma=False,
    )
```

```python
import jax
import jax.numpy as jnp
from jax import lax
from jax.experimental import pallas as pl
from jax.experimental.pallas import tpu as pltpu
from jax.sharding import PartitionSpec as P

D = 1024
HEAD_DIM = 128
STATES = 512
BLOCK = 512
SEG = 256
BUCKETS = 32


norm_eps = 1e-06
masked_score = -1e30
bucket_edges = (12, 16, 23, 32, 46, 64, 91)


def passed_along(value, axis, steps):
    count = lax.axis_size(axis)
    leading, last = (max(0, -steps), min(count, count - steps))
    return lax.ppermute(value, axis, [(source, source + steps) for source in range(leading, last)])


def bucket_of(relative):
    distance = jnp.abs(relative)
    far_bucket = 8 + sum(((distance >= boundary).astype(jnp.int32) for boundary in bucket_edges))
    near_far = jnp.where(distance < 8, distance, far_bucket)
    return near_far + 16 * (relative > 0).astype(jnp.int32)


def token_mask(seg_start, seq_length, block_index):
    positions = jnp.arange(BLOCK)
    offset = block_index * BLOCK
    prev_valid = (block_index > 0) & (offset - BLOCK + positions < seq_length)
    cur_valid = offset + positions < seq_length
    inside = (positions >= seg_start) & (positions < seg_start + SEG)
    prev_mask = (positions[None, :] > positions[:, None]) & prev_valid[None, :]
    cur_mask = (
        (positions[None, :] <= positions[:, None]) | inside[None, :] & inside[:, None]
    ) & cur_valid[None, :]
    state_mask = jnp.ones((BLOCK, STATES), jnp.bool_)
    return jnp.concatenate([prev_mask, cur_mask, state_mask], axis=1)


def state_mask_of(valid_blk):
    batch_count = valid_blk.shape[0]
    block_part = jnp.broadcast_to(valid_blk[:, None, :], (batch_count, STATES, BLOCK))
    return jnp.concatenate([block_part, jnp.ones((batch_count, STATES, STATES), jnp.bool_)], axis=2)


def layer_norm(values, gain_vec):
    centered = values - jnp.mean(values, axis=-1, keepdims=True)
    spread = jnp.mean(centered * centered, axis=-1, keepdims=True)
    return centered * lax.rsqrt(spread + norm_eps) * gain_vec


def norm_back(values, gain_vec, grad_out):
    _, pullback = jax.vjp(layer_norm, values, gain_vec)
    return pullback(grad_out)


def gelu_back(pre_act, grad_out):
    _, pullback = jax.vjp(jax.nn.gelu, pre_act)
    return pullback(grad_out)[0]


def to_low(array_in):
    return array_in.astype(jnp.bfloat16)


def matmul(left, right):
    return jnp.einsum("...k,kn->...n", left, right, preferred_element_type=jnp.float32)


def matmul_t(left, right):
    return jnp.einsum("...n,kn->...k", left, right, preferred_element_type=jnp.float32)


def outer_sum(left, right):
    left_flat = left.reshape(-1, left.shape[-1])
    right_flat = right.reshape(-1, right.shape[-1])
    return lax.dot_general(
        left_flat, right_flat, (((0,), (0,)), ((), ())), preferred_element_type=jnp.float32
    )


def gather_rows(values):
    return lax.all_gather(values, "tensor", axis=1, tiled=True)


def sum_rows(terms):
    return lax.psum_scatter(
        terms.astype(jnp.bfloat16), "tensor", scatter_dimension=1, tiled=True
    ).astype(jnp.float32)


def pass_state(rows_now):
    return passed_along(rows_now.astype(jnp.bfloat16), "seq", 1).astype(rows_now.dtype)


def pass_back(grad_now):
    return passed_along(grad_now.astype(jnp.bfloat16), "seq", -1).astype(grad_now.dtype)


def split_heads(rows_in):
    return rows_in.reshape(rows_in.shape[0], rows_in.shape[1] // HEAD_DIM, HEAD_DIM)


def score_block(query_rows, key_all, bias_all, allowed):
    scores = (
        jnp.einsum(
            "qhd,khd->hqk",
            split_heads(query_rows),
            split_heads(key_all),
            preferred_element_type=jnp.float32,
        )
        * HEAD_DIM ** (-0.5)
        + bias_all
    )
    return jnp.where(allowed[None], scores, masked_score)


def attend_forward(query_rows, key_all, value_all, bias_all, allowed):
    scores = score_block(query_rows, key_all, bias_all, allowed)
    row_max = jnp.max(scores, axis=-1, keepdims=True)
    exp_scores = jnp.exp(scores - row_max)
    row_total = jnp.sum(exp_scores, axis=-1, keepdims=True)
    weight_all = to_low(exp_scores / row_total)
    mixed_out = jnp.einsum(
        "hqk,khd->qhd", weight_all, split_heads(value_all), preferred_element_type=jnp.float32
    )
    return (
        to_low(mixed_out.reshape(query_rows.shape[0], -1)),
        (row_max + jnp.log(row_total))[..., 0],
    )


def attend_back(query_rows, key_all, value_all, bias_all, allowed, log_total, grad_mixed):
    scores = score_block(query_rows, key_all, bias_all, allowed)
    weight_all = jnp.where(allowed[None], jnp.exp(scores - log_total[..., None]), 0.0)
    grad_heads = split_heads(grad_mixed)
    grad_weight = jnp.einsum(
        "qhd,khd->hqk", grad_heads, split_heads(value_all), preferred_element_type=jnp.float32
    )
    row_inner = jnp.sum(weight_all * grad_weight, axis=-1, keepdims=True)
    grad_scores = to_low(weight_all * (grad_weight - row_inner))
    grad_query = jnp.einsum(
        "hqk,khd->qhd", grad_scores, split_heads(key_all), preferred_element_type=jnp.float32
    ) * HEAD_DIM ** (-0.5)
    grad_keys = jnp.einsum(
        "hqk,qhd->khd", grad_scores, split_heads(query_rows), preferred_element_type=jnp.float32
    ) * HEAD_DIM ** (-0.5)
    grad_values = jnp.einsum(
        "hqk,qhd->khd", to_low(weight_all), grad_heads, preferred_element_type=jnp.float32
    )
    return (
        grad_query.reshape(query_rows.shape[0], -1),
        grad_keys.reshape(key_all.shape[0], -1),
        grad_values.reshape(key_all.shape[0], -1),
        grad_scores,
    )


def bias_lookup(rel_bias, rel_table):
    table_heads = jnp.zeros((rel_bias.shape[1],) + rel_table.shape, jnp.float32)
    for bucket_id in range(BUCKETS):
        table_heads = table_heads + jnp.where(
            rel_table[None] == bucket_id, rel_bias[bucket_id][:, None, None], 0.0
        )
    return table_heads


def bias_sums(score_grad, rel_table):
    grad_wide = score_grad.astype(jnp.float32)
    columns = []
    for bucket_id in range(BUCKETS):
        columns.append(
            jnp.sum(jnp.where(rel_table[None, None] == bucket_id, grad_wide, 0.0), axis=(0, 2, 3))
        )
    return jnp.stack(columns, axis=0)


def body(
    inputs,
    seg_starts,
    lengths,
    init_state,
    attn_gain,
    state_gain,
    mlp_gain,
    w_query,
    w_key,
    w_value,
    w_out,
    w_squery,
    w_sout,
    w_up,
    w_down,
    rel_bias,
    gate_bias,
    out_cot,
    state_cot,
):
    seq_count = inputs.shape[0]
    chain_length = lax.axis_size("seq")
    block_index = lax.axis_index("seq")
    is_first = block_index == 0
    width_local = w_query.shape[1]
    head_count = width_local // HEAD_DIM
    gate_value = jax.nn.sigmoid(gate_bias)
    positions = jnp.arange(BLOCK)
    inputs_wide = inputs.astype(jnp.float32)
    tokens_low = gather_rows(to_low(layer_norm(inputs_wide, attn_gain)))
    query_tok = to_low(matmul(tokens_low, w_query))
    key_tok = to_low(matmul(tokens_low, w_key))
    value_tok = to_low(matmul(tokens_low, w_value))
    key_prev, value_prev = passed_along((key_tok, value_tok), "seq", 1)
    valid_keys = (block_index * BLOCK + positions)[None, :] < lengths[:, None]
    batched_attend = jax.vmap(attend_forward, in_axes=(0, 0, 0, None, 0))
    batched_back = jax.vmap(attend_back, in_axes=(0, 0, 0, None, 0, 0, 0))

    def state_forward(state_rows, key_blk, value_blk, valid_blk):
        state_low = lax.all_gather(
            to_low(layer_norm(state_rows, state_gain)), "tensor", axis=1, tiled=True
        )
        query_st = to_low(matmul(state_low, w_squery))
        key_st = to_low(matmul(state_low, w_key))
        value_st = to_low(matmul(state_low, w_value))
        key_all = jnp.concatenate([key_blk, key_st], axis=1)
        value_all = jnp.concatenate([value_blk, value_st], axis=1)
        mixed_st, lse_st = batched_attend(
            query_st, key_all, value_all, 0.0, state_mask_of(valid_blk)
        )
        update = lax.psum_scatter(
            matmul(mixed_st, w_sout).astype(jnp.bfloat16), "tensor", scatter_dimension=1, tiled=True
        ).astype(jnp.float32)
        state_next = gate_value * state_rows + (1.0 - gate_value) * update
        return (state_next, (state_low, query_st, key_st, value_st, mixed_st, lse_st, update))

    def state_backward(
        grad_out, state_rows, kept_one, key_blk, value_blk, valid_blk, extra_key, extra_value
    ):
        state_low, query_st, key_st, value_st, mixed_st, lse_st, update = kept_one
        gate_part = (
            jnp.sum(grad_out * (state_rows - update), axis=(0, 1)) * gate_value * (1.0 - gate_value)
        )
        grad_update = lax.all_gather(
            to_low((1.0 - gate_value) * grad_out), "tensor", axis=1, tiled=True
        )
        grad_mixed_st = to_low(matmul_t(grad_update, w_sout))
        sout_part = outer_sum(mixed_st, grad_update)
        key_all = jnp.concatenate([key_blk, key_st], axis=1)
        value_all = jnp.concatenate([value_blk, value_st], axis=1)
        grad_query_st, grad_keys_st, grad_values_st, _ = batched_back(
            query_st, key_all, value_all, 0.0, state_mask_of(valid_blk), lse_st, grad_mixed_st
        )
        query_low = to_low(grad_query_st)
        key_low = to_low(grad_keys_st[:, BLOCK:] + extra_key)
        value_low = to_low(grad_values_st[:, BLOCK:] + extra_value)
        squery_part = outer_sum(state_low, query_low)
        key_part = outer_sum(state_low, key_low)
        value_part = outer_sum(state_low, value_low)
        terms = (
            matmul_t(query_low, w_squery) + matmul_t(key_low, w_key) + matmul_t(value_low, w_value)
        )
        grad_normed = lax.psum_scatter(
            terms.astype(jnp.bfloat16), "tensor", scatter_dimension=1, tiled=True
        ).astype(jnp.float32)
        grad_rows_norm, gain_part = norm_back(state_rows, state_gain, grad_normed)
        grad_in = gate_value * grad_out + grad_rows_norm
        block_grads = (grad_keys_st[:, :BLOCK], grad_values_st[:, :BLOCK])
        return (
            grad_in,
            block_grads,
            (squery_part, key_part, value_part, sout_part, gain_part, gate_part),
        )

    zeros_rows = jnp.zeros((seq_count,) + init_state.shape, jnp.float32)
    narrow_zero = jnp.zeros((seq_count, STATES, width_local), jnp.bfloat16)
    stored_start = (
        zeros_rows,
        zeros_rows,
        jnp.zeros((seq_count, STATES, D), jnp.bfloat16),
        narrow_zero,
        narrow_zero,
        narrow_zero,
        narrow_zero,
        jnp.zeros((seq_count, head_count, STATES), jnp.float32),
        zeros_rows,
    )

    def forward_turn(turn_index, carry):
        incoming, stored_now = carry
        order_index = turn_index - block_index
        is_live = (order_index >= 0) & (order_index < seq_count)
        picked = jnp.clip(order_index, 0, seq_count - 1)
        rows_now = jnp.where(is_first, init_state[None], incoming)
        key_one = lax.dynamic_slice_in_dim(key_tok, picked, 1, 0)
        value_one = lax.dynamic_slice_in_dim(value_tok, picked, 1, 0)
        valid_one = lax.dynamic_slice_in_dim(valid_keys, picked, 1, 0)
        rows_next, kept_one = state_forward(rows_now, key_one, value_one, valid_one)
        fresh = (rows_now, rows_next) + kept_one
        stored_now = tuple(
            (
                jnp.where(
                    is_live,
                    lax.dynamic_update_slice_in_dim(whole_array, fresh_part, picked, 0),
                    whole_array,
                )
                for whole_array, fresh_part in zip(stored_now, fresh)
            )
        )
        return (pass_state(rows_next), stored_now)

    incoming_start = jnp.zeros((1,) + init_state.shape, jnp.float32)
    _, stored_all = lax.fori_loop(
        0, chain_length + seq_count - 1, forward_turn, (incoming_start, stored_start)
    )
    state_in = stored_all[0]
    state_out = stored_all[1]
    kept = stored_all[2:]
    key_all_tok = jnp.concatenate([key_prev, key_tok, kept[2]], axis=1)
    value_all_tok = jnp.concatenate([value_prev, value_tok, kept[3]], axis=1)
    allowed_tok = jax.vmap(token_mask, in_axes=(0, 0, None))(seg_starts[:, 0], lengths, block_index)
    rel_table = bucket_of((jnp.arange(2 * BLOCK) - BLOCK)[None, :] - positions[:, None])
    full_bias = jnp.concatenate(
        [bias_lookup(rel_bias, rel_table), jnp.zeros((head_count, BLOCK, STATES), jnp.float32)],
        axis=2,
    )
    mixed_tok, lse_tok = batched_attend(
        query_tok, key_all_tok, value_all_tok, full_bias, allowed_tok
    )
    hidden_in = inputs_wide + sum_rows(matmul(mixed_tok, w_out))
    mid_low = gather_rows(to_low(layer_norm(hidden_in, mlp_gain)))
    pre_act = matmul(mid_low, w_up)
    hidden_low = to_low(jax.nn.gelu(pre_act))
    mlp_rows = sum_rows(matmul(hidden_low, w_down))
    tokens_out = (hidden_in + mlp_rows).astype(jnp.bfloat16)
    cot_wide = out_cot.astype(jnp.float32)
    cot_used = gather_rows(out_cot)
    grad_hidden_act = matmul_t(cot_used, w_down)
    down_grad = outer_sum(hidden_low, cot_used)
    grad_pre = to_low(gelu_back(pre_act, grad_hidden_act))
    up_grad = outer_sum(mid_low, grad_pre)
    grad_normed_mid = sum_rows(matmul_t(grad_pre, w_up))
    grad_mid_in, mlp_gain_grad = norm_back(hidden_in, mlp_gain, grad_normed_mid)
    grad_hidden = cot_wide + grad_mid_in
    grad_attn_low = gather_rows(to_low(grad_hidden))
    grad_mixed = to_low(matmul_t(grad_attn_low, w_out))
    out_grad = outer_sum(mixed_tok, grad_attn_low)
    grad_query_tok, grad_keys_tok, grad_values_tok, grad_scores = batched_back(
        query_tok, key_all_tok, value_all_tok, full_bias, allowed_tok, lse_tok, grad_mixed
    )
    bias_grad = bias_sums(grad_scores[..., : 2 * BLOCK], rel_table)
    grad_key_next, grad_value_next = (
        passed_along(grad_keys_tok[:, :BLOCK].astype(jnp.bfloat16), "seq", -1).astype(jnp.float32),
        passed_along(grad_values_tok[:, :BLOCK].astype(jnp.bfloat16), "seq", -1).astype(
            jnp.float32
        ),
    )
    grad_key_own = grad_keys_tok[:, BLOCK : 2 * BLOCK] + grad_key_next
    grad_value_own = grad_values_tok[:, BLOCK : 2 * BLOCK] + grad_value_next
    grad_key_st_tok = grad_keys_tok[:, 2 * BLOCK :]
    grad_value_st_tok = grad_values_tok[:, 2 * BLOCK :]
    cot_rows = state_cot[:, 0].astype(jnp.float32)
    wide_zero = jnp.zeros((seq_count, BLOCK, width_local), jnp.float32)
    stored_back = (zeros_rows, wide_zero, wide_zero)
    totals_start = (
        jnp.zeros((D, width_local), jnp.float32),
        jnp.zeros((D, width_local), jnp.float32),
        jnp.zeros((D, width_local), jnp.float32),
        jnp.zeros((width_local, D), jnp.float32),
        jnp.zeros((D,), jnp.float32),
        jnp.zeros((D,), jnp.float32),
    )

    def backward_turn(turn_index, carry):
        incoming, stored_now, totals_now = carry
        order_index = turn_index - (chain_length - 1 - block_index)
        is_live = (order_index >= 0) & (order_index < seq_count)
        picked = jnp.clip(order_index, 0, seq_count - 1)

        def slice_one(whole_array):
            return lax.dynamic_slice_in_dim(whole_array, picked, 1, 0)

        grad_out = slice_one(cot_rows) + incoming
        kept_one = tuple((slice_one(kept_array) for kept_array in kept))
        grad_in, block_one, parts_one = state_backward(
            grad_out,
            slice_one(state_in),
            kept_one,
            slice_one(key_tok),
            slice_one(value_tok),
            slice_one(valid_keys),
            slice_one(grad_key_st_tok),
            slice_one(grad_value_st_tok),
        )
        fresh = (grad_in,) + block_one
        stored_now = tuple(
            (
                jnp.where(
                    is_live,
                    lax.dynamic_update_slice_in_dim(whole_array, fresh_part, picked, 0),
                    whole_array,
                )
                for whole_array, fresh_part in zip(stored_now, fresh)
            )
        )
        totals_now = tuple(
            (
                total_now + jnp.where(is_live, part_now, 0.0)
                for total_now, part_now in zip(totals_now, parts_one)
            )
        )
        return (pass_back(grad_in), stored_now, totals_now)

    incoming_start = jnp.zeros((1,) + init_state.shape, jnp.float32)
    _, stored_done, weight_parts = lax.fori_loop(
        0, chain_length + seq_count - 1, backward_turn, (incoming_start, stored_back, totals_start)
    )
    grad_in_all, grad_key_blk, grad_value_blk = stored_done
    query_low = to_low(grad_query_tok)
    key_low = to_low(grad_key_own + grad_key_blk)
    value_low = to_low(grad_value_own + grad_value_blk)
    query_grad = outer_sum(tokens_low, query_low)
    key_grad = outer_sum(tokens_low, key_low) + weight_parts[1]
    value_grad = outer_sum(tokens_low, value_low) + weight_parts[2]
    grad_tokens = sum_rows(
        matmul_t(query_low, w_query) + matmul_t(key_low, w_key) + matmul_t(value_low, w_value)
    )
    grad_in_norm, attn_gain_grad = norm_back(inputs_wide, attn_gain, grad_tokens)
    inputs_grad = grad_hidden + grad_in_norm
    state_part = jnp.where(is_first, jnp.sum(grad_in_all, axis=0), 0.0)
    gains = lax.psum(
        jnp.stack([attn_gain_grad, weight_parts[4], mlp_gain_grad, weight_parts[5]]), "tensor"
    )
    totals = (
        lax.psum(query_grad.astype(jnp.bfloat16), ("dp", "seq")).astype(jnp.float32),
        lax.psum(key_grad.astype(jnp.bfloat16), ("dp", "seq")).astype(jnp.float32),
        lax.psum(value_grad.astype(jnp.bfloat16), ("dp", "seq")).astype(jnp.float32),
        lax.psum(out_grad.astype(jnp.bfloat16), ("dp", "seq")).astype(jnp.float32),
        lax.psum(weight_parts[0].astype(jnp.bfloat16), ("dp", "seq")).astype(jnp.float32),
        lax.psum(weight_parts[3].astype(jnp.bfloat16), ("dp", "seq")).astype(jnp.float32),
        lax.psum(up_grad.astype(jnp.bfloat16), ("dp", "seq")).astype(jnp.float32),
        lax.psum(down_grad.astype(jnp.bfloat16), ("dp", "seq")).astype(jnp.float32),
        lax.psum(bias_grad.astype(jnp.bfloat16), ("dp", "seq")).astype(jnp.float32),
        lax.psum(state_part.astype(jnp.bfloat16), ("dp", "seq")).astype(jnp.float32),
        lax.psum(gains.astype(jnp.bfloat16), ("dp", "seq")).astype(jnp.float32),
    )
    gain_total = totals[10]
    return (
        tokens_out,
        state_out[:, None],
        inputs_grad,
        totals[9],
        gain_total[0],
        gain_total[1],
        gain_total[2],
        totals[0],
        totals[1],
        totals[2],
        totals[3],
        totals[4],
        totals[5],
        totals[6],
        totals[7],
        totals[8],
        gain_total[3],
    )


def chosen_body(mesh):
    if mesh.shape["seq"] == 4 and mesh.shape["tensor"] == 4:
        return line_body
    return body


MESH_ID = pl.DeviceIdType.MESH
ROWS = 128
CHUNKS = BLOCK // ROWS
LINE = 8
SCALE = HEAD_DIM ** (-0.5)
VMEM_LIMIT = 60 * 1024 * 1024


def dot_nn(left, right):
    return lax.dot_general(left, right, (((1,), (0,)), ((), ())), preferred_element_type=jnp.float32)


def dot_nt(left, right):
    return lax.dot_general(left, right, (((1,), (1,)), ((), ())), preferred_element_type=jnp.float32)


def dot_tn(left, right):
    return lax.dot_general(left, right, (((0,), (0,)), ((), ())), preferred_element_type=jnp.float32)


def line_place():
    place = lax.axis_index("seq")
    half = lax.rem(place, 2)
    rank = lax.axis_index("tensor")
    return place, half, rank


def span(index, size):
    return pl.ds(pl.multiple_of(index * size, size), size)


def fetch_pieces(kept, first, rows, target, sem):
    for owner in range(8):
        pltpu.make_async_copy(
            kept.at[owner, :, pl.ds(first, rows), :], target.at[:, owner], sem
        ).start()


def fetched(target, sem):
    pltpu.make_async_copy(target, target, sem).wait()


def norm_parts(rows):
    centered = rows - jnp.mean(rows, axis=-1, keepdims=True)
    spread = jnp.mean(centered * centered, axis=-1, keepdims=True)
    return centered, lax.rsqrt(spread + norm_eps)


def token_masks(scal, block_id, first_row):
    length = scal[0]
    start = scal[1 + block_id]
    row = lax.broadcasted_iota(jnp.int32, (ROWS, BLOCK), 0) + first_row
    col = lax.broadcasted_iota(jnp.int32, (ROWS, BLOCK), 1)
    prev_limit = jnp.where(block_id > 0, length - (block_id - 1) * BLOCK, 0)
    prev_ok = (col > row) & (col < prev_limit)
    row_in = (row >= start) & (row < start + SEG)
    col_in = (col >= start) & (col < start + SEG)
    cur_ok = ((col <= row) | (row_in & col_in)) & (col < length - block_id * BLOCK)
    return prev_ok, cur_ok


def state_block_mask(scal, block_id):
    col = lax.broadcasted_iota(jnp.int32, (ROWS, BLOCK), 1)
    return col < scal[0] - block_id * BLOCK


def softmax_of(score_parts):
    top = jnp.max(score_parts[0], axis=-1, keepdims=True)
    for part in score_parts[1:]:
        top = jnp.maximum(top, jnp.max(part, axis=-1, keepdims=True))
    raised = [jnp.exp(part - top) for part in score_parts]
    total = jnp.sum(raised[0], axis=-1, keepdims=True)
    for part in raised[1:]:
        total = total + jnp.sum(part, axis=-1, keepdims=True)
    inverse = 1.0 / total
    return [to_low(part * inverse) for part in raised], top + jnp.log(total)


def token_scores(scal, qkv, qkvst, bias, block_id, chunk):
    rows = span(chunk, ROWS)
    prev_id = jnp.maximum(block_id - 1, 0)
    query = qkv[block_id, rows, 0:128]
    prev_ok, cur_ok = token_masks(scal, block_id, chunk * ROWS)
    prev = dot_nt(query, qkv[prev_id, :, 128:256]) * SCALE + bias[rows, 0:BLOCK]
    cur = dot_nt(query, qkv[block_id, :, 128:256]) * SCALE + bias[rows, BLOCK : 2 * BLOCK]
    stt = dot_nt(query, qkvst[block_id, :, 128:256]) * SCALE
    prev = jnp.where(prev_ok, prev, masked_score)
    cur = jnp.where(cur_ok, cur, masked_score)
    return query, (prev, cur, stt)


def state_scores(scal, qkv, qkvst, block_id, chunk):
    query = qkvst[block_id, span(chunk, ROWS), 0:128]
    tok = dot_nt(query, qkv[block_id, :, 128:256]) * SCALE
    tok = jnp.where(state_block_mask(scal, block_id), tok, masked_score)
    stt = dot_nt(query, qkvst[block_id, :, 128:256]) * SCALE
    return query, (tok, stt)


def forward_kernel(
    scal, qkv, kept, w_state, vecs, bias,
    o_out, lse_out, state_rows, state_low, qkvst, lse_st, os_rows,
    held, os_all, w_sout, start, send_sem, pass_sem, recv_sem, local_sem,
):
    place, half, rank = line_place()
    fetch_pieces(kept, 32, 16, start, local_sem.at[0])
    fetch_pieces(kept, 0, 32, w_sout, local_sem.at[1])
    partner = place + 1 - 2 * half
    head = 2 * rank + half
    peers = [lax.rem(rank + step, 4) for step in (1, 2, 3)]
    barrier = pltpu.get_barrier_semaphore()
    for peer in peers:
        pl.semaphore_signal(
            barrier, inc=1, device_id={"seq": place, "tensor": peer}, device_id_type=MESH_ID
        )
    pl.semaphore_signal(
        barrier, inc=1, device_id={"seq": partner, "tensor": rank}, device_id_type=MESH_ID
    )
    fetched(start, local_sem.at[0])
    held[...] = start[...].reshape(STATES, D).astype(jnp.float32)
    gain = vecs[0:1, :]
    gate = vecs[1:2, :]
    pl.semaphore_wait(barrier, 4)
    fetched(w_sout, local_sem.at[1])

    def carry_copy(block_id, which, sem, seq_to, rank_to):
        part = os_all.at[block_id, :, span(which, 128)]
        return pltpu.make_async_remote_copy(
            src_ref=part,
            dst_ref=part,
            send_sem=sem,
            recv_sem=recv_sem.at[block_id, which],
            device_id={"seq": seq_to, "tensor": rank_to},
            device_id_type=MESH_ID,
        )

    def one_block(block_id, _):
        def project(chunk, _):
            rows = span(chunk, ROWS)
            centered, scale = norm_parts(held[rows, :])
            low = to_low(centered * scale * gain)
            state_low[block_id, rows, :] = low
            qkvst[block_id, rows, :] = to_low(dot_nn(low, w_state[...]))
            return 0

        lax.fori_loop(0, CHUNKS, project, 0)

        def attend_state(chunk, _):
            rows = span(chunk, ROWS)
            _, parts = state_scores(scal, qkv, qkvst, block_id, chunk)
            (w_tok, w_stt), total = softmax_of(parts)
            mixed = dot_nn(w_tok, qkv[block_id, :, 256:384]) + dot_nn(
                w_stt, qkvst[block_id, :, 256:384]
            )
            os_all[block_id, rows, span(head, 128)] = to_low(mixed)
            lse_st[block_id, rows, :] = total
            return 0

        lax.fori_loop(0, CHUNKS, attend_state, 0)
        for slot, peer in enumerate(peers):
            carry_copy(block_id, head, send_sem.at[block_id, slot], place, peer).start()
        carry_copy(block_id, head, send_sem.at[block_id, 3], partner, rank).start()

        def attend_token(chunk, _):
            rows = span(chunk, ROWS)
            _, parts = token_scores(scal, qkv, qkvst, bias, block_id, chunk)
            weights, total = softmax_of(parts)
            prev_id = jnp.maximum(block_id - 1, 0)
            mixed = (
                dot_nn(weights[0], qkv[prev_id, :, 256:384])
                + dot_nn(weights[1], qkv[block_id, :, 256:384])
                + dot_nn(weights[2], qkvst[block_id, :, 256:384])
            )
            o_out[block_id, rows, :] = to_low(mixed)
            lse_out[block_id, rows, :] = total
            return 0

        lax.fori_loop(0, CHUNKS, attend_token, 0)
        for slot, peer in enumerate(peers):
            other = 2 * peer + half
            carry_copy(block_id, other, send_sem.at[block_id, slot], place, peer).wait_recv()
            carry_copy(block_id, other, pass_sem.at[block_id, slot], partner, rank).start()
        for other_rank in range(4):
            carry_copy(
                block_id, 2 * other_rank + 1 - half, send_sem.at[block_id, 3], partner, rank
            ).wait_recv()

        def update(chunk, _):
            rows = span(chunk, ROWS)
            change = dot_nn(os_all[block_id, rows, :], w_sout[...].reshape(D, D))
            held[rows, :] = gate * held[rows, :] + (1.0 - gate) * change
            return 0

        lax.fori_loop(0, CHUNKS, update, 0)
        state_rows[block_id] = held[span(rank, 128), :]
        os_rows[block_id] = os_all[block_id, span(head, 64), :]
        return 0

    lax.fori_loop(0, 4, one_block, 0)

    def drain(block_id, _):
        for slot, peer in enumerate(peers):
            carry_copy(block_id, head, send_sem.at[block_id, slot], place, peer).wait_send()
            other = 2 * peer + half
            carry_copy(block_id, other, pass_sem.at[block_id, slot], partner, rank).wait_send()
        carry_copy(block_id, head, send_sem.at[block_id, 3], partner, rank).wait_send()
        return 0

    lax.fori_loop(0, 4, drain, 0)


def any_specs(count):
    return [pl.BlockSpec(memory_space=pl.ANY)] * count


def vmem_specs(count):
    return [pl.BlockSpec(memory_space=pltpu.VMEM)] * count


def forward_chain(scal, qkv, kept, w_state, vecs, bias):
    low, wide = jnp.bfloat16, jnp.float32
    shapes = (
        ((4, BLOCK, 128), low),
        ((4, BLOCK, 1), wide),
        ((4, 128, D), wide),
        ((4, STATES, D), low),
        ((4, STATES, 384), low),
        ((4, STATES, 1), wide),
        ((4, 64, D), low),
    )
    return pl.pallas_call(
        forward_kernel,
        out_shape=[jax.ShapeDtypeStruct(*one) for one in shapes],
        in_specs=[pl.BlockSpec(memory_space=pltpu.SMEM)]
        + vmem_specs(1)
        + any_specs(1)
        + vmem_specs(3),
        out_specs=vmem_specs(7),
        scratch_shapes=[
            pltpu.VMEM((STATES, D), wide),
            pltpu.VMEM((4, STATES, D), low),
            pltpu.VMEM((4, 8, 32, D), low),
            pltpu.VMEM((4, 8, 16, D), low),
            pltpu.SemaphoreType.DMA((4, 4)),
            pltpu.SemaphoreType.DMA((4, 3)),
            pltpu.SemaphoreType.DMA((4, 8)),
            pltpu.SemaphoreType.DMA((2,)),
        ],
        compiler_params=pltpu.CompilerParams(
            collective_id=1, has_side_effects=True, vmem_limit_bytes=VMEM_LIMIT
        ),
        cost_estimate=pl.CostEstimate(flops=20000000000, bytes_accessed=20000000, transcendentals=0),
        name="forward_chain",
    )(scal, qkv, kept, w_state, vecs, bias)


def backward_kernel(
    scal, qkv, d_o, lse_tok, qkvst, lse_st, state_rows, begin, cots, back, kept, vecs, bias,
    d_qkv, d_qkvst, du_rows, d_start, sums, dz_sum, state_out,
    key_acc, value_acc, st_key, st_value, dos_rows, dos_got, d_got, grad_in,
    states, w_back, w_sout, send_sem, recv_sem, local_sem, side_sem,
):
    place, half, rank = line_place()
    own_rows = pl.ds(pl.multiple_of(half * 64, 64), 64)
    loads = [
        pltpu.make_async_copy(
            state_rows.at[:, own_rows, :], states.at[pl.ds(1, 4)], local_sem.at[0]
        ),
        pltpu.make_async_copy(
            state_rows.at[place], state_out.at[place // 2], local_sem.at[3]
        ),
    ]
    for one in loads:
        one.start()
    fetch_pieces(kept, 0, 32, w_sout, local_sem.at[1])
    for owner in range(8):
        pltpu.make_async_copy(
            back.at[owner], w_back.at[:, owner // 4, :, owner % 4], local_sem.at[2]
        ).start()
    states[0] = to_low(begin[own_rows, :]).astype(jnp.float32)
    head = 2 * rank + half
    peers = []
    for step in range(1, LINE):
        other = lax.rem(head + step, LINE)
        peers.append((other, place - half + lax.rem(other, 2), other // 2))
    barrier = pltpu.get_barrier_semaphore()
    for _, seq_to, rank_to in peers:
        pl.semaphore_signal(
            barrier, inc=1, device_id={"seq": seq_to, "tensor": rank_to}, device_id_type=MESH_ID
        )
    beside = lax.rem(place + 2, 4)
    pl.semaphore_signal(barrier, inc=1, device_id={"seq": beside}, device_id_type=MESH_ID)

    def aside(block_id, row_set):
        return pltpu.make_async_remote_copy(
            src_ref=state_rows.at[block_id],
            dst_ref=state_out.at[row_set],
            send_sem=side_sem.at[0],
            recv_sem=side_sem.at[1],
            device_id={"seq": beside},
            device_id_type=MESH_ID,
        )

    gain = vecs[0:1, :]
    gate = vecs[1:2, :]
    key_acc[...] = jnp.zeros_like(key_acc)
    value_acc[...] = jnp.zeros_like(value_acc)
    dz_sum[...] = jnp.zeros_like(dz_sum)
    sums[...] = jnp.zeros_like(sums)
    grad_in[...] = jnp.zeros_like(grad_in)

    def back_parts(parts, total, grad, values):
        weights = [jnp.exp(part - total) for part in parts]
        d_weights = [dot_nt(grad, value) for value in values]
        inner = jnp.sum(weights[0] * d_weights[0], axis=-1, keepdims=True)
        for one, other in zip(weights[1:], d_weights[1:]):
            inner = inner + jnp.sum(one * other, axis=-1, keepdims=True)
        d_scores = [to_low(one * (other - inner)) for one, other in zip(weights, d_weights)]
        return [to_low(one) for one in weights], d_scores

    def token_back(block_id):
        prev_id = jnp.maximum(block_id - 1, 0)
        st_key[...] = jnp.zeros_like(st_key)
        st_value[...] = jnp.zeros_like(st_value)

        def one_chunk(chunk, _):
            rows = span(chunk, ROWS)
            query, parts = token_scores(scal, qkv, qkvst, bias, block_id, chunk)
            grad = d_o[block_id, rows, :]
            keys = (qkv[prev_id, :, 128:256], qkv[block_id, :, 128:256], qkvst[block_id, :, 128:256])
            values = (
                qkv[prev_id, :, 256:384], qkv[block_id, :, 256:384], qkvst[block_id, :, 256:384]
            )
            weights, d_scores = back_parts(parts, lse_tok[block_id, rows, :], grad, values)
            d_query = dot_nn(d_scores[0], keys[0])
            d_query = d_query + dot_nn(d_scores[1], keys[1]) + dot_nn(d_scores[2], keys[2])
            d_qkv[block_id, rows, 0:128] = to_low(d_query * SCALE)
            key_acc[prev_id] += dot_tn(d_scores[0], query) * SCALE
            value_acc[prev_id] += dot_tn(weights[0], grad)
            key_acc[block_id] += dot_tn(d_scores[1], query) * SCALE
            value_acc[block_id] += dot_tn(weights[1], grad)
            st_key[...] += dot_tn(d_scores[2], query) * SCALE
            st_value[...] += dot_tn(weights[2], grad)
            dz_sum[rows, 0:BLOCK] += d_scores[0].astype(jnp.float32)
            dz_sum[rows, BLOCK : 2 * BLOCK] += d_scores[1].astype(jnp.float32)
            return 0

        lax.fori_loop(0, CHUNKS, one_chunk, 0)

    token_back(3)
    pl.semaphore_wait(barrier, LINE)
    aside(beside, place // 2).start()
    loads[0].wait()
    fetched(w_sout, local_sem.at[1])
    fetched(w_back, local_sem.at[2])

    def mixed_copy(block_id, slot, sender, other, seq_to, rank_to):
        return pltpu.make_async_remote_copy(
            src_ref=dos_rows.at[block_id, :, span(other, 128)],
            dst_ref=dos_got.at[block_id, span(sender, 64), :],
            send_sem=send_sem.at[0, block_id, slot],
            recv_sem=recv_sem.at[0, block_id, sender],
            device_id={"seq": seq_to, "tensor": rank_to},
            device_id_type=MESH_ID,
        )

    def grads_copy(block_id, slot, sender, other, seq_to, rank_to):
        return pltpu.make_async_remote_copy(
            src_ref=d_qkvst.at[block_id, span(other, 64), :],
            dst_ref=d_got.at[block_id, sender],
            send_sem=send_sem.at[1, block_id, slot],
            recv_sem=recv_sem.at[1, block_id, sender],
            device_id={"seq": seq_to, "tensor": rank_to},
            device_id_type=MESH_ID,
        )

    def one_block(turn, _):
        block_id = 3 - turn
        grad_out = grad_in[...] + cots[block_id].astype(jnp.float32)
        sums[0:1, :] += jnp.sum(
            grad_out * (states[block_id] - states[block_id + 1]), axis=0, keepdims=True
        ) * gate
        change = to_low((1.0 - gate) * grad_out)
        du_rows[block_id] = change
        dos_rows[block_id] = to_low(dot_nt(change, w_sout[...].reshape(D, D)))
        for slot, (other, seq_to, rank_to) in enumerate(peers):
            mixed_copy(block_id, slot, head, other, seq_to, rank_to).start()
        dos_got[block_id, span(head, 64), :] = dos_rows[block_id, :, span(head, 128)]
        for slot, (other, seq_to, rank_to) in enumerate(peers):
            mixed_copy(block_id, slot, other, other, seq_to, rank_to).wait_recv()

        def one_chunk(chunk, _):
            rows = span(chunk, ROWS)
            query, parts = state_scores(scal, qkv, qkvst, block_id, chunk)
            grad = dos_got[block_id, rows, :]
            keys = (qkv[block_id, :, 128:256], qkvst[block_id, :, 128:256])
            values = (qkv[block_id, :, 256:384], qkvst[block_id, :, 256:384])
            weights, d_scores = back_parts(parts, lse_st[block_id, rows, :], grad, values)
            d_query = dot_nn(d_scores[0], keys[0]) + dot_nn(d_scores[1], keys[1])
            d_qkvst[block_id, rows, 0:128] = to_low(d_query * SCALE)
            key_acc[block_id] += dot_tn(d_scores[0], query) * SCALE
            value_acc[block_id] += dot_tn(weights[0], grad)
            st_key[...] += dot_tn(d_scores[1], query) * SCALE
            st_value[...] += dot_tn(weights[1], grad)
            return 0

        lax.fori_loop(0, CHUNKS, one_chunk, 0)
        d_qkvst[block_id, :, 128:256] = to_low(st_key[...])
        d_qkvst[block_id, :, 256:384] = to_low(st_value[...])
        for slot, (other, seq_to, rank_to) in enumerate(peers):
            grads_copy(block_id, slot, head, other, seq_to, rank_to).start()
        d_got[block_id, head] = d_qkvst[block_id, span(head, 64), :]

        @pl.when(turn < 3)
        def _():
            token_back(block_id - 1)

        d_qkv[block_id, :, 128:256] = to_low(key_acc[block_id])
        d_qkv[block_id, :, 256:384] = to_low(value_acc[block_id])
        for slot, (other, seq_to, rank_to) in enumerate(peers):
            grads_copy(block_id, slot, other, other, seq_to, rank_to).wait_recv()
        d_low = dot_nn(d_got[block_id, 0], w_back[0, 0].reshape(384, D))
        for other in range(1, LINE):
            d_low = d_low + dot_nn(
                d_got[block_id, other], w_back[other // 2, other % 2].reshape(384, D)
            )
        centered, scale = norm_parts(states[block_id])
        normed = centered * scale
        sums[1:2, :] += jnp.sum(d_low * normed, axis=0, keepdims=True)
        lifted = d_low * gain
        grad_in[...] = gate * grad_out + scale * (
            lifted
            - jnp.mean(lifted, axis=-1, keepdims=True)
            - normed * jnp.mean(lifted * normed, axis=-1, keepdims=True)
        )
        return 0

    lax.fori_loop(0, 4, one_block, 0)
    d_start[...] = grad_in[...]

    def drain(block_id, _):
        for slot, (other, seq_to, rank_to) in enumerate(peers):
            mixed_copy(block_id, slot, head, other, seq_to, rank_to).wait_send()
            grads_copy(block_id, slot, head, other, seq_to, rank_to).wait_send()
        return 0

    lax.fori_loop(0, 4, drain, 0)
    loads[1].wait()
    aside(beside, place // 2).wait_send()
    aside(place, 1 - place // 2).wait_recv()


def backward_chain(
    scal, qkv, d_o, lse_tok, qkvst, lse_st, state_rows, begin, cots, back, kept, vecs, bias
):
    low, wide = jnp.bfloat16, jnp.float32
    shapes = (
        ((4, BLOCK, 384), low),
        ((4, STATES, 384), low),
        ((4, 64, D), low),
        ((64, D), wide),
        ((8, D), wide),
        ((BLOCK, 2 * BLOCK), wide),
        ((2, 128, D), wide),
    )
    return pl.pallas_call(
        backward_kernel,
        out_shape=[jax.ShapeDtypeStruct(*one) for one in shapes],
        in_specs=[pl.BlockSpec(memory_space=pltpu.SMEM)]
        + vmem_specs(5)
        + any_specs(1)
        + vmem_specs(2)
        + any_specs(2)
        + vmem_specs(2),
        out_specs=vmem_specs(6) + any_specs(1),
        scratch_shapes=[
            pltpu.VMEM((4, BLOCK, 128), wide),
            pltpu.VMEM((4, BLOCK, 128), wide),
            pltpu.VMEM((STATES, 128), wide),
            pltpu.VMEM((STATES, 128), wide),
            pltpu.VMEM((4, 64, D), low),
            pltpu.VMEM((4, STATES, 128), low),
            pltpu.VMEM((4, LINE, 64, 384), low),
            pltpu.VMEM((64, D), wide),
            pltpu.VMEM((5, 64, D), wide),
            pltpu.VMEM((4, 2, 3, 4, 32, D), low),
            pltpu.VMEM((4, 8, 32, D), low),
            pltpu.SemaphoreType.DMA((2, 4, LINE - 1)),
            pltpu.SemaphoreType.DMA((2, 4, LINE)),
            pltpu.SemaphoreType.DMA((4,)),
            pltpu.SemaphoreType.DMA((2,)),
        ],
        compiler_params=pltpu.CompilerParams(
            collective_id=2, has_side_effects=True, vmem_limit_bytes=VMEM_LIMIT
        ),
        cost_estimate=pl.CostEstimate(flops=40000000000, bytes_accessed=40000000, transcendentals=0),
        name="backward_chain",
    )(scal, qkv, d_o, lse_tok, qkvst, lse_st, state_rows, begin, cots, back, kept, vecs, bias)


def plane_place():
    place, half, rank = line_place()
    side = lax.axis_index("dp")
    return side, place, half, rank


def plane_index(side, place):
    return 4 * side + place


def plane_gather(buf, rows, send_sem, recv_sem):
    side, place, half, rank = plane_place()
    across, beside = 1 - side, lax.rem(place + 2, 4)
    core = place + 1 - 2 * half
    me = plane_index(side, place)
    at_x, at_y = plane_index(across, place), plane_index(side, beside)
    at_d = plane_index(across, beside)
    to_x = {"dp": across}
    to_y = {"seq": beside}
    to_c = {"seq": core}
    size = rows // 2

    def piece(owner, part, slot, target):
        view = buf.at[owner, pl.ds(part * size, size), :]
        return pltpu.make_async_remote_copy(
            src_ref=view,
            dst_ref=view,
            send_sem=send_sem.at[slot],
            recv_sem=recv_sem.at[owner, part],
            device_id=target,
            device_id_type=MESH_ID,
        )

    sent = []

    def send(owner, part, target):
        one = piece(owner, part, len(sent), target)
        sent.append(one)
        one.start()

    def arrived(owner, part):
        piece(owner, part, 0, to_c).wait_recv()

    send(me, 0, to_x)
    send(me, 1, to_y)
    send(me, 1, to_x)
    send(me, 0, to_y)
    send(me, 0, to_c)
    send(me, 1, to_c)
    yield
    arrived(at_x, 0)
    send(at_x, 0, to_y)
    arrived(at_y, 1)
    send(at_y, 1, to_x)
    send(at_x, 0, to_c)
    send(at_y, 1, to_c)
    yield
    arrived(at_x, 1)
    send(at_x, 1, to_c)
    arrived(at_y, 0)
    send(at_y, 0, to_c)
    yield
    arrived(at_d, 0)
    send(at_d, 0, to_c)
    arrived(at_d, 1)
    send(at_d, 1, to_c)
    yield
    for owner in (
        plane_index(side, core),
        plane_index(across, core),
        plane_index(side, lax.rem(core + 2, 4)),
        plane_index(across, lax.rem(core + 2, 4)),
    ):
        arrived(owner, 0)
        arrived(owner, 1)
    for one in sent:
        one.wait_send()


def run_all(*steps):
    waiting = list(steps)
    while waiting:
        for one in list(waiting):
            try:
                next(one)
            except StopIteration:
                waiting.remove(one)


def plane_scatter(part, core_got, near_got, far_got, total, rows, send_sem, recv_sem):
    side, place, half, rank = plane_place()
    across, beside = 1 - side, lax.rem(place + 2, 4)
    core = place + 1 - 2 * half
    me = plane_index(side, place)
    at_x, at_y = plane_index(across, place), plane_index(side, beside)
    at_d = plane_index(across, beside)
    size = rows // 2
    halves = (pl.ds(0, size), pl.ds(size, size))

    def moved(source, target_ref, slot, target):
        return pltpu.make_async_remote_copy(
            src_ref=source,
            dst_ref=target_ref,
            send_sem=send_sem.at[slot],
            recv_sem=recv_sem.at[slot],
            device_id=target,
            device_id_type=MESH_ID,
        )

    order = (at_d, at_x, at_y, me)
    swapped = (
        plane_index(across, lax.rem(core + 2, 4)),
        plane_index(across, core),
        plane_index(side, lax.rem(core + 2, 4)),
        plane_index(side, core),
    )
    first = [
        moved(part.at[owner], core_got.at[slot], slot, {"seq": core})
        for slot, owner in enumerate(swapped)
    ]
    for one in first:
        one.start()

    def add_into(owner, view, other):
        part[owner, view, :] = to_low(
            part[owner, view, :].astype(jnp.float32) + other.astype(jnp.float32)
        )

    near = [
        moved(part.at[at_d, halves[0], :], near_got.at[0], 4, {"dp": across}),
        moved(part.at[at_d, halves[1], :], near_got.at[1], 5, {"seq": beside}),
        moved(part.at[at_x, halves[0], :], near_got.at[2], 6, {"dp": across}),
        moved(part.at[at_y, halves[1], :], near_got.at[3], 7, {"seq": beside}),
    ]
    for slot, owner in enumerate(order):
        first[slot].wait_recv()
        for view in halves:
            add_into(owner, view, core_got[slot, view, :])
        if slot == 0:
            near[0].start()
            near[1].start()
        if slot == 1:
            near[2].start()
        if slot == 2:
            near[3].start()
    yield
    near[0].wait_recv()
    add_into(at_y, halves[0], near_got[0])
    far = [
        moved(part.at[at_y, halves[0], :], far_got.at[0], 8, {"seq": beside}),
        moved(part.at[at_x, halves[1], :], far_got.at[1], 9, {"dp": across}),
    ]
    far[0].start()
    near[1].wait_recv()
    add_into(at_x, halves[1], near_got[1])
    far[1].start()
    yield
    near[2].wait_recv()
    add_into(me, halves[0], near_got[2])
    near[3].wait_recv()
    add_into(me, halves[1], near_got[3])
    yield
    for slot, view in enumerate(halves):
        far[slot].wait_recv()
        total[view, :] = part[me, view, :].astype(jnp.float32) + far_got[slot].astype(jnp.float32)
    for one in first + near + far:
        one.wait_send()


def group_peers():
    place, half, rank = line_place()
    here = 4 * place + rank
    peers = []
    for step in range(1, 16):
        other = lax.rem(here + step, 16)
        peers.append((other, other // 4, lax.rem(other, 4)))
    return here, peers


def greet(peers):
    side = lax.axis_index("dp")
    barrier = pltpu.get_barrier_semaphore()
    for _, seq_to, rank_to in peers:
        pl.semaphore_signal(
            barrier, inc=1, device_id={"seq": seq_to, "tensor": rank_to}, device_id_type=MESH_ID
        )
    pl.semaphore_signal(barrier, inc=1, device_id={"dp": 1 - side}, device_id_type=MESH_ID)
    pl.semaphore_wait(barrier, len(peers) + 1)


def middle_forward_kernel(
    mixed, tokens, kept, vecs,
    hidden, mixed_rows, mid_all,
    w_out, send_sem, recv_sem, ring_send, ring_recv, local_sem,
):
    fetch_pieces(kept, 48, 32, w_out, local_sem.at[0])
    side, place, half, rank = plane_place()
    mine = place // 2
    head = 2 * rank + half
    here, peers = group_peers()
    greet(peers)

    def rows_copy(slot, sender, seq_from, rank_from, seq_to, rank_to):
        return pltpu.make_async_remote_copy(
            src_ref=mixed.at[seq_to, span(rank_to, 128), :],
            dst_ref=mixed_rows.at[
                seq_from // 2, :, span(2 * rank_from + lax.rem(seq_from, 2), 128)
            ],
            send_sem=send_sem.at[slot],
            recv_sem=recv_sem.at[sender],
            device_id={"seq": seq_to, "tensor": rank_to},
            device_id_type=MESH_ID,
        )

    for slot, (_, seq_to, rank_to) in enumerate(peers):
        rows_copy(slot, here, place, rank, seq_to, rank_to).start()
    mixed_rows[mine, :, span(head, 128)] = mixed[place, span(rank, 128), :]
    for slot, (other, seq_to, rank_to) in enumerate(peers):
        rows_copy(slot, other, seq_to, rank_to, seq_to, rank_to).wait_recv()
    me = plane_index(side, place)
    gain = vecs[2:3, :]
    fetched(w_out, local_sem.at[0])

    def one(which, _):
        added = dot_nn(mixed_rows[which], w_out[...].reshape(D, D)) + tokens[which].astype(jnp.float32)
        hidden[which] = added
        centered, scale = norm_parts(added)
        mid_all[me, span(which, 128), :] = to_low(centered * scale * gain)
        return 0

    lax.fori_loop(0, 2, one, 0)
    run_all(plane_gather(mid_all, 256, ring_send, ring_recv))
    for slot, (_, seq_to, rank_to) in enumerate(peers):
        rows_copy(slot, here, place, rank, seq_to, rank_to).wait_send()


def middle_forward(mixed, tokens, kept, vecs):
    low, wide = jnp.bfloat16, jnp.float32
    shapes = (((2, 128, D), wide), ((2, 128, D), low), ((8, 256, D), low))
    return pl.pallas_call(
        middle_forward_kernel,
        out_shape=[jax.ShapeDtypeStruct(*one) for one in shapes],
        in_specs=vmem_specs(2) + any_specs(1) + vmem_specs(1),
        out_specs=vmem_specs(3),
        scratch_shapes=[
            pltpu.VMEM((4, 8, 32, D), low),
            pltpu.SemaphoreType.DMA((15,)),
            pltpu.SemaphoreType.DMA((16,)),
            pltpu.SemaphoreType.DMA((16,)),
            pltpu.SemaphoreType.DMA((8, 2)),
            pltpu.SemaphoreType.DMA((1,)),
        ],
        compiler_params=pltpu.CompilerParams(
            collective_id=3, has_side_effects=True, vmem_limit_bytes=VMEM_LIMIT
        ),
        cost_estimate=pl.CostEstimate(
            flops=30000000000, bytes_accessed=30000000, transcendentals=0
        ),
        name="middle_forward",
    )(mixed, tokens, kept, vecs)


def middle_backward_kernel(
    part, hidden, cots, kept, vecs,
    d_hidden, d_low, d_line, sums,
    work, core_got, near_got, far_got, total, d_rows, w_out,
    ring_send, ring_recv, send_sem, recv_sem, local_sem,
):
    fetch_pieces(kept, 48, 32, w_out, local_sem.at[0])
    load = pltpu.make_async_copy(part, work, local_sem.at[1])
    load.start()
    side, place, half, rank = plane_place()
    mine = place // 2
    head = 2 * rank + half
    here, peers = group_peers()
    greet(peers)
    load.wait()
    fetched(w_out, local_sem.at[0])
    run_all(plane_scatter(work, core_got, near_got, far_got, total, 256, ring_send, ring_recv))
    gain = vecs[2:3, :]
    sums[...] = jnp.zeros_like(sums)

    def one(which, _):
        rows = span(which, 128)
        grad = total[rows, :]
        centered, scale = norm_parts(hidden[which])
        normed = centered * scale
        sums[0:1, :] += jnp.sum(grad * normed, axis=0, keepdims=True)
        lifted = grad * gain
        back = cots[which].astype(jnp.float32) + scale * (
            lifted
            - jnp.mean(lifted, axis=-1, keepdims=True)
            - normed * jnp.mean(lifted * normed, axis=-1, keepdims=True)
        )
        d_hidden[which] = back
        d_low[which] = to_low(back)
        d_rows[which] = to_low(dot_nt(to_low(back), w_out[...].reshape(D, D)))
        return 0

    lax.fori_loop(0, 2, one, 0)

    def line_copy(slot, sender, seq_from, rank_from, seq_to, rank_to):
        return pltpu.make_async_remote_copy(
            src_ref=d_rows.at[seq_to // 2, :, span(2 * rank_to + lax.rem(seq_to, 2), 128)],
            dst_ref=d_line.at[seq_from, span(rank_from, 128), :],
            send_sem=send_sem.at[slot],
            recv_sem=recv_sem.at[sender],
            device_id={"seq": seq_to, "tensor": rank_to},
            device_id_type=MESH_ID,
        )

    for slot, (_, seq_to, rank_to) in enumerate(peers):
        line_copy(slot, here, place, rank, seq_to, rank_to).start()
    d_line[place, span(rank, 128), :] = d_rows[mine, :, span(head, 128)]
    for slot, (other, seq_to, rank_to) in enumerate(peers):
        line_copy(slot, other, seq_to, rank_to, seq_to, rank_to).wait_recv()
    for slot, (_, seq_to, rank_to) in enumerate(peers):
        line_copy(slot, here, place, rank, seq_to, rank_to).wait_send()


def middle_backward(part, hidden, cots, kept, vecs):
    low, wide = jnp.bfloat16, jnp.float32
    shapes = (((2, 128, D), wide), ((2, 128, D), low), ((4, BLOCK, 128), low), ((8, D), wide))
    return pl.pallas_call(
        middle_backward_kernel,
        out_shape=[jax.ShapeDtypeStruct(*one) for one in shapes],
        in_specs=any_specs(1) + vmem_specs(2) + any_specs(1) + vmem_specs(1),
        out_specs=vmem_specs(4),
        scratch_shapes=[
            pltpu.VMEM((8, 256, D), low),
            pltpu.VMEM((4, 256, D), low),
            pltpu.VMEM((4, 128, D), low),
            pltpu.VMEM((2, 128, D), low),
            pltpu.VMEM((256, D), wide),
            pltpu.VMEM((2, 128, D), low),
            pltpu.VMEM((4, 8, 32, D), low),
            pltpu.SemaphoreType.DMA((10,)),
            pltpu.SemaphoreType.DMA((10,)),
            pltpu.SemaphoreType.DMA((15,)),
            pltpu.SemaphoreType.DMA((16,)),
            pltpu.SemaphoreType.DMA((2,)),
        ],
        compiler_params=pltpu.CompilerParams(
            collective_id=4, has_side_effects=True, vmem_limit_bytes=VMEM_LIMIT
        ),
        cost_estimate=pl.CostEstimate(
            flops=30000000000, bytes_accessed=30000000, transcendentals=0
        ),
        name="middle_backward",
    )(part, hidden, cots, kept, vecs)


WIDE = 2048


def opening_kernel(
    tokens, w_qkv, piece, vecs, line,
    rows_all, qkv, kept, table,
    stage, send_sem, core_sem, recv_sem, piece_send, piece_recv, ring_send, ring_recv,
):
    side, place, half, rank = plane_place()
    mine = place // 2
    core = place + 1 - 2 * half
    other = lax.rem(place + 2, 4)
    me = plane_index(side, place)
    extra = piece.shape[0]
    barrier = pltpu.get_barrier_semaphore()
    greeted = [{"tensor": lax.rem(rank + step, 4)} for step in (1, 2, 3)]
    greeted += [{"seq": core}, {"seq": other}, {"dp": 1 - side}]
    for target in greeted:
        pl.semaphore_signal(barrier, inc=1, device_id=target, device_id_type=MESH_ID)
    gain = vecs[3:4, :]

    def normed(which):
        centered, scale = norm_parts(tokens[which].astype(jnp.float32))
        return to_low(centered * scale * gain)

    def moved(block_id, origin, sem, target):
        view = rows_all.at[block_id, span(origin, 128), :]
        return pltpu.make_async_remote_copy(
            src_ref=view,
            dst_ref=view,
            send_sem=sem,
            recv_sem=recv_sem.at[block_id, origin],
            device_id=target,
            device_id_type=MESH_ID,
        )

    stage[...] = normed(1 - mine)
    kept[me, span(rank, extra), :] = piece[...]
    pl.semaphore_wait(barrier, 6)
    aside = pltpu.make_async_remote_copy(
        src_ref=stage,
        dst_ref=rows_all.at[place, span(rank, 128), :],
        send_sem=send_sem.at[0, 0, 3],
        recv_sem=recv_sem.at[place, rank],
        device_id={"seq": other},
        device_id_type=MESH_ID,
    )
    aside.start()
    rows_all[place, span(rank, 128), :] = normed(mine)
    right, left = {"tensor": lax.rem(rank + 1, 4)}, {"tensor": lax.rem(rank + 3, 4)}
    blocks = (place, other)

    def pass_on(which, distance):
        block_id = blocks[which]

        @pl.when((rank < 3) & (rank >= distance))
        def _():
            moved(block_id, jnp.maximum(rank - distance, 0), send_sem.at[which, distance, 0], right).start()

        @pl.when((rank > 0) & (rank + distance <= 3))
        def _():
            moved(block_id, jnp.minimum(rank + distance, 3), send_sem.at[which, distance, 1], left).start()

    def pass_done(which, distance):
        block_id = blocks[which]

        @pl.when((rank < 3) & (rank >= distance))
        def _():
            moved(block_id, jnp.maximum(rank - distance, 0), send_sem.at[which, distance, 0], right).wait_send()

        @pl.when((rank > 0) & (rank + distance <= 3))
        def _():
            moved(block_id, jnp.minimum(rank + distance, 3), send_sem.at[which, distance, 1], left).wait_send()

    def project(block_id, origin):
        view = span(origin, 128)
        qkv[block_id, view, :] = to_low(dot_nn(rows_all[block_id, view, :], w_qkv[...]))

    def rows_steps():
        pass_on(0, 0)
        moved(place, rank, core_sem.at[0, rank], {"seq": core}).start()
        project(place, rank)
        moved(other, rank, send_sem.at[0, 0, 3], {"seq": other}).wait_recv()
        pass_on(1, 0)
        moved(other, rank, core_sem.at[1, rank], {"seq": core}).start()
        project(other, rank)
        yield
        for distance in (1, 2, 3):
            for which in (0, 1):
                block_id = blocks[which]
                for way, ok, origin in (
                    (0, rank >= distance, jnp.maximum(rank - distance, 0)),
                    (1, rank + distance <= 3, jnp.minimum(rank + distance, 3)),
                ):

                    @pl.when(ok)
                    def _():
                        moved(block_id, origin, send_sem.at[which, distance, way], right).wait_recv()
                        if distance < 3:
                            if way == 0:

                                @pl.when(rank < 3)
                                def _():
                                    moved(
                                        block_id, origin, send_sem.at[which, distance, 0], right
                                    ).start()

                            else:

                                @pl.when(rank > 0)
                                def _():
                                    moved(
                                        block_id, origin, send_sem.at[which, distance, 1], left
                                    ).start()

                        moved(block_id, origin, core_sem.at[which, origin], {"seq": core}).start()
                        project(block_id, origin)

                yield
        for which, block_id in enumerate((core, lax.rem(core + 2, 4))):
            for origin in range(4):
                moved(block_id, origin, core_sem.at[which, origin], {"seq": core}).wait_recv()
                project(block_id, origin)
        for which in (0, 1):
            for distance in (0, 1, 2):
                pass_done(which, distance)
            for origin in range(4):
                moved(blocks[which], origin, core_sem.at[which, origin], {"seq": core}).wait_send()

    def piece_move(slot, origin, target):
        view = kept.at[me, span(origin, extra), :]
        return pltpu.make_async_remote_copy(
            src_ref=view,
            dst_ref=view,
            send_sem=piece_send.at[slot],
            recv_sem=piece_recv.at[origin],
            device_id=target,
            device_id_type=MESH_ID,
        )

    def piece_steps():
        for slot in range(3):
            piece_move(slot, rank, greeted[slot]).start()
        first = line[...]
        row = lax.broadcasted_iota(jnp.int32, (8, WIDE), 0)
        for step in (1, 2, 4):
            first = jnp.where(row // step % 2 == 1, pltpu.roll(first, step, 1), first)

        def one(group, _):
            table[span(group, 8), :] = pltpu.roll(first, 8 * group, 1)[:, 0 : 2 * BLOCK]
            return 0

        lax.fori_loop(0, BLOCK // 8, one, 0)
        yield
        for slot in range(3):
            piece_move(slot, lax.rem(rank + slot + 1, 4), greeted[slot]).wait_recv()
        for _ in plane_gather(kept, 4 * extra, ring_send, ring_recv):
            yield
        for slot in range(3):
            piece_move(slot, rank, greeted[slot]).wait_send()

    run_all(rows_steps(), piece_steps())
    aside.wait_send()


def opening(tokens, w_qkv, piece, vecs, line):
    low, wide = jnp.bfloat16, jnp.float32
    extra = piece.shape[0]
    shapes = (
        ((4, BLOCK, D), low),
        ((4, BLOCK, 384), low),
        ((8, 4 * extra, D), low),
        ((BLOCK, 2 * BLOCK), wide),
    )
    return pl.pallas_call(
        opening_kernel,
        out_shape=[jax.ShapeDtypeStruct(*one) for one in shapes],
        in_specs=vmem_specs(5),
        out_specs=vmem_specs(4),
        scratch_shapes=[
            pltpu.VMEM((128, D), low),
            pltpu.SemaphoreType.DMA((2, 4, 4)),
            pltpu.SemaphoreType.DMA((2, 4)),
            pltpu.SemaphoreType.DMA((4, 4)),
            pltpu.SemaphoreType.DMA((3,)),
            pltpu.SemaphoreType.DMA((4,)),
            pltpu.SemaphoreType.DMA((16,)),
            pltpu.SemaphoreType.DMA((8, 2)),
        ],
        compiler_params=pltpu.CompilerParams(
            collective_id=5, has_side_effects=True, vmem_limit_bytes=VMEM_LIMIT
        ),
        cost_estimate=pl.CostEstimate(
            flops=30000000000, bytes_accessed=30000000, transcendentals=0
        ),
        name="opening",
    )(tokens, w_qkv, piece, vecs, line)


def pair_sum(part, near_got, far_got, result, rows, send_sem, recv_sem):
    side, place, half, rank = plane_place()
    mine = place // 2
    across, beside = 1 - side, 1 - mine
    me = 2 * side + mine
    at_x, at_y, at_d = 2 * across + mine, 2 * side + beside, 2 * across + beside
    to_x, to_y = {"dp": across}, {"seq": lax.rem(place + 2, 4)}
    size = rows // 2
    views = (pl.ds(0, size), pl.ds(size, size))

    def moved(source, target_ref, slot, target):
        return pltpu.make_async_remote_copy(
            src_ref=source,
            dst_ref=target_ref,
            send_sem=send_sem.at[slot],
            recv_sem=recv_sem.at[slot],
            device_id=target,
            device_id_type=MESH_ID,
        )

    def add_into(owner, view, other):
        part[owner, view, :] = to_low(
            part[owner, view, :].astype(jnp.float32) + other.astype(jnp.float32)
        )

    near = [
        moved(part.at[at_d, views[0], :], near_got.at[0], 0, to_x),
        moved(part.at[at_d, views[1], :], near_got.at[1], 1, to_y),
        moved(part.at[at_x, views[0], :], near_got.at[2], 2, to_x),
        moved(part.at[at_y, views[1], :], near_got.at[3], 3, to_y),
    ]
    for one in near:
        one.start()
    yield
    near[0].wait_recv()
    add_into(at_y, views[0], near_got[0])
    far = [
        moved(part.at[at_y, views[0], :], far_got.at[0], 4, to_y),
        moved(part.at[at_x, views[1], :], far_got.at[1], 5, to_x),
    ]
    far[0].start()
    near[1].wait_recv()
    add_into(at_x, views[1], near_got[1])
    far[1].start()
    yield
    near[2].wait_recv()
    add_into(me, views[0], near_got[2])
    near[3].wait_recv()
    add_into(me, views[1], near_got[3])
    for slot, view in enumerate(views):
        far[slot].wait_recv()
        result[me, view, :] = to_low(
            part[me, view, :].astype(jnp.float32) + far_got[slot].astype(jnp.float32)
        )

    def given(owner, which, slot, target):
        view = result.at[owner, views[which], :]
        return moved(view, view, slot, target)

    own = [
        given(me, 0, 6, to_x),
        given(me, 1, 7, to_y),
        given(me, 1, 8, to_x),
        given(me, 0, 9, to_y),
    ]
    for one in own:
        one.start()
    yield
    given(at_x, 0, 6, to_x).wait_recv()
    last = [given(at_x, 0, 10, to_y), given(at_y, 1, 11, to_x)]
    last[0].start()
    given(at_y, 1, 7, to_y).wait_recv()
    last[1].start()
    yield
    given(at_x, 1, 8, to_x).wait_recv()
    given(at_y, 0, 9, to_y).wait_recv()
    given(at_d, 0, 10, to_y).wait_recv()
    given(at_d, 1, 11, to_x).wait_recv()
    for one in near + far + own + last:
        one.wait_send()


PAIR_ROWS = 640


def closing_kernel(
    d_qkv, w_qkv, tokens, d_hidden, vecs, rows_hbm, low_hbm, d_qkvst_hbm, os_hbm, du_hbm,
    d_start, dz_hbm, small, out_part,
    inputs_grad, pair_out, sout_out, small_out,
    rows_all, state_low, d_qkvst, os_rows, du_rows, dz_sum,
    leave, came, sums, got, final, cross, cross_got,
    pair_part, pair_near, pair_far,
    work, core_got, near_got, far_got, total, z_part, z_got,
    diag, small_z, small_p,
    line_send, line_recv, way_send, way_recv, pair_send, pair_recv, core_sem,
    ring_send, ring_recv, zs_send, zs_recv, gather_send, gather_recv, small_send, small_recv, local_sem,
):
    loads = [
        pltpu.make_async_copy(source, target, local_sem.at[slot])
        for slot, (source, target) in enumerate(
            (
                (rows_hbm, rows_all),
                (d_qkvst_hbm, d_qkvst),
                (low_hbm, state_low),
                (os_hbm, os_rows),
                (du_hbm, du_rows),
                (dz_hbm, dz_sum),
            )
        )
    ]
    for one in loads:
        one.start()
    side, place, half, rank = plane_place()
    mine = place // 2
    core = place + 1 - 2 * half
    other = lax.rem(place + 2, 4)
    me = plane_index(side, place)
    ranks = [lax.rem(rank + step, 4) for step in (1, 2, 3)]
    spots_of = [lax.rem(me + step, 8) for step in range(1, 8)]
    barrier = pltpu.get_barrier_semaphore()
    for target in ranks:
        pl.semaphore_signal(barrier, inc=1, device_id={"tensor": target}, device_id_type=MESH_ID)
    for target in spots_of:
        pl.semaphore_signal(
            barrier,
            inc=1,
            device_id={"dp": target // 4, "seq": lax.rem(target, 4)},
            device_id_type=MESH_ID,
        )
    gain = vecs[3:4, :]
    right, left = {"tensor": lax.rem(rank + 1, 4)}, {"tensor": lax.rem(rank + 3, 4)}

    def moved(source, target_ref, send, recv, target):
        return pltpu.make_async_remote_copy(
            src_ref=source,
            dst_ref=target_ref,
            send_sem=send,
            recv_sem=recv,
            device_id=target,
            device_id_type=MESH_ID,
        )

    def to_core(which):
        return moved(
            leave.at[which], came.at[which], line_send.at[which], line_recv.at[which], {"seq": core}
        )

    def crossing():
        return moved(cross, cross_got, line_send.at[2], line_recv.at[2], {"seq": other})

    near = rank // 2
    at_end = (rank == 0) | (rank == 3)

    def hop(way, which, target):
        return moved(
            sums.at[which, target],
            got.at[way, which, target],
            way_send.at[which, target],
            way_recv.at[way, which, target],
            {"tensor": lax.rem(rank + 5 - 2 * way, 4)},
        )

    def target_of(way, distance):
        return (1 - way) * (3 - distance) + way * distance

    def pass_first(which):
        @pl.when(at_end)
        def _():
            for distance in range(3):
                hop(near, which, target_of(near, distance)).start()

    def pass_on(way, which, distance):
        @pl.when(jnp.logical_not(at_end))
        def _():
            target = target_of(way, distance)
            hop(way, which, target).wait_recv()
            sums[which, target] = to_low(
                sums[which, target].astype(jnp.float32)
                + got[way, which, target].astype(jnp.float32)
            )
            hop(way, which, target).start()

    def finish(which):
        final[which] = sums[which, rank].astype(jnp.float32)

        @pl.when(rank > 0)
        def _():
            hop(0, which, rank).wait_recv()
            final[which] += got[0, which, rank].astype(jnp.float32)

        @pl.when(rank < 3)
        def _():
            hop(1, which, rank).wait_recv()
            final[which] += got[1, which, rank].astype(jnp.float32)

    def line_steps():
        for which, block_id in enumerate((lax.rem(core + 2, 4), core)):

            def partner(chunk, _):
                rows = span(chunk, ROWS)
                leave[which, rows, :] = to_low(dot_nt(d_qkv[block_id, rows, :], w_qkv[...]))
                return 0

            lax.fori_loop(0, CHUNKS, partner, 0)
            if which == 0:
                pl.semaphore_wait(barrier, 10)
            to_core(which).start()
        for which, block_id in enumerate((other, place)):
            to_core(which).wait_recv()

            def own(chunk, _):
                rows = span(chunk, ROWS)
                sums[which, chunk] = to_low(
                    dot_nt(d_qkv[block_id, rows, :], w_qkv[...])
                    + came[which, rows, :].astype(jnp.float32)
                )
                return 0

            lax.fori_loop(0, CHUNKS, own, 0)
            pass_first(which)
        yield
        for which in (0, 1):
            pass_on(near, which, 0)
            yield
            pass_on(near, which, 1)
            pass_on(1 - near, which, 0)
            yield
            finish(which)
            if which == 0:
                cross[...] = to_low(final[0])
                crossing().start()
            yield
        crossing().wait_recv()
        final[0] = cross_got[...].astype(jnp.float32)
        small_z[rank] = small[...]
        for which, row_set in ((1, mine), (0, 1 - mine)):
            grad = final[which]
            centered, scale = norm_parts(tokens[row_set].astype(jnp.float32))
            normed = centered * scale
            small_z[rank, 0:1, :] += jnp.sum(grad * normed, axis=0, keepdims=True)
            lifted = grad * gain
            inputs_grad[row_set] = d_hidden[row_set] + scale * (
                lifted
                - jnp.mean(lifted, axis=-1, keepdims=True)
                - normed * jnp.mean(lifted * normed, axis=-1, keepdims=True)
            )
        crossing().wait_send()
        for which in (0, 1):
            to_core(which).wait_send()
            for target in range(4):

                @pl.when(rank != target)
                def _():
                    hop(0, which, target).wait_send()

    def pair_steps():
        loads[0].wait()
        loads[1].wait()
        loads[2].wait()
        for chunk in range(4):
            if chunk < 3:
                first = 128 * chunk

                def one(block_id, acc):
                    acc = acc + dot_tn(d_qkv[block_id, :, first : first + 128], rows_all[block_id])
                    if chunk > 0:
                        acc = acc + dot_tn(
                            d_qkvst[block_id, :, first : first + 128], state_low[block_id]
                        )
                    return acc

            else:

                def one(block_id, acc):
                    return acc + dot_tn(d_qkvst[block_id, :, 0:128], state_low[block_id])

            acc = lax.fori_loop(0, 4, one, jnp.zeros((128, D), jnp.float32))
            low = to_low(acc)
            first = 128 * chunk
            while first < 128 * (chunk + 1):
                owner, inside = first // 160, first % 160
                size = min(160 - inside, 128 * (chunk + 1) - first)
                begin = first - 128 * chunk
                pair_part[owner, inside : inside + size, :] = low[begin : begin + size, :]
                first += size
        pair_part[3, 32:96, :] = to_low(d_start[...])
        pair_part[3, 96:160, :] = jnp.zeros((64, D), jnp.bfloat16)
        for _ in pair_sum(
            pair_part, pair_near, pair_far, pair_out.at[half], 160, pair_send, pair_recv
        ):
            yield
        full = moved(
            pair_out.at[half], pair_out.at[half], core_sem.at[0], core_sem.at[1], {"seq": core}
        )
        full.start()
        yield
        moved(
            pair_out.at[1 - half], pair_out.at[1 - half], core_sem.at[0], core_sem.at[1],
            {"seq": core},
        ).wait_recv()
        full.wait_send()

    def sout_steps():
        loads[3].wait()
        loads[4].wait()
        for head in range(LINE):
            low = to_low(dot_tn(os_rows[:, 128 * head : 128 * head + 128], du_rows[...]))
            for piece in range(4):
                work[
                    4 * (head % 2) + piece, 32 * (head // 2) : 32 * (head // 2) + 32, :
                ] = low[32 * piece : 32 * piece + 32, :]
        for _ in plane_scatter(
            work, core_got, near_got, far_got, total, 128, ring_send, ring_recv
        ):
            yield
        z_part[:, 0:32, :] = to_low(total[...]).reshape(4, 32, D)
        z_part[:, 32:64, :] = out_part[...].reshape(4, 32, D)
        out = [
            moved(
                z_part.at[target], z_got.at[rank], zs_send.at[slot], zs_recv.at[rank],
                {"tensor": target},
            )
            for slot, target in enumerate(ranks)
        ]
        for one in out:
            one.start()
        z_got[rank] = z_part[rank]
        yield
        for slot, target in enumerate(ranks):
            moved(
                z_part.at[target], z_got.at[target], zs_send.at[slot], zs_recv.at[target],
                {"tensor": target},
            ).wait_recv()
        acc = z_got[0].astype(jnp.float32)
        for target in range(1, 4):
            acc = acc + z_got[target].astype(jnp.float32)
        sout_out[me] = to_low(acc)
        for _ in plane_gather(sout_out, 64, gather_send, gather_recv):
            yield
        for one in out:
            one.wait_send()

    def diag_steps():
        loads[5].wait()
        diag[...] = jnp.zeros_like(diag)
        for part in range(4):

            def one(group, _):
                rows = dz_sum[span(group, 8), :]
                wide = jnp.concatenate(
                    [rows, jnp.zeros((8, WIDE - 2 * BLOCK), jnp.float32)], axis=1
                )
                diag[...] += pltpu.roll(wide, lax.rem(WIDE - 8 * group, WIDE), 1)
                return 0

            lax.fori_loop(16 * part, 16 * part + 16, one, 0)
            yield
        total_line = diag[...]
        row = lax.broadcasted_iota(jnp.int32, (8, WIDE), 0)
        for step in (1, 2, 4):
            total_line = jnp.where(
                row // step % 2 == 1, pltpu.roll(total_line, WIDE - step, 1), total_line
            )
        lane = lax.broadcasted_iota(jnp.int32, (8, WIDE), 1)
        offset = jnp.where(lane >= WIDE - BLOCK, lane - WIDE - BLOCK, lane - BLOCK)
        bucket_ids = bucket_of(offset)
        spot = lax.broadcasted_iota(jnp.int32, (1, 256), 1) - BUCKETS * (2 * rank + half)
        placed = jnp.zeros((1, 256), jnp.float32)
        for bucket_id in range(BUCKETS):
            chosen = jnp.where(bucket_ids == bucket_id, total_line, 0.0)
            value = jnp.sum(jnp.sum(chosen, axis=0, keepdims=True), axis=1, keepdims=True)
            placed = jnp.where(spot == bucket_id, value, placed)
        diag[0:1, 0:256] = placed

    extra = sout_steps()
    run_all(line_steps(), pair_steps(), extra, diag_steps(), extra)
    small_z[rank, 4:5, 0:256] = diag[0:1, 0:256]

    def small_over_z(slot, sender, target):
        return moved(
            small_z.at[sender], small_z.at[sender], small_send.at[slot], small_recv.at[sender],
            {"tensor": target},
        )

    for slot, target in enumerate(ranks):
        small_over_z(slot, rank, target).start()
    for slot, target in enumerate(ranks):
        small_over_z(slot, target, target).wait_recv()
    small_p[me] = small_z[0] + small_z[1] + small_z[2] + small_z[3]

    def small_over_plane(slot, sender, target):
        return moved(
            small_p.at[sender], small_p.at[sender], small_send.at[3 + slot],
            small_recv.at[4 + sender],
            {"dp": target // 4, "seq": lax.rem(target, 4)},
        )

    for slot, target in enumerate(spots_of):
        small_over_plane(slot, me, target).start()
    for slot, target in enumerate(spots_of):
        small_over_plane(slot, target, target).wait_recv()
    acc = small_p[0]
    for target in range(1, 8):
        acc = acc + small_p[target]
    small_out[...] = acc
    for slot, target in enumerate(ranks):
        small_over_z(slot, rank, target).wait_send()
    for slot, target in enumerate(spots_of):
        small_over_plane(slot, me, target).wait_send()


def closing(
    d_qkv, w_qkv, tokens, d_hidden, vecs, rows_all, state_low, d_qkvst, os_rows, du_rows,
    d_start, dz_sum, small, out_part,
):
    low, wide = jnp.bfloat16, jnp.float32
    shapes = (
        ((2, 128, D), wide),
        ((2, 4, PAIR_ROWS // 4, D), low),
        ((8, 64, D), low),
        ((8, D), wide),
    )
    dma = pltpu.SemaphoreType.DMA
    return pl.pallas_call(
        closing_kernel,
        out_shape=[jax.ShapeDtypeStruct(*one) for one in shapes],
        in_specs=vmem_specs(5) + any_specs(5) + vmem_specs(1) + any_specs(1) + vmem_specs(2),
        out_specs=vmem_specs(4),
        scratch_shapes=[
            pltpu.VMEM((4, BLOCK, D), low),
            pltpu.VMEM((4, BLOCK, D), low),
            pltpu.VMEM((4, BLOCK, 384), low),
            pltpu.VMEM((256, D), low),
            pltpu.VMEM((256, D), low),
            pltpu.VMEM((BLOCK, 2 * BLOCK), wide),
            pltpu.VMEM((2, BLOCK, D), low),
            pltpu.VMEM((2, BLOCK, D), low),
            pltpu.VMEM((2, 4, 128, D), low),
            pltpu.VMEM((2, 2, 4, 128, D), low),
            pltpu.VMEM((2, 128, D), wide),
            pltpu.VMEM((128, D), low),
            pltpu.VMEM((128, D), low),
            pltpu.VMEM((4, PAIR_ROWS // 4, D), low),
            pltpu.VMEM((4, PAIR_ROWS // 8, D), low),
            pltpu.VMEM((2, PAIR_ROWS // 8, D), low),
            pltpu.VMEM((8, 128, D), low),
            pltpu.VMEM((4, 128, D), low),
            pltpu.VMEM((4, 64, D), low),
            pltpu.VMEM((2, 64, D), low),
            pltpu.VMEM((128, D), wide),
            pltpu.VMEM((4, 64, D), low),
            pltpu.VMEM((4, 64, D), low),
            pltpu.VMEM((8, WIDE), wide),
            pltpu.VMEM((4, 8, D), wide),
            pltpu.VMEM((8, 8, D), wide),
            dma((3,)), dma((3,)), dma((2, 4)), dma((2, 2, 4)), dma((12,)), dma((12,)), dma((2,)),
            dma((10,)), dma((10,)), dma((3,)), dma((4,)), dma((16,)), dma((8, 2)), dma((10,)),
            dma((12,)), dma((6,)),
        ],
        compiler_params=pltpu.CompilerParams(
            collective_id=6, has_side_effects=True, vmem_limit_bytes=VMEM_LIMIT
        ),
        cost_estimate=pl.CostEstimate(
            flops=30000000000, bytes_accessed=30000000, transcendentals=0
        ),
        name="closing",
    )(
        d_qkv, w_qkv, tokens, d_hidden, vecs, rows_all, state_low, d_qkvst, os_rows, du_rows,
        d_start, dz_sum, small, out_part,
    )


def finish_kernel(
    pair, pair_tail, two, ff,
    query, key, value, squery, out, sout, up, down, state,
):
    step = pl.program_id(0)
    wide = jnp.float32
    up[...] = ff[0, 0].astype(wide).T
    down[...] = ff[0, 1].astype(wide)
    sout[...] = two[0, 0:32].astype(wide)
    out[...] = two[0, 32:64].astype(wide)
    for which, target in enumerate((query, key, value, squery)):

        @pl.when(step // 2 == which)
        def _():
            target[...] = pair[0].astype(wide).T

    @pl.when(step == 0)
    def _():
        state[...] = pair_tail[...].reshape(128, D).astype(wide)


def finish_grads(pair, two, ff):
    wide = jnp.float32
    turned = [
        pl.BlockSpec((D, 128), lambda i, w=which: (0, jnp.clip(i - 2 * w, 0, 1)))
        for which in range(4)
    ]
    square = jax.ShapeDtypeStruct((D, 256), wide)
    rows = jax.ShapeDtypeStruct((256, D), wide)
    whole = jax.ShapeDtypeStruct((D, D), wide)
    return pl.pallas_call(
        finish_kernel,
        grid=(8,),
        out_shape=[square] * 4 + [rows] * 2 + [whole] * 2 + [jax.ShapeDtypeStruct((128, D), wide)],
        in_specs=[
            pl.BlockSpec((1, 128, D), lambda i: (i % 2, i // 2, 0)),
            pl.BlockSpec((2, 64, D), lambda i: (0, 8, 0)),
            pl.BlockSpec((1, 64, D), lambda i: (i, 0, 0)),
            pl.BlockSpec((1, 2, 128, D), lambda i: (i, 0, 0, 0)),
        ],
        out_specs=turned
        + [pl.BlockSpec((32, D), lambda i: (i, 0))] * 2
        + [pl.BlockSpec((D, 128), lambda i: (0, i)), pl.BlockSpec((128, D), lambda i: (i, 0))]
        + [pl.BlockSpec((128, D), lambda i: (0, 0))],
        compiler_params=pltpu.CompilerParams(vmem_limit_bytes=VMEM_LIMIT),
        name="finish_grads",
    )(pair, pair, two, ff)


def swap_seq(value):
    return lax.all_to_all(value, "seq", 0, 0, tiled=False)


def line_body(
    inputs,
    seg_starts,
    lengths,
    init_state,
    attn_gain,
    state_gain,
    mlp_gain,
    w_query,
    w_key,
    w_value,
    w_out,
    w_squery,
    w_sout,
    w_up,
    w_down,
    rel_bias,
    gate_bias,
    out_cot,
    state_cot,
):
    low, wide = jnp.bfloat16, jnp.float32
    place = lax.axis_index("seq")
    half = lax.rem(place, 2)
    mine = place // 2
    plane = ("dp", "seq")
    spot = 4 * lax.axis_index("dp") + place
    head_of = lambda weight: lax.dynamic_slice_in_dim(weight, half * 128, 128, 1)
    gate_value = jax.nn.sigmoid(gate_bias)
    vecs = jnp.stack(
        [state_gain, gate_value, mlp_gain, attn_gain] + [jnp.zeros_like(gate_value)] * 4
    )
    offsets = jnp.arange(WIDE) - BLOCK
    offsets = jnp.where(offsets >= WIDE - 2 * BLOCK, offsets - WIDE, offsets)
    bucket_ids = bucket_of(offsets)
    one_hot = bucket_ids[:, None] == jnp.arange(BUCKETS)[None, :]
    my_bias = jnp.where(half == 0, rel_bias[:, 0], rel_bias[:, 1])
    bias_line = jnp.sum(jnp.where(one_hot, my_bias[None, :], 0.0), axis=1)
    segs = jnp.broadcast_to(jnp.repeat(seg_starts[:, 0], 2)[:, None, None], (4, 1, 128))
    segs = swap_seq(segs)[:, 0, 0]
    cots = swap_seq(state_cot.reshape(4, 64, D))
    cot_used = lax.all_gather(out_cot.reshape(256, D), plane, axis=0, tiled=True)

    w_qkv = jnp.concatenate([head_of(w_query), head_of(w_key), head_of(w_value)], axis=1)
    w_state = jnp.concatenate([head_of(w_squery), w_qkv[:, 128:]], axis=1)
    piece = jnp.concatenate(
        [
            lax.dynamic_slice_in_dim(w_sout, spot * 32, 32, 0),
            to_low(lax.dynamic_slice_in_dim(init_state, spot * 16, 16, 0)),
            lax.dynamic_slice_in_dim(w_out, spot * 32, 32, 0),
        ],
        axis=0,
    )
    rows_all, qkv, kept, bias = opening(
        inputs, w_qkv, piece, vecs, jnp.broadcast_to(bias_line[None, :], (8, WIDE))
    )
    kept = kept.reshape(8, 4, 80, D)

    ff_own = w_up.shape[1] // 8
    piece_of = lambda weight: lax.dynamic_slice_in_dim(weight, spot * 32, 32, 1).T
    pieces = jnp.concatenate(
        [
            piece_of(w_squery),
            piece_of(w_key),
            piece_of(w_value),
            lax.dynamic_slice_in_dim(w_up, spot * ff_own, ff_own, 1).T,
            lax.dynamic_slice_in_dim(w_down, spot * ff_own, ff_own, 0),
        ],
        axis=0,
    )
    qkv, pieces, segs = lax.optimization_barrier((qkv, pieces, segs))
    scal = jnp.concatenate([lax.dynamic_slice_in_dim(lengths, mine, 1, 0), segs])
    spread = lax.all_gather(pieces, "tensor", axis=0, tiled=True).reshape(4, 96 + 2 * ff_own, D)
    up_rows = spread[:, 96 : 96 + ff_own].reshape(4 * ff_own, D)
    down_rows = spread[:, 96 + ff_own :].reshape(4 * ff_own, D)

    mixed, lse_tok, state_rows, state_low, qkvst, lse_st, os_rows = forward_chain(
        scal, qkv, kept, w_state, vecs, bias
    )
    mixed, back_piece, cots = lax.optimization_barrier(
        (mixed, spread[:, 0:96].reshape(384, D), cots)
    )
    w_back = lax.all_gather(back_piece, plane, axis=0, tiled=True)
    hidden_in, mixed_rows, mid_all = middle_forward(mixed, inputs, kept, vecs)
    mid_low = mid_all.reshape(2048, D)
    pre_act = matmul_t(mid_low, up_rows)
    hidden_low = to_low(jax.nn.gelu(pre_act))
    grad_hidden_act = matmul_t(cot_used, down_rows)
    grad_pre = to_low(gelu_back(pre_act, grad_hidden_act))
    d_mid_part = to_low(matmul(grad_pre, up_rows))
    ff_grads = jnp.stack(
        [
            outer_sum(grad_pre, mid_low).astype(low).reshape(4, ff_own, D),
            outer_sum(hidden_low, cot_used).astype(low).reshape(4, ff_own, D),
        ],
        axis=1,
    )
    d_mid_part, w_back, ff_grads = lax.optimization_barrier((d_mid_part, w_back, ff_grads))
    ff_sum = lax.psum_scatter(
        ff_grads.reshape(8 * ff_own, D), "tensor", scatter_dimension=0, tiled=True
    )
    grad_hidden, grad_low, d_mixed, mlp_sums = middle_backward(
        d_mid_part.reshape(8, 256, D), hidden_in, out_cot, kept, vecs
    )
    mlp_part = to_low(matmul(hidden_low, down_rows))
    out_part = outer_sum(mixed_rows, grad_low).astype(low)
    out_part = out_part.reshape(4, 8, 32, D).transpose(1, 0, 2, 3).reshape(D, D)
    d_mixed, mlp_part, ff_sum, out_part = lax.optimization_barrier(
        (d_mixed, mlp_part, ff_sum, out_part)
    )
    ff_total = lax.all_gather(ff_sum, plane, axis=0, tiled=True).reshape(8, 2, ff_own, D)
    mlp_rows = lax.psum_scatter(mlp_part, plane, scatter_dimension=0, tiled=True)
    out_part = lax.psum_scatter(out_part, plane, scatter_dimension=0, tiled=True)

    d_qkv, d_qkvst, du_rows, d_start, sums, dz_sum, state_out = backward_chain(
        scal, qkv, d_mixed, lse_tok, qkvst, lse_st, state_rows, init_state, cots,
        w_back.reshape(8, 4, 3, 32, D), kept, vecs, bias,
    )
    d_qkv, ff_total, out_part = lax.optimization_barrier((d_qkv, ff_total, out_part))
    tokens_out = (hidden_in + mlp_rows.reshape(2, 128, D).astype(wide)).astype(low)
    small = jnp.concatenate(
        [jnp.zeros((1, D), wide), sums[1:2], mlp_sums[0:1], sums[0:1], jnp.zeros((4, D), wide)]
    )
    inputs_grad, pair, two_grads, small = closing(
        d_qkv, w_qkv, inputs, grad_hidden, vecs, rows_all, state_low, d_qkvst,
        os_rows.reshape(256, D), du_rows.reshape(256, D), d_start, dz_sum, small, out_part,
    )
    pair = pair.reshape(2, PAIR_ROWS, D)
    (
        query_grad, key_grad, value_grad, squery_grad, out_grad, sout_grad, up_grad, down_grad,
        state_grad,
    ) = finish_grads(pair, two_grads, ff_total)
    bias_grad = lax.dynamic_slice_in_dim(
        small[4, : LINE * BUCKETS].reshape(4, 2, BUCKETS), lax.axis_index("tensor"), 1, 0
    )[0].T
    return (
        tokens_out,
        state_out[:, None],
        inputs_grad,
        state_grad,
        small[0],
        small[1],
        small[2],
        query_grad,
        key_grad,
        value_grad,
        out_grad,
        squery_grad,
        sout_grad,
        up_grad,
        down_grad,
        bias_grad,
        small[3],
    )


def solution(mesh):
    return jax.shard_map(
        chosen_body(mesh),
        mesh=mesh,
        in_specs=(
            P("dp", ("seq", "tensor"), None),
            P("dp", "seq"),
            P("dp"),
            P("tensor", None),
            P(),
            P(),
            P(),
            P(None, "tensor"),
            P(None, "tensor"),
            P(None, "tensor"),
            P("tensor", None),
            P(None, "tensor"),
            P("tensor", None),
            P(None, "tensor"),
            P("tensor", None),
            P(None, "tensor"),
            P(),
            P("dp", ("seq", "tensor"), None),
            P("dp", "seq", "tensor", None),
        ),
        out_specs=(
            P("dp", ("seq", "tensor"), None),
            P("dp", "seq", "tensor", None),
            P("dp", ("seq", "tensor"), None),
            P("tensor", None),
            P(),
            P(),
            P(),
            P(None, "tensor"),
            P(None, "tensor"),
            P(None, "tensor"),
            P("tensor", None),
            P(None, "tensor"),
            P("tensor", None),
            P(None, "tensor"),
            P("tensor", None),
            P(None, "tensor"),
            P(),
        ),
        check_vma=False,
    )
```

```python
import jax
import jax.numpy as jnp
from jax import lax
from jax.experimental import pallas as pl
from jax.experimental.pallas import tpu as pltpu
from jax.sharding import PartitionSpec as P

D = 1024
HEAD_DIM = 128
STATES = 512
BLOCK = 512
SEG = 256
BUCKETS = 32


norm_eps = 1e-06
masked_score = -1e30
bucket_edges = (12, 16, 23, 32, 46, 64, 91)


def passed_along(value, axis, steps):
    count = lax.axis_size(axis)
    leading, last = (max(0, -steps), min(count, count - steps))
    return lax.ppermute(value, axis, [(source, source + steps) for source in range(leading, last)])


def bucket_of(relative):
    distance = jnp.abs(relative)
    far_bucket = 8 + sum(((distance >= boundary).astype(jnp.int32) for boundary in bucket_edges))
    near_far = jnp.where(distance < 8, distance, far_bucket)
    return near_far + 16 * (relative > 0).astype(jnp.int32)


def token_mask(seg_start, seq_length, block_index):
    positions = jnp.arange(BLOCK)
    offset = block_index * BLOCK
    prev_valid = (block_index > 0) & (offset - BLOCK + positions < seq_length)
    cur_valid = offset + positions < seq_length
    inside = (positions >= seg_start) & (positions < seg_start + SEG)
    prev_mask = (positions[None, :] > positions[:, None]) & prev_valid[None, :]
    cur_mask = (
        (positions[None, :] <= positions[:, None]) | inside[None, :] & inside[:, None]
    ) & cur_valid[None, :]
    state_mask = jnp.ones((BLOCK, STATES), jnp.bool_)
    return jnp.concatenate([prev_mask, cur_mask, state_mask], axis=1)


def state_mask_of(valid_blk):
    batch_count = valid_blk.shape[0]
    block_part = jnp.broadcast_to(valid_blk[:, None, :], (batch_count, STATES, BLOCK))
    return jnp.concatenate([block_part, jnp.ones((batch_count, STATES, STATES), jnp.bool_)], axis=2)


def layer_norm(values, gain_vec):
    centered = values - jnp.mean(values, axis=-1, keepdims=True)
    spread = jnp.mean(centered * centered, axis=-1, keepdims=True)
    return centered * lax.rsqrt(spread + norm_eps) * gain_vec


def norm_back(values, gain_vec, grad_out):
    _, pullback = jax.vjp(layer_norm, values, gain_vec)
    return pullback(grad_out)


def gelu_back(pre_act, grad_out):
    _, pullback = jax.vjp(jax.nn.gelu, pre_act)
    return pullback(grad_out)[0]


def to_low(array_in):
    return array_in.astype(jnp.bfloat16)


def matmul(left, right):
    return jnp.einsum("...k,kn->...n", left, right, preferred_element_type=jnp.float32)


def matmul_t(left, right):
    return jnp.einsum("...n,kn->...k", left, right, preferred_element_type=jnp.float32)


def outer_sum(left, right):
    left_flat = left.reshape(-1, left.shape[-1])
    right_flat = right.reshape(-1, right.shape[-1])
    return lax.dot_general(
        left_flat, right_flat, (((0,), (0,)), ((), ())), preferred_element_type=jnp.float32
    )


def gather_rows(values):
    return lax.all_gather(values, "tensor", axis=1, tiled=True)


def sum_rows(terms):
    return lax.psum_scatter(
        terms.astype(jnp.bfloat16), "tensor", scatter_dimension=1, tiled=True
    ).astype(jnp.float32)


def pass_state(rows_now):
    return passed_along(rows_now.astype(jnp.bfloat16), "seq", 1).astype(rows_now.dtype)


def pass_back(grad_now):
    return passed_along(grad_now.astype(jnp.bfloat16), "seq", -1).astype(grad_now.dtype)


def split_heads(rows_in):
    return rows_in.reshape(rows_in.shape[0], rows_in.shape[1] // HEAD_DIM, HEAD_DIM)


def score_block(query_rows, key_all, bias_all, allowed):
    scores = (
        jnp.einsum(
            "qhd,khd->hqk",
            split_heads(query_rows),
            split_heads(key_all),
            preferred_element_type=jnp.float32,
        )
        * HEAD_DIM ** (-0.5)
        + bias_all
    )
    return jnp.where(allowed[None], scores, masked_score)


def attend_forward(query_rows, key_all, value_all, bias_all, allowed):
    scores = score_block(query_rows, key_all, bias_all, allowed)
    row_max = jnp.max(scores, axis=-1, keepdims=True)
    exp_scores = jnp.exp(scores - row_max)
    row_total = jnp.sum(exp_scores, axis=-1, keepdims=True)
    weight_all = to_low(exp_scores / row_total)
    mixed_out = jnp.einsum(
        "hqk,khd->qhd", weight_all, split_heads(value_all), preferred_element_type=jnp.float32
    )
    return (
        to_low(mixed_out.reshape(query_rows.shape[0], -1)),
        (row_max + jnp.log(row_total))[..., 0],
    )


def attend_back(query_rows, key_all, value_all, bias_all, allowed, log_total, grad_mixed):
    scores = score_block(query_rows, key_all, bias_all, allowed)
    weight_all = jnp.where(allowed[None], jnp.exp(scores - log_total[..., None]), 0.0)
    grad_heads = split_heads(grad_mixed)
    grad_weight = jnp.einsum(
        "qhd,khd->hqk", grad_heads, split_heads(value_all), preferred_element_type=jnp.float32
    )
    row_inner = jnp.sum(weight_all * grad_weight, axis=-1, keepdims=True)
    grad_scores = to_low(weight_all * (grad_weight - row_inner))
    grad_query = jnp.einsum(
        "hqk,khd->qhd", grad_scores, split_heads(key_all), preferred_element_type=jnp.float32
    ) * HEAD_DIM ** (-0.5)
    grad_keys = jnp.einsum(
        "hqk,qhd->khd", grad_scores, split_heads(query_rows), preferred_element_type=jnp.float32
    ) * HEAD_DIM ** (-0.5)
    grad_values = jnp.einsum(
        "hqk,qhd->khd", to_low(weight_all), grad_heads, preferred_element_type=jnp.float32
    )
    return (
        grad_query.reshape(query_rows.shape[0], -1),
        grad_keys.reshape(key_all.shape[0], -1),
        grad_values.reshape(key_all.shape[0], -1),
        grad_scores,
    )


def bias_lookup(rel_bias, rel_table):
    table_heads = jnp.zeros((rel_bias.shape[1],) + rel_table.shape, jnp.float32)
    for bucket_id in range(BUCKETS):
        table_heads = table_heads + jnp.where(
            rel_table[None] == bucket_id, rel_bias[bucket_id][:, None, None], 0.0
        )
    return table_heads


def bias_sums(score_grad, rel_table):
    grad_wide = score_grad.astype(jnp.float32)
    columns = []
    for bucket_id in range(BUCKETS):
        columns.append(
            jnp.sum(jnp.where(rel_table[None, None] == bucket_id, grad_wide, 0.0), axis=(0, 2, 3))
        )
    return jnp.stack(columns, axis=0)


def body(
    inputs,
    seg_starts,
    lengths,
    init_state,
    attn_gain,
    state_gain,
    mlp_gain,
    w_query,
    w_key,
    w_value,
    w_out,
    w_squery,
    w_sout,
    w_up,
    w_down,
    rel_bias,
    gate_bias,
    out_cot,
    state_cot,
):
    seq_count = inputs.shape[0]
    chain_length = lax.axis_size("seq")
    block_index = lax.axis_index("seq")
    is_first = block_index == 0
    width_local = w_query.shape[1]
    head_count = width_local // HEAD_DIM
    gate_value = jax.nn.sigmoid(gate_bias)
    positions = jnp.arange(BLOCK)
    inputs_wide = inputs.astype(jnp.float32)
    tokens_low = gather_rows(to_low(layer_norm(inputs_wide, attn_gain)))
    query_tok = to_low(matmul(tokens_low, w_query))
    key_tok = to_low(matmul(tokens_low, w_key))
    value_tok = to_low(matmul(tokens_low, w_value))
    key_prev, value_prev = passed_along((key_tok, value_tok), "seq", 1)
    valid_keys = (block_index * BLOCK + positions)[None, :] < lengths[:, None]
    batched_attend = jax.vmap(attend_forward, in_axes=(0, 0, 0, None, 0))
    batched_back = jax.vmap(attend_back, in_axes=(0, 0, 0, None, 0, 0, 0))

    def state_forward(state_rows, key_blk, value_blk, valid_blk):
        state_low = lax.all_gather(
            to_low(layer_norm(state_rows, state_gain)), "tensor", axis=1, tiled=True
        )
        query_st = to_low(matmul(state_low, w_squery))
        key_st = to_low(matmul(state_low, w_key))
        value_st = to_low(matmul(state_low, w_value))
        key_all = jnp.concatenate([key_blk, key_st], axis=1)
        value_all = jnp.concatenate([value_blk, value_st], axis=1)
        mixed_st, lse_st = batched_attend(
            query_st, key_all, value_all, 0.0, state_mask_of(valid_blk)
        )
        update = lax.psum_scatter(
            matmul(mixed_st, w_sout).astype(jnp.bfloat16), "tensor", scatter_dimension=1, tiled=True
        ).astype(jnp.float32)
        state_next = gate_value * state_rows + (1.0 - gate_value) * update
        return (state_next, (state_low, query_st, key_st, value_st, mixed_st, lse_st, update))

    def state_backward(
        grad_out, state_rows, kept_one, key_blk, value_blk, valid_blk, extra_key, extra_value
    ):
        state_low, query_st, key_st, value_st, mixed_st, lse_st, update = kept_one
        gate_part = (
            jnp.sum(grad_out * (state_rows - update), axis=(0, 1)) * gate_value * (1.0 - gate_value)
        )
        grad_update = lax.all_gather(
            to_low((1.0 - gate_value) * grad_out), "tensor", axis=1, tiled=True
        )
        grad_mixed_st = to_low(matmul_t(grad_update, w_sout))
        sout_part = outer_sum(mixed_st, grad_update)
        key_all = jnp.concatenate([key_blk, key_st], axis=1)
        value_all = jnp.concatenate([value_blk, value_st], axis=1)
        grad_query_st, grad_keys_st, grad_values_st, _ = batched_back(
            query_st, key_all, value_all, 0.0, state_mask_of(valid_blk), lse_st, grad_mixed_st
        )
        query_low = to_low(grad_query_st)
        key_low = to_low(grad_keys_st[:, BLOCK:] + extra_key)
        value_low = to_low(grad_values_st[:, BLOCK:] + extra_value)
        squery_part = outer_sum(state_low, query_low)
        key_part = outer_sum(state_low, key_low)
        value_part = outer_sum(state_low, value_low)
        terms = (
            matmul_t(query_low, w_squery) + matmul_t(key_low, w_key) + matmul_t(value_low, w_value)
        )
        grad_normed = lax.psum_scatter(
            terms.astype(jnp.bfloat16), "tensor", scatter_dimension=1, tiled=True
        ).astype(jnp.float32)
        grad_rows_norm, gain_part = norm_back(state_rows, state_gain, grad_normed)
        grad_in = gate_value * grad_out + grad_rows_norm
        block_grads = (grad_keys_st[:, :BLOCK], grad_values_st[:, :BLOCK])
        return (
            grad_in,
            block_grads,
            (squery_part, key_part, value_part, sout_part, gain_part, gate_part),
        )

    zeros_rows = jnp.zeros((seq_count,) + init_state.shape, jnp.float32)
    narrow_zero = jnp.zeros((seq_count, STATES, width_local), jnp.bfloat16)
    stored_start = (
        zeros_rows,
        zeros_rows,
        jnp.zeros((seq_count, STATES, D), jnp.bfloat16),
        narrow_zero,
        narrow_zero,
        narrow_zero,
        narrow_zero,
        jnp.zeros((seq_count, head_count, STATES), jnp.float32),
        zeros_rows,
    )

    def forward_turn(turn_index, carry):
        incoming, stored_now = carry
        order_index = turn_index - block_index
        is_live = (order_index >= 0) & (order_index < seq_count)
        picked = jnp.clip(order_index, 0, seq_count - 1)
        rows_now = jnp.where(is_first, init_state[None], incoming)
        key_one = lax.dynamic_slice_in_dim(key_tok, picked, 1, 0)
        value_one = lax.dynamic_slice_in_dim(value_tok, picked, 1, 0)
        valid_one = lax.dynamic_slice_in_dim(valid_keys, picked, 1, 0)
        rows_next, kept_one = state_forward(rows_now, key_one, value_one, valid_one)
        fresh = (rows_now, rows_next) + kept_one
        stored_now = tuple(
            (
                jnp.where(
                    is_live,
                    lax.dynamic_update_slice_in_dim(whole_array, fresh_part, picked, 0),
                    whole_array,
                )
                for whole_array, fresh_part in zip(stored_now, fresh)
            )
        )
        return (pass_state(rows_next), stored_now)

    incoming_start = jnp.zeros((1,) + init_state.shape, jnp.float32)
    _, stored_all = lax.fori_loop(
        0, chain_length + seq_count - 1, forward_turn, (incoming_start, stored_start)
    )
    state_in = stored_all[0]
    state_out = stored_all[1]
    kept = stored_all[2:]
    key_all_tok = jnp.concatenate([key_prev, key_tok, kept[2]], axis=1)
    value_all_tok = jnp.concatenate([value_prev, value_tok, kept[3]], axis=1)
    allowed_tok = jax.vmap(token_mask, in_axes=(0, 0, None))(seg_starts[:, 0], lengths, block_index)
    rel_table = bucket_of((jnp.arange(2 * BLOCK) - BLOCK)[None, :] - positions[:, None])
    full_bias = jnp.concatenate(
        [bias_lookup(rel_bias, rel_table), jnp.zeros((head_count, BLOCK, STATES), jnp.float32)],
        axis=2,
    )
    mixed_tok, lse_tok = batched_attend(
        query_tok, key_all_tok, value_all_tok, full_bias, allowed_tok
    )
    hidden_in = inputs_wide + sum_rows(matmul(mixed_tok, w_out))
    mid_low = gather_rows(to_low(layer_norm(hidden_in, mlp_gain)))
    pre_act = matmul(mid_low, w_up)
    hidden_low = to_low(jax.nn.gelu(pre_act))
    mlp_rows = sum_rows(matmul(hidden_low, w_down))
    tokens_out = (hidden_in + mlp_rows).astype(jnp.bfloat16)
    cot_wide = out_cot.astype(jnp.float32)
    cot_used = gather_rows(out_cot)
    grad_hidden_act = matmul_t(cot_used, w_down)
    down_grad = outer_sum(hidden_low, cot_used)
    grad_pre = to_low(gelu_back(pre_act, grad_hidden_act))
    up_grad = outer_sum(mid_low, grad_pre)
    grad_normed_mid = sum_rows(matmul_t(grad_pre, w_up))
    grad_mid_in, mlp_gain_grad = norm_back(hidden_in, mlp_gain, grad_normed_mid)
    grad_hidden = cot_wide + grad_mid_in
    grad_attn_low = gather_rows(to_low(grad_hidden))
    grad_mixed = to_low(matmul_t(grad_attn_low, w_out))
    out_grad = outer_sum(mixed_tok, grad_attn_low)
    grad_query_tok, grad_keys_tok, grad_values_tok, grad_scores = batched_back(
        query_tok, key_all_tok, value_all_tok, full_bias, allowed_tok, lse_tok, grad_mixed
    )
    bias_grad = bias_sums(grad_scores[..., : 2 * BLOCK], rel_table)
    grad_key_next, grad_value_next = (
        passed_along(grad_keys_tok[:, :BLOCK].astype(jnp.bfloat16), "seq", -1).astype(jnp.float32),
        passed_along(grad_values_tok[:, :BLOCK].astype(jnp.bfloat16), "seq", -1).astype(
            jnp.float32
        ),
    )
    grad_key_own = grad_keys_tok[:, BLOCK : 2 * BLOCK] + grad_key_next
    grad_value_own = grad_values_tok[:, BLOCK : 2 * BLOCK] + grad_value_next
    grad_key_st_tok = grad_keys_tok[:, 2 * BLOCK :]
    grad_value_st_tok = grad_values_tok[:, 2 * BLOCK :]
    cot_rows = state_cot[:, 0].astype(jnp.float32)
    wide_zero = jnp.zeros((seq_count, BLOCK, width_local), jnp.float32)
    stored_back = (zeros_rows, wide_zero, wide_zero)
    totals_start = (
        jnp.zeros((D, width_local), jnp.float32),
        jnp.zeros((D, width_local), jnp.float32),
        jnp.zeros((D, width_local), jnp.float32),
        jnp.zeros((width_local, D), jnp.float32),
        jnp.zeros((D,), jnp.float32),
        jnp.zeros((D,), jnp.float32),
    )

    def backward_turn(turn_index, carry):
        incoming, stored_now, totals_now = carry
        order_index = turn_index - (chain_length - 1 - block_index)
        is_live = (order_index >= 0) & (order_index < seq_count)
        picked = jnp.clip(order_index, 0, seq_count - 1)

        def slice_one(whole_array):
            return lax.dynamic_slice_in_dim(whole_array, picked, 1, 0)

        grad_out = slice_one(cot_rows) + incoming
        kept_one = tuple((slice_one(kept_array) for kept_array in kept))
        grad_in, block_one, parts_one = state_backward(
            grad_out,
            slice_one(state_in),
            kept_one,
            slice_one(key_tok),
            slice_one(value_tok),
            slice_one(valid_keys),
            slice_one(grad_key_st_tok),
            slice_one(grad_value_st_tok),
        )
        fresh = (grad_in,) + block_one
        stored_now = tuple(
            (
                jnp.where(
                    is_live,
                    lax.dynamic_update_slice_in_dim(whole_array, fresh_part, picked, 0),
                    whole_array,
                )
                for whole_array, fresh_part in zip(stored_now, fresh)
            )
        )
        totals_now = tuple(
            (
                total_now + jnp.where(is_live, part_now, 0.0)
                for total_now, part_now in zip(totals_now, parts_one)
            )
        )
        return (pass_back(grad_in), stored_now, totals_now)

    incoming_start = jnp.zeros((1,) + init_state.shape, jnp.float32)
    _, stored_done, weight_parts = lax.fori_loop(
        0, chain_length + seq_count - 1, backward_turn, (incoming_start, stored_back, totals_start)
    )
    grad_in_all, grad_key_blk, grad_value_blk = stored_done
    query_low = to_low(grad_query_tok)
    key_low = to_low(grad_key_own + grad_key_blk)
    value_low = to_low(grad_value_own + grad_value_blk)
    query_grad = outer_sum(tokens_low, query_low)
    key_grad = outer_sum(tokens_low, key_low) + weight_parts[1]
    value_grad = outer_sum(tokens_low, value_low) + weight_parts[2]
    grad_tokens = sum_rows(
        matmul_t(query_low, w_query) + matmul_t(key_low, w_key) + matmul_t(value_low, w_value)
    )
    grad_in_norm, attn_gain_grad = norm_back(inputs_wide, attn_gain, grad_tokens)
    inputs_grad = grad_hidden + grad_in_norm
    state_part = jnp.where(is_first, jnp.sum(grad_in_all, axis=0), 0.0)
    gains = lax.psum(
        jnp.stack([attn_gain_grad, weight_parts[4], mlp_gain_grad, weight_parts[5]]), "tensor"
    )
    totals = (
        lax.psum(query_grad.astype(jnp.bfloat16), ("dp", "seq")).astype(jnp.float32),
        lax.psum(key_grad.astype(jnp.bfloat16), ("dp", "seq")).astype(jnp.float32),
        lax.psum(value_grad.astype(jnp.bfloat16), ("dp", "seq")).astype(jnp.float32),
        lax.psum(out_grad.astype(jnp.bfloat16), ("dp", "seq")).astype(jnp.float32),
        lax.psum(weight_parts[0].astype(jnp.bfloat16), ("dp", "seq")).astype(jnp.float32),
        lax.psum(weight_parts[3].astype(jnp.bfloat16), ("dp", "seq")).astype(jnp.float32),
        lax.psum(up_grad.astype(jnp.bfloat16), ("dp", "seq")).astype(jnp.float32),
        lax.psum(down_grad.astype(jnp.bfloat16), ("dp", "seq")).astype(jnp.float32),
        lax.psum(bias_grad.astype(jnp.bfloat16), ("dp", "seq")).astype(jnp.float32),
        lax.psum(state_part.astype(jnp.bfloat16), ("dp", "seq")).astype(jnp.float32),
        lax.psum(gains.astype(jnp.bfloat16), ("dp", "seq")).astype(jnp.float32),
    )
    gain_total = totals[10]
    return (
        tokens_out,
        state_out[:, None],
        inputs_grad,
        totals[9],
        gain_total[0],
        gain_total[1],
        gain_total[2],
        totals[0],
        totals[1],
        totals[2],
        totals[3],
        totals[4],
        totals[5],
        totals[6],
        totals[7],
        totals[8],
        gain_total[3],
    )


def chosen_body(mesh):
    if mesh.shape["seq"] == 4 and mesh.shape["tensor"] == 4:
        return line_body
    return body


MESH_ID = pl.DeviceIdType.MESH
ROWS = 128
CHUNKS = BLOCK // ROWS
LINE = 8
SCALE = HEAD_DIM ** (-0.5)
VMEM_LIMIT = 60 * 1024 * 1024


def dot_nn(left, right):
    return lax.dot_general(left, right, (((1,), (0,)), ((), ())), preferred_element_type=jnp.float32)


def dot_nt(left, right):
    return lax.dot_general(left, right, (((1,), (1,)), ((), ())), preferred_element_type=jnp.float32)


def dot_tn(left, right):
    return lax.dot_general(left, right, (((0,), (0,)), ((), ())), preferred_element_type=jnp.float32)


def line_place():
    place = lax.axis_index("seq")
    half = lax.rem(place, 2)
    rank = lax.axis_index("tensor")
    return place, half, rank


def span(index, size):
    return pl.ds(pl.multiple_of(index * size, size), size)


def fetch_pieces(kept, first, rows, target, sem):
    for owner in range(8):
        pltpu.make_async_copy(
            kept.at[owner, :, pl.ds(first, rows), :], target.at[:, owner], sem
        ).start()


def fetched(target, sem):
    pltpu.make_async_copy(target, target, sem).wait()


def norm_parts(rows):
    centered = rows - jnp.mean(rows, axis=-1, keepdims=True)
    spread = jnp.mean(centered * centered, axis=-1, keepdims=True)
    return centered, lax.rsqrt(spread + norm_eps)


def token_masks(scal, block_id, first_row):
    length = scal[0]
    start = scal[1 + block_id]
    row = lax.broadcasted_iota(jnp.int32, (ROWS, BLOCK), 0) + first_row
    col = lax.broadcasted_iota(jnp.int32, (ROWS, BLOCK), 1)
    prev_limit = jnp.where(block_id > 0, length - (block_id - 1) * BLOCK, 0)
    prev_ok = (col > row) & (col < prev_limit)
    row_in = (row >= start) & (row < start + SEG)
    col_in = (col >= start) & (col < start + SEG)
    cur_ok = ((col <= row) | (row_in & col_in)) & (col < length - block_id * BLOCK)
    return prev_ok, cur_ok


def state_block_mask(scal, block_id):
    col = lax.broadcasted_iota(jnp.int32, (ROWS, BLOCK), 1)
    return col < scal[0] - block_id * BLOCK


def softmax_of(score_parts):
    top = jnp.max(score_parts[0], axis=-1, keepdims=True)
    for part in score_parts[1:]:
        top = jnp.maximum(top, jnp.max(part, axis=-1, keepdims=True))
    raised = [jnp.exp(part - top) for part in score_parts]
    total = jnp.sum(raised[0], axis=-1, keepdims=True)
    for part in raised[1:]:
        total = total + jnp.sum(part, axis=-1, keepdims=True)
    inverse = 1.0 / total
    return [to_low(part * inverse) for part in raised], top + jnp.log(total)


def token_scores(scal, qkv, qkvst, bias, block_id, chunk):
    rows = span(chunk, ROWS)
    prev_id = jnp.maximum(block_id - 1, 0)
    query = qkv[block_id, rows, 0:128]
    prev_ok, cur_ok = token_masks(scal, block_id, chunk * ROWS)
    prev = dot_nt(query, qkv[prev_id, :, 128:256]) * SCALE + bias[rows, 0:BLOCK]
    cur = dot_nt(query, qkv[block_id, :, 128:256]) * SCALE + bias[rows, BLOCK : 2 * BLOCK]
    stt = dot_nt(query, qkvst[block_id, :, 128:256]) * SCALE
    prev = jnp.where(prev_ok, prev, masked_score)
    cur = jnp.where(cur_ok, cur, masked_score)
    return query, (prev, cur, stt)


def state_scores(scal, qkv, qkvst, block_id, chunk):
    query = qkvst[block_id, span(chunk, ROWS), 0:128]
    tok = dot_nt(query, qkv[block_id, :, 128:256]) * SCALE
    tok = jnp.where(state_block_mask(scal, block_id), tok, masked_score)
    stt = dot_nt(query, qkvst[block_id, :, 128:256]) * SCALE
    return query, (tok, stt)


def forward_kernel(
    scal, qkv, kept, w_state, vecs, bias,
    o_out, lse_out, state_rows, state_low, qkvst, lse_st, os_rows,
    held, os_all, w_sout, start, send_sem, pass_sem, recv_sem, local_sem,
):
    place, half, rank = line_place()
    fetch_pieces(kept, 32, 16, start, local_sem.at[0])
    fetch_pieces(kept, 0, 32, w_sout, local_sem.at[1])
    partner = place + 1 - 2 * half
    head = 2 * rank + half
    peers = [lax.rem(rank + step, 4) for step in (1, 2, 3)]
    barrier = pltpu.get_barrier_semaphore()
    for peer in peers:
        pl.semaphore_signal(
            barrier, inc=1, device_id={"seq": place, "tensor": peer}, device_id_type=MESH_ID
        )
    pl.semaphore_signal(
        barrier, inc=1, device_id={"seq": partner, "tensor": rank}, device_id_type=MESH_ID
    )
    fetched(start, local_sem.at[0])
    held[...] = start[...].reshape(STATES, D).astype(jnp.float32)
    gain = vecs[0:1, :]
    gate = vecs[1:2, :]
    pl.semaphore_wait(barrier, 4)
    fetched(w_sout, local_sem.at[1])

    def carry_copy(block_id, which, sem, seq_to, rank_to):
        part = os_all.at[block_id, :, span(which, 128)]
        return pltpu.make_async_remote_copy(
            src_ref=part,
            dst_ref=part,
            send_sem=sem,
            recv_sem=recv_sem.at[block_id, which],
            device_id={"seq": seq_to, "tensor": rank_to},
            device_id_type=MESH_ID,
        )

    def one_block(block_id, _):
        def project(chunk, _):
            rows = span(chunk, ROWS)
            centered, scale = norm_parts(held[rows, :])
            low = to_low(centered * scale * gain)
            state_low[block_id, rows, :] = low
            qkvst[block_id, rows, :] = to_low(dot_nn(low, w_state[...]))
            return 0

        lax.fori_loop(0, CHUNKS, project, 0)

        def attend_state(chunk, _):
            rows = span(chunk, ROWS)
            _, parts = state_scores(scal, qkv, qkvst, block_id, chunk)
            (w_tok, w_stt), total = softmax_of(parts)
            mixed = dot_nn(w_tok, qkv[block_id, :, 256:384]) + dot_nn(
                w_stt, qkvst[block_id, :, 256:384]
            )
            os_all[block_id, rows, span(head, 128)] = to_low(mixed)
            lse_st[block_id, rows, :] = total
            return 0

        lax.fori_loop(0, CHUNKS, attend_state, 0)
        for slot, peer in enumerate(peers):
            carry_copy(block_id, head, send_sem.at[block_id, slot], place, peer).start()
        carry_copy(block_id, head, send_sem.at[block_id, 3], partner, rank).start()

        def attend_token(chunk, _):
            rows = span(chunk, ROWS)
            _, parts = token_scores(scal, qkv, qkvst, bias, block_id, chunk)
            weights, total = softmax_of(parts)
            prev_id = jnp.maximum(block_id - 1, 0)
            mixed = (
                dot_nn(weights[0], qkv[prev_id, :, 256:384])
                + dot_nn(weights[1], qkv[block_id, :, 256:384])
                + dot_nn(weights[2], qkvst[block_id, :, 256:384])
            )
            o_out[block_id, rows, :] = to_low(mixed)
            lse_out[block_id, rows, :] = total
            return 0

        lax.fori_loop(0, CHUNKS, attend_token, 0)
        for slot, peer in enumerate(peers):
            other = 2 * peer + half
            carry_copy(block_id, other, send_sem.at[block_id, slot], place, peer).wait_recv()
            carry_copy(block_id, other, pass_sem.at[block_id, slot], partner, rank).start()
        for other_rank in range(4):
            carry_copy(
                block_id, 2 * other_rank + 1 - half, send_sem.at[block_id, 3], partner, rank
            ).wait_recv()

        def update(chunk, _):
            rows = span(chunk, ROWS)
            change = dot_nn(os_all[block_id, rows, :], w_sout[...].reshape(D, D))
            held[rows, :] = gate * held[rows, :] + (1.0 - gate) * change
            return 0

        lax.fori_loop(0, CHUNKS, update, 0)
        state_rows[block_id] = held[span(rank, 128), :]
        os_rows[block_id] = os_all[block_id, span(head, 64), :]
        return 0

    lax.fori_loop(0, 4, one_block, 0)

    def drain(block_id, _):
        for slot, peer in enumerate(peers):
            carry_copy(block_id, head, send_sem.at[block_id, slot], place, peer).wait_send()
            other = 2 * peer + half
            carry_copy(block_id, other, pass_sem.at[block_id, slot], partner, rank).wait_send()
        carry_copy(block_id, head, send_sem.at[block_id, 3], partner, rank).wait_send()
        return 0

    lax.fori_loop(0, 4, drain, 0)


def any_specs(count):
    return [pl.BlockSpec(memory_space=pl.ANY)] * count


def vmem_specs(count):
    return [pl.BlockSpec(memory_space=pltpu.VMEM)] * count


def forward_chain(scal, qkv, kept, w_state, vecs, bias):
    low, wide = jnp.bfloat16, jnp.float32
    shapes = (
        ((4, BLOCK, 128), low),
        ((4, BLOCK, 1), wide),
        ((4, 128, D), wide),
        ((4, STATES, D), low),
        ((4, STATES, 384), low),
        ((4, STATES, 1), wide),
        ((4, 64, D), low),
    )
    return pl.pallas_call(
        forward_kernel,
        out_shape=[jax.ShapeDtypeStruct(*one) for one in shapes],
        in_specs=[pl.BlockSpec(memory_space=pltpu.SMEM)]
        + vmem_specs(1)
        + any_specs(1)
        + vmem_specs(3),
        out_specs=vmem_specs(7),
        scratch_shapes=[
            pltpu.VMEM((STATES, D), wide),
            pltpu.VMEM((4, STATES, D), low),
            pltpu.VMEM((4, 8, 32, D), low),
            pltpu.VMEM((4, 8, 16, D), low),
            pltpu.SemaphoreType.DMA((4, 4)),
            pltpu.SemaphoreType.DMA((4, 3)),
            pltpu.SemaphoreType.DMA((4, 8)),
            pltpu.SemaphoreType.DMA((2,)),
        ],
        compiler_params=pltpu.CompilerParams(
            collective_id=1, has_side_effects=True, vmem_limit_bytes=VMEM_LIMIT
        ),
        cost_estimate=pl.CostEstimate(flops=20000000000, bytes_accessed=20000000, transcendentals=0),
        name="forward_chain",
    )(scal, qkv, kept, w_state, vecs, bias)


def backward_kernel(
    scal, qkv, d_o, lse_tok, qkvst, lse_st, state_rows, begin, cots, back, kept, vecs, bias,
    extra, hidden,
    d_qkv, d_qkvst, du_rows, d_start, sums, dz_sum, state_out, tokens_out, out_part,
    key_acc, value_acc, st_key, st_value, dos_rows, dos_got, d_got, grad_in,
    states, w_back, w_sout, work, core_got, near_got, far_got, total,
    send_sem, recv_sem, local_sem, side_sem, ring_send, ring_recv,
):
    place, half, rank = line_place()
    own_rows = pl.ds(pl.multiple_of(half * 64, 64), 64)
    loads = [
        pltpu.make_async_copy(
            state_rows.at[:, own_rows, :], states.at[pl.ds(1, 4)], local_sem.at[0]
        ),
        pltpu.make_async_copy(
            state_rows.at[place], state_out.at[place // 2], local_sem.at[3]
        ),
        pltpu.make_async_copy(extra, work, local_sem.at[4]),
    ]
    for one in loads:
        one.start()
    fetch_pieces(kept, 0, 32, w_sout, local_sem.at[1])
    for owner in range(8):
        pltpu.make_async_copy(
            back.at[owner], w_back.at[:, owner // 4, :, owner % 4], local_sem.at[2]
        ).start()
    states[0] = to_low(begin[own_rows, :]).astype(jnp.float32)
    head = 2 * rank + half
    peers = []
    for step in range(1, LINE):
        other = lax.rem(head + step, LINE)
        peers.append((other, place - half + lax.rem(other, 2), other // 2))
    barrier = pltpu.get_barrier_semaphore()
    for _, seq_to, rank_to in peers:
        pl.semaphore_signal(
            barrier, inc=1, device_id={"seq": seq_to, "tensor": rank_to}, device_id_type=MESH_ID
        )
    beside = lax.rem(place + 2, 4)
    pl.semaphore_signal(barrier, inc=1, device_id={"seq": beside}, device_id_type=MESH_ID)
    pl.semaphore_signal(
        barrier, inc=1, device_id={"dp": 1 - lax.axis_index("dp")}, device_id_type=MESH_ID
    )
    plane_steps = plane_scatter(
        work, core_got, near_got, far_got, total, 384, ring_send, ring_recv
    )
    next(plane_steps)

    def aside(block_id, row_set):
        return pltpu.make_async_remote_copy(
            src_ref=state_rows.at[block_id],
            dst_ref=state_out.at[row_set],
            send_sem=side_sem.at[0],
            recv_sem=side_sem.at[1],
            device_id={"seq": beside},
            device_id_type=MESH_ID,
        )

    gain = vecs[0:1, :]
    gate = vecs[1:2, :]
    key_acc[...] = jnp.zeros_like(key_acc)
    value_acc[...] = jnp.zeros_like(value_acc)
    dz_sum[...] = jnp.zeros_like(dz_sum)
    sums[...] = jnp.zeros_like(sums)
    grad_in[...] = jnp.zeros_like(grad_in)

    def back_parts(parts, total, grad, values):
        weights = [jnp.exp(part - total) for part in parts]
        d_weights = [dot_nt(grad, value) for value in values]
        inner = jnp.sum(weights[0] * d_weights[0], axis=-1, keepdims=True)
        for one, other in zip(weights[1:], d_weights[1:]):
            inner = inner + jnp.sum(one * other, axis=-1, keepdims=True)
        d_scores = [to_low(one * (other - inner)) for one, other in zip(weights, d_weights)]
        return [to_low(one) for one in weights], d_scores

    def token_back(block_id):
        prev_id = jnp.maximum(block_id - 1, 0)
        st_key[...] = jnp.zeros_like(st_key)
        st_value[...] = jnp.zeros_like(st_value)

        def one_chunk(chunk, _):
            rows = span(chunk, ROWS)
            query, parts = token_scores(scal, qkv, qkvst, bias, block_id, chunk)
            grad = d_o[block_id, rows, :]
            keys = (qkv[prev_id, :, 128:256], qkv[block_id, :, 128:256], qkvst[block_id, :, 128:256])
            values = (
                qkv[prev_id, :, 256:384], qkv[block_id, :, 256:384], qkvst[block_id, :, 256:384]
            )
            weights, d_scores = back_parts(parts, lse_tok[block_id, rows, :], grad, values)
            d_query = dot_nn(d_scores[0], keys[0])
            d_query = d_query + dot_nn(d_scores[1], keys[1]) + dot_nn(d_scores[2], keys[2])
            d_qkv[block_id, rows, 0:128] = to_low(d_query * SCALE)
            key_acc[prev_id] += dot_tn(d_scores[0], query) * SCALE
            value_acc[prev_id] += dot_tn(weights[0], grad)
            key_acc[block_id] += dot_tn(d_scores[1], query) * SCALE
            value_acc[block_id] += dot_tn(weights[1], grad)
            st_key[...] += dot_tn(d_scores[2], query) * SCALE
            st_value[...] += dot_tn(weights[2], grad)
            dz_sum[rows, 0:BLOCK] += d_scores[0].astype(jnp.float32)
            dz_sum[rows, BLOCK : 2 * BLOCK] += d_scores[1].astype(jnp.float32)
            return 0

        lax.fori_loop(0, CHUNKS, one_chunk, 0)

    token_back(3)
    pl.semaphore_wait(barrier, LINE + 1)
    aside(beside, place // 2).start()
    loads[2].wait()
    loads[0].wait()
    fetched(w_sout, local_sem.at[1])
    fetched(w_back, local_sem.at[2])

    def mixed_copy(block_id, slot, sender, other, seq_to, rank_to):
        return pltpu.make_async_remote_copy(
            src_ref=dos_rows.at[block_id, :, span(other, 128)],
            dst_ref=dos_got.at[block_id, span(sender, 64), :],
            send_sem=send_sem.at[0, block_id, slot],
            recv_sem=recv_sem.at[0, block_id, sender],
            device_id={"seq": seq_to, "tensor": rank_to},
            device_id_type=MESH_ID,
        )

    def grads_copy(block_id, slot, sender, other, seq_to, rank_to):
        return pltpu.make_async_remote_copy(
            src_ref=d_qkvst.at[block_id, span(other, 64), :],
            dst_ref=d_got.at[block_id, sender],
            send_sem=send_sem.at[1, block_id, slot],
            recv_sem=recv_sem.at[1, block_id, sender],
            device_id={"seq": seq_to, "tensor": rank_to},
            device_id_type=MESH_ID,
        )

    def one_block(turn, _):
        block_id = 3 - turn
        grad_out = grad_in[...] + cots[block_id].astype(jnp.float32)
        sums[0:1, :] += jnp.sum(
            grad_out * (states[block_id] - states[block_id + 1]), axis=0, keepdims=True
        ) * gate
        change = to_low((1.0 - gate) * grad_out)
        du_rows[block_id] = change
        dos_rows[block_id] = to_low(dot_nt(change, w_sout[...].reshape(D, D)))
        for slot, (other, seq_to, rank_to) in enumerate(peers):
            mixed_copy(block_id, slot, head, other, seq_to, rank_to).start()
        dos_got[block_id, span(head, 64), :] = dos_rows[block_id, :, span(head, 128)]
        for slot, (other, seq_to, rank_to) in enumerate(peers):
            mixed_copy(block_id, slot, other, other, seq_to, rank_to).wait_recv()

        def one_chunk(chunk, _):
            rows = span(chunk, ROWS)
            query, parts = state_scores(scal, qkv, qkvst, block_id, chunk)
            grad = dos_got[block_id, rows, :]
            keys = (qkv[block_id, :, 128:256], qkvst[block_id, :, 128:256])
            values = (qkv[block_id, :, 256:384], qkvst[block_id, :, 256:384])
            weights, d_scores = back_parts(parts, lse_st[block_id, rows, :], grad, values)
            d_query = dot_nn(d_scores[0], keys[0]) + dot_nn(d_scores[1], keys[1])
            d_qkvst[block_id, rows, 0:128] = to_low(d_query * SCALE)
            key_acc[block_id] += dot_tn(d_scores[0], query) * SCALE
            value_acc[block_id] += dot_tn(weights[0], grad)
            st_key[...] += dot_tn(d_scores[1], query) * SCALE
            st_value[...] += dot_tn(weights[1], grad)
            return 0

        lax.fori_loop(0, CHUNKS, one_chunk, 0)
        d_qkvst[block_id, :, 128:256] = to_low(st_key[...])
        d_qkvst[block_id, :, 256:384] = to_low(st_value[...])
        for slot, (other, seq_to, rank_to) in enumerate(peers):
            grads_copy(block_id, slot, head, other, seq_to, rank_to).start()
        d_got[block_id, head] = d_qkvst[block_id, span(head, 64), :]

        for step in range(4):

            @pl.when(turn == step)
            def _():
                next(plane_steps, None)

        @pl.when(turn < 3)
        def _():
            token_back(block_id - 1)

        d_qkv[block_id, :, 128:256] = to_low(key_acc[block_id])
        d_qkv[block_id, :, 256:384] = to_low(value_acc[block_id])
        for slot, (other, seq_to, rank_to) in enumerate(peers):
            grads_copy(block_id, slot, other, other, seq_to, rank_to).wait_recv()
        d_low = dot_nn(d_got[block_id, 0], w_back[0, 0].reshape(384, D))
        for other in range(1, LINE):
            d_low = d_low + dot_nn(
                d_got[block_id, other], w_back[other // 2, other % 2].reshape(384, D)
            )
        centered, scale = norm_parts(states[block_id])
        normed = centered * scale
        sums[1:2, :] += jnp.sum(d_low * normed, axis=0, keepdims=True)
        lifted = d_low * gain
        grad_in[...] = gate * grad_out + scale * (
            lifted
            - jnp.mean(lifted, axis=-1, keepdims=True)
            - normed * jnp.mean(lifted * normed, axis=-1, keepdims=True)
        )
        return 0

    lax.fori_loop(0, 4, one_block, 0)
    d_start[...] = grad_in[...]

    def drain(block_id, _):
        for slot, (other, seq_to, rank_to) in enumerate(peers):
            mixed_copy(block_id, slot, head, other, seq_to, rank_to).wait_send()
            grads_copy(block_id, slot, head, other, seq_to, rank_to).wait_send()
        return 0

    lax.fori_loop(0, 4, drain, 0)
    for _ in plane_steps:
        pass
    for which in range(2):
        rows = pl.ds(128 * which, 128)
        tokens_out[which] = to_low(hidden[which] + total[rows, :])
    out_part[...] = to_low(total[256:384, :])
    loads[1].wait()
    aside(beside, place // 2).wait_send()
    aside(place, 1 - place // 2).wait_recv()


def backward_chain(
    scal, qkv, d_o, lse_tok, qkvst, lse_st, state_rows, begin, cots, back, kept, vecs, bias,
    extra, hidden,
):
    low, wide = jnp.bfloat16, jnp.float32
    shapes = (
        ((4, BLOCK, 384), low),
        ((4, STATES, 384), low),
        ((4, 64, D), low),
        ((64, D), wide),
        ((8, D), wide),
        ((BLOCK, 2 * BLOCK), wide),
        ((2, 128, D), wide),
        ((2, 128, D), low),
        ((128, D), low),
    )
    return pl.pallas_call(
        backward_kernel,
        out_shape=[jax.ShapeDtypeStruct(*one) for one in shapes],
        in_specs=[pl.BlockSpec(memory_space=pltpu.SMEM)]
        + vmem_specs(5)
        + any_specs(1)
        + vmem_specs(2)
        + any_specs(2)
        + vmem_specs(2)
        + any_specs(1)
        + vmem_specs(1),
        out_specs=vmem_specs(6) + any_specs(1) + vmem_specs(2),
        scratch_shapes=[
            pltpu.VMEM((4, BLOCK, 128), wide),
            pltpu.VMEM((4, BLOCK, 128), wide),
            pltpu.VMEM((STATES, 128), wide),
            pltpu.VMEM((STATES, 128), wide),
            pltpu.VMEM((4, 64, D), low),
            pltpu.VMEM((4, STATES, 128), low),
            pltpu.VMEM((4, LINE, 64, 384), low),
            pltpu.VMEM((64, D), wide),
            pltpu.VMEM((5, 64, D), wide),
            pltpu.VMEM((4, 2, 3, 4, 32, D), low),
            pltpu.VMEM((4, 8, 32, D), low),
            pltpu.VMEM((8, 384, D), low),
            pltpu.VMEM((4, 384, D), low),
            pltpu.VMEM((4, 192, D), low),
            pltpu.VMEM((2, 192, D), low),
            pltpu.VMEM((384, D), wide),
            pltpu.SemaphoreType.DMA((2, 4, LINE - 1)),
            pltpu.SemaphoreType.DMA((2, 4, LINE)),
            pltpu.SemaphoreType.DMA((5,)),
            pltpu.SemaphoreType.DMA((2,)),
            pltpu.SemaphoreType.DMA((10,)),
            pltpu.SemaphoreType.DMA((10,)),
        ],
        compiler_params=pltpu.CompilerParams(
            collective_id=2, has_side_effects=True, vmem_limit_bytes=VMEM_LIMIT
        ),
        cost_estimate=pl.CostEstimate(flops=40000000000, bytes_accessed=40000000, transcendentals=0),
        name="backward_chain",
    )(
        scal, qkv, d_o, lse_tok, qkvst, lse_st, state_rows, begin, cots, back, kept, vecs, bias,
        extra, hidden,
    )


def plane_place():
    place, half, rank = line_place()
    side = lax.axis_index("dp")
    return side, place, half, rank


def plane_index(side, place):
    return 4 * side + place


def plane_gather(buf, rows, send_sem, recv_sem):
    side, place, half, rank = plane_place()
    across, beside = 1 - side, lax.rem(place + 2, 4)
    core = place + 1 - 2 * half
    me = plane_index(side, place)
    at_x, at_y = plane_index(across, place), plane_index(side, beside)
    at_d = plane_index(across, beside)
    to_x = {"dp": across}
    to_y = {"seq": beside}
    to_c = {"seq": core}
    size = rows // 2

    def piece(owner, part, slot, target):
        view = buf.at[owner, pl.ds(part * size, size), :]
        return pltpu.make_async_remote_copy(
            src_ref=view,
            dst_ref=view,
            send_sem=send_sem.at[slot],
            recv_sem=recv_sem.at[owner, part],
            device_id=target,
            device_id_type=MESH_ID,
        )

    sent = []

    def send(owner, part, target):
        one = piece(owner, part, len(sent), target)
        sent.append(one)
        one.start()

    def arrived(owner, part):
        piece(owner, part, 0, to_c).wait_recv()

    send(me, 0, to_x)
    send(me, 1, to_y)
    send(me, 1, to_x)
    send(me, 0, to_y)
    send(me, 0, to_c)
    send(me, 1, to_c)
    yield
    arrived(at_x, 0)
    send(at_x, 0, to_y)
    arrived(at_y, 1)
    send(at_y, 1, to_x)
    send(at_x, 0, to_c)
    send(at_y, 1, to_c)
    yield
    arrived(at_x, 1)
    send(at_x, 1, to_c)
    arrived(at_y, 0)
    send(at_y, 0, to_c)
    yield
    arrived(at_d, 0)
    send(at_d, 0, to_c)
    arrived(at_d, 1)
    send(at_d, 1, to_c)
    yield
    for owner in (
        plane_index(side, core),
        plane_index(across, core),
        plane_index(side, lax.rem(core + 2, 4)),
        plane_index(across, lax.rem(core + 2, 4)),
    ):
        arrived(owner, 0)
        arrived(owner, 1)
    for one in sent:
        one.wait_send()


def run_all(*steps):
    waiting = list(steps)
    while waiting:
        for one in list(waiting):
            try:
                next(one)
            except StopIteration:
                waiting.remove(one)


def plane_scatter(part, core_got, near_got, far_got, total, rows, send_sem, recv_sem):
    side, place, half, rank = plane_place()
    across, beside = 1 - side, lax.rem(place + 2, 4)
    core = place + 1 - 2 * half
    me = plane_index(side, place)
    at_x, at_y = plane_index(across, place), plane_index(side, beside)
    at_d = plane_index(across, beside)
    size = rows // 2
    halves = (pl.ds(0, size), pl.ds(size, size))

    def moved(source, target_ref, slot, target):
        return pltpu.make_async_remote_copy(
            src_ref=source,
            dst_ref=target_ref,
            send_sem=send_sem.at[slot],
            recv_sem=recv_sem.at[slot],
            device_id=target,
            device_id_type=MESH_ID,
        )

    order = (at_d, at_x, at_y, me)
    swapped = (
        plane_index(across, lax.rem(core + 2, 4)),
        plane_index(across, core),
        plane_index(side, lax.rem(core + 2, 4)),
        plane_index(side, core),
    )
    def add_into(owner, view, other):
        part[owner, view, :] = to_low(
            part[owner, view, :].astype(jnp.float32) + other.astype(jnp.float32)
        )

    near = [
        moved(part.at[at_d, halves[0], :], near_got.at[0], 4, {"dp": across}),
        moved(part.at[at_d, halves[1], :], near_got.at[1], 5, {"seq": beside}),
        moved(part.at[at_x, halves[0], :], near_got.at[2], 6, {"dp": across}),
        moved(part.at[at_y, halves[1], :], near_got.at[3], 7, {"seq": beside}),
    ]
    first = [
        moved(part.at[owner], core_got.at[slot], slot, {"seq": core})
        for slot, owner in enumerate(swapped)
    ]
    far = [
        moved(part.at[at_y, halves[0], :], far_got.at[0], 8, {"seq": beside}),
        moved(part.at[at_x, halves[1], :], far_got.at[1], 9, {"dp": across}),
    ]
    yield
    for one in first:
        one.start()
    for slot, owner in enumerate(order):
        first[slot].wait_recv()
        for view in halves:
            add_into(owner, view, core_got[slot, view, :])
        if slot == 0:
            near[0].start()
            near[1].start()
        if slot == 1:
            near[2].start()
        if slot == 2:
            near[3].start()
    yield
    near[0].wait_recv()
    add_into(at_y, halves[0], near_got[0])
    far[0].start()
    near[1].wait_recv()
    add_into(at_x, halves[1], near_got[1])
    far[1].start()
    yield
    near[2].wait_recv()
    add_into(me, halves[0], near_got[2])
    near[3].wait_recv()
    add_into(me, halves[1], near_got[3])
    yield
    for slot, view in enumerate(halves):
        far[slot].wait_recv()
        total[view, :] = part[me, view, :].astype(jnp.float32) + far_got[slot].astype(jnp.float32)
    for one in first + near + far:
        one.wait_send()


def group_peers():
    place, half, rank = line_place()
    here = 4 * place + rank
    peers = []
    for step in range(1, 16):
        other = lax.rem(here + step, 16)
        peers.append((other, other // 4, lax.rem(other, 4)))
    return here, peers


def greet(peers):
    side = lax.axis_index("dp")
    barrier = pltpu.get_barrier_semaphore()
    for _, seq_to, rank_to in peers:
        pl.semaphore_signal(
            barrier, inc=1, device_id={"seq": seq_to, "tensor": rank_to}, device_id_type=MESH_ID
        )
    pl.semaphore_signal(barrier, inc=1, device_id={"dp": 1 - side}, device_id_type=MESH_ID)
    pl.semaphore_wait(barrier, len(peers) + 1)


def middle_kernel(
    mixed, tokens, kept, spread, cot_hbm, vecs,
    hidden, d_hidden, d_line, sums, extra, ff_grads,
    mixed_rows, mid_all, gl_all, dpre_all, work, core_got, near_got, far_got, total, d_rows,
    d_low, w_out, up, down, cot_all,
    send_sem, recv_sem, ring_send, ring_recv, sum_send, sum_recv, back_send, back_recv, local_sem,
):
    low, wide = jnp.bfloat16, jnp.float32
    side, place, half, rank = plane_place()
    mine = place // 2
    head = 2 * rank + half
    across, beside = 1 - side, lax.rem(place + 2, 4)
    core = place + 1 - 2 * half
    core_beside = lax.rem(core + 2, 4)
    me = plane_index(side, place)
    at_x, at_y = plane_index(across, place), plane_index(side, beside)
    at_d = plane_index(across, beside)
    me_c, x_c = plane_index(side, core), plane_index(across, core)
    y_c, d_c = plane_index(side, core_beside), plane_index(across, core_beside)
    to_x, to_y, to_c = {"dp": across}, {"seq": beside}, {"seq": core}
    here, peers = group_peers()
    fetch_pieces(kept, 48, 32, w_out, local_sem.at[0])
    ff_own = up.shape[1]
    first = spread.shape[1] - 2 * ff_own
    loads = [
        pltpu.make_async_copy(spread.at[:, pl.ds(first, ff_own), :], up, local_sem.at[1]),
        pltpu.make_async_copy(spread.at[:, pl.ds(first + ff_own, ff_own), :], down, local_sem.at[2]),
        pltpu.make_async_copy(cot_hbm, cot_all, local_sem.at[3]),
    ]
    for one in loads:
        one.start()
    greet(peers)

    def rows_copy(slot, sender, seq_from, rank_from, seq_to, rank_to):
        return pltpu.make_async_remote_copy(
            src_ref=mixed.at[seq_to, span(rank_to, 128), :],
            dst_ref=mixed_rows.at[
                seq_from // 2, :, span(2 * rank_from + lax.rem(seq_from, 2), 128)
            ],
            send_sem=send_sem.at[slot],
            recv_sem=recv_sem.at[sender],
            device_id={"seq": seq_to, "tensor": rank_to},
            device_id_type=MESH_ID,
        )

    for slot, (_, seq_to, rank_to) in enumerate(peers):
        rows_copy(slot, here, place, rank, seq_to, rank_to).start()
    mixed_rows[mine, :, span(head, 128)] = mixed[place, span(rank, 128), :]
    fetched(w_out, local_sem.at[0])
    for slot, (other, seq_to, rank_to) in enumerate(peers):
        rows_copy(slot, other, seq_to, rank_to, seq_to, rank_to).wait_recv()
    gain = vecs[2:3, :]

    def project(which, _):
        added = dot_nn(mixed_rows[which], w_out[...].reshape(D, D)) + tokens[which].astype(wide)
        hidden[which] = added
        centered, scale = norm_parts(added)
        mid_all[me, span(which, 128), :] = to_low(centered * scale * gain)
        return 0

    lax.fori_loop(0, 2, project, 0)

    def piece(owner, part, slot, target):
        view = mid_all.at[owner, pl.ds(part * 128, 128), :]
        return pltpu.make_async_remote_copy(
            src_ref=view,
            dst_ref=view,
            send_sem=ring_send.at[slot],
            recv_sem=ring_recv.at[owner, part],
            device_id=target,
            device_id_type=MESH_ID,
        )

    own = [
        piece(me, 0, 0, to_x), piece(me, 1, 1, to_y), piece(me, 1, 2, to_x), piece(me, 0, 3, to_y),
        piece(me, 0, 4, to_c), piece(me, 1, 5, to_c),
    ]
    on_x0, on_y1 = piece(at_x, 0, 6, to_y), piece(at_y, 1, 7, to_x)
    to_core = [
        piece(at_x, 0, 8, to_c), piece(at_y, 1, 9, to_c), piece(at_x, 1, 10, to_c),
        piece(at_y, 0, 11, to_c), piece(at_d, 0, 12, to_c), piece(at_d, 1, 13, to_c),
    ]
    wait_of = {
        (name, part): piece(owner, part, 0, to_c)
        for name, owner in (
            ("x", at_x), ("y", at_y), ("d", at_d), ("mc", me_c), ("xc", x_c), ("yc", y_c), ("dc", d_c)
        )
        for part in (0, 1)
    }

    def moved(source, target_ref, slot, target):
        return pltpu.make_async_remote_copy(
            src_ref=source,
            dst_ref=target_ref,
            send_sem=sum_send.at[slot],
            recv_sem=sum_recv.at[slot],
            device_id=target,
            device_id_type=MESH_ID,
        )

    views = (pl.ds(0, 128), pl.ds(128, 128))
    swap = [
        moved(work.at[owner], core_got.at[slot], slot, to_c)
        for slot, owner in enumerate((d_c, x_c, y_c, me_c))
    ]
    near = [
        moved(work.at[at_d, views[0], :], near_got.at[0], 4, to_x),
        moved(work.at[at_d, views[1], :], near_got.at[1], 5, to_y),
        moved(work.at[at_x, views[0], :], near_got.at[2], 6, to_x),
        moved(work.at[at_y, views[1], :], near_got.at[3], 7, to_y),
    ]
    far = [
        moved(work.at[at_y, views[0], :], far_got.at[0], 8, to_y),
        moved(work.at[at_x, views[1], :], far_got.at[1], 9, to_x),
    ]

    def add_into(owner, view, other):
        work[owner, view, :] = to_low(work[owner, view, :].astype(wide) + other.astype(wide))

    def add_core(slot, owner):
        swap[slot].wait_recv()
        for view in views:
            add_into(owner, view, core_got[slot, view, :])

    for one in own:
        one.start()
    loads[0].wait()
    loads[1].wait()
    loads[2].wait()
    owners = (me, me_c, at_x, at_y, x_c, y_c, at_d, d_c)

    def one_chunk(turn, _):
        @pl.when(turn == 1)
        def _():
            wait_of["mc", 0].wait_recv()
            wait_of["mc", 1].wait_recv()

        @pl.when(turn == 2)
        def _():
            swap[3].start()
            wait_of["x", 0].wait_recv()
            on_x0.start()
            wait_of["y", 1].wait_recv()
            on_y1.start()
            to_core[0].start()
            to_core[1].start()
            wait_of["x", 1].wait_recv()
            to_core[2].start()
            wait_of["y", 0].wait_recv()
            to_core[3].start()

        @pl.when(turn == 4)
        def _():
            wait_of["xc", 0].wait_recv()
            wait_of["xc", 1].wait_recv()

        @pl.when(turn == 5)
        def _():
            swap[1].start()
            wait_of["yc", 0].wait_recv()
            wait_of["yc", 1].wait_recv()

        @pl.when(turn == 6)
        def _():
            swap[2].start()
            wait_of["d", 0].wait_recv()
            to_core[4].start()
            wait_of["d", 1].wait_recv()
            to_core[5].start()
            add_core(1, at_x)
            near[2].start()
            add_core(2, at_y)
            near[3].start()

        @pl.when(turn == 7)
        def _():
            wait_of["dc", 0].wait_recv()
            wait_of["dc", 1].wait_recv()

        owner = owners[7]
        for index in range(7):
            owner = jnp.where(turn == index, owners[index], owner)
        up_rows = up[...].reshape(4 * ff_own, D)
        down_rows = down[...].reshape(4 * ff_own, D)

        def part(which, _):
            rows = span(which, 128)
            pre = dot_nt(mid_all[owner, rows, :], up_rows)
            square = pre * pre
            bend = jnp.tanh(GELU_SCALE * (pre + 0.044715 * (pre * square)))
            gl_all[owner, rows, :] = to_low(0.5 * pre * (1.0 + bend))
            slope = 0.5 * (1.0 + bend) + 0.5 * pre * (1.0 - bend * bend) * (
                GELU_SCALE * (1.0 + 3.0 * 0.044715 * square)
            )
            grad = to_low(dot_nt(cot_all[owner, rows, :], down_rows) * slope)
            dpre_all[owner, rows, :] = grad
            work[owner, rows, :] = to_low(dot_nn(grad, up_rows))
            return 0

        lax.fori_loop(0, 2, part, 0)
        return 0

    lax.fori_loop(0, 8, one_chunk, 0)
    swap[0].start()
    add_core(0, at_d)
    near[0].start()
    near[1].start()
    add_core(3, me)

    def grads(index, _):
        quarter, kind = index // 2, lax.rem(index, 2)
        columns = span(quarter, 128)

        @pl.when(kind == 0)
        def _():
            def add(owner, acc):
                return acc + dot_tn(dpre_all[owner, :, columns], mid_all[owner])

            ff_grads[quarter, 0] = to_low(lax.fori_loop(0, 8, add, jnp.zeros((128, D), wide)))

        @pl.when(kind == 1)
        def _():
            def add(owner, acc):
                return acc + dot_tn(gl_all[owner, :, columns], cot_all[owner])

            ff_grads[quarter, 1] = to_low(lax.fori_loop(0, 8, add, jnp.zeros((128, D), wide)))

        return 0

    lax.fori_loop(0, 8, grads, 0)
    near[0].wait_recv()
    add_into(at_y, views[0], near_got[0])
    far[0].start()
    near[1].wait_recv()
    add_into(at_x, views[1], near_got[1])
    far[1].start()
    near[2].wait_recv()
    add_into(me, views[0], near_got[2])
    near[3].wait_recv()
    add_into(me, views[1], near_got[3])

    def outward(owner, _):
        down_rows = down[...].reshape(4 * ff_own, D)
        for which in range(2):
            rows = pl.ds(128 * which, 128)
            extra[owner, rows, :] = to_low(dot_nn(gl_all[owner, rows, :], down_rows))
        return 0

    lax.fori_loop(0, 8, outward, 0)
    for slot, view in enumerate(views):
        far[slot].wait_recv()
        total[view, :] = work[me, view, :].astype(wide) + far_got[slot].astype(wide)
    sums[...] = jnp.zeros_like(sums)

    def back(which, _):
        rows = span(which, 128)
        grad = total[rows, :]
        centered, scale = norm_parts(hidden[which])
        normed = centered * scale
        sums[0:1, :] += jnp.sum(grad * normed, axis=0, keepdims=True)
        lifted = grad * gain
        row_grad = cot_all[me, rows, :].astype(wide) + scale * (
            lifted
            - jnp.mean(lifted, axis=-1, keepdims=True)
            - normed * jnp.mean(lifted * normed, axis=-1, keepdims=True)
        )
        d_hidden[which] = row_grad
        d_low[which] = to_low(row_grad)
        d_rows[which] = to_low(dot_nt(to_low(row_grad), w_out[...].reshape(D, D)))
        return 0

    lax.fori_loop(0, 2, back, 0)

    def line_copy(slot, sender, seq_from, rank_from, seq_to, rank_to):
        return pltpu.make_async_remote_copy(
            src_ref=d_rows.at[seq_to // 2, :, span(2 * rank_to + lax.rem(seq_to, 2), 128)],
            dst_ref=d_line.at[seq_from, span(rank_from, 128), :],
            send_sem=back_send.at[slot],
            recv_sem=back_recv.at[sender],
            device_id={"seq": seq_to, "tensor": rank_to},
            device_id_type=MESH_ID,
        )

    for slot, (_, seq_to, rank_to) in enumerate(peers):
        line_copy(slot, here, place, rank, seq_to, rank_to).start()
    d_line[place, span(rank, 128), :] = d_rows[mine, :, span(head, 128)]
    for index in range(LINE):
        columns = pl.ds(128 * index, 128)
        part = dot_tn(mixed_rows[0, :, columns], d_low[0]) + dot_tn(
            mixed_rows[1, :, columns], d_low[1]
        )
        part = to_low(part)
        for block in range(4):
            extra[
                4 * (index % 2) + block, 256 + 32 * (index // 2) : 288 + 32 * (index // 2), :
            ] = part[32 * block : 32 * block + 32, :]
    for slot, (other, seq_to, rank_to) in enumerate(peers):
        line_copy(slot, other, seq_to, rank_to, seq_to, rank_to).wait_recv()
    for slot, (_, seq_to, rank_to) in enumerate(peers):
        rows_copy(slot, here, place, rank, seq_to, rank_to).wait_send()
        line_copy(slot, here, place, rank, seq_to, rank_to).wait_send()
    for one in own + [on_x0, on_y1] + to_core + swap + near + far:
        one.wait_send()


GELU_SCALE = 0.7978845608028654


def middle(mixed, tokens, kept, spread, cot_all, vecs):
    low, wide = jnp.bfloat16, jnp.float32
    ff_own = (spread.shape[1] - SPREAD_FIRST) // 2
    shapes = (
        ((2, 128, D), wide),
        ((2, 128, D), wide),
        ((4, BLOCK, 128), low),
        ((8, D), wide),
        ((8, 384, D), low),
        ((4, 2, ff_own, D), low),
    )
    dma = pltpu.SemaphoreType.DMA
    return pl.pallas_call(
        middle_kernel,
        out_shape=[jax.ShapeDtypeStruct(*one) for one in shapes],
        in_specs=vmem_specs(2) + any_specs(3) + vmem_specs(1),
        out_specs=vmem_specs(6),
        scratch_shapes=[
            pltpu.VMEM((2, 128, D), low),
            pltpu.VMEM((8, 256, D), low),
            pltpu.VMEM((8, 256, 4 * ff_own), low),
            pltpu.VMEM((8, 256, 4 * ff_own), low),
            pltpu.VMEM((8, 256, D), low),
            pltpu.VMEM((4, 256, D), low),
            pltpu.VMEM((4, 128, D), low),
            pltpu.VMEM((2, 128, D), low),
            pltpu.VMEM((256, D), wide),
            pltpu.VMEM((2, 128, D), low),
            pltpu.VMEM((2, 128, D), low),
            pltpu.VMEM((4, 8, 32, D), low),
            pltpu.VMEM((4, ff_own, D), low),
            pltpu.VMEM((4, ff_own, D), low),
            pltpu.VMEM((8, 256, D), low),
            dma((15,)), dma((16,)), dma((14,)), dma((8, 2)), dma((10,)), dma((10,)), dma((15,)),
            dma((16,)), dma((4,)),
        ],
        compiler_params=pltpu.CompilerParams(
            collective_id=3, has_side_effects=True, vmem_limit_bytes=VMEM_LIMIT
        ),
        cost_estimate=pl.CostEstimate(
            flops=60000000000, bytes_accessed=60000000, transcendentals=0
        ),
        name="middle",
    )(mixed, tokens, kept, spread, cot_all, vecs)


SPREAD_FIRST = 96


WIDE = 2048


def opening_kernel(
    tokens, w_qkv, piece, vecs, line,
    rows_all, qkv, kept, table,
    stage, send_sem, core_sem, recv_sem, piece_send, piece_recv, ring_send, ring_recv,
):
    side, place, half, rank = plane_place()
    mine = place // 2
    core = place + 1 - 2 * half
    other = lax.rem(place + 2, 4)
    me = plane_index(side, place)
    extra = piece.shape[0]
    barrier = pltpu.get_barrier_semaphore()
    greeted = [{"tensor": lax.rem(rank + step, 4)} for step in (1, 2, 3)]
    greeted += [{"seq": core}, {"seq": other}, {"dp": 1 - side}]
    for target in greeted:
        pl.semaphore_signal(barrier, inc=1, device_id=target, device_id_type=MESH_ID)
    gain = vecs[3:4, :]

    def normed(which):
        centered, scale = norm_parts(tokens[which].astype(jnp.float32))
        return to_low(centered * scale * gain)

    def moved(block_id, origin, sem, target):
        view = rows_all.at[block_id, span(origin, 128), :]
        return pltpu.make_async_remote_copy(
            src_ref=view,
            dst_ref=view,
            send_sem=sem,
            recv_sem=recv_sem.at[block_id, origin],
            device_id=target,
            device_id_type=MESH_ID,
        )

    stage[...] = normed(1 - mine)
    kept[me, span(rank, extra), :] = piece[...]
    pl.semaphore_wait(barrier, 6)
    aside = pltpu.make_async_remote_copy(
        src_ref=stage,
        dst_ref=rows_all.at[place, span(rank, 128), :],
        send_sem=send_sem.at[0, 0, 3],
        recv_sem=recv_sem.at[place, rank],
        device_id={"seq": other},
        device_id_type=MESH_ID,
    )
    aside.start()
    rows_all[place, span(rank, 128), :] = normed(mine)
    right, left = {"tensor": lax.rem(rank + 1, 4)}, {"tensor": lax.rem(rank + 3, 4)}
    blocks = (place, other)

    def pass_on(which, distance):
        block_id = blocks[which]

        @pl.when((rank < 3) & (rank >= distance))
        def _():
            moved(block_id, jnp.maximum(rank - distance, 0), send_sem.at[which, distance, 0], right).start()

        @pl.when((rank > 0) & (rank + distance <= 3))
        def _():
            moved(block_id, jnp.minimum(rank + distance, 3), send_sem.at[which, distance, 1], left).start()

    def pass_done(which, distance):
        block_id = blocks[which]

        @pl.when((rank < 3) & (rank >= distance))
        def _():
            moved(block_id, jnp.maximum(rank - distance, 0), send_sem.at[which, distance, 0], right).wait_send()

        @pl.when((rank > 0) & (rank + distance <= 3))
        def _():
            moved(block_id, jnp.minimum(rank + distance, 3), send_sem.at[which, distance, 1], left).wait_send()

    def project(block_id, origin):
        view = span(origin, 128)
        qkv[block_id, view, :] = to_low(dot_nn(rows_all[block_id, view, :], w_qkv[...]))

    def rows_steps():
        pass_on(0, 0)
        moved(place, rank, core_sem.at[0, rank], {"seq": core}).start()
        project(place, rank)
        moved(other, rank, send_sem.at[0, 0, 3], {"seq": other}).wait_recv()
        pass_on(1, 0)
        moved(other, rank, core_sem.at[1, rank], {"seq": core}).start()
        project(other, rank)
        yield
        for distance in (1, 2, 3):
            for which in (0, 1):
                block_id = blocks[which]
                for way, ok, origin in (
                    (0, rank >= distance, jnp.maximum(rank - distance, 0)),
                    (1, rank + distance <= 3, jnp.minimum(rank + distance, 3)),
                ):

                    @pl.when(ok)
                    def _():
                        moved(block_id, origin, send_sem.at[which, distance, way], right).wait_recv()
                        if distance < 3:
                            if way == 0:

                                @pl.when(rank < 3)
                                def _():
                                    moved(
                                        block_id, origin, send_sem.at[which, distance, 0], right
                                    ).start()

                            else:

                                @pl.when(rank > 0)
                                def _():
                                    moved(
                                        block_id, origin, send_sem.at[which, distance, 1], left
                                    ).start()

                        moved(block_id, origin, core_sem.at[which, origin], {"seq": core}).start()
                        project(block_id, origin)

                yield
        for which, block_id in enumerate((core, lax.rem(core + 2, 4))):
            for origin in range(4):
                moved(block_id, origin, core_sem.at[which, origin], {"seq": core}).wait_recv()
                project(block_id, origin)
        for which in (0, 1):
            for distance in (0, 1, 2):
                pass_done(which, distance)
            for origin in range(4):
                moved(blocks[which], origin, core_sem.at[which, origin], {"seq": core}).wait_send()

    def piece_move(slot, origin, target):
        view = kept.at[me, span(origin, extra), :]
        return pltpu.make_async_remote_copy(
            src_ref=view,
            dst_ref=view,
            send_sem=piece_send.at[slot],
            recv_sem=piece_recv.at[origin],
            device_id=target,
            device_id_type=MESH_ID,
        )

    def piece_steps():
        for slot in range(3):
            piece_move(slot, rank, greeted[slot]).start()
        first = line[...]
        row = lax.broadcasted_iota(jnp.int32, (8, WIDE), 0)
        for step in (1, 2, 4):
            first = jnp.where(row // step % 2 == 1, pltpu.roll(first, step, 1), first)

        def one(group, _):
            table[span(group, 8), :] = pltpu.roll(first, 8 * group, 1)[:, 0 : 2 * BLOCK]
            return 0

        lax.fori_loop(0, BLOCK // 8, one, 0)
        yield
        for slot in range(3):
            piece_move(slot, lax.rem(rank + slot + 1, 4), greeted[slot]).wait_recv()
        for _ in plane_gather(kept, 4 * extra, ring_send, ring_recv):
            yield
        for slot in range(3):
            piece_move(slot, rank, greeted[slot]).wait_send()

    run_all(rows_steps(), piece_steps())
    aside.wait_send()


def opening(tokens, w_qkv, piece, vecs, line):
    low, wide = jnp.bfloat16, jnp.float32
    extra = piece.shape[0]
    shapes = (
        ((4, BLOCK, D), low),
        ((4, BLOCK, 384), low),
        ((8, 4 * extra, D), low),
        ((BLOCK, 2 * BLOCK), wide),
    )
    return pl.pallas_call(
        opening_kernel,
        out_shape=[jax.ShapeDtypeStruct(*one) for one in shapes],
        in_specs=vmem_specs(5),
        out_specs=vmem_specs(4),
        scratch_shapes=[
            pltpu.VMEM((128, D), low),
            pltpu.SemaphoreType.DMA((2, 4, 4)),
            pltpu.SemaphoreType.DMA((2, 4)),
            pltpu.SemaphoreType.DMA((4, 4)),
            pltpu.SemaphoreType.DMA((3,)),
            pltpu.SemaphoreType.DMA((4,)),
            pltpu.SemaphoreType.DMA((16,)),
            pltpu.SemaphoreType.DMA((8, 2)),
        ],
        compiler_params=pltpu.CompilerParams(
            collective_id=5, has_side_effects=True, vmem_limit_bytes=VMEM_LIMIT
        ),
        cost_estimate=pl.CostEstimate(
            flops=30000000000, bytes_accessed=30000000, transcendentals=0
        ),
        name="opening",
    )(tokens, w_qkv, piece, vecs, line)


def pair_sum(part, near_got, far_got, result, rows, send_sem, recv_sem):
    side, place, half, rank = plane_place()
    mine = place // 2
    across, beside = 1 - side, 1 - mine
    me = 2 * side + mine
    at_x, at_y, at_d = 2 * across + mine, 2 * side + beside, 2 * across + beside
    to_x, to_y = {"dp": across}, {"seq": lax.rem(place + 2, 4)}
    size = rows // 2
    views = (pl.ds(0, size), pl.ds(size, size))

    def moved(source, target_ref, slot, target):
        return pltpu.make_async_remote_copy(
            src_ref=source,
            dst_ref=target_ref,
            send_sem=send_sem.at[slot],
            recv_sem=recv_sem.at[slot],
            device_id=target,
            device_id_type=MESH_ID,
        )

    def add_into(owner, view, other):
        part[owner, view, :] = to_low(
            part[owner, view, :].astype(jnp.float32) + other.astype(jnp.float32)
        )

    near = [
        moved(part.at[at_d, views[0], :], near_got.at[0], 0, to_x),
        moved(part.at[at_d, views[1], :], near_got.at[1], 1, to_y),
        moved(part.at[at_x, views[0], :], near_got.at[2], 2, to_x),
        moved(part.at[at_y, views[1], :], near_got.at[3], 3, to_y),
    ]
    for one in near:
        one.start()
    yield
    near[0].wait_recv()
    add_into(at_y, views[0], near_got[0])
    far = [
        moved(part.at[at_y, views[0], :], far_got.at[0], 4, to_y),
        moved(part.at[at_x, views[1], :], far_got.at[1], 5, to_x),
    ]
    far[0].start()
    near[1].wait_recv()
    add_into(at_x, views[1], near_got[1])
    far[1].start()
    yield
    near[2].wait_recv()
    add_into(me, views[0], near_got[2])
    near[3].wait_recv()
    add_into(me, views[1], near_got[3])
    for slot, view in enumerate(views):
        far[slot].wait_recv()
        result[me, view, :] = to_low(
            part[me, view, :].astype(jnp.float32) + far_got[slot].astype(jnp.float32)
        )

    def given(owner, which, slot, target):
        view = result.at[owner, views[which], :]
        return moved(view, view, slot, target)

    own = [
        given(me, 0, 6, to_x),
        given(me, 1, 7, to_y),
        given(me, 1, 8, to_x),
        given(me, 0, 9, to_y),
    ]
    for one in own:
        one.start()
    yield
    given(at_x, 0, 6, to_x).wait_recv()
    last = [given(at_x, 0, 10, to_y), given(at_y, 1, 11, to_x)]
    last[0].start()
    given(at_y, 1, 7, to_y).wait_recv()
    last[1].start()
    yield
    given(at_x, 1, 8, to_x).wait_recv()
    given(at_y, 0, 9, to_y).wait_recv()
    given(at_d, 0, 10, to_y).wait_recv()
    given(at_d, 1, 11, to_x).wait_recv()
    for one in near + far + own + last:
        one.wait_send()


PAIR_ROWS = 640


def closing_kernel(
    d_qkv, w_qkv, tokens, d_hidden, vecs, rows_hbm, low_hbm, d_qkvst_hbm, os_hbm, du_hbm,
    d_start, dz_hbm, small, out_part,
    inputs_grad, pair_out, sout_out, small_out,
    rows_all, state_low, d_qkvst, os_rows, du_rows, dz_sum,
    leave, came, sums, got, final, cross, cross_got,
    pair_part, pair_near, pair_far,
    work, core_got, near_got, far_got, total, z_part, z_got,
    diag, small_z, small_p,
    line_send, line_recv, way_send, way_recv, pair_send, pair_recv, core_sem,
    ring_send, ring_recv, zs_send, zs_recv, gather_send, gather_recv, small_send, small_recv, local_sem,
):
    loads = [
        pltpu.make_async_copy(source, target, local_sem.at[slot])
        for slot, (source, target) in enumerate(
            (
                (rows_hbm, rows_all),
                (d_qkvst_hbm, d_qkvst),
                (low_hbm, state_low),
                (os_hbm, os_rows),
                (du_hbm, du_rows),
                (dz_hbm, dz_sum),
            )
        )
    ]
    for one in loads:
        one.start()
    side, place, half, rank = plane_place()
    mine = place // 2
    core = place + 1 - 2 * half
    other = lax.rem(place + 2, 4)
    me = plane_index(side, place)
    ranks = [lax.rem(rank + step, 4) for step in (1, 2, 3)]
    spots_of = [lax.rem(me + step, 8) for step in range(1, 8)]
    barrier = pltpu.get_barrier_semaphore()
    for target in ranks:
        pl.semaphore_signal(barrier, inc=1, device_id={"tensor": target}, device_id_type=MESH_ID)
    for target in spots_of:
        pl.semaphore_signal(
            barrier,
            inc=1,
            device_id={"dp": target // 4, "seq": lax.rem(target, 4)},
            device_id_type=MESH_ID,
        )
    gain = vecs[3:4, :]
    right, left = {"tensor": lax.rem(rank + 1, 4)}, {"tensor": lax.rem(rank + 3, 4)}

    def moved(source, target_ref, send, recv, target):
        return pltpu.make_async_remote_copy(
            src_ref=source,
            dst_ref=target_ref,
            send_sem=send,
            recv_sem=recv,
            device_id=target,
            device_id_type=MESH_ID,
        )

    def to_core(which):
        return moved(
            leave.at[which], came.at[which], line_send.at[which], line_recv.at[which], {"seq": core}
        )

    def crossing():
        return moved(cross, cross_got, line_send.at[2], line_recv.at[2], {"seq": other})

    near = rank // 2
    at_end = (rank == 0) | (rank == 3)

    def hop(way, which, target):
        return moved(
            sums.at[which, target],
            got.at[way, which, target],
            way_send.at[which, target],
            way_recv.at[way, which, target],
            {"tensor": lax.rem(rank + 5 - 2 * way, 4)},
        )

    def target_of(way, distance):
        return (1 - way) * (3 - distance) + way * distance

    def pass_first(which):
        @pl.when(at_end)
        def _():
            for distance in range(3):
                hop(near, which, target_of(near, distance)).start()

    def pass_on(way, which, distance):
        @pl.when(jnp.logical_not(at_end))
        def _():
            target = target_of(way, distance)
            hop(way, which, target).wait_recv()
            sums[which, target] = to_low(
                sums[which, target].astype(jnp.float32)
                + got[way, which, target].astype(jnp.float32)
            )
            hop(way, which, target).start()

    def finish(which):
        final[which] = sums[which, rank].astype(jnp.float32)

        @pl.when(rank > 0)
        def _():
            hop(0, which, rank).wait_recv()
            final[which] += got[0, which, rank].astype(jnp.float32)

        @pl.when(rank < 3)
        def _():
            hop(1, which, rank).wait_recv()
            final[which] += got[1, which, rank].astype(jnp.float32)

    def line_steps():
        for which, block_id in enumerate((lax.rem(core + 2, 4), core)):

            def partner(chunk, _):
                rows = span(chunk, ROWS)
                leave[which, rows, :] = to_low(dot_nt(d_qkv[block_id, rows, :], w_qkv[...]))
                return 0

            lax.fori_loop(0, CHUNKS, partner, 0)
            if which == 0:
                pl.semaphore_wait(barrier, 10)
            to_core(which).start()
        for which, block_id in enumerate((other, place)):
            to_core(which).wait_recv()

            def own(chunk, _):
                rows = span(chunk, ROWS)
                sums[which, chunk] = to_low(
                    dot_nt(d_qkv[block_id, rows, :], w_qkv[...])
                    + came[which, rows, :].astype(jnp.float32)
                )
                return 0

            lax.fori_loop(0, CHUNKS, own, 0)
            pass_first(which)
        yield
        for which in (0, 1):
            pass_on(near, which, 0)
            yield
            pass_on(near, which, 1)
            pass_on(1 - near, which, 0)
            yield
            finish(which)
            if which == 0:
                cross[...] = to_low(final[0])
                crossing().start()
            yield
        crossing().wait_recv()
        final[0] = cross_got[...].astype(jnp.float32)
        small_z[rank] = small[...]
        for which, row_set in ((1, mine), (0, 1 - mine)):
            grad = final[which]
            centered, scale = norm_parts(tokens[row_set].astype(jnp.float32))
            normed = centered * scale
            small_z[rank, 0:1, :] += jnp.sum(grad * normed, axis=0, keepdims=True)
            lifted = grad * gain
            inputs_grad[row_set] = d_hidden[row_set] + scale * (
                lifted
                - jnp.mean(lifted, axis=-1, keepdims=True)
                - normed * jnp.mean(lifted * normed, axis=-1, keepdims=True)
            )
        crossing().wait_send()
        for which in (0, 1):
            to_core(which).wait_send()
            for target in range(4):

                @pl.when(rank != target)
                def _():
                    hop(0, which, target).wait_send()

    def pair_steps():
        loads[0].wait()
        loads[1].wait()
        loads[2].wait()
        for chunk in range(4):
            if chunk < 3:
                first = 128 * chunk

                def one(block_id, acc):
                    acc = acc + dot_tn(d_qkv[block_id, :, first : first + 128], rows_all[block_id])
                    if chunk > 0:
                        acc = acc + dot_tn(
                            d_qkvst[block_id, :, first : first + 128], state_low[block_id]
                        )
                    return acc

            else:

                def one(block_id, acc):
                    return acc + dot_tn(d_qkvst[block_id, :, 0:128], state_low[block_id])

            acc = lax.fori_loop(0, 4, one, jnp.zeros((128, D), jnp.float32))
            low = to_low(acc)
            first = 128 * chunk
            while first < 128 * (chunk + 1):
                owner, inside = first // 160, first % 160
                size = min(160 - inside, 128 * (chunk + 1) - first)
                begin = first - 128 * chunk
                pair_part[owner, inside : inside + size, :] = low[begin : begin + size, :]
                first += size
        pair_part[3, 32:96, :] = to_low(d_start[...])
        pair_part[3, 96:160, :] = jnp.zeros((64, D), jnp.bfloat16)
        for _ in pair_sum(
            pair_part, pair_near, pair_far, pair_out.at[half], 160, pair_send, pair_recv
        ):
            yield
        full = moved(
            pair_out.at[half], pair_out.at[half], core_sem.at[0], core_sem.at[1], {"seq": core}
        )
        full.start()
        yield
        moved(
            pair_out.at[1 - half], pair_out.at[1 - half], core_sem.at[0], core_sem.at[1],
            {"seq": core},
        ).wait_recv()
        full.wait_send()

    def sout_steps():
        loads[3].wait()
        loads[4].wait()
        for head in range(LINE):
            low = to_low(dot_tn(os_rows[:, 128 * head : 128 * head + 128], du_rows[...]))
            for piece in range(4):
                work[
                    4 * (head % 2) + piece, 32 * (head // 2) : 32 * (head // 2) + 32, :
                ] = low[32 * piece : 32 * piece + 32, :]
        for _ in plane_scatter(
            work, core_got, near_got, far_got, total, 128, ring_send, ring_recv
        ):
            yield
        z_part[:, 0:32, :] = to_low(total[...]).reshape(4, 32, D)
        z_part[:, 32:64, :] = out_part[...].reshape(4, 32, D)
        out = [
            moved(
                z_part.at[target], z_got.at[rank], zs_send.at[slot], zs_recv.at[rank],
                {"tensor": target},
            )
            for slot, target in enumerate(ranks)
        ]
        for one in out:
            one.start()
        z_got[rank] = z_part[rank]
        yield
        for slot, target in enumerate(ranks):
            moved(
                z_part.at[target], z_got.at[target], zs_send.at[slot], zs_recv.at[target],
                {"tensor": target},
            ).wait_recv()
        acc = z_got[0].astype(jnp.float32)
        for target in range(1, 4):
            acc = acc + z_got[target].astype(jnp.float32)
        sout_out[me] = to_low(acc)
        for _ in plane_gather(sout_out, 64, gather_send, gather_recv):
            yield
        for one in out:
            one.wait_send()

    def diag_steps():
        loads[5].wait()
        diag[...] = jnp.zeros_like(diag)
        for part in range(4):

            def one(group, _):
                rows = dz_sum[span(group, 8), :]
                wide = jnp.concatenate(
                    [rows, jnp.zeros((8, WIDE - 2 * BLOCK), jnp.float32)], axis=1
                )
                diag[...] += pltpu.roll(wide, lax.rem(WIDE - 8 * group, WIDE), 1)
                return 0

            lax.fori_loop(16 * part, 16 * part + 16, one, 0)
            yield
        total_line = diag[...]
        row = lax.broadcasted_iota(jnp.int32, (8, WIDE), 0)
        for step in (1, 2, 4):
            total_line = jnp.where(
                row // step % 2 == 1, pltpu.roll(total_line, WIDE - step, 1), total_line
            )
        lane = lax.broadcasted_iota(jnp.int32, (8, WIDE), 1)
        offset = jnp.where(lane >= WIDE - BLOCK, lane - WIDE - BLOCK, lane - BLOCK)
        bucket_ids = bucket_of(offset)
        spot = lax.broadcasted_iota(jnp.int32, (1, 256), 1) - BUCKETS * (2 * rank + half)
        placed = jnp.zeros((1, 256), jnp.float32)
        for bucket_id in range(BUCKETS):
            chosen = jnp.where(bucket_ids == bucket_id, total_line, 0.0)
            value = jnp.sum(jnp.sum(chosen, axis=0, keepdims=True), axis=1, keepdims=True)
            placed = jnp.where(spot == bucket_id, value, placed)
        diag[0:1, 0:256] = placed

    extra = sout_steps()
    run_all(line_steps(), pair_steps(), extra, diag_steps(), extra)
    small_z[rank, 4:5, 0:256] = diag[0:1, 0:256]

    def small_over_z(slot, sender, target):
        return moved(
            small_z.at[sender], small_z.at[sender], small_send.at[slot], small_recv.at[sender],
            {"tensor": target},
        )

    for slot, target in enumerate(ranks):
        small_over_z(slot, rank, target).start()
    for slot, target in enumerate(ranks):
        small_over_z(slot, target, target).wait_recv()
    small_p[me] = small_z[0] + small_z[1] + small_z[2] + small_z[3]

    def small_over_plane(slot, sender, target):
        return moved(
            small_p.at[sender], small_p.at[sender], small_send.at[3 + slot],
            small_recv.at[4 + sender],
            {"dp": target // 4, "seq": lax.rem(target, 4)},
        )

    for slot, target in enumerate(spots_of):
        small_over_plane(slot, me, target).start()
    for slot, target in enumerate(spots_of):
        small_over_plane(slot, target, target).wait_recv()
    acc = small_p[0]
    for target in range(1, 8):
        acc = acc + small_p[target]
    small_out[...] = acc
    for slot, target in enumerate(ranks):
        small_over_z(slot, rank, target).wait_send()
    for slot, target in enumerate(spots_of):
        small_over_plane(slot, me, target).wait_send()


def closing(
    d_qkv, w_qkv, tokens, d_hidden, vecs, rows_all, state_low, d_qkvst, os_rows, du_rows,
    d_start, dz_sum, small, out_part,
):
    low, wide = jnp.bfloat16, jnp.float32
    shapes = (
        ((2, 128, D), wide),
        ((2, 4, PAIR_ROWS // 4, D), low),
        ((8, 64, D), low),
        ((8, D), wide),
    )
    dma = pltpu.SemaphoreType.DMA
    return pl.pallas_call(
        closing_kernel,
        out_shape=[jax.ShapeDtypeStruct(*one) for one in shapes],
        in_specs=vmem_specs(5) + any_specs(5) + vmem_specs(1) + any_specs(1) + vmem_specs(2),
        out_specs=vmem_specs(4),
        scratch_shapes=[
            pltpu.VMEM((4, BLOCK, D), low),
            pltpu.VMEM((4, BLOCK, D), low),
            pltpu.VMEM((4, BLOCK, 384), low),
            pltpu.VMEM((256, D), low),
            pltpu.VMEM((256, D), low),
            pltpu.VMEM((BLOCK, 2 * BLOCK), wide),
            pltpu.VMEM((2, BLOCK, D), low),
            pltpu.VMEM((2, BLOCK, D), low),
            pltpu.VMEM((2, 4, 128, D), low),
            pltpu.VMEM((2, 2, 4, 128, D), low),
            pltpu.VMEM((2, 128, D), wide),
            pltpu.VMEM((128, D), low),
            pltpu.VMEM((128, D), low),
            pltpu.VMEM((4, PAIR_ROWS // 4, D), low),
            pltpu.VMEM((4, PAIR_ROWS // 8, D), low),
            pltpu.VMEM((2, PAIR_ROWS // 8, D), low),
            pltpu.VMEM((8, 128, D), low),
            pltpu.VMEM((4, 128, D), low),
            pltpu.VMEM((4, 64, D), low),
            pltpu.VMEM((2, 64, D), low),
            pltpu.VMEM((128, D), wide),
            pltpu.VMEM((4, 64, D), low),
            pltpu.VMEM((4, 64, D), low),
            pltpu.VMEM((8, WIDE), wide),
            pltpu.VMEM((4, 8, D), wide),
            pltpu.VMEM((8, 8, D), wide),
            dma((3,)), dma((3,)), dma((2, 4)), dma((2, 2, 4)), dma((12,)), dma((12,)), dma((2,)),
            dma((10,)), dma((10,)), dma((3,)), dma((4,)), dma((16,)), dma((8, 2)), dma((10,)),
            dma((12,)), dma((6,)),
        ],
        compiler_params=pltpu.CompilerParams(
            collective_id=6, has_side_effects=True, vmem_limit_bytes=VMEM_LIMIT
        ),
        cost_estimate=pl.CostEstimate(
            flops=30000000000, bytes_accessed=30000000, transcendentals=0
        ),
        name="closing",
    )(
        d_qkv, w_qkv, tokens, d_hidden, vecs, rows_all, state_low, d_qkvst, os_rows, du_rows,
        d_start, dz_sum, small, out_part,
    )


def finish_kernel(
    pair, pair_tail, two, ff,
    query, key, value, squery, out, sout, up, down, state,
):
    step = pl.program_id(0)
    wide = jnp.float32
    up[...] = ff[0, 0].astype(wide).T
    down[...] = ff[0, 1].astype(wide)
    sout[...] = two[0, 0:32].astype(wide)
    out[...] = two[0, 32:64].astype(wide)
    for which, target in enumerate((query, key, value, squery)):

        @pl.when(step // 2 == which)
        def _():
            target[...] = pair[0].astype(wide).T

    @pl.when(step == 0)
    def _():
        state[...] = pair_tail[...].reshape(128, D).astype(wide)


def finish_grads(pair, two, ff):
    wide = jnp.float32
    turned = [
        pl.BlockSpec((D, 128), lambda i, w=which: (0, jnp.clip(i - 2 * w, 0, 1)))
        for which in range(4)
    ]
    square = jax.ShapeDtypeStruct((D, 256), wide)
    rows = jax.ShapeDtypeStruct((256, D), wide)
    whole = jax.ShapeDtypeStruct((D, D), wide)
    return pl.pallas_call(
        finish_kernel,
        grid=(8,),
        out_shape=[square] * 4 + [rows] * 2 + [whole] * 2 + [jax.ShapeDtypeStruct((128, D), wide)],
        in_specs=[
            pl.BlockSpec((1, 128, D), lambda i: (i % 2, i // 2, 0)),
            pl.BlockSpec((2, 64, D), lambda i: (0, 8, 0)),
            pl.BlockSpec((1, 64, D), lambda i: (i, 0, 0)),
            pl.BlockSpec((1, 2, 128, D), lambda i: (i, 0, 0, 0)),
        ],
        out_specs=turned
        + [pl.BlockSpec((32, D), lambda i: (i, 0))] * 2
        + [pl.BlockSpec((D, 128), lambda i: (0, i)), pl.BlockSpec((128, D), lambda i: (i, 0))]
        + [pl.BlockSpec((128, D), lambda i: (0, 0))],
        compiler_params=pltpu.CompilerParams(vmem_limit_bytes=VMEM_LIMIT),
        name="finish_grads",
    )(pair, pair, two, ff)


def swap_seq(value):
    return lax.all_to_all(value, "seq", 0, 0, tiled=False)


def line_body(
    inputs,
    seg_starts,
    lengths,
    init_state,
    attn_gain,
    state_gain,
    mlp_gain,
    w_query,
    w_key,
    w_value,
    w_out,
    w_squery,
    w_sout,
    w_up,
    w_down,
    rel_bias,
    gate_bias,
    out_cot,
    state_cot,
):
    low, wide = jnp.bfloat16, jnp.float32
    place = lax.axis_index("seq")
    half = lax.rem(place, 2)
    mine = place // 2
    plane = ("dp", "seq")
    spot = 4 * lax.axis_index("dp") + place
    head_of = lambda weight: lax.dynamic_slice_in_dim(weight, half * 128, 128, 1)
    gate_value = jax.nn.sigmoid(gate_bias)
    vecs = jnp.stack(
        [state_gain, gate_value, mlp_gain, attn_gain] + [jnp.zeros_like(gate_value)] * 4
    )
    offsets = jnp.arange(WIDE) - BLOCK
    offsets = jnp.where(offsets >= WIDE - 2 * BLOCK, offsets - WIDE, offsets)
    bucket_ids = bucket_of(offsets)
    one_hot = bucket_ids[:, None] == jnp.arange(BUCKETS)[None, :]
    my_bias = jnp.where(half == 0, rel_bias[:, 0], rel_bias[:, 1])
    bias_line = jnp.sum(jnp.where(one_hot, my_bias[None, :], 0.0), axis=1)
    segs = jnp.broadcast_to(jnp.repeat(seg_starts[:, 0], 2)[:, None, None], (4, 1, 128))
    segs = swap_seq(segs)[:, 0, 0]
    cots = swap_seq(state_cot.reshape(4, 64, D))
    cot_used = lax.all_gather(out_cot.reshape(256, D), plane, axis=0, tiled=True)

    w_qkv = jnp.concatenate([head_of(w_query), head_of(w_key), head_of(w_value)], axis=1)
    w_state = jnp.concatenate([head_of(w_squery), w_qkv[:, 128:]], axis=1)
    piece = jnp.concatenate(
        [
            lax.dynamic_slice_in_dim(w_sout, spot * 32, 32, 0),
            to_low(lax.dynamic_slice_in_dim(init_state, spot * 16, 16, 0)),
            lax.dynamic_slice_in_dim(w_out, spot * 32, 32, 0),
        ],
        axis=0,
    )
    rows_all, qkv, kept, bias = opening(
        inputs, w_qkv, piece, vecs, jnp.broadcast_to(bias_line[None, :], (8, WIDE))
    )
    kept = kept.reshape(8, 4, 80, D)

    ff_own = w_up.shape[1] // 8
    piece_of = lambda weight: lax.dynamic_slice_in_dim(weight, spot * 32, 32, 1).T
    pieces = jnp.concatenate(
        [
            piece_of(w_squery),
            piece_of(w_key),
            piece_of(w_value),
            lax.dynamic_slice_in_dim(w_up, spot * ff_own, ff_own, 1).T,
            lax.dynamic_slice_in_dim(w_down, spot * ff_own, ff_own, 0),
        ],
        axis=0,
    )
    qkv, pieces, segs, cot_used = lax.optimization_barrier((qkv, pieces, segs, cot_used))
    scal = jnp.concatenate([lax.dynamic_slice_in_dim(lengths, mine, 1, 0), segs])
    spread = lax.all_gather(pieces, "tensor", axis=0, tiled=True).reshape(4, 96 + 2 * ff_own, D)
    mixed, lse_tok, state_rows, state_low, qkvst, lse_st, os_rows = forward_chain(
        scal, qkv, kept, w_state, vecs, bias
    )
    mixed, back_piece, cots = lax.optimization_barrier(
        (mixed, spread[:, 0:96].reshape(384, D), cots)
    )
    w_back = lax.all_gather(back_piece, plane, axis=0, tiled=True)
    hidden_in, grad_hidden, d_mixed, mlp_sums, extra, ff_grads = middle(
        mixed, inputs, kept, spread, cot_used.reshape(8, 256, D), vecs
    )
    d_mixed, w_back, ff_grads = lax.optimization_barrier((d_mixed, w_back, ff_grads))
    ff_sum = lax.psum_scatter(
        ff_grads.reshape(ff_grads.shape[2] * 8, D), "tensor", scatter_dimension=0, tiled=True
    )
    (
        d_qkv, d_qkvst, du_rows, d_start, sums, dz_sum, state_out, tokens_out, out_part,
    ) = backward_chain(
        scal, qkv, d_mixed, lse_tok, qkvst, lse_st, state_rows, init_state, cots,
        w_back.reshape(8, 4, 3, 32, D), kept, vecs, bias, extra, hidden_in,
    )
    d_qkv, ff_sum = lax.optimization_barrier((d_qkv, ff_sum))
    ff_total = lax.all_gather(ff_sum, plane, axis=0, tiled=True).reshape(8, 2, ff_own, D)
    small = jnp.concatenate(
        [jnp.zeros((1, D), wide), sums[1:2], mlp_sums[0:1], sums[0:1], jnp.zeros((4, D), wide)]
    )
    inputs_grad, pair, two_grads, small = closing(
        d_qkv, w_qkv, inputs, grad_hidden, vecs, rows_all, state_low, d_qkvst,
        os_rows.reshape(256, D), du_rows.reshape(256, D), d_start, dz_sum, small, out_part,
    )
    pair = pair.reshape(2, PAIR_ROWS, D)
    (
        query_grad, key_grad, value_grad, squery_grad, out_grad, sout_grad, up_grad, down_grad,
        state_grad,
    ) = finish_grads(pair, two_grads, ff_total)
    bias_grad = lax.dynamic_slice_in_dim(
        small[4, : LINE * BUCKETS].reshape(4, 2, BUCKETS), lax.axis_index("tensor"), 1, 0
    )[0].T
    return (
        tokens_out,
        state_out[:, None],
        inputs_grad,
        state_grad,
        small[0],
        small[1],
        small[2],
        query_grad,
        key_grad,
        value_grad,
        out_grad,
        squery_grad,
        sout_grad,
        up_grad,
        down_grad,
        bias_grad,
        small[3],
    )


def solution(mesh):
    return jax.shard_map(
        chosen_body(mesh),
        mesh=mesh,
        in_specs=(
            P("dp", ("seq", "tensor"), None),
            P("dp", "seq"),
            P("dp"),
            P("tensor", None),
            P(),
            P(),
            P(),
            P(None, "tensor"),
            P(None, "tensor"),
            P(None, "tensor"),
            P("tensor", None),
            P(None, "tensor"),
            P("tensor", None),
            P(None, "tensor"),
            P("tensor", None),
            P(None, "tensor"),
            P(),
            P("dp", ("seq", "tensor"), None),
            P("dp", "seq", "tensor", None),
        ),
        out_specs=(
            P("dp", ("seq", "tensor"), None),
            P("dp", "seq", "tensor", None),
            P("dp", ("seq", "tensor"), None),
            P("tensor", None),
            P(),
            P(),
            P(),
            P(None, "tensor"),
            P(None, "tensor"),
            P(None, "tensor"),
            P("tensor", None),
            P(None, "tensor"),
            P("tensor", None),
            P(None, "tensor"),
            P("tensor", None),
            P(None, "tensor"),
            P(),
        ),
        check_vma=False,
    )
```

```python
import jax
import jax.numpy as jnp
from jax import lax
from jax.experimental import pallas as pl
from jax.experimental.pallas import tpu as pltpu
from jax.sharding import PartitionSpec as P

D = 1024
HEAD_DIM = 128
STATES = 512
BLOCK = 512
SEG = 256
BUCKETS = 32


norm_eps = 1e-06
masked_score = -1e30
bucket_edges = (12, 16, 23, 32, 46, 64, 91)


def passed_along(value, axis, steps):
    count = lax.axis_size(axis)
    leading, last = (max(0, -steps), min(count, count - steps))
    return lax.ppermute(value, axis, [(source, source + steps) for source in range(leading, last)])


def bucket_of(relative):
    distance = jnp.abs(relative)
    far_bucket = 8 + sum(((distance >= boundary).astype(jnp.int32) for boundary in bucket_edges))
    near_far = jnp.where(distance < 8, distance, far_bucket)
    return near_far + 16 * (relative > 0).astype(jnp.int32)


def token_mask(seg_start, seq_length, block_index):
    positions = jnp.arange(BLOCK)
    offset = block_index * BLOCK
    prev_valid = (block_index > 0) & (offset - BLOCK + positions < seq_length)
    cur_valid = offset + positions < seq_length
    inside = (positions >= seg_start) & (positions < seg_start + SEG)
    prev_mask = (positions[None, :] > positions[:, None]) & prev_valid[None, :]
    cur_mask = (
        (positions[None, :] <= positions[:, None]) | inside[None, :] & inside[:, None]
    ) & cur_valid[None, :]
    state_mask = jnp.ones((BLOCK, STATES), jnp.bool_)
    return jnp.concatenate([prev_mask, cur_mask, state_mask], axis=1)


def state_mask_of(valid_blk):
    batch_count = valid_blk.shape[0]
    block_part = jnp.broadcast_to(valid_blk[:, None, :], (batch_count, STATES, BLOCK))
    return jnp.concatenate([block_part, jnp.ones((batch_count, STATES, STATES), jnp.bool_)], axis=2)


def layer_norm(values, gain_vec):
    centered = values - jnp.mean(values, axis=-1, keepdims=True)
    spread = jnp.mean(centered * centered, axis=-1, keepdims=True)
    return centered * lax.rsqrt(spread + norm_eps) * gain_vec


def norm_back(values, gain_vec, grad_out):
    _, pullback = jax.vjp(layer_norm, values, gain_vec)
    return pullback(grad_out)


def gelu_back(pre_act, grad_out):
    _, pullback = jax.vjp(jax.nn.gelu, pre_act)
    return pullback(grad_out)[0]


def to_low(array_in):
    return array_in.astype(jnp.bfloat16)


def matmul(left, right):
    return jnp.einsum("...k,kn->...n", left, right, preferred_element_type=jnp.float32)


def matmul_t(left, right):
    return jnp.einsum("...n,kn->...k", left, right, preferred_element_type=jnp.float32)


def outer_sum(left, right):
    left_flat = left.reshape(-1, left.shape[-1])
    right_flat = right.reshape(-1, right.shape[-1])
    return lax.dot_general(
        left_flat, right_flat, (((0,), (0,)), ((), ())), preferred_element_type=jnp.float32
    )


def gather_rows(values):
    return lax.all_gather(values, "tensor", axis=1, tiled=True)


def sum_rows(terms):
    return lax.psum_scatter(
        terms.astype(jnp.bfloat16), "tensor", scatter_dimension=1, tiled=True
    ).astype(jnp.float32)


def pass_state(rows_now):
    return passed_along(rows_now.astype(jnp.bfloat16), "seq", 1).astype(rows_now.dtype)


def pass_back(grad_now):
    return passed_along(grad_now.astype(jnp.bfloat16), "seq", -1).astype(grad_now.dtype)


def split_heads(rows_in):
    return rows_in.reshape(rows_in.shape[0], rows_in.shape[1] // HEAD_DIM, HEAD_DIM)


def score_block(query_rows, key_all, bias_all, allowed):
    scores = (
        jnp.einsum(
            "qhd,khd->hqk",
            split_heads(query_rows),
            split_heads(key_all),
            preferred_element_type=jnp.float32,
        )
        * HEAD_DIM ** (-0.5)
        + bias_all
    )
    return jnp.where(allowed[None], scores, masked_score)


def attend_forward(query_rows, key_all, value_all, bias_all, allowed):
    scores = score_block(query_rows, key_all, bias_all, allowed)
    row_max = jnp.max(scores, axis=-1, keepdims=True)
    exp_scores = jnp.exp(scores - row_max)
    row_total = jnp.sum(exp_scores, axis=-1, keepdims=True)
    weight_all = to_low(exp_scores / row_total)
    mixed_out = jnp.einsum(
        "hqk,khd->qhd", weight_all, split_heads(value_all), preferred_element_type=jnp.float32
    )
    return (
        to_low(mixed_out.reshape(query_rows.shape[0], -1)),
        (row_max + jnp.log(row_total))[..., 0],
    )


def attend_back(query_rows, key_all, value_all, bias_all, allowed, log_total, grad_mixed):
    scores = score_block(query_rows, key_all, bias_all, allowed)
    weight_all = jnp.where(allowed[None], jnp.exp(scores - log_total[..., None]), 0.0)
    grad_heads = split_heads(grad_mixed)
    grad_weight = jnp.einsum(
        "qhd,khd->hqk", grad_heads, split_heads(value_all), preferred_element_type=jnp.float32
    )
    row_inner = jnp.sum(weight_all * grad_weight, axis=-1, keepdims=True)
    grad_scores = to_low(weight_all * (grad_weight - row_inner))
    grad_query = jnp.einsum(
        "hqk,khd->qhd", grad_scores, split_heads(key_all), preferred_element_type=jnp.float32
    ) * HEAD_DIM ** (-0.5)
    grad_keys = jnp.einsum(
        "hqk,qhd->khd", grad_scores, split_heads(query_rows), preferred_element_type=jnp.float32
    ) * HEAD_DIM ** (-0.5)
    grad_values = jnp.einsum(
        "hqk,qhd->khd", to_low(weight_all), grad_heads, preferred_element_type=jnp.float32
    )
    return (
        grad_query.reshape(query_rows.shape[0], -1),
        grad_keys.reshape(key_all.shape[0], -1),
        grad_values.reshape(key_all.shape[0], -1),
        grad_scores,
    )


def bias_lookup(rel_bias, rel_table):
    table_heads = jnp.zeros((rel_bias.shape[1],) + rel_table.shape, jnp.float32)
    for bucket_id in range(BUCKETS):
        table_heads = table_heads + jnp.where(
            rel_table[None] == bucket_id, rel_bias[bucket_id][:, None, None], 0.0
        )
    return table_heads


def bias_sums(score_grad, rel_table):
    grad_wide = score_grad.astype(jnp.float32)
    columns = []
    for bucket_id in range(BUCKETS):
        columns.append(
            jnp.sum(jnp.where(rel_table[None, None] == bucket_id, grad_wide, 0.0), axis=(0, 2, 3))
        )
    return jnp.stack(columns, axis=0)


def body(
    inputs,
    seg_starts,
    lengths,
    init_state,
    attn_gain,
    state_gain,
    mlp_gain,
    w_query,
    w_key,
    w_value,
    w_out,
    w_squery,
    w_sout,
    w_up,
    w_down,
    rel_bias,
    gate_bias,
    out_cot,
    state_cot,
):
    seq_count = inputs.shape[0]
    chain_length = lax.axis_size("seq")
    block_index = lax.axis_index("seq")
    is_first = block_index == 0
    width_local = w_query.shape[1]
    head_count = width_local // HEAD_DIM
    gate_value = jax.nn.sigmoid(gate_bias)
    positions = jnp.arange(BLOCK)
    inputs_wide = inputs.astype(jnp.float32)
    tokens_low = gather_rows(to_low(layer_norm(inputs_wide, attn_gain)))
    query_tok = to_low(matmul(tokens_low, w_query))
    key_tok = to_low(matmul(tokens_low, w_key))
    value_tok = to_low(matmul(tokens_low, w_value))
    key_prev, value_prev = passed_along((key_tok, value_tok), "seq", 1)
    valid_keys = (block_index * BLOCK + positions)[None, :] < lengths[:, None]
    batched_attend = jax.vmap(attend_forward, in_axes=(0, 0, 0, None, 0))
    batched_back = jax.vmap(attend_back, in_axes=(0, 0, 0, None, 0, 0, 0))

    def state_forward(state_rows, key_blk, value_blk, valid_blk):
        state_low = lax.all_gather(
            to_low(layer_norm(state_rows, state_gain)), "tensor", axis=1, tiled=True
        )
        query_st = to_low(matmul(state_low, w_squery))
        key_st = to_low(matmul(state_low, w_key))
        value_st = to_low(matmul(state_low, w_value))
        key_all = jnp.concatenate([key_blk, key_st], axis=1)
        value_all = jnp.concatenate([value_blk, value_st], axis=1)
        mixed_st, lse_st = batched_attend(
            query_st, key_all, value_all, 0.0, state_mask_of(valid_blk)
        )
        update = lax.psum_scatter(
            matmul(mixed_st, w_sout).astype(jnp.bfloat16), "tensor", scatter_dimension=1, tiled=True
        ).astype(jnp.float32)
        state_next = gate_value * state_rows + (1.0 - gate_value) * update
        return (state_next, (state_low, query_st, key_st, value_st, mixed_st, lse_st, update))

    def state_backward(
        grad_out, state_rows, kept_one, key_blk, value_blk, valid_blk, extra_key, extra_value
    ):
        state_low, query_st, key_st, value_st, mixed_st, lse_st, update = kept_one
        gate_part = (
            jnp.sum(grad_out * (state_rows - update), axis=(0, 1)) * gate_value * (1.0 - gate_value)
        )
        grad_update = lax.all_gather(
            to_low((1.0 - gate_value) * grad_out), "tensor", axis=1, tiled=True
        )
        grad_mixed_st = to_low(matmul_t(grad_update, w_sout))
        sout_part = outer_sum(mixed_st, grad_update)
        key_all = jnp.concatenate([key_blk, key_st], axis=1)
        value_all = jnp.concatenate([value_blk, value_st], axis=1)
        grad_query_st, grad_keys_st, grad_values_st, _ = batched_back(
            query_st, key_all, value_all, 0.0, state_mask_of(valid_blk), lse_st, grad_mixed_st
        )
        query_low = to_low(grad_query_st)
        key_low = to_low(grad_keys_st[:, BLOCK:] + extra_key)
        value_low = to_low(grad_values_st[:, BLOCK:] + extra_value)
        squery_part = outer_sum(state_low, query_low)
        key_part = outer_sum(state_low, key_low)
        value_part = outer_sum(state_low, value_low)
        terms = (
            matmul_t(query_low, w_squery) + matmul_t(key_low, w_key) + matmul_t(value_low, w_value)
        )
        grad_normed = lax.psum_scatter(
            terms.astype(jnp.bfloat16), "tensor", scatter_dimension=1, tiled=True
        ).astype(jnp.float32)
        grad_rows_norm, gain_part = norm_back(state_rows, state_gain, grad_normed)
        grad_in = gate_value * grad_out + grad_rows_norm
        block_grads = (grad_keys_st[:, :BLOCK], grad_values_st[:, :BLOCK])
        return (
            grad_in,
            block_grads,
            (squery_part, key_part, value_part, sout_part, gain_part, gate_part),
        )

    zeros_rows = jnp.zeros((seq_count,) + init_state.shape, jnp.float32)
    narrow_zero = jnp.zeros((seq_count, STATES, width_local), jnp.bfloat16)
    stored_start = (
        zeros_rows,
        zeros_rows,
        jnp.zeros((seq_count, STATES, D), jnp.bfloat16),
        narrow_zero,
        narrow_zero,
        narrow_zero,
        narrow_zero,
        jnp.zeros((seq_count, head_count, STATES), jnp.float32),
        zeros_rows,
    )

    def forward_turn(turn_index, carry):
        incoming, stored_now = carry
        order_index = turn_index - block_index
        is_live = (order_index >= 0) & (order_index < seq_count)
        picked = jnp.clip(order_index, 0, seq_count - 1)
        rows_now = jnp.where(is_first, init_state[None], incoming)
        key_one = lax.dynamic_slice_in_dim(key_tok, picked, 1, 0)
        value_one = lax.dynamic_slice_in_dim(value_tok, picked, 1, 0)
        valid_one = lax.dynamic_slice_in_dim(valid_keys, picked, 1, 0)
        rows_next, kept_one = state_forward(rows_now, key_one, value_one, valid_one)
        fresh = (rows_now, rows_next) + kept_one
        stored_now = tuple(
            (
                jnp.where(
                    is_live,
                    lax.dynamic_update_slice_in_dim(whole_array, fresh_part, picked, 0),
                    whole_array,
                )
                for whole_array, fresh_part in zip(stored_now, fresh)
            )
        )
        return (pass_state(rows_next), stored_now)

    incoming_start = jnp.zeros((1,) + init_state.shape, jnp.float32)
    _, stored_all = lax.fori_loop(
        0, chain_length + seq_count - 1, forward_turn, (incoming_start, stored_start)
    )
    state_in = stored_all[0]
    state_out = stored_all[1]
    kept = stored_all[2:]
    key_all_tok = jnp.concatenate([key_prev, key_tok, kept[2]], axis=1)
    value_all_tok = jnp.concatenate([value_prev, value_tok, kept[3]], axis=1)
    allowed_tok = jax.vmap(token_mask, in_axes=(0, 0, None))(seg_starts[:, 0], lengths, block_index)
    rel_table = bucket_of((jnp.arange(2 * BLOCK) - BLOCK)[None, :] - positions[:, None])
    full_bias = jnp.concatenate(
        [bias_lookup(rel_bias, rel_table), jnp.zeros((head_count, BLOCK, STATES), jnp.float32)],
        axis=2,
    )
    mixed_tok, lse_tok = batched_attend(
        query_tok, key_all_tok, value_all_tok, full_bias, allowed_tok
    )
    hidden_in = inputs_wide + sum_rows(matmul(mixed_tok, w_out))
    mid_low = gather_rows(to_low(layer_norm(hidden_in, mlp_gain)))
    pre_act = matmul(mid_low, w_up)
    hidden_low = to_low(jax.nn.gelu(pre_act))
    mlp_rows = sum_rows(matmul(hidden_low, w_down))
    tokens_out = (hidden_in + mlp_rows).astype(jnp.bfloat16)
    cot_wide = out_cot.astype(jnp.float32)
    cot_used = gather_rows(out_cot)
    grad_hidden_act = matmul_t(cot_used, w_down)
    down_grad = outer_sum(hidden_low, cot_used)
    grad_pre = to_low(gelu_back(pre_act, grad_hidden_act))
    up_grad = outer_sum(mid_low, grad_pre)
    grad_normed_mid = sum_rows(matmul_t(grad_pre, w_up))
    grad_mid_in, mlp_gain_grad = norm_back(hidden_in, mlp_gain, grad_normed_mid)
    grad_hidden = cot_wide + grad_mid_in
    grad_attn_low = gather_rows(to_low(grad_hidden))
    grad_mixed = to_low(matmul_t(grad_attn_low, w_out))
    out_grad = outer_sum(mixed_tok, grad_attn_low)
    grad_query_tok, grad_keys_tok, grad_values_tok, grad_scores = batched_back(
        query_tok, key_all_tok, value_all_tok, full_bias, allowed_tok, lse_tok, grad_mixed
    )
    bias_grad = bias_sums(grad_scores[..., : 2 * BLOCK], rel_table)
    grad_key_next, grad_value_next = (
        passed_along(grad_keys_tok[:, :BLOCK].astype(jnp.bfloat16), "seq", -1).astype(jnp.float32),
        passed_along(grad_values_tok[:, :BLOCK].astype(jnp.bfloat16), "seq", -1).astype(
            jnp.float32
        ),
    )
    grad_key_own = grad_keys_tok[:, BLOCK : 2 * BLOCK] + grad_key_next
    grad_value_own = grad_values_tok[:, BLOCK : 2 * BLOCK] + grad_value_next
    grad_key_st_tok = grad_keys_tok[:, 2 * BLOCK :]
    grad_value_st_tok = grad_values_tok[:, 2 * BLOCK :]
    cot_rows = state_cot[:, 0].astype(jnp.float32)
    wide_zero = jnp.zeros((seq_count, BLOCK, width_local), jnp.float32)
    stored_back = (zeros_rows, wide_zero, wide_zero)
    totals_start = (
        jnp.zeros((D, width_local), jnp.float32),
        jnp.zeros((D, width_local), jnp.float32),
        jnp.zeros((D, width_local), jnp.float32),
        jnp.zeros((width_local, D), jnp.float32),
        jnp.zeros((D,), jnp.float32),
        jnp.zeros((D,), jnp.float32),
    )

    def backward_turn(turn_index, carry):
        incoming, stored_now, totals_now = carry
        order_index = turn_index - (chain_length - 1 - block_index)
        is_live = (order_index >= 0) & (order_index < seq_count)
        picked = jnp.clip(order_index, 0, seq_count - 1)

        def slice_one(whole_array):
            return lax.dynamic_slice_in_dim(whole_array, picked, 1, 0)

        grad_out = slice_one(cot_rows) + incoming
        kept_one = tuple((slice_one(kept_array) for kept_array in kept))
        grad_in, block_one, parts_one = state_backward(
            grad_out,
            slice_one(state_in),
            kept_one,
            slice_one(key_tok),
            slice_one(value_tok),
            slice_one(valid_keys),
            slice_one(grad_key_st_tok),
            slice_one(grad_value_st_tok),
        )
        fresh = (grad_in,) + block_one
        stored_now = tuple(
            (
                jnp.where(
                    is_live,
                    lax.dynamic_update_slice_in_dim(whole_array, fresh_part, picked, 0),
                    whole_array,
                )
                for whole_array, fresh_part in zip(stored_now, fresh)
            )
        )
        totals_now = tuple(
            (
                total_now + jnp.where(is_live, part_now, 0.0)
                for total_now, part_now in zip(totals_now, parts_one)
            )
        )
        return (pass_back(grad_in), stored_now, totals_now)

    incoming_start = jnp.zeros((1,) + init_state.shape, jnp.float32)
    _, stored_done, weight_parts = lax.fori_loop(
        0, chain_length + seq_count - 1, backward_turn, (incoming_start, stored_back, totals_start)
    )
    grad_in_all, grad_key_blk, grad_value_blk = stored_done
    query_low = to_low(grad_query_tok)
    key_low = to_low(grad_key_own + grad_key_blk)
    value_low = to_low(grad_value_own + grad_value_blk)
    query_grad = outer_sum(tokens_low, query_low)
    key_grad = outer_sum(tokens_low, key_low) + weight_parts[1]
    value_grad = outer_sum(tokens_low, value_low) + weight_parts[2]
    grad_tokens = sum_rows(
        matmul_t(query_low, w_query) + matmul_t(key_low, w_key) + matmul_t(value_low, w_value)
    )
    grad_in_norm, attn_gain_grad = norm_back(inputs_wide, attn_gain, grad_tokens)
    inputs_grad = grad_hidden + grad_in_norm
    state_part = jnp.where(is_first, jnp.sum(grad_in_all, axis=0), 0.0)
    gains = lax.psum(
        jnp.stack([attn_gain_grad, weight_parts[4], mlp_gain_grad, weight_parts[5]]), "tensor"
    )
    totals = (
        lax.psum(query_grad.astype(jnp.bfloat16), ("dp", "seq")).astype(jnp.float32),
        lax.psum(key_grad.astype(jnp.bfloat16), ("dp", "seq")).astype(jnp.float32),
        lax.psum(value_grad.astype(jnp.bfloat16), ("dp", "seq")).astype(jnp.float32),
        lax.psum(out_grad.astype(jnp.bfloat16), ("dp", "seq")).astype(jnp.float32),
        lax.psum(weight_parts[0].astype(jnp.bfloat16), ("dp", "seq")).astype(jnp.float32),
        lax.psum(weight_parts[3].astype(jnp.bfloat16), ("dp", "seq")).astype(jnp.float32),
        lax.psum(up_grad.astype(jnp.bfloat16), ("dp", "seq")).astype(jnp.float32),
        lax.psum(down_grad.astype(jnp.bfloat16), ("dp", "seq")).astype(jnp.float32),
        lax.psum(bias_grad.astype(jnp.bfloat16), ("dp", "seq")).astype(jnp.float32),
        lax.psum(state_part.astype(jnp.bfloat16), ("dp", "seq")).astype(jnp.float32),
        lax.psum(gains.astype(jnp.bfloat16), ("dp", "seq")).astype(jnp.float32),
    )
    gain_total = totals[10]
    return (
        tokens_out,
        state_out[:, None],
        inputs_grad,
        totals[9],
        gain_total[0],
        gain_total[1],
        gain_total[2],
        totals[0],
        totals[1],
        totals[2],
        totals[3],
        totals[4],
        totals[5],
        totals[6],
        totals[7],
        totals[8],
        gain_total[3],
    )


def chosen_body(mesh):
    if mesh.shape["seq"] == 4 and mesh.shape["tensor"] == 4:
        return line_body
    return body


MESH_ID = pl.DeviceIdType.MESH
ROWS = 128
CHUNKS = BLOCK // ROWS
LINE = 8
SCALE = HEAD_DIM ** (-0.5)
VMEM_LIMIT = 60 * 1024 * 1024


def dot_nn(left, right):
    return lax.dot_general(left, right, (((1,), (0,)), ((), ())), preferred_element_type=jnp.float32)


def dot_nt(left, right):
    return lax.dot_general(left, right, (((1,), (1,)), ((), ())), preferred_element_type=jnp.float32)


def dot_tn(left, right):
    return lax.dot_general(left, right, (((0,), (0,)), ((), ())), preferred_element_type=jnp.float32)


def line_place():
    place = lax.axis_index("seq")
    half = lax.rem(place, 2)
    rank = lax.axis_index("tensor")
    return place, half, rank


def span(index, size):
    return pl.ds(pl.multiple_of(index * size, size), size)


def fetch_pieces(kept, first, rows, target, sem):
    for owner in range(8):
        pltpu.make_async_copy(
            kept.at[owner, :, pl.ds(first, rows), :], target.at[:, owner], sem
        ).start()


def fetch_columns(weights, target, sem):
    half = lax.rem(lax.axis_index("seq"), 2)
    for index, weight in enumerate(weights):
        pltpu.make_async_copy(
            weight.at[:, span(half, 128)], target.at[:, pl.ds(128 * index, 128)], sem
        ).start()


def fetched(target, sem):
    pltpu.make_async_copy(target, target, sem).wait()


def norm_parts(rows):
    centered = rows - jnp.mean(rows, axis=-1, keepdims=True)
    spread = jnp.mean(centered * centered, axis=-1, keepdims=True)
    return centered, lax.rsqrt(spread + norm_eps)


def mark(marks, block_id, row):
    return marks[block_id, pl.ds(row, 1), 0:1]


def sequence_marks(marks, block_id):
    mine = lax.axis_index("seq") // 2
    return mark(marks, block_id, mine), mark(marks, 0, 2 + mine)


def token_masks(marks, block_id, first_row):
    start, length = sequence_marks(marks, block_id)
    row = lax.broadcasted_iota(jnp.int32, (ROWS, BLOCK), 0) + first_row
    col = lax.broadcasted_iota(jnp.int32, (ROWS, BLOCK), 1)
    prev_limit = jnp.where(block_id > 0, length - (block_id - 1) * BLOCK, 0)
    prev_ok = (col > row) & (col < prev_limit)
    row_in = (row >= start) & (row < start + SEG)
    col_in = (col >= start) & (col < start + SEG)
    cur_ok = ((col <= row) | (row_in & col_in)) & (col < length - block_id * BLOCK)
    return prev_ok, cur_ok


def state_block_mask(marks, block_id):
    _, length = sequence_marks(marks, block_id)
    col = lax.broadcasted_iota(jnp.int32, (ROWS, BLOCK), 1)
    return col < length - block_id * BLOCK


def softmax_of(score_parts):
    top = jnp.max(score_parts[0], axis=-1, keepdims=True)
    for part in score_parts[1:]:
        top = jnp.maximum(top, jnp.max(part, axis=-1, keepdims=True))
    raised = [jnp.exp(part - top) for part in score_parts]
    total = jnp.sum(raised[0], axis=-1, keepdims=True)
    for part in raised[1:]:
        total = total + jnp.sum(part, axis=-1, keepdims=True)
    inverse = 1.0 / total
    return [to_low(part * inverse) for part in raised], top + jnp.log(total)


def token_scores(scal, qkv, qkvst, bias, block_id, chunk):
    rows = span(chunk, ROWS)
    prev_id = jnp.maximum(block_id - 1, 0)
    query = qkv[block_id, rows, 0:128]
    prev_ok, cur_ok = token_masks(scal, block_id, chunk * ROWS)
    prev = dot_nt(query, qkv[prev_id, :, 128:256]) * SCALE + bias[rows, 0:BLOCK]
    cur = dot_nt(query, qkv[block_id, :, 128:256]) * SCALE + bias[rows, BLOCK : 2 * BLOCK]
    stt = dot_nt(query, qkvst[block_id, :, 128:256]) * SCALE
    prev = jnp.where(prev_ok, prev, masked_score)
    cur = jnp.where(cur_ok, cur, masked_score)
    return query, (prev, cur, stt)


def state_scores(scal, qkv, qkvst, block_id, chunk):
    query = qkvst[block_id, span(chunk, ROWS), 0:128]
    tok = dot_nt(query, qkv[block_id, :, 128:256]) * SCALE
    tok = jnp.where(state_block_mask(scal, block_id), tok, masked_score)
    stt = dot_nt(query, qkvst[block_id, :, 128:256]) * SCALE
    return query, (tok, stt)


HALVES = 2
HALF_ROWS = STATES // HALVES
HALF_CHUNKS = HALF_ROWS // ROWS


def forward_kernel(
    marks, qkv, kept, w_squery, w_qkv, vecs, bias, state_cot, back_own,
    o_out, lse_out, state_rows, low_out, qkvst, lse_st, os_rows, cots, back,
    held, os_all, state_low, w_sout, start, w_state,
    way_send, core_send, recv_sem, local_sem, low_sem, cot_send, cot_recv,
    piece_send, piece_recv, ring_send, ring_recv,
):
    side, place, half, rank = plane_place()
    me = plane_index(side, place)
    partner = place + 1 - 2 * half
    head = 2 * rank + half
    fetch_pieces(kept, 32, 16, start, local_sem.at[0])
    fetch_columns((w_squery,), w_state, local_sem.at[2])
    fetch_pieces(kept, 0, 32, w_sout, local_sem.at[1])
    own_cot = pltpu.make_async_copy(state_cot.at[place], cots.at[place], local_sem.at[4])
    own_cot.start()
    own_piece = pltpu.make_async_copy(back_own, back.at[me, rank], local_sem.at[3])
    own_piece.start()
    ranks = [lax.rem(rank + step, 4) for step in (1, 2, 3)]
    seats = [lax.rem(place + step, 4) for step in (1, 2, 3)]
    barrier = pltpu.get_barrier_semaphore()
    for target in [{"tensor": one} for one in ranks] + [{"seq": one} for one in seats] + [
        {"dp": 1 - side}
    ]:
        pl.semaphore_signal(barrier, inc=1, device_id=target, device_id_type=MESH_ID)
    fetched(start, local_sem.at[0])
    held[...] = start[...].reshape(STATES, D).astype(jnp.float32)
    gain = vecs[0:1, :]
    gate = vecs[1:2, :]
    fetched(w_state, local_sem.at[2])

    def project(block_id, part):
        def one(chunk, _):
            rows = span(chunk, ROWS)
            centered, scale = norm_parts(held[rows, :])
            low = to_low(centered * scale * gain)
            state_low[block_id, rows, :] = low
            qkvst[block_id, rows, 0:128] = to_low(dot_nn(low, w_state[...]))
            qkvst[block_id, rows, 128:384] = to_low(dot_nn(low, w_qkv[:, 128:384]))
            return 0

        lax.fori_loop(HALF_CHUNKS * part, HALF_CHUNKS * (part + 1), one, 0)

    pl.semaphore_wait(barrier, 7)

    def piece_move(origin, part, slot, target):
        return pltpu.make_async_remote_copy(
            src_ref=back_own.at[part],
            dst_ref=back.at[me, origin, part],
            send_sem=piece_send.at[part, slot],
            recv_sem=piece_recv.at[part, origin],
            device_id={"tensor": target},
            device_id_type=MESH_ID,
        )

    def send_piece(part):
        for slot, target in enumerate(ranks):
            piece_move(rank, part, slot, target).start()

    gather = plane_gather(
        lambda owner, part: back.at[owner, pl.ds(2 * part, 2)], ring_send, ring_recv
    )
    next(gather)
    send_piece(0)
    for part in range(HALVES):
        project(0, part)
    right, left = {"tensor": lax.rem(rank + 1, 4)}, {"tensor": lax.rem(rank + 3, 4)}

    def moved(block_id, part, which, sem, target):
        view = os_all.at[block_id, pl.ds(HALF_ROWS * part, HALF_ROWS), span(which, 128)]
        return pltpu.make_async_remote_copy(
            src_ref=view,
            dst_ref=view,
            send_sem=sem,
            recv_sem=recv_sem.at[block_id, part, which],
            device_id=target,
            device_id_type=MESH_ID,
        )

    def cot_move(index, origin, slot, target):
        return pltpu.make_async_remote_copy(
            src_ref=state_cot.at[index],
            dst_ref=cots.at[origin],
            send_sem=cot_send.at[slot],
            recv_sem=cot_recv.at[origin],
            device_id={"seq": target},
            device_id_type=MESH_ID,
        )

    for slot, target in enumerate(seats):
        cot_move(target, place, slot, target).start()
    fetched(w_sout, local_sem.at[1])

    def origin_of(way, distance):
        if way == 0:
            return jnp.maximum(rank - distance, 0)
        return jnp.minimum(rank + distance, 3)

    def ways(distance):
        return (
            (0, rank >= distance, (rank >= distance) & (rank < 3), right),
            (1, rank + distance <= 3, (rank + distance <= 3) & (rank > 0), left),
        )

    def relay(block_id, part, distance, waiting):
        for way, comes, goes, target in ways(distance):
            which = 2 * origin_of(way, distance) + half
            sem = way_send.at[block_id, part, min(distance, 2), way]
            core_sem = core_send.at[block_id, part, which // 2]
            if distance > 0:

                @pl.when(comes)
                def _():
                    to_core = moved(block_id, part, which, core_sem, {"seq": partner})
                    if waiting:
                        moved(block_id, part, which, sem, target).wait_recv()
                        to_core.start()
                    else:
                        to_core.wait_send()

            if distance < 3:

                @pl.when(goes)
                def _():
                    one = moved(block_id, part, which, sem, target)
                    if waiting:
                        one.start()
                    else:
                        one.wait_send()

        if distance == 0:
            mine = moved(
                block_id, part, head, core_send.at[block_id, part, rank], {"seq": partner}
            )
            if waiting:
                mine.start()
            else:
                mine.wait_send()

    def one_block(block_id, _):
        def attend_state(chunk, _):
            rows = span(chunk, ROWS)
            _, parts = state_scores(marks, qkv, qkvst, block_id, chunk)
            (w_tok, w_stt), total = softmax_of(parts)
            mixed = dot_nn(w_tok, qkv[block_id, :, 256:384]) + dot_nn(
                w_stt, qkvst[block_id, :, 256:384]
            )
            os_all[block_id, rows, span(head, 128)] = to_low(mixed)
            lse_st[block_id, rows, :] = total
            return 0

        def attend_token(chunk, _):
            rows = span(chunk, ROWS)
            _, parts = token_scores(marks, qkv, qkvst, bias, block_id, chunk)
            weights, total = softmax_of(parts)
            prev_id = jnp.maximum(block_id - 1, 0)
            mixed = (
                dot_nn(weights[0], qkv[prev_id, :, 256:384])
                + dot_nn(weights[1], qkv[block_id, :, 256:384])
                + dot_nn(weights[2], qkvst[block_id, :, 256:384])
            )
            o_out[block_id, rows, :] = to_low(mixed)
            lse_out[block_id, rows, :] = total
            return 0

        def attend_both(part, _):
            lax.fori_loop(HALF_CHUNKS * part, HALF_CHUNKS * (part + 1), attend_state, 0)
            for value in range(HALVES):

                @pl.when(part == value)
                def _():
                    relay(block_id, value, 0, True)

            return 0

        lax.fori_loop(0, HALVES, attend_both, 0)
        pltpu.make_async_copy(
            state_low.at[block_id], low_out.at[block_id], low_sem.at[block_id]
        ).start()

        @pl.when(block_id == 2)
        def _():
            own_piece.wait()
            for part in range(3):
                for slot, target in enumerate(ranks):
                    piece_move(target, part, slot, target).wait_recv()
            next(gather)

        @pl.when(block_id == 3)
        def _():
            next(gather)
            next(gather)

        def between(step, _):
            for value, (distance, part) in enumerate(((1, 0), (1, 1), (2, 0), (2, 1))):

                @pl.when(step == value)
                def _():
                    relay(block_id, part, distance, True)

            return attend_token(step, 0)

        lax.fori_loop(0, 4, between, 0)

        def settle(part, _):
            for value in range(HALVES):

                @pl.when(part == value)
                def _():
                    relay(block_id, value, 3, True)
                    for origin in range(4):
                        moved(
                            block_id, value, 2 * origin + 1 - half,
                            core_send.at[block_id, value, origin], {"seq": partner},
                        ).wait_recv()

                    if value == HALVES - 1:
                        for turn in (0, 1):

                            @pl.when(block_id == turn)
                            def _():
                                send_piece(turn + 1)

            def update(chunk, _):
                rows = span(chunk, ROWS)
                change = dot_nn(os_all[block_id, rows, :], w_sout[...].reshape(D, D))
                held[rows, :] = gate * held[rows, :] + (1.0 - gate) * change
                return 0

            lax.fori_loop(HALF_CHUNKS * part, HALF_CHUNKS * (part + 1), update, 0)

            @pl.when(block_id < 3)
            def _():
                project(block_id + 1, part)

            return 0

        lax.fori_loop(0, HALVES, settle, 0)
        state_rows[block_id] = held[span(rank, 128), :]
        os_rows[block_id] = os_all[block_id, span(head, 64), :]
        return 0

    lax.fori_loop(0, 4, one_block, 0)

    def drain(block_id, _):
        for part in range(HALVES):
            for distance in range(4):
                relay(block_id, part, distance, False)
        pltpu.make_async_copy(
            state_low.at[block_id], low_out.at[block_id], low_sem.at[block_id]
        ).wait()
        return 0

    lax.fori_loop(0, 4, drain, 0)
    own_cot.wait()
    for part in range(3):
        for slot, target in enumerate(ranks):
            piece_move(rank, part, slot, target).wait_send()
    for _ in gather:
        pass
    for slot, target in enumerate(seats):
        cot_move(target, place, slot, target).wait_send()
        cot_move(place, target, slot, target).wait_recv()


def any_specs(count):
    return [pl.BlockSpec(memory_space=pl.ANY)] * count


def vmem_specs(count):
    return [pl.BlockSpec(memory_space=pltpu.VMEM)] * count


def forward_chain(
    marks, qkv, kept, w_squery, w_qkv, vecs, bias, state_cot, back_own
):
    low, wide = jnp.bfloat16, jnp.float32
    shapes = (
        ((4, BLOCK, 128), low),
        ((4, BLOCK, 1), wide),
        ((4, 128, D), wide),
        ((4, STATES, D), low),
        ((4, STATES, 384), low),
        ((4, STATES, 1), wide),
        ((4, 64, D), low),
        ((4, 64, D), low),
        ((8, 4, 3, 32, D), low),
    )
    dma = pltpu.SemaphoreType.DMA
    return pl.pallas_call(
        forward_kernel,
        out_shape=[jax.ShapeDtypeStruct(*one) for one in shapes],
        in_specs=vmem_specs(2) + any_specs(2) + vmem_specs(3) + any_specs(2),
        out_specs=vmem_specs(3) + any_specs(1) + vmem_specs(3) + any_specs(2),
        scratch_shapes=[
            pltpu.VMEM((STATES, D), wide),
            pltpu.VMEM((4, STATES, D), low),
            pltpu.VMEM((4, STATES, D), low),
            pltpu.VMEM((4, 8, 32, D), low),
            pltpu.VMEM((4, 8, 16, D), low),
            pltpu.VMEM((D, 128), low),
            dma((4, HALVES, 3, 2)),
            dma((4, HALVES, 4)),
            dma((4, HALVES, 8)),
            dma((5,)),
            dma((4,)),
            dma((3,)),
            dma((4,)),
            dma((3, 3)),
            dma((3, 4)),
            dma((14,)),
            dma((8, 2)),
        ],
        compiler_params=pltpu.CompilerParams(
            collective_id=1, has_side_effects=True, vmem_limit_bytes=VMEM_LIMIT
        ),
        cost_estimate=pl.CostEstimate(
            flops=60000000000, bytes_accessed=60000000, transcendentals=0
        ),
        name="forward_chain",
    )(marks, qkv, kept, w_squery, w_qkv, vecs, bias, state_cot, back_own)


def backward_kernel(
    scal, qkv, d_o, lse_tok, qkvst, lse_st, state_rows, begin, cots, back, kept, vecs, bias,
    extra, hidden,
    d_qkv, d_qkvst, du_rows, d_start, sums, dz_sum, state_out, tokens_out, out_part,
    key_acc, value_acc, st_key, st_value, dos_rows, dos_got, d_got, grad_in,
    states, w_back, w_sout, work, core_got, near_got, far_got, total,
    send_sem, recv_sem, local_sem, side_sem, ring_send, ring_recv,
):
    place, half, rank = line_place()
    own_rows = pl.ds(pl.multiple_of(half * 64, 64), 64)
    loads = [
        pltpu.make_async_copy(
            state_rows.at[:, own_rows, :], states.at[pl.ds(1, 4)], local_sem.at[0]
        ),
        pltpu.make_async_copy(
            state_rows.at[place], state_out.at[place // 2], local_sem.at[3]
        ),
        pltpu.make_async_copy(extra, work, local_sem.at[4]),
    ]
    for one in loads:
        one.start()
    fetch_pieces(kept, 0, 32, w_sout, local_sem.at[1])
    for owner in range(8):
        pltpu.make_async_copy(
            back.at[owner], w_back.at[:, owner // 4, :, owner % 4], local_sem.at[2]
        ).start()
    states[0] = to_low(begin[own_rows, :]).astype(jnp.float32)
    head = 2 * rank + half
    peers = []
    for step in range(1, LINE):
        other = lax.rem(head + step, LINE)
        peers.append((other, place - half + lax.rem(other, 2), other // 2))
    barrier = pltpu.get_barrier_semaphore()
    for _, seq_to, rank_to in peers:
        pl.semaphore_signal(
            barrier, inc=1, device_id={"seq": seq_to, "tensor": rank_to}, device_id_type=MESH_ID
        )
    beside = lax.rem(place + 2, 4)
    pl.semaphore_signal(barrier, inc=1, device_id={"seq": beside}, device_id_type=MESH_ID)
    pl.semaphore_signal(
        barrier, inc=1, device_id={"dp": 1 - lax.axis_index("dp")}, device_id_type=MESH_ID
    )
    plane_steps = plane_scatter(
        work, core_got, near_got, far_got, total, 384, ring_send, ring_recv
    )
    next(plane_steps)

    def aside(block_id, row_set):
        return pltpu.make_async_remote_copy(
            src_ref=state_rows.at[block_id],
            dst_ref=state_out.at[row_set],
            send_sem=side_sem.at[0],
            recv_sem=side_sem.at[1],
            device_id={"seq": beside},
            device_id_type=MESH_ID,
        )

    gain = vecs[0:1, :]
    gate = vecs[1:2, :]
    key_acc[...] = jnp.zeros_like(key_acc)
    value_acc[...] = jnp.zeros_like(value_acc)
    dz_sum[...] = jnp.zeros_like(dz_sum)
    sums[...] = jnp.zeros_like(sums)
    grad_in[...] = jnp.zeros_like(grad_in)

    def back_parts(parts, total, grad, values):
        weights = [jnp.exp(part - total) for part in parts]
        d_weights = [dot_nt(grad, value) for value in values]
        inner = jnp.sum(weights[0] * d_weights[0], axis=-1, keepdims=True)
        for one, other in zip(weights[1:], d_weights[1:]):
            inner = inner + jnp.sum(one * other, axis=-1, keepdims=True)
        d_scores = [to_low(one * (other - inner)) for one, other in zip(weights, d_weights)]
        return [to_low(one) for one in weights], d_scores

    def token_back(block_id):
        prev_id = jnp.maximum(block_id - 1, 0)
        st_key[...] = jnp.zeros_like(st_key)
        st_value[...] = jnp.zeros_like(st_value)

        def one_chunk(chunk, _):
            rows = span(chunk, ROWS)
            query, parts = token_scores(scal, qkv, qkvst, bias, block_id, chunk)
            grad = d_o[block_id, rows, :]
            keys = (qkv[prev_id, :, 128:256], qkv[block_id, :, 128:256], qkvst[block_id, :, 128:256])
            values = (
                qkv[prev_id, :, 256:384], qkv[block_id, :, 256:384], qkvst[block_id, :, 256:384]
            )
            weights, d_scores = back_parts(parts, lse_tok[block_id, rows, :], grad, values)
            d_query = dot_nn(d_scores[0], keys[0])
            d_query = d_query + dot_nn(d_scores[1], keys[1]) + dot_nn(d_scores[2], keys[2])
            d_qkv[block_id, rows, 0:128] = to_low(d_query * SCALE)
            key_acc[prev_id] += dot_tn(d_scores[0], query) * SCALE
            value_acc[prev_id] += dot_tn(weights[0], grad)
            key_acc[block_id] += dot_tn(d_scores[1], query) * SCALE
            value_acc[block_id] += dot_tn(weights[1], grad)
            st_key[...] += dot_tn(d_scores[2], query) * SCALE
            st_value[...] += dot_tn(weights[2], grad)
            dz_sum[rows, 0:BLOCK] += d_scores[0].astype(jnp.float32)
            dz_sum[rows, BLOCK : 2 * BLOCK] += d_scores[1].astype(jnp.float32)
            return 0

        lax.fori_loop(0, CHUNKS, one_chunk, 0)

    token_back(3)
    pl.semaphore_wait(barrier, LINE + 1)
    aside(beside, place // 2).start()
    loads[2].wait()
    loads[0].wait()
    fetched(w_sout, local_sem.at[1])
    fetched(w_back, local_sem.at[2])

    def mixed_copy(block_id, slot, sender, other, seq_to, rank_to):
        return pltpu.make_async_remote_copy(
            src_ref=dos_rows.at[block_id, :, span(other, 128)],
            dst_ref=dos_got.at[block_id, span(sender, 64), :],
            send_sem=send_sem.at[0, block_id, slot],
            recv_sem=recv_sem.at[0, block_id, sender],
            device_id={"seq": seq_to, "tensor": rank_to},
            device_id_type=MESH_ID,
        )

    def grads_copy(block_id, slot, sender, other, seq_to, rank_to):
        return pltpu.make_async_remote_copy(
            src_ref=d_qkvst.at[block_id, span(other, 64), :],
            dst_ref=d_got.at[block_id, sender],
            send_sem=send_sem.at[1, block_id, slot],
            recv_sem=recv_sem.at[1, block_id, sender],
            device_id={"seq": seq_to, "tensor": rank_to},
            device_id_type=MESH_ID,
        )

    def one_block(turn, _):
        block_id = 3 - turn
        grad_out = grad_in[...] + cots[block_id].astype(jnp.float32)
        sums[0:1, :] += jnp.sum(
            grad_out * (states[block_id] - states[block_id + 1]), axis=0, keepdims=True
        ) * gate
        change = to_low((1.0 - gate) * grad_out)
        du_rows[block_id] = change
        dos_rows[block_id] = to_low(dot_nt(change, w_sout[...].reshape(D, D)))
        for slot, (other, seq_to, rank_to) in enumerate(peers):
            mixed_copy(block_id, slot, head, other, seq_to, rank_to).start()
        dos_got[block_id, span(head, 64), :] = dos_rows[block_id, :, span(head, 128)]
        for slot, (other, seq_to, rank_to) in enumerate(peers):
            mixed_copy(block_id, slot, other, other, seq_to, rank_to).wait_recv()

        def one_chunk(chunk, _):
            rows = span(chunk, ROWS)
            query, parts = state_scores(scal, qkv, qkvst, block_id, chunk)
            grad = dos_got[block_id, rows, :]
            keys = (qkv[block_id, :, 128:256], qkvst[block_id, :, 128:256])
            values = (qkv[block_id, :, 256:384], qkvst[block_id, :, 256:384])
            weights, d_scores = back_parts(parts, lse_st[block_id, rows, :], grad, values)
            d_query = dot_nn(d_scores[0], keys[0]) + dot_nn(d_scores[1], keys[1])
            d_qkvst[block_id, rows, 0:128] = to_low(d_query * SCALE)
            key_acc[block_id] += dot_tn(d_scores[0], query) * SCALE
            value_acc[block_id] += dot_tn(weights[0], grad)
            st_key[...] += dot_tn(d_scores[1], query) * SCALE
            st_value[...] += dot_tn(weights[1], grad)
            return 0

        lax.fori_loop(0, CHUNKS, one_chunk, 0)
        d_qkvst[block_id, :, 128:256] = to_low(st_key[...])
        d_qkvst[block_id, :, 256:384] = to_low(st_value[...])
        for slot, (other, seq_to, rank_to) in enumerate(peers):
            grads_copy(block_id, slot, head, other, seq_to, rank_to).start()
        d_got[block_id, head] = d_qkvst[block_id, span(head, 64), :]

        for step in range(4):

            @pl.when(turn == step)
            def _():
                next(plane_steps, None)

        @pl.when(turn < 3)
        def _():
            token_back(block_id - 1)

        d_qkv[block_id, :, 128:256] = to_low(key_acc[block_id])
        d_qkv[block_id, :, 256:384] = to_low(value_acc[block_id])
        for slot, (other, seq_to, rank_to) in enumerate(peers):
            grads_copy(block_id, slot, other, other, seq_to, rank_to).wait_recv()
        d_low = dot_nn(d_got[block_id, 0], w_back[0, 0].reshape(384, D))
        for other in range(1, LINE):
            d_low = d_low + dot_nn(
                d_got[block_id, other], w_back[other // 2, other % 2].reshape(384, D)
            )
        centered, scale = norm_parts(states[block_id])
        normed = centered * scale
        sums[1:2, :] += jnp.sum(d_low * normed, axis=0, keepdims=True)
        lifted = d_low * gain
        grad_in[...] = gate * grad_out + scale * (
            lifted
            - jnp.mean(lifted, axis=-1, keepdims=True)
            - normed * jnp.mean(lifted * normed, axis=-1, keepdims=True)
        )
        return 0

    lax.fori_loop(0, 4, one_block, 0)
    d_start[...] = grad_in[...]

    def drain(block_id, _):
        for slot, (other, seq_to, rank_to) in enumerate(peers):
            mixed_copy(block_id, slot, head, other, seq_to, rank_to).wait_send()
            grads_copy(block_id, slot, head, other, seq_to, rank_to).wait_send()
        return 0

    lax.fori_loop(0, 4, drain, 0)
    for _ in plane_steps:
        pass
    for which in range(2):
        rows = pl.ds(128 * which, 128)
        tokens_out[which] = to_low(hidden[which] + total[rows, :])
    out_part[...] = to_low(total[256:384, :])
    loads[1].wait()
    aside(beside, place // 2).wait_send()
    aside(place, 1 - place // 2).wait_recv()


def backward_chain(
    scal, qkv, d_o, lse_tok, qkvst, lse_st, state_rows, begin, cots, back, kept, vecs, bias,
    extra, hidden,
):
    low, wide = jnp.bfloat16, jnp.float32
    shapes = (
        ((4, BLOCK, 384), low),
        ((4, STATES, 384), low),
        ((4, 64, D), low),
        ((64, D), wide),
        ((8, D), wide),
        ((BLOCK, 2 * BLOCK), wide),
        ((2, 128, D), wide),
        ((2, 128, D), low),
        ((128, D), low),
    )
    return pl.pallas_call(
        backward_kernel,
        out_shape=[jax.ShapeDtypeStruct(*one) for one in shapes],
        in_specs=vmem_specs(6)
        + any_specs(1)
        + vmem_specs(2)
        + any_specs(2)
        + vmem_specs(2)
        + any_specs(1)
        + vmem_specs(1),
        out_specs=vmem_specs(6) + any_specs(1) + vmem_specs(2),
        scratch_shapes=[
            pltpu.VMEM((4, BLOCK, 128), wide),
            pltpu.VMEM((4, BLOCK, 128), wide),
            pltpu.VMEM((STATES, 128), wide),
            pltpu.VMEM((STATES, 128), wide),
            pltpu.VMEM((4, 64, D), low),
            pltpu.VMEM((4, STATES, 128), low),
            pltpu.VMEM((4, LINE, 64, 384), low),
            pltpu.VMEM((64, D), wide),
            pltpu.VMEM((5, 64, D), wide),
            pltpu.VMEM((4, 2, 3, 4, 32, D), low),
            pltpu.VMEM((4, 8, 32, D), low),
            pltpu.VMEM((8, 384, D), low),
            pltpu.VMEM((4, 384, D), low),
            pltpu.VMEM((4, 192, D), low),
            pltpu.VMEM((2, 192, D), low),
            pltpu.VMEM((384, D), wide),
            pltpu.SemaphoreType.DMA((2, 4, LINE - 1)),
            pltpu.SemaphoreType.DMA((2, 4, LINE)),
            pltpu.SemaphoreType.DMA((5,)),
            pltpu.SemaphoreType.DMA((2,)),
            pltpu.SemaphoreType.DMA((10,)),
            pltpu.SemaphoreType.DMA((10,)),
        ],
        compiler_params=pltpu.CompilerParams(
            collective_id=2, has_side_effects=True, vmem_limit_bytes=VMEM_LIMIT
        ),
        cost_estimate=pl.CostEstimate(flops=40000000000, bytes_accessed=40000000, transcendentals=0),
        name="backward_chain",
    )(
        scal, qkv, d_o, lse_tok, qkvst, lse_st, state_rows, begin, cots, back, kept, vecs, bias,
        extra, hidden,
    )


def plane_place():
    place, half, rank = line_place()
    side = lax.axis_index("dp")
    return side, place, half, rank


def plane_index(side, place):
    return 4 * side + place


def row_halves(buf, rows):
    size = rows // 2
    return lambda owner, part: buf.at[owner, pl.ds(part * size, size), :]


def plane_gather(view, send_sem, recv_sem):
    side, place, half, rank = plane_place()
    across, beside = 1 - side, lax.rem(place + 2, 4)
    core = place + 1 - 2 * half
    me = plane_index(side, place)
    at_x, at_y = plane_index(across, place), plane_index(side, beside)
    at_d = plane_index(across, beside)
    to_x, to_y, to_c = {"dp": across}, {"seq": beside}, {"seq": core}

    def piece(owner, part, slot, target):
        one = view(owner, part)
        return pltpu.make_async_remote_copy(
            src_ref=one,
            dst_ref=one,
            send_sem=send_sem.at[slot],
            recv_sem=recv_sem.at[owner, part],
            device_id=target,
            device_id_type=MESH_ID,
        )

    own = [
        piece(me, 0, 0, to_x), piece(me, 1, 1, to_y), piece(me, 1, 2, to_x), piece(me, 0, 3, to_y),
        piece(me, 0, 4, to_c), piece(me, 1, 5, to_c),
    ]
    on_x0, on_y1 = piece(at_x, 0, 6, to_y), piece(at_y, 1, 7, to_x)
    came = [
        (piece(owner, part, 0, to_c), piece(owner, part, slot, to_c))
        for owner, part, slot in (
            (at_x, 0, 8), (at_y, 1, 9), (at_x, 1, 10), (at_y, 0, 11), (at_d, 0, 12), (at_d, 1, 13)
        )
    ]
    core_came = [
        piece(owner, part, 0, to_c)
        for owner in (
            plane_index(side, core),
            plane_index(across, core),
            plane_index(side, lax.rem(core + 2, 4)),
            plane_index(across, lax.rem(core + 2, 4)),
        )
        for part in (0, 1)
    ]
    yield
    for one in own:
        one.start()
    yield
    came[0][0].wait_recv()
    on_x0.start()
    came[1][0].wait_recv()
    on_y1.start()
    came[0][1].start()
    came[1][1].start()
    yield
    for index in (2, 3):
        came[index][0].wait_recv()
        came[index][1].start()
    yield
    for index in (4, 5):
        came[index][0].wait_recv()
        came[index][1].start()
    yield
    for one in core_came:
        one.wait_recv()
    for one in own + [on_x0, on_y1] + [two for _, two in came]:
        one.wait_send()


def run_all(*steps):
    waiting = list(steps)
    while waiting:
        for one in list(waiting):
            try:
                next(one)
            except StopIteration:
                waiting.remove(one)


def plane_scatter(part, core_got, near_got, far_got, total, rows, send_sem, recv_sem):
    side, place, half, rank = plane_place()
    across, beside = 1 - side, lax.rem(place + 2, 4)
    core = place + 1 - 2 * half
    me = plane_index(side, place)
    at_x, at_y = plane_index(across, place), plane_index(side, beside)
    at_d = plane_index(across, beside)
    size = rows // 2
    halves = (pl.ds(0, size), pl.ds(size, size))

    def moved(source, target_ref, slot, target):
        return pltpu.make_async_remote_copy(
            src_ref=source,
            dst_ref=target_ref,
            send_sem=send_sem.at[slot],
            recv_sem=recv_sem.at[slot],
            device_id=target,
            device_id_type=MESH_ID,
        )

    order = (at_d, at_x, at_y, me)
    swapped = (
        plane_index(across, lax.rem(core + 2, 4)),
        plane_index(across, core),
        plane_index(side, lax.rem(core + 2, 4)),
        plane_index(side, core),
    )
    def add_into(owner, view, other):
        part[owner, view, :] = to_low(
            part[owner, view, :].astype(jnp.float32) + other.astype(jnp.float32)
        )

    near = [
        moved(part.at[at_d, halves[0], :], near_got.at[0], 4, {"dp": across}),
        moved(part.at[at_d, halves[1], :], near_got.at[1], 5, {"seq": beside}),
        moved(part.at[at_x, halves[0], :], near_got.at[2], 6, {"dp": across}),
        moved(part.at[at_y, halves[1], :], near_got.at[3], 7, {"seq": beside}),
    ]
    first = [
        moved(part.at[owner], core_got.at[slot], slot, {"seq": core})
        for slot, owner in enumerate(swapped)
    ]
    far = [
        moved(part.at[at_y, halves[0], :], far_got.at[0], 8, {"seq": beside}),
        moved(part.at[at_x, halves[1], :], far_got.at[1], 9, {"dp": across}),
    ]
    yield
    for one in first:
        one.start()
    for slot, owner in enumerate(order):
        first[slot].wait_recv()
        for view in halves:
            add_into(owner, view, core_got[slot, view, :])
        if slot == 0:
            near[0].start()
            near[1].start()
        if slot == 1:
            near[2].start()
        if slot == 2:
            near[3].start()
    yield
    near[0].wait_recv()
    add_into(at_y, halves[0], near_got[0])
    far[0].start()
    near[1].wait_recv()
    add_into(at_x, halves[1], near_got[1])
    far[1].start()
    yield
    near[2].wait_recv()
    add_into(me, halves[0], near_got[2])
    near[3].wait_recv()
    add_into(me, halves[1], near_got[3])
    yield
    for slot, view in enumerate(halves):
        far[slot].wait_recv()
        total[view, :] = part[me, view, :].astype(jnp.float32) + far_got[slot].astype(jnp.float32)
    for one in first + near + far:
        one.wait_send()


def group_peers():
    place, half, rank = line_place()
    here = 4 * place + rank
    peers = []
    for step in range(1, 16):
        other = lax.rem(here + step, 16)
        peers.append((other, other // 4, lax.rem(other, 4)))
    return here, peers


def greet(peers):
    side = lax.axis_index("dp")
    barrier = pltpu.get_barrier_semaphore()
    for _, seq_to, rank_to in peers:
        pl.semaphore_signal(
            barrier, inc=1, device_id={"seq": seq_to, "tensor": rank_to}, device_id_type=MESH_ID
        )
    pl.semaphore_signal(barrier, inc=1, device_id={"dp": 1 - side}, device_id_type=MESH_ID)
    pl.semaphore_wait(barrier, len(peers) + 1)


def middle_kernel(
    mixed, tokens, kept, spread, cot_hbm, vecs,
    hidden, d_hidden, d_line, sums, extra, ff_grads,
    mixed_rows, mid_all, gl_all, dpre_all, work, core_got, near_got, far_got, total, d_rows,
    d_low, w_out, up, down, cot_all,
    send_sem, recv_sem, ring_send, ring_recv, sum_send, sum_recv, back_send, back_recv, local_sem,
):
    low, wide = jnp.bfloat16, jnp.float32
    side, place, half, rank = plane_place()
    mine = place // 2
    head = 2 * rank + half
    across, beside = 1 - side, lax.rem(place + 2, 4)
    core = place + 1 - 2 * half
    core_beside = lax.rem(core + 2, 4)
    me = plane_index(side, place)
    at_x, at_y = plane_index(across, place), plane_index(side, beside)
    at_d = plane_index(across, beside)
    me_c, x_c = plane_index(side, core), plane_index(across, core)
    y_c, d_c = plane_index(side, core_beside), plane_index(across, core_beside)
    to_x, to_y, to_c = {"dp": across}, {"seq": beside}, {"seq": core}
    here, peers = group_peers()
    fetch_pieces(kept, 48, 32, w_out, local_sem.at[0])
    ff_own = up.shape[1]
    first = spread.shape[1] - 2 * ff_own
    loads = [
        pltpu.make_async_copy(spread.at[:, pl.ds(first, ff_own), :], up, local_sem.at[1]),
        pltpu.make_async_copy(spread.at[:, pl.ds(first + ff_own, ff_own), :], down, local_sem.at[2]),
        pltpu.make_async_copy(cot_hbm, cot_all, local_sem.at[3]),
    ]
    for one in loads:
        one.start()
    greet(peers)

    def rows_copy(slot, sender, seq_from, rank_from, seq_to, rank_to):
        return pltpu.make_async_remote_copy(
            src_ref=mixed.at[seq_to, span(rank_to, 128), :],
            dst_ref=mixed_rows.at[
                seq_from // 2, :, span(2 * rank_from + lax.rem(seq_from, 2), 128)
            ],
            send_sem=send_sem.at[slot],
            recv_sem=recv_sem.at[sender],
            device_id={"seq": seq_to, "tensor": rank_to},
            device_id_type=MESH_ID,
        )

    for slot, (_, seq_to, rank_to) in enumerate(peers):
        rows_copy(slot, here, place, rank, seq_to, rank_to).start()
    mixed_rows[mine, :, span(head, 128)] = mixed[place, span(rank, 128), :]
    fetched(w_out, local_sem.at[0])
    for slot, (other, seq_to, rank_to) in enumerate(peers):
        rows_copy(slot, other, seq_to, rank_to, seq_to, rank_to).wait_recv()
    gain = vecs[2:3, :]

    def project(which, _):
        added = dot_nn(mixed_rows[which], w_out[...].reshape(D, D)) + tokens[which].astype(wide)
        hidden[which] = added
        centered, scale = norm_parts(added)
        mid_all[me, span(which, 128), :] = to_low(centered * scale * gain)
        return 0

    lax.fori_loop(0, 2, project, 0)

    def piece(owner, part, slot, target):
        view = mid_all.at[owner, pl.ds(part * 128, 128), :]
        return pltpu.make_async_remote_copy(
            src_ref=view,
            dst_ref=view,
            send_sem=ring_send.at[slot],
            recv_sem=ring_recv.at[owner, part],
            device_id=target,
            device_id_type=MESH_ID,
        )

    own = [
        piece(me, 0, 0, to_x), piece(me, 1, 1, to_y), piece(me, 1, 2, to_x), piece(me, 0, 3, to_y),
        piece(me, 0, 4, to_c), piece(me, 1, 5, to_c),
    ]
    on_x0, on_y1 = piece(at_x, 0, 6, to_y), piece(at_y, 1, 7, to_x)
    to_core = [
        piece(at_x, 0, 8, to_c), piece(at_y, 1, 9, to_c), piece(at_x, 1, 10, to_c),
        piece(at_y, 0, 11, to_c), piece(at_d, 0, 12, to_c), piece(at_d, 1, 13, to_c),
    ]
    wait_of = {
        (name, part): piece(owner, part, 0, to_c)
        for name, owner in (
            ("x", at_x), ("y", at_y), ("d", at_d), ("mc", me_c), ("xc", x_c), ("yc", y_c), ("dc", d_c)
        )
        for part in (0, 1)
    }

    def moved(source, target_ref, slot, target):
        return pltpu.make_async_remote_copy(
            src_ref=source,
            dst_ref=target_ref,
            send_sem=sum_send.at[slot],
            recv_sem=sum_recv.at[slot],
            device_id=target,
            device_id_type=MESH_ID,
        )

    views = (pl.ds(0, 128), pl.ds(128, 128))
    swap = [
        moved(work.at[owner], core_got.at[slot], slot, to_c)
        for slot, owner in enumerate((d_c, x_c, y_c, me_c))
    ]
    near = [
        moved(work.at[at_d, views[0], :], near_got.at[0], 4, to_x),
        moved(work.at[at_d, views[1], :], near_got.at[1], 5, to_y),
        moved(work.at[at_x, views[0], :], near_got.at[2], 6, to_x),
        moved(work.at[at_y, views[1], :], near_got.at[3], 7, to_y),
    ]
    far = [
        moved(work.at[at_y, views[0], :], far_got.at[0], 8, to_y),
        moved(work.at[at_x, views[1], :], far_got.at[1], 9, to_x),
    ]

    def add_into(owner, view, other):
        work[owner, view, :] = to_low(work[owner, view, :].astype(wide) + other.astype(wide))

    def add_core(slot, owner):
        swap[slot].wait_recv()
        for view in views:
            add_into(owner, view, core_got[slot, view, :])

    for one in own:
        one.start()
    loads[0].wait()
    loads[1].wait()
    loads[2].wait()
    owners = (me, me_c, at_x, at_y, x_c, y_c, at_d, d_c)

    def one_chunk(turn, _):
        @pl.when(turn == 1)
        def _():
            wait_of["mc", 0].wait_recv()
            wait_of["mc", 1].wait_recv()

        @pl.when(turn == 2)
        def _():
            swap[3].start()
            wait_of["x", 0].wait_recv()
            on_x0.start()
            wait_of["y", 1].wait_recv()
            on_y1.start()
            to_core[0].start()
            to_core[1].start()
            wait_of["x", 1].wait_recv()
            to_core[2].start()
            wait_of["y", 0].wait_recv()
            to_core[3].start()

        @pl.when(turn == 4)
        def _():
            wait_of["xc", 0].wait_recv()
            wait_of["xc", 1].wait_recv()

        @pl.when(turn == 5)
        def _():
            swap[1].start()
            wait_of["yc", 0].wait_recv()
            wait_of["yc", 1].wait_recv()

        @pl.when(turn == 6)
        def _():
            swap[2].start()
            wait_of["d", 0].wait_recv()
            to_core[4].start()
            wait_of["d", 1].wait_recv()
            to_core[5].start()
            add_core(1, at_x)
            near[2].start()
            add_core(2, at_y)
            near[3].start()

        @pl.when(turn == 7)
        def _():
            wait_of["dc", 0].wait_recv()
            wait_of["dc", 1].wait_recv()

        owner = owners[7]
        for index in range(7):
            owner = jnp.where(turn == index, owners[index], owner)
        up_rows = up[...].reshape(4 * ff_own, D)
        down_rows = down[...].reshape(4 * ff_own, D)

        def part(which, _):
            rows = span(which, 128)
            pre = dot_nt(mid_all[owner, rows, :], up_rows)
            square = pre * pre
            bend = jnp.tanh(GELU_SCALE * (pre + 0.044715 * (pre * square)))
            gl_all[owner, rows, :] = to_low(0.5 * pre * (1.0 + bend))
            slope = 0.5 * (1.0 + bend) + 0.5 * pre * (1.0 - bend * bend) * (
                GELU_SCALE * (1.0 + 3.0 * 0.044715 * square)
            )
            grad = to_low(dot_nt(cot_all[owner, rows, :], down_rows) * slope)
            dpre_all[owner, rows, :] = grad
            work[owner, rows, :] = to_low(dot_nn(grad, up_rows))
            return 0

        lax.fori_loop(0, 2, part, 0)
        return 0

    lax.fori_loop(0, 8, one_chunk, 0)
    swap[0].start()
    add_core(0, at_d)
    near[0].start()
    near[1].start()
    add_core(3, me)

    def grads(index, _):
        quarter, kind = index // 2, lax.rem(index, 2)
        columns = span(quarter, 128)

        @pl.when(kind == 0)
        def _():
            def add(owner, acc):
                return acc + dot_tn(dpre_all[owner, :, columns], mid_all[owner])

            ff_grads[quarter, 0] = to_low(lax.fori_loop(0, 8, add, jnp.zeros((128, D), wide)))

        @pl.when(kind == 1)
        def _():
            def add(owner, acc):
                return acc + dot_tn(gl_all[owner, :, columns], cot_all[owner])

            ff_grads[quarter, 1] = to_low(lax.fori_loop(0, 8, add, jnp.zeros((128, D), wide)))

        return 0

    lax.fori_loop(0, 8, grads, 0)
    near[0].wait_recv()
    add_into(at_y, views[0], near_got[0])
    far[0].start()
    near[1].wait_recv()
    add_into(at_x, views[1], near_got[1])
    far[1].start()
    near[2].wait_recv()
    add_into(me, views[0], near_got[2])
    near[3].wait_recv()
    add_into(me, views[1], near_got[3])

    def outward(owner, _):
        down_rows = down[...].reshape(4 * ff_own, D)
        for which in range(2):
            rows = pl.ds(128 * which, 128)
            extra[owner, rows, :] = to_low(dot_nn(gl_all[owner, rows, :], down_rows))
        return 0

    lax.fori_loop(0, 8, outward, 0)
    for slot, view in enumerate(views):
        far[slot].wait_recv()
        total[view, :] = work[me, view, :].astype(wide) + far_got[slot].astype(wide)
    sums[...] = jnp.zeros_like(sums)

    def back(which, _):
        rows = span(which, 128)
        grad = total[rows, :]
        centered, scale = norm_parts(hidden[which])
        normed = centered * scale
        sums[0:1, :] += jnp.sum(grad * normed, axis=0, keepdims=True)
        lifted = grad * gain
        row_grad = cot_all[me, rows, :].astype(wide) + scale * (
            lifted
            - jnp.mean(lifted, axis=-1, keepdims=True)
            - normed * jnp.mean(lifted * normed, axis=-1, keepdims=True)
        )
        d_hidden[which] = row_grad
        d_low[which] = to_low(row_grad)
        d_rows[which] = to_low(dot_nt(to_low(row_grad), w_out[...].reshape(D, D)))
        return 0

    lax.fori_loop(0, 2, back, 0)

    def line_copy(slot, sender, seq_from, rank_from, seq_to, rank_to):
        return pltpu.make_async_remote_copy(
            src_ref=d_rows.at[seq_to // 2, :, span(2 * rank_to + lax.rem(seq_to, 2), 128)],
            dst_ref=d_line.at[seq_from, span(rank_from, 128), :],
            send_sem=back_send.at[slot],
            recv_sem=back_recv.at[sender],
            device_id={"seq": seq_to, "tensor": rank_to},
            device_id_type=MESH_ID,
        )

    for slot, (_, seq_to, rank_to) in enumerate(peers):
        line_copy(slot, here, place, rank, seq_to, rank_to).start()
    d_line[place, span(rank, 128), :] = d_rows[mine, :, span(head, 128)]
    for index in range(LINE):
        columns = pl.ds(128 * index, 128)
        part = dot_tn(mixed_rows[0, :, columns], d_low[0]) + dot_tn(
            mixed_rows[1, :, columns], d_low[1]
        )
        part = to_low(part)
        for block in range(4):
            extra[
                4 * (index % 2) + block, 256 + 32 * (index // 2) : 288 + 32 * (index // 2), :
            ] = part[32 * block : 32 * block + 32, :]
    for slot, (other, seq_to, rank_to) in enumerate(peers):
        line_copy(slot, other, seq_to, rank_to, seq_to, rank_to).wait_recv()
    for slot, (_, seq_to, rank_to) in enumerate(peers):
        rows_copy(slot, here, place, rank, seq_to, rank_to).wait_send()
        line_copy(slot, here, place, rank, seq_to, rank_to).wait_send()
    for one in own + [on_x0, on_y1] + to_core + swap + near + far:
        one.wait_send()


GELU_SCALE = 0.7978845608028654


def middle(mixed, tokens, kept, spread, cot_all, vecs):
    low, wide = jnp.bfloat16, jnp.float32
    ff_own = (spread.shape[1] - SPREAD_FIRST) // 2
    shapes = (
        ((2, 128, D), wide),
        ((2, 128, D), wide),
        ((4, BLOCK, 128), low),
        ((8, D), wide),
        ((8, 384, D), low),
        ((4, 2, ff_own, D), low),
    )
    dma = pltpu.SemaphoreType.DMA
    return pl.pallas_call(
        middle_kernel,
        out_shape=[jax.ShapeDtypeStruct(*one) for one in shapes],
        in_specs=vmem_specs(2) + any_specs(3) + vmem_specs(1),
        out_specs=vmem_specs(6),
        scratch_shapes=[
            pltpu.VMEM((2, 128, D), low),
            pltpu.VMEM((8, 256, D), low),
            pltpu.VMEM((8, 256, 4 * ff_own), low),
            pltpu.VMEM((8, 256, 4 * ff_own), low),
            pltpu.VMEM((8, 256, D), low),
            pltpu.VMEM((4, 256, D), low),
            pltpu.VMEM((4, 128, D), low),
            pltpu.VMEM((2, 128, D), low),
            pltpu.VMEM((256, D), wide),
            pltpu.VMEM((2, 128, D), low),
            pltpu.VMEM((2, 128, D), low),
            pltpu.VMEM((4, 8, 32, D), low),
            pltpu.VMEM((4, ff_own, D), low),
            pltpu.VMEM((4, ff_own, D), low),
            pltpu.VMEM((8, 256, D), low),
            dma((15,)), dma((16,)), dma((14,)), dma((8, 2)), dma((10,)), dma((10,)), dma((15,)),
            dma((16,)), dma((4,)),
        ],
        compiler_params=pltpu.CompilerParams(
            collective_id=3, has_side_effects=True, vmem_limit_bytes=VMEM_LIMIT
        ),
        cost_estimate=pl.CostEstimate(
            flops=60000000000, bytes_accessed=60000000, transcendentals=0
        ),
        name="middle",
    )(mixed, tokens, kept, spread, cot_all, vecs)


SPREAD_FIRST = 0


WIDE = 2048


def opening_kernel(
    tokens, w_query, w_key, w_value, w_sout, w_out, begin, vecs, rel_bias, marks_own,
    rows_all, qkv, kept, table, marks, w_qkv,
    begin_rows, bias_rows, stage, send_sem, core_sem, recv_sem, piece_send, piece_recv, ring_send, ring_recv,
    mark_send, mark_recv, local_sem,
):
    side, place, half, rank = plane_place()
    mine = place // 2
    core = place + 1 - 2 * half
    other = lax.rem(place + 2, 4)
    me = plane_index(side, place)
    extra = 80
    fetch_columns((w_query, w_key, w_value), w_qkv, local_sem.at[0])
    loads = [
        pltpu.make_async_copy(
            w_sout.at[span(me, 32), :], kept.at[me, pl.ds(80 * rank, 32), :], local_sem.at[1]
        ),
        pltpu.make_async_copy(
            w_out.at[span(me, 32), :], kept.at[me, pl.ds(80 * rank + 48, 32), :], local_sem.at[3]
        ),
        pltpu.make_async_copy(begin.at[span(me, 16), :], begin_rows, local_sem.at[2]),
    ]
    for one in loads:
        one.start()
    barrier = pltpu.get_barrier_semaphore()
    greeted = [{"tensor": lax.rem(rank + step, 4)} for step in (1, 2, 3)]
    seats = [lax.rem(place + step, 4) for step in (1, 2, 3)]
    greeted += [{"seq": one} for one in seats] + [{"dp": 1 - side}]
    for target in greeted:
        pl.semaphore_signal(barrier, inc=1, device_id=target, device_id_type=MESH_ID)
    gain = vecs[3:4, :]

    def normed(which):
        centered, scale = norm_parts(tokens[which].astype(jnp.float32))
        return to_low(centered * scale * gain)

    def moved(block_id, origin, sem, target):
        view = rows_all.at[block_id, span(origin, 128), :]
        return pltpu.make_async_remote_copy(
            src_ref=view,
            dst_ref=view,
            send_sem=sem,
            recv_sem=recv_sem.at[block_id, origin],
            device_id=target,
            device_id_type=MESH_ID,
        )

    stage[...] = normed(1 - mine)
    marks[place] = marks_own[...]
    pl.semaphore_wait(barrier, 7)
    aside = pltpu.make_async_remote_copy(
        src_ref=stage,
        dst_ref=rows_all.at[place, span(rank, 128), :],
        send_sem=send_sem.at[0, 0, 3],
        recv_sem=recv_sem.at[place, rank],
        device_id={"seq": other},
        device_id_type=MESH_ID,
    )
    aside.start()

    def mark_move(slot, origin, target):
        return pltpu.make_async_remote_copy(
            src_ref=marks.at[origin],
            dst_ref=marks.at[origin],
            send_sem=mark_send.at[slot],
            recv_sem=mark_recv.at[origin],
            device_id={"seq": target},
            device_id_type=MESH_ID,
        )

    def piece_move(slot, origin, target):
        view = kept.at[me, span(origin, extra), :]
        return pltpu.make_async_remote_copy(
            src_ref=view,
            dst_ref=view,
            send_sem=piece_send.at[slot],
            recv_sem=piece_recv.at[origin],
            device_id=target,
            device_id_type=MESH_ID,
        )

    for one in loads:
        one.wait()
    kept[me, pl.ds(pl.multiple_of(80 * rank + 32, 16), 16), :] = to_low(begin_rows[...])
    for slot in range(3):
        piece_move(slot, rank, greeted[slot]).start()
    for slot, target in enumerate(seats):
        mark_move(slot, place, target).start()
    rows_all[place, span(rank, 128), :] = normed(mine)
    right, left = {"tensor": lax.rem(rank + 1, 4)}, {"tensor": lax.rem(rank + 3, 4)}
    blocks = (place, other)

    def pass_on(which, distance):
        block_id = blocks[which]

        @pl.when((rank < 3) & (rank >= distance))
        def _():
            moved(block_id, jnp.maximum(rank - distance, 0), send_sem.at[which, distance, 0], right).start()

        @pl.when((rank > 0) & (rank + distance <= 3))
        def _():
            moved(block_id, jnp.minimum(rank + distance, 3), send_sem.at[which, distance, 1], left).start()

    def pass_done(which, distance):
        block_id = blocks[which]

        @pl.when((rank < 3) & (rank >= distance))
        def _():
            moved(block_id, jnp.maximum(rank - distance, 0), send_sem.at[which, distance, 0], right).wait_send()

        @pl.when((rank > 0) & (rank + distance <= 3))
        def _():
            moved(block_id, jnp.minimum(rank + distance, 3), send_sem.at[which, distance, 1], left).wait_send()

    def project(block_id, origin):
        view = span(origin, 128)
        qkv[block_id, view, :] = to_low(dot_nn(rows_all[block_id, view, :], w_qkv[...]))

    def rows_steps():
        pass_on(0, 0)
        fetched(w_qkv, local_sem.at[0])
        moved(place, rank, core_sem.at[0, rank], {"seq": core}).start()
        project(place, rank)
        moved(other, rank, send_sem.at[0, 0, 3], {"seq": other}).wait_recv()
        pass_on(1, 0)
        moved(other, rank, core_sem.at[1, rank], {"seq": core}).start()
        project(other, rank)
        yield
        for distance in (1, 2, 3):
            for which in (0, 1):
                block_id = blocks[which]
                for way, ok, origin in (
                    (0, rank >= distance, jnp.maximum(rank - distance, 0)),
                    (1, rank + distance <= 3, jnp.minimum(rank + distance, 3)),
                ):

                    @pl.when(ok)
                    def _():
                        moved(block_id, origin, send_sem.at[which, distance, way], right).wait_recv()
                        if distance < 3:
                            if way == 0:

                                @pl.when(rank < 3)
                                def _():
                                    moved(
                                        block_id, origin, send_sem.at[which, distance, 0], right
                                    ).start()

                            else:

                                @pl.when(rank > 0)
                                def _():
                                    moved(
                                        block_id, origin, send_sem.at[which, distance, 1], left
                                    ).start()

                        moved(block_id, origin, core_sem.at[which, origin], {"seq": core}).start()
                        project(block_id, origin)

                yield
        for which, block_id in enumerate((core, lax.rem(core + 2, 4))):
            for origin in range(4):
                moved(block_id, origin, core_sem.at[which, origin], {"seq": core}).wait_recv()
                project(block_id, origin)
        for which in (0, 1):
            for distance in (0, 1, 2):
                pass_done(which, distance)
            for origin in range(4):
                moved(blocks[which], origin, core_sem.at[which, origin], {"seq": core}).wait_send()

    def piece_steps():
        for slot in range(3):
            piece_move(slot, lax.rem(rank + slot + 1, 4), greeted[slot]).wait_recv()
        for _ in plane_gather(row_halves(kept, 4 * extra), ring_send, ring_recv):
            yield
        for slot in range(3):
            piece_move(slot, rank, greeted[slot]).wait_send()

    def bias_steps():
        lane = lax.broadcasted_iota(jnp.int32, (8, WIDE), 1)
        bucket_ids = bucket_of(jnp.where(lane >= WIDE - BLOCK, lane - WIDE - BLOCK, lane - BLOCK))
        first = jnp.zeros((8, WIDE), jnp.float32)
        for bucket_id in range(BUCKETS):
            first = jnp.where(bucket_ids == bucket_id, rel_bias[bucket_id, half], first)
        row = lax.broadcasted_iota(jnp.int32, (8, WIDE), 0)
        for step in (1, 2, 4):
            first = jnp.where(row // step % 2 == 1, pltpu.roll(first, step, 1), first)
        bias_rows[...] = first
        yield

        def one(group, _):
            table[span(group, 8), :] = pltpu.roll(bias_rows[...], 8 * group, 1)[:, 0 : 2 * BLOCK]
            return 0

        for part in range(4):
            lax.fori_loop(16 * part, 16 * part + 16, one, 0)
            yield

    run_all(rows_steps(), piece_steps(), bias_steps())
    aside.wait_send()
    for slot, target in enumerate(seats):
        mark_move(slot, place, target).wait_send()
        mark_move(slot, target, target).wait_recv()


def opening(tokens, w_query, w_key, w_value, w_sout, w_out, begin, vecs, rel_bias, marks):
    low, wide = jnp.bfloat16, jnp.float32
    shapes = (
        ((4, BLOCK, D), low),
        ((4, BLOCK, 384), low),
        ((8, 4 * 80, D), low),
        ((BLOCK, 2 * BLOCK), wide),
        ((4, 8, 128), jnp.int32),
        ((D, 384), low),
    )
    dma = pltpu.SemaphoreType.DMA
    outs = pl.pallas_call(
        opening_kernel,
        out_shape=[jax.ShapeDtypeStruct(*one) for one in shapes],
        in_specs=vmem_specs(1)
        + any_specs(6)
        + vmem_specs(1)
        + [pl.BlockSpec(memory_space=pltpu.SMEM)]
        + vmem_specs(1),
        out_specs=vmem_specs(6),
        scratch_shapes=[
            pltpu.VMEM((16, D), wide),
            pltpu.VMEM((8, WIDE), wide),
            pltpu.VMEM((128, D), low),
            dma((2, 4, 4)),
            dma((2, 4)),
            dma((4, 4)),
            dma((3,)),
            dma((4,)),
            dma((14,)),
            dma((8, 2)),
            dma((3,)),
            dma((4,)),
            dma((4,)),
        ],
        compiler_params=pltpu.CompilerParams(
            collective_id=5, has_side_effects=True, vmem_limit_bytes=VMEM_LIMIT
        ),
        cost_estimate=pl.CostEstimate(
            flops=30000000000, bytes_accessed=30000000, transcendentals=0
        ),
        name="opening",
    )(tokens, w_query, w_key, w_value, w_sout, w_out, begin, vecs, rel_bias, marks)
    rows_all, qkv, kept, table, marks, w_qkv = outs
    return rows_all, qkv, kept.reshape(8, 4, 80, D), table, marks, w_qkv


def pair_sum(part, near_got, far_got, result, rows, send_sem, recv_sem):
    side, place, half, rank = plane_place()
    mine = place // 2
    across, beside = 1 - side, 1 - mine
    me = 2 * side + mine
    at_x, at_y, at_d = 2 * across + mine, 2 * side + beside, 2 * across + beside
    to_x, to_y = {"dp": across}, {"seq": lax.rem(place + 2, 4)}
    size = rows // 2
    views = (pl.ds(0, size), pl.ds(size, size))

    def moved(source, target_ref, slot, target):
        return pltpu.make_async_remote_copy(
            src_ref=source,
            dst_ref=target_ref,
            send_sem=send_sem.at[slot],
            recv_sem=recv_sem.at[slot],
            device_id=target,
            device_id_type=MESH_ID,
        )

    def add_into(owner, view, other):
        part[owner, view, :] = to_low(
            part[owner, view, :].astype(jnp.float32) + other.astype(jnp.float32)
        )

    near = [
        moved(part.at[at_d, views[0], :], near_got.at[0], 0, to_x),
        moved(part.at[at_d, views[1], :], near_got.at[1], 1, to_y),
        moved(part.at[at_x, views[0], :], near_got.at[2], 2, to_x),
        moved(part.at[at_y, views[1], :], near_got.at[3], 3, to_y),
    ]
    for one in near:
        one.start()
    yield
    near[0].wait_recv()
    add_into(at_y, views[0], near_got[0])
    far = [
        moved(part.at[at_y, views[0], :], far_got.at[0], 4, to_y),
        moved(part.at[at_x, views[1], :], far_got.at[1], 5, to_x),
    ]
    far[0].start()
    near[1].wait_recv()
    add_into(at_x, views[1], near_got[1])
    far[1].start()
    yield
    near[2].wait_recv()
    add_into(me, views[0], near_got[2])
    near[3].wait_recv()
    add_into(me, views[1], near_got[3])
    for slot, view in enumerate(views):
        far[slot].wait_recv()
        result[me, view, :] = to_low(
            part[me, view, :].astype(jnp.float32) + far_got[slot].astype(jnp.float32)
        )

    def given(owner, which, slot, target):
        view = result.at[owner, views[which], :]
        return moved(view, view, slot, target)

    own = [
        given(me, 0, 6, to_x),
        given(me, 1, 7, to_y),
        given(me, 1, 8, to_x),
        given(me, 0, 9, to_y),
    ]
    for one in own:
        one.start()
    yield
    given(at_x, 0, 6, to_x).wait_recv()
    last = [given(at_x, 0, 10, to_y), given(at_y, 1, 11, to_x)]
    last[0].start()
    given(at_y, 1, 7, to_y).wait_recv()
    last[1].start()
    yield
    given(at_x, 1, 8, to_x).wait_recv()
    given(at_y, 0, 9, to_y).wait_recv()
    given(at_d, 0, 10, to_y).wait_recv()
    given(at_d, 1, 11, to_x).wait_recv()
    for one in near + far + own + last:
        one.wait_send()


PAIR_ROWS = 640


def closing_kernel(
    d_qkv, w_qkv, tokens, d_hidden, vecs, rows_hbm, low_hbm, d_qkvst_hbm, os_hbm, du_hbm,
    d_start, dz_hbm, small, out_part,
    inputs_grad, pair_out, sout_out, small_out,
    rows_all, state_low, d_qkvst, os_rows, du_rows, dz_sum,
    leave, came, sums, got, final, cross, cross_got,
    pair_part, pair_near, pair_far,
    work, core_got, near_got, far_got, total, z_part, z_got,
    diag, small_z, small_p,
    line_send, line_recv, way_send, way_recv, pair_send, pair_recv, core_sem,
    ring_send, ring_recv, zs_send, zs_recv, gather_send, gather_recv, small_send, small_recv, local_sem,
):
    loads = [
        pltpu.make_async_copy(source, target, local_sem.at[slot])
        for slot, (source, target) in enumerate(
            (
                (rows_hbm, rows_all),
                (d_qkvst_hbm, d_qkvst),
                (low_hbm, state_low),
                (os_hbm, os_rows),
                (du_hbm, du_rows),
                (dz_hbm, dz_sum),
            )
        )
    ]
    for one in loads:
        one.start()
    side, place, half, rank = plane_place()
    mine = place // 2
    core = place + 1 - 2 * half
    other = lax.rem(place + 2, 4)
    me = plane_index(side, place)
    ranks = [lax.rem(rank + step, 4) for step in (1, 2, 3)]
    spots_of = [lax.rem(me + step, 8) for step in range(1, 8)]
    barrier = pltpu.get_barrier_semaphore()
    for target in ranks:
        pl.semaphore_signal(barrier, inc=1, device_id={"tensor": target}, device_id_type=MESH_ID)
    for target in spots_of:
        pl.semaphore_signal(
            barrier,
            inc=1,
            device_id={"dp": target // 4, "seq": lax.rem(target, 4)},
            device_id_type=MESH_ID,
        )
    gain = vecs[3:4, :]
    right, left = {"tensor": lax.rem(rank + 1, 4)}, {"tensor": lax.rem(rank + 3, 4)}

    def moved(source, target_ref, send, recv, target):
        return pltpu.make_async_remote_copy(
            src_ref=source,
            dst_ref=target_ref,
            send_sem=send,
            recv_sem=recv,
            device_id=target,
            device_id_type=MESH_ID,
        )

    def to_core(which):
        return moved(
            leave.at[which], came.at[which], line_send.at[which], line_recv.at[which], {"seq": core}
        )

    def crossing():
        return moved(cross, cross_got, line_send.at[2], line_recv.at[2], {"seq": other})

    near = rank // 2
    at_end = (rank == 0) | (rank == 3)

    def hop(way, which, target):
        return moved(
            sums.at[which, target],
            got.at[way, which, target],
            way_send.at[which, target],
            way_recv.at[way, which, target],
            {"tensor": lax.rem(rank + 5 - 2 * way, 4)},
        )

    def target_of(way, distance):
        return (1 - way) * (3 - distance) + way * distance

    def pass_first(which):
        @pl.when(at_end)
        def _():
            for distance in range(3):
                hop(near, which, target_of(near, distance)).start()

    def pass_on(way, which, distance):
        @pl.when(jnp.logical_not(at_end))
        def _():
            target = target_of(way, distance)
            hop(way, which, target).wait_recv()
            sums[which, target] = to_low(
                sums[which, target].astype(jnp.float32)
                + got[way, which, target].astype(jnp.float32)
            )
            hop(way, which, target).start()

    def finish(which):
        final[which] = sums[which, rank].astype(jnp.float32)

        @pl.when(rank > 0)
        def _():
            hop(0, which, rank).wait_recv()
            final[which] += got[0, which, rank].astype(jnp.float32)

        @pl.when(rank < 3)
        def _():
            hop(1, which, rank).wait_recv()
            final[which] += got[1, which, rank].astype(jnp.float32)

    def line_steps():
        for which, block_id in enumerate((lax.rem(core + 2, 4), core)):

            def partner(chunk, _):
                rows = span(chunk, ROWS)
                leave[which, rows, :] = to_low(dot_nt(d_qkv[block_id, rows, :], w_qkv[...]))
                return 0

            lax.fori_loop(0, CHUNKS, partner, 0)
            if which == 0:
                pl.semaphore_wait(barrier, 10)
            to_core(which).start()
        for which, block_id in enumerate((other, place)):
            to_core(which).wait_recv()

            def own(chunk, _):
                rows = span(chunk, ROWS)
                sums[which, chunk] = to_low(
                    dot_nt(d_qkv[block_id, rows, :], w_qkv[...])
                    + came[which, rows, :].astype(jnp.float32)
                )
                return 0

            lax.fori_loop(0, CHUNKS, own, 0)
            pass_first(which)
        yield
        for which in (0, 1):
            pass_on(near, which, 0)
            yield
            pass_on(near, which, 1)
            pass_on(1 - near, which, 0)
            yield
            finish(which)
            if which == 0:
                cross[...] = to_low(final[0])
                crossing().start()
            yield
        crossing().wait_recv()
        final[0] = cross_got[...].astype(jnp.float32)
        small_z[rank] = small[...]
        for which, row_set in ((1, mine), (0, 1 - mine)):
            grad = final[which]
            centered, scale = norm_parts(tokens[row_set].astype(jnp.float32))
            normed = centered * scale
            small_z[rank, 0:1, :] += jnp.sum(grad * normed, axis=0, keepdims=True)
            lifted = grad * gain
            inputs_grad[row_set] = d_hidden[row_set] + scale * (
                lifted
                - jnp.mean(lifted, axis=-1, keepdims=True)
                - normed * jnp.mean(lifted * normed, axis=-1, keepdims=True)
            )
        crossing().wait_send()
        for which in (0, 1):
            to_core(which).wait_send()
            for target in range(4):

                @pl.when(rank != target)
                def _():
                    hop(0, which, target).wait_send()

    def pair_steps():
        loads[0].wait()
        loads[1].wait()
        loads[2].wait()
        for chunk in range(4):
            if chunk < 3:
                first = 128 * chunk

                def one(block_id, acc):
                    acc = acc + dot_tn(d_qkv[block_id, :, first : first + 128], rows_all[block_id])
                    if chunk > 0:
                        acc = acc + dot_tn(
                            d_qkvst[block_id, :, first : first + 128], state_low[block_id]
                        )
                    return acc

            else:

                def one(block_id, acc):
                    return acc + dot_tn(d_qkvst[block_id, :, 0:128], state_low[block_id])

            acc = lax.fori_loop(0, 4, one, jnp.zeros((128, D), jnp.float32))
            low = to_low(acc)
            first = 128 * chunk
            while first < 128 * (chunk + 1):
                owner, inside = first // 160, first % 160
                size = min(160 - inside, 128 * (chunk + 1) - first)
                begin = first - 128 * chunk
                pair_part[owner, inside : inside + size, :] = low[begin : begin + size, :]
                first += size
        pair_part[3, 32:96, :] = to_low(d_start[...])
        pair_part[3, 96:160, :] = jnp.zeros((64, D), jnp.bfloat16)
        for _ in pair_sum(
            pair_part, pair_near, pair_far, pair_out.at[half], 160, pair_send, pair_recv
        ):
            yield
        full = moved(
            pair_out.at[half], pair_out.at[half], core_sem.at[0], core_sem.at[1], {"seq": core}
        )
        full.start()
        yield
        moved(
            pair_out.at[1 - half], pair_out.at[1 - half], core_sem.at[0], core_sem.at[1],
            {"seq": core},
        ).wait_recv()
        full.wait_send()

    def sout_steps():
        loads[3].wait()
        loads[4].wait()
        for head in range(LINE):
            low = to_low(dot_tn(os_rows[:, 128 * head : 128 * head + 128], du_rows[...]))
            for piece in range(4):
                work[
                    4 * (head % 2) + piece, 32 * (head // 2) : 32 * (head // 2) + 32, :
                ] = low[32 * piece : 32 * piece + 32, :]
        for _ in plane_scatter(
            work, core_got, near_got, far_got, total, 128, ring_send, ring_recv
        ):
            yield
        z_part[:, 0:32, :] = to_low(total[...]).reshape(4, 32, D)
        z_part[:, 32:64, :] = out_part[...].reshape(4, 32, D)
        out = [
            moved(
                z_part.at[target], z_got.at[rank], zs_send.at[slot], zs_recv.at[rank],
                {"tensor": target},
            )
            for slot, target in enumerate(ranks)
        ]
        for one in out:
            one.start()
        z_got[rank] = z_part[rank]
        yield
        for slot, target in enumerate(ranks):
            moved(
                z_part.at[target], z_got.at[target], zs_send.at[slot], zs_recv.at[target],
                {"tensor": target},
            ).wait_recv()
        acc = z_got[0].astype(jnp.float32)
        for target in range(1, 4):
            acc = acc + z_got[target].astype(jnp.float32)
        sout_out[me] = to_low(acc)
        for _ in plane_gather(row_halves(sout_out, 64), gather_send, gather_recv):
            yield
        for one in out:
            one.wait_send()

    def diag_steps():
        loads[5].wait()
        diag[...] = jnp.zeros_like(diag)
        for part in range(4):

            def one(group, _):
                rows = dz_sum[span(group, 8), :]
                wide = jnp.concatenate(
                    [rows, jnp.zeros((8, WIDE - 2 * BLOCK), jnp.float32)], axis=1
                )
                diag[...] += pltpu.roll(wide, lax.rem(WIDE - 8 * group, WIDE), 1)
                return 0

            lax.fori_loop(16 * part, 16 * part + 16, one, 0)
            yield
        total_line = diag[...]
        row = lax.broadcasted_iota(jnp.int32, (8, WIDE), 0)
        for step in (1, 2, 4):
            total_line = jnp.where(
                row // step % 2 == 1, pltpu.roll(total_line, WIDE - step, 1), total_line
            )
        lane = lax.broadcasted_iota(jnp.int32, (8, WIDE), 1)
        offset = jnp.where(lane >= WIDE - BLOCK, lane - WIDE - BLOCK, lane - BLOCK)
        bucket_ids = bucket_of(offset)
        spot = lax.broadcasted_iota(jnp.int32, (1, 256), 1) - BUCKETS * (2 * rank + half)
        placed = jnp.zeros((1, 256), jnp.float32)
        for bucket_id in range(BUCKETS):
            chosen = jnp.where(bucket_ids == bucket_id, total_line, 0.0)
            value = jnp.sum(jnp.sum(chosen, axis=0, keepdims=True), axis=1, keepdims=True)
            placed = jnp.where(spot == bucket_id, value, placed)
        diag[0:1, 0:256] = placed

    extra = sout_steps()
    run_all(line_steps(), pair_steps(), extra, diag_steps(), extra)
    small_z[rank, 4:5, 0:256] = diag[0:1, 0:256]

    def small_over_z(slot, sender, target):
        return moved(
            small_z.at[sender], small_z.at[sender], small_send.at[slot], small_recv.at[sender],
            {"tensor": target},
        )

    for slot, target in enumerate(ranks):
        small_over_z(slot, rank, target).start()
    for slot, target in enumerate(ranks):
        small_over_z(slot, target, target).wait_recv()
    small_p[me] = small_z[0] + small_z[1] + small_z[2] + small_z[3]

    def small_over_plane(slot, sender, target):
        return moved(
            small_p.at[sender], small_p.at[sender], small_send.at[3 + slot],
            small_recv.at[4 + sender],
            {"dp": target // 4, "seq": lax.rem(target, 4)},
        )

    for slot, target in enumerate(spots_of):
        small_over_plane(slot, me, target).start()
    for slot, target in enumerate(spots_of):
        small_over_plane(slot, target, target).wait_recv()
    acc = small_p[0]
    for target in range(1, 8):
        acc = acc + small_p[target]
    small_out[...] = acc
    for slot, target in enumerate(ranks):
        small_over_z(slot, rank, target).wait_send()
    for slot, target in enumerate(spots_of):
        small_over_plane(slot, me, target).wait_send()


def closing(
    d_qkv, w_qkv, tokens, d_hidden, vecs, rows_all, state_low, d_qkvst, os_rows, du_rows,
    d_start, dz_sum, small, out_part,
):
    low, wide = jnp.bfloat16, jnp.float32
    shapes = (
        ((2, 128, D), wide),
        ((2, 4, PAIR_ROWS // 4, D), low),
        ((8, 64, D), low),
        ((8, D), wide),
    )
    dma = pltpu.SemaphoreType.DMA
    return pl.pallas_call(
        closing_kernel,
        out_shape=[jax.ShapeDtypeStruct(*one) for one in shapes],
        in_specs=vmem_specs(5) + any_specs(5) + vmem_specs(1) + any_specs(1) + vmem_specs(2),
        out_specs=vmem_specs(4),
        scratch_shapes=[
            pltpu.VMEM((4, BLOCK, D), low),
            pltpu.VMEM((4, BLOCK, D), low),
            pltpu.VMEM((4, BLOCK, 384), low),
            pltpu.VMEM((256, D), low),
            pltpu.VMEM((256, D), low),
            pltpu.VMEM((BLOCK, 2 * BLOCK), wide),
            pltpu.VMEM((2, BLOCK, D), low),
            pltpu.VMEM((2, BLOCK, D), low),
            pltpu.VMEM((2, 4, 128, D), low),
            pltpu.VMEM((2, 2, 4, 128, D), low),
            pltpu.VMEM((2, 128, D), wide),
            pltpu.VMEM((128, D), low),
            pltpu.VMEM((128, D), low),
            pltpu.VMEM((4, PAIR_ROWS // 4, D), low),
            pltpu.VMEM((4, PAIR_ROWS // 8, D), low),
            pltpu.VMEM((2, PAIR_ROWS // 8, D), low),
            pltpu.VMEM((8, 128, D), low),
            pltpu.VMEM((4, 128, D), low),
            pltpu.VMEM((4, 64, D), low),
            pltpu.VMEM((2, 64, D), low),
            pltpu.VMEM((128, D), wide),
            pltpu.VMEM((4, 64, D), low),
            pltpu.VMEM((4, 64, D), low),
            pltpu.VMEM((8, WIDE), wide),
            pltpu.VMEM((4, 8, D), wide),
            pltpu.VMEM((8, 8, D), wide),
            dma((3,)), dma((3,)), dma((2, 4)), dma((2, 2, 4)), dma((12,)), dma((12,)), dma((2,)),
            dma((10,)), dma((10,)), dma((3,)), dma((4,)), dma((16,)), dma((8, 2)), dma((10,)),
            dma((12,)), dma((6,)),
        ],
        compiler_params=pltpu.CompilerParams(
            collective_id=6, has_side_effects=True, vmem_limit_bytes=VMEM_LIMIT
        ),
        cost_estimate=pl.CostEstimate(
            flops=30000000000, bytes_accessed=30000000, transcendentals=0
        ),
        name="closing",
    )(
        d_qkv, w_qkv, tokens, d_hidden, vecs, rows_all, state_low, d_qkvst, os_rows, du_rows,
        d_start, dz_sum, small, out_part,
    )


def finish_kernel(
    pair, pair_tail, two, ff,
    query, key, value, squery, out, sout, up, down, state,
):
    step = pl.program_id(0)
    wide = jnp.float32
    up[...] = ff[0, 0].astype(wide).T
    down[...] = ff[0, 1].astype(wide)
    sout[...] = two[0, 0:32].astype(wide)
    out[...] = two[0, 32:64].astype(wide)
    for which, target in enumerate((query, key, value, squery)):

        @pl.when(step // 2 == which)
        def _():
            target[...] = pair[0].astype(wide).T

    @pl.when(step == 0)
    def _():
        state[...] = pair_tail[...].reshape(128, D).astype(wide)


def finish_grads(pair, two, ff):
    wide = jnp.float32
    turned = [
        pl.BlockSpec((D, 128), lambda i, w=which: (0, jnp.clip(i - 2 * w, 0, 1)))
        for which in range(4)
    ]
    square = jax.ShapeDtypeStruct((D, 256), wide)
    rows = jax.ShapeDtypeStruct((256, D), wide)
    whole = jax.ShapeDtypeStruct((D, D), wide)
    return pl.pallas_call(
        finish_kernel,
        grid=(8,),
        out_shape=[square] * 4 + [rows] * 2 + [whole] * 2 + [jax.ShapeDtypeStruct((128, D), wide)],
        in_specs=[
            pl.BlockSpec((1, 128, D), lambda i: (i % 2, i // 2, 0)),
            pl.BlockSpec((2, 64, D), lambda i: (0, 8, 0)),
            pl.BlockSpec((1, 64, D), lambda i: (i, 0, 0)),
            pl.BlockSpec((1, 2, 128, D), lambda i: (i, 0, 0, 0)),
        ],
        out_specs=turned
        + [pl.BlockSpec((32, D), lambda i: (i, 0))] * 2
        + [pl.BlockSpec((D, 128), lambda i: (0, i)), pl.BlockSpec((128, D), lambda i: (i, 0))]
        + [pl.BlockSpec((128, D), lambda i: (0, 0))],
        compiler_params=pltpu.CompilerParams(vmem_limit_bytes=VMEM_LIMIT),
        name="finish_grads",
    )(pair, pair, two, ff)


def swap_seq(value):
    return lax.all_to_all(value, "seq", 0, 0, tiled=False)


def line_body(
    inputs,
    seg_starts,
    lengths,
    init_state,
    attn_gain,
    state_gain,
    mlp_gain,
    w_query,
    w_key,
    w_value,
    w_out,
    w_squery,
    w_sout,
    w_up,
    w_down,
    rel_bias,
    gate_bias,
    out_cot,
    state_cot,
):
    low, wide = jnp.bfloat16, jnp.float32
    place = lax.axis_index("seq")
    half = lax.rem(place, 2)
    mine = place // 2
    plane = ("dp", "seq")
    spot = 4 * lax.axis_index("dp") + place
    gate_value = jax.nn.sigmoid(gate_bias)
    vecs = jnp.stack(
        [state_gain, gate_value, mlp_gain, attn_gain] + [jnp.zeros_like(gate_value)] * 4
    )
    marks = jnp.concatenate([seg_starts[:, 0], lengths, jnp.zeros((4,), jnp.int32)])
    marks = jnp.broadcast_to(marks[:, None], (8, 128))
    cot_used = lax.all_gather(out_cot.reshape(256, D), plane, axis=0, tiled=True)
    rows_all, qkv, kept, bias, marks, w_qkv = opening(
        inputs, w_query, w_key, w_value, w_sout, w_out, init_state, vecs, rel_bias, marks
    )

    ff_own = w_up.shape[1] // 8
    piece_of = lambda weight: lax.dynamic_slice_in_dim(weight, spot * 32, 32, 1).T
    back_own = jnp.stack(
        [
            piece_of(w_squery),
            piece_of(w_key),
            piece_of(w_value),
        ]
    )
    pieces = jnp.concatenate(
        [
            lax.dynamic_slice_in_dim(w_up, spot * ff_own, ff_own, 1).T,
            lax.dynamic_slice_in_dim(w_down, spot * ff_own, ff_own, 0),
        ],
        axis=0,
    )
    qkv, pieces, cot_used, back_own = lax.optimization_barrier(
        (qkv, pieces, cot_used, back_own)
    )
    spread = lax.all_gather(pieces, "tensor", axis=0, tiled=True).reshape(4, 2 * ff_own, D)
    mixed, lse_tok, state_rows, state_low, qkvst, lse_st, os_rows, cots, back = forward_chain(
        marks, qkv, kept, w_squery, w_qkv, vecs, bias, state_cot.reshape(4, 64, D), back_own
    )
    hidden_in, grad_hidden, d_mixed, mlp_sums, extra, ff_grads = middle(
        mixed, inputs, kept, spread, cot_used.reshape(8, 256, D), vecs
    )
    d_mixed, ff_grads = lax.optimization_barrier((d_mixed, ff_grads))
    ff_sum = lax.psum_scatter(
        ff_grads.reshape(ff_grads.shape[2] * 8, D), "tensor", scatter_dimension=0, tiled=True
    )
    (
        d_qkv, d_qkvst, du_rows, d_start, sums, dz_sum, state_out, tokens_out, out_part,
    ) = backward_chain(
        marks, qkv, d_mixed, lse_tok, qkvst, lse_st, state_rows, init_state, cots,
        back, kept, vecs, bias, extra, hidden_in,
    )
    d_qkv, ff_sum = lax.optimization_barrier((d_qkv, ff_sum))
    ff_total = lax.all_gather(ff_sum, plane, axis=0, tiled=True).reshape(8, 2, ff_own, D)
    small = jnp.concatenate(
        [jnp.zeros((1, D), wide), sums[1:2], mlp_sums[0:1], sums[0:1], jnp.zeros((4, D), wide)]
    )
    inputs_grad, pair, two_grads, small = closing(
        d_qkv, w_qkv, inputs, grad_hidden, vecs, rows_all, state_low, d_qkvst,
        os_rows.reshape(256, D), du_rows.reshape(256, D), d_start, dz_sum, small, out_part,
    )
    pair = pair.reshape(2, PAIR_ROWS, D)
    (
        query_grad, key_grad, value_grad, squery_grad, out_grad, sout_grad, up_grad, down_grad,
        state_grad,
    ) = finish_grads(pair, two_grads, ff_total)
    bias_grad = lax.dynamic_slice_in_dim(
        small[4, : LINE * BUCKETS].reshape(4, 2, BUCKETS), lax.axis_index("tensor"), 1, 0
    )[0].T
    return (
        tokens_out,
        state_out[:, None],
        inputs_grad,
        state_grad,
        small[0],
        small[1],
        small[2],
        query_grad,
        key_grad,
        value_grad,
        out_grad,
        squery_grad,
        sout_grad,
        up_grad,
        down_grad,
        bias_grad,
        small[3],
    )


def solution(mesh):
    return jax.shard_map(
        chosen_body(mesh),
        mesh=mesh,
        in_specs=(
            P("dp", ("seq", "tensor"), None),
            P("dp", "seq"),
            P("dp"),
            P("tensor", None),
            P(),
            P(),
            P(),
            P(None, "tensor"),
            P(None, "tensor"),
            P(None, "tensor"),
            P("tensor", None),
            P(None, "tensor"),
            P("tensor", None),
            P(None, "tensor"),
            P("tensor", None),
            P(None, "tensor"),
            P(),
            P("dp", ("seq", "tensor"), None),
            P("dp", "seq", "tensor", None),
        ),
        out_specs=(
            P("dp", ("seq", "tensor"), None),
            P("dp", "seq", "tensor", None),
            P("dp", ("seq", "tensor"), None),
            P("tensor", None),
            P(),
            P(),
            P(),
            P(None, "tensor"),
            P(None, "tensor"),
            P(None, "tensor"),
            P("tensor", None),
            P(None, "tensor"),
            P("tensor", None),
            P(None, "tensor"),
            P("tensor", None),
            P(None, "tensor"),
            P(),
        ),
        check_vma=False,
    )
```

```python
import jax
import jax.numpy as jnp
from jax import lax
from jax.experimental import pallas as pl
from jax.experimental.pallas import tpu as pltpu
from jax.sharding import PartitionSpec as P

D = 1024
HEAD_DIM = 128
STATES = 512
BLOCK = 512
SEG = 256
BUCKETS = 32


norm_eps = 1e-06
masked_score = -1e30
bucket_edges = (12, 16, 23, 32, 46, 64, 91)


def passed_along(value, axis, steps):
    count = lax.axis_size(axis)
    leading, last = (max(0, -steps), min(count, count - steps))
    return lax.ppermute(value, axis, [(source, source + steps) for source in range(leading, last)])


def bucket_of(relative):
    distance = jnp.abs(relative)
    far_bucket = 8 + sum(((distance >= boundary).astype(jnp.int32) for boundary in bucket_edges))
    near_far = jnp.where(distance < 8, distance, far_bucket)
    return near_far + 16 * (relative > 0).astype(jnp.int32)


def token_mask(seg_start, seq_length, block_index):
    positions = jnp.arange(BLOCK)
    offset = block_index * BLOCK
    prev_valid = (block_index > 0) & (offset - BLOCK + positions < seq_length)
    cur_valid = offset + positions < seq_length
    inside = (positions >= seg_start) & (positions < seg_start + SEG)
    prev_mask = (positions[None, :] > positions[:, None]) & prev_valid[None, :]
    cur_mask = (
        (positions[None, :] <= positions[:, None]) | inside[None, :] & inside[:, None]
    ) & cur_valid[None, :]
    state_mask = jnp.ones((BLOCK, STATES), jnp.bool_)
    return jnp.concatenate([prev_mask, cur_mask, state_mask], axis=1)


def state_mask_of(valid_blk):
    batch_count = valid_blk.shape[0]
    block_part = jnp.broadcast_to(valid_blk[:, None, :], (batch_count, STATES, BLOCK))
    return jnp.concatenate([block_part, jnp.ones((batch_count, STATES, STATES), jnp.bool_)], axis=2)


def layer_norm(values, gain_vec):
    centered = values - jnp.mean(values, axis=-1, keepdims=True)
    spread = jnp.mean(centered * centered, axis=-1, keepdims=True)
    return centered * lax.rsqrt(spread + norm_eps) * gain_vec


def norm_back(values, gain_vec, grad_out):
    _, pullback = jax.vjp(layer_norm, values, gain_vec)
    return pullback(grad_out)


def gelu_back(pre_act, grad_out):
    _, pullback = jax.vjp(jax.nn.gelu, pre_act)
    return pullback(grad_out)[0]


def to_low(array_in):
    return array_in.astype(jnp.bfloat16)


def matmul(left, right):
    return jnp.einsum("...k,kn->...n", left, right, preferred_element_type=jnp.float32)


def matmul_t(left, right):
    return jnp.einsum("...n,kn->...k", left, right, preferred_element_type=jnp.float32)


def outer_sum(left, right):
    left_flat = left.reshape(-1, left.shape[-1])
    right_flat = right.reshape(-1, right.shape[-1])
    return lax.dot_general(
        left_flat, right_flat, (((0,), (0,)), ((), ())), preferred_element_type=jnp.float32
    )


def gather_rows(values):
    return lax.all_gather(values, "tensor", axis=1, tiled=True)


def sum_rows(terms):
    return lax.psum_scatter(
        terms.astype(jnp.bfloat16), "tensor", scatter_dimension=1, tiled=True
    ).astype(jnp.float32)


def pass_state(rows_now):
    return passed_along(rows_now.astype(jnp.bfloat16), "seq", 1).astype(rows_now.dtype)


def pass_back(grad_now):
    return passed_along(grad_now.astype(jnp.bfloat16), "seq", -1).astype(grad_now.dtype)


def split_heads(rows_in):
    return rows_in.reshape(rows_in.shape[0], rows_in.shape[1] // HEAD_DIM, HEAD_DIM)


def score_block(query_rows, key_all, bias_all, allowed):
    scores = (
        jnp.einsum(
            "qhd,khd->hqk",
            split_heads(query_rows),
            split_heads(key_all),
            preferred_element_type=jnp.float32,
        )
        * HEAD_DIM ** (-0.5)
        + bias_all
    )
    return jnp.where(allowed[None], scores, masked_score)


def attend_forward(query_rows, key_all, value_all, bias_all, allowed):
    scores = score_block(query_rows, key_all, bias_all, allowed)
    row_max = jnp.max(scores, axis=-1, keepdims=True)
    exp_scores = jnp.exp(scores - row_max)
    row_total = jnp.sum(exp_scores, axis=-1, keepdims=True)
    weight_all = to_low(exp_scores / row_total)
    mixed_out = jnp.einsum(
        "hqk,khd->qhd", weight_all, split_heads(value_all), preferred_element_type=jnp.float32
    )
    return (
        to_low(mixed_out.reshape(query_rows.shape[0], -1)),
        (row_max + jnp.log(row_total))[..., 0],
    )


def attend_back(query_rows, key_all, value_all, bias_all, allowed, log_total, grad_mixed):
    scores = score_block(query_rows, key_all, bias_all, allowed)
    weight_all = jnp.where(allowed[None], jnp.exp(scores - log_total[..., None]), 0.0)
    grad_heads = split_heads(grad_mixed)
    grad_weight = jnp.einsum(
        "qhd,khd->hqk", grad_heads, split_heads(value_all), preferred_element_type=jnp.float32
    )
    row_inner = jnp.sum(weight_all * grad_weight, axis=-1, keepdims=True)
    grad_scores = to_low(weight_all * (grad_weight - row_inner))
    grad_query = jnp.einsum(
        "hqk,khd->qhd", grad_scores, split_heads(key_all), preferred_element_type=jnp.float32
    ) * HEAD_DIM ** (-0.5)
    grad_keys = jnp.einsum(
        "hqk,qhd->khd", grad_scores, split_heads(query_rows), preferred_element_type=jnp.float32
    ) * HEAD_DIM ** (-0.5)
    grad_values = jnp.einsum(
        "hqk,qhd->khd", to_low(weight_all), grad_heads, preferred_element_type=jnp.float32
    )
    return (
        grad_query.reshape(query_rows.shape[0], -1),
        grad_keys.reshape(key_all.shape[0], -1),
        grad_values.reshape(key_all.shape[0], -1),
        grad_scores,
    )


def bias_lookup(rel_bias, rel_table):
    table_heads = jnp.zeros((rel_bias.shape[1],) + rel_table.shape, jnp.float32)
    for bucket_id in range(BUCKETS):
        table_heads = table_heads + jnp.where(
            rel_table[None] == bucket_id, rel_bias[bucket_id][:, None, None], 0.0
        )
    return table_heads


def bias_sums(score_grad, rel_table):
    grad_wide = score_grad.astype(jnp.float32)
    columns = []
    for bucket_id in range(BUCKETS):
        columns.append(
            jnp.sum(jnp.where(rel_table[None, None] == bucket_id, grad_wide, 0.0), axis=(0, 2, 3))
        )
    return jnp.stack(columns, axis=0)


def body(
    inputs,
    seg_starts,
    lengths,
    init_state,
    attn_gain,
    state_gain,
    mlp_gain,
    w_query,
    w_key,
    w_value,
    w_out,
    w_squery,
    w_sout,
    w_up,
    w_down,
    rel_bias,
    gate_bias,
    out_cot,
    state_cot,
):
    seq_count = inputs.shape[0]
    chain_length = lax.axis_size("seq")
    block_index = lax.axis_index("seq")
    is_first = block_index == 0
    width_local = w_query.shape[1]
    head_count = width_local // HEAD_DIM
    gate_value = jax.nn.sigmoid(gate_bias)
    positions = jnp.arange(BLOCK)
    inputs_wide = inputs.astype(jnp.float32)
    tokens_low = gather_rows(to_low(layer_norm(inputs_wide, attn_gain)))
    query_tok = to_low(matmul(tokens_low, w_query))
    key_tok = to_low(matmul(tokens_low, w_key))
    value_tok = to_low(matmul(tokens_low, w_value))
    key_prev, value_prev = passed_along((key_tok, value_tok), "seq", 1)
    valid_keys = (block_index * BLOCK + positions)[None, :] < lengths[:, None]
    batched_attend = jax.vmap(attend_forward, in_axes=(0, 0, 0, None, 0))
    batched_back = jax.vmap(attend_back, in_axes=(0, 0, 0, None, 0, 0, 0))

    def state_forward(state_rows, key_blk, value_blk, valid_blk):
        state_low = lax.all_gather(
            to_low(layer_norm(state_rows, state_gain)), "tensor", axis=1, tiled=True
        )
        query_st = to_low(matmul(state_low, w_squery))
        key_st = to_low(matmul(state_low, w_key))
        value_st = to_low(matmul(state_low, w_value))
        key_all = jnp.concatenate([key_blk, key_st], axis=1)
        value_all = jnp.concatenate([value_blk, value_st], axis=1)
        mixed_st, lse_st = batched_attend(
            query_st, key_all, value_all, 0.0, state_mask_of(valid_blk)
        )
        update = lax.psum_scatter(
            matmul(mixed_st, w_sout).astype(jnp.bfloat16), "tensor", scatter_dimension=1, tiled=True
        ).astype(jnp.float32)
        state_next = gate_value * state_rows + (1.0 - gate_value) * update
        return (state_next, (state_low, query_st, key_st, value_st, mixed_st, lse_st, update))

    def state_backward(
        grad_out, state_rows, kept_one, key_blk, value_blk, valid_blk, extra_key, extra_value
    ):
        state_low, query_st, key_st, value_st, mixed_st, lse_st, update = kept_one
        gate_part = (
            jnp.sum(grad_out * (state_rows - update), axis=(0, 1)) * gate_value * (1.0 - gate_value)
        )
        grad_update = lax.all_gather(
            to_low((1.0 - gate_value) * grad_out), "tensor", axis=1, tiled=True
        )
        grad_mixed_st = to_low(matmul_t(grad_update, w_sout))
        sout_part = outer_sum(mixed_st, grad_update)
        key_all = jnp.concatenate([key_blk, key_st], axis=1)
        value_all = jnp.concatenate([value_blk, value_st], axis=1)
        grad_query_st, grad_keys_st, grad_values_st, _ = batched_back(
            query_st, key_all, value_all, 0.0, state_mask_of(valid_blk), lse_st, grad_mixed_st
        )
        query_low = to_low(grad_query_st)
        key_low = to_low(grad_keys_st[:, BLOCK:] + extra_key)
        value_low = to_low(grad_values_st[:, BLOCK:] + extra_value)
        squery_part = outer_sum(state_low, query_low)
        key_part = outer_sum(state_low, key_low)
        value_part = outer_sum(state_low, value_low)
        terms = (
            matmul_t(query_low, w_squery) + matmul_t(key_low, w_key) + matmul_t(value_low, w_value)
        )
        grad_normed = lax.psum_scatter(
            terms.astype(jnp.bfloat16), "tensor", scatter_dimension=1, tiled=True
        ).astype(jnp.float32)
        grad_rows_norm, gain_part = norm_back(state_rows, state_gain, grad_normed)
        grad_in = gate_value * grad_out + grad_rows_norm
        block_grads = (grad_keys_st[:, :BLOCK], grad_values_st[:, :BLOCK])
        return (
            grad_in,
            block_grads,
            (squery_part, key_part, value_part, sout_part, gain_part, gate_part),
        )

    zeros_rows = jnp.zeros((seq_count,) + init_state.shape, jnp.float32)
    narrow_zero = jnp.zeros((seq_count, STATES, width_local), jnp.bfloat16)
    stored_start = (
        zeros_rows,
        zeros_rows,
        jnp.zeros((seq_count, STATES, D), jnp.bfloat16),
        narrow_zero,
        narrow_zero,
        narrow_zero,
        narrow_zero,
        jnp.zeros((seq_count, head_count, STATES), jnp.float32),
        zeros_rows,
    )

    def forward_turn(turn_index, carry):
        incoming, stored_now = carry
        order_index = turn_index - block_index
        is_live = (order_index >= 0) & (order_index < seq_count)
        picked = jnp.clip(order_index, 0, seq_count - 1)
        rows_now = jnp.where(is_first, init_state[None], incoming)
        key_one = lax.dynamic_slice_in_dim(key_tok, picked, 1, 0)
        value_one = lax.dynamic_slice_in_dim(value_tok, picked, 1, 0)
        valid_one = lax.dynamic_slice_in_dim(valid_keys, picked, 1, 0)
        rows_next, kept_one = state_forward(rows_now, key_one, value_one, valid_one)
        fresh = (rows_now, rows_next) + kept_one
        stored_now = tuple(
            (
                jnp.where(
                    is_live,
                    lax.dynamic_update_slice_in_dim(whole_array, fresh_part, picked, 0),
                    whole_array,
                )
                for whole_array, fresh_part in zip(stored_now, fresh)
            )
        )
        return (pass_state(rows_next), stored_now)

    incoming_start = jnp.zeros((1,) + init_state.shape, jnp.float32)
    _, stored_all = lax.fori_loop(
        0, chain_length + seq_count - 1, forward_turn, (incoming_start, stored_start)
    )
    state_in = stored_all[0]
    state_out = stored_all[1]
    kept = stored_all[2:]
    key_all_tok = jnp.concatenate([key_prev, key_tok, kept[2]], axis=1)
    value_all_tok = jnp.concatenate([value_prev, value_tok, kept[3]], axis=1)
    allowed_tok = jax.vmap(token_mask, in_axes=(0, 0, None))(seg_starts[:, 0], lengths, block_index)
    rel_table = bucket_of((jnp.arange(2 * BLOCK) - BLOCK)[None, :] - positions[:, None])
    full_bias = jnp.concatenate(
        [bias_lookup(rel_bias, rel_table), jnp.zeros((head_count, BLOCK, STATES), jnp.float32)],
        axis=2,
    )
    mixed_tok, lse_tok = batched_attend(
        query_tok, key_all_tok, value_all_tok, full_bias, allowed_tok
    )
    hidden_in = inputs_wide + sum_rows(matmul(mixed_tok, w_out))
    mid_low = gather_rows(to_low(layer_norm(hidden_in, mlp_gain)))
    pre_act = matmul(mid_low, w_up)
    hidden_low = to_low(jax.nn.gelu(pre_act))
    mlp_rows = sum_rows(matmul(hidden_low, w_down))
    tokens_out = (hidden_in + mlp_rows).astype(jnp.bfloat16)
    cot_wide = out_cot.astype(jnp.float32)
    cot_used = gather_rows(out_cot)
    grad_hidden_act = matmul_t(cot_used, w_down)
    down_grad = outer_sum(hidden_low, cot_used)
    grad_pre = to_low(gelu_back(pre_act, grad_hidden_act))
    up_grad = outer_sum(mid_low, grad_pre)
    grad_normed_mid = sum_rows(matmul_t(grad_pre, w_up))
    grad_mid_in, mlp_gain_grad = norm_back(hidden_in, mlp_gain, grad_normed_mid)
    grad_hidden = cot_wide + grad_mid_in
    grad_attn_low = gather_rows(to_low(grad_hidden))
    grad_mixed = to_low(matmul_t(grad_attn_low, w_out))
    out_grad = outer_sum(mixed_tok, grad_attn_low)
    grad_query_tok, grad_keys_tok, grad_values_tok, grad_scores = batched_back(
        query_tok, key_all_tok, value_all_tok, full_bias, allowed_tok, lse_tok, grad_mixed
    )
    bias_grad = bias_sums(grad_scores[..., : 2 * BLOCK], rel_table)
    grad_key_next, grad_value_next = (
        passed_along(grad_keys_tok[:, :BLOCK].astype(jnp.bfloat16), "seq", -1).astype(jnp.float32),
        passed_along(grad_values_tok[:, :BLOCK].astype(jnp.bfloat16), "seq", -1).astype(
            jnp.float32
        ),
    )
    grad_key_own = grad_keys_tok[:, BLOCK : 2 * BLOCK] + grad_key_next
    grad_value_own = grad_values_tok[:, BLOCK : 2 * BLOCK] + grad_value_next
    grad_key_st_tok = grad_keys_tok[:, 2 * BLOCK :]
    grad_value_st_tok = grad_values_tok[:, 2 * BLOCK :]
    cot_rows = state_cot[:, 0].astype(jnp.float32)
    wide_zero = jnp.zeros((seq_count, BLOCK, width_local), jnp.float32)
    stored_back = (zeros_rows, wide_zero, wide_zero)
    totals_start = (
        jnp.zeros((D, width_local), jnp.float32),
        jnp.zeros((D, width_local), jnp.float32),
        jnp.zeros((D, width_local), jnp.float32),
        jnp.zeros((width_local, D), jnp.float32),
        jnp.zeros((D,), jnp.float32),
        jnp.zeros((D,), jnp.float32),
    )

    def backward_turn(turn_index, carry):
        incoming, stored_now, totals_now = carry
        order_index = turn_index - (chain_length - 1 - block_index)
        is_live = (order_index >= 0) & (order_index < seq_count)
        picked = jnp.clip(order_index, 0, seq_count - 1)

        def slice_one(whole_array):
            return lax.dynamic_slice_in_dim(whole_array, picked, 1, 0)

        grad_out = slice_one(cot_rows) + incoming
        kept_one = tuple((slice_one(kept_array) for kept_array in kept))
        grad_in, block_one, parts_one = state_backward(
            grad_out,
            slice_one(state_in),
            kept_one,
            slice_one(key_tok),
            slice_one(value_tok),
            slice_one(valid_keys),
            slice_one(grad_key_st_tok),
            slice_one(grad_value_st_tok),
        )
        fresh = (grad_in,) + block_one
        stored_now = tuple(
            (
                jnp.where(
                    is_live,
                    lax.dynamic_update_slice_in_dim(whole_array, fresh_part, picked, 0),
                    whole_array,
                )
                for whole_array, fresh_part in zip(stored_now, fresh)
            )
        )
        totals_now = tuple(
            (
                total_now + jnp.where(is_live, part_now, 0.0)
                for total_now, part_now in zip(totals_now, parts_one)
            )
        )
        return (pass_back(grad_in), stored_now, totals_now)

    incoming_start = jnp.zeros((1,) + init_state.shape, jnp.float32)
    _, stored_done, weight_parts = lax.fori_loop(
        0, chain_length + seq_count - 1, backward_turn, (incoming_start, stored_back, totals_start)
    )
    grad_in_all, grad_key_blk, grad_value_blk = stored_done
    query_low = to_low(grad_query_tok)
    key_low = to_low(grad_key_own + grad_key_blk)
    value_low = to_low(grad_value_own + grad_value_blk)
    query_grad = outer_sum(tokens_low, query_low)
    key_grad = outer_sum(tokens_low, key_low) + weight_parts[1]
    value_grad = outer_sum(tokens_low, value_low) + weight_parts[2]
    grad_tokens = sum_rows(
        matmul_t(query_low, w_query) + matmul_t(key_low, w_key) + matmul_t(value_low, w_value)
    )
    grad_in_norm, attn_gain_grad = norm_back(inputs_wide, attn_gain, grad_tokens)
    inputs_grad = grad_hidden + grad_in_norm
    state_part = jnp.where(is_first, jnp.sum(grad_in_all, axis=0), 0.0)
    gains = lax.psum(
        jnp.stack([attn_gain_grad, weight_parts[4], mlp_gain_grad, weight_parts[5]]), "tensor"
    )
    totals = (
        lax.psum(query_grad.astype(jnp.bfloat16), ("dp", "seq")).astype(jnp.float32),
        lax.psum(key_grad.astype(jnp.bfloat16), ("dp", "seq")).astype(jnp.float32),
        lax.psum(value_grad.astype(jnp.bfloat16), ("dp", "seq")).astype(jnp.float32),
        lax.psum(out_grad.astype(jnp.bfloat16), ("dp", "seq")).astype(jnp.float32),
        lax.psum(weight_parts[0].astype(jnp.bfloat16), ("dp", "seq")).astype(jnp.float32),
        lax.psum(weight_parts[3].astype(jnp.bfloat16), ("dp", "seq")).astype(jnp.float32),
        lax.psum(up_grad.astype(jnp.bfloat16), ("dp", "seq")).astype(jnp.float32),
        lax.psum(down_grad.astype(jnp.bfloat16), ("dp", "seq")).astype(jnp.float32),
        lax.psum(bias_grad.astype(jnp.bfloat16), ("dp", "seq")).astype(jnp.float32),
        lax.psum(state_part.astype(jnp.bfloat16), ("dp", "seq")).astype(jnp.float32),
        lax.psum(gains.astype(jnp.bfloat16), ("dp", "seq")).astype(jnp.float32),
    )
    gain_total = totals[10]
    return (
        tokens_out,
        state_out[:, None],
        inputs_grad,
        totals[9],
        gain_total[0],
        gain_total[1],
        gain_total[2],
        totals[0],
        totals[1],
        totals[2],
        totals[3],
        totals[4],
        totals[5],
        totals[6],
        totals[7],
        totals[8],
        gain_total[3],
    )


def chosen_body(mesh):
    if mesh.shape["seq"] == 4 and mesh.shape["tensor"] == 4:
        return line_body
    return body


MESH_ID = pl.DeviceIdType.MESH
ROWS = 128
CHUNKS = BLOCK // ROWS
LINE = 8
SCALE = HEAD_DIM ** (-0.5)
VMEM_LIMIT = 60 * 1024 * 1024


def dot_nn(left, right):
    return lax.dot_general(left, right, (((1,), (0,)), ((), ())), preferred_element_type=jnp.float32)


def dot_nt(left, right):
    return lax.dot_general(left, right, (((1,), (1,)), ((), ())), preferred_element_type=jnp.float32)


def dot_tn(left, right):
    return lax.dot_general(left, right, (((0,), (0,)), ((), ())), preferred_element_type=jnp.float32)


def line_place():
    place = lax.axis_index("seq")
    half = lax.rem(place, 2)
    rank = lax.axis_index("tensor")
    return place, half, rank


def span(index, size):
    return pl.ds(pl.multiple_of(index * size, size), size)


def fetch_pieces(kept, first, rows, target, sem):
    for owner in range(8):
        pltpu.make_async_copy(
            kept.at[owner, :, pl.ds(first, rows), :], target.at[:, owner], sem
        ).start()


def fetch_columns(weights, target, sem):
    half = lax.rem(lax.axis_index("seq"), 2)
    for index, weight in enumerate(weights):
        pltpu.make_async_copy(
            weight.at[:, span(half, 128)], target.at[:, pl.ds(128 * index, 128)], sem
        ).start()


def fetched(target, sem):
    pltpu.make_async_copy(target, target, sem).wait()


def norm_parts(rows):
    centered = rows - jnp.mean(rows, axis=-1, keepdims=True)
    spread = jnp.mean(centered * centered, axis=-1, keepdims=True)
    return centered, lax.rsqrt(spread + norm_eps)


def mark(marks, block_id, row):
    return marks[block_id, pl.ds(row, 1), 0:1]


def sequence_marks(marks, block_id):
    mine = lax.axis_index("seq") // 2
    return mark(marks, block_id, mine), mark(marks, 0, 2 + mine)


def token_masks(marks, block_id, first_row):
    start, length = sequence_marks(marks, block_id)
    row = lax.broadcasted_iota(jnp.int32, (ROWS, BLOCK), 0) + first_row
    col = lax.broadcasted_iota(jnp.int32, (ROWS, BLOCK), 1)
    prev_limit = jnp.where(block_id > 0, length - (block_id - 1) * BLOCK, 0)
    prev_ok = (col > row) & (col < prev_limit)
    row_in = (row >= start) & (row < start + SEG)
    col_in = (col >= start) & (col < start + SEG)
    cur_ok = ((col <= row) | (row_in & col_in)) & (col < length - block_id * BLOCK)
    return prev_ok, cur_ok


def state_block_mask(marks, block_id):
    _, length = sequence_marks(marks, block_id)
    col = lax.broadcasted_iota(jnp.int32, (ROWS, BLOCK), 1)
    return col < length - block_id * BLOCK


def softmax_of(score_parts):
    top = jnp.max(score_parts[0], axis=-1, keepdims=True)
    for part in score_parts[1:]:
        top = jnp.maximum(top, jnp.max(part, axis=-1, keepdims=True))
    raised = [jnp.exp(part - top) for part in score_parts]
    total = jnp.sum(raised[0], axis=-1, keepdims=True)
    for part in raised[1:]:
        total = total + jnp.sum(part, axis=-1, keepdims=True)
    inverse = 1.0 / total
    return [to_low(part * inverse) for part in raised], top + jnp.log(total)


def token_scores(scal, qkv, qkvst, bias, block_id, chunk):
    rows = span(chunk, ROWS)
    prev_id = jnp.maximum(block_id - 1, 0)
    query = qkv[block_id, rows, 0:128]
    prev_ok, cur_ok = token_masks(scal, block_id, chunk * ROWS)
    prev = dot_nt(query, qkv[prev_id, :, 128:256]) * SCALE + bias[rows, 0:BLOCK]
    cur = dot_nt(query, qkv[block_id, :, 128:256]) * SCALE + bias[rows, BLOCK : 2 * BLOCK]
    stt = dot_nt(query, qkvst[block_id, :, 128:256]) * SCALE
    prev = jnp.where(prev_ok, prev, masked_score)
    cur = jnp.where(cur_ok, cur, masked_score)
    return query, (prev, cur, stt)


def state_scores(scal, qkv, qkvst, block_id, chunk):
    query = qkvst[block_id, span(chunk, ROWS), 0:128]
    tok = dot_nt(query, qkv[block_id, :, 128:256]) * SCALE
    tok = jnp.where(state_block_mask(scal, block_id), tok, masked_score)
    stt = dot_nt(query, qkvst[block_id, :, 128:256]) * SCALE
    return query, (tok, stt)


HALVES = 2
HALF_ROWS = STATES // HALVES
HALF_CHUNKS = HALF_ROWS // ROWS


def forward_kernel(
    marks, qkv, kept, w_squery, w_qkv, vecs, bias, state_cot, back_own,
    o_out, lse_out, state_rows, low_out, qkvst, lse_st, os_rows, cots, back,
    held, os_all, state_low, w_sout, start, w_state,
    way_send, core_send, recv_sem, local_sem, low_sem, cot_send, cot_recv,
    piece_send, piece_recv, ring_send, ring_recv,
):
    side, place, half, rank = plane_place()
    me = plane_index(side, place)
    partner = place + 1 - 2 * half
    head = 2 * rank + half
    fetch_pieces(kept, 32, 16, start, local_sem.at[0])
    fetch_columns((w_squery,), w_state, local_sem.at[2])
    fetch_pieces(kept, 0, 32, w_sout, local_sem.at[1])
    own_cot = pltpu.make_async_copy(state_cot.at[place], cots.at[place], local_sem.at[4])
    own_cot.start()
    own_piece = pltpu.make_async_copy(back_own, back.at[me, rank], local_sem.at[3])
    own_piece.start()
    ranks = [lax.rem(rank + step, 4) for step in (1, 2, 3)]
    seats = [lax.rem(place + step, 4) for step in (1, 2, 3)]
    barrier = pltpu.get_barrier_semaphore()
    for target in [{"tensor": one} for one in ranks] + [{"seq": one} for one in seats] + [
        {"dp": 1 - side}
    ]:
        pl.semaphore_signal(barrier, inc=1, device_id=target, device_id_type=MESH_ID)
    fetched(start, local_sem.at[0])
    held[...] = start[...].reshape(STATES, D).astype(jnp.float32)
    gain = vecs[0:1, :]
    gate = vecs[1:2, :]
    fetched(w_state, local_sem.at[2])

    def project(block_id, part):
        def one(chunk, _):
            rows = span(chunk, ROWS)
            centered, scale = norm_parts(held[rows, :])
            low = to_low(centered * scale * gain)
            state_low[block_id, rows, :] = low
            qkvst[block_id, rows, 0:128] = to_low(dot_nn(low, w_state[...]))
            qkvst[block_id, rows, 128:384] = to_low(dot_nn(low, w_qkv[:, 128:384]))
            return 0

        lax.fori_loop(HALF_CHUNKS * part, HALF_CHUNKS * (part + 1), one, 0)

    pl.semaphore_wait(barrier, 7)

    def piece_move(origin, part, slot, target):
        return pltpu.make_async_remote_copy(
            src_ref=back_own.at[part],
            dst_ref=back.at[me, origin, part],
            send_sem=piece_send.at[part, slot],
            recv_sem=piece_recv.at[part, origin],
            device_id={"tensor": target},
            device_id_type=MESH_ID,
        )

    def send_piece(part):
        for slot, target in enumerate(ranks):
            piece_move(rank, part, slot, target).start()

    gather = plane_gather(
        lambda owner, part: back.at[owner, pl.ds(2 * part, 2)], ring_send, ring_recv
    )
    next(gather)
    send_piece(0)
    for part in range(HALVES):
        project(0, part)
    right, left = {"tensor": lax.rem(rank + 1, 4)}, {"tensor": lax.rem(rank + 3, 4)}

    def moved(block_id, part, which, sem, target):
        view = os_all.at[block_id, pl.ds(HALF_ROWS * part, HALF_ROWS), span(which, 128)]
        return pltpu.make_async_remote_copy(
            src_ref=view,
            dst_ref=view,
            send_sem=sem,
            recv_sem=recv_sem.at[block_id, part, which],
            device_id=target,
            device_id_type=MESH_ID,
        )

    def cot_move(index, origin, slot, target):
        return pltpu.make_async_remote_copy(
            src_ref=state_cot.at[index],
            dst_ref=cots.at[origin],
            send_sem=cot_send.at[slot],
            recv_sem=cot_recv.at[origin],
            device_id={"seq": target},
            device_id_type=MESH_ID,
        )

    for slot, target in enumerate(seats):
        cot_move(target, place, slot, target).start()
    fetched(w_sout, local_sem.at[1])

    def origin_of(way, distance):
        if way == 0:
            return jnp.maximum(rank - distance, 0)
        return jnp.minimum(rank + distance, 3)

    def ways(distance):
        return (
            (0, rank >= distance, (rank >= distance) & (rank < 3), right),
            (1, rank + distance <= 3, (rank + distance <= 3) & (rank > 0), left),
        )

    def relay(block_id, part, distance, waiting):
        for way, comes, goes, target in ways(distance):
            which = 2 * origin_of(way, distance) + half
            sem = way_send.at[block_id, part, min(distance, 2), way]
            core_sem = core_send.at[block_id, part, which // 2]
            if distance > 0:

                @pl.when(comes)
                def _():
                    to_core = moved(block_id, part, which, core_sem, {"seq": partner})
                    if waiting:
                        moved(block_id, part, which, sem, target).wait_recv()
                        to_core.start()
                    else:
                        to_core.wait_send()

            if distance < 3:

                @pl.when(goes)
                def _():
                    one = moved(block_id, part, which, sem, target)
                    if waiting:
                        one.start()
                    else:
                        one.wait_send()

        if distance == 0:
            mine = moved(
                block_id, part, head, core_send.at[block_id, part, rank], {"seq": partner}
            )
            if waiting:
                mine.start()
            else:
                mine.wait_send()

    def one_block(block_id, _):
        def attend_state(chunk, _):
            rows = span(chunk, ROWS)
            _, parts = state_scores(marks, qkv, qkvst, block_id, chunk)
            (w_tok, w_stt), total = softmax_of(parts)
            mixed = dot_nn(w_tok, qkv[block_id, :, 256:384]) + dot_nn(
                w_stt, qkvst[block_id, :, 256:384]
            )
            os_all[block_id, rows, span(head, 128)] = to_low(mixed)
            lse_st[block_id, rows, :] = total
            return 0

        def attend_token(chunk, _):
            rows = span(chunk, ROWS)
            _, parts = token_scores(marks, qkv, qkvst, bias, block_id, chunk)
            weights, total = softmax_of(parts)
            prev_id = jnp.maximum(block_id - 1, 0)
            mixed = (
                dot_nn(weights[0], qkv[prev_id, :, 256:384])
                + dot_nn(weights[1], qkv[block_id, :, 256:384])
                + dot_nn(weights[2], qkvst[block_id, :, 256:384])
            )
            o_out[block_id, rows, :] = to_low(mixed)
            lse_out[block_id, rows, :] = total
            return 0

        def attend_both(part, _):
            lax.fori_loop(HALF_CHUNKS * part, HALF_CHUNKS * (part + 1), attend_state, 0)
            for value in range(HALVES):

                @pl.when(part == value)
                def _():
                    relay(block_id, value, 0, True)

            return 0

        lax.fori_loop(0, HALVES, attend_both, 0)
        pltpu.make_async_copy(
            state_low.at[block_id], low_out.at[block_id], low_sem.at[block_id]
        ).start()

        @pl.when(block_id == 2)
        def _():
            own_piece.wait()
            for part in range(3):
                for slot, target in enumerate(ranks):
                    piece_move(target, part, slot, target).wait_recv()
            next(gather)

        @pl.when(block_id == 3)
        def _():
            next(gather)
            next(gather)

        def between(step, _):
            for value, (distance, part) in enumerate(((1, 0), (1, 1), (2, 0), (2, 1))):

                @pl.when(step == value)
                def _():
                    relay(block_id, part, distance, True)

            return attend_token(step, 0)

        lax.fori_loop(0, 4, between, 0)

        def settle(part, _):
            for value in range(HALVES):

                @pl.when(part == value)
                def _():
                    relay(block_id, value, 3, True)
                    for origin in range(4):
                        moved(
                            block_id, value, 2 * origin + 1 - half,
                            core_send.at[block_id, value, origin], {"seq": partner},
                        ).wait_recv()

                    if value == HALVES - 1:
                        for turn in (0, 1):

                            @pl.when(block_id == turn)
                            def _():
                                send_piece(turn + 1)

            def update(chunk, _):
                rows = span(chunk, ROWS)
                change = dot_nn(os_all[block_id, rows, :], w_sout[...].reshape(D, D))
                held[rows, :] = gate * held[rows, :] + (1.0 - gate) * change
                return 0

            lax.fori_loop(HALF_CHUNKS * part, HALF_CHUNKS * (part + 1), update, 0)

            @pl.when(block_id < 3)
            def _():
                project(block_id + 1, part)

            return 0

        lax.fori_loop(0, HALVES, settle, 0)
        state_rows[block_id] = held[span(rank, 128), :]
        os_rows[block_id] = os_all[block_id, span(head, 64), :]
        return 0

    lax.fori_loop(0, 4, one_block, 0)

    def drain(block_id, _):
        for part in range(HALVES):
            for distance in range(4):
                relay(block_id, part, distance, False)
        pltpu.make_async_copy(
            state_low.at[block_id], low_out.at[block_id], low_sem.at[block_id]
        ).wait()
        return 0

    lax.fori_loop(0, 4, drain, 0)
    own_cot.wait()
    for part in range(3):
        for slot, target in enumerate(ranks):
            piece_move(rank, part, slot, target).wait_send()
    for _ in gather:
        pass
    for slot, target in enumerate(seats):
        cot_move(target, place, slot, target).wait_send()
        cot_move(place, target, slot, target).wait_recv()


def any_specs(count):
    return [pl.BlockSpec(memory_space=pl.ANY)] * count


def vmem_specs(count):
    return [pl.BlockSpec(memory_space=pltpu.VMEM)] * count


def forward_chain(
    marks, qkv, kept, w_squery, w_qkv, vecs, bias, state_cot, back_own
):
    low, wide = jnp.bfloat16, jnp.float32
    shapes = (
        ((4, BLOCK, 128), low),
        ((4, BLOCK, 1), wide),
        ((4, 128, D), wide),
        ((4, STATES, D), low),
        ((4, STATES, 384), low),
        ((4, STATES, 1), wide),
        ((4, 64, D), low),
        ((4, 64, D), low),
        ((8, 4, 3, 32, D), low),
    )
    dma = pltpu.SemaphoreType.DMA
    return pl.pallas_call(
        forward_kernel,
        out_shape=[jax.ShapeDtypeStruct(*one) for one in shapes],
        in_specs=vmem_specs(2) + any_specs(2) + vmem_specs(3) + any_specs(2),
        out_specs=vmem_specs(3) + any_specs(1) + vmem_specs(3) + any_specs(2),
        scratch_shapes=[
            pltpu.VMEM((STATES, D), wide),
            pltpu.VMEM((4, STATES, D), low),
            pltpu.VMEM((4, STATES, D), low),
            pltpu.VMEM((4, 8, 32, D), low),
            pltpu.VMEM((4, 8, 16, D), low),
            pltpu.VMEM((D, 128), low),
            dma((4, HALVES, 3, 2)),
            dma((4, HALVES, 4)),
            dma((4, HALVES, 8)),
            dma((5,)),
            dma((4,)),
            dma((3,)),
            dma((4,)),
            dma((3, 3)),
            dma((3, 4)),
            dma((14,)),
            dma((8, 2)),
        ],
        compiler_params=pltpu.CompilerParams(
            collective_id=1, has_side_effects=True, vmem_limit_bytes=VMEM_LIMIT
        ),
        cost_estimate=pl.CostEstimate(
            flops=60000000000, bytes_accessed=60000000, transcendentals=0
        ),
        name="forward_chain",
    )(marks, qkv, kept, w_squery, w_qkv, vecs, bias, state_cot, back_own)


def backward_kernel(
    scal, qkv, d_o, lse_tok, qkvst, lse_st, state_rows, begin, cots, back, kept, vecs, bias,
    extra, hidden,
    d_qkv, d_qkvst, du_rows, d_start, sums, dz_sum, state_out, tokens_out, out_part,
    key_acc, value_acc, st_key, st_value, dos_rows, dos_got, d_got, grad_in,
    states, w_back, w_sout, work, core_got, near_got, far_got, total,
    send_sem, recv_sem, local_sem, side_sem, ring_send, ring_recv,
):
    place, half, rank = line_place()
    own_rows = pl.ds(pl.multiple_of(half * 64, 64), 64)
    loads = [
        pltpu.make_async_copy(
            state_rows.at[:, own_rows, :], states.at[pl.ds(1, 4)], local_sem.at[0]
        ),
        pltpu.make_async_copy(
            state_rows.at[place], state_out.at[place // 2], local_sem.at[3]
        ),
        pltpu.make_async_copy(extra, work, local_sem.at[4]),
    ]
    for one in loads:
        one.start()
    fetch_pieces(kept, 0, 32, w_sout, local_sem.at[1])
    for owner in range(8):
        pltpu.make_async_copy(
            back.at[owner], w_back.at[:, owner // 4, :, owner % 4], local_sem.at[2]
        ).start()
    states[0] = to_low(begin[own_rows, :]).astype(jnp.float32)
    head = 2 * rank + half
    peers = []
    for step in range(1, LINE):
        other = lax.rem(head + step, LINE)
        peers.append((other, place - half + lax.rem(other, 2), other // 2))
    barrier = pltpu.get_barrier_semaphore()
    for _, seq_to, rank_to in peers:
        pl.semaphore_signal(
            barrier, inc=1, device_id={"seq": seq_to, "tensor": rank_to}, device_id_type=MESH_ID
        )
    beside = lax.rem(place + 2, 4)
    pl.semaphore_signal(barrier, inc=1, device_id={"seq": beside}, device_id_type=MESH_ID)
    pl.semaphore_signal(
        barrier, inc=1, device_id={"dp": 1 - lax.axis_index("dp")}, device_id_type=MESH_ID
    )
    plane_steps = plane_scatter(
        work, core_got, near_got, far_got, total, 384, ring_send, ring_recv
    )
    next(plane_steps)

    def aside(block_id, row_set):
        return pltpu.make_async_remote_copy(
            src_ref=state_rows.at[block_id],
            dst_ref=state_out.at[row_set],
            send_sem=side_sem.at[0],
            recv_sem=side_sem.at[1],
            device_id={"seq": beside},
            device_id_type=MESH_ID,
        )

    gain = vecs[0:1, :]
    gate = vecs[1:2, :]
    key_acc[...] = jnp.zeros_like(key_acc)
    value_acc[...] = jnp.zeros_like(value_acc)
    dz_sum[...] = jnp.zeros_like(dz_sum)
    sums[...] = jnp.zeros_like(sums)
    grad_in[...] = jnp.zeros_like(grad_in)

    def back_parts(parts, total, grad, values):
        weights = [jnp.exp(part - total) for part in parts]
        d_weights = [dot_nt(grad, value) for value in values]
        inner = jnp.sum(weights[0] * d_weights[0], axis=-1, keepdims=True)
        for one, other in zip(weights[1:], d_weights[1:]):
            inner = inner + jnp.sum(one * other, axis=-1, keepdims=True)
        d_scores = [to_low(one * (other - inner)) for one, other in zip(weights, d_weights)]
        return [to_low(one) for one in weights], d_scores

    def token_back(block_id):
        prev_id = jnp.maximum(block_id - 1, 0)
        st_key[...] = jnp.zeros_like(st_key)
        st_value[...] = jnp.zeros_like(st_value)

        def one_chunk(chunk, _):
            rows = span(chunk, ROWS)
            query, parts = token_scores(scal, qkv, qkvst, bias, block_id, chunk)
            grad = d_o[block_id, rows, :]
            keys = (qkv[prev_id, :, 128:256], qkv[block_id, :, 128:256], qkvst[block_id, :, 128:256])
            values = (
                qkv[prev_id, :, 256:384], qkv[block_id, :, 256:384], qkvst[block_id, :, 256:384]
            )
            weights, d_scores = back_parts(parts, lse_tok[block_id, rows, :], grad, values)
            d_query = dot_nn(d_scores[0], keys[0])
            d_query = d_query + dot_nn(d_scores[1], keys[1]) + dot_nn(d_scores[2], keys[2])
            d_qkv[block_id, rows, 0:128] = to_low(d_query * SCALE)
            key_acc[prev_id] += dot_tn(d_scores[0], query) * SCALE
            value_acc[prev_id] += dot_tn(weights[0], grad)
            key_acc[block_id] += dot_tn(d_scores[1], query) * SCALE
            value_acc[block_id] += dot_tn(weights[1], grad)
            st_key[...] += dot_tn(d_scores[2], query) * SCALE
            st_value[...] += dot_tn(weights[2], grad)
            dz_sum[rows, 0:BLOCK] += d_scores[0].astype(jnp.float32)
            dz_sum[rows, BLOCK : 2 * BLOCK] += d_scores[1].astype(jnp.float32)
            return 0

        lax.fori_loop(0, CHUNKS, one_chunk, 0)

    token_back(3)
    pl.semaphore_wait(barrier, LINE + 1)
    aside(beside, place // 2).start()
    loads[2].wait()
    loads[0].wait()
    fetched(w_sout, local_sem.at[1])
    fetched(w_back, local_sem.at[2])

    def mixed_copy(block_id, slot, sender, other, seq_to, rank_to):
        return pltpu.make_async_remote_copy(
            src_ref=dos_rows.at[block_id, :, span(other, 128)],
            dst_ref=dos_got.at[block_id, span(sender, 64), :],
            send_sem=send_sem.at[0, block_id, slot],
            recv_sem=recv_sem.at[0, block_id, sender],
            device_id={"seq": seq_to, "tensor": rank_to},
            device_id_type=MESH_ID,
        )

    def grads_copy(block_id, slot, sender, other, seq_to, rank_to):
        return pltpu.make_async_remote_copy(
            src_ref=d_qkvst.at[block_id, span(other, 64), :],
            dst_ref=d_got.at[block_id, sender],
            send_sem=send_sem.at[1, block_id, slot],
            recv_sem=recv_sem.at[1, block_id, sender],
            device_id={"seq": seq_to, "tensor": rank_to},
            device_id_type=MESH_ID,
        )

    def one_block(turn, _):
        block_id = 3 - turn
        grad_out = grad_in[...] + cots[block_id].astype(jnp.float32)
        sums[0:1, :] += jnp.sum(
            grad_out * (states[block_id] - states[block_id + 1]), axis=0, keepdims=True
        ) * gate
        change = to_low((1.0 - gate) * grad_out)
        du_rows[block_id] = change
        dos_rows[block_id] = to_low(dot_nt(change, w_sout[...].reshape(D, D)))
        for slot, (other, seq_to, rank_to) in enumerate(peers):
            mixed_copy(block_id, slot, head, other, seq_to, rank_to).start()
        dos_got[block_id, span(head, 64), :] = dos_rows[block_id, :, span(head, 128)]
        for slot, (other, seq_to, rank_to) in enumerate(peers):
            mixed_copy(block_id, slot, other, other, seq_to, rank_to).wait_recv()

        def one_chunk(chunk, _):
            rows = span(chunk, ROWS)
            query, parts = state_scores(scal, qkv, qkvst, block_id, chunk)
            grad = dos_got[block_id, rows, :]
            keys = (qkv[block_id, :, 128:256], qkvst[block_id, :, 128:256])
            values = (qkv[block_id, :, 256:384], qkvst[block_id, :, 256:384])
            weights, d_scores = back_parts(parts, lse_st[block_id, rows, :], grad, values)
            d_query = dot_nn(d_scores[0], keys[0]) + dot_nn(d_scores[1], keys[1])
            d_qkvst[block_id, rows, 0:128] = to_low(d_query * SCALE)
            key_acc[block_id] += dot_tn(d_scores[0], query) * SCALE
            value_acc[block_id] += dot_tn(weights[0], grad)
            st_key[...] += dot_tn(d_scores[1], query) * SCALE
            st_value[...] += dot_tn(weights[1], grad)
            return 0

        lax.fori_loop(0, CHUNKS, one_chunk, 0)
        d_qkvst[block_id, :, 128:256] = to_low(st_key[...])
        d_qkvst[block_id, :, 256:384] = to_low(st_value[...])
        for slot, (other, seq_to, rank_to) in enumerate(peers):
            grads_copy(block_id, slot, head, other, seq_to, rank_to).start()
        d_got[block_id, head] = d_qkvst[block_id, span(head, 64), :]

        for step in range(4):

            @pl.when(turn == step)
            def _():
                next(plane_steps, None)

        @pl.when(turn < 3)
        def _():
            token_back(block_id - 1)

        d_qkv[block_id, :, 128:256] = to_low(key_acc[block_id])
        d_qkv[block_id, :, 256:384] = to_low(value_acc[block_id])
        for slot, (other, seq_to, rank_to) in enumerate(peers):
            grads_copy(block_id, slot, other, other, seq_to, rank_to).wait_recv()
        d_low = dot_nn(d_got[block_id, 0], w_back[0, 0].reshape(384, D))
        for other in range(1, LINE):
            d_low = d_low + dot_nn(
                d_got[block_id, other], w_back[other // 2, other % 2].reshape(384, D)
            )
        centered, scale = norm_parts(states[block_id])
        normed = centered * scale
        sums[1:2, :] += jnp.sum(d_low * normed, axis=0, keepdims=True)
        lifted = d_low * gain
        grad_in[...] = gate * grad_out + scale * (
            lifted
            - jnp.mean(lifted, axis=-1, keepdims=True)
            - normed * jnp.mean(lifted * normed, axis=-1, keepdims=True)
        )
        return 0

    lax.fori_loop(0, 4, one_block, 0)
    d_start[...] = grad_in[...]

    def drain(block_id, _):
        for slot, (other, seq_to, rank_to) in enumerate(peers):
            mixed_copy(block_id, slot, head, other, seq_to, rank_to).wait_send()
            grads_copy(block_id, slot, head, other, seq_to, rank_to).wait_send()
        return 0

    lax.fori_loop(0, 4, drain, 0)
    for _ in plane_steps:
        pass
    for which in range(2):
        rows = pl.ds(128 * which, 128)
        tokens_out[which] = to_low(hidden[which] + total[rows, :])
    out_part[...] = to_low(total[256:384, :])
    loads[1].wait()
    aside(beside, place // 2).wait_send()
    aside(place, 1 - place // 2).wait_recv()


def backward_chain(
    scal, qkv, d_o, lse_tok, qkvst, lse_st, state_rows, begin, cots, back, kept, vecs, bias,
    extra, hidden,
):
    low, wide = jnp.bfloat16, jnp.float32
    shapes = (
        ((4, BLOCK, 384), low),
        ((4, STATES, 384), low),
        ((4, 64, D), low),
        ((64, D), wide),
        ((8, D), wide),
        ((BLOCK, 2 * BLOCK), wide),
        ((2, 128, D), wide),
        ((2, 128, D), low),
        ((128, D), low),
    )
    return pl.pallas_call(
        backward_kernel,
        out_shape=[jax.ShapeDtypeStruct(*one) for one in shapes],
        in_specs=vmem_specs(6)
        + any_specs(1)
        + vmem_specs(2)
        + any_specs(2)
        + vmem_specs(2)
        + any_specs(1)
        + vmem_specs(1),
        out_specs=vmem_specs(6) + any_specs(1) + vmem_specs(2),
        scratch_shapes=[
            pltpu.VMEM((4, BLOCK, 128), wide),
            pltpu.VMEM((4, BLOCK, 128), wide),
            pltpu.VMEM((STATES, 128), wide),
            pltpu.VMEM((STATES, 128), wide),
            pltpu.VMEM((4, 64, D), low),
            pltpu.VMEM((4, STATES, 128), low),
            pltpu.VMEM((4, LINE, 64, 384), low),
            pltpu.VMEM((64, D), wide),
            pltpu.VMEM((5, 64, D), wide),
            pltpu.VMEM((4, 2, 3, 4, 32, D), low),
            pltpu.VMEM((4, 8, 32, D), low),
            pltpu.VMEM((8, 384, D), low),
            pltpu.VMEM((4, 384, D), low),
            pltpu.VMEM((4, 192, D), low),
            pltpu.VMEM((2, 192, D), low),
            pltpu.VMEM((384, D), wide),
            pltpu.SemaphoreType.DMA((2, 4, LINE - 1)),
            pltpu.SemaphoreType.DMA((2, 4, LINE)),
            pltpu.SemaphoreType.DMA((5,)),
            pltpu.SemaphoreType.DMA((2,)),
            pltpu.SemaphoreType.DMA((10,)),
            pltpu.SemaphoreType.DMA((10,)),
        ],
        compiler_params=pltpu.CompilerParams(
            collective_id=2, has_side_effects=True, vmem_limit_bytes=VMEM_LIMIT
        ),
        cost_estimate=pl.CostEstimate(flops=40000000000, bytes_accessed=40000000, transcendentals=0),
        name="backward_chain",
    )(
        scal, qkv, d_o, lse_tok, qkvst, lse_st, state_rows, begin, cots, back, kept, vecs, bias,
        extra, hidden,
    )


def plane_place():
    place, half, rank = line_place()
    side = lax.axis_index("dp")
    return side, place, half, rank


def plane_index(side, place):
    return 4 * side + place


def row_halves(buf, rows):
    size = rows // 2
    return lambda owner, part: buf.at[owner, pl.ds(part * size, size), :]


def plane_gather(view, send_sem, recv_sem):
    side, place, half, rank = plane_place()
    across, beside = 1 - side, lax.rem(place + 2, 4)
    core = place + 1 - 2 * half
    me = plane_index(side, place)
    at_x, at_y = plane_index(across, place), plane_index(side, beside)
    at_d = plane_index(across, beside)
    to_x, to_y, to_c = {"dp": across}, {"seq": beside}, {"seq": core}

    def piece(owner, part, slot, target):
        one = view(owner, part)
        return pltpu.make_async_remote_copy(
            src_ref=one,
            dst_ref=one,
            send_sem=send_sem.at[slot],
            recv_sem=recv_sem.at[owner, part],
            device_id=target,
            device_id_type=MESH_ID,
        )

    own = [
        piece(me, 0, 0, to_x), piece(me, 1, 1, to_y), piece(me, 1, 2, to_x), piece(me, 0, 3, to_y),
        piece(me, 0, 4, to_c), piece(me, 1, 5, to_c),
    ]
    on_x0, on_y1 = piece(at_x, 0, 6, to_y), piece(at_y, 1, 7, to_x)
    came = [
        (piece(owner, part, 0, to_c), piece(owner, part, slot, to_c))
        for owner, part, slot in (
            (at_x, 0, 8), (at_y, 1, 9), (at_x, 1, 10), (at_y, 0, 11), (at_d, 0, 12), (at_d, 1, 13)
        )
    ]
    core_came = [
        piece(owner, part, 0, to_c)
        for owner in (
            plane_index(side, core),
            plane_index(across, core),
            plane_index(side, lax.rem(core + 2, 4)),
            plane_index(across, lax.rem(core + 2, 4)),
        )
        for part in (0, 1)
    ]
    yield
    for one in own:
        one.start()
    yield
    came[0][0].wait_recv()
    on_x0.start()
    came[1][0].wait_recv()
    on_y1.start()
    came[0][1].start()
    came[1][1].start()
    yield
    for index in (2, 3):
        came[index][0].wait_recv()
        came[index][1].start()
    yield
    for index in (4, 5):
        came[index][0].wait_recv()
        came[index][1].start()
    yield
    for one in core_came:
        one.wait_recv()
    for one in own + [on_x0, on_y1] + [two for _, two in came]:
        one.wait_send()


def run_all(*steps):
    waiting = list(steps)
    while waiting:
        for one in list(waiting):
            try:
                next(one)
            except StopIteration:
                waiting.remove(one)


def plane_scatter(part, core_got, near_got, far_got, total, rows, send_sem, recv_sem):
    side, place, half, rank = plane_place()
    across, beside = 1 - side, lax.rem(place + 2, 4)
    core = place + 1 - 2 * half
    me = plane_index(side, place)
    at_x, at_y = plane_index(across, place), plane_index(side, beside)
    at_d = plane_index(across, beside)
    size = rows // 2
    halves = (pl.ds(0, size), pl.ds(size, size))

    def moved(source, target_ref, slot, target):
        return pltpu.make_async_remote_copy(
            src_ref=source,
            dst_ref=target_ref,
            send_sem=send_sem.at[slot],
            recv_sem=recv_sem.at[slot],
            device_id=target,
            device_id_type=MESH_ID,
        )

    order = (at_d, at_x, at_y, me)
    swapped = (
        plane_index(across, lax.rem(core + 2, 4)),
        plane_index(across, core),
        plane_index(side, lax.rem(core + 2, 4)),
        plane_index(side, core),
    )
    def add_into(owner, view, other):
        part[owner, view, :] = to_low(
            part[owner, view, :].astype(jnp.float32) + other.astype(jnp.float32)
        )

    near = [
        moved(part.at[at_d, halves[0], :], near_got.at[0], 4, {"dp": across}),
        moved(part.at[at_d, halves[1], :], near_got.at[1], 5, {"seq": beside}),
        moved(part.at[at_x, halves[0], :], near_got.at[2], 6, {"dp": across}),
        moved(part.at[at_y, halves[1], :], near_got.at[3], 7, {"seq": beside}),
    ]
    first = [
        moved(part.at[owner], core_got.at[slot], slot, {"seq": core})
        for slot, owner in enumerate(swapped)
    ]
    far = [
        moved(part.at[at_y, halves[0], :], far_got.at[0], 8, {"seq": beside}),
        moved(part.at[at_x, halves[1], :], far_got.at[1], 9, {"dp": across}),
    ]
    yield
    for one in first:
        one.start()
    for slot, owner in enumerate(order):
        first[slot].wait_recv()
        for view in halves:
            add_into(owner, view, core_got[slot, view, :])
        if slot == 0:
            near[0].start()
            near[1].start()
        if slot == 1:
            near[2].start()
        if slot == 2:
            near[3].start()
    yield
    near[0].wait_recv()
    add_into(at_y, halves[0], near_got[0])
    far[0].start()
    near[1].wait_recv()
    add_into(at_x, halves[1], near_got[1])
    far[1].start()
    yield
    near[2].wait_recv()
    add_into(me, halves[0], near_got[2])
    near[3].wait_recv()
    add_into(me, halves[1], near_got[3])
    yield
    for slot, view in enumerate(halves):
        far[slot].wait_recv()
        total[view, :] = part[me, view, :].astype(jnp.float32) + far_got[slot].astype(jnp.float32)
    for one in first + near + far:
        one.wait_send()


def group_peers():
    place, half, rank = line_place()
    here = 4 * place + rank
    peers = []
    for step in range(1, 16):
        other = lax.rem(here + step, 16)
        peers.append((other, other // 4, lax.rem(other, 4)))
    return here, peers


def greet(peers):
    side = lax.axis_index("dp")
    barrier = pltpu.get_barrier_semaphore()
    for _, seq_to, rank_to in peers:
        pl.semaphore_signal(
            barrier, inc=1, device_id={"seq": seq_to, "tensor": rank_to}, device_id_type=MESH_ID
        )
    pl.semaphore_signal(barrier, inc=1, device_id={"dp": 1 - side}, device_id_type=MESH_ID)
    pl.semaphore_wait(barrier, len(peers) + 1)


def middle_kernel(
    mixed, tokens, kept, spread, cot_hbm, vecs,
    hidden, d_hidden, d_line, sums, extra, ff_grads,
    mixed_rows, mid_all, gl_all, dpre_all, work, core_got, near_got, far_got, total, d_rows,
    d_low, w_out, up, down, cot_all,
    send_sem, recv_sem, ring_send, ring_recv, sum_send, sum_recv, back_send, back_recv, local_sem,
):
    low, wide = jnp.bfloat16, jnp.float32
    side, place, half, rank = plane_place()
    mine = place // 2
    head = 2 * rank + half
    across, beside = 1 - side, lax.rem(place + 2, 4)
    core = place + 1 - 2 * half
    core_beside = lax.rem(core + 2, 4)
    me = plane_index(side, place)
    at_x, at_y = plane_index(across, place), plane_index(side, beside)
    at_d = plane_index(across, beside)
    me_c, x_c = plane_index(side, core), plane_index(across, core)
    y_c, d_c = plane_index(side, core_beside), plane_index(across, core_beside)
    to_x, to_y, to_c = {"dp": across}, {"seq": beside}, {"seq": core}
    here, peers = group_peers()
    fetch_pieces(kept, 48, 32, w_out, local_sem.at[0])
    ff_own = up.shape[1]
    first = spread.shape[1] - 2 * ff_own
    loads = [
        pltpu.make_async_copy(spread.at[:, pl.ds(first, ff_own), :], up, local_sem.at[1]),
        pltpu.make_async_copy(spread.at[:, pl.ds(first + ff_own, ff_own), :], down, local_sem.at[2]),
        pltpu.make_async_copy(cot_hbm, cot_all, local_sem.at[3]),
    ]
    for one in loads:
        one.start()
    greet(peers)

    def rows_copy(slot, sender, seq_from, rank_from, seq_to, rank_to):
        return pltpu.make_async_remote_copy(
            src_ref=mixed.at[seq_to, span(rank_to, 128), :],
            dst_ref=mixed_rows.at[
                seq_from // 2, :, span(2 * rank_from + lax.rem(seq_from, 2), 128)
            ],
            send_sem=send_sem.at[slot],
            recv_sem=recv_sem.at[sender],
            device_id={"seq": seq_to, "tensor": rank_to},
            device_id_type=MESH_ID,
        )

    for slot, (_, seq_to, rank_to) in enumerate(peers):
        rows_copy(slot, here, place, rank, seq_to, rank_to).start()
    mixed_rows[mine, :, span(head, 128)] = mixed[place, span(rank, 128), :]
    fetched(w_out, local_sem.at[0])
    for slot, (other, seq_to, rank_to) in enumerate(peers):
        rows_copy(slot, other, seq_to, rank_to, seq_to, rank_to).wait_recv()
    gain = vecs[2:3, :]

    def project(which, _):
        added = dot_nn(mixed_rows[which], w_out[...].reshape(D, D)) + tokens[which].astype(wide)
        hidden[which] = added
        centered, scale = norm_parts(added)
        mid_all[me, span(which, 128), :] = to_low(centered * scale * gain)
        return 0

    lax.fori_loop(0, 2, project, 0)

    def piece(owner, part, slot, target):
        view = mid_all.at[owner, pl.ds(part * 128, 128), :]
        return pltpu.make_async_remote_copy(
            src_ref=view,
            dst_ref=view,
            send_sem=ring_send.at[slot],
            recv_sem=ring_recv.at[owner, part],
            device_id=target,
            device_id_type=MESH_ID,
        )

    own = [
        piece(me, 0, 0, to_x), piece(me, 1, 1, to_y), piece(me, 1, 2, to_x), piece(me, 0, 3, to_y),
        piece(me, 0, 4, to_c), piece(me, 1, 5, to_c),
    ]
    on_x0, on_y1 = piece(at_x, 0, 6, to_y), piece(at_y, 1, 7, to_x)
    to_core = [
        piece(at_x, 0, 8, to_c), piece(at_y, 1, 9, to_c), piece(at_x, 1, 10, to_c),
        piece(at_y, 0, 11, to_c), piece(at_d, 0, 12, to_c), piece(at_d, 1, 13, to_c),
    ]
    wait_of = {
        (name, part): piece(owner, part, 0, to_c)
        for name, owner in (
            ("x", at_x), ("y", at_y), ("d", at_d), ("mc", me_c), ("xc", x_c), ("yc", y_c), ("dc", d_c)
        )
        for part in (0, 1)
    }

    def moved(source, target_ref, slot, target):
        return pltpu.make_async_remote_copy(
            src_ref=source,
            dst_ref=target_ref,
            send_sem=sum_send.at[slot],
            recv_sem=sum_recv.at[slot],
            device_id=target,
            device_id_type=MESH_ID,
        )

    views = (pl.ds(0, 128), pl.ds(128, 128))
    swap = [
        moved(work.at[owner], core_got.at[slot], slot, to_c)
        for slot, owner in enumerate((d_c, x_c, y_c, me_c))
    ]
    near = [
        moved(work.at[at_d, views[0], :], near_got.at[0], 4, to_x),
        moved(work.at[at_d, views[1], :], near_got.at[1], 5, to_y),
        moved(work.at[at_x, views[0], :], near_got.at[2], 6, to_x),
        moved(work.at[at_y, views[1], :], near_got.at[3], 7, to_y),
    ]
    far = [
        moved(work.at[at_y, views[0], :], far_got.at[0], 8, to_y),
        moved(work.at[at_x, views[1], :], far_got.at[1], 9, to_x),
    ]

    def add_into(owner, view, other):
        work[owner, view, :] = to_low(work[owner, view, :].astype(wide) + other.astype(wide))

    def add_core(slot, owner):
        swap[slot].wait_recv()
        for view in views:
            add_into(owner, view, core_got[slot, view, :])

    for one in own:
        one.start()
    loads[0].wait()
    loads[1].wait()
    loads[2].wait()
    owners = (me, me_c, at_x, at_y, x_c, y_c, at_d, d_c)

    def one_chunk(turn, _):
        @pl.when(turn == 1)
        def _():
            wait_of["mc", 0].wait_recv()
            wait_of["mc", 1].wait_recv()

        @pl.when(turn == 2)
        def _():
            swap[3].start()
            wait_of["x", 0].wait_recv()
            on_x0.start()
            wait_of["y", 1].wait_recv()
            on_y1.start()
            to_core[0].start()
            to_core[1].start()
            wait_of["x", 1].wait_recv()
            to_core[2].start()
            wait_of["y", 0].wait_recv()
            to_core[3].start()

        @pl.when(turn == 4)
        def _():
            wait_of["xc", 0].wait_recv()
            wait_of["xc", 1].wait_recv()

        @pl.when(turn == 5)
        def _():
            swap[1].start()
            wait_of["yc", 0].wait_recv()
            wait_of["yc", 1].wait_recv()

        @pl.when(turn == 6)
        def _():
            swap[2].start()
            wait_of["d", 0].wait_recv()
            to_core[4].start()
            wait_of["d", 1].wait_recv()
            to_core[5].start()
            add_core(1, at_x)
            near[2].start()
            add_core(2, at_y)
            near[3].start()

        @pl.when(turn == 7)
        def _():
            wait_of["dc", 0].wait_recv()
            wait_of["dc", 1].wait_recv()

        owner = owners[7]
        for index in range(7):
            owner = jnp.where(turn == index, owners[index], owner)
        up_rows = up[...].reshape(4 * ff_own, D)
        down_rows = down[...].reshape(4 * ff_own, D)

        def part(which, _):
            rows = span(which, 128)
            pre = dot_nt(mid_all[owner, rows, :], up_rows)
            square = pre * pre
            bend = jnp.tanh(GELU_SCALE * (pre + 0.044715 * (pre * square)))
            gl_all[owner, rows, :] = to_low(0.5 * pre * (1.0 + bend))
            slope = 0.5 * (1.0 + bend) + 0.5 * pre * (1.0 - bend * bend) * (
                GELU_SCALE * (1.0 + 3.0 * 0.044715 * square)
            )
            grad = to_low(dot_nt(cot_all[owner, rows, :], down_rows) * slope)
            dpre_all[owner, rows, :] = grad
            work[owner, rows, :] = to_low(dot_nn(grad, up_rows))
            return 0

        lax.fori_loop(0, 2, part, 0)
        return 0

    lax.fori_loop(0, 8, one_chunk, 0)
    swap[0].start()
    add_core(0, at_d)
    near[0].start()
    near[1].start()
    add_core(3, me)

    def grads(index, _):
        quarter, kind = index // 2, lax.rem(index, 2)
        columns = span(quarter, 128)

        @pl.when(kind == 0)
        def _():
            def add(owner, acc):
                return acc + dot_tn(dpre_all[owner, :, columns], mid_all[owner])

            ff_grads[quarter, 0] = to_low(lax.fori_loop(0, 8, add, jnp.zeros((128, D), wide)))

        @pl.when(kind == 1)
        def _():
            def add(owner, acc):
                return acc + dot_tn(gl_all[owner, :, columns], cot_all[owner])

            ff_grads[quarter, 1] = to_low(lax.fori_loop(0, 8, add, jnp.zeros((128, D), wide)))

        return 0

    lax.fori_loop(0, 8, grads, 0)
    near[0].wait_recv()
    add_into(at_y, views[0], near_got[0])
    far[0].start()
    near[1].wait_recv()
    add_into(at_x, views[1], near_got[1])
    far[1].start()
    near[2].wait_recv()
    add_into(me, views[0], near_got[2])
    near[3].wait_recv()
    add_into(me, views[1], near_got[3])

    def outward(owner, _):
        down_rows = down[...].reshape(4 * ff_own, D)
        for which in range(2):
            rows = pl.ds(128 * which, 128)
            extra[owner, rows, :] = to_low(dot_nn(gl_all[owner, rows, :], down_rows))
        return 0

    lax.fori_loop(0, 8, outward, 0)
    for slot, view in enumerate(views):
        far[slot].wait_recv()
        total[view, :] = work[me, view, :].astype(wide) + far_got[slot].astype(wide)
    sums[...] = jnp.zeros_like(sums)

    def back(which, _):
        rows = span(which, 128)
        grad = total[rows, :]
        centered, scale = norm_parts(hidden[which])
        normed = centered * scale
        sums[0:1, :] += jnp.sum(grad * normed, axis=0, keepdims=True)
        lifted = grad * gain
        row_grad = cot_all[me, rows, :].astype(wide) + scale * (
            lifted
            - jnp.mean(lifted, axis=-1, keepdims=True)
            - normed * jnp.mean(lifted * normed, axis=-1, keepdims=True)
        )
        d_hidden[which] = row_grad
        d_low[which] = to_low(row_grad)
        d_rows[which] = to_low(dot_nt(to_low(row_grad), w_out[...].reshape(D, D)))
        return 0

    lax.fori_loop(0, 2, back, 0)

    def line_copy(slot, sender, seq_from, rank_from, seq_to, rank_to):
        return pltpu.make_async_remote_copy(
            src_ref=d_rows.at[seq_to // 2, :, span(2 * rank_to + lax.rem(seq_to, 2), 128)],
            dst_ref=d_line.at[seq_from, span(rank_from, 128), :],
            send_sem=back_send.at[slot],
            recv_sem=back_recv.at[sender],
            device_id={"seq": seq_to, "tensor": rank_to},
            device_id_type=MESH_ID,
        )

    for slot, (_, seq_to, rank_to) in enumerate(peers):
        line_copy(slot, here, place, rank, seq_to, rank_to).start()
    d_line[place, span(rank, 128), :] = d_rows[mine, :, span(head, 128)]
    def outer(index, _):
        columns = span(index, 128)
        part = dot_tn(mixed_rows[0, :, columns], d_low[0]) + dot_tn(
            mixed_rows[1, :, columns], d_low[1]
        )
        part = to_low(part)
        for block in range(4):
            extra[
                4 * lax.rem(index, 2) + block,
                pl.ds(pl.multiple_of(256 + 32 * (index // 2), 32), 32),
                :,
            ] = part[32 * block : 32 * block + 32, :]
        return 0

    lax.fori_loop(0, LINE, outer, 0)
    for slot, (other, seq_to, rank_to) in enumerate(peers):
        line_copy(slot, other, seq_to, rank_to, seq_to, rank_to).wait_recv()
    for slot, (_, seq_to, rank_to) in enumerate(peers):
        rows_copy(slot, here, place, rank, seq_to, rank_to).wait_send()
        line_copy(slot, here, place, rank, seq_to, rank_to).wait_send()
    for one in own + [on_x0, on_y1] + to_core + swap + near + far:
        one.wait_send()


GELU_SCALE = 0.7978845608028654


def middle(mixed, tokens, kept, spread, cot_all, vecs):
    low, wide = jnp.bfloat16, jnp.float32
    ff_own = (spread.shape[1] - SPREAD_FIRST) // 2
    shapes = (
        ((2, 128, D), wide),
        ((2, 128, D), wide),
        ((4, BLOCK, 128), low),
        ((8, D), wide),
        ((8, 384, D), low),
        ((4, 2, ff_own, D), low),
    )
    dma = pltpu.SemaphoreType.DMA
    return pl.pallas_call(
        middle_kernel,
        out_shape=[jax.ShapeDtypeStruct(*one) for one in shapes],
        in_specs=vmem_specs(2) + any_specs(3) + vmem_specs(1),
        out_specs=vmem_specs(6),
        scratch_shapes=[
            pltpu.VMEM((2, 128, D), low),
            pltpu.VMEM((8, 256, D), low),
            pltpu.VMEM((8, 256, 4 * ff_own), low),
            pltpu.VMEM((8, 256, 4 * ff_own), low),
            pltpu.VMEM((8, 256, D), low),
            pltpu.VMEM((4, 256, D), low),
            pltpu.VMEM((4, 128, D), low),
            pltpu.VMEM((2, 128, D), low),
            pltpu.VMEM((256, D), wide),
            pltpu.VMEM((2, 128, D), low),
            pltpu.VMEM((2, 128, D), low),
            pltpu.VMEM((4, 8, 32, D), low),
            pltpu.VMEM((4, ff_own, D), low),
            pltpu.VMEM((4, ff_own, D), low),
            pltpu.VMEM((8, 256, D), low),
            dma((15,)), dma((16,)), dma((14,)), dma((8, 2)), dma((10,)), dma((10,)), dma((15,)),
            dma((16,)), dma((4,)),
        ],
        compiler_params=pltpu.CompilerParams(
            collective_id=3, has_side_effects=True, vmem_limit_bytes=VMEM_LIMIT
        ),
        cost_estimate=pl.CostEstimate(
            flops=60000000000, bytes_accessed=60000000, transcendentals=0
        ),
        name="middle",
    )(mixed, tokens, kept, spread, cot_all, vecs)


SPREAD_FIRST = 0


WIDE = 2048


def opening_kernel(
    tokens, w_query, w_key, w_value, w_sout, w_out, begin, vecs, rel_bias, marks_own,
    rows_all, qkv, kept, table, marks, w_qkv,
    begin_rows, bias_rows, stage, send_sem, core_sem, recv_sem, piece_send, piece_recv, ring_send, ring_recv,
    mark_send, mark_recv, local_sem,
):
    side, place, half, rank = plane_place()
    mine = place // 2
    core = place + 1 - 2 * half
    other = lax.rem(place + 2, 4)
    me = plane_index(side, place)
    extra = 80
    fetch_columns((w_query, w_key, w_value), w_qkv, local_sem.at[0])
    loads = [
        pltpu.make_async_copy(
            w_sout.at[span(me, 32), :], kept.at[me, pl.ds(80 * rank, 32), :], local_sem.at[1]
        ),
        pltpu.make_async_copy(
            w_out.at[span(me, 32), :], kept.at[me, pl.ds(80 * rank + 48, 32), :], local_sem.at[3]
        ),
        pltpu.make_async_copy(begin.at[span(me, 16), :], begin_rows, local_sem.at[2]),
    ]
    for one in loads:
        one.start()
    barrier = pltpu.get_barrier_semaphore()
    greeted = [{"tensor": lax.rem(rank + step, 4)} for step in (1, 2, 3)]
    seats = [lax.rem(place + step, 4) for step in (1, 2, 3)]
    greeted += [{"seq": one} for one in seats] + [{"dp": 1 - side}]
    for target in greeted:
        pl.semaphore_signal(barrier, inc=1, device_id=target, device_id_type=MESH_ID)
    gain = vecs[3:4, :]

    def normed(which):
        centered, scale = norm_parts(tokens[which].astype(jnp.float32))
        return to_low(centered * scale * gain)

    def moved(block_id, origin, sem, target):
        view = rows_all.at[block_id, span(origin, 128), :]
        return pltpu.make_async_remote_copy(
            src_ref=view,
            dst_ref=view,
            send_sem=sem,
            recv_sem=recv_sem.at[block_id, origin],
            device_id=target,
            device_id_type=MESH_ID,
        )

    stage[...] = normed(1 - mine)
    marks[place] = marks_own[...]
    pl.semaphore_wait(barrier, 7)
    aside = pltpu.make_async_remote_copy(
        src_ref=stage,
        dst_ref=rows_all.at[place, span(rank, 128), :],
        send_sem=send_sem.at[0, 0, 3],
        recv_sem=recv_sem.at[place, rank],
        device_id={"seq": other},
        device_id_type=MESH_ID,
    )
    aside.start()

    def mark_move(slot, origin, target):
        return pltpu.make_async_remote_copy(
            src_ref=marks.at[origin],
            dst_ref=marks.at[origin],
            send_sem=mark_send.at[slot],
            recv_sem=mark_recv.at[origin],
            device_id={"seq": target},
            device_id_type=MESH_ID,
        )

    def piece_move(slot, origin, target):
        view = kept.at[me, span(origin, extra), :]
        return pltpu.make_async_remote_copy(
            src_ref=view,
            dst_ref=view,
            send_sem=piece_send.at[slot],
            recv_sem=piece_recv.at[origin],
            device_id=target,
            device_id_type=MESH_ID,
        )

    for one in loads:
        one.wait()
    kept[me, pl.ds(pl.multiple_of(80 * rank + 32, 16), 16), :] = to_low(begin_rows[...])
    for slot in range(3):
        piece_move(slot, rank, greeted[slot]).start()
    for slot, target in enumerate(seats):
        mark_move(slot, place, target).start()
    rows_all[place, span(rank, 128), :] = normed(mine)
    right, left = {"tensor": lax.rem(rank + 1, 4)}, {"tensor": lax.rem(rank + 3, 4)}
    blocks = (place, other)

    def pass_on(which, distance):
        block_id = blocks[which]

        @pl.when((rank < 3) & (rank >= distance))
        def _():
            moved(block_id, jnp.maximum(rank - distance, 0), send_sem.at[which, distance, 0], right).start()

        @pl.when((rank > 0) & (rank + distance <= 3))
        def _():
            moved(block_id, jnp.minimum(rank + distance, 3), send_sem.at[which, distance, 1], left).start()

    def pass_done(which, distance):
        block_id = blocks[which]

        @pl.when((rank < 3) & (rank >= distance))
        def _():
            moved(block_id, jnp.maximum(rank - distance, 0), send_sem.at[which, distance, 0], right).wait_send()

        @pl.when((rank > 0) & (rank + distance <= 3))
        def _():
            moved(block_id, jnp.minimum(rank + distance, 3), send_sem.at[which, distance, 1], left).wait_send()

    def project(block_id, origin):
        view = span(origin, 128)
        qkv[block_id, view, :] = to_low(dot_nn(rows_all[block_id, view, :], w_qkv[...]))

    def rows_steps():
        pass_on(0, 0)
        fetched(w_qkv, local_sem.at[0])
        moved(place, rank, core_sem.at[0, rank], {"seq": core}).start()
        project(place, rank)
        moved(other, rank, send_sem.at[0, 0, 3], {"seq": other}).wait_recv()
        pass_on(1, 0)
        moved(other, rank, core_sem.at[1, rank], {"seq": core}).start()
        project(other, rank)
        yield
        for distance in (1, 2, 3):
            for which in (0, 1):
                block_id = blocks[which]
                for way, ok, origin in (
                    (0, rank >= distance, jnp.maximum(rank - distance, 0)),
                    (1, rank + distance <= 3, jnp.minimum(rank + distance, 3)),
                ):

                    @pl.when(ok)
                    def _():
                        moved(block_id, origin, send_sem.at[which, distance, way], right).wait_recv()
                        if distance < 3:
                            if way == 0:

                                @pl.when(rank < 3)
                                def _():
                                    moved(
                                        block_id, origin, send_sem.at[which, distance, 0], right
                                    ).start()

                            else:

                                @pl.when(rank > 0)
                                def _():
                                    moved(
                                        block_id, origin, send_sem.at[which, distance, 1], left
                                    ).start()

                        moved(block_id, origin, core_sem.at[which, origin], {"seq": core}).start()
                        project(block_id, origin)

                yield
        for which, block_id in enumerate((core, lax.rem(core + 2, 4))):
            for origin in range(4):
                moved(block_id, origin, core_sem.at[which, origin], {"seq": core}).wait_recv()
                project(block_id, origin)
        for which in (0, 1):
            for distance in (0, 1, 2):
                pass_done(which, distance)
            for origin in range(4):
                moved(blocks[which], origin, core_sem.at[which, origin], {"seq": core}).wait_send()

    def piece_steps():
        for slot in range(3):
            piece_move(slot, lax.rem(rank + slot + 1, 4), greeted[slot]).wait_recv()
        for _ in plane_gather(row_halves(kept, 4 * extra), ring_send, ring_recv):
            yield
        for slot in range(3):
            piece_move(slot, rank, greeted[slot]).wait_send()

    def bias_steps():
        lane = lax.broadcasted_iota(jnp.int32, (8, WIDE), 1)
        bucket_ids = bucket_of(jnp.where(lane >= WIDE - BLOCK, lane - WIDE - BLOCK, lane - BLOCK))
        first = jnp.zeros((8, WIDE), jnp.float32)
        for bucket_id in range(BUCKETS):
            first = jnp.where(bucket_ids == bucket_id, rel_bias[bucket_id, half], first)
        row = lax.broadcasted_iota(jnp.int32, (8, WIDE), 0)
        for step in (1, 2, 4):
            first = jnp.where(row // step % 2 == 1, pltpu.roll(first, step, 1), first)
        bias_rows[...] = first
        yield

        def one(group, _):
            table[span(group, 8), :] = pltpu.roll(bias_rows[...], 8 * group, 1)[:, 0 : 2 * BLOCK]
            return 0

        for part in range(4):
            lax.fori_loop(16 * part, 16 * part + 16, one, 0)
            yield

    run_all(rows_steps(), piece_steps(), bias_steps())
    aside.wait_send()
    for slot, target in enumerate(seats):
        mark_move(slot, place, target).wait_send()
        mark_move(slot, target, target).wait_recv()


def opening(tokens, w_query, w_key, w_value, w_sout, w_out, begin, vecs, rel_bias, marks):
    low, wide = jnp.bfloat16, jnp.float32
    shapes = (
        ((4, BLOCK, D), low),
        ((4, BLOCK, 384), low),
        ((8, 4 * 80, D), low),
        ((BLOCK, 2 * BLOCK), wide),
        ((4, 8, 128), jnp.int32),
        ((D, 384), low),
    )
    dma = pltpu.SemaphoreType.DMA
    outs = pl.pallas_call(
        opening_kernel,
        out_shape=[jax.ShapeDtypeStruct(*one) for one in shapes],
        in_specs=vmem_specs(1)
        + any_specs(6)
        + vmem_specs(1)
        + [pl.BlockSpec(memory_space=pltpu.SMEM)]
        + vmem_specs(1),
        out_specs=vmem_specs(6),
        scratch_shapes=[
            pltpu.VMEM((16, D), wide),
            pltpu.VMEM((8, WIDE), wide),
            pltpu.VMEM((128, D), low),
            dma((2, 4, 4)),
            dma((2, 4)),
            dma((4, 4)),
            dma((3,)),
            dma((4,)),
            dma((14,)),
            dma((8, 2)),
            dma((3,)),
            dma((4,)),
            dma((4,)),
        ],
        compiler_params=pltpu.CompilerParams(
            collective_id=5, has_side_effects=True, vmem_limit_bytes=VMEM_LIMIT
        ),
        cost_estimate=pl.CostEstimate(
            flops=30000000000, bytes_accessed=30000000, transcendentals=0
        ),
        name="opening",
    )(tokens, w_query, w_key, w_value, w_sout, w_out, begin, vecs, rel_bias, marks)
    rows_all, qkv, kept, table, marks, w_qkv = outs
    return rows_all, qkv, kept.reshape(8, 4, 80, D), table, marks, w_qkv


def pair_sum(part, near_got, far_got, result, rows, send_sem, recv_sem):
    side, place, half, rank = plane_place()
    mine = place // 2
    across, beside = 1 - side, 1 - mine
    me = 2 * side + mine
    at_x, at_y, at_d = 2 * across + mine, 2 * side + beside, 2 * across + beside
    to_x, to_y = {"dp": across}, {"seq": lax.rem(place + 2, 4)}
    size = rows // 2
    views = (pl.ds(0, size), pl.ds(size, size))

    def moved(source, target_ref, slot, target):
        return pltpu.make_async_remote_copy(
            src_ref=source,
            dst_ref=target_ref,
            send_sem=send_sem.at[slot],
            recv_sem=recv_sem.at[slot],
            device_id=target,
            device_id_type=MESH_ID,
        )

    def add_into(owner, view, other):
        part[owner, view, :] = to_low(
            part[owner, view, :].astype(jnp.float32) + other.astype(jnp.float32)
        )

    near = [
        moved(part.at[at_d, views[0], :], near_got.at[0], 0, to_x),
        moved(part.at[at_d, views[1], :], near_got.at[1], 1, to_y),
        moved(part.at[at_x, views[0], :], near_got.at[2], 2, to_x),
        moved(part.at[at_y, views[1], :], near_got.at[3], 3, to_y),
    ]
    for one in near:
        one.start()
    yield
    near[0].wait_recv()
    add_into(at_y, views[0], near_got[0])
    far = [
        moved(part.at[at_y, views[0], :], far_got.at[0], 4, to_y),
        moved(part.at[at_x, views[1], :], far_got.at[1], 5, to_x),
    ]
    far[0].start()
    near[1].wait_recv()
    add_into(at_x, views[1], near_got[1])
    far[1].start()
    yield
    near[2].wait_recv()
    add_into(me, views[0], near_got[2])
    near[3].wait_recv()
    add_into(me, views[1], near_got[3])
    for slot, view in enumerate(views):
        far[slot].wait_recv()
        result[me, view, :] = to_low(
            part[me, view, :].astype(jnp.float32) + far_got[slot].astype(jnp.float32)
        )

    def given(owner, which, slot, target):
        view = result.at[owner, views[which], :]
        return moved(view, view, slot, target)

    own = [
        given(me, 0, 6, to_x),
        given(me, 1, 7, to_y),
        given(me, 1, 8, to_x),
        given(me, 0, 9, to_y),
    ]
    for one in own:
        one.start()
    yield
    given(at_x, 0, 6, to_x).wait_recv()
    last = [given(at_x, 0, 10, to_y), given(at_y, 1, 11, to_x)]
    last[0].start()
    given(at_y, 1, 7, to_y).wait_recv()
    last[1].start()
    yield
    given(at_x, 1, 8, to_x).wait_recv()
    given(at_y, 0, 9, to_y).wait_recv()
    given(at_d, 0, 10, to_y).wait_recv()
    given(at_d, 1, 11, to_x).wait_recv()
    for one in near + far + own + last:
        one.wait_send()


PAIR_ROWS = 640


def closing_kernel(
    d_qkv, w_qkv, tokens, d_hidden, vecs, rows_hbm, low_hbm, d_qkvst_hbm, os_hbm, du_hbm,
    d_start, dz_hbm, small, out_part,
    inputs_grad, pair_out, sout_out, small_out,
    rows_all, state_low, d_qkvst, os_rows, du_rows, dz_sum,
    leave, came, sums, got, final, cross, cross_got,
    pair_whole, pair_part, pair_near, pair_far,
    work, core_got, near_got, far_got, total, z_part, z_got,
    diag, small_z, small_p,
    line_send, line_recv, way_send, way_recv, pair_send, pair_recv, core_sem,
    ring_send, ring_recv, zs_send, zs_recv, gather_send, gather_recv, small_send, small_recv, local_sem,
):
    loads = [
        pltpu.make_async_copy(source, target, local_sem.at[slot])
        for slot, (source, target) in enumerate(
            (
                (rows_hbm, rows_all),
                (d_qkvst_hbm, d_qkvst),
                (low_hbm, state_low),
                (os_hbm, os_rows),
                (du_hbm, du_rows),
                (dz_hbm, dz_sum),
            )
        )
    ]
    for one in loads:
        one.start()
    side, place, half, rank = plane_place()
    mine = place // 2
    core = place + 1 - 2 * half
    other = lax.rem(place + 2, 4)
    me = plane_index(side, place)
    ranks = [lax.rem(rank + step, 4) for step in (1, 2, 3)]
    spots_of = [lax.rem(me + step, 8) for step in range(1, 8)]
    barrier = pltpu.get_barrier_semaphore()
    for target in ranks:
        pl.semaphore_signal(barrier, inc=1, device_id={"tensor": target}, device_id_type=MESH_ID)
    for target in spots_of:
        pl.semaphore_signal(
            barrier,
            inc=1,
            device_id={"dp": target // 4, "seq": lax.rem(target, 4)},
            device_id_type=MESH_ID,
        )
    gain = vecs[3:4, :]
    right, left = {"tensor": lax.rem(rank + 1, 4)}, {"tensor": lax.rem(rank + 3, 4)}

    def moved(source, target_ref, send, recv, target):
        return pltpu.make_async_remote_copy(
            src_ref=source,
            dst_ref=target_ref,
            send_sem=send,
            recv_sem=recv,
            device_id=target,
            device_id_type=MESH_ID,
        )

    def to_core(which):
        return moved(
            leave.at[which], came.at[which], line_send.at[which], line_recv.at[which], {"seq": core}
        )

    def crossing():
        return moved(cross, cross_got, line_send.at[2], line_recv.at[2], {"seq": other})

    near = rank // 2
    at_end = (rank == 0) | (rank == 3)

    def hop(way, which, target):
        return moved(
            sums.at[which, target],
            got.at[way, which, target],
            way_send.at[which, target],
            way_recv.at[way, which, target],
            {"tensor": lax.rem(rank + 5 - 2 * way, 4)},
        )

    def target_of(way, distance):
        return (1 - way) * (3 - distance) + way * distance

    def pass_first(which):
        @pl.when(at_end)
        def _():
            for distance in range(3):
                hop(near, which, target_of(near, distance)).start()

    def pass_on(way, which, distance):
        @pl.when(jnp.logical_not(at_end))
        def _():
            target = target_of(way, distance)
            hop(way, which, target).wait_recv()
            sums[which, target] = to_low(
                sums[which, target].astype(jnp.float32)
                + got[way, which, target].astype(jnp.float32)
            )
            hop(way, which, target).start()

    def finish(which):
        final[which] = sums[which, rank].astype(jnp.float32)

        @pl.when(rank > 0)
        def _():
            hop(0, which, rank).wait_recv()
            final[which] += got[0, which, rank].astype(jnp.float32)

        @pl.when(rank < 3)
        def _():
            hop(1, which, rank).wait_recv()
            final[which] += got[1, which, rank].astype(jnp.float32)

    def line_steps():
        for which, block_id in enumerate((lax.rem(core + 2, 4), core)):

            def partner(chunk, _):
                rows = span(chunk, ROWS)
                leave[which, rows, :] = to_low(dot_nt(d_qkv[block_id, rows, :], w_qkv[...]))
                return 0

            lax.fori_loop(0, CHUNKS, partner, 0)
            if which == 0:
                pl.semaphore_wait(barrier, 10)
            to_core(which).start()
        for which, block_id in enumerate((other, place)):
            to_core(which).wait_recv()

            def own(chunk, _):
                rows = span(chunk, ROWS)
                sums[which, chunk] = to_low(
                    dot_nt(d_qkv[block_id, rows, :], w_qkv[...])
                    + came[which, rows, :].astype(jnp.float32)
                )
                return 0

            lax.fori_loop(0, CHUNKS, own, 0)
            pass_first(which)
        yield
        for which in (0, 1):
            pass_on(near, which, 0)
            yield
            pass_on(near, which, 1)
            pass_on(1 - near, which, 0)
            yield
            finish(which)
            if which == 0:
                cross[...] = to_low(final[0])
                crossing().start()
            yield
        crossing().wait_recv()
        final[0] = cross_got[...].astype(jnp.float32)
        small_z[rank] = small[...]
        for which, row_set in ((1, mine), (0, 1 - mine)):
            grad = final[which]
            centered, scale = norm_parts(tokens[row_set].astype(jnp.float32))
            normed = centered * scale
            small_z[rank, 0:1, :] += jnp.sum(grad * normed, axis=0, keepdims=True)
            lifted = grad * gain
            inputs_grad[row_set] = d_hidden[row_set] + scale * (
                lifted
                - jnp.mean(lifted, axis=-1, keepdims=True)
                - normed * jnp.mean(lifted * normed, axis=-1, keepdims=True)
            )
        crossing().wait_send()
        for which in (0, 1):
            to_core(which).wait_send()
            for target in range(4):

                @pl.when(rank != target)
                def _():
                    hop(0, which, target).wait_send()

    def pair_steps():
        loads[0].wait()
        loads[1].wait()
        loads[2].wait()
        def one_part(part, _):
            token_columns = span(jnp.minimum(part, 2), 128)
            state_columns = span(lax.rem(part, 3), 128)

            def token_add(block_id, acc):
                return acc + dot_tn(d_qkv[block_id, :, token_columns], rows_all[block_id])

            def state_add(block_id, acc):
                return acc + dot_tn(d_qkvst[block_id, :, state_columns], state_low[block_id])

            acc = lax.fori_loop(
                0, jnp.where(part < 3, 4, 0), token_add, jnp.zeros((128, D), jnp.float32)
            )
            acc = lax.fori_loop(0, jnp.where(part > 0, 4, 0), state_add, acc)
            pair_whole[span(part, 128), :] = to_low(acc)
            return 0

        lax.fori_loop(0, 4, one_part, 0)
        for owner in range(3):
            pair_part[owner] = pair_whole[160 * owner : 160 * owner + 160, :]
        pair_part[3, 0:32, :] = pair_whole[480:512, :]
        pair_part[3, 32:96, :] = to_low(d_start[...])
        pair_part[3, 96:160, :] = jnp.zeros((64, D), jnp.bfloat16)
        for _ in pair_sum(
            pair_part, pair_near, pair_far, pair_out.at[half], 160, pair_send, pair_recv
        ):
            yield
        full = moved(
            pair_out.at[half], pair_out.at[half], core_sem.at[0], core_sem.at[1], {"seq": core}
        )
        full.start()
        yield
        moved(
            pair_out.at[1 - half], pair_out.at[1 - half], core_sem.at[0], core_sem.at[1],
            {"seq": core},
        ).wait_recv()
        full.wait_send()

    def sout_steps():
        loads[3].wait()
        loads[4].wait()
        def one_head(head, _):
            part = to_low(dot_tn(os_rows[:, span(head, 128)], du_rows[...]))
            for block in range(4):
                work[4 * lax.rem(head, 2) + block, span(head // 2, 32), :] = part[
                    32 * block : 32 * block + 32, :
                ]
            return 0

        lax.fori_loop(0, LINE, one_head, 0)
        for _ in plane_scatter(
            work, core_got, near_got, far_got, total, 128, ring_send, ring_recv
        ):
            yield
        z_part[:, 0:32, :] = to_low(total[...]).reshape(4, 32, D)
        z_part[:, 32:64, :] = out_part[...].reshape(4, 32, D)
        out = [
            moved(
                z_part.at[target], z_got.at[rank], zs_send.at[slot], zs_recv.at[rank],
                {"tensor": target},
            )
            for slot, target in enumerate(ranks)
        ]
        for one in out:
            one.start()
        z_got[rank] = z_part[rank]
        yield
        for slot, target in enumerate(ranks):
            moved(
                z_part.at[target], z_got.at[target], zs_send.at[slot], zs_recv.at[target],
                {"tensor": target},
            ).wait_recv()
        acc = z_got[0].astype(jnp.float32)
        for target in range(1, 4):
            acc = acc + z_got[target].astype(jnp.float32)
        sout_out[me] = to_low(acc)
        for _ in plane_gather(row_halves(sout_out, 64), gather_send, gather_recv):
            yield
        for one in out:
            one.wait_send()

    def diag_steps():
        loads[5].wait()
        diag[...] = jnp.zeros_like(diag)
        for part in range(4):

            def one(group, _):
                rows = dz_sum[span(group, 8), :]
                wide = jnp.concatenate(
                    [rows, jnp.zeros((8, WIDE - 2 * BLOCK), jnp.float32)], axis=1
                )
                diag[...] += pltpu.roll(wide, lax.rem(WIDE - 8 * group, WIDE), 1)
                return 0

            lax.fori_loop(16 * part, 16 * part + 16, one, 0)
            yield
        total_line = diag[...]
        row = lax.broadcasted_iota(jnp.int32, (8, WIDE), 0)
        for step in (1, 2, 4):
            total_line = jnp.where(
                row // step % 2 == 1, pltpu.roll(total_line, WIDE - step, 1), total_line
            )
        lane = lax.broadcasted_iota(jnp.int32, (8, WIDE), 1)
        offset = jnp.where(lane >= WIDE - BLOCK, lane - WIDE - BLOCK, lane - BLOCK)
        bucket_ids = bucket_of(offset)
        spot = lax.broadcasted_iota(jnp.int32, (1, 256), 1) - BUCKETS * (2 * rank + half)
        placed = jnp.zeros((1, 256), jnp.float32)
        for bucket_id in range(BUCKETS):
            chosen = jnp.where(bucket_ids == bucket_id, total_line, 0.0)
            value = jnp.sum(jnp.sum(chosen, axis=0, keepdims=True), axis=1, keepdims=True)
            placed = jnp.where(spot == bucket_id, value, placed)
        diag[0:1, 0:256] = placed

    extra = sout_steps()
    run_all(line_steps(), pair_steps(), extra, diag_steps(), extra)
    small_z[rank, 4:5, 0:256] = diag[0:1, 0:256]

    def small_over_z(slot, sender, target):
        return moved(
            small_z.at[sender], small_z.at[sender], small_send.at[slot], small_recv.at[sender],
            {"tensor": target},
        )

    for slot, target in enumerate(ranks):
        small_over_z(slot, rank, target).start()
    for slot, target in enumerate(ranks):
        small_over_z(slot, target, target).wait_recv()
    small_p[me] = small_z[0] + small_z[1] + small_z[2] + small_z[3]

    def small_over_plane(slot, sender, target):
        return moved(
            small_p.at[sender], small_p.at[sender], small_send.at[3 + slot],
            small_recv.at[4 + sender],
            {"dp": target // 4, "seq": lax.rem(target, 4)},
        )

    for slot, target in enumerate(spots_of):
        small_over_plane(slot, me, target).start()
    for slot, target in enumerate(spots_of):
        small_over_plane(slot, target, target).wait_recv()
    acc = small_p[0]
    for target in range(1, 8):
        acc = acc + small_p[target]
    small_out[...] = acc
    for slot, target in enumerate(ranks):
        small_over_z(slot, rank, target).wait_send()
    for slot, target in enumerate(spots_of):
        small_over_plane(slot, me, target).wait_send()


def closing(
    d_qkv, w_qkv, tokens, d_hidden, vecs, rows_all, state_low, d_qkvst, os_rows, du_rows,
    d_start, dz_sum, small, out_part,
):
    low, wide = jnp.bfloat16, jnp.float32
    shapes = (
        ((2, 128, D), wide),
        ((2, 4, PAIR_ROWS // 4, D), low),
        ((8, 64, D), low),
        ((8, D), wide),
    )
    dma = pltpu.SemaphoreType.DMA
    return pl.pallas_call(
        closing_kernel,
        out_shape=[jax.ShapeDtypeStruct(*one) for one in shapes],
        in_specs=vmem_specs(5) + any_specs(5) + vmem_specs(1) + any_specs(1) + vmem_specs(2),
        out_specs=vmem_specs(4),
        scratch_shapes=[
            pltpu.VMEM((4, BLOCK, D), low),
            pltpu.VMEM((4, BLOCK, D), low),
            pltpu.VMEM((4, BLOCK, 384), low),
            pltpu.VMEM((256, D), low),
            pltpu.VMEM((256, D), low),
            pltpu.VMEM((BLOCK, 2 * BLOCK), wide),
            pltpu.VMEM((2, BLOCK, D), low),
            pltpu.VMEM((2, BLOCK, D), low),
            pltpu.VMEM((2, 4, 128, D), low),
            pltpu.VMEM((2, 2, 4, 128, D), low),
            pltpu.VMEM((2, 128, D), wide),
            pltpu.VMEM((128, D), low),
            pltpu.VMEM((128, D), low),
            pltpu.VMEM((512, D), low),
            pltpu.VMEM((4, PAIR_ROWS // 4, D), low),
            pltpu.VMEM((4, PAIR_ROWS // 8, D), low),
            pltpu.VMEM((2, PAIR_ROWS // 8, D), low),
            pltpu.VMEM((8, 128, D), low),
            pltpu.VMEM((4, 128, D), low),
            pltpu.VMEM((4, 64, D), low),
            pltpu.VMEM((2, 64, D), low),
            pltpu.VMEM((128, D), wide),
            pltpu.VMEM((4, 64, D), low),
            pltpu.VMEM((4, 64, D), low),
            pltpu.VMEM((8, WIDE), wide),
            pltpu.VMEM((4, 8, D), wide),
            pltpu.VMEM((8, 8, D), wide),
            dma((3,)), dma((3,)), dma((2, 4)), dma((2, 2, 4)), dma((12,)), dma((12,)), dma((2,)),
            dma((10,)), dma((10,)), dma((3,)), dma((4,)), dma((16,)), dma((8, 2)), dma((10,)),
            dma((12,)), dma((6,)),
        ],
        compiler_params=pltpu.CompilerParams(
            collective_id=6, has_side_effects=True, vmem_limit_bytes=VMEM_LIMIT
        ),
        cost_estimate=pl.CostEstimate(
            flops=30000000000, bytes_accessed=30000000, transcendentals=0
        ),
        name="closing",
    )(
        d_qkv, w_qkv, tokens, d_hidden, vecs, rows_all, state_low, d_qkvst, os_rows, du_rows,
        d_start, dz_sum, small, out_part,
    )


def finish_kernel(
    pair, pair_tail, two, ff,
    query, key, value, squery, out, sout, up, down, state,
):
    step = pl.program_id(0)
    wide = jnp.float32
    up[...] = ff[0, 0].astype(wide).T
    down[...] = ff[0, 1].astype(wide)
    sout[...] = two[0, 0:32].astype(wide)
    out[...] = two[0, 32:64].astype(wide)
    for which, target in enumerate((query, key, value, squery)):

        @pl.when(step // 2 == which)
        def _():
            target[...] = pair[0].astype(wide).T

    @pl.when(step == 0)
    def _():
        state[...] = pair_tail[...].reshape(128, D).astype(wide)


def finish_grads(pair, two, ff):
    wide = jnp.float32
    turned = [
        pl.BlockSpec((D, 128), lambda i, w=which: (0, jnp.clip(i - 2 * w, 0, 1)))
        for which in range(4)
    ]
    square = jax.ShapeDtypeStruct((D, 256), wide)
    rows = jax.ShapeDtypeStruct((256, D), wide)
    whole = jax.ShapeDtypeStruct((D, D), wide)
    return pl.pallas_call(
        finish_kernel,
        grid=(8,),
        out_shape=[square] * 4 + [rows] * 2 + [whole] * 2 + [jax.ShapeDtypeStruct((128, D), wide)],
        in_specs=[
            pl.BlockSpec((1, 128, D), lambda i: (i % 2, i // 2, 0)),
            pl.BlockSpec((2, 64, D), lambda i: (0, 8, 0)),
            pl.BlockSpec((1, 64, D), lambda i: (i, 0, 0)),
            pl.BlockSpec((1, 2, 128, D), lambda i: (i, 0, 0, 0)),
        ],
        out_specs=turned
        + [pl.BlockSpec((32, D), lambda i: (i, 0))] * 2
        + [pl.BlockSpec((D, 128), lambda i: (0, i)), pl.BlockSpec((128, D), lambda i: (i, 0))]
        + [pl.BlockSpec((128, D), lambda i: (0, 0))],
        compiler_params=pltpu.CompilerParams(vmem_limit_bytes=VMEM_LIMIT),
        name="finish_grads",
    )(pair, pair, two, ff)


def swap_seq(value):
    return lax.all_to_all(value, "seq", 0, 0, tiled=False)


def line_body(
    inputs,
    seg_starts,
    lengths,
    init_state,
    attn_gain,
    state_gain,
    mlp_gain,
    w_query,
    w_key,
    w_value,
    w_out,
    w_squery,
    w_sout,
    w_up,
    w_down,
    rel_bias,
    gate_bias,
    out_cot,
    state_cot,
):
    low, wide = jnp.bfloat16, jnp.float32
    place = lax.axis_index("seq")
    half = lax.rem(place, 2)
    mine = place // 2
    plane = ("dp", "seq")
    spot = 4 * lax.axis_index("dp") + place
    gate_value = jax.nn.sigmoid(gate_bias)
    vecs = jnp.stack(
        [state_gain, gate_value, mlp_gain, attn_gain] + [jnp.zeros_like(gate_value)] * 4
    )
    marks = jnp.concatenate([seg_starts[:, 0], lengths, jnp.zeros((4,), jnp.int32)])
    marks = jnp.broadcast_to(marks[:, None], (8, 128))
    rows_all, qkv, kept, bias, marks, w_qkv = opening(
        inputs, w_query, w_key, w_value, w_sout, w_out, init_state, vecs, rel_bias, marks
    )

    ff_own = w_up.shape[1] // 8
    piece_of = lambda weight: lax.dynamic_slice_in_dim(weight, spot * 32, 32, 1).T
    back_own = jnp.stack(
        [
            piece_of(w_squery),
            piece_of(w_key),
            piece_of(w_value),
        ]
    )
    pieces = jnp.concatenate(
        [
            lax.dynamic_slice_in_dim(w_up, spot * ff_own, ff_own, 1).T,
            lax.dynamic_slice_in_dim(w_down, spot * ff_own, ff_own, 0),
        ],
        axis=0,
    )
    qkv, pieces, back_own, cot_own = lax.optimization_barrier((qkv, pieces, back_own, out_cot))
    spread = lax.all_gather(pieces, "tensor", axis=0, tiled=True).reshape(4, 2 * ff_own, D)
    cot_used = lax.all_gather(cot_own.reshape(256, D), plane, axis=0, tiled=True)
    mixed, lse_tok, state_rows, state_low, qkvst, lse_st, os_rows, cots, back = forward_chain(
        marks, qkv, kept, w_squery, w_qkv, vecs, bias, state_cot.reshape(4, 64, D), back_own
    )
    hidden_in, grad_hidden, d_mixed, mlp_sums, extra, ff_grads = middle(
        mixed, inputs, kept, spread, cot_used.reshape(8, 256, D), vecs
    )
    d_mixed, ff_grads = lax.optimization_barrier((d_mixed, ff_grads))
    ff_sum = lax.psum_scatter(
        ff_grads.reshape(ff_grads.shape[2] * 8, D), "tensor", scatter_dimension=0, tiled=True
    )
    (
        d_qkv, d_qkvst, du_rows, d_start, sums, dz_sum, state_out, tokens_out, out_part,
    ) = backward_chain(
        marks, qkv, d_mixed, lse_tok, qkvst, lse_st, state_rows, init_state, cots,
        back, kept, vecs, bias, extra, hidden_in,
    )
    d_qkv, ff_sum = lax.optimization_barrier((d_qkv, ff_sum))
    ff_total = lax.all_gather(ff_sum, plane, axis=0, tiled=True).reshape(8, 2, ff_own, D)
    small = jnp.concatenate(
        [jnp.zeros((1, D), wide), sums[1:2], mlp_sums[0:1], sums[0:1], jnp.zeros((4, D), wide)]
    )
    inputs_grad, pair, two_grads, small = closing(
        d_qkv, w_qkv, inputs, grad_hidden, vecs, rows_all, state_low, d_qkvst,
        os_rows.reshape(256, D), du_rows.reshape(256, D), d_start, dz_sum, small, out_part,
    )
    pair = pair.reshape(2, PAIR_ROWS, D)
    (
        query_grad, key_grad, value_grad, squery_grad, out_grad, sout_grad, up_grad, down_grad,
        state_grad,
    ) = finish_grads(pair, two_grads, ff_total)
    bias_grad = lax.dynamic_slice_in_dim(
        small[4, : LINE * BUCKETS].reshape(4, 2, BUCKETS), lax.axis_index("tensor"), 1, 0
    )[0].T
    return (
        tokens_out,
        state_out[:, None],
        inputs_grad,
        state_grad,
        small[0],
        small[1],
        small[2],
        query_grad,
        key_grad,
        value_grad,
        out_grad,
        squery_grad,
        sout_grad,
        up_grad,
        down_grad,
        bias_grad,
        small[3],
    )


def solution(mesh):
    return jax.shard_map(
        chosen_body(mesh),
        mesh=mesh,
        in_specs=(
            P("dp", ("seq", "tensor"), None),
            P("dp", "seq"),
            P("dp"),
            P("tensor", None),
            P(),
            P(),
            P(),
            P(None, "tensor"),
            P(None, "tensor"),
            P(None, "tensor"),
            P("tensor", None),
            P(None, "tensor"),
            P("tensor", None),
            P(None, "tensor"),
            P("tensor", None),
            P(None, "tensor"),
            P(),
            P("dp", ("seq", "tensor"), None),
            P("dp", "seq", "tensor", None),
        ),
        out_specs=(
            P("dp", ("seq", "tensor"), None),
            P("dp", "seq", "tensor", None),
            P("dp", ("seq", "tensor"), None),
            P("tensor", None),
            P(),
            P(),
            P(),
            P(None, "tensor"),
            P(None, "tensor"),
            P(None, "tensor"),
            P("tensor", None),
            P(None, "tensor"),
            P("tensor", None),
            P(None, "tensor"),
            P("tensor", None),
            P(None, "tensor"),
            P(),
        ),
        check_vma=False,
    )
```

```python
import jax
import jax.numpy as jnp
from jax import lax
from jax.experimental import pallas as pl
from jax.experimental.pallas import tpu as pltpu
from jax.sharding import PartitionSpec as P

D = 1024
HEAD_DIM = 128
STATES = 512
BLOCK = 512
SEG = 256
BUCKETS = 32


norm_eps = 1e-06
masked_score = -1e30
bucket_edges = (12, 16, 23, 32, 46, 64, 91)


def passed_along(value, axis, steps):
    count = lax.axis_size(axis)
    leading, last = (max(0, -steps), min(count, count - steps))
    return lax.ppermute(value, axis, [(source, source + steps) for source in range(leading, last)])


def bucket_of(relative):
    distance = jnp.abs(relative)
    far_bucket = 8 + sum(((distance >= boundary).astype(jnp.int32) for boundary in bucket_edges))
    near_far = jnp.where(distance < 8, distance, far_bucket)
    return near_far + 16 * (relative > 0).astype(jnp.int32)


def token_mask(seg_start, seq_length, block_index):
    positions = jnp.arange(BLOCK)
    offset = block_index * BLOCK
    prev_valid = (block_index > 0) & (offset - BLOCK + positions < seq_length)
    cur_valid = offset + positions < seq_length
    inside = (positions >= seg_start) & (positions < seg_start + SEG)
    prev_mask = (positions[None, :] > positions[:, None]) & prev_valid[None, :]
    cur_mask = (
        (positions[None, :] <= positions[:, None]) | inside[None, :] & inside[:, None]
    ) & cur_valid[None, :]
    state_mask = jnp.ones((BLOCK, STATES), jnp.bool_)
    return jnp.concatenate([prev_mask, cur_mask, state_mask], axis=1)


def state_mask_of(valid_blk):
    batch_count = valid_blk.shape[0]
    block_part = jnp.broadcast_to(valid_blk[:, None, :], (batch_count, STATES, BLOCK))
    return jnp.concatenate([block_part, jnp.ones((batch_count, STATES, STATES), jnp.bool_)], axis=2)


def layer_norm(values, gain_vec):
    centered = values - jnp.mean(values, axis=-1, keepdims=True)
    spread = jnp.mean(centered * centered, axis=-1, keepdims=True)
    return centered * lax.rsqrt(spread + norm_eps) * gain_vec


def norm_back(values, gain_vec, grad_out):
    _, pullback = jax.vjp(layer_norm, values, gain_vec)
    return pullback(grad_out)


def gelu_back(pre_act, grad_out):
    _, pullback = jax.vjp(jax.nn.gelu, pre_act)
    return pullback(grad_out)[0]


def to_low(array_in):
    return array_in.astype(jnp.bfloat16)


def matmul(left, right):
    return jnp.einsum("...k,kn->...n", left, right, preferred_element_type=jnp.float32)


def matmul_t(left, right):
    return jnp.einsum("...n,kn->...k", left, right, preferred_element_type=jnp.float32)


def outer_sum(left, right):
    left_flat = left.reshape(-1, left.shape[-1])
    right_flat = right.reshape(-1, right.shape[-1])
    return lax.dot_general(
        left_flat, right_flat, (((0,), (0,)), ((), ())), preferred_element_type=jnp.float32
    )


def gather_rows(values):
    return lax.all_gather(values, "tensor", axis=1, tiled=True)


def sum_rows(terms):
    return lax.psum_scatter(
        terms.astype(jnp.bfloat16), "tensor", scatter_dimension=1, tiled=True
    ).astype(jnp.float32)


def pass_state(rows_now):
    return passed_along(rows_now.astype(jnp.bfloat16), "seq", 1).astype(rows_now.dtype)


def pass_back(grad_now):
    return passed_along(grad_now.astype(jnp.bfloat16), "seq", -1).astype(grad_now.dtype)


def split_heads(rows_in):
    return rows_in.reshape(rows_in.shape[0], rows_in.shape[1] // HEAD_DIM, HEAD_DIM)


def score_block(query_rows, key_all, bias_all, allowed):
    scores = (
        jnp.einsum(
            "qhd,khd->hqk",
            split_heads(query_rows),
            split_heads(key_all),
            preferred_element_type=jnp.float32,
        )
        * HEAD_DIM ** (-0.5)
        + bias_all
    )
    return jnp.where(allowed[None], scores, masked_score)


def attend_forward(query_rows, key_all, value_all, bias_all, allowed):
    scores = score_block(query_rows, key_all, bias_all, allowed)
    row_max = jnp.max(scores, axis=-1, keepdims=True)
    exp_scores = jnp.exp(scores - row_max)
    row_total = jnp.sum(exp_scores, axis=-1, keepdims=True)
    weight_all = to_low(exp_scores / row_total)
    mixed_out = jnp.einsum(
        "hqk,khd->qhd", weight_all, split_heads(value_all), preferred_element_type=jnp.float32
    )
    return (
        to_low(mixed_out.reshape(query_rows.shape[0], -1)),
        (row_max + jnp.log(row_total))[..., 0],
    )


def attend_back(query_rows, key_all, value_all, bias_all, allowed, log_total, grad_mixed):
    scores = score_block(query_rows, key_all, bias_all, allowed)
    weight_all = jnp.where(allowed[None], jnp.exp(scores - log_total[..., None]), 0.0)
    grad_heads = split_heads(grad_mixed)
    grad_weight = jnp.einsum(
        "qhd,khd->hqk", grad_heads, split_heads(value_all), preferred_element_type=jnp.float32
    )
    row_inner = jnp.sum(weight_all * grad_weight, axis=-1, keepdims=True)
    grad_scores = to_low(weight_all * (grad_weight - row_inner))
    grad_query = jnp.einsum(
        "hqk,khd->qhd", grad_scores, split_heads(key_all), preferred_element_type=jnp.float32
    ) * HEAD_DIM ** (-0.5)
    grad_keys = jnp.einsum(
        "hqk,qhd->khd", grad_scores, split_heads(query_rows), preferred_element_type=jnp.float32
    ) * HEAD_DIM ** (-0.5)
    grad_values = jnp.einsum(
        "hqk,qhd->khd", to_low(weight_all), grad_heads, preferred_element_type=jnp.float32
    )
    return (
        grad_query.reshape(query_rows.shape[0], -1),
        grad_keys.reshape(key_all.shape[0], -1),
        grad_values.reshape(key_all.shape[0], -1),
        grad_scores,
    )


def bias_lookup(rel_bias, rel_table):
    table_heads = jnp.zeros((rel_bias.shape[1],) + rel_table.shape, jnp.float32)
    for bucket_id in range(BUCKETS):
        table_heads = table_heads + jnp.where(
            rel_table[None] == bucket_id, rel_bias[bucket_id][:, None, None], 0.0
        )
    return table_heads


def bias_sums(score_grad, rel_table):
    grad_wide = score_grad.astype(jnp.float32)
    columns = []
    for bucket_id in range(BUCKETS):
        columns.append(
            jnp.sum(jnp.where(rel_table[None, None] == bucket_id, grad_wide, 0.0), axis=(0, 2, 3))
        )
    return jnp.stack(columns, axis=0)


def body(
    inputs,
    seg_starts,
    lengths,
    init_state,
    attn_gain,
    state_gain,
    mlp_gain,
    w_query,
    w_key,
    w_value,
    w_out,
    w_squery,
    w_sout,
    w_up,
    w_down,
    rel_bias,
    gate_bias,
    out_cot,
    state_cot,
):
    seq_count = inputs.shape[0]
    chain_length = lax.axis_size("seq")
    block_index = lax.axis_index("seq")
    is_first = block_index == 0
    width_local = w_query.shape[1]
    head_count = width_local // HEAD_DIM
    gate_value = jax.nn.sigmoid(gate_bias)
    positions = jnp.arange(BLOCK)
    inputs_wide = inputs.astype(jnp.float32)
    tokens_low = gather_rows(to_low(layer_norm(inputs_wide, attn_gain)))
    query_tok = to_low(matmul(tokens_low, w_query))
    key_tok = to_low(matmul(tokens_low, w_key))
    value_tok = to_low(matmul(tokens_low, w_value))
    key_prev, value_prev = passed_along((key_tok, value_tok), "seq", 1)
    valid_keys = (block_index * BLOCK + positions)[None, :] < lengths[:, None]
    batched_attend = jax.vmap(attend_forward, in_axes=(0, 0, 0, None, 0))
    batched_back = jax.vmap(attend_back, in_axes=(0, 0, 0, None, 0, 0, 0))

    def state_forward(state_rows, key_blk, value_blk, valid_blk):
        state_low = lax.all_gather(
            to_low(layer_norm(state_rows, state_gain)), "tensor", axis=1, tiled=True
        )
        query_st = to_low(matmul(state_low, w_squery))
        key_st = to_low(matmul(state_low, w_key))
        value_st = to_low(matmul(state_low, w_value))
        key_all = jnp.concatenate([key_blk, key_st], axis=1)
        value_all = jnp.concatenate([value_blk, value_st], axis=1)
        mixed_st, lse_st = batched_attend(
            query_st, key_all, value_all, 0.0, state_mask_of(valid_blk)
        )
        update = lax.psum_scatter(
            matmul(mixed_st, w_sout).astype(jnp.bfloat16), "tensor", scatter_dimension=1, tiled=True
        ).astype(jnp.float32)
        state_next = gate_value * state_rows + (1.0 - gate_value) * update
        return (state_next, (state_low, query_st, key_st, value_st, mixed_st, lse_st, update))

    def state_backward(
        grad_out, state_rows, kept_one, key_blk, value_blk, valid_blk, extra_key, extra_value
    ):
        state_low, query_st, key_st, value_st, mixed_st, lse_st, update = kept_one
        gate_part = (
            jnp.sum(grad_out * (state_rows - update), axis=(0, 1)) * gate_value * (1.0 - gate_value)
        )
        grad_update = lax.all_gather(
            to_low((1.0 - gate_value) * grad_out), "tensor", axis=1, tiled=True
        )
        grad_mixed_st = to_low(matmul_t(grad_update, w_sout))
        sout_part = outer_sum(mixed_st, grad_update)
        key_all = jnp.concatenate([key_blk, key_st], axis=1)
        value_all = jnp.concatenate([value_blk, value_st], axis=1)
        grad_query_st, grad_keys_st, grad_values_st, _ = batched_back(
            query_st, key_all, value_all, 0.0, state_mask_of(valid_blk), lse_st, grad_mixed_st
        )
        query_low = to_low(grad_query_st)
        key_low = to_low(grad_keys_st[:, BLOCK:] + extra_key)
        value_low = to_low(grad_values_st[:, BLOCK:] + extra_value)
        squery_part = outer_sum(state_low, query_low)
        key_part = outer_sum(state_low, key_low)
        value_part = outer_sum(state_low, value_low)
        terms = (
            matmul_t(query_low, w_squery) + matmul_t(key_low, w_key) + matmul_t(value_low, w_value)
        )
        grad_normed = lax.psum_scatter(
            terms.astype(jnp.bfloat16), "tensor", scatter_dimension=1, tiled=True
        ).astype(jnp.float32)
        grad_rows_norm, gain_part = norm_back(state_rows, state_gain, grad_normed)
        grad_in = gate_value * grad_out + grad_rows_norm
        block_grads = (grad_keys_st[:, :BLOCK], grad_values_st[:, :BLOCK])
        return (
            grad_in,
            block_grads,
            (squery_part, key_part, value_part, sout_part, gain_part, gate_part),
        )

    zeros_rows = jnp.zeros((seq_count,) + init_state.shape, jnp.float32)
    narrow_zero = jnp.zeros((seq_count, STATES, width_local), jnp.bfloat16)
    stored_start = (
        zeros_rows,
        zeros_rows,
        jnp.zeros((seq_count, STATES, D), jnp.bfloat16),
        narrow_zero,
        narrow_zero,
        narrow_zero,
        narrow_zero,
        jnp.zeros((seq_count, head_count, STATES), jnp.float32),
        zeros_rows,
    )

    def forward_turn(turn_index, carry):
        incoming, stored_now = carry
        order_index = turn_index - block_index
        is_live = (order_index >= 0) & (order_index < seq_count)
        picked = jnp.clip(order_index, 0, seq_count - 1)
        rows_now = jnp.where(is_first, init_state[None], incoming)
        key_one = lax.dynamic_slice_in_dim(key_tok, picked, 1, 0)
        value_one = lax.dynamic_slice_in_dim(value_tok, picked, 1, 0)
        valid_one = lax.dynamic_slice_in_dim(valid_keys, picked, 1, 0)
        rows_next, kept_one = state_forward(rows_now, key_one, value_one, valid_one)
        fresh = (rows_now, rows_next) + kept_one
        stored_now = tuple(
            (
                jnp.where(
                    is_live,
                    lax.dynamic_update_slice_in_dim(whole_array, fresh_part, picked, 0),
                    whole_array,
                )
                for whole_array, fresh_part in zip(stored_now, fresh)
            )
        )
        return (pass_state(rows_next), stored_now)

    incoming_start = jnp.zeros((1,) + init_state.shape, jnp.float32)
    _, stored_all = lax.fori_loop(
        0, chain_length + seq_count - 1, forward_turn, (incoming_start, stored_start)
    )
    state_in = stored_all[0]
    state_out = stored_all[1]
    kept = stored_all[2:]
    key_all_tok = jnp.concatenate([key_prev, key_tok, kept[2]], axis=1)
    value_all_tok = jnp.concatenate([value_prev, value_tok, kept[3]], axis=1)
    allowed_tok = jax.vmap(token_mask, in_axes=(0, 0, None))(seg_starts[:, 0], lengths, block_index)
    rel_table = bucket_of((jnp.arange(2 * BLOCK) - BLOCK)[None, :] - positions[:, None])
    full_bias = jnp.concatenate(
        [bias_lookup(rel_bias, rel_table), jnp.zeros((head_count, BLOCK, STATES), jnp.float32)],
        axis=2,
    )
    mixed_tok, lse_tok = batched_attend(
        query_tok, key_all_tok, value_all_tok, full_bias, allowed_tok
    )
    hidden_in = inputs_wide + sum_rows(matmul(mixed_tok, w_out))
    mid_low = gather_rows(to_low(layer_norm(hidden_in, mlp_gain)))
    pre_act = matmul(mid_low, w_up)
    hidden_low = to_low(jax.nn.gelu(pre_act))
    mlp_rows = sum_rows(matmul(hidden_low, w_down))
    tokens_out = (hidden_in + mlp_rows).astype(jnp.bfloat16)
    cot_wide = out_cot.astype(jnp.float32)
    cot_used = gather_rows(out_cot)
    grad_hidden_act = matmul_t(cot_used, w_down)
    down_grad = outer_sum(hidden_low, cot_used)
    grad_pre = to_low(gelu_back(pre_act, grad_hidden_act))
    up_grad = outer_sum(mid_low, grad_pre)
    grad_normed_mid = sum_rows(matmul_t(grad_pre, w_up))
    grad_mid_in, mlp_gain_grad = norm_back(hidden_in, mlp_gain, grad_normed_mid)
    grad_hidden = cot_wide + grad_mid_in
    grad_attn_low = gather_rows(to_low(grad_hidden))
    grad_mixed = to_low(matmul_t(grad_attn_low, w_out))
    out_grad = outer_sum(mixed_tok, grad_attn_low)
    grad_query_tok, grad_keys_tok, grad_values_tok, grad_scores = batched_back(
        query_tok, key_all_tok, value_all_tok, full_bias, allowed_tok, lse_tok, grad_mixed
    )
    bias_grad = bias_sums(grad_scores[..., : 2 * BLOCK], rel_table)
    grad_key_next, grad_value_next = (
        passed_along(grad_keys_tok[:, :BLOCK].astype(jnp.bfloat16), "seq", -1).astype(jnp.float32),
        passed_along(grad_values_tok[:, :BLOCK].astype(jnp.bfloat16), "seq", -1).astype(
            jnp.float32
        ),
    )
    grad_key_own = grad_keys_tok[:, BLOCK : 2 * BLOCK] + grad_key_next
    grad_value_own = grad_values_tok[:, BLOCK : 2 * BLOCK] + grad_value_next
    grad_key_st_tok = grad_keys_tok[:, 2 * BLOCK :]
    grad_value_st_tok = grad_values_tok[:, 2 * BLOCK :]
    cot_rows = state_cot[:, 0].astype(jnp.float32)
    wide_zero = jnp.zeros((seq_count, BLOCK, width_local), jnp.float32)
    stored_back = (zeros_rows, wide_zero, wide_zero)
    totals_start = (
        jnp.zeros((D, width_local), jnp.float32),
        jnp.zeros((D, width_local), jnp.float32),
        jnp.zeros((D, width_local), jnp.float32),
        jnp.zeros((width_local, D), jnp.float32),
        jnp.zeros((D,), jnp.float32),
        jnp.zeros((D,), jnp.float32),
    )

    def backward_turn(turn_index, carry):
        incoming, stored_now, totals_now = carry
        order_index = turn_index - (chain_length - 1 - block_index)
        is_live = (order_index >= 0) & (order_index < seq_count)
        picked = jnp.clip(order_index, 0, seq_count - 1)

        def slice_one(whole_array):
            return lax.dynamic_slice_in_dim(whole_array, picked, 1, 0)

        grad_out = slice_one(cot_rows) + incoming
        kept_one = tuple((slice_one(kept_array) for kept_array in kept))
        grad_in, block_one, parts_one = state_backward(
            grad_out,
            slice_one(state_in),
            kept_one,
            slice_one(key_tok),
            slice_one(value_tok),
            slice_one(valid_keys),
            slice_one(grad_key_st_tok),
            slice_one(grad_value_st_tok),
        )
        fresh = (grad_in,) + block_one
        stored_now = tuple(
            (
                jnp.where(
                    is_live,
                    lax.dynamic_update_slice_in_dim(whole_array, fresh_part, picked, 0),
                    whole_array,
                )
                for whole_array, fresh_part in zip(stored_now, fresh)
            )
        )
        totals_now = tuple(
            (
                total_now + jnp.where(is_live, part_now, 0.0)
                for total_now, part_now in zip(totals_now, parts_one)
            )
        )
        return (pass_back(grad_in), stored_now, totals_now)

    incoming_start = jnp.zeros((1,) + init_state.shape, jnp.float32)
    _, stored_done, weight_parts = lax.fori_loop(
        0, chain_length + seq_count - 1, backward_turn, (incoming_start, stored_back, totals_start)
    )
    grad_in_all, grad_key_blk, grad_value_blk = stored_done
    query_low = to_low(grad_query_tok)
    key_low = to_low(grad_key_own + grad_key_blk)
    value_low = to_low(grad_value_own + grad_value_blk)
    query_grad = outer_sum(tokens_low, query_low)
    key_grad = outer_sum(tokens_low, key_low) + weight_parts[1]
    value_grad = outer_sum(tokens_low, value_low) + weight_parts[2]
    grad_tokens = sum_rows(
        matmul_t(query_low, w_query) + matmul_t(key_low, w_key) + matmul_t(value_low, w_value)
    )
    grad_in_norm, attn_gain_grad = norm_back(inputs_wide, attn_gain, grad_tokens)
    inputs_grad = grad_hidden + grad_in_norm
    state_part = jnp.where(is_first, jnp.sum(grad_in_all, axis=0), 0.0)
    gains = lax.psum(
        jnp.stack([attn_gain_grad, weight_parts[4], mlp_gain_grad, weight_parts[5]]), "tensor"
    )
    totals = (
        lax.psum(query_grad.astype(jnp.bfloat16), ("dp", "seq")).astype(jnp.float32),
        lax.psum(key_grad.astype(jnp.bfloat16), ("dp", "seq")).astype(jnp.float32),
        lax.psum(value_grad.astype(jnp.bfloat16), ("dp", "seq")).astype(jnp.float32),
        lax.psum(out_grad.astype(jnp.bfloat16), ("dp", "seq")).astype(jnp.float32),
        lax.psum(weight_parts[0].astype(jnp.bfloat16), ("dp", "seq")).astype(jnp.float32),
        lax.psum(weight_parts[3].astype(jnp.bfloat16), ("dp", "seq")).astype(jnp.float32),
        lax.psum(up_grad.astype(jnp.bfloat16), ("dp", "seq")).astype(jnp.float32),
        lax.psum(down_grad.astype(jnp.bfloat16), ("dp", "seq")).astype(jnp.float32),
        lax.psum(bias_grad.astype(jnp.bfloat16), ("dp", "seq")).astype(jnp.float32),
        lax.psum(state_part.astype(jnp.bfloat16), ("dp", "seq")).astype(jnp.float32),
        lax.psum(gains.astype(jnp.bfloat16), ("dp", "seq")).astype(jnp.float32),
    )
    gain_total = totals[10]
    return (
        tokens_out,
        state_out[:, None],
        inputs_grad,
        totals[9],
        gain_total[0],
        gain_total[1],
        gain_total[2],
        totals[0],
        totals[1],
        totals[2],
        totals[3],
        totals[4],
        totals[5],
        totals[6],
        totals[7],
        totals[8],
        gain_total[3],
    )


def chosen_body(mesh):
    if mesh.shape["seq"] == 4 and mesh.shape["tensor"] == 4:
        return line_body
    return body


MESH_ID = pl.DeviceIdType.MESH
ROWS = 128
CHUNKS = BLOCK // ROWS
LINE = 8
SCALE = HEAD_DIM ** (-0.5)
VMEM_LIMIT = 60 * 1024 * 1024


def dot_nn(left, right):
    return lax.dot_general(left, right, (((1,), (0,)), ((), ())), preferred_element_type=jnp.float32)


def dot_nt(left, right):
    return lax.dot_general(left, right, (((1,), (1,)), ((), ())), preferred_element_type=jnp.float32)


def dot_tn(left, right):
    return lax.dot_general(left, right, (((0,), (0,)), ((), ())), preferred_element_type=jnp.float32)


def line_place():
    place = lax.axis_index("seq")
    half = lax.rem(place, 2)
    rank = lax.axis_index("tensor")
    return place, half, rank


def span(index, size):
    return pl.ds(pl.multiple_of(index * size, size), size)


def fetch_pieces(kept, first, rows, target, sem):
    for owner in range(8):
        pltpu.make_async_copy(
            kept.at[owner, :, pl.ds(first, rows), :], target.at[:, owner], sem
        ).start()


def fetch_columns(weights, target, sem):
    half = lax.rem(lax.axis_index("seq"), 2)
    for index, weight in enumerate(weights):
        pltpu.make_async_copy(
            weight.at[:, span(half, 128)], target.at[:, pl.ds(128 * index, 128)], sem
        ).start()


def fetched(target, sem):
    pltpu.make_async_copy(target, target, sem).wait()


def norm_parts(rows):
    centered = rows - jnp.mean(rows, axis=-1, keepdims=True)
    spread = jnp.mean(centered * centered, axis=-1, keepdims=True)
    return centered, lax.rsqrt(spread + norm_eps)


def mark(marks, block_id, row):
    return marks[block_id, pl.ds(row, 1), 0:1]


def sequence_marks(marks, block_id):
    mine = lax.axis_index("seq") // 2
    return mark(marks, block_id, mine), mark(marks, 0, 2 + mine)


def token_masks(marks, block_id, first_row):
    start, length = sequence_marks(marks, block_id)
    row = lax.broadcasted_iota(jnp.int32, (ROWS, BLOCK), 0) + first_row
    col = lax.broadcasted_iota(jnp.int32, (ROWS, BLOCK), 1)
    prev_limit = jnp.where(block_id > 0, length - (block_id - 1) * BLOCK, 0)
    prev_ok = (col > row) & (col < prev_limit)
    row_in = (row >= start) & (row < start + SEG)
    col_in = (col >= start) & (col < start + SEG)
    cur_ok = ((col <= row) | (row_in & col_in)) & (col < length - block_id * BLOCK)
    return prev_ok, cur_ok


def state_block_mask(marks, block_id):
    _, length = sequence_marks(marks, block_id)
    col = lax.broadcasted_iota(jnp.int32, (ROWS, BLOCK), 1)
    return col < length - block_id * BLOCK


def softmax_of(score_parts):
    top = jnp.max(score_parts[0], axis=-1, keepdims=True)
    for part in score_parts[1:]:
        top = jnp.maximum(top, jnp.max(part, axis=-1, keepdims=True))
    raised = [jnp.exp(part - top) for part in score_parts]
    total = jnp.sum(raised[0], axis=-1, keepdims=True)
    for part in raised[1:]:
        total = total + jnp.sum(part, axis=-1, keepdims=True)
    inverse = 1.0 / total
    return [to_low(part * inverse) for part in raised], top + jnp.log(total)


def token_scores(scal, qkv, qkvst, bias, block_id, chunk):
    rows = span(chunk, ROWS)
    prev_id = jnp.maximum(block_id - 1, 0)
    query = qkv[block_id, rows, 0:128]
    prev_ok, cur_ok = token_masks(scal, block_id, chunk * ROWS)
    prev = dot_nt(query, qkv[prev_id, :, 128:256]) * SCALE + bias[rows, 0:BLOCK]
    cur = dot_nt(query, qkv[block_id, :, 128:256]) * SCALE + bias[rows, BLOCK : 2 * BLOCK]
    stt = dot_nt(query, qkvst[block_id, :, 128:256]) * SCALE
    prev = jnp.where(prev_ok, prev, masked_score)
    cur = jnp.where(cur_ok, cur, masked_score)
    return query, (prev, cur, stt)


def state_scores(scal, qkv, qkvst, block_id, chunk):
    query = qkvst[block_id, span(chunk, ROWS), 0:128]
    tok = dot_nt(query, qkv[block_id, :, 128:256]) * SCALE
    tok = jnp.where(state_block_mask(scal, block_id), tok, masked_score)
    stt = dot_nt(query, qkvst[block_id, :, 128:256]) * SCALE
    return query, (tok, stt)


HALVES = 2
HALF_ROWS = STATES // HALVES
HALF_CHUNKS = HALF_ROWS // ROWS


def forward_kernel(
    marks, qkv, kept, w_squery, w_qkv, vecs, bias, state_cot, back_own,
    o_out, lse_out, state_rows, low_out, qkvst, lse_st, os_rows, cots, back,
    held, os_all, state_low, w_sout, start, w_state,
    way_send, core_send, recv_sem, local_sem, low_sem, cot_send, cot_recv,
    piece_send, piece_recv, ring_send, ring_recv,
):
    side, place, half, rank = plane_place()
    me = plane_index(side, place)
    partner = place + 1 - 2 * half
    head = 2 * rank + half
    fetch_pieces(kept, 32, 16, start, local_sem.at[0])
    fetch_columns((w_squery,), w_state, local_sem.at[2])
    fetch_pieces(kept, 0, 32, w_sout, local_sem.at[1])
    own_cot = pltpu.make_async_copy(state_cot.at[place], cots.at[place], local_sem.at[4])
    own_cot.start()
    own_piece = pltpu.make_async_copy(back_own, back.at[me, rank], local_sem.at[3])
    own_piece.start()
    ranks = [lax.rem(rank + step, 4) for step in (1, 2, 3)]
    seats = [lax.rem(place + step, 4) for step in (1, 2, 3)]
    barrier = pltpu.get_barrier_semaphore()
    for target in [{"tensor": one} for one in ranks] + [{"seq": one} for one in seats] + [
        {"dp": 1 - side}
    ]:
        pl.semaphore_signal(barrier, inc=1, device_id=target, device_id_type=MESH_ID)
    fetched(start, local_sem.at[0])
    held[...] = start[...].reshape(STATES, D).astype(jnp.float32)
    gain = vecs[0:1, :]
    gate = vecs[1:2, :]
    fetched(w_state, local_sem.at[2])

    def project(block_id, part):
        def one(chunk, _):
            rows = span(chunk, ROWS)
            centered, scale = norm_parts(held[rows, :])
            low = to_low(centered * scale * gain)
            state_low[block_id, rows, :] = low
            qkvst[block_id, rows, 0:128] = to_low(dot_nn(low, w_state[...]))
            qkvst[block_id, rows, 128:384] = to_low(dot_nn(low, w_qkv[:, 128:384]))
            return 0

        lax.fori_loop(HALF_CHUNKS * part, HALF_CHUNKS * (part + 1), one, 0)

    pl.semaphore_wait(barrier, 7)

    def piece_move(origin, part, slot, target):
        return pltpu.make_async_remote_copy(
            src_ref=back_own.at[part],
            dst_ref=back.at[me, origin, part],
            send_sem=piece_send.at[part, slot],
            recv_sem=piece_recv.at[part, origin],
            device_id={"tensor": target},
            device_id_type=MESH_ID,
        )

    def send_piece(part):
        for slot, target in enumerate(ranks):
            piece_move(rank, part, slot, target).start()

    gather = plane_gather(
        lambda owner, part: back.at[owner, pl.ds(2 * part, 2)], ring_send, ring_recv
    )
    next(gather)
    send_piece(0)
    for part in range(HALVES):
        project(0, part)
    right, left = {"tensor": lax.rem(rank + 1, 4)}, {"tensor": lax.rem(rank + 3, 4)}

    def moved(block_id, part, which, sem, target):
        view = os_all.at[block_id, pl.ds(HALF_ROWS * part, HALF_ROWS), span(which, 128)]
        return pltpu.make_async_remote_copy(
            src_ref=view,
            dst_ref=view,
            send_sem=sem,
            recv_sem=recv_sem.at[block_id, part, which],
            device_id=target,
            device_id_type=MESH_ID,
        )

    def cot_move(index, origin, slot, target):
        return pltpu.make_async_remote_copy(
            src_ref=state_cot.at[index],
            dst_ref=cots.at[origin],
            send_sem=cot_send.at[slot],
            recv_sem=cot_recv.at[origin],
            device_id={"seq": target},
            device_id_type=MESH_ID,
        )

    for slot, target in enumerate(seats):
        cot_move(target, place, slot, target).start()
    fetched(w_sout, local_sem.at[1])

    def origin_of(way, distance):
        if way == 0:
            return jnp.maximum(rank - distance, 0)
        return jnp.minimum(rank + distance, 3)

    def ways(distance):
        return (
            (0, rank >= distance, (rank >= distance) & (rank < 3), right),
            (1, rank + distance <= 3, (rank + distance <= 3) & (rank > 0), left),
        )

    def relay(block_id, part, distance, waiting):
        for way, comes, goes, target in ways(distance):
            which = 2 * origin_of(way, distance) + half
            sem = way_send.at[block_id, part, min(distance, 2), way]
            core_sem = core_send.at[block_id, part, which // 2]
            if distance > 0:

                @pl.when(comes)
                def _():
                    to_core = moved(block_id, part, which, core_sem, {"seq": partner})
                    if waiting:
                        moved(block_id, part, which, sem, target).wait_recv()
                        to_core.start()
                    else:
                        to_core.wait_send()

            if distance < 3:

                @pl.when(goes)
                def _():
                    one = moved(block_id, part, which, sem, target)
                    if waiting:
                        one.start()
                    else:
                        one.wait_send()

        if distance == 0:
            mine = moved(
                block_id, part, head, core_send.at[block_id, part, rank], {"seq": partner}
            )
            if waiting:
                mine.start()
            else:
                mine.wait_send()

    def one_block(block_id, _):
        def attend_state(chunk, _):
            rows = span(chunk, ROWS)
            _, parts = state_scores(marks, qkv, qkvst, block_id, chunk)
            (w_tok, w_stt), total = softmax_of(parts)
            mixed = dot_nn(w_tok, qkv[block_id, :, 256:384]) + dot_nn(
                w_stt, qkvst[block_id, :, 256:384]
            )
            os_all[block_id, rows, span(head, 128)] = to_low(mixed)
            lse_st[block_id, rows, :] = total
            return 0

        def attend_token(chunk, _):
            rows = span(chunk, ROWS)
            _, parts = token_scores(marks, qkv, qkvst, bias, block_id, chunk)
            weights, total = softmax_of(parts)
            prev_id = jnp.maximum(block_id - 1, 0)
            mixed = (
                dot_nn(weights[0], qkv[prev_id, :, 256:384])
                + dot_nn(weights[1], qkv[block_id, :, 256:384])
                + dot_nn(weights[2], qkvst[block_id, :, 256:384])
            )
            o_out[block_id, rows, :] = to_low(mixed)
            lse_out[block_id, rows, :] = total
            return 0

        def attend_both(part, _):
            lax.fori_loop(HALF_CHUNKS * part, HALF_CHUNKS * (part + 1), attend_state, 0)
            for value in range(HALVES):

                @pl.when(part == value)
                def _():
                    relay(block_id, value, 0, True)

            return 0

        lax.fori_loop(0, HALVES, attend_both, 0)
        pltpu.make_async_copy(
            state_low.at[block_id], low_out.at[block_id], low_sem.at[block_id]
        ).start()

        @pl.when(block_id == 2)
        def _():
            own_piece.wait()
            for part in range(3):
                for slot, target in enumerate(ranks):
                    piece_move(target, part, slot, target).wait_recv()
            next(gather)

        @pl.when(block_id == 3)
        def _():
            next(gather)
            next(gather)

        def between(step, _):
            for value, (distance, part) in enumerate(((1, 0), (1, 1), (2, 0), (2, 1))):

                @pl.when(step == value)
                def _():
                    relay(block_id, part, distance, True)

            return attend_token(step, 0)

        lax.fori_loop(0, 4, between, 0)

        def settle(part, _):
            for value in range(HALVES):

                @pl.when(part == value)
                def _():
                    relay(block_id, value, 3, True)
                    for origin in range(4):
                        moved(
                            block_id, value, 2 * origin + 1 - half,
                            core_send.at[block_id, value, origin], {"seq": partner},
                        ).wait_recv()

                    if value == HALVES - 1:
                        for turn in (0, 1):

                            @pl.when(block_id == turn)
                            def _():
                                send_piece(turn + 1)

            def update(chunk, _):
                rows = span(chunk, ROWS)
                change = dot_nn(os_all[block_id, rows, :], w_sout[...].reshape(D, D))
                held[rows, :] = gate * held[rows, :] + (1.0 - gate) * change
                return 0

            lax.fori_loop(HALF_CHUNKS * part, HALF_CHUNKS * (part + 1), update, 0)

            @pl.when(block_id < 3)
            def _():
                project(block_id + 1, part)

            return 0

        lax.fori_loop(0, HALVES, settle, 0)
        state_rows[block_id] = held[span(rank, 128), :]
        os_rows[block_id] = os_all[block_id, span(head, 64), :]
        return 0

    lax.fori_loop(0, 4, one_block, 0)

    def drain(block_id, _):
        for part in range(HALVES):
            for distance in range(4):
                relay(block_id, part, distance, False)
        pltpu.make_async_copy(
            state_low.at[block_id], low_out.at[block_id], low_sem.at[block_id]
        ).wait()
        return 0

    lax.fori_loop(0, 4, drain, 0)
    own_cot.wait()
    for part in range(3):
        for slot, target in enumerate(ranks):
            piece_move(rank, part, slot, target).wait_send()
    for _ in gather:
        pass
    for slot, target in enumerate(seats):
        cot_move(target, place, slot, target).wait_send()
        cot_move(place, target, slot, target).wait_recv()


def any_specs(count):
    return [pl.BlockSpec(memory_space=pl.ANY)] * count


def vmem_specs(count):
    return [pl.BlockSpec(memory_space=pltpu.VMEM)] * count


def forward_chain(
    marks, qkv, kept, w_squery, w_qkv, vecs, bias, state_cot, back_own
):
    low, wide = jnp.bfloat16, jnp.float32
    shapes = (
        ((4, BLOCK, 128), low),
        ((4, BLOCK, 1), wide),
        ((4, 128, D), wide),
        ((4, STATES, D), low),
        ((4, STATES, 384), low),
        ((4, STATES, 1), wide),
        ((4, 64, D), low),
        ((4, 64, D), low),
        ((8, 4, 3, 32, D), low),
    )
    dma = pltpu.SemaphoreType.DMA
    return pl.pallas_call(
        forward_kernel,
        out_shape=[jax.ShapeDtypeStruct(*one) for one in shapes],
        in_specs=vmem_specs(2) + any_specs(2) + vmem_specs(3) + any_specs(2),
        out_specs=vmem_specs(3) + any_specs(1) + vmem_specs(3) + any_specs(2),
        scratch_shapes=[
            pltpu.VMEM((STATES, D), wide),
            pltpu.VMEM((4, STATES, D), low),
            pltpu.VMEM((4, STATES, D), low),
            pltpu.VMEM((4, 8, 32, D), low),
            pltpu.VMEM((4, 8, 16, D), low),
            pltpu.VMEM((D, 128), low),
            dma((4, HALVES, 3, 2)),
            dma((4, HALVES, 4)),
            dma((4, HALVES, 8)),
            dma((5,)),
            dma((4,)),
            dma((3,)),
            dma((4,)),
            dma((3, 3)),
            dma((3, 4)),
            dma((14,)),
            dma((8, 2)),
        ],
        compiler_params=pltpu.CompilerParams(
            collective_id=1, has_side_effects=True, vmem_limit_bytes=VMEM_LIMIT
        ),
        cost_estimate=pl.CostEstimate(
            flops=60000000000, bytes_accessed=60000000, transcendentals=0
        ),
        name="forward_chain",
    )(marks, qkv, kept, w_squery, w_qkv, vecs, bias, state_cot, back_own)


def backward_kernel(
    scal, qkv, d_o, lse_tok, qkvst, lse_st, state_rows, begin, cots, back, kept, vecs, bias,
    extra, hidden, rows_hbm, low_hbm, w_qkv,
    du_rows, d_start, sums, state_out, tokens_out, out_part, partial, pair_grads,
    dz_sum, diag, d_qkv, d_qkvst, rows_buf, low_buf, leave, came, grad_acc,
    key_acc, value_acc, st_key, st_value, dos_rows, dos_got, d_got, grad_in,
    states, w_back, w_sout, work, core_got, near_got, far_got, total,
    send_sem, recv_sem, local_sem, side_sem, ring_send, ring_recv, buf_sem, core_sem, came_sem,
):
    place, half, rank = line_place()
    own_rows = pl.ds(pl.multiple_of(half * 64, 64), 64)
    loads = [
        pltpu.make_async_copy(
            state_rows.at[:, own_rows, :], states.at[pl.ds(1, 4)], local_sem.at[0]
        ),
        pltpu.make_async_copy(
            state_rows.at[place], state_out.at[place // 2], local_sem.at[3]
        ),
        pltpu.make_async_copy(extra, work, local_sem.at[4]),
    ]
    for one in loads:
        one.start()
    fetch_pieces(kept, 0, 32, w_sout, local_sem.at[1])
    for owner in range(8):
        pltpu.make_async_copy(
            back.at[owner], w_back.at[:, owner // 4, :, owner % 4], local_sem.at[2]
        ).start()
    states[0] = to_low(begin[own_rows, :]).astype(jnp.float32)

    def block_loads(block_id):
        slot = lax.rem(block_id, 2)
        return [
            pltpu.make_async_copy(
                source.at[block_id], target.at[slot], buf_sem.at[index, slot]
            )
            for index, (source, target) in enumerate(((rows_hbm, rows_buf), (low_hbm, low_buf)))
        ]

    for one in block_loads(3):
        one.start()
    head = 2 * rank + half
    peers = []
    for step in range(1, LINE):
        other = lax.rem(head + step, LINE)
        peers.append((other, place - half + lax.rem(other, 2), other // 2))
    barrier = pltpu.get_barrier_semaphore()
    for _, seq_to, rank_to in peers:
        pl.semaphore_signal(
            barrier, inc=1, device_id={"seq": seq_to, "tensor": rank_to}, device_id_type=MESH_ID
        )
    beside = lax.rem(place + 2, 4)
    pl.semaphore_signal(barrier, inc=1, device_id={"seq": beside}, device_id_type=MESH_ID)
    pl.semaphore_signal(
        barrier, inc=1, device_id={"dp": 1 - lax.axis_index("dp")}, device_id_type=MESH_ID
    )
    plane_steps = plane_scatter(
        work, core_got, near_got, far_got, total, 384, ring_send, ring_recv
    )
    next(plane_steps)

    def aside(block_id, row_set):
        return pltpu.make_async_remote_copy(
            src_ref=state_rows.at[block_id],
            dst_ref=state_out.at[row_set],
            send_sem=side_sem.at[0],
            recv_sem=side_sem.at[1],
            device_id={"seq": beside},
            device_id_type=MESH_ID,
        )

    gain = vecs[0:1, :]
    gate = vecs[1:2, :]
    key_acc[...] = jnp.zeros_like(key_acc)
    value_acc[...] = jnp.zeros_like(value_acc)
    dz_sum[...] = jnp.zeros_like(dz_sum)
    sums[...] = jnp.zeros_like(sums)
    grad_in[...] = jnp.zeros_like(grad_in)
    grad_acc[...] = jnp.zeros_like(grad_acc)
    core = place + 1 - 2 * half

    def place_in(block_id, owner):
        return jnp.where(block_id == owner, 1, 0)

    def leaving(slot):
        return pltpu.make_async_remote_copy(
            src_ref=leave.at[slot],
            dst_ref=came.at[slot],
            send_sem=core_sem.at[slot],
            recv_sem=came_sem.at[slot],
            device_id={"seq": core},
            device_id_type=MESH_ID,
        )

    def add_came(slot):
        leaving(slot).wait_recv()

        def one(chunk, _):
            partial[slot, chunk] = to_low(
                partial[slot, chunk].astype(jnp.float32)
                + came[slot, span(chunk, 128), :].astype(jnp.float32)
            )
            return 0

        lax.fori_loop(0, 4, one, 0)

    def bucket_sums():
        diag[...] = jnp.zeros_like(diag)

        def one(group, _):
            rows = dz_sum[span(group, 8), :]
            wide = jnp.concatenate([rows, jnp.zeros((8, WIDE - 2 * BLOCK), jnp.float32)], axis=1)
            diag[...] += pltpu.roll(wide, lax.rem(WIDE - 8 * group, WIDE), 1)
            return 0

        lax.fori_loop(0, BLOCK // 8, one, 0)
        line = diag[...]
        row = lax.broadcasted_iota(jnp.int32, (8, WIDE), 0)
        for step in (1, 2, 4):
            line = jnp.where(row // step % 2 == 1, pltpu.roll(line, WIDE - step, 1), line)
        lane = lax.broadcasted_iota(jnp.int32, (8, WIDE), 1)
        bucket_ids = bucket_of(jnp.where(lane >= WIDE - BLOCK, lane - WIDE - BLOCK, lane - BLOCK))
        spot = lax.broadcasted_iota(jnp.int32, (1, 256), 1) - BUCKETS * head
        placed = jnp.zeros((1, 256), jnp.float32)
        for bucket_id in range(BUCKETS):
            chosen = jnp.where(bucket_ids == bucket_id, line, 0.0)
            value = jnp.sum(jnp.sum(chosen, axis=0, keepdims=True), axis=1, keepdims=True)
            placed = jnp.where(spot == bucket_id, value, placed)
        sums[2:3, 0:256] = placed

    def block_products(block_id):
        slot = lax.rem(block_id, 2)
        for one in block_loads(block_id):
            one.wait()

        @pl.when(block_id > 0)
        def _():
            for one in block_loads(jnp.maximum(block_id - 1, 0)):
                one.start()

        def one_part(part, _):
            rows = span(part, 128)

            @pl.when(part < 3)
            def _():
                grad_acc[rows, :] += dot_tn(
                    d_qkv[block_id, :, span(jnp.minimum(part, 2), 128)], rows_buf[slot]
                )

            @pl.when(part > 0)
            def _():
                grad_acc[rows, :] += dot_tn(
                    d_qkvst[block_id, :, span(lax.rem(part, 3), 128)], low_buf[slot]
                )

            return 0

        lax.fori_loop(0, 4, one_part, 0)
        kept_here = lax.rem(block_id, 2) == half
        mine_slot, core_slot = place_in(block_id, place), place_in(block_id, core)

        def one_chunk(chunk, _):
            rows = span(chunk, 128)
            value = to_low(dot_nt(d_qkv[block_id, rows, :], w_qkv[...]))

            @pl.when(kept_here)
            def _():
                partial[mine_slot, chunk] = value

            @pl.when(jnp.logical_not(kept_here))
            def _():
                leave[core_slot, rows, :] = value

            return 0

        lax.fori_loop(0, 4, one_chunk, 0)

        @pl.when(jnp.logical_not(kept_here))
        def _():
            leaving(core_slot).start()

    def back_parts(parts, total, grad, values):
        weights = [jnp.exp(part - total) for part in parts]
        d_weights = [dot_nt(grad, value) for value in values]
        inner = jnp.sum(weights[0] * d_weights[0], axis=-1, keepdims=True)
        for one, other in zip(weights[1:], d_weights[1:]):
            inner = inner + jnp.sum(one * other, axis=-1, keepdims=True)
        d_scores = [to_low(one * (other - inner)) for one, other in zip(weights, d_weights)]
        return [to_low(one) for one in weights], d_scores

    def token_back(block_id):
        prev_id = jnp.maximum(block_id - 1, 0)
        st_key[...] = jnp.zeros_like(st_key)
        st_value[...] = jnp.zeros_like(st_value)

        def one_chunk(chunk, _):
            rows = span(chunk, ROWS)
            query, parts = token_scores(scal, qkv, qkvst, bias, block_id, chunk)
            grad = d_o[block_id, rows, :]
            keys = (qkv[prev_id, :, 128:256], qkv[block_id, :, 128:256], qkvst[block_id, :, 128:256])
            values = (
                qkv[prev_id, :, 256:384], qkv[block_id, :, 256:384], qkvst[block_id, :, 256:384]
            )
            weights, d_scores = back_parts(parts, lse_tok[block_id, rows, :], grad, values)
            d_query = dot_nn(d_scores[0], keys[0])
            d_query = d_query + dot_nn(d_scores[1], keys[1]) + dot_nn(d_scores[2], keys[2])
            d_qkv[block_id, rows, 0:128] = to_low(d_query * SCALE)
            key_acc[prev_id] += dot_tn(d_scores[0], query) * SCALE
            value_acc[prev_id] += dot_tn(weights[0], grad)
            key_acc[block_id] += dot_tn(d_scores[1], query) * SCALE
            value_acc[block_id] += dot_tn(weights[1], grad)
            st_key[...] += dot_tn(d_scores[2], query) * SCALE
            st_value[...] += dot_tn(weights[2], grad)
            dz_sum[rows, 0:BLOCK] += d_scores[0].astype(jnp.float32)
            dz_sum[rows, BLOCK : 2 * BLOCK] += d_scores[1].astype(jnp.float32)
            return 0

        lax.fori_loop(0, CHUNKS, one_chunk, 0)

    token_back(3)
    pl.semaphore_wait(barrier, LINE + 1)
    aside(beside, place // 2).start()
    loads[2].wait()
    loads[0].wait()
    fetched(w_sout, local_sem.at[1])
    fetched(w_back, local_sem.at[2])

    def mixed_copy(block_id, slot, sender, other, seq_to, rank_to):
        return pltpu.make_async_remote_copy(
            src_ref=dos_rows.at[block_id, :, span(other, 128)],
            dst_ref=dos_got.at[block_id, span(sender, 64), :],
            send_sem=send_sem.at[0, block_id, slot],
            recv_sem=recv_sem.at[0, block_id, sender],
            device_id={"seq": seq_to, "tensor": rank_to},
            device_id_type=MESH_ID,
        )

    def grads_copy(block_id, slot, sender, other, seq_to, rank_to):
        return pltpu.make_async_remote_copy(
            src_ref=d_qkvst.at[block_id, span(other, 64), :],
            dst_ref=d_got.at[block_id, sender],
            send_sem=send_sem.at[1, block_id, slot],
            recv_sem=recv_sem.at[1, block_id, sender],
            device_id={"seq": seq_to, "tensor": rank_to},
            device_id_type=MESH_ID,
        )

    def one_block(turn, _):
        block_id = 3 - turn
        grad_out = grad_in[...] + cots[block_id].astype(jnp.float32)
        sums[0:1, :] += jnp.sum(
            grad_out * (states[block_id] - states[block_id + 1]), axis=0, keepdims=True
        ) * gate
        change = to_low((1.0 - gate) * grad_out)
        du_rows[block_id] = change
        dos_rows[block_id] = to_low(dot_nt(change, w_sout[...].reshape(D, D)))
        for slot, (other, seq_to, rank_to) in enumerate(peers):
            mixed_copy(block_id, slot, head, other, seq_to, rank_to).start()
        dos_got[block_id, span(head, 64), :] = dos_rows[block_id, :, span(head, 128)]
        for slot, (other, seq_to, rank_to) in enumerate(peers):
            mixed_copy(block_id, slot, other, other, seq_to, rank_to).wait_recv()

        def one_chunk(chunk, _):
            rows = span(chunk, ROWS)
            query, parts = state_scores(scal, qkv, qkvst, block_id, chunk)
            grad = dos_got[block_id, rows, :]
            keys = (qkv[block_id, :, 128:256], qkvst[block_id, :, 128:256])
            values = (qkv[block_id, :, 256:384], qkvst[block_id, :, 256:384])
            weights, d_scores = back_parts(parts, lse_st[block_id, rows, :], grad, values)
            d_query = dot_nn(d_scores[0], keys[0]) + dot_nn(d_scores[1], keys[1])
            d_qkvst[block_id, rows, 0:128] = to_low(d_query * SCALE)
            key_acc[block_id] += dot_tn(d_scores[0], query) * SCALE
            value_acc[block_id] += dot_tn(weights[0], grad)
            st_key[...] += dot_tn(d_scores[1], query) * SCALE
            st_value[...] += dot_tn(weights[1], grad)
            return 0

        lax.fori_loop(0, CHUNKS, one_chunk, 0)
        d_qkvst[block_id, :, 128:256] = to_low(st_key[...])
        d_qkvst[block_id, :, 256:384] = to_low(st_value[...])
        for slot, (other, seq_to, rank_to) in enumerate(peers):
            grads_copy(block_id, slot, head, other, seq_to, rank_to).start()
        d_got[block_id, head] = d_qkvst[block_id, span(head, 64), :]

        for step in range(4):

            @pl.when(turn == step)
            def _():
                next(plane_steps, None)

        @pl.when(turn == 3)
        def _():
            bucket_sums()

        @pl.when(turn < 3)
        def _():
            token_back(block_id - 1)

        d_qkv[block_id, :, 128:256] = to_low(key_acc[block_id])
        d_qkv[block_id, :, 256:384] = to_low(value_acc[block_id])
        block_products(block_id)

        @pl.when(turn == 2)
        def _():
            add_came(place_in(2 + half, place))

        for slot, (other, seq_to, rank_to) in enumerate(peers):
            grads_copy(block_id, slot, other, other, seq_to, rank_to).wait_recv()
        d_low = dot_nn(d_got[block_id, 0], w_back[0, 0].reshape(384, D))
        for other in range(1, LINE):
            d_low = d_low + dot_nn(
                d_got[block_id, other], w_back[other // 2, other % 2].reshape(384, D)
            )
        centered, scale = norm_parts(states[block_id])
        normed = centered * scale
        sums[1:2, :] += jnp.sum(d_low * normed, axis=0, keepdims=True)
        lifted = d_low * gain
        grad_in[...] = gate * grad_out + scale * (
            lifted
            - jnp.mean(lifted, axis=-1, keepdims=True)
            - normed * jnp.mean(lifted * normed, axis=-1, keepdims=True)
        )
        return 0

    lax.fori_loop(0, 4, one_block, 0)
    d_start[...] = grad_in[...]

    def drain(block_id, _):
        for slot, (other, seq_to, rank_to) in enumerate(peers):
            mixed_copy(block_id, slot, head, other, seq_to, rank_to).wait_send()
            grads_copy(block_id, slot, head, other, seq_to, rank_to).wait_send()
        return 0

    lax.fori_loop(0, 4, drain, 0)
    pair_grads[...] = to_low(grad_acc[...])
    for _ in plane_steps:
        pass
    add_came(place_in(half, place))
    for slot in range(2):
        leaving(slot).wait_send()
    for which in range(2):
        rows = pl.ds(128 * which, 128)
        tokens_out[which] = to_low(hidden[which] + total[rows, :])
    out_part[...] = to_low(total[256:384, :])
    loads[1].wait()
    aside(beside, place // 2).wait_send()
    aside(place, 1 - place // 2).wait_recv()


def backward_chain(
    scal, qkv, d_o, lse_tok, qkvst, lse_st, state_rows, begin, cots, back, kept, vecs, bias,
    extra, hidden, rows_all, state_low, w_qkv,
):
    low, wide = jnp.bfloat16, jnp.float32
    shapes = (
        ((4, 64, D), low),
        ((64, D), wide),
        ((8, D), wide),
        ((2, 128, D), wide),
        ((2, 128, D), low),
        ((128, D), low),
        ((2, 4, 128, D), low),
        ((512, D), low),
    )
    return pl.pallas_call(
        backward_kernel,
        out_shape=[jax.ShapeDtypeStruct(*one) for one in shapes],
        in_specs=vmem_specs(6)
        + any_specs(1)
        + vmem_specs(2)
        + any_specs(2)
        + vmem_specs(2)
        + any_specs(1)
        + vmem_specs(1)
        + any_specs(2)
        + vmem_specs(1),
        out_specs=vmem_specs(3) + any_specs(1) + vmem_specs(4),
        scratch_shapes=[
            pltpu.VMEM((BLOCK, 2 * BLOCK), wide),
            pltpu.VMEM((8, WIDE), wide),
            pltpu.VMEM((4, BLOCK, 384), low),
            pltpu.VMEM((4, STATES, 384), low),
            pltpu.VMEM((2, BLOCK, D), low),
            pltpu.VMEM((2, STATES, D), low),
            pltpu.VMEM((2, BLOCK, D), low),
            pltpu.VMEM((2, BLOCK, D), low),
            pltpu.VMEM((512, D), wide),
            pltpu.VMEM((4, BLOCK, 128), wide),
            pltpu.VMEM((4, BLOCK, 128), wide),
            pltpu.VMEM((STATES, 128), wide),
            pltpu.VMEM((STATES, 128), wide),
            pltpu.VMEM((4, 64, D), low),
            pltpu.VMEM((4, STATES, 128), low),
            pltpu.VMEM((4, LINE, 64, 384), low),
            pltpu.VMEM((64, D), wide),
            pltpu.VMEM((5, 64, D), wide),
            pltpu.VMEM((4, 2, 3, 4, 32, D), low),
            pltpu.VMEM((4, 8, 32, D), low),
            pltpu.VMEM((8, 384, D), low),
            pltpu.VMEM((4, 384, D), low),
            pltpu.VMEM((4, 192, D), low),
            pltpu.VMEM((2, 192, D), low),
            pltpu.VMEM((384, D), wide),
            pltpu.SemaphoreType.DMA((2, 4, LINE - 1)),
            pltpu.SemaphoreType.DMA((2, 4, LINE)),
            pltpu.SemaphoreType.DMA((5,)),
            pltpu.SemaphoreType.DMA((2,)),
            pltpu.SemaphoreType.DMA((10,)),
            pltpu.SemaphoreType.DMA((10,)),
            pltpu.SemaphoreType.DMA((2, 2)),
            pltpu.SemaphoreType.DMA((2,)),
            pltpu.SemaphoreType.DMA((2,)),
        ],
        compiler_params=pltpu.CompilerParams(
            collective_id=2, has_side_effects=True, vmem_limit_bytes=VMEM_LIMIT
        ),
        cost_estimate=pl.CostEstimate(flops=40000000000, bytes_accessed=40000000, transcendentals=0),
        name="backward_chain",
    )(
        scal, qkv, d_o, lse_tok, qkvst, lse_st, state_rows, begin, cots, back, kept, vecs, bias,
        extra, hidden, rows_all, state_low, w_qkv,
    )


def plane_place():
    place, half, rank = line_place()
    side = lax.axis_index("dp")
    return side, place, half, rank


def plane_index(side, place):
    return 4 * side + place


def row_halves(buf, rows):
    size = rows // 2
    return lambda owner, part: buf.at[owner, pl.ds(part * size, size), :]


def plane_gather(view, send_sem, recv_sem):
    side, place, half, rank = plane_place()
    across, beside = 1 - side, lax.rem(place + 2, 4)
    core = place + 1 - 2 * half
    me = plane_index(side, place)
    at_x, at_y = plane_index(across, place), plane_index(side, beside)
    at_d = plane_index(across, beside)
    to_x, to_y, to_c = {"dp": across}, {"seq": beside}, {"seq": core}

    def piece(owner, part, slot, target):
        one = view(owner, part)
        return pltpu.make_async_remote_copy(
            src_ref=one,
            dst_ref=one,
            send_sem=send_sem.at[slot],
            recv_sem=recv_sem.at[owner, part],
            device_id=target,
            device_id_type=MESH_ID,
        )

    own = [
        piece(me, 0, 0, to_x), piece(me, 1, 1, to_y), piece(me, 1, 2, to_x), piece(me, 0, 3, to_y),
        piece(me, 0, 4, to_c), piece(me, 1, 5, to_c),
    ]
    on_x0, on_y1 = piece(at_x, 0, 6, to_y), piece(at_y, 1, 7, to_x)
    came = [
        (piece(owner, part, 0, to_c), piece(owner, part, slot, to_c))
        for owner, part, slot in (
            (at_x, 0, 8), (at_y, 1, 9), (at_x, 1, 10), (at_y, 0, 11), (at_d, 0, 12), (at_d, 1, 13)
        )
    ]
    core_came = [
        piece(owner, part, 0, to_c)
        for owner in (
            plane_index(side, core),
            plane_index(across, core),
            plane_index(side, lax.rem(core + 2, 4)),
            plane_index(across, lax.rem(core + 2, 4)),
        )
        for part in (0, 1)
    ]
    yield
    for one in own:
        one.start()
    yield
    came[0][0].wait_recv()
    on_x0.start()
    came[1][0].wait_recv()
    on_y1.start()
    came[0][1].start()
    came[1][1].start()
    yield
    for index in (2, 3):
        came[index][0].wait_recv()
        came[index][1].start()
    yield
    for index in (4, 5):
        came[index][0].wait_recv()
        came[index][1].start()
    yield
    for one in core_came:
        one.wait_recv()
    for one in own + [on_x0, on_y1] + [two for _, two in came]:
        one.wait_send()


def run_all(*steps):
    waiting = list(steps)
    while waiting:
        for one in list(waiting):
            try:
                next(one)
            except StopIteration:
                waiting.remove(one)


def plane_scatter(part, core_got, near_got, far_got, total, rows, send_sem, recv_sem):
    side, place, half, rank = plane_place()
    across, beside = 1 - side, lax.rem(place + 2, 4)
    core = place + 1 - 2 * half
    me = plane_index(side, place)
    at_x, at_y = plane_index(across, place), plane_index(side, beside)
    at_d = plane_index(across, beside)
    size = rows // 2
    halves = (pl.ds(0, size), pl.ds(size, size))

    def moved(source, target_ref, slot, target):
        return pltpu.make_async_remote_copy(
            src_ref=source,
            dst_ref=target_ref,
            send_sem=send_sem.at[slot],
            recv_sem=recv_sem.at[slot],
            device_id=target,
            device_id_type=MESH_ID,
        )

    order = (at_d, at_x, at_y, me)
    swapped = (
        plane_index(across, lax.rem(core + 2, 4)),
        plane_index(across, core),
        plane_index(side, lax.rem(core + 2, 4)),
        plane_index(side, core),
    )
    def add_into(owner, view, other):
        part[owner, view, :] = to_low(
            part[owner, view, :].astype(jnp.float32) + other.astype(jnp.float32)
        )

    near = [
        moved(part.at[at_d, halves[0], :], near_got.at[0], 4, {"dp": across}),
        moved(part.at[at_d, halves[1], :], near_got.at[1], 5, {"seq": beside}),
        moved(part.at[at_x, halves[0], :], near_got.at[2], 6, {"dp": across}),
        moved(part.at[at_y, halves[1], :], near_got.at[3], 7, {"seq": beside}),
    ]
    first = [
        moved(part.at[owner], core_got.at[slot], slot, {"seq": core})
        for slot, owner in enumerate(swapped)
    ]
    far = [
        moved(part.at[at_y, halves[0], :], far_got.at[0], 8, {"seq": beside}),
        moved(part.at[at_x, halves[1], :], far_got.at[1], 9, {"dp": across}),
    ]
    yield
    for one in first:
        one.start()
    for slot, owner in enumerate(order):
        first[slot].wait_recv()
        for view in halves:
            add_into(owner, view, core_got[slot, view, :])
        if slot == 0:
            near[0].start()
            near[1].start()
        if slot == 1:
            near[2].start()
        if slot == 2:
            near[3].start()
    yield
    near[0].wait_recv()
    add_into(at_y, halves[0], near_got[0])
    far[0].start()
    near[1].wait_recv()
    add_into(at_x, halves[1], near_got[1])
    far[1].start()
    yield
    near[2].wait_recv()
    add_into(me, halves[0], near_got[2])
    near[3].wait_recv()
    add_into(me, halves[1], near_got[3])
    yield
    for slot, view in enumerate(halves):
        far[slot].wait_recv()
        total[view, :] = part[me, view, :].astype(jnp.float32) + far_got[slot].astype(jnp.float32)
    for one in first + near + far:
        one.wait_send()


def group_peers():
    place, half, rank = line_place()
    here = 4 * place + rank
    peers = []
    for step in range(1, 16):
        other = lax.rem(here + step, 16)
        peers.append((other, other // 4, lax.rem(other, 4)))
    return here, peers


def greet(peers):
    side = lax.axis_index("dp")
    barrier = pltpu.get_barrier_semaphore()
    for _, seq_to, rank_to in peers:
        pl.semaphore_signal(
            barrier, inc=1, device_id={"seq": seq_to, "tensor": rank_to}, device_id_type=MESH_ID
        )
    pl.semaphore_signal(barrier, inc=1, device_id={"dp": 1 - side}, device_id_type=MESH_ID)
    pl.semaphore_wait(barrier, len(peers) + 1)


def middle_kernel(
    mixed, tokens, kept, spread, cot_hbm, vecs,
    hidden, d_hidden, d_line, sums, extra, ff_grads,
    mixed_rows, mid_all, gl_all, dpre_all, work, core_got, near_got, far_got, total, d_rows,
    d_low, w_out, up, down, cot_all,
    send_sem, recv_sem, ring_send, ring_recv, sum_send, sum_recv, back_send, back_recv, local_sem,
):
    low, wide = jnp.bfloat16, jnp.float32
    side, place, half, rank = plane_place()
    mine = place // 2
    head = 2 * rank + half
    across, beside = 1 - side, lax.rem(place + 2, 4)
    core = place + 1 - 2 * half
    core_beside = lax.rem(core + 2, 4)
    me = plane_index(side, place)
    at_x, at_y = plane_index(across, place), plane_index(side, beside)
    at_d = plane_index(across, beside)
    me_c, x_c = plane_index(side, core), plane_index(across, core)
    y_c, d_c = plane_index(side, core_beside), plane_index(across, core_beside)
    to_x, to_y, to_c = {"dp": across}, {"seq": beside}, {"seq": core}
    here, peers = group_peers()
    fetch_pieces(kept, 48, 32, w_out, local_sem.at[0])
    ff_own = up.shape[1]
    first = spread.shape[1] - 2 * ff_own
    loads = [
        pltpu.make_async_copy(spread.at[:, pl.ds(first, ff_own), :], up, local_sem.at[1]),
        pltpu.make_async_copy(spread.at[:, pl.ds(first + ff_own, ff_own), :], down, local_sem.at[2]),
        pltpu.make_async_copy(cot_hbm, cot_all, local_sem.at[3]),
    ]
    for one in loads:
        one.start()
    greet(peers)

    def rows_copy(slot, sender, seq_from, rank_from, seq_to, rank_to):
        return pltpu.make_async_remote_copy(
            src_ref=mixed.at[seq_to, span(rank_to, 128), :],
            dst_ref=mixed_rows.at[
                seq_from // 2, :, span(2 * rank_from + lax.rem(seq_from, 2), 128)
            ],
            send_sem=send_sem.at[slot],
            recv_sem=recv_sem.at[sender],
            device_id={"seq": seq_to, "tensor": rank_to},
            device_id_type=MESH_ID,
        )

    for slot, (_, seq_to, rank_to) in enumerate(peers):
        rows_copy(slot, here, place, rank, seq_to, rank_to).start()
    mixed_rows[mine, :, span(head, 128)] = mixed[place, span(rank, 128), :]
    fetched(w_out, local_sem.at[0])
    for slot, (other, seq_to, rank_to) in enumerate(peers):
        rows_copy(slot, other, seq_to, rank_to, seq_to, rank_to).wait_recv()
    gain = vecs[2:3, :]

    def project(which, _):
        added = dot_nn(mixed_rows[which], w_out[...].reshape(D, D)) + tokens[which].astype(wide)
        hidden[which] = added
        centered, scale = norm_parts(added)
        mid_all[me, span(which, 128), :] = to_low(centered * scale * gain)
        return 0

    lax.fori_loop(0, 2, project, 0)

    def piece(owner, part, slot, target):
        view = mid_all.at[owner, pl.ds(part * 128, 128), :]
        return pltpu.make_async_remote_copy(
            src_ref=view,
            dst_ref=view,
            send_sem=ring_send.at[slot],
            recv_sem=ring_recv.at[owner, part],
            device_id=target,
            device_id_type=MESH_ID,
        )

    own = [
        piece(me, 0, 0, to_x), piece(me, 1, 1, to_y), piece(me, 1, 2, to_x), piece(me, 0, 3, to_y),
        piece(me, 0, 4, to_c), piece(me, 1, 5, to_c),
    ]
    on_x0, on_y1 = piece(at_x, 0, 6, to_y), piece(at_y, 1, 7, to_x)
    to_core = [
        piece(at_x, 0, 8, to_c), piece(at_y, 1, 9, to_c), piece(at_x, 1, 10, to_c),
        piece(at_y, 0, 11, to_c), piece(at_d, 0, 12, to_c), piece(at_d, 1, 13, to_c),
    ]
    wait_of = {
        (name, part): piece(owner, part, 0, to_c)
        for name, owner in (
            ("x", at_x), ("y", at_y), ("d", at_d), ("mc", me_c), ("xc", x_c), ("yc", y_c), ("dc", d_c)
        )
        for part in (0, 1)
    }

    def moved(source, target_ref, slot, target):
        return pltpu.make_async_remote_copy(
            src_ref=source,
            dst_ref=target_ref,
            send_sem=sum_send.at[slot],
            recv_sem=sum_recv.at[slot],
            device_id=target,
            device_id_type=MESH_ID,
        )

    views = (pl.ds(0, 128), pl.ds(128, 128))
    swap = [
        moved(work.at[owner], core_got.at[slot], slot, to_c)
        for slot, owner in enumerate((d_c, x_c, y_c, me_c))
    ]
    near = [
        moved(work.at[at_d, views[0], :], near_got.at[0], 4, to_x),
        moved(work.at[at_d, views[1], :], near_got.at[1], 5, to_y),
        moved(work.at[at_x, views[0], :], near_got.at[2], 6, to_x),
        moved(work.at[at_y, views[1], :], near_got.at[3], 7, to_y),
    ]
    far = [
        moved(work.at[at_y, views[0], :], far_got.at[0], 8, to_y),
        moved(work.at[at_x, views[1], :], far_got.at[1], 9, to_x),
    ]

    def add_into(owner, view, other):
        work[owner, view, :] = to_low(work[owner, view, :].astype(wide) + other.astype(wide))

    def add_core(slot, owner):
        swap[slot].wait_recv()
        for view in views:
            add_into(owner, view, core_got[slot, view, :])

    for one in own:
        one.start()
    loads[0].wait()
    loads[1].wait()
    loads[2].wait()
    owners = (me, me_c, at_x, at_y, x_c, y_c, at_d, d_c)

    def one_chunk(turn, _):
        @pl.when(turn == 1)
        def _():
            wait_of["mc", 0].wait_recv()
            wait_of["mc", 1].wait_recv()

        @pl.when(turn == 2)
        def _():
            swap[3].start()
            wait_of["x", 0].wait_recv()
            on_x0.start()
            wait_of["y", 1].wait_recv()
            on_y1.start()
            to_core[0].start()
            to_core[1].start()
            wait_of["x", 1].wait_recv()
            to_core[2].start()
            wait_of["y", 0].wait_recv()
            to_core[3].start()

        @pl.when(turn == 4)
        def _():
            wait_of["xc", 0].wait_recv()
            wait_of["xc", 1].wait_recv()

        @pl.when(turn == 5)
        def _():
            swap[1].start()
            wait_of["yc", 0].wait_recv()
            wait_of["yc", 1].wait_recv()

        @pl.when(turn == 6)
        def _():
            swap[2].start()
            wait_of["d", 0].wait_recv()
            to_core[4].start()
            wait_of["d", 1].wait_recv()
            to_core[5].start()
            add_core(1, at_x)
            near[2].start()
            add_core(2, at_y)
            near[3].start()

        @pl.when(turn == 7)
        def _():
            wait_of["dc", 0].wait_recv()
            wait_of["dc", 1].wait_recv()

        owner = owners[7]
        for index in range(7):
            owner = jnp.where(turn == index, owners[index], owner)
        up_rows = up[...].reshape(4 * ff_own, D)
        down_rows = down[...].reshape(4 * ff_own, D)

        def part(which, _):
            rows = span(which, 128)
            pre = dot_nt(mid_all[owner, rows, :], up_rows)
            square = pre * pre
            bend = jnp.tanh(GELU_SCALE * (pre + 0.044715 * (pre * square)))
            gl_all[owner, rows, :] = to_low(0.5 * pre * (1.0 + bend))
            slope = 0.5 * (1.0 + bend) + 0.5 * pre * (1.0 - bend * bend) * (
                GELU_SCALE * (1.0 + 3.0 * 0.044715 * square)
            )
            grad = to_low(dot_nt(cot_all[owner, rows, :], down_rows) * slope)
            dpre_all[owner, rows, :] = grad
            work[owner, rows, :] = to_low(dot_nn(grad, up_rows))
            return 0

        lax.fori_loop(0, 2, part, 0)
        return 0

    lax.fori_loop(0, 8, one_chunk, 0)
    swap[0].start()
    add_core(0, at_d)
    near[0].start()
    near[1].start()
    add_core(3, me)

    def grads(index, _):
        quarter, kind = index // 2, lax.rem(index, 2)
        columns = span(quarter, 128)

        @pl.when(kind == 0)
        def _():
            def add(owner, acc):
                return acc + dot_tn(dpre_all[owner, :, columns], mid_all[owner])

            ff_grads[quarter, 0] = to_low(lax.fori_loop(0, 8, add, jnp.zeros((128, D), wide)))

        @pl.when(kind == 1)
        def _():
            def add(owner, acc):
                return acc + dot_tn(gl_all[owner, :, columns], cot_all[owner])

            ff_grads[quarter, 1] = to_low(lax.fori_loop(0, 8, add, jnp.zeros((128, D), wide)))

        return 0

    lax.fori_loop(0, 8, grads, 0)
    near[0].wait_recv()
    add_into(at_y, views[0], near_got[0])
    far[0].start()
    near[1].wait_recv()
    add_into(at_x, views[1], near_got[1])
    far[1].start()
    near[2].wait_recv()
    add_into(me, views[0], near_got[2])
    near[3].wait_recv()
    add_into(me, views[1], near_got[3])

    def outward(owner, _):
        down_rows = down[...].reshape(4 * ff_own, D)
        for which in range(2):
            rows = pl.ds(128 * which, 128)
            extra[owner, rows, :] = to_low(dot_nn(gl_all[owner, rows, :], down_rows))
        return 0

    lax.fori_loop(0, 8, outward, 0)
    for slot, view in enumerate(views):
        far[slot].wait_recv()
        total[view, :] = work[me, view, :].astype(wide) + far_got[slot].astype(wide)
    sums[...] = jnp.zeros_like(sums)

    def back(which, _):
        rows = span(which, 128)
        grad = total[rows, :]
        centered, scale = norm_parts(hidden[which])
        normed = centered * scale
        sums[0:1, :] += jnp.sum(grad * normed, axis=0, keepdims=True)
        lifted = grad * gain
        row_grad = cot_all[me, rows, :].astype(wide) + scale * (
            lifted
            - jnp.mean(lifted, axis=-1, keepdims=True)
            - normed * jnp.mean(lifted * normed, axis=-1, keepdims=True)
        )
        d_hidden[which] = row_grad
        d_low[which] = to_low(row_grad)
        d_rows[which] = to_low(dot_nt(to_low(row_grad), w_out[...].reshape(D, D)))
        return 0

    lax.fori_loop(0, 2, back, 0)

    def line_copy(slot, sender, seq_from, rank_from, seq_to, rank_to):
        return pltpu.make_async_remote_copy(
            src_ref=d_rows.at[seq_to // 2, :, span(2 * rank_to + lax.rem(seq_to, 2), 128)],
            dst_ref=d_line.at[seq_from, span(rank_from, 128), :],
            send_sem=back_send.at[slot],
            recv_sem=back_recv.at[sender],
            device_id={"seq": seq_to, "tensor": rank_to},
            device_id_type=MESH_ID,
        )

    for slot, (_, seq_to, rank_to) in enumerate(peers):
        line_copy(slot, here, place, rank, seq_to, rank_to).start()
    d_line[place, span(rank, 128), :] = d_rows[mine, :, span(head, 128)]
    for index in range(LINE):
        columns = pl.ds(128 * index, 128)
        part = dot_tn(mixed_rows[0, :, columns], d_low[0]) + dot_tn(
            mixed_rows[1, :, columns], d_low[1]
        )
        part = to_low(part)
        for block in range(4):
            extra[
                4 * (index % 2) + block, 256 + 32 * (index // 2) : 288 + 32 * (index // 2), :
            ] = part[32 * block : 32 * block + 32, :]
    for slot, (other, seq_to, rank_to) in enumerate(peers):
        line_copy(slot, other, seq_to, rank_to, seq_to, rank_to).wait_recv()
    for slot, (_, seq_to, rank_to) in enumerate(peers):
        rows_copy(slot, here, place, rank, seq_to, rank_to).wait_send()
        line_copy(slot, here, place, rank, seq_to, rank_to).wait_send()
    for one in own + [on_x0, on_y1] + to_core + swap + near + far:
        one.wait_send()


GELU_SCALE = 0.7978845608028654


def middle(mixed, tokens, kept, spread, cot_all, vecs):
    low, wide = jnp.bfloat16, jnp.float32
    ff_own = (spread.shape[1] - SPREAD_FIRST) // 2
    shapes = (
        ((2, 128, D), wide),
        ((2, 128, D), wide),
        ((4, BLOCK, 128), low),
        ((8, D), wide),
        ((8, 384, D), low),
        ((4, 2, ff_own, D), low),
    )
    dma = pltpu.SemaphoreType.DMA
    return pl.pallas_call(
        middle_kernel,
        out_shape=[jax.ShapeDtypeStruct(*one) for one in shapes],
        in_specs=vmem_specs(2) + any_specs(3) + vmem_specs(1),
        out_specs=vmem_specs(6),
        scratch_shapes=[
            pltpu.VMEM((2, 128, D), low),
            pltpu.VMEM((8, 256, D), low),
            pltpu.VMEM((8, 256, 4 * ff_own), low),
            pltpu.VMEM((8, 256, 4 * ff_own), low),
            pltpu.VMEM((8, 256, D), low),
            pltpu.VMEM((4, 256, D), low),
            pltpu.VMEM((4, 128, D), low),
            pltpu.VMEM((2, 128, D), low),
            pltpu.VMEM((256, D), wide),
            pltpu.VMEM((2, 128, D), low),
            pltpu.VMEM((2, 128, D), low),
            pltpu.VMEM((4, 8, 32, D), low),
            pltpu.VMEM((4, ff_own, D), low),
            pltpu.VMEM((4, ff_own, D), low),
            pltpu.VMEM((8, 256, D), low),
            dma((15,)), dma((16,)), dma((14,)), dma((8, 2)), dma((10,)), dma((10,)), dma((15,)),
            dma((16,)), dma((4,)),
        ],
        compiler_params=pltpu.CompilerParams(
            collective_id=3, has_side_effects=True, vmem_limit_bytes=VMEM_LIMIT
        ),
        cost_estimate=pl.CostEstimate(
            flops=60000000000, bytes_accessed=60000000, transcendentals=0
        ),
        name="middle",
    )(mixed, tokens, kept, spread, cot_all, vecs)


SPREAD_FIRST = 0


WIDE = 2048


def opening_kernel(
    tokens, w_query, w_key, w_value, w_sout, w_out, begin, vecs, rel_bias, marks_own,
    rows_all, qkv, kept, table, marks, w_qkv,
    begin_rows, bias_rows, stage, send_sem, core_sem, recv_sem, piece_send, piece_recv, ring_send, ring_recv,
    mark_send, mark_recv, local_sem,
):
    side, place, half, rank = plane_place()
    mine = place // 2
    core = place + 1 - 2 * half
    other = lax.rem(place + 2, 4)
    me = plane_index(side, place)
    extra = 80
    fetch_columns((w_query, w_key, w_value), w_qkv, local_sem.at[0])
    loads = [
        pltpu.make_async_copy(
            w_sout.at[span(me, 32), :], kept.at[me, pl.ds(80 * rank, 32), :], local_sem.at[1]
        ),
        pltpu.make_async_copy(
            w_out.at[span(me, 32), :], kept.at[me, pl.ds(80 * rank + 48, 32), :], local_sem.at[3]
        ),
        pltpu.make_async_copy(begin.at[span(me, 16), :], begin_rows, local_sem.at[2]),
    ]
    for one in loads:
        one.start()
    barrier = pltpu.get_barrier_semaphore()
    greeted = [{"tensor": lax.rem(rank + step, 4)} for step in (1, 2, 3)]
    seats = [lax.rem(place + step, 4) for step in (1, 2, 3)]
    greeted += [{"seq": one} for one in seats] + [{"dp": 1 - side}]
    for target in greeted:
        pl.semaphore_signal(barrier, inc=1, device_id=target, device_id_type=MESH_ID)
    gain = vecs[3:4, :]

    def normed(which):
        centered, scale = norm_parts(tokens[which].astype(jnp.float32))
        return to_low(centered * scale * gain)

    def moved(block_id, origin, sem, target):
        view = rows_all.at[block_id, span(origin, 128), :]
        return pltpu.make_async_remote_copy(
            src_ref=view,
            dst_ref=view,
            send_sem=sem,
            recv_sem=recv_sem.at[block_id, origin],
            device_id=target,
            device_id_type=MESH_ID,
        )

    stage[...] = normed(1 - mine)
    marks[place] = marks_own[...]
    pl.semaphore_wait(barrier, 7)
    aside = pltpu.make_async_remote_copy(
        src_ref=stage,
        dst_ref=rows_all.at[place, span(rank, 128), :],
        send_sem=send_sem.at[0, 0, 3],
        recv_sem=recv_sem.at[place, rank],
        device_id={"seq": other},
        device_id_type=MESH_ID,
    )
    aside.start()

    def mark_move(slot, origin, target):
        return pltpu.make_async_remote_copy(
            src_ref=marks.at[origin],
            dst_ref=marks.at[origin],
            send_sem=mark_send.at[slot],
            recv_sem=mark_recv.at[origin],
            device_id={"seq": target},
            device_id_type=MESH_ID,
        )

    def piece_move(slot, origin, target):
        view = kept.at[me, span(origin, extra), :]
        return pltpu.make_async_remote_copy(
            src_ref=view,
            dst_ref=view,
            send_sem=piece_send.at[slot],
            recv_sem=piece_recv.at[origin],
            device_id=target,
            device_id_type=MESH_ID,
        )

    for one in loads:
        one.wait()
    kept[me, pl.ds(pl.multiple_of(80 * rank + 32, 16), 16), :] = to_low(begin_rows[...])
    for slot in range(3):
        piece_move(slot, rank, greeted[slot]).start()
    for slot, target in enumerate(seats):
        mark_move(slot, place, target).start()
    rows_all[place, span(rank, 128), :] = normed(mine)
    right, left = {"tensor": lax.rem(rank + 1, 4)}, {"tensor": lax.rem(rank + 3, 4)}
    blocks = (place, other)

    def pass_on(which, distance):
        block_id = blocks[which]

        @pl.when((rank < 3) & (rank >= distance))
        def _():
            moved(block_id, jnp.maximum(rank - distance, 0), send_sem.at[which, distance, 0], right).start()

        @pl.when((rank > 0) & (rank + distance <= 3))
        def _():
            moved(block_id, jnp.minimum(rank + distance, 3), send_sem.at[which, distance, 1], left).start()

    def pass_done(which, distance):
        block_id = blocks[which]

        @pl.when((rank < 3) & (rank >= distance))
        def _():
            moved(block_id, jnp.maximum(rank - distance, 0), send_sem.at[which, distance, 0], right).wait_send()

        @pl.when((rank > 0) & (rank + distance <= 3))
        def _():
            moved(block_id, jnp.minimum(rank + distance, 3), send_sem.at[which, distance, 1], left).wait_send()

    def project(block_id, origin):
        view = span(origin, 128)
        qkv[block_id, view, :] = to_low(dot_nn(rows_all[block_id, view, :], w_qkv[...]))

    def rows_steps():
        pass_on(0, 0)
        fetched(w_qkv, local_sem.at[0])
        moved(place, rank, core_sem.at[0, rank], {"seq": core}).start()
        project(place, rank)
        moved(other, rank, send_sem.at[0, 0, 3], {"seq": other}).wait_recv()
        pass_on(1, 0)
        moved(other, rank, core_sem.at[1, rank], {"seq": core}).start()
        project(other, rank)
        yield
        for distance in (1, 2, 3):
            for which in (0, 1):
                block_id = blocks[which]
                for way, ok, origin in (
                    (0, rank >= distance, jnp.maximum(rank - distance, 0)),
                    (1, rank + distance <= 3, jnp.minimum(rank + distance, 3)),
                ):

                    @pl.when(ok)
                    def _():
                        moved(block_id, origin, send_sem.at[which, distance, way], right).wait_recv()
                        if distance < 3:
                            if way == 0:

                                @pl.when(rank < 3)
                                def _():
                                    moved(
                                        block_id, origin, send_sem.at[which, distance, 0], right
                                    ).start()

                            else:

                                @pl.when(rank > 0)
                                def _():
                                    moved(
                                        block_id, origin, send_sem.at[which, distance, 1], left
                                    ).start()

                        moved(block_id, origin, core_sem.at[which, origin], {"seq": core}).start()
                        project(block_id, origin)

                yield
        for which, block_id in enumerate((core, lax.rem(core + 2, 4))):
            for origin in range(4):
                moved(block_id, origin, core_sem.at[which, origin], {"seq": core}).wait_recv()
                project(block_id, origin)
        for which in (0, 1):
            for distance in (0, 1, 2):
                pass_done(which, distance)
            for origin in range(4):
                moved(blocks[which], origin, core_sem.at[which, origin], {"seq": core}).wait_send()

    def piece_steps():
        for slot in range(3):
            piece_move(slot, lax.rem(rank + slot + 1, 4), greeted[slot]).wait_recv()
        for _ in plane_gather(row_halves(kept, 4 * extra), ring_send, ring_recv):
            yield
        for slot in range(3):
            piece_move(slot, rank, greeted[slot]).wait_send()

    def bias_steps():
        lane = lax.broadcasted_iota(jnp.int32, (8, WIDE), 1)
        bucket_ids = bucket_of(jnp.where(lane >= WIDE - BLOCK, lane - WIDE - BLOCK, lane - BLOCK))
        first = jnp.zeros((8, WIDE), jnp.float32)
        for bucket_id in range(BUCKETS):
            first = jnp.where(bucket_ids == bucket_id, rel_bias[bucket_id, half], first)
        row = lax.broadcasted_iota(jnp.int32, (8, WIDE), 0)
        for step in (1, 2, 4):
            first = jnp.where(row // step % 2 == 1, pltpu.roll(first, step, 1), first)
        bias_rows[...] = first
        yield

        def one(group, _):
            table[span(group, 8), :] = pltpu.roll(bias_rows[...], 8 * group, 1)[:, 0 : 2 * BLOCK]
            return 0

        for part in range(4):
            lax.fori_loop(16 * part, 16 * part + 16, one, 0)
            yield

    run_all(rows_steps(), piece_steps(), bias_steps())
    aside.wait_send()
    for slot, target in enumerate(seats):
        mark_move(slot, place, target).wait_send()
        mark_move(slot, target, target).wait_recv()


def opening(tokens, w_query, w_key, w_value, w_sout, w_out, begin, vecs, rel_bias, marks):
    low, wide = jnp.bfloat16, jnp.float32
    shapes = (
        ((4, BLOCK, D), low),
        ((4, BLOCK, 384), low),
        ((8, 4 * 80, D), low),
        ((BLOCK, 2 * BLOCK), wide),
        ((4, 8, 128), jnp.int32),
        ((D, 384), low),
    )
    dma = pltpu.SemaphoreType.DMA
    outs = pl.pallas_call(
        opening_kernel,
        out_shape=[jax.ShapeDtypeStruct(*one) for one in shapes],
        in_specs=vmem_specs(1)
        + any_specs(6)
        + vmem_specs(1)
        + [pl.BlockSpec(memory_space=pltpu.SMEM)]
        + vmem_specs(1),
        out_specs=vmem_specs(6),
        scratch_shapes=[
            pltpu.VMEM((16, D), wide),
            pltpu.VMEM((8, WIDE), wide),
            pltpu.VMEM((128, D), low),
            dma((2, 4, 4)),
            dma((2, 4)),
            dma((4, 4)),
            dma((3,)),
            dma((4,)),
            dma((14,)),
            dma((8, 2)),
            dma((3,)),
            dma((4,)),
            dma((4,)),
        ],
        compiler_params=pltpu.CompilerParams(
            collective_id=5, has_side_effects=True, vmem_limit_bytes=VMEM_LIMIT
        ),
        cost_estimate=pl.CostEstimate(
            flops=30000000000, bytes_accessed=30000000, transcendentals=0
        ),
        name="opening",
    )(tokens, w_query, w_key, w_value, w_sout, w_out, begin, vecs, rel_bias, marks)
    rows_all, qkv, kept, table, marks, w_qkv = outs
    return rows_all, qkv, kept.reshape(8, 4, 80, D), table, marks, w_qkv


def pair_sum(part, near_got, far_got, result, rows, send_sem, recv_sem):
    side, place, half, rank = plane_place()
    mine = place // 2
    across, beside = 1 - side, 1 - mine
    me = 2 * side + mine
    at_x, at_y, at_d = 2 * across + mine, 2 * side + beside, 2 * across + beside
    to_x, to_y = {"dp": across}, {"seq": lax.rem(place + 2, 4)}
    size = rows // 2
    views = (pl.ds(0, size), pl.ds(size, size))

    def moved(source, target_ref, slot, target):
        return pltpu.make_async_remote_copy(
            src_ref=source,
            dst_ref=target_ref,
            send_sem=send_sem.at[slot],
            recv_sem=recv_sem.at[slot],
            device_id=target,
            device_id_type=MESH_ID,
        )

    def add_into(owner, view, other):
        part[owner, view, :] = to_low(
            part[owner, view, :].astype(jnp.float32) + other.astype(jnp.float32)
        )

    near = [
        moved(part.at[at_d, views[0], :], near_got.at[0], 0, to_x),
        moved(part.at[at_d, views[1], :], near_got.at[1], 1, to_y),
        moved(part.at[at_x, views[0], :], near_got.at[2], 2, to_x),
        moved(part.at[at_y, views[1], :], near_got.at[3], 3, to_y),
    ]
    for one in near:
        one.start()
    yield
    near[0].wait_recv()
    add_into(at_y, views[0], near_got[0])
    far = [
        moved(part.at[at_y, views[0], :], far_got.at[0], 4, to_y),
        moved(part.at[at_x, views[1], :], far_got.at[1], 5, to_x),
    ]
    far[0].start()
    near[1].wait_recv()
    add_into(at_x, views[1], near_got[1])
    far[1].start()
    yield
    near[2].wait_recv()
    add_into(me, views[0], near_got[2])
    near[3].wait_recv()
    add_into(me, views[1], near_got[3])
    for slot, view in enumerate(views):
        far[slot].wait_recv()
        result[me, view, :] = to_low(
            part[me, view, :].astype(jnp.float32) + far_got[slot].astype(jnp.float32)
        )

    def given(owner, which, slot, target):
        view = result.at[owner, views[which], :]
        return moved(view, view, slot, target)

    own = [
        given(me, 0, 6, to_x),
        given(me, 1, 7, to_y),
        given(me, 1, 8, to_x),
        given(me, 0, 9, to_y),
    ]
    for one in own:
        one.start()
    yield
    given(at_x, 0, 6, to_x).wait_recv()
    last = [given(at_x, 0, 10, to_y), given(at_y, 1, 11, to_x)]
    last[0].start()
    given(at_y, 1, 7, to_y).wait_recv()
    last[1].start()
    yield
    given(at_x, 1, 8, to_x).wait_recv()
    given(at_y, 0, 9, to_y).wait_recv()
    given(at_d, 0, 10, to_y).wait_recv()
    given(at_d, 1, 11, to_x).wait_recv()
    for one in near + far + own + last:
        one.wait_send()


PAIR_ROWS = 640


def closing_kernel(
    partial, pair_grads, tokens, d_hidden, vecs, os_hbm, du_hbm, d_start, small,
    out_part,
    inputs_grad, pair_out, sout_out, small_out,
    os_rows, du_rows, sums, got, final, cross, cross_got,
    pair_part, pair_near, pair_far,
    work, core_got, near_got, far_got, total, z_part, z_got,
    small_z, small_p,
    line_send, line_recv, way_send, way_recv, pair_send, pair_recv, core_sem,
    ring_send, ring_recv, zs_send, zs_recv, gather_send, gather_recv, small_send, small_recv, local_sem,
):
    loads = [
        pltpu.make_async_copy(source, target, local_sem.at[slot])
        for slot, (source, target) in enumerate(
            (
                (partial, sums),
                (os_hbm, os_rows),
                (du_hbm, du_rows),
            )
        )
    ]
    for one in loads:
        one.start()
    side, place, half, rank = plane_place()
    mine = place // 2
    core = place + 1 - 2 * half
    other = lax.rem(place + 2, 4)
    me = plane_index(side, place)
    ranks = [lax.rem(rank + step, 4) for step in (1, 2, 3)]
    spots_of = [lax.rem(me + step, 8) for step in range(1, 8)]
    barrier = pltpu.get_barrier_semaphore()
    for target in ranks:
        pl.semaphore_signal(barrier, inc=1, device_id={"tensor": target}, device_id_type=MESH_ID)
    for target in spots_of:
        pl.semaphore_signal(
            barrier,
            inc=1,
            device_id={"dp": target // 4, "seq": lax.rem(target, 4)},
            device_id_type=MESH_ID,
        )
    gain = vecs[3:4, :]
    right, left = {"tensor": lax.rem(rank + 1, 4)}, {"tensor": lax.rem(rank + 3, 4)}

    def moved(source, target_ref, send, recv, target):
        return pltpu.make_async_remote_copy(
            src_ref=source,
            dst_ref=target_ref,
            send_sem=send,
            recv_sem=recv,
            device_id=target,
            device_id_type=MESH_ID,
        )

    def crossing():
        return moved(cross, cross_got, line_send.at[0], line_recv.at[0], {"seq": other})

    near = rank // 2
    at_end = (rank == 0) | (rank == 3)

    def hop(way, which, target):
        return moved(
            sums.at[which, target],
            got.at[way, which, target],
            way_send.at[which, target],
            way_recv.at[way, which, target],
            {"tensor": lax.rem(rank + 5 - 2 * way, 4)},
        )

    def target_of(way, distance):
        return (1 - way) * (3 - distance) + way * distance

    def pass_first(which):
        @pl.when(at_end)
        def _():
            for distance in range(3):
                hop(near, which, target_of(near, distance)).start()

    def pass_on(way, which, distance):
        @pl.when(jnp.logical_not(at_end))
        def _():
            target = target_of(way, distance)
            hop(way, which, target).wait_recv()
            sums[which, target] = to_low(
                sums[which, target].astype(jnp.float32)
                + got[way, which, target].astype(jnp.float32)
            )
            hop(way, which, target).start()

    def finish(which):
        final[which] = sums[which, rank].astype(jnp.float32)

        @pl.when(rank > 0)
        def _():
            hop(0, which, rank).wait_recv()
            final[which] += got[0, which, rank].astype(jnp.float32)

        @pl.when(rank < 3)
        def _():
            hop(1, which, rank).wait_recv()
            final[which] += got[1, which, rank].astype(jnp.float32)

    def line_steps():
        loads[0].wait()
        pl.semaphore_wait(barrier, 10)
        for which in (0, 1):
            pass_first(which)
        yield
        for which in (0, 1):
            pass_on(near, which, 0)
            yield
            pass_on(near, which, 1)
            pass_on(1 - near, which, 0)
            yield
            finish(which)
            if which == 0:
                cross[...] = to_low(final[0])
                crossing().start()
            yield
        crossing().wait_recv()
        final[0] = cross_got[...].astype(jnp.float32)
        small_z[rank] = small[...]
        for which, row_set in ((1, mine), (0, 1 - mine)):
            grad = final[which]
            centered, scale = norm_parts(tokens[row_set].astype(jnp.float32))
            normed = centered * scale
            small_z[rank, 0:1, :] += jnp.sum(grad * normed, axis=0, keepdims=True)
            lifted = grad * gain
            inputs_grad[row_set] = d_hidden[row_set] + scale * (
                lifted
                - jnp.mean(lifted, axis=-1, keepdims=True)
                - normed * jnp.mean(lifted * normed, axis=-1, keepdims=True)
            )
        crossing().wait_send()
        for which in (0, 1):
            for target in range(4):

                @pl.when(rank != target)
                def _():
                    hop(0, which, target).wait_send()

    def pair_steps():
        for owner in range(3):
            pair_part[owner] = pair_grads[160 * owner : 160 * owner + 160, :]
        pair_part[3, 0:32, :] = pair_grads[480:512, :]
        pair_part[3, 32:96, :] = to_low(d_start[...])
        pair_part[3, 96:160, :] = jnp.zeros((64, D), jnp.bfloat16)
        for _ in pair_sum(
            pair_part, pair_near, pair_far, pair_out.at[half], 160, pair_send, pair_recv
        ):
            yield
        full = moved(
            pair_out.at[half], pair_out.at[half], core_sem.at[0], core_sem.at[1], {"seq": core}
        )
        full.start()
        yield
        moved(
            pair_out.at[1 - half], pair_out.at[1 - half], core_sem.at[0], core_sem.at[1],
            {"seq": core},
        ).wait_recv()
        full.wait_send()

    def sout_steps():
        loads[1].wait()
        loads[2].wait()
        for head in range(LINE):
            low = to_low(dot_tn(os_rows[:, 128 * head : 128 * head + 128], du_rows[...]))
            for piece in range(4):
                work[
                    4 * (head % 2) + piece, 32 * (head // 2) : 32 * (head // 2) + 32, :
                ] = low[32 * piece : 32 * piece + 32, :]
        for _ in plane_scatter(
            work, core_got, near_got, far_got, total, 128, ring_send, ring_recv
        ):
            yield
        z_part[:, 0:32, :] = to_low(total[...]).reshape(4, 32, D)
        z_part[:, 32:64, :] = out_part[...].reshape(4, 32, D)
        out = [
            moved(
                z_part.at[target], z_got.at[rank], zs_send.at[slot], zs_recv.at[rank],
                {"tensor": target},
            )
            for slot, target in enumerate(ranks)
        ]
        for one in out:
            one.start()
        z_got[rank] = z_part[rank]
        yield
        for slot, target in enumerate(ranks):
            moved(
                z_part.at[target], z_got.at[target], zs_send.at[slot], zs_recv.at[target],
                {"tensor": target},
            ).wait_recv()
        acc = z_got[0].astype(jnp.float32)
        for target in range(1, 4):
            acc = acc + z_got[target].astype(jnp.float32)
        sout_out[me] = to_low(acc)
        for _ in plane_gather(row_halves(sout_out, 64), gather_send, gather_recv):
            yield
        for one in out:
            one.wait_send()

    run_all(sout_steps(), line_steps(), pair_steps())

    def small_over_z(slot, sender, target):
        return moved(
            small_z.at[sender], small_z.at[sender], small_send.at[slot], small_recv.at[sender],
            {"tensor": target},
        )

    for slot, target in enumerate(ranks):
        small_over_z(slot, rank, target).start()
    for slot, target in enumerate(ranks):
        small_over_z(slot, target, target).wait_recv()
    small_p[me] = small_z[0] + small_z[1] + small_z[2] + small_z[3]

    def small_over_plane(slot, sender, target):
        return moved(
            small_p.at[sender], small_p.at[sender], small_send.at[3 + slot],
            small_recv.at[4 + sender],
            {"dp": target // 4, "seq": lax.rem(target, 4)},
        )

    for slot, target in enumerate(spots_of):
        small_over_plane(slot, me, target).start()
    for slot, target in enumerate(spots_of):
        small_over_plane(slot, target, target).wait_recv()
    acc = small_p[0]
    for target in range(1, 8):
        acc = acc + small_p[target]
    small_out[...] = acc
    for slot, target in enumerate(ranks):
        small_over_z(slot, rank, target).wait_send()
    for slot, target in enumerate(spots_of):
        small_over_plane(slot, me, target).wait_send()


def closing(
    partial, pair_grads, tokens, d_hidden, vecs, os_rows, du_rows, d_start, small,
    out_part,
):
    low, wide = jnp.bfloat16, jnp.float32
    shapes = (
        ((2, 128, D), wide),
        ((2, 4, PAIR_ROWS // 4, D), low),
        ((8, 64, D), low),
        ((8, D), wide),
    )
    dma = pltpu.SemaphoreType.DMA
    return pl.pallas_call(
        closing_kernel,
        out_shape=[jax.ShapeDtypeStruct(*one) for one in shapes],
        in_specs=any_specs(1)
        + vmem_specs(4)
        + any_specs(2)
        + vmem_specs(3),
        out_specs=vmem_specs(4),
        scratch_shapes=[
            pltpu.VMEM((256, D), low),
            pltpu.VMEM((256, D), low),
            pltpu.VMEM((2, 4, 128, D), low),
            pltpu.VMEM((2, 2, 4, 128, D), low),
            pltpu.VMEM((2, 128, D), wide),
            pltpu.VMEM((128, D), low),
            pltpu.VMEM((128, D), low),
            pltpu.VMEM((4, PAIR_ROWS // 4, D), low),
            pltpu.VMEM((4, PAIR_ROWS // 8, D), low),
            pltpu.VMEM((2, PAIR_ROWS // 8, D), low),
            pltpu.VMEM((8, 128, D), low),
            pltpu.VMEM((4, 128, D), low),
            pltpu.VMEM((4, 64, D), low),
            pltpu.VMEM((2, 64, D), low),
            pltpu.VMEM((128, D), wide),
            pltpu.VMEM((4, 64, D), low),
            pltpu.VMEM((4, 64, D), low),
            pltpu.VMEM((4, 8, D), wide),
            pltpu.VMEM((8, 8, D), wide),
            dma((1,)), dma((1,)), dma((2, 4)), dma((2, 2, 4)), dma((12,)), dma((12,)), dma((2,)),
            dma((10,)), dma((10,)), dma((3,)), dma((4,)), dma((16,)), dma((8, 2)), dma((10,)),
            dma((12,)), dma((3,)),
        ],
        compiler_params=pltpu.CompilerParams(
            collective_id=6, has_side_effects=True, vmem_limit_bytes=VMEM_LIMIT
        ),
        cost_estimate=pl.CostEstimate(
            flops=30000000000, bytes_accessed=30000000, transcendentals=0
        ),
        name="closing",
    )(
        partial, pair_grads, tokens, d_hidden, vecs, os_rows, du_rows, d_start, small,
        out_part,
    )


def finish_kernel(
    pair, pair_tail, two, ff,
    query, key, value, squery, out, sout, up, down, state,
):
    step = pl.program_id(0)
    wide = jnp.float32
    up[...] = ff[0, 0].astype(wide).T
    down[...] = ff[0, 1].astype(wide)
    sout[...] = two[0, 0:32].astype(wide)
    out[...] = two[0, 32:64].astype(wide)
    for which, target in enumerate((query, key, value, squery)):

        @pl.when(step // 2 == which)
        def _():
            target[...] = pair[0].astype(wide).T

    @pl.when(step == 0)
    def _():
        state[...] = pair_tail[...].reshape(128, D).astype(wide)


def finish_grads(pair, two, ff):
    wide = jnp.float32
    turned = [
        pl.BlockSpec((D, 128), lambda i, w=which: (0, jnp.clip(i - 2 * w, 0, 1)))
        for which in range(4)
    ]
    square = jax.ShapeDtypeStruct((D, 256), wide)
    rows = jax.ShapeDtypeStruct((256, D), wide)
    whole = jax.ShapeDtypeStruct((D, D), wide)
    return pl.pallas_call(
        finish_kernel,
        grid=(8,),
        out_shape=[square] * 4 + [rows] * 2 + [whole] * 2 + [jax.ShapeDtypeStruct((128, D), wide)],
        in_specs=[
            pl.BlockSpec((1, 128, D), lambda i: (i % 2, i // 2, 0)),
            pl.BlockSpec((2, 64, D), lambda i: (0, 8, 0)),
            pl.BlockSpec((1, 64, D), lambda i: (i, 0, 0)),
            pl.BlockSpec((1, 2, 128, D), lambda i: (i, 0, 0, 0)),
        ],
        out_specs=turned
        + [pl.BlockSpec((32, D), lambda i: (i, 0))] * 2
        + [pl.BlockSpec((D, 128), lambda i: (0, i)), pl.BlockSpec((128, D), lambda i: (i, 0))]
        + [pl.BlockSpec((128, D), lambda i: (0, 0))],
        compiler_params=pltpu.CompilerParams(vmem_limit_bytes=VMEM_LIMIT),
        name="finish_grads",
    )(pair, pair, two, ff)


def swap_seq(value):
    return lax.all_to_all(value, "seq", 0, 0, tiled=False)


def line_body(
    inputs,
    seg_starts,
    lengths,
    init_state,
    attn_gain,
    state_gain,
    mlp_gain,
    w_query,
    w_key,
    w_value,
    w_out,
    w_squery,
    w_sout,
    w_up,
    w_down,
    rel_bias,
    gate_bias,
    out_cot,
    state_cot,
):
    low, wide = jnp.bfloat16, jnp.float32
    place = lax.axis_index("seq")
    half = lax.rem(place, 2)
    mine = place // 2
    plane = ("dp", "seq")
    spot = 4 * lax.axis_index("dp") + place
    gate_value = jax.nn.sigmoid(gate_bias)
    vecs = jnp.stack(
        [state_gain, gate_value, mlp_gain, attn_gain] + [jnp.zeros_like(gate_value)] * 4
    )
    marks = jnp.concatenate([seg_starts[:, 0], lengths, jnp.zeros((4,), jnp.int32)])
    marks = jnp.broadcast_to(marks[:, None], (8, 128))
    cot_used = lax.all_gather(out_cot.reshape(256, D), plane, axis=0, tiled=True)
    rows_all, qkv, kept, bias, marks, w_qkv = opening(
        inputs, w_query, w_key, w_value, w_sout, w_out, init_state, vecs, rel_bias, marks
    )

    ff_own = w_up.shape[1] // 8
    piece_of = lambda weight: lax.dynamic_slice_in_dim(weight, spot * 32, 32, 1).T
    back_own = jnp.stack(
        [
            piece_of(w_squery),
            piece_of(w_key),
            piece_of(w_value),
        ]
    )
    pieces = jnp.concatenate(
        [
            lax.dynamic_slice_in_dim(w_up, spot * ff_own, ff_own, 1).T,
            lax.dynamic_slice_in_dim(w_down, spot * ff_own, ff_own, 0),
        ],
        axis=0,
    )
    qkv, pieces, cot_used, back_own = lax.optimization_barrier(
        (qkv, pieces, cot_used, back_own)
    )
    spread = lax.all_gather(pieces, "tensor", axis=0, tiled=True).reshape(4, 2 * ff_own, D)
    mixed, lse_tok, state_rows, state_low, qkvst, lse_st, os_rows, cots, back = forward_chain(
        marks, qkv, kept, w_squery, w_qkv, vecs, bias, state_cot.reshape(4, 64, D), back_own
    )
    hidden_in, grad_hidden, d_mixed, mlp_sums, extra, ff_grads = middle(
        mixed, inputs, kept, spread, cot_used.reshape(8, 256, D), vecs
    )
    d_mixed, ff_grads = lax.optimization_barrier((d_mixed, ff_grads))
    ff_sum = lax.psum_scatter(
        ff_grads.reshape(ff_grads.shape[2] * 8, D), "tensor", scatter_dimension=0, tiled=True
    )
    (
        du_rows, d_start, sums, state_out, tokens_out, out_part, partial, pair_grads,
    ) = backward_chain(
        marks, qkv, d_mixed, lse_tok, qkvst, lse_st, state_rows, init_state, cots,
        back, kept, vecs, bias, extra, hidden_in, rows_all, state_low, w_qkv,
    )
    partial, ff_sum = lax.optimization_barrier((partial, ff_sum))
    ff_total = lax.all_gather(ff_sum, plane, axis=0, tiled=True).reshape(8, 2, ff_own, D)
    small = jnp.concatenate(
        [jnp.zeros((1, D), wide), sums[1:2], mlp_sums[0:1], sums[0:1], sums[2:3], jnp.zeros((3, D), wide)]
    )
    inputs_grad, pair, two_grads, small = closing(
        partial, pair_grads, inputs, grad_hidden, vecs, os_rows.reshape(256, D),
        du_rows.reshape(256, D), d_start, small, out_part,
    )
    pair = pair.reshape(2, PAIR_ROWS, D)
    (
        query_grad, key_grad, value_grad, squery_grad, out_grad, sout_grad, up_grad, down_grad,
        state_grad,
    ) = finish_grads(pair, two_grads, ff_total)
    bias_grad = lax.dynamic_slice_in_dim(
        small[4, : LINE * BUCKETS].reshape(4, 2, BUCKETS), lax.axis_index("tensor"), 1, 0
    )[0].T
    return (
        tokens_out,
        state_out[:, None],
        inputs_grad,
        state_grad,
        small[0],
        small[1],
        small[2],
        query_grad,
        key_grad,
        value_grad,
        out_grad,
        squery_grad,
        sout_grad,
        up_grad,
        down_grad,
        bias_grad,
        small[3],
    )


def solution(mesh):
    return jax.shard_map(
        chosen_body(mesh),
        mesh=mesh,
        in_specs=(
            P("dp", ("seq", "tensor"), None),
            P("dp", "seq"),
            P("dp"),
            P("tensor", None),
            P(),
            P(),
            P(),
            P(None, "tensor"),
            P(None, "tensor"),
            P(None, "tensor"),
            P("tensor", None),
            P(None, "tensor"),
            P("tensor", None),
            P(None, "tensor"),
            P("tensor", None),
            P(None, "tensor"),
            P(),
            P("dp", ("seq", "tensor"), None),
            P("dp", "seq", "tensor", None),
        ),
        out_specs=(
            P("dp", ("seq", "tensor"), None),
            P("dp", "seq", "tensor", None),
            P("dp", ("seq", "tensor"), None),
            P("tensor", None),
            P(),
            P(),
            P(),
            P(None, "tensor"),
            P(None, "tensor"),
            P(None, "tensor"),
            P("tensor", None),
            P(None, "tensor"),
            P("tensor", None),
            P(None, "tensor"),
            P("tensor", None),
            P(None, "tensor"),
            P(),
        ),
        check_vma=False,
    )
```

```python
import jax
import jax.numpy as jnp
from jax import lax
from jax.experimental import pallas as pl
from jax.experimental.pallas import tpu as pltpu
from jax.sharding import PartitionSpec as P

D = 1024
HEAD_DIM = 128
STATES = 512
BLOCK = 512
SEG = 256
BUCKETS = 32


norm_eps = 1e-06
masked_score = -1e30
bucket_edges = (12, 16, 23, 32, 46, 64, 91)


def passed_along(value, axis, steps):
    count = lax.axis_size(axis)
    leading, last = (max(0, -steps), min(count, count - steps))
    return lax.ppermute(value, axis, [(source, source + steps) for source in range(leading, last)])


def bucket_of(relative):
    distance = jnp.abs(relative)
    far_bucket = 8 + sum(((distance >= boundary).astype(jnp.int32) for boundary in bucket_edges))
    near_far = jnp.where(distance < 8, distance, far_bucket)
    return near_far + 16 * (relative > 0).astype(jnp.int32)


def token_mask(seg_start, seq_length, block_index):
    positions = jnp.arange(BLOCK)
    offset = block_index * BLOCK
    prev_valid = (block_index > 0) & (offset - BLOCK + positions < seq_length)
    cur_valid = offset + positions < seq_length
    inside = (positions >= seg_start) & (positions < seg_start + SEG)
    prev_mask = (positions[None, :] > positions[:, None]) & prev_valid[None, :]
    cur_mask = (
        (positions[None, :] <= positions[:, None]) | inside[None, :] & inside[:, None]
    ) & cur_valid[None, :]
    state_mask = jnp.ones((BLOCK, STATES), jnp.bool_)
    return jnp.concatenate([prev_mask, cur_mask, state_mask], axis=1)


def state_mask_of(valid_blk):
    batch_count = valid_blk.shape[0]
    block_part = jnp.broadcast_to(valid_blk[:, None, :], (batch_count, STATES, BLOCK))
    return jnp.concatenate([block_part, jnp.ones((batch_count, STATES, STATES), jnp.bool_)], axis=2)


def layer_norm(values, gain_vec):
    centered = values - jnp.mean(values, axis=-1, keepdims=True)
    spread = jnp.mean(centered * centered, axis=-1, keepdims=True)
    return centered * lax.rsqrt(spread + norm_eps) * gain_vec


def norm_back(values, gain_vec, grad_out):
    _, pullback = jax.vjp(layer_norm, values, gain_vec)
    return pullback(grad_out)


def gelu_back(pre_act, grad_out):
    _, pullback = jax.vjp(jax.nn.gelu, pre_act)
    return pullback(grad_out)[0]


def to_low(array_in):
    return array_in.astype(jnp.bfloat16)


def matmul(left, right):
    return jnp.einsum("...k,kn->...n", left, right, preferred_element_type=jnp.float32)


def matmul_t(left, right):
    return jnp.einsum("...n,kn->...k", left, right, preferred_element_type=jnp.float32)


def outer_sum(left, right):
    left_flat = left.reshape(-1, left.shape[-1])
    right_flat = right.reshape(-1, right.shape[-1])
    return lax.dot_general(
        left_flat, right_flat, (((0,), (0,)), ((), ())), preferred_element_type=jnp.float32
    )


def gather_rows(values):
    return lax.all_gather(values, "tensor", axis=1, tiled=True)


def sum_rows(terms):
    return lax.psum_scatter(
        terms.astype(jnp.bfloat16), "tensor", scatter_dimension=1, tiled=True
    ).astype(jnp.float32)


def pass_state(rows_now):
    return passed_along(rows_now.astype(jnp.bfloat16), "seq", 1).astype(rows_now.dtype)


def pass_back(grad_now):
    return passed_along(grad_now.astype(jnp.bfloat16), "seq", -1).astype(grad_now.dtype)


def split_heads(rows_in):
    return rows_in.reshape(rows_in.shape[0], rows_in.shape[1] // HEAD_DIM, HEAD_DIM)


def score_block(query_rows, key_all, bias_all, allowed):
    scores = (
        jnp.einsum(
            "qhd,khd->hqk",
            split_heads(query_rows),
            split_heads(key_all),
            preferred_element_type=jnp.float32,
        )
        * HEAD_DIM ** (-0.5)
        + bias_all
    )
    return jnp.where(allowed[None], scores, masked_score)


def attend_forward(query_rows, key_all, value_all, bias_all, allowed):
    scores = score_block(query_rows, key_all, bias_all, allowed)
    row_max = jnp.max(scores, axis=-1, keepdims=True)
    exp_scores = jnp.exp(scores - row_max)
    row_total = jnp.sum(exp_scores, axis=-1, keepdims=True)
    weight_all = to_low(exp_scores / row_total)
    mixed_out = jnp.einsum(
        "hqk,khd->qhd", weight_all, split_heads(value_all), preferred_element_type=jnp.float32
    )
    return (
        to_low(mixed_out.reshape(query_rows.shape[0], -1)),
        (row_max + jnp.log(row_total))[..., 0],
    )


def attend_back(query_rows, key_all, value_all, bias_all, allowed, log_total, grad_mixed):
    scores = score_block(query_rows, key_all, bias_all, allowed)
    weight_all = jnp.where(allowed[None], jnp.exp(scores - log_total[..., None]), 0.0)
    grad_heads = split_heads(grad_mixed)
    grad_weight = jnp.einsum(
        "qhd,khd->hqk", grad_heads, split_heads(value_all), preferred_element_type=jnp.float32
    )
    row_inner = jnp.sum(weight_all * grad_weight, axis=-1, keepdims=True)
    grad_scores = to_low(weight_all * (grad_weight - row_inner))
    grad_query = jnp.einsum(
        "hqk,khd->qhd", grad_scores, split_heads(key_all), preferred_element_type=jnp.float32
    ) * HEAD_DIM ** (-0.5)
    grad_keys = jnp.einsum(
        "hqk,qhd->khd", grad_scores, split_heads(query_rows), preferred_element_type=jnp.float32
    ) * HEAD_DIM ** (-0.5)
    grad_values = jnp.einsum(
        "hqk,qhd->khd", to_low(weight_all), grad_heads, preferred_element_type=jnp.float32
    )
    return (
        grad_query.reshape(query_rows.shape[0], -1),
        grad_keys.reshape(key_all.shape[0], -1),
        grad_values.reshape(key_all.shape[0], -1),
        grad_scores,
    )


def bias_lookup(rel_bias, rel_table):
    table_heads = jnp.zeros((rel_bias.shape[1],) + rel_table.shape, jnp.float32)
    for bucket_id in range(BUCKETS):
        table_heads = table_heads + jnp.where(
            rel_table[None] == bucket_id, rel_bias[bucket_id][:, None, None], 0.0
        )
    return table_heads


def bias_sums(score_grad, rel_table):
    grad_wide = score_grad.astype(jnp.float32)
    columns = []
    for bucket_id in range(BUCKETS):
        columns.append(
            jnp.sum(jnp.where(rel_table[None, None] == bucket_id, grad_wide, 0.0), axis=(0, 2, 3))
        )
    return jnp.stack(columns, axis=0)


def body(
    inputs,
    seg_starts,
    lengths,
    init_state,
    attn_gain,
    state_gain,
    mlp_gain,
    w_query,
    w_key,
    w_value,
    w_out,
    w_squery,
    w_sout,
    w_up,
    w_down,
    rel_bias,
    gate_bias,
    out_cot,
    state_cot,
):
    seq_count = inputs.shape[0]
    chain_length = lax.axis_size("seq")
    block_index = lax.axis_index("seq")
    is_first = block_index == 0
    width_local = w_query.shape[1]
    head_count = width_local // HEAD_DIM
    gate_value = jax.nn.sigmoid(gate_bias)
    positions = jnp.arange(BLOCK)
    inputs_wide = inputs.astype(jnp.float32)
    tokens_low = gather_rows(to_low(layer_norm(inputs_wide, attn_gain)))
    query_tok = to_low(matmul(tokens_low, w_query))
    key_tok = to_low(matmul(tokens_low, w_key))
    value_tok = to_low(matmul(tokens_low, w_value))
    key_prev, value_prev = passed_along((key_tok, value_tok), "seq", 1)
    valid_keys = (block_index * BLOCK + positions)[None, :] < lengths[:, None]
    batched_attend = jax.vmap(attend_forward, in_axes=(0, 0, 0, None, 0))
    batched_back = jax.vmap(attend_back, in_axes=(0, 0, 0, None, 0, 0, 0))

    def state_forward(state_rows, key_blk, value_blk, valid_blk):
        state_low = lax.all_gather(
            to_low(layer_norm(state_rows, state_gain)), "tensor", axis=1, tiled=True
        )
        query_st = to_low(matmul(state_low, w_squery))
        key_st = to_low(matmul(state_low, w_key))
        value_st = to_low(matmul(state_low, w_value))
        key_all = jnp.concatenate([key_blk, key_st], axis=1)
        value_all = jnp.concatenate([value_blk, value_st], axis=1)
        mixed_st, lse_st = batched_attend(
            query_st, key_all, value_all, 0.0, state_mask_of(valid_blk)
        )
        update = lax.psum_scatter(
            matmul(mixed_st, w_sout).astype(jnp.bfloat16), "tensor", scatter_dimension=1, tiled=True
        ).astype(jnp.float32)
        state_next = gate_value * state_rows + (1.0 - gate_value) * update
        return (state_next, (state_low, query_st, key_st, value_st, mixed_st, lse_st, update))

    def state_backward(
        grad_out, state_rows, kept_one, key_blk, value_blk, valid_blk, extra_key, extra_value
    ):
        state_low, query_st, key_st, value_st, mixed_st, lse_st, update = kept_one
        gate_part = (
            jnp.sum(grad_out * (state_rows - update), axis=(0, 1)) * gate_value * (1.0 - gate_value)
        )
        grad_update = lax.all_gather(
            to_low((1.0 - gate_value) * grad_out), "tensor", axis=1, tiled=True
        )
        grad_mixed_st = to_low(matmul_t(grad_update, w_sout))
        sout_part = outer_sum(mixed_st, grad_update)
        key_all = jnp.concatenate([key_blk, key_st], axis=1)
        value_all = jnp.concatenate([value_blk, value_st], axis=1)
        grad_query_st, grad_keys_st, grad_values_st, _ = batched_back(
            query_st, key_all, value_all, 0.0, state_mask_of(valid_blk), lse_st, grad_mixed_st
        )
        query_low = to_low(grad_query_st)
        key_low = to_low(grad_keys_st[:, BLOCK:] + extra_key)
        value_low = to_low(grad_values_st[:, BLOCK:] + extra_value)
        squery_part = outer_sum(state_low, query_low)
        key_part = outer_sum(state_low, key_low)
        value_part = outer_sum(state_low, value_low)
        terms = (
            matmul_t(query_low, w_squery) + matmul_t(key_low, w_key) + matmul_t(value_low, w_value)
        )
        grad_normed = lax.psum_scatter(
            terms.astype(jnp.bfloat16), "tensor", scatter_dimension=1, tiled=True
        ).astype(jnp.float32)
        grad_rows_norm, gain_part = norm_back(state_rows, state_gain, grad_normed)
        grad_in = gate_value * grad_out + grad_rows_norm
        block_grads = (grad_keys_st[:, :BLOCK], grad_values_st[:, :BLOCK])
        return (
            grad_in,
            block_grads,
            (squery_part, key_part, value_part, sout_part, gain_part, gate_part),
        )

    zeros_rows = jnp.zeros((seq_count,) + init_state.shape, jnp.float32)
    narrow_zero = jnp.zeros((seq_count, STATES, width_local), jnp.bfloat16)
    stored_start = (
        zeros_rows,
        zeros_rows,
        jnp.zeros((seq_count, STATES, D), jnp.bfloat16),
        narrow_zero,
        narrow_zero,
        narrow_zero,
        narrow_zero,
        jnp.zeros((seq_count, head_count, STATES), jnp.float32),
        zeros_rows,
    )

    def forward_turn(turn_index, carry):
        incoming, stored_now = carry
        order_index = turn_index - block_index
        is_live = (order_index >= 0) & (order_index < seq_count)
        picked = jnp.clip(order_index, 0, seq_count - 1)
        rows_now = jnp.where(is_first, init_state[None], incoming)
        key_one = lax.dynamic_slice_in_dim(key_tok, picked, 1, 0)
        value_one = lax.dynamic_slice_in_dim(value_tok, picked, 1, 0)
        valid_one = lax.dynamic_slice_in_dim(valid_keys, picked, 1, 0)
        rows_next, kept_one = state_forward(rows_now, key_one, value_one, valid_one)
        fresh = (rows_now, rows_next) + kept_one
        stored_now = tuple(
            (
                jnp.where(
                    is_live,
                    lax.dynamic_update_slice_in_dim(whole_array, fresh_part, picked, 0),
                    whole_array,
                )
                for whole_array, fresh_part in zip(stored_now, fresh)
            )
        )
        return (pass_state(rows_next), stored_now)

    incoming_start = jnp.zeros((1,) + init_state.shape, jnp.float32)
    _, stored_all = lax.fori_loop(
        0, chain_length + seq_count - 1, forward_turn, (incoming_start, stored_start)
    )
    state_in = stored_all[0]
    state_out = stored_all[1]
    kept = stored_all[2:]
    key_all_tok = jnp.concatenate([key_prev, key_tok, kept[2]], axis=1)
    value_all_tok = jnp.concatenate([value_prev, value_tok, kept[3]], axis=1)
    allowed_tok = jax.vmap(token_mask, in_axes=(0, 0, None))(seg_starts[:, 0], lengths, block_index)
    rel_table = bucket_of((jnp.arange(2 * BLOCK) - BLOCK)[None, :] - positions[:, None])
    full_bias = jnp.concatenate(
        [bias_lookup(rel_bias, rel_table), jnp.zeros((head_count, BLOCK, STATES), jnp.float32)],
        axis=2,
    )
    mixed_tok, lse_tok = batched_attend(
        query_tok, key_all_tok, value_all_tok, full_bias, allowed_tok
    )
    hidden_in = inputs_wide + sum_rows(matmul(mixed_tok, w_out))
    mid_low = gather_rows(to_low(layer_norm(hidden_in, mlp_gain)))
    pre_act = matmul(mid_low, w_up)
    hidden_low = to_low(jax.nn.gelu(pre_act))
    mlp_rows = sum_rows(matmul(hidden_low, w_down))
    tokens_out = (hidden_in + mlp_rows).astype(jnp.bfloat16)
    cot_wide = out_cot.astype(jnp.float32)
    cot_used = gather_rows(out_cot)
    grad_hidden_act = matmul_t(cot_used, w_down)
    down_grad = outer_sum(hidden_low, cot_used)
    grad_pre = to_low(gelu_back(pre_act, grad_hidden_act))
    up_grad = outer_sum(mid_low, grad_pre)
    grad_normed_mid = sum_rows(matmul_t(grad_pre, w_up))
    grad_mid_in, mlp_gain_grad = norm_back(hidden_in, mlp_gain, grad_normed_mid)
    grad_hidden = cot_wide + grad_mid_in
    grad_attn_low = gather_rows(to_low(grad_hidden))
    grad_mixed = to_low(matmul_t(grad_attn_low, w_out))
    out_grad = outer_sum(mixed_tok, grad_attn_low)
    grad_query_tok, grad_keys_tok, grad_values_tok, grad_scores = batched_back(
        query_tok, key_all_tok, value_all_tok, full_bias, allowed_tok, lse_tok, grad_mixed
    )
    bias_grad = bias_sums(grad_scores[..., : 2 * BLOCK], rel_table)
    grad_key_next, grad_value_next = (
        passed_along(grad_keys_tok[:, :BLOCK].astype(jnp.bfloat16), "seq", -1).astype(jnp.float32),
        passed_along(grad_values_tok[:, :BLOCK].astype(jnp.bfloat16), "seq", -1).astype(
            jnp.float32
        ),
    )
    grad_key_own = grad_keys_tok[:, BLOCK : 2 * BLOCK] + grad_key_next
    grad_value_own = grad_values_tok[:, BLOCK : 2 * BLOCK] + grad_value_next
    grad_key_st_tok = grad_keys_tok[:, 2 * BLOCK :]
    grad_value_st_tok = grad_values_tok[:, 2 * BLOCK :]
    cot_rows = state_cot[:, 0].astype(jnp.float32)
    wide_zero = jnp.zeros((seq_count, BLOCK, width_local), jnp.float32)
    stored_back = (zeros_rows, wide_zero, wide_zero)
    totals_start = (
        jnp.zeros((D, width_local), jnp.float32),
        jnp.zeros((D, width_local), jnp.float32),
        jnp.zeros((D, width_local), jnp.float32),
        jnp.zeros((width_local, D), jnp.float32),
        jnp.zeros((D,), jnp.float32),
        jnp.zeros((D,), jnp.float32),
    )

    def backward_turn(turn_index, carry):
        incoming, stored_now, totals_now = carry
        order_index = turn_index - (chain_length - 1 - block_index)
        is_live = (order_index >= 0) & (order_index < seq_count)
        picked = jnp.clip(order_index, 0, seq_count - 1)

        def slice_one(whole_array):
            return lax.dynamic_slice_in_dim(whole_array, picked, 1, 0)

        grad_out = slice_one(cot_rows) + incoming
        kept_one = tuple((slice_one(kept_array) for kept_array in kept))
        grad_in, block_one, parts_one = state_backward(
            grad_out,
            slice_one(state_in),
            kept_one,
            slice_one(key_tok),
            slice_one(value_tok),
            slice_one(valid_keys),
            slice_one(grad_key_st_tok),
            slice_one(grad_value_st_tok),
        )
        fresh = (grad_in,) + block_one
        stored_now = tuple(
            (
                jnp.where(
                    is_live,
                    lax.dynamic_update_slice_in_dim(whole_array, fresh_part, picked, 0),
                    whole_array,
                )
                for whole_array, fresh_part in zip(stored_now, fresh)
            )
        )
        totals_now = tuple(
            (
                total_now + jnp.where(is_live, part_now, 0.0)
                for total_now, part_now in zip(totals_now, parts_one)
            )
        )
        return (pass_back(grad_in), stored_now, totals_now)

    incoming_start = jnp.zeros((1,) + init_state.shape, jnp.float32)
    _, stored_done, weight_parts = lax.fori_loop(
        0, chain_length + seq_count - 1, backward_turn, (incoming_start, stored_back, totals_start)
    )
    grad_in_all, grad_key_blk, grad_value_blk = stored_done
    query_low = to_low(grad_query_tok)
    key_low = to_low(grad_key_own + grad_key_blk)
    value_low = to_low(grad_value_own + grad_value_blk)
    query_grad = outer_sum(tokens_low, query_low)
    key_grad = outer_sum(tokens_low, key_low) + weight_parts[1]
    value_grad = outer_sum(tokens_low, value_low) + weight_parts[2]
    grad_tokens = sum_rows(
        matmul_t(query_low, w_query) + matmul_t(key_low, w_key) + matmul_t(value_low, w_value)
    )
    grad_in_norm, attn_gain_grad = norm_back(inputs_wide, attn_gain, grad_tokens)
    inputs_grad = grad_hidden + grad_in_norm
    state_part = jnp.where(is_first, jnp.sum(grad_in_all, axis=0), 0.0)
    gains = lax.psum(
        jnp.stack([attn_gain_grad, weight_parts[4], mlp_gain_grad, weight_parts[5]]), "tensor"
    )
    totals = (
        lax.psum(query_grad.astype(jnp.bfloat16), ("dp", "seq")).astype(jnp.float32),
        lax.psum(key_grad.astype(jnp.bfloat16), ("dp", "seq")).astype(jnp.float32),
        lax.psum(value_grad.astype(jnp.bfloat16), ("dp", "seq")).astype(jnp.float32),
        lax.psum(out_grad.astype(jnp.bfloat16), ("dp", "seq")).astype(jnp.float32),
        lax.psum(weight_parts[0].astype(jnp.bfloat16), ("dp", "seq")).astype(jnp.float32),
        lax.psum(weight_parts[3].astype(jnp.bfloat16), ("dp", "seq")).astype(jnp.float32),
        lax.psum(up_grad.astype(jnp.bfloat16), ("dp", "seq")).astype(jnp.float32),
        lax.psum(down_grad.astype(jnp.bfloat16), ("dp", "seq")).astype(jnp.float32),
        lax.psum(bias_grad.astype(jnp.bfloat16), ("dp", "seq")).astype(jnp.float32),
        lax.psum(state_part.astype(jnp.bfloat16), ("dp", "seq")).astype(jnp.float32),
        lax.psum(gains.astype(jnp.bfloat16), ("dp", "seq")).astype(jnp.float32),
    )
    gain_total = totals[10]
    return (
        tokens_out,
        state_out[:, None],
        inputs_grad,
        totals[9],
        gain_total[0],
        gain_total[1],
        gain_total[2],
        totals[0],
        totals[1],
        totals[2],
        totals[3],
        totals[4],
        totals[5],
        totals[6],
        totals[7],
        totals[8],
        gain_total[3],
    )


def chosen_body(mesh):
    if mesh.shape["seq"] == 4 and mesh.shape["tensor"] == 4:
        return line_body
    return body


MESH_ID = pl.DeviceIdType.MESH
ROWS = 128
CHUNKS = BLOCK // ROWS
LINE = 8
SCALE = HEAD_DIM ** (-0.5)
VMEM_LIMIT = 60 * 1024 * 1024


def dot_nn(left, right):
    return lax.dot_general(left, right, (((1,), (0,)), ((), ())), preferred_element_type=jnp.float32)


def dot_nt(left, right):
    return lax.dot_general(left, right, (((1,), (1,)), ((), ())), preferred_element_type=jnp.float32)


def dot_tn(left, right):
    return lax.dot_general(left, right, (((0,), (0,)), ((), ())), preferred_element_type=jnp.float32)


def line_place():
    place = lax.axis_index("seq")
    half = lax.rem(place, 2)
    rank = lax.axis_index("tensor")
    return place, half, rank


def span(index, size):
    return pl.ds(pl.multiple_of(index * size, size), size)


def fetch_pieces(kept, first, rows, target, sem):
    for owner in range(8):
        pltpu.make_async_copy(
            kept.at[owner, :, pl.ds(first, rows), :], target.at[:, owner], sem
        ).start()


def fetch_columns(weights, target, sem):
    half = lax.rem(lax.axis_index("seq"), 2)
    for index, weight in enumerate(weights):
        pltpu.make_async_copy(
            weight.at[:, span(half, 128)], target.at[:, pl.ds(128 * index, 128)], sem
        ).start()


def fetched(target, sem):
    pltpu.make_async_copy(target, target, sem).wait()


def norm_parts(rows):
    centered = rows - jnp.mean(rows, axis=-1, keepdims=True)
    spread = jnp.mean(centered * centered, axis=-1, keepdims=True)
    return centered, lax.rsqrt(spread + norm_eps)


def mark(marks, block_id, row):
    return marks[block_id, pl.ds(row, 1), 0:1]


def sequence_marks(marks, block_id):
    mine = lax.axis_index("seq") // 2
    return mark(marks, block_id, mine), mark(marks, 0, 2 + mine)


def token_masks(marks, block_id, first_row):
    start, length = sequence_marks(marks, block_id)
    row = lax.broadcasted_iota(jnp.int32, (ROWS, BLOCK), 0) + first_row
    col = lax.broadcasted_iota(jnp.int32, (ROWS, BLOCK), 1)
    prev_limit = jnp.where(block_id > 0, length - (block_id - 1) * BLOCK, 0)
    prev_ok = (col > row) & (col < prev_limit)
    row_in = (row >= start) & (row < start + SEG)
    col_in = (col >= start) & (col < start + SEG)
    cur_ok = ((col <= row) | (row_in & col_in)) & (col < length - block_id * BLOCK)
    return prev_ok, cur_ok


def state_block_mask(marks, block_id):
    _, length = sequence_marks(marks, block_id)
    col = lax.broadcasted_iota(jnp.int32, (ROWS, BLOCK), 1)
    return col < length - block_id * BLOCK


def softmax_of(score_parts):
    top = jnp.max(score_parts[0], axis=-1, keepdims=True)
    for part in score_parts[1:]:
        top = jnp.maximum(top, jnp.max(part, axis=-1, keepdims=True))
    raised = [jnp.exp(part - top) for part in score_parts]
    total = jnp.sum(raised[0], axis=-1, keepdims=True)
    for part in raised[1:]:
        total = total + jnp.sum(part, axis=-1, keepdims=True)
    inverse = 1.0 / total
    return [to_low(part * inverse) for part in raised], top + jnp.log(total)


def token_scores(scal, qkv, qkvst, bias, block_id, chunk):
    rows = span(chunk, ROWS)
    prev_id = jnp.maximum(block_id - 1, 0)
    query = qkv[block_id, rows, 0:128]
    prev_ok, cur_ok = token_masks(scal, block_id, chunk * ROWS)
    prev = dot_nt(query, qkv[prev_id, :, 128:256]) * SCALE + bias[rows, 0:BLOCK]
    cur = dot_nt(query, qkv[block_id, :, 128:256]) * SCALE + bias[rows, BLOCK : 2 * BLOCK]
    stt = dot_nt(query, qkvst[block_id, :, 128:256]) * SCALE
    prev = jnp.where(prev_ok, prev, masked_score)
    cur = jnp.where(cur_ok, cur, masked_score)
    return query, (prev, cur, stt)


def state_scores(scal, qkv, qkvst, block_id, chunk):
    query = qkvst[block_id, span(chunk, ROWS), 0:128]
    tok = dot_nt(query, qkv[block_id, :, 128:256]) * SCALE
    tok = jnp.where(state_block_mask(scal, block_id), tok, masked_score)
    stt = dot_nt(query, qkvst[block_id, :, 128:256]) * SCALE
    return query, (tok, stt)


HALVES = 2
HALF_ROWS = STATES // HALVES
HALF_CHUNKS = HALF_ROWS // ROWS


def forward_kernel(
    marks, qkv, kept, w_squery, w_qkv, vecs, bias, state_cot, back_own,
    o_out, lse_out, state_rows, low_out, qkvst, lse_st, os_rows, cots, back,
    held, os_all, state_low, w_sout, start, w_state,
    way_send, core_send, recv_sem, local_sem, low_sem, cot_send, cot_recv,
    piece_send, piece_recv, ring_send, ring_recv,
):
    side, place, half, rank = plane_place()
    me = plane_index(side, place)
    partner = place + 1 - 2 * half
    head = 2 * rank + half
    fetch_pieces(kept, 32, 16, start, local_sem.at[0])
    fetch_columns((w_squery,), w_state, local_sem.at[2])
    fetch_pieces(kept, 0, 32, w_sout, local_sem.at[1])
    own_cot = pltpu.make_async_copy(state_cot.at[place], cots.at[place], local_sem.at[4])
    own_cot.start()
    own_piece = pltpu.make_async_copy(back_own, back.at[me, rank], local_sem.at[3])
    own_piece.start()
    ranks = [lax.rem(rank + step, 4) for step in (1, 2, 3)]
    seats = [lax.rem(place + step, 4) for step in (1, 2, 3)]
    barrier = pltpu.get_barrier_semaphore()
    for target in [{"tensor": one} for one in ranks] + [{"seq": one} for one in seats] + [
        {"dp": 1 - side}
    ]:
        pl.semaphore_signal(barrier, inc=1, device_id=target, device_id_type=MESH_ID)
    fetched(start, local_sem.at[0])
    held[...] = start[...].reshape(STATES, D).astype(jnp.float32)
    gain = vecs[0:1, :]
    gate = vecs[1:2, :]
    fetched(w_state, local_sem.at[2])

    def project(block_id, part):
        def one(chunk, _):
            rows = span(chunk, ROWS)
            centered, scale = norm_parts(held[rows, :])
            low = to_low(centered * scale * gain)
            state_low[block_id, rows, :] = low
            qkvst[block_id, rows, 0:128] = to_low(dot_nn(low, w_state[...]))
            qkvst[block_id, rows, 128:384] = to_low(dot_nn(low, w_qkv[:, 128:384]))
            return 0

        lax.fori_loop(HALF_CHUNKS * part, HALF_CHUNKS * (part + 1), one, 0)

    pl.semaphore_wait(barrier, 7)

    def piece_move(origin, part, slot, target):
        return pltpu.make_async_remote_copy(
            src_ref=back_own.at[part],
            dst_ref=back.at[me, origin, part],
            send_sem=piece_send.at[part, slot],
            recv_sem=piece_recv.at[part, origin],
            device_id={"tensor": target},
            device_id_type=MESH_ID,
        )

    def send_piece(part):
        for slot, target in enumerate(ranks):
            piece_move(rank, part, slot, target).start()

    gather = plane_gather(
        lambda owner, part: back.at[owner, pl.ds(2 * part, 2)], ring_send, ring_recv
    )
    next(gather)
    send_piece(0)
    for part in range(HALVES):
        project(0, part)
    right, left = {"tensor": lax.rem(rank + 1, 4)}, {"tensor": lax.rem(rank + 3, 4)}

    def moved(block_id, part, which, sem, target):
        view = os_all.at[block_id, pl.ds(HALF_ROWS * part, HALF_ROWS), span(which, 128)]
        return pltpu.make_async_remote_copy(
            src_ref=view,
            dst_ref=view,
            send_sem=sem,
            recv_sem=recv_sem.at[block_id, part, which],
            device_id=target,
            device_id_type=MESH_ID,
        )

    def cot_move(index, origin, slot, target):
        return pltpu.make_async_remote_copy(
            src_ref=state_cot.at[index],
            dst_ref=cots.at[origin],
            send_sem=cot_send.at[slot],
            recv_sem=cot_recv.at[origin],
            device_id={"seq": target},
            device_id_type=MESH_ID,
        )

    for slot, target in enumerate(seats):
        cot_move(target, place, slot, target).start()
    fetched(w_sout, local_sem.at[1])

    def origin_of(way, distance):
        if way == 0:
            return jnp.maximum(rank - distance, 0)
        return jnp.minimum(rank + distance, 3)

    def ways(distance):
        return (
            (0, rank >= distance, (rank >= distance) & (rank < 3), right),
            (1, rank + distance <= 3, (rank + distance <= 3) & (rank > 0), left),
        )

    def relay(block_id, part, distance, waiting):
        for way, comes, goes, target in ways(distance):
            which = 2 * origin_of(way, distance) + half
            sem = way_send.at[block_id, part, min(distance, 2), way]
            core_sem = core_send.at[block_id, part, which // 2]
            if distance > 0:

                @pl.when(comes)
                def _():
                    to_core = moved(block_id, part, which, core_sem, {"seq": partner})
                    if waiting:
                        moved(block_id, part, which, sem, target).wait_recv()
                        to_core.start()
                    else:
                        to_core.wait_send()

            if distance < 3:

                @pl.when(goes)
                def _():
                    one = moved(block_id, part, which, sem, target)
                    if waiting:
                        one.start()
                    else:
                        one.wait_send()

        if distance == 0:
            mine = moved(
                block_id, part, head, core_send.at[block_id, part, rank], {"seq": partner}
            )
            if waiting:
                mine.start()
            else:
                mine.wait_send()

    def one_block(block_id, _):
        def attend_state(chunk, _):
            rows = span(chunk, ROWS)
            _, parts = state_scores(marks, qkv, qkvst, block_id, chunk)
            (w_tok, w_stt), total = softmax_of(parts)
            mixed = dot_nn(w_tok, qkv[block_id, :, 256:384]) + dot_nn(
                w_stt, qkvst[block_id, :, 256:384]
            )
            os_all[block_id, rows, span(head, 128)] = to_low(mixed)
            lse_st[block_id, rows, :] = total
            return 0

        def attend_token(chunk, _):
            rows = span(chunk, ROWS)
            _, parts = token_scores(marks, qkv, qkvst, bias, block_id, chunk)
            weights, total = softmax_of(parts)
            prev_id = jnp.maximum(block_id - 1, 0)
            mixed = (
                dot_nn(weights[0], qkv[prev_id, :, 256:384])
                + dot_nn(weights[1], qkv[block_id, :, 256:384])
                + dot_nn(weights[2], qkvst[block_id, :, 256:384])
            )
            o_out[block_id, rows, :] = to_low(mixed)
            lse_out[block_id, rows, :] = total
            return 0

        def attend_both(part, _):
            lax.fori_loop(HALF_CHUNKS * part, HALF_CHUNKS * (part + 1), attend_state, 0)
            for value in range(HALVES):

                @pl.when(part == value)
                def _():
                    relay(block_id, value, 0, True)

            return 0

        lax.fori_loop(0, HALVES, attend_both, 0)
        pltpu.make_async_copy(
            state_low.at[block_id], low_out.at[block_id], low_sem.at[block_id]
        ).start()

        @pl.when(block_id == 2)
        def _():
            own_piece.wait()
            for part in range(3):
                for slot, target in enumerate(ranks):
                    piece_move(target, part, slot, target).wait_recv()
            next(gather)

        @pl.when(block_id == 3)
        def _():
            next(gather)
            next(gather)

        def between(step, _):
            for value, (distance, part) in enumerate(((1, 0), (1, 1), (2, 0), (2, 1))):

                @pl.when(step == value)
                def _():
                    relay(block_id, part, distance, True)

            return attend_token(step, 0)

        lax.fori_loop(0, 4, between, 0)

        def settle(part, _):
            for value in range(HALVES):

                @pl.when(part == value)
                def _():
                    relay(block_id, value, 3, True)
                    for origin in range(4):
                        moved(
                            block_id, value, 2 * origin + 1 - half,
                            core_send.at[block_id, value, origin], {"seq": partner},
                        ).wait_recv()

                    if value == HALVES - 1:
                        for turn in (0, 1):

                            @pl.when(block_id == turn)
                            def _():
                                send_piece(turn + 1)

            def update(chunk, _):
                rows = span(chunk, ROWS)
                change = dot_nn(os_all[block_id, rows, :], w_sout[...].reshape(D, D))
                held[rows, :] = gate * held[rows, :] + (1.0 - gate) * change
                return 0

            lax.fori_loop(HALF_CHUNKS * part, HALF_CHUNKS * (part + 1), update, 0)

            @pl.when(block_id < 3)
            def _():
                project(block_id + 1, part)

            return 0

        lax.fori_loop(0, HALVES, settle, 0)
        state_rows[block_id] = held[span(rank, 128), :]
        os_rows[block_id] = os_all[block_id, span(head, 64), :]
        return 0

    lax.fori_loop(0, 4, one_block, 0)

    def drain(block_id, _):
        for part in range(HALVES):
            for distance in range(4):
                relay(block_id, part, distance, False)
        pltpu.make_async_copy(
            state_low.at[block_id], low_out.at[block_id], low_sem.at[block_id]
        ).wait()
        return 0

    lax.fori_loop(0, 4, drain, 0)
    own_cot.wait()
    for part in range(3):
        for slot, target in enumerate(ranks):
            piece_move(rank, part, slot, target).wait_send()
    for _ in gather:
        pass
    for slot, target in enumerate(seats):
        cot_move(target, place, slot, target).wait_send()
        cot_move(place, target, slot, target).wait_recv()


def any_specs(count):
    return [pl.BlockSpec(memory_space=pl.ANY)] * count


def vmem_specs(count):
    return [pl.BlockSpec(memory_space=pltpu.VMEM)] * count


def forward_chain(
    marks, qkv, kept, w_squery, w_qkv, vecs, bias, state_cot, back_own
):
    low, wide = jnp.bfloat16, jnp.float32
    shapes = (
        ((4, BLOCK, 128), low),
        ((4, BLOCK, 1), wide),
        ((4, 128, D), wide),
        ((4, STATES, D), low),
        ((4, STATES, 384), low),
        ((4, STATES, 1), wide),
        ((4, 64, D), low),
        ((4, 64, D), low),
        ((8, 4, 3, 32, D), low),
    )
    dma = pltpu.SemaphoreType.DMA
    return pl.pallas_call(
        forward_kernel,
        out_shape=[jax.ShapeDtypeStruct(*one) for one in shapes],
        in_specs=vmem_specs(2) + any_specs(2) + vmem_specs(3) + any_specs(2),
        out_specs=vmem_specs(3) + any_specs(1) + vmem_specs(3) + any_specs(2),
        scratch_shapes=[
            pltpu.VMEM((STATES, D), wide),
            pltpu.VMEM((4, STATES, D), low),
            pltpu.VMEM((4, STATES, D), low),
            pltpu.VMEM((4, 8, 32, D), low),
            pltpu.VMEM((4, 8, 16, D), low),
            pltpu.VMEM((D, 128), low),
            dma((4, HALVES, 3, 2)),
            dma((4, HALVES, 4)),
            dma((4, HALVES, 8)),
            dma((5,)),
            dma((4,)),
            dma((3,)),
            dma((4,)),
            dma((3, 3)),
            dma((3, 4)),
            dma((14,)),
            dma((8, 2)),
        ],
        compiler_params=pltpu.CompilerParams(
            collective_id=1, has_side_effects=True, vmem_limit_bytes=VMEM_LIMIT
        ),
        cost_estimate=pl.CostEstimate(
            flops=60000000000, bytes_accessed=60000000, transcendentals=0
        ),
        name="forward_chain",
    )(marks, qkv, kept, w_squery, w_qkv, vecs, bias, state_cot, back_own)


def backward_kernel(
    scal, qkv, d_o, lse_tok, qkvst, lse_st, state_rows, begin, cots, back, kept, vecs, bias,
    extra, hidden, rows_hbm, low_hbm, w_qkv,
    du_rows, d_start, sums, state_out, tokens_out, out_part, partial, pair_grads,
    dz_sum, diag, d_qkv, d_qkvst, rows_buf, low_buf, leave, came, grad_acc,
    key_acc, value_acc, st_key, st_value, dos_rows, dos_got, d_got, grad_in,
    states, w_back, w_sout, work, core_got, near_got, far_got, total,
    send_sem, recv_sem, local_sem, side_sem, ring_send, ring_recv, buf_sem, core_sem, came_sem,
):
    place, half, rank = line_place()
    own_rows = pl.ds(pl.multiple_of(half * 64, 64), 64)
    loads = [
        pltpu.make_async_copy(
            state_rows.at[:, own_rows, :], states.at[pl.ds(1, 4)], local_sem.at[0]
        ),
        pltpu.make_async_copy(
            state_rows.at[place], state_out.at[place // 2], local_sem.at[3]
        ),
        pltpu.make_async_copy(extra, work, local_sem.at[4]),
    ]
    for one in loads:
        one.start()
    fetch_pieces(kept, 0, 32, w_sout, local_sem.at[1])
    for owner in range(8):
        pltpu.make_async_copy(
            back.at[owner], w_back.at[:, owner // 4, :, owner % 4], local_sem.at[2]
        ).start()
    states[0] = to_low(begin[own_rows, :]).astype(jnp.float32)

    def block_loads(block_id):
        slot = lax.rem(block_id, 2)
        return [
            pltpu.make_async_copy(
                source.at[block_id], target.at[slot], buf_sem.at[index, slot]
            )
            for index, (source, target) in enumerate(((rows_hbm, rows_buf), (low_hbm, low_buf)))
        ]

    for one in block_loads(3):
        one.start()
    head = 2 * rank + half
    peers = []
    for step in (4, 3, 5, 2, 6, 1, 7):
        other = lax.rem(head + step, LINE)
        peers.append((other, place - half + lax.rem(other, 2), other // 2))
    barrier = pltpu.get_barrier_semaphore()
    for _, seq_to, rank_to in peers:
        pl.semaphore_signal(
            barrier, inc=1, device_id={"seq": seq_to, "tensor": rank_to}, device_id_type=MESH_ID
        )
    beside = lax.rem(place + 2, 4)
    pl.semaphore_signal(barrier, inc=1, device_id={"seq": beside}, device_id_type=MESH_ID)
    pl.semaphore_signal(
        barrier, inc=1, device_id={"dp": 1 - lax.axis_index("dp")}, device_id_type=MESH_ID
    )
    plane_steps = plane_scatter(
        work, core_got, near_got, far_got, total, 384, ring_send, ring_recv
    )
    next(plane_steps)

    def aside(block_id, row_set):
        return pltpu.make_async_remote_copy(
            src_ref=state_rows.at[block_id],
            dst_ref=state_out.at[row_set],
            send_sem=side_sem.at[0],
            recv_sem=side_sem.at[1],
            device_id={"seq": beside},
            device_id_type=MESH_ID,
        )

    gain = vecs[0:1, :]
    gate = vecs[1:2, :]
    key_acc[...] = jnp.zeros_like(key_acc)
    value_acc[...] = jnp.zeros_like(value_acc)
    dz_sum[...] = jnp.zeros_like(dz_sum)
    sums[...] = jnp.zeros_like(sums)
    grad_in[...] = jnp.zeros_like(grad_in)
    grad_acc[...] = jnp.zeros_like(grad_acc)
    core = place + 1 - 2 * half

    def place_in(block_id, owner):
        return jnp.where(block_id == owner, 1, 0)

    def leaving(slot):
        return pltpu.make_async_remote_copy(
            src_ref=leave.at[slot],
            dst_ref=came.at[slot],
            send_sem=core_sem.at[slot],
            recv_sem=came_sem.at[slot],
            device_id={"seq": core},
            device_id_type=MESH_ID,
        )

    def add_came(slot):
        leaving(slot).wait_recv()

        def one(chunk, _):
            partial[slot, chunk] = to_low(
                partial[slot, chunk].astype(jnp.float32)
                + came[slot, span(chunk, 128), :].astype(jnp.float32)
            )
            return 0

        lax.fori_loop(0, 4, one, 0)

    def bucket_sums():
        diag[...] = jnp.zeros_like(diag)

        def one(group, _):
            rows = dz_sum[span(group, 8), :]
            wide = jnp.concatenate([rows, jnp.zeros((8, WIDE - 2 * BLOCK), jnp.float32)], axis=1)
            diag[...] += pltpu.roll(wide, lax.rem(WIDE - 8 * group, WIDE), 1)
            return 0

        lax.fori_loop(0, BLOCK // 8, one, 0)
        line = diag[...]
        row = lax.broadcasted_iota(jnp.int32, (8, WIDE), 0)
        for step in (1, 2, 4):
            line = jnp.where(row // step % 2 == 1, pltpu.roll(line, WIDE - step, 1), line)
        lane = lax.broadcasted_iota(jnp.int32, (8, WIDE), 1)
        bucket_ids = bucket_of(jnp.where(lane >= WIDE - BLOCK, lane - WIDE - BLOCK, lane - BLOCK))
        spot = lax.broadcasted_iota(jnp.int32, (1, 256), 1) - BUCKETS * head
        placed = jnp.zeros((1, 256), jnp.float32)
        for bucket_id in range(BUCKETS):
            chosen = jnp.where(bucket_ids == bucket_id, line, 0.0)
            value = jnp.sum(jnp.sum(chosen, axis=0, keepdims=True), axis=1, keepdims=True)
            placed = jnp.where(spot == bucket_id, value, placed)
        sums[2:3, 0:256] = placed

    def block_products(block_id):
        slot = lax.rem(block_id, 2)
        for one in block_loads(block_id):
            one.wait()

        @pl.when(block_id > 0)
        def _():
            for one in block_loads(jnp.maximum(block_id - 1, 0)):
                one.start()

        def one_part(part, _):
            rows = span(part, 128)

            @pl.when(part < 3)
            def _():
                grad_acc[rows, :] += dot_tn(
                    d_qkv[block_id, :, span(jnp.minimum(part, 2), 128)], rows_buf[slot]
                )

            @pl.when(part > 0)
            def _():
                grad_acc[rows, :] += dot_tn(
                    d_qkvst[block_id, :, span(lax.rem(part, 3), 128)], low_buf[slot]
                )

            return 0

        lax.fori_loop(0, 4, one_part, 0)
        kept_here = lax.rem(block_id, 2) == half
        mine_slot, core_slot = place_in(block_id, place), place_in(block_id, core)

        def one_chunk(chunk, _):
            rows = span(chunk, 128)
            value = to_low(dot_nt(d_qkv[block_id, rows, :], w_qkv[...]))

            @pl.when(kept_here)
            def _():
                partial[mine_slot, chunk] = value

            @pl.when(jnp.logical_not(kept_here))
            def _():
                leave[core_slot, rows, :] = value

            return 0

        lax.fori_loop(0, 4, one_chunk, 0)

        @pl.when(jnp.logical_not(kept_here))
        def _():
            leaving(core_slot).start()

    def back_parts(parts, total, grad, values):
        weights = [jnp.exp(part - total) for part in parts]
        d_weights = [dot_nt(grad, value) for value in values]
        inner = jnp.sum(weights[0] * d_weights[0], axis=-1, keepdims=True)
        for one, other in zip(weights[1:], d_weights[1:]):
            inner = inner + jnp.sum(one * other, axis=-1, keepdims=True)
        d_scores = [to_low(one * (other - inner)) for one, other in zip(weights, d_weights)]
        return [to_low(one) for one in weights], d_scores

    def token_back(block_id):
        prev_id = jnp.maximum(block_id - 1, 0)
        st_key[...] = jnp.zeros_like(st_key)
        st_value[...] = jnp.zeros_like(st_value)

        def one_chunk(chunk, _):
            rows = span(chunk, ROWS)
            query, parts = token_scores(scal, qkv, qkvst, bias, block_id, chunk)
            grad = d_o[block_id, rows, :]
            keys = (qkv[prev_id, :, 128:256], qkv[block_id, :, 128:256], qkvst[block_id, :, 128:256])
            values = (
                qkv[prev_id, :, 256:384], qkv[block_id, :, 256:384], qkvst[block_id, :, 256:384]
            )
            weights, d_scores = back_parts(parts, lse_tok[block_id, rows, :], grad, values)
            d_query = dot_nn(d_scores[0], keys[0])
            d_query = d_query + dot_nn(d_scores[1], keys[1]) + dot_nn(d_scores[2], keys[2])
            d_qkv[block_id, rows, 0:128] = to_low(d_query * SCALE)
            key_acc[prev_id] += dot_tn(d_scores[0], query) * SCALE
            value_acc[prev_id] += dot_tn(weights[0], grad)
            key_acc[block_id] += dot_tn(d_scores[1], query) * SCALE
            value_acc[block_id] += dot_tn(weights[1], grad)
            st_key[...] += dot_tn(d_scores[2], query) * SCALE
            st_value[...] += dot_tn(weights[2], grad)
            dz_sum[rows, 0:BLOCK] += d_scores[0].astype(jnp.float32)
            dz_sum[rows, BLOCK : 2 * BLOCK] += d_scores[1].astype(jnp.float32)
            return 0

        lax.fori_loop(0, CHUNKS, one_chunk, 0)

    token_back(3)
    pl.semaphore_wait(barrier, LINE + 1)
    aside(beside, place // 2).start()
    loads[2].wait()
    loads[0].wait()
    fetched(w_sout, local_sem.at[1])
    fetched(w_back, local_sem.at[2])

    def mixed_copy(block_id, slot, sender, other, seq_to, rank_to):
        return pltpu.make_async_remote_copy(
            src_ref=dos_rows.at[block_id, :, span(other, 128)],
            dst_ref=dos_got.at[block_id, span(sender, 64), :],
            send_sem=send_sem.at[0, block_id, slot],
            recv_sem=recv_sem.at[0, block_id, sender],
            device_id={"seq": seq_to, "tensor": rank_to},
            device_id_type=MESH_ID,
        )

    def grads_copy(block_id, slot, sender, other, seq_to, rank_to):
        return pltpu.make_async_remote_copy(
            src_ref=d_qkvst.at[block_id, span(other, 64), :],
            dst_ref=d_got.at[block_id, sender],
            send_sem=send_sem.at[1, block_id, slot],
            recv_sem=recv_sem.at[1, block_id, sender],
            device_id={"seq": seq_to, "tensor": rank_to},
            device_id_type=MESH_ID,
        )

    def one_block(turn, _):
        block_id = 3 - turn
        grad_out = grad_in[...] + cots[block_id].astype(jnp.float32)
        sums[0:1, :] += jnp.sum(
            grad_out * (states[block_id] - states[block_id + 1]), axis=0, keepdims=True
        ) * gate
        change = to_low((1.0 - gate) * grad_out)
        du_rows[block_id] = change
        dos_rows[block_id] = to_low(dot_nt(change, w_sout[...].reshape(D, D)))
        for slot, (other, seq_to, rank_to) in enumerate(peers):
            mixed_copy(block_id, slot, head, other, seq_to, rank_to).start()
        dos_got[block_id, span(head, 64), :] = dos_rows[block_id, :, span(head, 128)]
        for slot, (other, seq_to, rank_to) in enumerate(peers):
            mixed_copy(block_id, slot, other, other, seq_to, rank_to).wait_recv()

        def one_chunk(chunk, _):
            rows = span(chunk, ROWS)
            query, parts = state_scores(scal, qkv, qkvst, block_id, chunk)
            grad = dos_got[block_id, rows, :]
            keys = (qkv[block_id, :, 128:256], qkvst[block_id, :, 128:256])
            values = (qkv[block_id, :, 256:384], qkvst[block_id, :, 256:384])
            weights, d_scores = back_parts(parts, lse_st[block_id, rows, :], grad, values)
            d_query = dot_nn(d_scores[0], keys[0]) + dot_nn(d_scores[1], keys[1])
            d_qkvst[block_id, rows, 0:128] = to_low(d_query * SCALE)
            key_acc[block_id] += dot_tn(d_scores[0], query) * SCALE
            value_acc[block_id] += dot_tn(weights[0], grad)
            st_key[...] += dot_tn(d_scores[1], query) * SCALE
            st_value[...] += dot_tn(weights[1], grad)
            return 0

        lax.fori_loop(0, CHUNKS, one_chunk, 0)
        d_qkvst[block_id, :, 128:256] = to_low(st_key[...])
        d_qkvst[block_id, :, 256:384] = to_low(st_value[...])
        for slot, (other, seq_to, rank_to) in enumerate(peers):
            grads_copy(block_id, slot, head, other, seq_to, rank_to).start()
        d_got[block_id, head] = d_qkvst[block_id, span(head, 64), :]

        for step in range(4):

            @pl.when(turn == step)
            def _():
                next(plane_steps, None)

        @pl.when(turn == 3)
        def _():
            bucket_sums()

        @pl.when(turn < 3)
        def _():
            token_back(block_id - 1)

        d_qkv[block_id, :, 128:256] = to_low(key_acc[block_id])
        d_qkv[block_id, :, 256:384] = to_low(value_acc[block_id])
        block_products(block_id)

        @pl.when(turn == 2)
        def _():
            add_came(place_in(2 + half, place))

        for slot, (other, seq_to, rank_to) in enumerate(peers):
            grads_copy(block_id, slot, other, other, seq_to, rank_to).wait_recv()
        d_low = dot_nn(d_got[block_id, 0], w_back[0, 0].reshape(384, D))
        for other in range(1, LINE):
            d_low = d_low + dot_nn(
                d_got[block_id, other], w_back[other // 2, other % 2].reshape(384, D)
            )
        centered, scale = norm_parts(states[block_id])
        normed = centered * scale
        sums[1:2, :] += jnp.sum(d_low * normed, axis=0, keepdims=True)
        lifted = d_low * gain
        grad_in[...] = gate * grad_out + scale * (
            lifted
            - jnp.mean(lifted, axis=-1, keepdims=True)
            - normed * jnp.mean(lifted * normed, axis=-1, keepdims=True)
        )
        return 0

    lax.fori_loop(0, 4, one_block, 0)
    d_start[...] = grad_in[...]

    def drain(block_id, _):
        for slot, (other, seq_to, rank_to) in enumerate(peers):
            mixed_copy(block_id, slot, head, other, seq_to, rank_to).wait_send()
            grads_copy(block_id, slot, head, other, seq_to, rank_to).wait_send()
        return 0

    lax.fori_loop(0, 4, drain, 0)
    pair_grads[...] = to_low(grad_acc[...])
    for _ in plane_steps:
        pass
    add_came(place_in(half, place))
    for slot in range(2):
        leaving(slot).wait_send()
    for which in range(2):
        rows = pl.ds(128 * which, 128)
        tokens_out[which] = to_low(hidden[which] + total[rows, :])
    out_part[...] = to_low(total[256:384, :])
    loads[1].wait()
    aside(beside, place // 2).wait_send()
    aside(place, 1 - place // 2).wait_recv()


def backward_chain(
    scal, qkv, d_o, lse_tok, qkvst, lse_st, state_rows, begin, cots, back, kept, vecs, bias,
    extra, hidden, rows_all, state_low, w_qkv,
):
    low, wide = jnp.bfloat16, jnp.float32
    shapes = (
        ((4, 64, D), low),
        ((64, D), wide),
        ((8, D), wide),
        ((2, 128, D), wide),
        ((2, 128, D), low),
        ((128, D), low),
        ((2, 4, 128, D), low),
        ((512, D), low),
    )
    return pl.pallas_call(
        backward_kernel,
        out_shape=[jax.ShapeDtypeStruct(*one) for one in shapes],
        in_specs=vmem_specs(6)
        + any_specs(1)
        + vmem_specs(2)
        + any_specs(2)
        + vmem_specs(2)
        + any_specs(1)
        + vmem_specs(1)
        + any_specs(2)
        + vmem_specs(1),
        out_specs=vmem_specs(3) + any_specs(1) + vmem_specs(4),
        scratch_shapes=[
            pltpu.VMEM((BLOCK, 2 * BLOCK), wide),
            pltpu.VMEM((8, WIDE), wide),
            pltpu.VMEM((4, BLOCK, 384), low),
            pltpu.VMEM((4, STATES, 384), low),
            pltpu.VMEM((2, BLOCK, D), low),
            pltpu.VMEM((2, STATES, D), low),
            pltpu.VMEM((2, BLOCK, D), low),
            pltpu.VMEM((2, BLOCK, D), low),
            pltpu.VMEM((512, D), wide),
            pltpu.VMEM((4, BLOCK, 128), wide),
            pltpu.VMEM((4, BLOCK, 128), wide),
            pltpu.VMEM((STATES, 128), wide),
            pltpu.VMEM((STATES, 128), wide),
            pltpu.VMEM((4, 64, D), low),
            pltpu.VMEM((4, STATES, 128), low),
            pltpu.VMEM((4, LINE, 64, 384), low),
            pltpu.VMEM((64, D), wide),
            pltpu.VMEM((5, 64, D), wide),
            pltpu.VMEM((4, 2, 3, 4, 32, D), low),
            pltpu.VMEM((4, 8, 32, D), low),
            pltpu.VMEM((8, 384, D), low),
            pltpu.VMEM((4, 384, D), low),
            pltpu.VMEM((4, 192, D), low),
            pltpu.VMEM((2, 192, D), low),
            pltpu.VMEM((384, D), wide),
            pltpu.SemaphoreType.DMA((2, 4, LINE - 1)),
            pltpu.SemaphoreType.DMA((2, 4, LINE)),
            pltpu.SemaphoreType.DMA((5,)),
            pltpu.SemaphoreType.DMA((2,)),
            pltpu.SemaphoreType.DMA((10,)),
            pltpu.SemaphoreType.DMA((10,)),
            pltpu.SemaphoreType.DMA((2, 2)),
            pltpu.SemaphoreType.DMA((2,)),
            pltpu.SemaphoreType.DMA((2,)),
        ],
        compiler_params=pltpu.CompilerParams(
            collective_id=2, has_side_effects=True, vmem_limit_bytes=VMEM_LIMIT
        ),
        cost_estimate=pl.CostEstimate(flops=40000000000, bytes_accessed=40000000, transcendentals=0),
        name="backward_chain",
    )(
        scal, qkv, d_o, lse_tok, qkvst, lse_st, state_rows, begin, cots, back, kept, vecs, bias,
        extra, hidden, rows_all, state_low, w_qkv,
    )


def plane_place():
    place, half, rank = line_place()
    side = lax.axis_index("dp")
    return side, place, half, rank


def plane_index(side, place):
    return 4 * side + place


def row_halves(buf, rows):
    size = rows // 2
    return lambda owner, part: buf.at[owner, pl.ds(part * size, size), :]


def plane_gather(view, send_sem, recv_sem):
    side, place, half, rank = plane_place()
    across, beside = 1 - side, lax.rem(place + 2, 4)
    core = place + 1 - 2 * half
    me = plane_index(side, place)
    at_x, at_y = plane_index(across, place), plane_index(side, beside)
    at_d = plane_index(across, beside)
    to_x, to_y, to_c = {"dp": across}, {"seq": beside}, {"seq": core}

    def piece(owner, part, slot, target):
        one = view(owner, part)
        return pltpu.make_async_remote_copy(
            src_ref=one,
            dst_ref=one,
            send_sem=send_sem.at[slot],
            recv_sem=recv_sem.at[owner, part],
            device_id=target,
            device_id_type=MESH_ID,
        )

    own = [
        piece(me, 0, 0, to_x), piece(me, 1, 1, to_y), piece(me, 1, 2, to_x), piece(me, 0, 3, to_y),
        piece(me, 0, 4, to_c), piece(me, 1, 5, to_c),
    ]
    on_x0, on_y1 = piece(at_x, 0, 6, to_y), piece(at_y, 1, 7, to_x)
    came = [
        (piece(owner, part, 0, to_c), piece(owner, part, slot, to_c))
        for owner, part, slot in (
            (at_x, 0, 8), (at_y, 1, 9), (at_x, 1, 10), (at_y, 0, 11), (at_d, 0, 12), (at_d, 1, 13)
        )
    ]
    core_came = [
        piece(owner, part, 0, to_c)
        for owner in (
            plane_index(side, core),
            plane_index(across, core),
            plane_index(side, lax.rem(core + 2, 4)),
            plane_index(across, lax.rem(core + 2, 4)),
        )
        for part in (0, 1)
    ]
    yield
    for one in own:
        one.start()
    yield
    came[0][0].wait_recv()
    on_x0.start()
    came[1][0].wait_recv()
    on_y1.start()
    came[0][1].start()
    came[1][1].start()
    yield
    for index in (2, 3):
        came[index][0].wait_recv()
        came[index][1].start()
    yield
    for index in (4, 5):
        came[index][0].wait_recv()
        came[index][1].start()
    yield
    for one in core_came:
        one.wait_recv()
    for one in own + [on_x0, on_y1] + [two for _, two in came]:
        one.wait_send()


def run_all(*steps):
    waiting = list(steps)
    while waiting:
        for one in list(waiting):
            try:
                next(one)
            except StopIteration:
                waiting.remove(one)


def plane_scatter(part, core_got, near_got, far_got, total, rows, send_sem, recv_sem):
    side, place, half, rank = plane_place()
    across, beside = 1 - side, lax.rem(place + 2, 4)
    core = place + 1 - 2 * half
    me = plane_index(side, place)
    at_x, at_y = plane_index(across, place), plane_index(side, beside)
    at_d = plane_index(across, beside)
    size = rows // 2
    halves = (pl.ds(0, size), pl.ds(size, size))

    def moved(source, target_ref, slot, target):
        return pltpu.make_async_remote_copy(
            src_ref=source,
            dst_ref=target_ref,
            send_sem=send_sem.at[slot],
            recv_sem=recv_sem.at[slot],
            device_id=target,
            device_id_type=MESH_ID,
        )

    order = (at_d, at_x, at_y, me)
    swapped = (
        plane_index(across, lax.rem(core + 2, 4)),
        plane_index(across, core),
        plane_index(side, lax.rem(core + 2, 4)),
        plane_index(side, core),
    )
    def add_into(owner, view, other):
        part[owner, view, :] = to_low(
            part[owner, view, :].astype(jnp.float32) + other.astype(jnp.float32)
        )

    near = [
        moved(part.at[at_d, halves[0], :], near_got.at[0], 4, {"dp": across}),
        moved(part.at[at_d, halves[1], :], near_got.at[1], 5, {"seq": beside}),
        moved(part.at[at_x, halves[0], :], near_got.at[2], 6, {"dp": across}),
        moved(part.at[at_y, halves[1], :], near_got.at[3], 7, {"seq": beside}),
    ]
    first = [
        moved(part.at[owner], core_got.at[slot], slot, {"seq": core})
        for slot, owner in enumerate(swapped)
    ]
    far = [
        moved(part.at[at_y, halves[0], :], far_got.at[0], 8, {"seq": beside}),
        moved(part.at[at_x, halves[1], :], far_got.at[1], 9, {"dp": across}),
    ]
    yield
    for one in first:
        one.start()
    for slot, owner in enumerate(order):
        first[slot].wait_recv()
        for view in halves:
            add_into(owner, view, core_got[slot, view, :])
        if slot == 0:
            near[0].start()
            near[1].start()
        if slot == 1:
            near[2].start()
        if slot == 2:
            near[3].start()
    yield
    near[0].wait_recv()
    add_into(at_y, halves[0], near_got[0])
    far[0].start()
    near[1].wait_recv()
    add_into(at_x, halves[1], near_got[1])
    far[1].start()
    yield
    near[2].wait_recv()
    add_into(me, halves[0], near_got[2])
    near[3].wait_recv()
    add_into(me, halves[1], near_got[3])
    yield
    for slot, view in enumerate(halves):
        far[slot].wait_recv()
        total[view, :] = part[me, view, :].astype(jnp.float32) + far_got[slot].astype(jnp.float32)
    for one in first + near + far:
        one.wait_send()


def group_peers():
    place, half, rank = line_place()
    here = 4 * place + rank
    peers = []
    for step in range(1, 16):
        other = lax.rem(here + step, 16)
        peers.append((other, other // 4, lax.rem(other, 4)))
    return here, peers


def greet(peers):
    side = lax.axis_index("dp")
    barrier = pltpu.get_barrier_semaphore()
    for _, seq_to, rank_to in peers:
        pl.semaphore_signal(
            barrier, inc=1, device_id={"seq": seq_to, "tensor": rank_to}, device_id_type=MESH_ID
        )
    pl.semaphore_signal(barrier, inc=1, device_id={"dp": 1 - side}, device_id_type=MESH_ID)
    pl.semaphore_wait(barrier, len(peers) + 1)


def middle_kernel(
    mixed, tokens, kept, spread, cot_hbm, vecs,
    hidden, d_hidden, d_line, sums, extra, ff_grads,
    mixed_rows, mid_all, gl_all, dpre_all, work, core_got, near_got, far_got, total, d_rows,
    d_low, w_out, up, down, cot_all,
    send_sem, recv_sem, ring_send, ring_recv, sum_send, sum_recv, back_send, back_recv, local_sem,
):
    low, wide = jnp.bfloat16, jnp.float32
    side, place, half, rank = plane_place()
    mine = place // 2
    head = 2 * rank + half
    across, beside = 1 - side, lax.rem(place + 2, 4)
    core = place + 1 - 2 * half
    core_beside = lax.rem(core + 2, 4)
    me = plane_index(side, place)
    at_x, at_y = plane_index(across, place), plane_index(side, beside)
    at_d = plane_index(across, beside)
    me_c, x_c = plane_index(side, core), plane_index(across, core)
    y_c, d_c = plane_index(side, core_beside), plane_index(across, core_beside)
    to_x, to_y, to_c = {"dp": across}, {"seq": beside}, {"seq": core}
    here, peers = group_peers()
    fetch_pieces(kept, 48, 32, w_out, local_sem.at[0])
    ff_own = up.shape[1]
    first = spread.shape[1] - 2 * ff_own
    loads = [
        pltpu.make_async_copy(spread.at[:, pl.ds(first, ff_own), :], up, local_sem.at[1]),
        pltpu.make_async_copy(spread.at[:, pl.ds(first + ff_own, ff_own), :], down, local_sem.at[2]),
        pltpu.make_async_copy(cot_hbm, cot_all, local_sem.at[3]),
    ]
    for one in loads:
        one.start()
    greet(peers)

    def rows_copy(slot, sender, seq_from, rank_from, seq_to, rank_to):
        return pltpu.make_async_remote_copy(
            src_ref=mixed.at[seq_to, span(rank_to, 128), :],
            dst_ref=mixed_rows.at[
                seq_from // 2, :, span(2 * rank_from + lax.rem(seq_from, 2), 128)
            ],
            send_sem=send_sem.at[slot],
            recv_sem=recv_sem.at[sender],
            device_id={"seq": seq_to, "tensor": rank_to},
            device_id_type=MESH_ID,
        )

    for slot, (_, seq_to, rank_to) in enumerate(peers):
        rows_copy(slot, here, place, rank, seq_to, rank_to).start()
    mixed_rows[mine, :, span(head, 128)] = mixed[place, span(rank, 128), :]
    fetched(w_out, local_sem.at[0])
    for slot, (other, seq_to, rank_to) in enumerate(peers):
        rows_copy(slot, other, seq_to, rank_to, seq_to, rank_to).wait_recv()
    gain = vecs[2:3, :]

    def project(which, _):
        added = dot_nn(mixed_rows[which], w_out[...].reshape(D, D)) + tokens[which].astype(wide)
        hidden[which] = added
        centered, scale = norm_parts(added)
        mid_all[me, span(which, 128), :] = to_low(centered * scale * gain)
        return 0

    lax.fori_loop(0, 2, project, 0)

    def piece(owner, part, slot, target):
        view = mid_all.at[owner, pl.ds(part * 128, 128), :]
        return pltpu.make_async_remote_copy(
            src_ref=view,
            dst_ref=view,
            send_sem=ring_send.at[slot],
            recv_sem=ring_recv.at[owner, part],
            device_id=target,
            device_id_type=MESH_ID,
        )

    own = [
        piece(me, 0, 0, to_x), piece(me, 1, 1, to_y), piece(me, 1, 2, to_x), piece(me, 0, 3, to_y),
        piece(me, 0, 4, to_c), piece(me, 1, 5, to_c),
    ]
    on_x0, on_y1 = piece(at_x, 0, 6, to_y), piece(at_y, 1, 7, to_x)
    to_core = [
        piece(at_x, 0, 8, to_c), piece(at_y, 1, 9, to_c), piece(at_x, 1, 10, to_c),
        piece(at_y, 0, 11, to_c), piece(at_d, 0, 12, to_c), piece(at_d, 1, 13, to_c),
    ]
    wait_of = {
        (name, part): piece(owner, part, 0, to_c)
        for name, owner in (
            ("x", at_x), ("y", at_y), ("d", at_d), ("mc", me_c), ("xc", x_c), ("yc", y_c), ("dc", d_c)
        )
        for part in (0, 1)
    }

    def moved(source, target_ref, slot, target):
        return pltpu.make_async_remote_copy(
            src_ref=source,
            dst_ref=target_ref,
            send_sem=sum_send.at[slot],
            recv_sem=sum_recv.at[slot],
            device_id=target,
            device_id_type=MESH_ID,
        )

    views = (pl.ds(0, 128), pl.ds(128, 128))
    swap = [
        moved(work.at[owner], core_got.at[slot], slot, to_c)
        for slot, owner in enumerate((d_c, x_c, y_c, me_c))
    ]
    near = [
        moved(work.at[at_d, views[0], :], near_got.at[0], 4, to_x),
        moved(work.at[at_d, views[1], :], near_got.at[1], 5, to_y),
        moved(work.at[at_x, views[0], :], near_got.at[2], 6, to_x),
        moved(work.at[at_y, views[1], :], near_got.at[3], 7, to_y),
    ]
    far = [
        moved(work.at[at_y, views[0], :], far_got.at[0], 8, to_y),
        moved(work.at[at_x, views[1], :], far_got.at[1], 9, to_x),
    ]

    def add_into(owner, view, other):
        work[owner, view, :] = to_low(work[owner, view, :].astype(wide) + other.astype(wide))

    def add_core(slot, owner):
        swap[slot].wait_recv()
        for view in views:
            add_into(owner, view, core_got[slot, view, :])

    for one in own:
        one.start()
    loads[0].wait()
    loads[1].wait()
    loads[2].wait()
    owners = (me, me_c, at_x, at_y, x_c, y_c, at_d, d_c)

    def one_chunk(turn, _):
        @pl.when(turn == 1)
        def _():
            wait_of["mc", 0].wait_recv()
            wait_of["mc", 1].wait_recv()

        @pl.when(turn == 2)
        def _():
            swap[3].start()
            wait_of["x", 0].wait_recv()
            on_x0.start()
            wait_of["y", 1].wait_recv()
            on_y1.start()
            to_core[0].start()
            to_core[1].start()
            wait_of["x", 1].wait_recv()
            to_core[2].start()
            wait_of["y", 0].wait_recv()
            to_core[3].start()

        @pl.when(turn == 4)
        def _():
            wait_of["xc", 0].wait_recv()
            wait_of["xc", 1].wait_recv()

        @pl.when(turn == 5)
        def _():
            swap[1].start()
            wait_of["yc", 0].wait_recv()
            wait_of["yc", 1].wait_recv()

        @pl.when(turn == 6)
        def _():
            swap[2].start()
            wait_of["d", 0].wait_recv()
            to_core[4].start()
            wait_of["d", 1].wait_recv()
            to_core[5].start()
            add_core(1, at_x)
            near[2].start()
            add_core(2, at_y)
            near[3].start()

        @pl.when(turn == 7)
        def _():
            wait_of["dc", 0].wait_recv()
            wait_of["dc", 1].wait_recv()

        owner = owners[7]
        for index in range(7):
            owner = jnp.where(turn == index, owners[index], owner)
        up_rows = up[...].reshape(4 * ff_own, D)
        down_rows = down[...].reshape(4 * ff_own, D)

        def part(which, _):
            rows = span(which, 128)
            pre = dot_nt(mid_all[owner, rows, :], up_rows)
            square = pre * pre
            bend = jnp.tanh(GELU_SCALE * (pre + 0.044715 * (pre * square)))
            gl_all[owner, rows, :] = to_low(0.5 * pre * (1.0 + bend))
            slope = 0.5 * (1.0 + bend) + 0.5 * pre * (1.0 - bend * bend) * (
                GELU_SCALE * (1.0 + 3.0 * 0.044715 * square)
            )
            grad = to_low(dot_nt(cot_all[owner, rows, :], down_rows) * slope)
            dpre_all[owner, rows, :] = grad
            work[owner, rows, :] = to_low(dot_nn(grad, up_rows))
            return 0

        lax.fori_loop(0, 2, part, 0)
        return 0

    lax.fori_loop(0, 8, one_chunk, 0)
    swap[0].start()
    add_core(0, at_d)
    near[0].start()
    near[1].start()
    add_core(3, me)

    def grads(index, _):
        quarter, kind = index // 2, lax.rem(index, 2)
        columns = span(quarter, 128)

        @pl.when(kind == 0)
        def _():
            def add(owner, acc):
                return acc + dot_tn(dpre_all[owner, :, columns], mid_all[owner])

            ff_grads[quarter, 0] = to_low(lax.fori_loop(0, 8, add, jnp.zeros((128, D), wide)))

        @pl.when(kind == 1)
        def _():
            def add(owner, acc):
                return acc + dot_tn(gl_all[owner, :, columns], cot_all[owner])

            ff_grads[quarter, 1] = to_low(lax.fori_loop(0, 8, add, jnp.zeros((128, D), wide)))

        return 0

    lax.fori_loop(0, 8, grads, 0)
    near[0].wait_recv()
    add_into(at_y, views[0], near_got[0])
    far[0].start()
    near[1].wait_recv()
    add_into(at_x, views[1], near_got[1])
    far[1].start()
    near[2].wait_recv()
    add_into(me, views[0], near_got[2])
    near[3].wait_recv()
    add_into(me, views[1], near_got[3])

    def outward(owner, _):
        down_rows = down[...].reshape(4 * ff_own, D)
        for which in range(2):
            rows = pl.ds(128 * which, 128)
            extra[owner, rows, :] = to_low(dot_nn(gl_all[owner, rows, :], down_rows))
        return 0

    lax.fori_loop(0, 8, outward, 0)
    for slot, view in enumerate(views):
        far[slot].wait_recv()
        total[view, :] = work[me, view, :].astype(wide) + far_got[slot].astype(wide)
    sums[...] = jnp.zeros_like(sums)

    def back(which, _):
        rows = span(which, 128)
        grad = total[rows, :]
        centered, scale = norm_parts(hidden[which])
        normed = centered * scale
        sums[0:1, :] += jnp.sum(grad * normed, axis=0, keepdims=True)
        lifted = grad * gain
        row_grad = cot_all[me, rows, :].astype(wide) + scale * (
            lifted
            - jnp.mean(lifted, axis=-1, keepdims=True)
            - normed * jnp.mean(lifted * normed, axis=-1, keepdims=True)
        )
        d_hidden[which] = row_grad
        d_low[which] = to_low(row_grad)
        d_rows[which] = to_low(dot_nt(to_low(row_grad), w_out[...].reshape(D, D)))
        return 0

    lax.fori_loop(0, 2, back, 0)

    def line_copy(slot, sender, seq_from, rank_from, seq_to, rank_to):
        return pltpu.make_async_remote_copy(
            src_ref=d_rows.at[seq_to // 2, :, span(2 * rank_to + lax.rem(seq_to, 2), 128)],
            dst_ref=d_line.at[seq_from, span(rank_from, 128), :],
            send_sem=back_send.at[slot],
            recv_sem=back_recv.at[sender],
            device_id={"seq": seq_to, "tensor": rank_to},
            device_id_type=MESH_ID,
        )

    for slot, (_, seq_to, rank_to) in enumerate(peers):
        line_copy(slot, here, place, rank, seq_to, rank_to).start()
    d_line[place, span(rank, 128), :] = d_rows[mine, :, span(head, 128)]
    for index in range(LINE):
        columns = pl.ds(128 * index, 128)
        part = dot_tn(mixed_rows[0, :, columns], d_low[0]) + dot_tn(
            mixed_rows[1, :, columns], d_low[1]
        )
        part = to_low(part)
        for block in range(4):
            extra[
                4 * (index % 2) + block, 256 + 32 * (index // 2) : 288 + 32 * (index // 2), :
            ] = part[32 * block : 32 * block + 32, :]
    for slot, (other, seq_to, rank_to) in enumerate(peers):
        line_copy(slot, other, seq_to, rank_to, seq_to, rank_to).wait_recv()
    for slot, (_, seq_to, rank_to) in enumerate(peers):
        rows_copy(slot, here, place, rank, seq_to, rank_to).wait_send()
        line_copy(slot, here, place, rank, seq_to, rank_to).wait_send()
    for one in own + [on_x0, on_y1] + to_core + swap + near + far:
        one.wait_send()


GELU_SCALE = 0.7978845608028654


def middle(mixed, tokens, kept, spread, cot_all, vecs):
    low, wide = jnp.bfloat16, jnp.float32
    ff_own = (spread.shape[1] - SPREAD_FIRST) // 2
    shapes = (
        ((2, 128, D), wide),
        ((2, 128, D), wide),
        ((4, BLOCK, 128), low),
        ((8, D), wide),
        ((8, 384, D), low),
        ((4, 2, ff_own, D), low),
    )
    dma = pltpu.SemaphoreType.DMA
    return pl.pallas_call(
        middle_kernel,
        out_shape=[jax.ShapeDtypeStruct(*one) for one in shapes],
        in_specs=vmem_specs(2) + any_specs(3) + vmem_specs(1),
        out_specs=vmem_specs(6),
        scratch_shapes=[
            pltpu.VMEM((2, 128, D), low),
            pltpu.VMEM((8, 256, D), low),
            pltpu.VMEM((8, 256, 4 * ff_own), low),
            pltpu.VMEM((8, 256, 4 * ff_own), low),
            pltpu.VMEM((8, 256, D), low),
            pltpu.VMEM((4, 256, D), low),
            pltpu.VMEM((4, 128, D), low),
            pltpu.VMEM((2, 128, D), low),
            pltpu.VMEM((256, D), wide),
            pltpu.VMEM((2, 128, D), low),
            pltpu.VMEM((2, 128, D), low),
            pltpu.VMEM((4, 8, 32, D), low),
            pltpu.VMEM((4, ff_own, D), low),
            pltpu.VMEM((4, ff_own, D), low),
            pltpu.VMEM((8, 256, D), low),
            dma((15,)), dma((16,)), dma((14,)), dma((8, 2)), dma((10,)), dma((10,)), dma((15,)),
            dma((16,)), dma((4,)),
        ],
        compiler_params=pltpu.CompilerParams(
            collective_id=3, has_side_effects=True, vmem_limit_bytes=VMEM_LIMIT
        ),
        cost_estimate=pl.CostEstimate(
            flops=60000000000, bytes_accessed=60000000, transcendentals=0
        ),
        name="middle",
    )(mixed, tokens, kept, spread, cot_all, vecs)


SPREAD_FIRST = 0


WIDE = 2048


def opening_kernel(
    tokens, w_query, w_key, w_value, w_sout, w_out, begin, vecs, rel_bias, marks_own,
    rows_all, qkv, kept, table, marks, w_qkv,
    begin_rows, bias_rows, stage, send_sem, core_sem, recv_sem, piece_send, piece_recv, ring_send, ring_recv,
    mark_send, mark_recv, local_sem,
):
    side, place, half, rank = plane_place()
    mine = place // 2
    core = place + 1 - 2 * half
    other = lax.rem(place + 2, 4)
    me = plane_index(side, place)
    extra = 80
    fetch_columns((w_query, w_key, w_value), w_qkv, local_sem.at[0])
    loads = [
        pltpu.make_async_copy(
            w_sout.at[span(me, 32), :], kept.at[me, pl.ds(80 * rank, 32), :], local_sem.at[1]
        ),
        pltpu.make_async_copy(
            w_out.at[span(me, 32), :], kept.at[me, pl.ds(80 * rank + 48, 32), :], local_sem.at[3]
        ),
        pltpu.make_async_copy(begin.at[span(me, 16), :], begin_rows, local_sem.at[2]),
    ]
    for one in loads:
        one.start()
    barrier = pltpu.get_barrier_semaphore()
    greeted = [{"tensor": lax.rem(rank + step, 4)} for step in (1, 2, 3)]
    seats = [lax.rem(place + step, 4) for step in (1, 2, 3)]
    greeted += [{"seq": one} for one in seats] + [{"dp": 1 - side}]
    for target in greeted:
        pl.semaphore_signal(barrier, inc=1, device_id=target, device_id_type=MESH_ID)
    gain = vecs[3:4, :]

    def normed(which):
        centered, scale = norm_parts(tokens[which].astype(jnp.float32))
        return to_low(centered * scale * gain)

    def moved(block_id, origin, sem, target):
        view = rows_all.at[block_id, span(origin, 128), :]
        return pltpu.make_async_remote_copy(
            src_ref=view,
            dst_ref=view,
            send_sem=sem,
            recv_sem=recv_sem.at[block_id, origin],
            device_id=target,
            device_id_type=MESH_ID,
        )

    stage[...] = normed(1 - mine)
    marks[place] = marks_own[...]
    pl.semaphore_wait(barrier, 7)
    aside = pltpu.make_async_remote_copy(
        src_ref=stage,
        dst_ref=rows_all.at[place, span(rank, 128), :],
        send_sem=send_sem.at[0, 0, 3],
        recv_sem=recv_sem.at[place, rank],
        device_id={"seq": other},
        device_id_type=MESH_ID,
    )
    aside.start()

    def mark_move(slot, origin, target):
        return pltpu.make_async_remote_copy(
            src_ref=marks.at[origin],
            dst_ref=marks.at[origin],
            send_sem=mark_send.at[slot],
            recv_sem=mark_recv.at[origin],
            device_id={"seq": target},
            device_id_type=MESH_ID,
        )

    def piece_move(slot, origin, target):
        view = kept.at[me, span(origin, extra), :]
        return pltpu.make_async_remote_copy(
            src_ref=view,
            dst_ref=view,
            send_sem=piece_send.at[slot],
            recv_sem=piece_recv.at[origin],
            device_id=target,
            device_id_type=MESH_ID,
        )

    for one in loads:
        one.wait()
    kept[me, pl.ds(pl.multiple_of(80 * rank + 32, 16), 16), :] = to_low(begin_rows[...])
    for slot in range(3):
        piece_move(slot, rank, greeted[slot]).start()
    for slot, target in enumerate(seats):
        mark_move(slot, place, target).start()
    rows_all[place, span(rank, 128), :] = normed(mine)
    right, left = {"tensor": lax.rem(rank + 1, 4)}, {"tensor": lax.rem(rank + 3, 4)}
    blocks = (place, other)

    def pass_on(which, distance):
        block_id = blocks[which]

        @pl.when((rank < 3) & (rank >= distance))
        def _():
            moved(block_id, jnp.maximum(rank - distance, 0), send_sem.at[which, distance, 0], right).start()

        @pl.when((rank > 0) & (rank + distance <= 3))
        def _():
            moved(block_id, jnp.minimum(rank + distance, 3), send_sem.at[which, distance, 1], left).start()

    def pass_done(which, distance):
        block_id = blocks[which]

        @pl.when((rank < 3) & (rank >= distance))
        def _():
            moved(block_id, jnp.maximum(rank - distance, 0), send_sem.at[which, distance, 0], right).wait_send()

        @pl.when((rank > 0) & (rank + distance <= 3))
        def _():
            moved(block_id, jnp.minimum(rank + distance, 3), send_sem.at[which, distance, 1], left).wait_send()

    def project(block_id, origin):
        view = span(origin, 128)
        qkv[block_id, view, :] = to_low(dot_nn(rows_all[block_id, view, :], w_qkv[...]))

    def rows_steps():
        pass_on(0, 0)
        fetched(w_qkv, local_sem.at[0])
        moved(place, rank, core_sem.at[0, rank], {"seq": core}).start()
        project(place, rank)
        moved(other, rank, send_sem.at[0, 0, 3], {"seq": other}).wait_recv()
        pass_on(1, 0)
        moved(other, rank, core_sem.at[1, rank], {"seq": core}).start()
        project(other, rank)
        yield
        for distance in (1, 2, 3):
            for which in (0, 1):
                block_id = blocks[which]
                for way, ok, origin in (
                    (0, rank >= distance, jnp.maximum(rank - distance, 0)),
                    (1, rank + distance <= 3, jnp.minimum(rank + distance, 3)),
                ):

                    @pl.when(ok)
                    def _():
                        moved(block_id, origin, send_sem.at[which, distance, way], right).wait_recv()
                        if distance < 3:
                            if way == 0:

                                @pl.when(rank < 3)
                                def _():
                                    moved(
                                        block_id, origin, send_sem.at[which, distance, 0], right
                                    ).start()

                            else:

                                @pl.when(rank > 0)
                                def _():
                                    moved(
                                        block_id, origin, send_sem.at[which, distance, 1], left
                                    ).start()

                        moved(block_id, origin, core_sem.at[which, origin], {"seq": core}).start()
                        project(block_id, origin)

                yield
        for which, block_id in enumerate((core, lax.rem(core + 2, 4))):
            for origin in range(4):
                moved(block_id, origin, core_sem.at[which, origin], {"seq": core}).wait_recv()
                project(block_id, origin)
        for which in (0, 1):
            for distance in (0, 1, 2):
                pass_done(which, distance)
            for origin in range(4):
                moved(blocks[which], origin, core_sem.at[which, origin], {"seq": core}).wait_send()

    def piece_steps():
        for slot in range(3):
            piece_move(slot, lax.rem(rank + slot + 1, 4), greeted[slot]).wait_recv()
        for _ in plane_gather(row_halves(kept, 4 * extra), ring_send, ring_recv):
            yield
        for slot in range(3):
            piece_move(slot, rank, greeted[slot]).wait_send()

    def bias_steps():
        lane = lax.broadcasted_iota(jnp.int32, (8, WIDE), 1)
        bucket_ids = bucket_of(jnp.where(lane >= WIDE - BLOCK, lane - WIDE - BLOCK, lane - BLOCK))
        first = jnp.zeros((8, WIDE), jnp.float32)
        for bucket_id in range(BUCKETS):
            first = jnp.where(bucket_ids == bucket_id, rel_bias[bucket_id, half], first)
        row = lax.broadcasted_iota(jnp.int32, (8, WIDE), 0)
        for step in (1, 2, 4):
            first = jnp.where(row // step % 2 == 1, pltpu.roll(first, step, 1), first)
        bias_rows[...] = first
        yield

        def one(group, _):
            table[span(group, 8), :] = pltpu.roll(bias_rows[...], 8 * group, 1)[:, 0 : 2 * BLOCK]
            return 0

        for part in range(4):
            lax.fori_loop(16 * part, 16 * part + 16, one, 0)
            yield

    run_all(rows_steps(), piece_steps(), bias_steps())
    aside.wait_send()
    for slot, target in enumerate(seats):
        mark_move(slot, place, target).wait_send()
        mark_move(slot, target, target).wait_recv()


def opening(tokens, w_query, w_key, w_value, w_sout, w_out, begin, vecs, rel_bias, marks):
    low, wide = jnp.bfloat16, jnp.float32
    shapes = (
        ((4, BLOCK, D), low),
        ((4, BLOCK, 384), low),
        ((8, 4 * 80, D), low),
        ((BLOCK, 2 * BLOCK), wide),
        ((4, 8, 128), jnp.int32),
        ((D, 384), low),
    )
    dma = pltpu.SemaphoreType.DMA
    outs = pl.pallas_call(
        opening_kernel,
        out_shape=[jax.ShapeDtypeStruct(*one) for one in shapes],
        in_specs=vmem_specs(1)
        + any_specs(6)
        + vmem_specs(1)
        + [pl.BlockSpec(memory_space=pltpu.SMEM)]
        + vmem_specs(1),
        out_specs=vmem_specs(6),
        scratch_shapes=[
            pltpu.VMEM((16, D), wide),
            pltpu.VMEM((8, WIDE), wide),
            pltpu.VMEM((128, D), low),
            dma((2, 4, 4)),
            dma((2, 4)),
            dma((4, 4)),
            dma((3,)),
            dma((4,)),
            dma((14,)),
            dma((8, 2)),
            dma((3,)),
            dma((4,)),
            dma((4,)),
        ],
        compiler_params=pltpu.CompilerParams(
            collective_id=5, has_side_effects=True, vmem_limit_bytes=VMEM_LIMIT
        ),
        cost_estimate=pl.CostEstimate(
            flops=30000000000, bytes_accessed=30000000, transcendentals=0
        ),
        name="opening",
    )(tokens, w_query, w_key, w_value, w_sout, w_out, begin, vecs, rel_bias, marks)
    rows_all, qkv, kept, table, marks, w_qkv = outs
    return rows_all, qkv, kept.reshape(8, 4, 80, D), table, marks, w_qkv


def pair_sum(part, near_got, far_got, result, rows, send_sem, recv_sem):
    side, place, half, rank = plane_place()
    mine = place // 2
    across, beside = 1 - side, 1 - mine
    me = 2 * side + mine
    at_x, at_y, at_d = 2 * across + mine, 2 * side + beside, 2 * across + beside
    to_x, to_y = {"dp": across}, {"seq": lax.rem(place + 2, 4)}
    size = rows // 2
    views = (pl.ds(0, size), pl.ds(size, size))

    def moved(source, target_ref, slot, target):
        return pltpu.make_async_remote_copy(
            src_ref=source,
            dst_ref=target_ref,
            send_sem=send_sem.at[slot],
            recv_sem=recv_sem.at[slot],
            device_id=target,
            device_id_type=MESH_ID,
        )

    def add_into(owner, view, other):
        part[owner, view, :] = to_low(
            part[owner, view, :].astype(jnp.float32) + other.astype(jnp.float32)
        )

    near = [
        moved(part.at[at_d, views[0], :], near_got.at[0], 0, to_x),
        moved(part.at[at_d, views[1], :], near_got.at[1], 1, to_y),
        moved(part.at[at_x, views[0], :], near_got.at[2], 2, to_x),
        moved(part.at[at_y, views[1], :], near_got.at[3], 3, to_y),
    ]
    for one in near:
        one.start()
    yield
    near[0].wait_recv()
    add_into(at_y, views[0], near_got[0])
    far = [
        moved(part.at[at_y, views[0], :], far_got.at[0], 4, to_y),
        moved(part.at[at_x, views[1], :], far_got.at[1], 5, to_x),
    ]
    far[0].start()
    near[1].wait_recv()
    add_into(at_x, views[1], near_got[1])
    far[1].start()
    yield
    near[2].wait_recv()
    add_into(me, views[0], near_got[2])
    near[3].wait_recv()
    add_into(me, views[1], near_got[3])
    for slot, view in enumerate(views):
        far[slot].wait_recv()
        result[me, view, :] = to_low(
            part[me, view, :].astype(jnp.float32) + far_got[slot].astype(jnp.float32)
        )

    def given(owner, which, slot, target):
        view = result.at[owner, views[which], :]
        return moved(view, view, slot, target)

    own = [
        given(me, 0, 6, to_x),
        given(me, 1, 7, to_y),
        given(me, 1, 8, to_x),
        given(me, 0, 9, to_y),
    ]
    for one in own:
        one.start()
    yield
    given(at_x, 0, 6, to_x).wait_recv()
    last = [given(at_x, 0, 10, to_y), given(at_y, 1, 11, to_x)]
    last[0].start()
    given(at_y, 1, 7, to_y).wait_recv()
    last[1].start()
    yield
    given(at_x, 1, 8, to_x).wait_recv()
    given(at_y, 0, 9, to_y).wait_recv()
    given(at_d, 0, 10, to_y).wait_recv()
    given(at_d, 1, 11, to_x).wait_recv()
    for one in near + far + own + last:
        one.wait_send()


PAIR_ROWS = 640


def closing_kernel(
    partial, pair_grads, tokens, d_hidden, vecs, os_hbm, du_hbm, d_start, mlp_sums, state_sums,
    out_part,
    inputs_grad, pair_out, sout_out, small_out,
    os_rows, du_rows, sums, got, final, cross, cross_got,
    pair_part, pair_near, pair_far,
    work, core_got, near_got, far_got, total, z_part, z_got,
    small_z, small_p,
    line_send, line_recv, way_send, way_recv, pair_send, pair_recv, core_sem,
    ring_send, ring_recv, zs_send, zs_recv, gather_send, gather_recv, small_send, small_recv, local_sem,
):
    loads = [
        pltpu.make_async_copy(source, target, local_sem.at[slot])
        for slot, (source, target) in enumerate(
            (
                (partial, sums),
                (os_hbm, os_rows),
                (du_hbm, du_rows),
            )
        )
    ]
    for one in loads:
        one.start()
    side, place, half, rank = plane_place()
    mine = place // 2
    core = place + 1 - 2 * half
    other = lax.rem(place + 2, 4)
    me = plane_index(side, place)
    ranks = [lax.rem(rank + step, 4) for step in (1, 2, 3)]
    spots_of = [lax.rem(me + step, 8) for step in range(1, 8)]
    barrier = pltpu.get_barrier_semaphore()
    for target in ranks:
        pl.semaphore_signal(barrier, inc=1, device_id={"tensor": target}, device_id_type=MESH_ID)
    for target in spots_of:
        pl.semaphore_signal(
            barrier,
            inc=1,
            device_id={"dp": target // 4, "seq": lax.rem(target, 4)},
            device_id_type=MESH_ID,
        )
    gain = vecs[3:4, :]
    right, left = {"tensor": lax.rem(rank + 1, 4)}, {"tensor": lax.rem(rank + 3, 4)}

    def moved(source, target_ref, send, recv, target):
        return pltpu.make_async_remote_copy(
            src_ref=source,
            dst_ref=target_ref,
            send_sem=send,
            recv_sem=recv,
            device_id=target,
            device_id_type=MESH_ID,
        )

    def crossing():
        return moved(cross, cross_got, line_send.at[0], line_recv.at[0], {"seq": other})

    near = rank // 2
    at_end = (rank == 0) | (rank == 3)

    def hop(way, which, target):
        return moved(
            sums.at[which, target],
            got.at[way, which, target],
            way_send.at[which, target],
            way_recv.at[way, which, target],
            {"tensor": lax.rem(rank + 5 - 2 * way, 4)},
        )

    def target_of(way, distance):
        return (1 - way) * (3 - distance) + way * distance

    def pass_first(which):
        @pl.when(at_end)
        def _():
            for distance in range(3):
                hop(near, which, target_of(near, distance)).start()

    def pass_on(way, which, distance):
        @pl.when(jnp.logical_not(at_end))
        def _():
            target = target_of(way, distance)
            hop(way, which, target).wait_recv()
            sums[which, target] = to_low(
                sums[which, target].astype(jnp.float32)
                + got[way, which, target].astype(jnp.float32)
            )
            hop(way, which, target).start()

    def finish(which):
        final[which] = sums[which, rank].astype(jnp.float32)

        @pl.when(rank > 0)
        def _():
            hop(0, which, rank).wait_recv()
            final[which] += got[0, which, rank].astype(jnp.float32)

        @pl.when(rank < 3)
        def _():
            hop(1, which, rank).wait_recv()
            final[which] += got[1, which, rank].astype(jnp.float32)

    def small_over_z(slot, sender, target):
        return moved(
            small_z.at[sender], small_z.at[sender], small_send.at[slot], small_recv.at[sender],
            {"tensor": target},
        )

    def small_over_plane(slot, sender, target):
        return moved(
            small_p.at[sender], small_p.at[sender], small_send.at[3 + slot],
            small_recv.at[4 + sender],
            {"dp": target // 4, "seq": lax.rem(target, 4)},
        )

    def line_steps():
        loads[0].wait()
        pl.semaphore_wait(barrier, 10)
        for which in (0, 1):
            pass_first(which)
        yield
        for which in (0, 1):
            pass_on(near, which, 0)
            yield
            pass_on(near, which, 1)
            pass_on(1 - near, which, 0)
            yield
            finish(which)
            if which == 0:
                cross[...] = to_low(final[0])
                crossing().start()
            yield
        crossing().wait_recv()
        final[0] = cross_got[...].astype(jnp.float32)
        small_z[rank] = jnp.zeros((8, D), jnp.float32)
        for row, source in enumerate(
            (state_sums[1:2, :], mlp_sums[0:1, :], state_sums[0:1, :], state_sums[2:3, :])
        ):
            small_z[rank, row + 1 : row + 2, :] = source
        for which, row_set in ((1, mine), (0, 1 - mine)):
            grad = final[which]
            centered, scale = norm_parts(tokens[row_set].astype(jnp.float32))
            normed = centered * scale
            small_z[rank, 0:1, :] += jnp.sum(grad * normed, axis=0, keepdims=True)
            lifted = grad * gain
            inputs_grad[row_set] = d_hidden[row_set] + scale * (
                lifted
                - jnp.mean(lifted, axis=-1, keepdims=True)
                - normed * jnp.mean(lifted * normed, axis=-1, keepdims=True)
            )
        for slot, target in enumerate(ranks):
            small_over_z(slot, rank, target).start()
        crossing().wait_send()
        yield
        for slot, target in enumerate(ranks):
            small_over_z(slot, target, target).wait_recv()
        small_p[me] = small_z[0] + small_z[1] + small_z[2] + small_z[3]
        for slot, target in enumerate(spots_of):
            small_over_plane(slot, me, target).start()
        yield
        for slot, target in enumerate(spots_of):
            small_over_plane(slot, target, target).wait_recv()
        acc = small_p[0]
        for target in range(1, 8):
            acc = acc + small_p[target]
        small_out[...] = acc
        for slot, target in enumerate(ranks):
            small_over_z(slot, rank, target).wait_send()
        for slot, target in enumerate(spots_of):
            small_over_plane(slot, me, target).wait_send()
        for which in (0, 1):
            for target in range(4):

                @pl.when(rank != target)
                def _():
                    hop(0, which, target).wait_send()

    def pair_steps():
        for owner in range(3):
            pair_part[owner] = pair_grads[160 * owner : 160 * owner + 160, :]
        pair_part[3, 0:32, :] = pair_grads[480:512, :]
        pair_part[3, 32:96, :] = to_low(d_start[...])
        pair_part[3, 96:160, :] = jnp.zeros((64, D), jnp.bfloat16)
        for _ in pair_sum(
            pair_part, pair_near, pair_far, pair_out.at[half], 160, pair_send, pair_recv
        ):
            yield
        full = moved(
            pair_out.at[half], pair_out.at[half], core_sem.at[0], core_sem.at[1], {"seq": core}
        )
        full.start()
        yield
        moved(
            pair_out.at[1 - half], pair_out.at[1 - half], core_sem.at[0], core_sem.at[1],
            {"seq": core},
        ).wait_recv()
        full.wait_send()

    def sout_steps():
        loads[1].wait()
        loads[2].wait()
        for head in range(LINE):
            low = to_low(dot_tn(os_rows[:, 128 * head : 128 * head + 128], du_rows[...]))
            for piece in range(4):
                work[
                    4 * (head % 2) + piece, 32 * (head // 2) : 32 * (head // 2) + 32, :
                ] = low[32 * piece : 32 * piece + 32, :]
        for _ in plane_scatter(
            work, core_got, near_got, far_got, total, 128, ring_send, ring_recv
        ):
            yield
        z_part[:, 0:32, :] = to_low(total[...]).reshape(4, 32, D)
        z_part[:, 32:64, :] = out_part[...].reshape(4, 32, D)
        out = [
            moved(
                z_part.at[target], z_got.at[rank], zs_send.at[slot], zs_recv.at[rank],
                {"tensor": target},
            )
            for slot, target in enumerate(ranks)
        ]
        for one in out:
            one.start()
        z_got[rank] = z_part[rank]
        yield
        for slot, target in enumerate(ranks):
            moved(
                z_part.at[target], z_got.at[target], zs_send.at[slot], zs_recv.at[target],
                {"tensor": target},
            ).wait_recv()
        acc = z_got[0].astype(jnp.float32)
        for target in range(1, 4):
            acc = acc + z_got[target].astype(jnp.float32)
        sout_out[me] = to_low(acc)
        for _ in plane_gather(row_halves(sout_out, 64), gather_send, gather_recv):
            yield
        for one in out:
            one.wait_send()

    run_all(sout_steps(), line_steps(), pair_steps())


def closing(
    partial, pair_grads, tokens, d_hidden, vecs, os_rows, du_rows, d_start, mlp_sums, state_sums,
    out_part,
):
    low, wide = jnp.bfloat16, jnp.float32
    shapes = (
        ((2, 128, D), wide),
        ((2, 4, PAIR_ROWS // 4, D), low),
        ((8, 64, D), low),
        ((8, D), wide),
    )
    dma = pltpu.SemaphoreType.DMA
    return pl.pallas_call(
        closing_kernel,
        out_shape=[jax.ShapeDtypeStruct(*one) for one in shapes],
        in_specs=any_specs(1)
        + vmem_specs(4)
        + any_specs(2)
        + vmem_specs(4),
        out_specs=vmem_specs(4),
        scratch_shapes=[
            pltpu.VMEM((256, D), low),
            pltpu.VMEM((256, D), low),
            pltpu.VMEM((2, 4, 128, D), low),
            pltpu.VMEM((2, 2, 4, 128, D), low),
            pltpu.VMEM((2, 128, D), wide),
            pltpu.VMEM((128, D), low),
            pltpu.VMEM((128, D), low),
            pltpu.VMEM((4, PAIR_ROWS // 4, D), low),
            pltpu.VMEM((4, PAIR_ROWS // 8, D), low),
            pltpu.VMEM((2, PAIR_ROWS // 8, D), low),
            pltpu.VMEM((8, 128, D), low),
            pltpu.VMEM((4, 128, D), low),
            pltpu.VMEM((4, 64, D), low),
            pltpu.VMEM((2, 64, D), low),
            pltpu.VMEM((128, D), wide),
            pltpu.VMEM((4, 64, D), low),
            pltpu.VMEM((4, 64, D), low),
            pltpu.VMEM((4, 8, D), wide),
            pltpu.VMEM((8, 8, D), wide),
            dma((1,)), dma((1,)), dma((2, 4)), dma((2, 2, 4)), dma((12,)), dma((12,)), dma((2,)),
            dma((10,)), dma((10,)), dma((3,)), dma((4,)), dma((16,)), dma((8, 2)), dma((10,)),
            dma((12,)), dma((3,)),
        ],
        compiler_params=pltpu.CompilerParams(
            collective_id=6, has_side_effects=True, vmem_limit_bytes=VMEM_LIMIT
        ),
        cost_estimate=pl.CostEstimate(
            flops=30000000000, bytes_accessed=30000000, transcendentals=0
        ),
        name="closing",
    )(
        partial, pair_grads, tokens, d_hidden, vecs, os_rows, du_rows, d_start, mlp_sums,
        state_sums, out_part,
    )


def finish_kernel(
    pair, pair_tail, two, ff,
    query, key, value, squery, out, sout, up, down, state,
):
    step = pl.program_id(0)
    wide = jnp.float32
    up[...] = ff[0, 0].astype(wide).T
    down[...] = ff[0, 1].astype(wide)
    sout[...] = two[0, 0:32].astype(wide)
    out[...] = two[0, 32:64].astype(wide)
    for which, target in enumerate((query, key, value, squery)):

        @pl.when(step // 2 == which)
        def _():
            target[...] = pair[0].astype(wide).T

    @pl.when(step == 0)
    def _():
        state[...] = pair_tail[...].reshape(128, D).astype(wide)


def finish_grads(pair, two, ff):
    wide = jnp.float32
    turned = [
        pl.BlockSpec((D, 128), lambda i, w=which: (0, jnp.clip(i - 2 * w, 0, 1)))
        for which in range(4)
    ]
    square = jax.ShapeDtypeStruct((D, 256), wide)
    rows = jax.ShapeDtypeStruct((256, D), wide)
    whole = jax.ShapeDtypeStruct((D, D), wide)
    return pl.pallas_call(
        finish_kernel,
        grid=(8,),
        out_shape=[square] * 4 + [rows] * 2 + [whole] * 2 + [jax.ShapeDtypeStruct((128, D), wide)],
        in_specs=[
            pl.BlockSpec((1, 128, D), lambda i: (i % 2, i // 2, 0)),
            pl.BlockSpec((2, 64, D), lambda i: (0, 8, 0)),
            pl.BlockSpec((1, 64, D), lambda i: (i, 0, 0)),
            pl.BlockSpec((1, 2, 128, D), lambda i: (i, 0, 0, 0)),
        ],
        out_specs=turned
        + [pl.BlockSpec((32, D), lambda i: (i, 0))] * 2
        + [pl.BlockSpec((D, 128), lambda i: (0, i)), pl.BlockSpec((128, D), lambda i: (i, 0))]
        + [pl.BlockSpec((128, D), lambda i: (0, 0))],
        compiler_params=pltpu.CompilerParams(vmem_limit_bytes=VMEM_LIMIT),
        name="finish_grads",
    )(pair, pair, two, ff)


def swap_seq(value):
    return lax.all_to_all(value, "seq", 0, 0, tiled=False)


def line_body(
    inputs,
    seg_starts,
    lengths,
    init_state,
    attn_gain,
    state_gain,
    mlp_gain,
    w_query,
    w_key,
    w_value,
    w_out,
    w_squery,
    w_sout,
    w_up,
    w_down,
    rel_bias,
    gate_bias,
    out_cot,
    state_cot,
):
    low, wide = jnp.bfloat16, jnp.float32
    place = lax.axis_index("seq")
    half = lax.rem(place, 2)
    mine = place // 2
    plane = ("dp", "seq")
    spot = 4 * lax.axis_index("dp") + place
    gate_value = jax.nn.sigmoid(gate_bias)
    vecs = jnp.stack(
        [state_gain, gate_value, mlp_gain, attn_gain] + [jnp.zeros_like(gate_value)] * 4
    )
    marks = jnp.concatenate([seg_starts[:, 0], lengths, jnp.zeros((4,), jnp.int32)])
    marks = jnp.broadcast_to(marks[:, None], (8, 128))
    cot_used = lax.all_gather(out_cot.reshape(256, D), plane, axis=0, tiled=True)
    rows_all, qkv, kept, bias, marks, w_qkv = opening(
        inputs, w_query, w_key, w_value, w_sout, w_out, init_state, vecs, rel_bias, marks
    )

    ff_own = w_up.shape[1] // 8
    piece_of = lambda weight: lax.dynamic_slice_in_dim(weight, spot * 32, 32, 1).T
    back_own = jnp.stack(
        [
            piece_of(w_squery),
            piece_of(w_key),
            piece_of(w_value),
        ]
    )
    pieces = jnp.concatenate(
        [
            lax.dynamic_slice_in_dim(w_up, spot * ff_own, ff_own, 1).T,
            lax.dynamic_slice_in_dim(w_down, spot * ff_own, ff_own, 0),
        ],
        axis=0,
    )
    qkv, pieces, cot_used, back_own = lax.optimization_barrier(
        (qkv, pieces, cot_used, back_own)
    )
    spread = lax.all_gather(pieces, "tensor", axis=0, tiled=True).reshape(4, 2 * ff_own, D)
    mixed, lse_tok, state_rows, state_low, qkvst, lse_st, os_rows, cots, back = forward_chain(
        marks, qkv, kept, w_squery, w_qkv, vecs, bias, state_cot.reshape(4, 64, D), back_own
    )
    hidden_in, grad_hidden, d_mixed, mlp_sums, extra, ff_grads = middle(
        mixed, inputs, kept, spread, cot_used.reshape(8, 256, D), vecs
    )
    d_mixed, ff_grads = lax.optimization_barrier((d_mixed, ff_grads))
    ff_sum = lax.psum_scatter(
        ff_grads.reshape(ff_grads.shape[2] * 8, D), "tensor", scatter_dimension=0, tiled=True
    )
    (
        du_rows, d_start, sums, state_out, tokens_out, out_part, partial, pair_grads,
    ) = backward_chain(
        marks, qkv, d_mixed, lse_tok, qkvst, lse_st, state_rows, init_state, cots,
        back, kept, vecs, bias, extra, hidden_in, rows_all, state_low, w_qkv,
    )
    partial, ff_sum = lax.optimization_barrier((partial, ff_sum))
    ff_total = lax.all_gather(ff_sum, plane, axis=0, tiled=True).reshape(8, 2, ff_own, D)
    inputs_grad, pair, two_grads, small = closing(
        partial, pair_grads, inputs, grad_hidden, vecs, os_rows.reshape(256, D),
        du_rows.reshape(256, D), d_start, mlp_sums, sums, out_part,
    )
    pair = pair.reshape(2, PAIR_ROWS, D)
    (
        query_grad, key_grad, value_grad, squery_grad, out_grad, sout_grad, up_grad, down_grad,
        state_grad,
    ) = finish_grads(pair, two_grads, ff_total)
    bias_grad = lax.dynamic_slice_in_dim(
        small[4, : LINE * BUCKETS].reshape(4, 2, BUCKETS), lax.axis_index("tensor"), 1, 0
    )[0].T
    return (
        tokens_out,
        state_out[:, None],
        inputs_grad,
        state_grad,
        small[0],
        small[1],
        small[2],
        query_grad,
        key_grad,
        value_grad,
        out_grad,
        squery_grad,
        sout_grad,
        up_grad,
        down_grad,
        bias_grad,
        small[3],
    )


def solution(mesh):
    return jax.shard_map(
        chosen_body(mesh),
        mesh=mesh,
        in_specs=(
            P("dp", ("seq", "tensor"), None),
            P("dp", "seq"),
            P("dp"),
            P("tensor", None),
            P(),
            P(),
            P(),
            P(None, "tensor"),
            P(None, "tensor"),
            P(None, "tensor"),
            P("tensor", None),
            P(None, "tensor"),
            P("tensor", None),
            P(None, "tensor"),
            P("tensor", None),
            P(None, "tensor"),
            P(),
            P("dp", ("seq", "tensor"), None),
            P("dp", "seq", "tensor", None),
        ),
        out_specs=(
            P("dp", ("seq", "tensor"), None),
            P("dp", "seq", "tensor", None),
            P("dp", ("seq", "tensor"), None),
            P("tensor", None),
            P(),
            P(),
            P(),
            P(None, "tensor"),
            P(None, "tensor"),
            P(None, "tensor"),
            P("tensor", None),
            P(None, "tensor"),
            P("tensor", None),
            P(None, "tensor"),
            P("tensor", None),
            P(None, "tensor"),
            P(),
        ),
        check_vma=False,
    )
```

```python
import jax
import jax.numpy as jnp
from jax import lax
from jax.experimental import pallas as pl
from jax.experimental.pallas import tpu as pltpu
from jax.sharding import PartitionSpec as P

D = 1024
HEAD_DIM = 128
STATES = 512
BLOCK = 512
SEG = 256
BUCKETS = 32


norm_eps = 1e-06
masked_score = -1e30
bucket_edges = (12, 16, 23, 32, 46, 64, 91)


def passed_along(value, axis, steps):
    count = lax.axis_size(axis)
    leading, last = (max(0, -steps), min(count, count - steps))
    return lax.ppermute(value, axis, [(source, source + steps) for source in range(leading, last)])


def bucket_of(relative):
    distance = jnp.abs(relative)
    far_bucket = 8 + sum(((distance >= boundary).astype(jnp.int32) for boundary in bucket_edges))
    near_far = jnp.where(distance < 8, distance, far_bucket)
    return near_far + 16 * (relative > 0).astype(jnp.int32)


def token_mask(seg_start, seq_length, block_index):
    positions = jnp.arange(BLOCK)
    offset = block_index * BLOCK
    prev_valid = (block_index > 0) & (offset - BLOCK + positions < seq_length)
    cur_valid = offset + positions < seq_length
    inside = (positions >= seg_start) & (positions < seg_start + SEG)
    prev_mask = (positions[None, :] > positions[:, None]) & prev_valid[None, :]
    cur_mask = (
        (positions[None, :] <= positions[:, None]) | inside[None, :] & inside[:, None]
    ) & cur_valid[None, :]
    state_mask = jnp.ones((BLOCK, STATES), jnp.bool_)
    return jnp.concatenate([prev_mask, cur_mask, state_mask], axis=1)


def state_mask_of(valid_blk):
    batch_count = valid_blk.shape[0]
    block_part = jnp.broadcast_to(valid_blk[:, None, :], (batch_count, STATES, BLOCK))
    return jnp.concatenate([block_part, jnp.ones((batch_count, STATES, STATES), jnp.bool_)], axis=2)


def layer_norm(values, gain_vec):
    centered = values - jnp.mean(values, axis=-1, keepdims=True)
    spread = jnp.mean(centered * centered, axis=-1, keepdims=True)
    return centered * lax.rsqrt(spread + norm_eps) * gain_vec


def norm_back(values, gain_vec, grad_out):
    _, pullback = jax.vjp(layer_norm, values, gain_vec)
    return pullback(grad_out)


def gelu_back(pre_act, grad_out):
    _, pullback = jax.vjp(jax.nn.gelu, pre_act)
    return pullback(grad_out)[0]


def to_low(array_in):
    return array_in.astype(jnp.bfloat16)


def matmul(left, right):
    return jnp.einsum("...k,kn->...n", left, right, preferred_element_type=jnp.float32)


def matmul_t(left, right):
    return jnp.einsum("...n,kn->...k", left, right, preferred_element_type=jnp.float32)


def outer_sum(left, right):
    left_flat = left.reshape(-1, left.shape[-1])
    right_flat = right.reshape(-1, right.shape[-1])
    return lax.dot_general(
        left_flat, right_flat, (((0,), (0,)), ((), ())), preferred_element_type=jnp.float32
    )


def gather_rows(values):
    return lax.all_gather(values, "tensor", axis=1, tiled=True)


def sum_rows(terms):
    return lax.psum_scatter(
        terms.astype(jnp.bfloat16), "tensor", scatter_dimension=1, tiled=True
    ).astype(jnp.float32)


def pass_state(rows_now):
    return passed_along(rows_now.astype(jnp.bfloat16), "seq", 1).astype(rows_now.dtype)


def pass_back(grad_now):
    return passed_along(grad_now.astype(jnp.bfloat16), "seq", -1).astype(grad_now.dtype)


def split_heads(rows_in):
    return rows_in.reshape(rows_in.shape[0], rows_in.shape[1] // HEAD_DIM, HEAD_DIM)


def score_block(query_rows, key_all, bias_all, allowed):
    scores = (
        jnp.einsum(
            "qhd,khd->hqk",
            split_heads(query_rows),
            split_heads(key_all),
            preferred_element_type=jnp.float32,
        )
        * HEAD_DIM ** (-0.5)
        + bias_all
    )
    return jnp.where(allowed[None], scores, masked_score)


def attend_forward(query_rows, key_all, value_all, bias_all, allowed):
    scores = score_block(query_rows, key_all, bias_all, allowed)
    row_max = jnp.max(scores, axis=-1, keepdims=True)
    exp_scores = jnp.exp(scores - row_max)
    row_total = jnp.sum(exp_scores, axis=-1, keepdims=True)
    weight_all = to_low(exp_scores / row_total)
    mixed_out = jnp.einsum(
        "hqk,khd->qhd", weight_all, split_heads(value_all), preferred_element_type=jnp.float32
    )
    return (
        to_low(mixed_out.reshape(query_rows.shape[0], -1)),
        (row_max + jnp.log(row_total))[..., 0],
    )


def attend_back(query_rows, key_all, value_all, bias_all, allowed, log_total, grad_mixed):
    scores = score_block(query_rows, key_all, bias_all, allowed)
    weight_all = jnp.where(allowed[None], jnp.exp(scores - log_total[..., None]), 0.0)
    grad_heads = split_heads(grad_mixed)
    grad_weight = jnp.einsum(
        "qhd,khd->hqk", grad_heads, split_heads(value_all), preferred_element_type=jnp.float32
    )
    row_inner = jnp.sum(weight_all * grad_weight, axis=-1, keepdims=True)
    grad_scores = to_low(weight_all * (grad_weight - row_inner))
    grad_query = jnp.einsum(
        "hqk,khd->qhd", grad_scores, split_heads(key_all), preferred_element_type=jnp.float32
    ) * HEAD_DIM ** (-0.5)
    grad_keys = jnp.einsum(
        "hqk,qhd->khd", grad_scores, split_heads(query_rows), preferred_element_type=jnp.float32
    ) * HEAD_DIM ** (-0.5)
    grad_values = jnp.einsum(
        "hqk,qhd->khd", to_low(weight_all), grad_heads, preferred_element_type=jnp.float32
    )
    return (
        grad_query.reshape(query_rows.shape[0], -1),
        grad_keys.reshape(key_all.shape[0], -1),
        grad_values.reshape(key_all.shape[0], -1),
        grad_scores,
    )


def bias_lookup(rel_bias, rel_table):
    table_heads = jnp.zeros((rel_bias.shape[1],) + rel_table.shape, jnp.float32)
    for bucket_id in range(BUCKETS):
        table_heads = table_heads + jnp.where(
            rel_table[None] == bucket_id, rel_bias[bucket_id][:, None, None], 0.0
        )
    return table_heads


def bias_sums(score_grad, rel_table):
    grad_wide = score_grad.astype(jnp.float32)
    columns = []
    for bucket_id in range(BUCKETS):
        columns.append(
            jnp.sum(jnp.where(rel_table[None, None] == bucket_id, grad_wide, 0.0), axis=(0, 2, 3))
        )
    return jnp.stack(columns, axis=0)


def body(
    inputs,
    seg_starts,
    lengths,
    init_state,
    attn_gain,
    state_gain,
    mlp_gain,
    w_query,
    w_key,
    w_value,
    w_out,
    w_squery,
    w_sout,
    w_up,
    w_down,
    rel_bias,
    gate_bias,
    out_cot,
    state_cot,
):
    seq_count = inputs.shape[0]
    chain_length = lax.axis_size("seq")
    block_index = lax.axis_index("seq")
    is_first = block_index == 0
    width_local = w_query.shape[1]
    head_count = width_local // HEAD_DIM
    gate_value = jax.nn.sigmoid(gate_bias)
    positions = jnp.arange(BLOCK)
    inputs_wide = inputs.astype(jnp.float32)
    tokens_low = gather_rows(to_low(layer_norm(inputs_wide, attn_gain)))
    query_tok = to_low(matmul(tokens_low, w_query))
    key_tok = to_low(matmul(tokens_low, w_key))
    value_tok = to_low(matmul(tokens_low, w_value))
    key_prev, value_prev = passed_along((key_tok, value_tok), "seq", 1)
    valid_keys = (block_index * BLOCK + positions)[None, :] < lengths[:, None]
    batched_attend = jax.vmap(attend_forward, in_axes=(0, 0, 0, None, 0))
    batched_back = jax.vmap(attend_back, in_axes=(0, 0, 0, None, 0, 0, 0))

    def state_forward(state_rows, key_blk, value_blk, valid_blk):
        state_low = lax.all_gather(
            to_low(layer_norm(state_rows, state_gain)), "tensor", axis=1, tiled=True
        )
        query_st = to_low(matmul(state_low, w_squery))
        key_st = to_low(matmul(state_low, w_key))
        value_st = to_low(matmul(state_low, w_value))
        key_all = jnp.concatenate([key_blk, key_st], axis=1)
        value_all = jnp.concatenate([value_blk, value_st], axis=1)
        mixed_st, lse_st = batched_attend(
            query_st, key_all, value_all, 0.0, state_mask_of(valid_blk)
        )
        update = lax.psum_scatter(
            matmul(mixed_st, w_sout).astype(jnp.bfloat16), "tensor", scatter_dimension=1, tiled=True
        ).astype(jnp.float32)
        state_next = gate_value * state_rows + (1.0 - gate_value) * update
        return (state_next, (state_low, query_st, key_st, value_st, mixed_st, lse_st, update))

    def state_backward(
        grad_out, state_rows, kept_one, key_blk, value_blk, valid_blk, extra_key, extra_value
    ):
        state_low, query_st, key_st, value_st, mixed_st, lse_st, update = kept_one
        gate_part = (
            jnp.sum(grad_out * (state_rows - update), axis=(0, 1)) * gate_value * (1.0 - gate_value)
        )
        grad_update = lax.all_gather(
            to_low((1.0 - gate_value) * grad_out), "tensor", axis=1, tiled=True
        )
        grad_mixed_st = to_low(matmul_t(grad_update, w_sout))
        sout_part = outer_sum(mixed_st, grad_update)
        key_all = jnp.concatenate([key_blk, key_st], axis=1)
        value_all = jnp.concatenate([value_blk, value_st], axis=1)
        grad_query_st, grad_keys_st, grad_values_st, _ = batched_back(
            query_st, key_all, value_all, 0.0, state_mask_of(valid_blk), lse_st, grad_mixed_st
        )
        query_low = to_low(grad_query_st)
        key_low = to_low(grad_keys_st[:, BLOCK:] + extra_key)
        value_low = to_low(grad_values_st[:, BLOCK:] + extra_value)
        squery_part = outer_sum(state_low, query_low)
        key_part = outer_sum(state_low, key_low)
        value_part = outer_sum(state_low, value_low)
        terms = (
            matmul_t(query_low, w_squery) + matmul_t(key_low, w_key) + matmul_t(value_low, w_value)
        )
        grad_normed = lax.psum_scatter(
            terms.astype(jnp.bfloat16), "tensor", scatter_dimension=1, tiled=True
        ).astype(jnp.float32)
        grad_rows_norm, gain_part = norm_back(state_rows, state_gain, grad_normed)
        grad_in = gate_value * grad_out + grad_rows_norm
        block_grads = (grad_keys_st[:, :BLOCK], grad_values_st[:, :BLOCK])
        return (
            grad_in,
            block_grads,
            (squery_part, key_part, value_part, sout_part, gain_part, gate_part),
        )

    zeros_rows = jnp.zeros((seq_count,) + init_state.shape, jnp.float32)
    narrow_zero = jnp.zeros((seq_count, STATES, width_local), jnp.bfloat16)
    stored_start = (
        zeros_rows,
        zeros_rows,
        jnp.zeros((seq_count, STATES, D), jnp.bfloat16),
        narrow_zero,
        narrow_zero,
        narrow_zero,
        narrow_zero,
        jnp.zeros((seq_count, head_count, STATES), jnp.float32),
        zeros_rows,
    )

    def forward_turn(turn_index, carry):
        incoming, stored_now = carry
        order_index = turn_index - block_index
        is_live = (order_index >= 0) & (order_index < seq_count)
        picked = jnp.clip(order_index, 0, seq_count - 1)
        rows_now = jnp.where(is_first, init_state[None], incoming)
        key_one = lax.dynamic_slice_in_dim(key_tok, picked, 1, 0)
        value_one = lax.dynamic_slice_in_dim(value_tok, picked, 1, 0)
        valid_one = lax.dynamic_slice_in_dim(valid_keys, picked, 1, 0)
        rows_next, kept_one = state_forward(rows_now, key_one, value_one, valid_one)
        fresh = (rows_now, rows_next) + kept_one
        stored_now = tuple(
            (
                jnp.where(
                    is_live,
                    lax.dynamic_update_slice_in_dim(whole_array, fresh_part, picked, 0),
                    whole_array,
                )
                for whole_array, fresh_part in zip(stored_now, fresh)
            )
        )
        return (pass_state(rows_next), stored_now)

    incoming_start = jnp.zeros((1,) + init_state.shape, jnp.float32)
    _, stored_all = lax.fori_loop(
        0, chain_length + seq_count - 1, forward_turn, (incoming_start, stored_start)
    )
    state_in = stored_all[0]
    state_out = stored_all[1]
    kept = stored_all[2:]
    key_all_tok = jnp.concatenate([key_prev, key_tok, kept[2]], axis=1)
    value_all_tok = jnp.concatenate([value_prev, value_tok, kept[3]], axis=1)
    allowed_tok = jax.vmap(token_mask, in_axes=(0, 0, None))(seg_starts[:, 0], lengths, block_index)
    rel_table = bucket_of((jnp.arange(2 * BLOCK) - BLOCK)[None, :] - positions[:, None])
    full_bias = jnp.concatenate(
        [bias_lookup(rel_bias, rel_table), jnp.zeros((head_count, BLOCK, STATES), jnp.float32)],
        axis=2,
    )
    mixed_tok, lse_tok = batched_attend(
        query_tok, key_all_tok, value_all_tok, full_bias, allowed_tok
    )
    hidden_in = inputs_wide + sum_rows(matmul(mixed_tok, w_out))
    mid_low = gather_rows(to_low(layer_norm(hidden_in, mlp_gain)))
    pre_act = matmul(mid_low, w_up)
    hidden_low = to_low(jax.nn.gelu(pre_act))
    mlp_rows = sum_rows(matmul(hidden_low, w_down))
    tokens_out = (hidden_in + mlp_rows).astype(jnp.bfloat16)
    cot_wide = out_cot.astype(jnp.float32)
    cot_used = gather_rows(out_cot)
    grad_hidden_act = matmul_t(cot_used, w_down)
    down_grad = outer_sum(hidden_low, cot_used)
    grad_pre = to_low(gelu_back(pre_act, grad_hidden_act))
    up_grad = outer_sum(mid_low, grad_pre)
    grad_normed_mid = sum_rows(matmul_t(grad_pre, w_up))
    grad_mid_in, mlp_gain_grad = norm_back(hidden_in, mlp_gain, grad_normed_mid)
    grad_hidden = cot_wide + grad_mid_in
    grad_attn_low = gather_rows(to_low(grad_hidden))
    grad_mixed = to_low(matmul_t(grad_attn_low, w_out))
    out_grad = outer_sum(mixed_tok, grad_attn_low)
    grad_query_tok, grad_keys_tok, grad_values_tok, grad_scores = batched_back(
        query_tok, key_all_tok, value_all_tok, full_bias, allowed_tok, lse_tok, grad_mixed
    )
    bias_grad = bias_sums(grad_scores[..., : 2 * BLOCK], rel_table)
    grad_key_next, grad_value_next = (
        passed_along(grad_keys_tok[:, :BLOCK].astype(jnp.bfloat16), "seq", -1).astype(jnp.float32),
        passed_along(grad_values_tok[:, :BLOCK].astype(jnp.bfloat16), "seq", -1).astype(
            jnp.float32
        ),
    )
    grad_key_own = grad_keys_tok[:, BLOCK : 2 * BLOCK] + grad_key_next
    grad_value_own = grad_values_tok[:, BLOCK : 2 * BLOCK] + grad_value_next
    grad_key_st_tok = grad_keys_tok[:, 2 * BLOCK :]
    grad_value_st_tok = grad_values_tok[:, 2 * BLOCK :]
    cot_rows = state_cot[:, 0].astype(jnp.float32)
    wide_zero = jnp.zeros((seq_count, BLOCK, width_local), jnp.float32)
    stored_back = (zeros_rows, wide_zero, wide_zero)
    totals_start = (
        jnp.zeros((D, width_local), jnp.float32),
        jnp.zeros((D, width_local), jnp.float32),
        jnp.zeros((D, width_local), jnp.float32),
        jnp.zeros((width_local, D), jnp.float32),
        jnp.zeros((D,), jnp.float32),
        jnp.zeros((D,), jnp.float32),
    )

    def backward_turn(turn_index, carry):
        incoming, stored_now, totals_now = carry
        order_index = turn_index - (chain_length - 1 - block_index)
        is_live = (order_index >= 0) & (order_index < seq_count)
        picked = jnp.clip(order_index, 0, seq_count - 1)

        def slice_one(whole_array):
            return lax.dynamic_slice_in_dim(whole_array, picked, 1, 0)

        grad_out = slice_one(cot_rows) + incoming
        kept_one = tuple((slice_one(kept_array) for kept_array in kept))
        grad_in, block_one, parts_one = state_backward(
            grad_out,
            slice_one(state_in),
            kept_one,
            slice_one(key_tok),
            slice_one(value_tok),
            slice_one(valid_keys),
            slice_one(grad_key_st_tok),
            slice_one(grad_value_st_tok),
        )
        fresh = (grad_in,) + block_one
        stored_now = tuple(
            (
                jnp.where(
                    is_live,
                    lax.dynamic_update_slice_in_dim(whole_array, fresh_part, picked, 0),
                    whole_array,
                )
                for whole_array, fresh_part in zip(stored_now, fresh)
            )
        )
        totals_now = tuple(
            (
                total_now + jnp.where(is_live, part_now, 0.0)
                for total_now, part_now in zip(totals_now, parts_one)
            )
        )
        return (pass_back(grad_in), stored_now, totals_now)

    incoming_start = jnp.zeros((1,) + init_state.shape, jnp.float32)
    _, stored_done, weight_parts = lax.fori_loop(
        0, chain_length + seq_count - 1, backward_turn, (incoming_start, stored_back, totals_start)
    )
    grad_in_all, grad_key_blk, grad_value_blk = stored_done
    query_low = to_low(grad_query_tok)
    key_low = to_low(grad_key_own + grad_key_blk)
    value_low = to_low(grad_value_own + grad_value_blk)
    query_grad = outer_sum(tokens_low, query_low)
    key_grad = outer_sum(tokens_low, key_low) + weight_parts[1]
    value_grad = outer_sum(tokens_low, value_low) + weight_parts[2]
    grad_tokens = sum_rows(
        matmul_t(query_low, w_query) + matmul_t(key_low, w_key) + matmul_t(value_low, w_value)
    )
    grad_in_norm, attn_gain_grad = norm_back(inputs_wide, attn_gain, grad_tokens)
    inputs_grad = grad_hidden + grad_in_norm
    state_part = jnp.where(is_first, jnp.sum(grad_in_all, axis=0), 0.0)
    gains = lax.psum(
        jnp.stack([attn_gain_grad, weight_parts[4], mlp_gain_grad, weight_parts[5]]), "tensor"
    )
    totals = (
        lax.psum(query_grad.astype(jnp.bfloat16), ("dp", "seq")).astype(jnp.float32),
        lax.psum(key_grad.astype(jnp.bfloat16), ("dp", "seq")).astype(jnp.float32),
        lax.psum(value_grad.astype(jnp.bfloat16), ("dp", "seq")).astype(jnp.float32),
        lax.psum(out_grad.astype(jnp.bfloat16), ("dp", "seq")).astype(jnp.float32),
        lax.psum(weight_parts[0].astype(jnp.bfloat16), ("dp", "seq")).astype(jnp.float32),
        lax.psum(weight_parts[3].astype(jnp.bfloat16), ("dp", "seq")).astype(jnp.float32),
        lax.psum(up_grad.astype(jnp.bfloat16), ("dp", "seq")).astype(jnp.float32),
        lax.psum(down_grad.astype(jnp.bfloat16), ("dp", "seq")).astype(jnp.float32),
        lax.psum(bias_grad.astype(jnp.bfloat16), ("dp", "seq")).astype(jnp.float32),
        lax.psum(state_part.astype(jnp.bfloat16), ("dp", "seq")).astype(jnp.float32),
        lax.psum(gains.astype(jnp.bfloat16), ("dp", "seq")).astype(jnp.float32),
    )
    gain_total = totals[10]
    return (
        tokens_out,
        state_out[:, None],
        inputs_grad,
        totals[9],
        gain_total[0],
        gain_total[1],
        gain_total[2],
        totals[0],
        totals[1],
        totals[2],
        totals[3],
        totals[4],
        totals[5],
        totals[6],
        totals[7],
        totals[8],
        gain_total[3],
    )


def chosen_body(mesh):
    if mesh.shape["seq"] == 4 and mesh.shape["tensor"] == 4:
        return line_body
    return body


MESH_ID = pl.DeviceIdType.MESH
ROWS = 128
CHUNKS = BLOCK // ROWS
LINE = 8
SCALE = HEAD_DIM ** (-0.5)
VMEM_LIMIT = 60 * 1024 * 1024


def dot_nn(left, right):
    return lax.dot_general(left, right, (((1,), (0,)), ((), ())), preferred_element_type=jnp.float32)


def dot_nt(left, right):
    return lax.dot_general(left, right, (((1,), (1,)), ((), ())), preferred_element_type=jnp.float32)


def dot_tn(left, right):
    return lax.dot_general(left, right, (((0,), (0,)), ((), ())), preferred_element_type=jnp.float32)


def line_place():
    place = lax.axis_index("seq")
    half = lax.rem(place, 2)
    rank = lax.axis_index("tensor")
    return place, half, rank


def span(index, size):
    return pl.ds(pl.multiple_of(index * size, size), size)


def fetch_pieces(kept, first, rows, target, sem):
    for owner in range(8):
        pltpu.make_async_copy(
            kept.at[owner, :, pl.ds(first, rows), :], target.at[:, owner], sem
        ).start()


def fetch_columns(weights, target, sem):
    half = lax.rem(lax.axis_index("seq"), 2)
    for index, weight in enumerate(weights):
        pltpu.make_async_copy(
            weight.at[:, span(half, 128)], target.at[:, pl.ds(128 * index, 128)], sem
        ).start()


def fetched(target, sem):
    pltpu.make_async_copy(target, target, sem).wait()


def norm_parts(rows):
    centered = rows - jnp.mean(rows, axis=-1, keepdims=True)
    spread = jnp.mean(centered * centered, axis=-1, keepdims=True)
    return centered, lax.rsqrt(spread + norm_eps)


def mark(marks, block_id, row):
    return marks[block_id, pl.ds(row, 1), 0:1]


def sequence_marks(marks, block_id):
    mine = lax.axis_index("seq") // 2
    return mark(marks, block_id, mine), mark(marks, 0, 2 + mine)


def token_masks(marks, block_id, first_row):
    start, length = sequence_marks(marks, block_id)
    row = lax.broadcasted_iota(jnp.int32, (ROWS, BLOCK), 0) + first_row
    col = lax.broadcasted_iota(jnp.int32, (ROWS, BLOCK), 1)
    prev_limit = jnp.where(block_id > 0, length - (block_id - 1) * BLOCK, 0)
    prev_ok = (col > row) & (col < prev_limit)
    row_in = (row >= start) & (row < start + SEG)
    col_in = (col >= start) & (col < start + SEG)
    cur_ok = ((col <= row) | (row_in & col_in)) & (col < length - block_id * BLOCK)
    return prev_ok, cur_ok


def state_block_mask(marks, block_id):
    _, length = sequence_marks(marks, block_id)
    col = lax.broadcasted_iota(jnp.int32, (ROWS, BLOCK), 1)
    return col < length - block_id * BLOCK


def softmax_of(score_parts):
    top = jnp.max(score_parts[0], axis=-1, keepdims=True)
    for part in score_parts[1:]:
        top = jnp.maximum(top, jnp.max(part, axis=-1, keepdims=True))
    raised = [jnp.exp(part - top) for part in score_parts]
    total = jnp.sum(raised[0], axis=-1, keepdims=True)
    for part in raised[1:]:
        total = total + jnp.sum(part, axis=-1, keepdims=True)
    inverse = 1.0 / total
    return [to_low(part * inverse) for part in raised], top + jnp.log(total)


def token_scores(scal, qkv, qkvst, bias, block_id, chunk):
    rows = span(chunk, ROWS)
    prev_id = jnp.maximum(block_id - 1, 0)
    query = qkv[block_id, rows, 0:128]
    prev_ok, cur_ok = token_masks(scal, block_id, chunk * ROWS)
    prev = dot_nt(query, qkv[prev_id, :, 128:256]) * SCALE + bias[rows, 0:BLOCK]
    cur = dot_nt(query, qkv[block_id, :, 128:256]) * SCALE + bias[rows, BLOCK : 2 * BLOCK]
    stt = dot_nt(query, qkvst[block_id, :, 128:256]) * SCALE
    prev = jnp.where(prev_ok, prev, masked_score)
    cur = jnp.where(cur_ok, cur, masked_score)
    return query, (prev, cur, stt)


def state_scores(scal, qkv, qkvst, block_id, chunk):
    query = qkvst[block_id, span(chunk, ROWS), 0:128]
    tok = dot_nt(query, qkv[block_id, :, 128:256]) * SCALE
    tok = jnp.where(state_block_mask(scal, block_id), tok, masked_score)
    stt = dot_nt(query, qkvst[block_id, :, 128:256]) * SCALE
    return query, (tok, stt)


HALVES = 2
HALF_ROWS = STATES // HALVES
HALF_CHUNKS = HALF_ROWS // ROWS


def forward_kernel(
    marks, qkv, kept, w_squery, w_qkv, vecs, bias, state_cot, back_own,
    o_out, lse_out, state_rows, low_out, qkvst, lse_st, os_rows, cots, back,
    held, os_all, state_low, w_sout, start, w_state,
    way_send, core_send, recv_sem, local_sem, low_sem, cot_send, cot_recv,
    piece_send, piece_recv, ring_send, ring_recv,
):
    side, place, half, rank = plane_place()
    me = plane_index(side, place)
    partner = place + 1 - 2 * half
    head = 2 * rank + half
    fetch_pieces(kept, 32, 16, start, local_sem.at[0])
    fetch_columns((w_squery,), w_state, local_sem.at[2])
    fetch_pieces(kept, 0, 32, w_sout, local_sem.at[1])
    own_cot = pltpu.make_async_copy(state_cot.at[place], cots.at[place], local_sem.at[4])
    own_cot.start()
    own_piece = pltpu.make_async_copy(back_own, back.at[me, rank], local_sem.at[3])
    own_piece.start()
    ranks = [lax.rem(rank + step, 4) for step in (1, 2, 3)]
    seats = [lax.rem(place + step, 4) for step in (1, 2, 3)]
    barrier = pltpu.get_barrier_semaphore()
    for target in [{"tensor": one} for one in ranks] + [{"seq": one} for one in seats] + [
        {"dp": 1 - side}
    ]:
        pl.semaphore_signal(barrier, inc=1, device_id=target, device_id_type=MESH_ID)
    fetched(start, local_sem.at[0])
    held[...] = start[...].reshape(STATES, D).astype(jnp.float32)
    gain = vecs[0:1, :]
    gate = vecs[1:2, :]
    fetched(w_state, local_sem.at[2])

    def project(block_id, part):
        def one(chunk, _):
            rows = span(chunk, ROWS)
            centered, scale = norm_parts(held[rows, :])
            low = to_low(centered * scale * gain)
            state_low[block_id, rows, :] = low
            qkvst[block_id, rows, 0:128] = to_low(dot_nn(low, w_state[...]))
            qkvst[block_id, rows, 128:384] = to_low(dot_nn(low, w_qkv[:, 128:384]))
            return 0

        lax.fori_loop(HALF_CHUNKS * part, HALF_CHUNKS * (part + 1), one, 0)

    pl.semaphore_wait(barrier, 7)

    def piece_move(origin, part, slot, target):
        return pltpu.make_async_remote_copy(
            src_ref=back_own.at[part],
            dst_ref=back.at[me, origin, part],
            send_sem=piece_send.at[part, slot],
            recv_sem=piece_recv.at[part, origin],
            device_id={"tensor": target},
            device_id_type=MESH_ID,
        )

    def send_piece(part):
        for slot, target in enumerate(ranks):
            piece_move(rank, part, slot, target).start()

    gather = plane_gather(
        lambda owner, part: back.at[owner, pl.ds(2 * part, 2)], ring_send, ring_recv
    )
    next(gather)
    send_piece(0)
    for part in range(HALVES):
        project(0, part)
    right, left = {"tensor": lax.rem(rank + 1, 4)}, {"tensor": lax.rem(rank + 3, 4)}

    def moved(block_id, part, which, sem, target):
        view = os_all.at[block_id, pl.ds(HALF_ROWS * part, HALF_ROWS), span(which, 128)]
        return pltpu.make_async_remote_copy(
            src_ref=view,
            dst_ref=view,
            send_sem=sem,
            recv_sem=recv_sem.at[block_id, part, which],
            device_id=target,
            device_id_type=MESH_ID,
        )

    def cot_move(index, origin, slot, target):
        return pltpu.make_async_remote_copy(
            src_ref=state_cot.at[index],
            dst_ref=cots.at[origin],
            send_sem=cot_send.at[slot],
            recv_sem=cot_recv.at[origin],
            device_id={"seq": target},
            device_id_type=MESH_ID,
        )

    for slot, target in enumerate(seats):
        cot_move(target, place, slot, target).start()
    fetched(w_sout, local_sem.at[1])

    def origin_of(way, distance):
        if way == 0:
            return jnp.maximum(rank - distance, 0)
        return jnp.minimum(rank + distance, 3)

    def ways(distance):
        return (
            (0, rank >= distance, (rank >= distance) & (rank < 3), right),
            (1, rank + distance <= 3, (rank + distance <= 3) & (rank > 0), left),
        )

    def relay(block_id, part, distance, waiting):
        for way, comes, goes, target in ways(distance):
            which = 2 * origin_of(way, distance) + half
            sem = way_send.at[block_id, part, min(distance, 2), way]
            core_sem = core_send.at[block_id, part, which // 2]
            if distance > 0:

                @pl.when(comes)
                def _():
                    to_core = moved(block_id, part, which, core_sem, {"seq": partner})
                    if waiting:
                        moved(block_id, part, which, sem, target).wait_recv()
                        to_core.start()
                    else:
                        to_core.wait_send()

            if distance < 3:

                @pl.when(goes)
                def _():
                    one = moved(block_id, part, which, sem, target)
                    if waiting:
                        one.start()
                    else:
                        one.wait_send()

        if distance == 0:
            mine = moved(
                block_id, part, head, core_send.at[block_id, part, rank], {"seq": partner}
            )
            if waiting:
                mine.start()
            else:
                mine.wait_send()

    def one_block(block_id, _):
        def attend_state(chunk, _):
            rows = span(chunk, ROWS)
            _, parts = state_scores(marks, qkv, qkvst, block_id, chunk)
            (w_tok, w_stt), total = softmax_of(parts)
            mixed = dot_nn(w_tok, qkv[block_id, :, 256:384]) + dot_nn(
                w_stt, qkvst[block_id, :, 256:384]
            )
            os_all[block_id, rows, span(head, 128)] = to_low(mixed)
            lse_st[block_id, rows, :] = total
            return 0

        def attend_token(chunk, _):
            rows = span(chunk, ROWS)
            _, parts = token_scores(marks, qkv, qkvst, bias, block_id, chunk)
            weights, total = softmax_of(parts)
            prev_id = jnp.maximum(block_id - 1, 0)
            mixed = (
                dot_nn(weights[0], qkv[prev_id, :, 256:384])
                + dot_nn(weights[1], qkv[block_id, :, 256:384])
                + dot_nn(weights[2], qkvst[block_id, :, 256:384])
            )
            o_out[block_id, rows, :] = to_low(mixed)
            lse_out[block_id, rows, :] = total
            return 0

        def attend_both(part, _):
            lax.fori_loop(HALF_CHUNKS * part, HALF_CHUNKS * (part + 1), attend_state, 0)
            for value in range(HALVES):

                @pl.when(part == value)
                def _():
                    relay(block_id, value, 0, True)

            return 0

        lax.fori_loop(0, HALVES, attend_both, 0)
        pltpu.make_async_copy(
            state_low.at[block_id], low_out.at[block_id], low_sem.at[block_id]
        ).start()

        @pl.when(block_id == 2)
        def _():
            own_piece.wait()
            for part in range(3):
                for slot, target in enumerate(ranks):
                    piece_move(target, part, slot, target).wait_recv()
            next(gather)

        @pl.when(block_id == 3)
        def _():
            next(gather)
            next(gather)

        def between(step, _):
            for value, (distance, part) in enumerate(((1, 0), (1, 1), (2, 0), (2, 1))):

                @pl.when(step == value)
                def _():
                    relay(block_id, part, distance, True)

            return attend_token(step, 0)

        lax.fori_loop(0, 4, between, 0)

        def settle(part, _):
            for value in range(HALVES):

                @pl.when(part == value)
                def _():
                    relay(block_id, value, 3, True)
                    for origin in range(4):
                        moved(
                            block_id, value, 2 * origin + 1 - half,
                            core_send.at[block_id, value, origin], {"seq": partner},
                        ).wait_recv()

                    if value == HALVES - 1:
                        for turn in (0, 1):

                            @pl.when(block_id == turn)
                            def _():
                                send_piece(turn + 1)

            def update(chunk, _):
                rows = span(chunk, ROWS)
                change = dot_nn(os_all[block_id, rows, :], w_sout[...].reshape(D, D))
                held[rows, :] = gate * held[rows, :] + (1.0 - gate) * change
                return 0

            lax.fori_loop(HALF_CHUNKS * part, HALF_CHUNKS * (part + 1), update, 0)

            @pl.when(block_id < 3)
            def _():
                project(block_id + 1, part)

            return 0

        lax.fori_loop(0, HALVES, settle, 0)
        state_rows[block_id] = held[span(rank, 128), :]
        os_rows[block_id] = os_all[block_id, span(head, 64), :]
        return 0

    lax.fori_loop(0, 4, one_block, 0)

    def drain(block_id, _):
        for part in range(HALVES):
            for distance in range(4):
                relay(block_id, part, distance, False)
        pltpu.make_async_copy(
            state_low.at[block_id], low_out.at[block_id], low_sem.at[block_id]
        ).wait()
        return 0

    lax.fori_loop(0, 4, drain, 0)
    own_cot.wait()
    for part in range(3):
        for slot, target in enumerate(ranks):
            piece_move(rank, part, slot, target).wait_send()
    for _ in gather:
        pass
    for slot, target in enumerate(seats):
        cot_move(target, place, slot, target).wait_send()
        cot_move(place, target, slot, target).wait_recv()


def any_specs(count):
    return [pl.BlockSpec(memory_space=pl.ANY)] * count


def vmem_specs(count):
    return [pl.BlockSpec(memory_space=pltpu.VMEM)] * count


def forward_chain(
    marks, qkv, kept, w_squery, w_qkv, vecs, bias, state_cot, back_own
):
    low, wide = jnp.bfloat16, jnp.float32
    shapes = (
        ((4, BLOCK, 128), low),
        ((4, BLOCK, 1), wide),
        ((4, 128, D), wide),
        ((4, STATES, D), low),
        ((4, STATES, 384), low),
        ((4, STATES, 1), wide),
        ((4, 64, D), low),
        ((4, 64, D), low),
        ((8, 4, 3, 32, D), low),
    )
    dma = pltpu.SemaphoreType.DMA
    return pl.pallas_call(
        forward_kernel,
        out_shape=[jax.ShapeDtypeStruct(*one) for one in shapes],
        in_specs=vmem_specs(2) + any_specs(2) + vmem_specs(3) + any_specs(2),
        out_specs=vmem_specs(3) + any_specs(1) + vmem_specs(3) + any_specs(2),
        scratch_shapes=[
            pltpu.VMEM((STATES, D), wide),
            pltpu.VMEM((4, STATES, D), low),
            pltpu.VMEM((4, STATES, D), low),
            pltpu.VMEM((4, 8, 32, D), low),
            pltpu.VMEM((4, 8, 16, D), low),
            pltpu.VMEM((D, 128), low),
            dma((4, HALVES, 3, 2)),
            dma((4, HALVES, 4)),
            dma((4, HALVES, 8)),
            dma((5,)),
            dma((4,)),
            dma((3,)),
            dma((4,)),
            dma((3, 3)),
            dma((3, 4)),
            dma((14,)),
            dma((8, 2)),
        ],
        compiler_params=pltpu.CompilerParams(
            collective_id=1, has_side_effects=True, vmem_limit_bytes=VMEM_LIMIT
        ),
        cost_estimate=pl.CostEstimate(
            flops=60000000000, bytes_accessed=60000000, transcendentals=0
        ),
        name="forward_chain",
    )(marks, qkv, kept, w_squery, w_qkv, vecs, bias, state_cot, back_own)


def backward_kernel(
    scal, qkv, d_o, lse_tok, qkvst, lse_st, state_rows, begin, cots, back, kept, vecs, bias,
    extra, hidden, rows_hbm, low_hbm, w_qkv, os_rows,
    du_rows, d_start, sums, state_out, tokens_out, out_part, partial, pair_grads, sout_part,
    dz_sum, diag, d_qkv, d_qkvst, rows_buf, low_buf, leave, came, grad_acc,
    key_acc, value_acc, st_key, st_value, dos_rows, dos_got, d_got, grad_in,
    states, w_back, w_sout, work, core_got, near_got, far_got, total,
    send_sem, recv_sem, local_sem, side_sem, ring_send, ring_recv, buf_sem, core_sem, came_sem,
    near_two, far_two, two_send, two_recv,
):
    place, half, rank = line_place()
    own_rows = pl.ds(pl.multiple_of(half * 64, 64), 64)
    loads = [
        pltpu.make_async_copy(
            state_rows.at[:, own_rows, :], states.at[pl.ds(1, 4)], local_sem.at[0]
        ),
        pltpu.make_async_copy(
            state_rows.at[place], state_out.at[place // 2], local_sem.at[3]
        ),
        pltpu.make_async_copy(extra, work, local_sem.at[4]),
    ]
    for one in loads:
        one.start()
    fetch_pieces(kept, 0, 32, w_sout, local_sem.at[1])
    for owner in range(8):
        pltpu.make_async_copy(
            back.at[owner], w_back.at[:, owner // 4, :, owner % 4], local_sem.at[2]
        ).start()
    states[0] = to_low(begin[own_rows, :]).astype(jnp.float32)

    def block_loads(block_id):
        slot = lax.rem(block_id, 2)
        return [
            pltpu.make_async_copy(
                source.at[block_id], target.at[slot], buf_sem.at[index, slot]
            )
            for index, (source, target) in enumerate(((rows_hbm, rows_buf), (low_hbm, low_buf)))
        ]

    for one in block_loads(3):
        one.start()
    head = 2 * rank + half
    peers = []
    for step in (4, 3, 5, 2, 6, 1, 7):
        other = lax.rem(head + step, LINE)
        peers.append((other, place - half + lax.rem(other, 2), other // 2))
    barrier = pltpu.get_barrier_semaphore()
    for _, seq_to, rank_to in peers:
        pl.semaphore_signal(
            barrier, inc=1, device_id={"seq": seq_to, "tensor": rank_to}, device_id_type=MESH_ID
        )
    beside = lax.rem(place + 2, 4)
    pl.semaphore_signal(barrier, inc=1, device_id={"seq": beside}, device_id_type=MESH_ID)
    pl.semaphore_signal(
        barrier, inc=1, device_id={"dp": 1 - lax.axis_index("dp")}, device_id_type=MESH_ID
    )
    plane_steps = plane_scatter(
        work, core_got, near_got, far_got, total, 384, ring_send, ring_recv
    )
    next(plane_steps)
    short = pl.ds(0, 128)
    sout_steps = plane_scatter(
        work.at[:, short, :], core_got.at[:, short, :], near_two, far_two, total.at[short, :],
        128, two_send, two_recv,
    )
    next(sout_steps)

    def sout_products():
        def one(index, _):
            part = to_low(
                dot_tn(os_rows[:, span(index, 128)], du_rows[...].reshape(256, D))
            )
            for block in range(4):
                work[4 * lax.rem(index, 2) + block, span(index // 2, 32), :] = part[
                    32 * block : 32 * block + 32, :
                ]
            return 0

        lax.fori_loop(0, LINE, one, 0)

    def plane_results():
        for which in range(2):
            rows = pl.ds(128 * which, 128)
            tokens_out[which] = to_low(hidden[which] + total[rows, :])
        out_part[...] = to_low(total[256:384, :])


    def aside(block_id, row_set):
        return pltpu.make_async_remote_copy(
            src_ref=state_rows.at[block_id],
            dst_ref=state_out.at[row_set],
            send_sem=side_sem.at[0],
            recv_sem=side_sem.at[1],
            device_id={"seq": beside},
            device_id_type=MESH_ID,
        )

    gain = vecs[0:1, :]
    gate = vecs[1:2, :]
    key_acc[...] = jnp.zeros_like(key_acc)
    value_acc[...] = jnp.zeros_like(value_acc)
    dz_sum[...] = jnp.zeros_like(dz_sum)
    sums[...] = jnp.zeros_like(sums)
    grad_in[...] = jnp.zeros_like(grad_in)
    grad_acc[...] = jnp.zeros_like(grad_acc)
    core = place + 1 - 2 * half

    def place_in(block_id, owner):
        return jnp.where(block_id == owner, 1, 0)

    def leaving(slot):
        return pltpu.make_async_remote_copy(
            src_ref=leave.at[slot],
            dst_ref=came.at[slot],
            send_sem=core_sem.at[slot],
            recv_sem=came_sem.at[slot],
            device_id={"seq": core},
            device_id_type=MESH_ID,
        )

    def add_came(slot):
        leaving(slot).wait_recv()

        def one(chunk, _):
            partial[slot, chunk] = to_low(
                partial[slot, chunk].astype(jnp.float32)
                + came[slot, span(chunk, 128), :].astype(jnp.float32)
            )
            return 0

        lax.fori_loop(0, 4, one, 0)

    def bucket_sums():
        diag[...] = jnp.zeros_like(diag)

        def one(group, _):
            rows = dz_sum[span(group, 8), :]
            wide = jnp.concatenate([rows, jnp.zeros((8, WIDE - 2 * BLOCK), jnp.float32)], axis=1)
            diag[...] += pltpu.roll(wide, lax.rem(WIDE - 8 * group, WIDE), 1)
            return 0

        lax.fori_loop(0, BLOCK // 8, one, 0)
        line = diag[...]
        row = lax.broadcasted_iota(jnp.int32, (8, WIDE), 0)
        for step in (1, 2, 4):
            line = jnp.where(row // step % 2 == 1, pltpu.roll(line, WIDE - step, 1), line)
        lane = lax.broadcasted_iota(jnp.int32, (8, WIDE), 1)
        bucket_ids = bucket_of(jnp.where(lane >= WIDE - BLOCK, lane - WIDE - BLOCK, lane - BLOCK))
        spot = lax.broadcasted_iota(jnp.int32, (1, 256), 1) - BUCKETS * head
        placed = jnp.zeros((1, 256), jnp.float32)
        for bucket_id in range(BUCKETS):
            chosen = jnp.where(bucket_ids == bucket_id, line, 0.0)
            value = jnp.sum(jnp.sum(chosen, axis=0, keepdims=True), axis=1, keepdims=True)
            placed = jnp.where(spot == bucket_id, value, placed)
        sums[2:3, 0:256] = placed

    def block_products(block_id):
        slot = lax.rem(block_id, 2)
        for one in block_loads(block_id):
            one.wait()

        @pl.when(block_id > 0)
        def _():
            for one in block_loads(jnp.maximum(block_id - 1, 0)):
                one.start()

        def one_part(part, _):
            rows = span(part, 128)

            @pl.when(part < 3)
            def _():
                grad_acc[rows, :] += dot_tn(
                    d_qkv[block_id, :, span(jnp.minimum(part, 2), 128)], rows_buf[slot]
                )

            @pl.when(part > 0)
            def _():
                grad_acc[rows, :] += dot_tn(
                    d_qkvst[block_id, :, span(lax.rem(part, 3), 128)], low_buf[slot]
                )

            return 0

        lax.fori_loop(0, 4, one_part, 0)
        kept_here = lax.rem(block_id, 2) == half
        mine_slot, core_slot = place_in(block_id, place), place_in(block_id, core)

        def one_chunk(chunk, _):
            rows = span(chunk, 128)
            value = to_low(dot_nt(d_qkv[block_id, rows, :], w_qkv[...]))

            @pl.when(kept_here)
            def _():
                partial[mine_slot, chunk] = value

            @pl.when(jnp.logical_not(kept_here))
            def _():
                leave[core_slot, rows, :] = value

            return 0

        lax.fori_loop(0, 4, one_chunk, 0)

        @pl.when(jnp.logical_not(kept_here))
        def _():
            leaving(core_slot).start()

    def back_parts(parts, total, grad, values):
        weights = [jnp.exp(part - total) for part in parts]
        d_weights = [dot_nt(grad, value) for value in values]
        inner = jnp.sum(weights[0] * d_weights[0], axis=-1, keepdims=True)
        for one, other in zip(weights[1:], d_weights[1:]):
            inner = inner + jnp.sum(one * other, axis=-1, keepdims=True)
        d_scores = [to_low(one * (other - inner)) for one, other in zip(weights, d_weights)]
        return [to_low(one) for one in weights], d_scores

    def token_back(block_id):
        prev_id = jnp.maximum(block_id - 1, 0)
        st_key[...] = jnp.zeros_like(st_key)
        st_value[...] = jnp.zeros_like(st_value)

        def one_chunk(chunk, _):
            rows = span(chunk, ROWS)
            query, parts = token_scores(scal, qkv, qkvst, bias, block_id, chunk)
            grad = d_o[block_id, rows, :]
            keys = (qkv[prev_id, :, 128:256], qkv[block_id, :, 128:256], qkvst[block_id, :, 128:256])
            values = (
                qkv[prev_id, :, 256:384], qkv[block_id, :, 256:384], qkvst[block_id, :, 256:384]
            )
            weights, d_scores = back_parts(parts, lse_tok[block_id, rows, :], grad, values)
            d_query = dot_nn(d_scores[0], keys[0])
            d_query = d_query + dot_nn(d_scores[1], keys[1]) + dot_nn(d_scores[2], keys[2])
            d_qkv[block_id, rows, 0:128] = to_low(d_query * SCALE)
            key_acc[prev_id] += dot_tn(d_scores[0], query) * SCALE
            value_acc[prev_id] += dot_tn(weights[0], grad)
            key_acc[block_id] += dot_tn(d_scores[1], query) * SCALE
            value_acc[block_id] += dot_tn(weights[1], grad)
            st_key[...] += dot_tn(d_scores[2], query) * SCALE
            st_value[...] += dot_tn(weights[2], grad)
            dz_sum[rows, 0:BLOCK] += d_scores[0].astype(jnp.float32)
            dz_sum[rows, BLOCK : 2 * BLOCK] += d_scores[1].astype(jnp.float32)
            return 0

        lax.fori_loop(0, CHUNKS, one_chunk, 0)

    token_back(3)
    pl.semaphore_wait(barrier, LINE + 1)
    aside(beside, place // 2).start()
    loads[2].wait()
    loads[0].wait()
    fetched(w_sout, local_sem.at[1])
    fetched(w_back, local_sem.at[2])

    def mixed_copy(block_id, slot, sender, other, seq_to, rank_to):
        return pltpu.make_async_remote_copy(
            src_ref=dos_rows.at[block_id, :, span(other, 128)],
            dst_ref=dos_got.at[block_id, span(sender, 64), :],
            send_sem=send_sem.at[0, block_id, slot],
            recv_sem=recv_sem.at[0, block_id, sender],
            device_id={"seq": seq_to, "tensor": rank_to},
            device_id_type=MESH_ID,
        )

    def grads_copy(block_id, slot, sender, other, seq_to, rank_to):
        return pltpu.make_async_remote_copy(
            src_ref=d_qkvst.at[block_id, span(other, 64), :],
            dst_ref=d_got.at[block_id, sender],
            send_sem=send_sem.at[1, block_id, slot],
            recv_sem=recv_sem.at[1, block_id, sender],
            device_id={"seq": seq_to, "tensor": rank_to},
            device_id_type=MESH_ID,
        )

    def one_block(turn, _):
        block_id = 3 - turn
        grad_out = grad_in[...] + cots[block_id].astype(jnp.float32)
        sums[0:1, :] += jnp.sum(
            grad_out * (states[block_id] - states[block_id + 1]), axis=0, keepdims=True
        ) * gate
        change = to_low((1.0 - gate) * grad_out)
        du_rows[block_id] = change
        dos_rows[block_id] = to_low(dot_nt(change, w_sout[...].reshape(D, D)))
        for slot, (other, seq_to, rank_to) in enumerate(peers):
            mixed_copy(block_id, slot, head, other, seq_to, rank_to).start()
        dos_got[block_id, span(head, 64), :] = dos_rows[block_id, :, span(head, 128)]

        @pl.when(turn > 0)
        def _():
            block_products(block_id + 1)

        @pl.when(turn == 3)
        def _():
            sout_products()

        for slot, (other, seq_to, rank_to) in enumerate(peers):
            mixed_copy(block_id, slot, other, other, seq_to, rank_to).wait_recv()

        def one_chunk(chunk, _):
            rows = span(chunk, ROWS)
            query, parts = state_scores(scal, qkv, qkvst, block_id, chunk)
            grad = dos_got[block_id, rows, :]
            keys = (qkv[block_id, :, 128:256], qkvst[block_id, :, 128:256])
            values = (qkv[block_id, :, 256:384], qkvst[block_id, :, 256:384])
            weights, d_scores = back_parts(parts, lse_st[block_id, rows, :], grad, values)
            d_query = dot_nn(d_scores[0], keys[0]) + dot_nn(d_scores[1], keys[1])
            d_qkvst[block_id, rows, 0:128] = to_low(d_query * SCALE)
            key_acc[block_id] += dot_tn(d_scores[0], query) * SCALE
            value_acc[block_id] += dot_tn(weights[0], grad)
            st_key[...] += dot_tn(d_scores[1], query) * SCALE
            st_value[...] += dot_tn(weights[1], grad)
            return 0

        lax.fori_loop(0, CHUNKS, one_chunk, 0)
        d_qkvst[block_id, :, 128:256] = to_low(st_key[...])
        d_qkvst[block_id, :, 256:384] = to_low(st_value[...])
        for slot, (other, seq_to, rank_to) in enumerate(peers):
            grads_copy(block_id, slot, head, other, seq_to, rank_to).start()
        d_got[block_id, head] = d_qkvst[block_id, span(head, 64), :]

        for step in range(3):

            @pl.when(turn == step)
            def _():
                next(plane_steps)
                if step == 2:
                    next(plane_steps, None)
                    plane_results()

        @pl.when(turn == 3)
        def _():
            next(sout_steps)
            add_came(place_in(2 + half, place))
            bucket_sums()
            next(sout_steps)

        @pl.when(turn < 3)
        def _():
            token_back(block_id - 1)

        d_qkv[block_id, :, 128:256] = to_low(key_acc[block_id])
        d_qkv[block_id, :, 256:384] = to_low(value_acc[block_id])
        @pl.when(turn == 3)
        def _():
            block_products(0)
            next(sout_steps)

        for slot, (other, seq_to, rank_to) in enumerate(peers):
            grads_copy(block_id, slot, other, other, seq_to, rank_to).wait_recv()
        d_low = dot_nn(d_got[block_id, 0], w_back[0, 0].reshape(384, D))
        for other in range(1, LINE):
            d_low = d_low + dot_nn(
                d_got[block_id, other], w_back[other // 2, other % 2].reshape(384, D)
            )
        centered, scale = norm_parts(states[block_id])
        normed = centered * scale
        sums[1:2, :] += jnp.sum(d_low * normed, axis=0, keepdims=True)
        lifted = d_low * gain
        grad_in[...] = gate * grad_out + scale * (
            lifted
            - jnp.mean(lifted, axis=-1, keepdims=True)
            - normed * jnp.mean(lifted * normed, axis=-1, keepdims=True)
        )
        return 0

    lax.fori_loop(0, 4, one_block, 0)
    d_start[...] = grad_in[...]

    def drain(block_id, _):
        for slot, (other, seq_to, rank_to) in enumerate(peers):
            mixed_copy(block_id, slot, head, other, seq_to, rank_to).wait_send()
            grads_copy(block_id, slot, head, other, seq_to, rank_to).wait_send()
        return 0

    lax.fori_loop(0, 4, drain, 0)
    pair_grads[...] = to_low(grad_acc[...])
    for _ in sout_steps:
        pass
    sout_part[...] = to_low(total[0:128, :])
    add_came(place_in(half, place))
    for slot in range(2):
        leaving(slot).wait_send()
    loads[1].wait()
    aside(beside, place // 2).wait_send()
    aside(place, 1 - place // 2).wait_recv()


def backward_chain(
    scal, qkv, d_o, lse_tok, qkvst, lse_st, state_rows, begin, cots, back, kept, vecs, bias,
    extra, hidden, rows_all, state_low, w_qkv, os_rows,
):
    low, wide = jnp.bfloat16, jnp.float32
    shapes = (
        ((4, 64, D), low),
        ((64, D), wide),
        ((8, D), wide),
        ((2, 128, D), wide),
        ((2, 128, D), low),
        ((128, D), low),
        ((2, 4, 128, D), low),
        ((512, D), low),
        ((128, D), low),
    )
    return pl.pallas_call(
        backward_kernel,
        out_shape=[jax.ShapeDtypeStruct(*one) for one in shapes],
        in_specs=vmem_specs(6)
        + any_specs(1)
        + vmem_specs(2)
        + any_specs(2)
        + vmem_specs(2)
        + any_specs(1)
        + vmem_specs(1)
        + any_specs(2)
        + vmem_specs(2),
        out_specs=vmem_specs(3) + any_specs(1) + vmem_specs(5),
        scratch_shapes=[
            pltpu.VMEM((BLOCK, 2 * BLOCK), wide),
            pltpu.VMEM((8, WIDE), wide),
            pltpu.VMEM((4, BLOCK, 384), low),
            pltpu.VMEM((4, STATES, 384), low),
            pltpu.VMEM((2, BLOCK, D), low),
            pltpu.VMEM((2, STATES, D), low),
            pltpu.VMEM((2, BLOCK, D), low),
            pltpu.VMEM((2, BLOCK, D), low),
            pltpu.VMEM((512, D), wide),
            pltpu.VMEM((4, BLOCK, 128), wide),
            pltpu.VMEM((4, BLOCK, 128), wide),
            pltpu.VMEM((STATES, 128), wide),
            pltpu.VMEM((STATES, 128), wide),
            pltpu.VMEM((4, 64, D), low),
            pltpu.VMEM((4, STATES, 128), low),
            pltpu.VMEM((4, LINE, 64, 384), low),
            pltpu.VMEM((64, D), wide),
            pltpu.VMEM((5, 64, D), wide),
            pltpu.VMEM((4, 2, 3, 4, 32, D), low),
            pltpu.VMEM((4, 8, 32, D), low),
            pltpu.VMEM((8, 384, D), low),
            pltpu.VMEM((4, 384, D), low),
            pltpu.VMEM((4, 192, D), low),
            pltpu.VMEM((2, 192, D), low),
            pltpu.VMEM((384, D), wide),
            pltpu.SemaphoreType.DMA((2, 4, LINE - 1)),
            pltpu.SemaphoreType.DMA((2, 4, LINE)),
            pltpu.SemaphoreType.DMA((5,)),
            pltpu.SemaphoreType.DMA((2,)),
            pltpu.SemaphoreType.DMA((10,)),
            pltpu.SemaphoreType.DMA((10,)),
            pltpu.SemaphoreType.DMA((2, 2)),
            pltpu.SemaphoreType.DMA((2,)),
            pltpu.SemaphoreType.DMA((2,)),
            pltpu.VMEM((4, 64, D), low),
            pltpu.VMEM((2, 64, D), low),
            pltpu.SemaphoreType.DMA((10,)),
            pltpu.SemaphoreType.DMA((10,)),
        ],
        compiler_params=pltpu.CompilerParams(
            collective_id=2, has_side_effects=True, vmem_limit_bytes=63 * 1024 * 1024
        ),
        cost_estimate=pl.CostEstimate(flops=40000000000, bytes_accessed=40000000, transcendentals=0),
        name="backward_chain",
    )(
        scal, qkv, d_o, lse_tok, qkvst, lse_st, state_rows, begin, cots, back, kept, vecs, bias,
        extra, hidden, rows_all, state_low, w_qkv, os_rows,
    )


def plane_place():
    place, half, rank = line_place()
    side = lax.axis_index("dp")
    return side, place, half, rank


def plane_index(side, place):
    return 4 * side + place


def row_halves(buf, rows):
    size = rows // 2
    return lambda owner, part: buf.at[owner, pl.ds(part * size, size), :]


def plane_gather(view, send_sem, recv_sem):
    side, place, half, rank = plane_place()
    across, beside = 1 - side, lax.rem(place + 2, 4)
    core = place + 1 - 2 * half
    me = plane_index(side, place)
    at_x, at_y = plane_index(across, place), plane_index(side, beside)
    at_d = plane_index(across, beside)
    to_x, to_y, to_c = {"dp": across}, {"seq": beside}, {"seq": core}

    def piece(owner, part, slot, target):
        one = view(owner, part)
        return pltpu.make_async_remote_copy(
            src_ref=one,
            dst_ref=one,
            send_sem=send_sem.at[slot],
            recv_sem=recv_sem.at[owner, part],
            device_id=target,
            device_id_type=MESH_ID,
        )

    own = [
        piece(me, 0, 0, to_x), piece(me, 1, 1, to_y), piece(me, 1, 2, to_x), piece(me, 0, 3, to_y),
        piece(me, 0, 4, to_c), piece(me, 1, 5, to_c),
    ]
    on_x0, on_y1 = piece(at_x, 0, 6, to_y), piece(at_y, 1, 7, to_x)
    came = [
        (piece(owner, part, 0, to_c), piece(owner, part, slot, to_c))
        for owner, part, slot in (
            (at_x, 0, 8), (at_y, 1, 9), (at_x, 1, 10), (at_y, 0, 11), (at_d, 0, 12), (at_d, 1, 13)
        )
    ]
    core_came = [
        piece(owner, part, 0, to_c)
        for owner in (
            plane_index(side, core),
            plane_index(across, core),
            plane_index(side, lax.rem(core + 2, 4)),
            plane_index(across, lax.rem(core + 2, 4)),
        )
        for part in (0, 1)
    ]
    yield
    for one in own:
        one.start()
    yield
    came[0][0].wait_recv()
    on_x0.start()
    came[1][0].wait_recv()
    on_y1.start()
    came[0][1].start()
    came[1][1].start()
    yield
    for index in (2, 3):
        came[index][0].wait_recv()
        came[index][1].start()
    yield
    for index in (4, 5):
        came[index][0].wait_recv()
        came[index][1].start()
    yield
    for one in core_came:
        one.wait_recv()
    for one in own + [on_x0, on_y1] + [two for _, two in came]:
        one.wait_send()


def run_all(*steps):
    waiting = list(steps)
    while waiting:
        for one in list(waiting):
            try:
                next(one)
            except StopIteration:
                waiting.remove(one)


def plane_scatter(part, core_got, near_got, far_got, total, rows, send_sem, recv_sem):
    side, place, half, rank = plane_place()
    across, beside = 1 - side, lax.rem(place + 2, 4)
    core = place + 1 - 2 * half
    me = plane_index(side, place)
    at_x, at_y = plane_index(across, place), plane_index(side, beside)
    at_d = plane_index(across, beside)
    size = rows // 2
    halves = (pl.ds(0, size), pl.ds(size, size))

    def moved(source, target_ref, slot, target):
        return pltpu.make_async_remote_copy(
            src_ref=source,
            dst_ref=target_ref,
            send_sem=send_sem.at[slot],
            recv_sem=recv_sem.at[slot],
            device_id=target,
            device_id_type=MESH_ID,
        )

    order = (at_d, at_x, at_y, me)
    swapped = (
        plane_index(across, lax.rem(core + 2, 4)),
        plane_index(across, core),
        plane_index(side, lax.rem(core + 2, 4)),
        plane_index(side, core),
    )
    def add_into(owner, view, other):
        part[owner, view, :] = to_low(
            part[owner, view, :].astype(jnp.float32) + other.astype(jnp.float32)
        )

    near = [
        moved(part.at[at_d, halves[0], :], near_got.at[0], 4, {"dp": across}),
        moved(part.at[at_d, halves[1], :], near_got.at[1], 5, {"seq": beside}),
        moved(part.at[at_x, halves[0], :], near_got.at[2], 6, {"dp": across}),
        moved(part.at[at_y, halves[1], :], near_got.at[3], 7, {"seq": beside}),
    ]
    first = [
        moved(part.at[owner], core_got.at[slot], slot, {"seq": core})
        for slot, owner in enumerate(swapped)
    ]
    far = [
        moved(part.at[at_y, halves[0], :], far_got.at[0], 8, {"seq": beside}),
        moved(part.at[at_x, halves[1], :], far_got.at[1], 9, {"dp": across}),
    ]
    yield
    for one in first:
        one.start()
    for slot, owner in enumerate(order):
        first[slot].wait_recv()
        for view in halves:
            add_into(owner, view, core_got[slot, view, :])
        if slot == 0:
            near[0].start()
            near[1].start()
        if slot == 1:
            near[2].start()
        if slot == 2:
            near[3].start()
    yield
    near[0].wait_recv()
    add_into(at_y, halves[0], near_got[0])
    far[0].start()
    near[1].wait_recv()
    add_into(at_x, halves[1], near_got[1])
    far[1].start()
    yield
    near[2].wait_recv()
    add_into(me, halves[0], near_got[2])
    near[3].wait_recv()
    add_into(me, halves[1], near_got[3])
    yield
    for slot, view in enumerate(halves):
        far[slot].wait_recv()
        total[view, :] = part[me, view, :].astype(jnp.float32) + far_got[slot].astype(jnp.float32)
    for one in first + near + far:
        one.wait_send()


def group_peers():
    place, half, rank = line_place()
    here = 4 * place + rank
    peers = []
    for step in range(1, 16):
        other = lax.rem(here + step, 16)
        peers.append((other, other // 4, lax.rem(other, 4)))
    return here, peers


def greet(peers):
    side = lax.axis_index("dp")
    barrier = pltpu.get_barrier_semaphore()
    for _, seq_to, rank_to in peers:
        pl.semaphore_signal(
            barrier, inc=1, device_id={"seq": seq_to, "tensor": rank_to}, device_id_type=MESH_ID
        )
    pl.semaphore_signal(barrier, inc=1, device_id={"dp": 1 - side}, device_id_type=MESH_ID)
    pl.semaphore_wait(barrier, len(peers) + 1)


def middle_kernel(
    mixed, tokens, kept, spread, cot_hbm, vecs,
    hidden, d_hidden, d_line, sums, extra, ff_grads,
    mixed_rows, mid_all, gl_all, dpre_all, work, core_got, near_got, far_got, total, d_rows,
    d_low, w_out, up, down, cot_all,
    send_sem, recv_sem, ring_send, ring_recv, sum_send, sum_recv, back_send, back_recv, local_sem,
):
    low, wide = jnp.bfloat16, jnp.float32
    side, place, half, rank = plane_place()
    mine = place // 2
    head = 2 * rank + half
    across, beside = 1 - side, lax.rem(place + 2, 4)
    core = place + 1 - 2 * half
    core_beside = lax.rem(core + 2, 4)
    me = plane_index(side, place)
    at_x, at_y = plane_index(across, place), plane_index(side, beside)
    at_d = plane_index(across, beside)
    me_c, x_c = plane_index(side, core), plane_index(across, core)
    y_c, d_c = plane_index(side, core_beside), plane_index(across, core_beside)
    to_x, to_y, to_c = {"dp": across}, {"seq": beside}, {"seq": core}
    here, peers = group_peers()
    fetch_pieces(kept, 48, 32, w_out, local_sem.at[0])
    ff_own = up.shape[1]
    first = spread.shape[1] - 2 * ff_own
    loads = [
        pltpu.make_async_copy(spread.at[:, pl.ds(first, ff_own), :], up, local_sem.at[1]),
        pltpu.make_async_copy(spread.at[:, pl.ds(first + ff_own, ff_own), :], down, local_sem.at[2]),
        pltpu.make_async_copy(cot_hbm, cot_all, local_sem.at[3]),
    ]
    for one in loads:
        one.start()
    greet(peers)

    def rows_copy(slot, sender, seq_from, rank_from, seq_to, rank_to):
        return pltpu.make_async_remote_copy(
            src_ref=mixed.at[seq_to, span(rank_to, 128), :],
            dst_ref=mixed_rows.at[
                seq_from // 2, :, span(2 * rank_from + lax.rem(seq_from, 2), 128)
            ],
            send_sem=send_sem.at[slot],
            recv_sem=recv_sem.at[sender],
            device_id={"seq": seq_to, "tensor": rank_to},
            device_id_type=MESH_ID,
        )

    for slot, (_, seq_to, rank_to) in enumerate(peers):
        rows_copy(slot, here, place, rank, seq_to, rank_to).start()
    mixed_rows[mine, :, span(head, 128)] = mixed[place, span(rank, 128), :]
    fetched(w_out, local_sem.at[0])
    for slot, (other, seq_to, rank_to) in enumerate(peers):
        rows_copy(slot, other, seq_to, rank_to, seq_to, rank_to).wait_recv()
    gain = vecs[2:3, :]

    def project(which, _):
        added = dot_nn(mixed_rows[which], w_out[...].reshape(D, D)) + tokens[which].astype(wide)
        hidden[which] = added
        centered, scale = norm_parts(added)
        mid_all[me, span(which, 128), :] = to_low(centered * scale * gain)
        return 0

    lax.fori_loop(0, 2, project, 0)

    def piece(owner, part, slot, target):
        view = mid_all.at[owner, pl.ds(part * 128, 128), :]
        return pltpu.make_async_remote_copy(
            src_ref=view,
            dst_ref=view,
            send_sem=ring_send.at[slot],
            recv_sem=ring_recv.at[owner, part],
            device_id=target,
            device_id_type=MESH_ID,
        )

    own = [
        piece(me, 0, 0, to_x), piece(me, 1, 1, to_y), piece(me, 1, 2, to_x), piece(me, 0, 3, to_y),
        piece(me, 0, 4, to_c), piece(me, 1, 5, to_c),
    ]
    on_x0, on_y1 = piece(at_x, 0, 6, to_y), piece(at_y, 1, 7, to_x)
    to_core = [
        piece(at_x, 0, 8, to_c), piece(at_y, 1, 9, to_c), piece(at_x, 1, 10, to_c),
        piece(at_y, 0, 11, to_c), piece(at_d, 0, 12, to_c), piece(at_d, 1, 13, to_c),
    ]
    wait_of = {
        (name, part): piece(owner, part, 0, to_c)
        for name, owner in (
            ("x", at_x), ("y", at_y), ("d", at_d), ("mc", me_c), ("xc", x_c), ("yc", y_c), ("dc", d_c)
        )
        for part in (0, 1)
    }

    def moved(source, target_ref, slot, target):
        return pltpu.make_async_remote_copy(
            src_ref=source,
            dst_ref=target_ref,
            send_sem=sum_send.at[slot],
            recv_sem=sum_recv.at[slot],
            device_id=target,
            device_id_type=MESH_ID,
        )

    views = (pl.ds(0, 128), pl.ds(128, 128))
    swap = [
        moved(work.at[owner], core_got.at[slot], slot, to_c)
        for slot, owner in enumerate((d_c, x_c, y_c, me_c))
    ]
    near = [
        moved(work.at[at_d, views[0], :], near_got.at[0], 4, to_x),
        moved(work.at[at_d, views[1], :], near_got.at[1], 5, to_y),
        moved(work.at[at_x, views[0], :], near_got.at[2], 6, to_x),
        moved(work.at[at_y, views[1], :], near_got.at[3], 7, to_y),
    ]
    far = [
        moved(work.at[at_y, views[0], :], far_got.at[0], 8, to_y),
        moved(work.at[at_x, views[1], :], far_got.at[1], 9, to_x),
    ]

    def add_into(owner, view, other):
        work[owner, view, :] = to_low(work[owner, view, :].astype(wide) + other.astype(wide))

    def add_core(slot, owner):
        swap[slot].wait_recv()
        for view in views:
            add_into(owner, view, core_got[slot, view, :])

    for one in own:
        one.start()
    loads[0].wait()
    loads[1].wait()
    loads[2].wait()
    order = (
        (me, 0), (me, 1), (me_c, 0), (me_c, 1), (at_x, 0), (at_y, 1), (x_c, 0), (y_c, 1),
        (at_x, 1), (at_y, 0), (x_c, 1), (y_c, 0), (at_d, 0), (at_d, 1), (d_c, 0), (d_c, 1),
    )

    def before_four():
        swap[3].start()
        wait_of["x", 0].wait_recv()
        on_x0.start()
        to_core[0].start()
        wait_of["y", 1].wait_recv()
        on_y1.start()
        to_core[1].start()

    def before_eight():
        wait_of["x", 1].wait_recv()
        to_core[2].start()
        wait_of["y", 0].wait_recv()
        to_core[3].start()

    def before_eleven():
        swap[1].start()
        wait_of["yc", 0].wait_recv()

    def before_twelve():
        swap[2].start()
        wait_of["d", 0].wait_recv()
        to_core[4].start()
        wait_of["d", 1].wait_recv()
        to_core[5].start()

    def before_fourteen():
        add_core(1, at_x)
        near[2].start()
        add_core(2, at_y)
        near[3].start()
        wait_of["dc", 0].wait_recv()

    ahead = {
        2: wait_of["mc", 0].wait_recv,
        3: wait_of["mc", 1].wait_recv,
        4: before_four,
        6: wait_of["xc", 0].wait_recv,
        7: wait_of["yc", 1].wait_recv,
        8: before_eight,
        10: wait_of["xc", 1].wait_recv,
        11: before_eleven,
        12: before_twelve,
        14: before_fourteen,
        15: wait_of["dc", 1].wait_recv,
    }

    def one_chunk(turn, _):
        for value, action in ahead.items():

            @pl.when(turn == value)
            def _():
                action()

        owner, which = order[15]
        for index in range(15):
            owner = jnp.where(turn == index, order[index][0], owner)
            which = jnp.where(turn == index, order[index][1], which)
        up_rows = up[...].reshape(4 * ff_own, D)
        down_rows = down[...].reshape(4 * ff_own, D)
        rows = span(which, 128)
        pre = dot_nt(mid_all[owner, rows, :], up_rows)
        square = pre * pre
        bend = jnp.tanh(GELU_SCALE * (pre + 0.044715 * (pre * square)))
        gl_all[owner, rows, :] = to_low(0.5 * pre * (1.0 + bend))
        slope = 0.5 * (1.0 + bend) + 0.5 * pre * (1.0 - bend * bend) * (
            GELU_SCALE * (1.0 + 3.0 * 0.044715 * square)
        )
        grad = to_low(dot_nt(cot_all[owner, rows, :], down_rows) * slope)
        dpre_all[owner, rows, :] = grad
        work[owner, rows, :] = to_low(dot_nn(grad, up_rows))
        return 0

    lax.fori_loop(0, 16, one_chunk, 0)
    swap[0].start()
    add_core(0, at_d)
    near[0].start()
    near[1].start()
    add_core(3, me)

    def grads(index, _):
        quarter, kind = index // 2, lax.rem(index, 2)
        columns = span(quarter, 128)

        @pl.when(kind == 0)
        def _():
            def add(owner, acc):
                return acc + dot_tn(dpre_all[owner, :, columns], mid_all[owner])

            ff_grads[quarter, 0] = to_low(lax.fori_loop(0, 8, add, jnp.zeros((128, D), wide)))

        @pl.when(kind == 1)
        def _():
            def add(owner, acc):
                return acc + dot_tn(gl_all[owner, :, columns], cot_all[owner])

            ff_grads[quarter, 1] = to_low(lax.fori_loop(0, 8, add, jnp.zeros((128, D), wide)))

        return 0

    lax.fori_loop(0, NEAR_GRADS, grads, 0)
    near[0].wait_recv()
    add_into(at_y, views[0], near_got[0])
    far[0].start()
    near[1].wait_recv()
    add_into(at_x, views[1], near_got[1])
    far[1].start()
    near[2].wait_recv()
    add_into(me, views[0], near_got[2])
    near[3].wait_recv()
    add_into(me, views[1], near_got[3])

    def outward(owner, _):
        down_rows = down[...].reshape(4 * ff_own, D)
        for which in range(2):
            rows = pl.ds(128 * which, 128)
            extra[owner, rows, :] = to_low(dot_nn(gl_all[owner, rows, :], down_rows))
        return 0

    lax.fori_loop(0, 8, outward, 0)
    lax.fori_loop(NEAR_GRADS, FAR_GRADS, grads, 0)
    for slot, view in enumerate(views):
        far[slot].wait_recv()
        total[view, :] = work[me, view, :].astype(wide) + far_got[slot].astype(wide)
    sums[...] = jnp.zeros_like(sums)

    def back(which, _):
        rows = span(which, 128)
        grad = total[rows, :]
        centered, scale = norm_parts(hidden[which])
        normed = centered * scale
        sums[0:1, :] += jnp.sum(grad * normed, axis=0, keepdims=True)
        lifted = grad * gain
        row_grad = cot_all[me, rows, :].astype(wide) + scale * (
            lifted
            - jnp.mean(lifted, axis=-1, keepdims=True)
            - normed * jnp.mean(lifted * normed, axis=-1, keepdims=True)
        )
        d_hidden[which] = row_grad
        d_low[which] = to_low(row_grad)
        d_rows[which] = to_low(dot_nt(to_low(row_grad), w_out[...].reshape(D, D)))
        return 0

    lax.fori_loop(0, 2, back, 0)

    def line_copy(slot, sender, seq_from, rank_from, seq_to, rank_to):
        return pltpu.make_async_remote_copy(
            src_ref=d_rows.at[seq_to // 2, :, span(2 * rank_to + lax.rem(seq_to, 2), 128)],
            dst_ref=d_line.at[seq_from, span(rank_from, 128), :],
            send_sem=back_send.at[slot],
            recv_sem=back_recv.at[sender],
            device_id={"seq": seq_to, "tensor": rank_to},
            device_id_type=MESH_ID,
        )

    for slot, (_, seq_to, rank_to) in enumerate(peers):
        line_copy(slot, here, place, rank, seq_to, rank_to).start()
    d_line[place, span(rank, 128), :] = d_rows[mine, :, span(head, 128)]
    lax.fori_loop(FAR_GRADS, 8, grads, 0)
    for index in range(LINE):
        columns = pl.ds(128 * index, 128)
        part = dot_tn(mixed_rows[0, :, columns], d_low[0]) + dot_tn(
            mixed_rows[1, :, columns], d_low[1]
        )
        part = to_low(part)
        for block in range(4):
            extra[
                4 * (index % 2) + block, 256 + 32 * (index // 2) : 288 + 32 * (index // 2), :
            ] = part[32 * block : 32 * block + 32, :]
    for slot, (other, seq_to, rank_to) in enumerate(peers):
        line_copy(slot, other, seq_to, rank_to, seq_to, rank_to).wait_recv()
    for slot, (_, seq_to, rank_to) in enumerate(peers):
        rows_copy(slot, here, place, rank, seq_to, rank_to).wait_send()
        line_copy(slot, here, place, rank, seq_to, rank_to).wait_send()
    for one in own + [on_x0, on_y1] + to_core + swap + near + far:
        one.wait_send()


GELU_SCALE = 0.7978845608028654
NEAR_GRADS = 3
FAR_GRADS = 4


def middle(mixed, tokens, kept, spread, cot_all, vecs):
    low, wide = jnp.bfloat16, jnp.float32
    ff_own = (spread.shape[1] - SPREAD_FIRST) // 2
    shapes = (
        ((2, 128, D), wide),
        ((2, 128, D), wide),
        ((4, BLOCK, 128), low),
        ((8, D), wide),
        ((8, 384, D), low),
        ((4, 2, ff_own, D), low),
    )
    dma = pltpu.SemaphoreType.DMA
    return pl.pallas_call(
        middle_kernel,
        out_shape=[jax.ShapeDtypeStruct(*one) for one in shapes],
        in_specs=vmem_specs(2) + any_specs(3) + vmem_specs(1),
        out_specs=vmem_specs(6),
        scratch_shapes=[
            pltpu.VMEM((2, 128, D), low),
            pltpu.VMEM((8, 256, D), low),
            pltpu.VMEM((8, 256, 4 * ff_own), low),
            pltpu.VMEM((8, 256, 4 * ff_own), low),
            pltpu.VMEM((8, 256, D), low),
            pltpu.VMEM((4, 256, D), low),
            pltpu.VMEM((4, 128, D), low),
            pltpu.VMEM((2, 128, D), low),
            pltpu.VMEM((256, D), wide),
            pltpu.VMEM((2, 128, D), low),
            pltpu.VMEM((2, 128, D), low),
            pltpu.VMEM((4, 8, 32, D), low),
            pltpu.VMEM((4, ff_own, D), low),
            pltpu.VMEM((4, ff_own, D), low),
            pltpu.VMEM((8, 256, D), low),
            dma((15,)), dma((16,)), dma((14,)), dma((8, 2)), dma((10,)), dma((10,)), dma((15,)),
            dma((16,)), dma((4,)),
        ],
        compiler_params=pltpu.CompilerParams(
            collective_id=3, has_side_effects=True, vmem_limit_bytes=VMEM_LIMIT
        ),
        cost_estimate=pl.CostEstimate(
            flops=60000000000, bytes_accessed=60000000, transcendentals=0
        ),
        name="middle",
    )(mixed, tokens, kept, spread, cot_all, vecs)


SPREAD_FIRST = 0


WIDE = 2048


def opening_kernel(
    tokens, w_query, w_key, w_value, w_sout, w_out, begin, vecs, marks_own,
    rows_all, qkv, kept, table, marks, w_qkv,
    begin_rows, bias_rows, stage, send_sem, core_sem, recv_sem, piece_send, piece_recv, ring_send, ring_recv,
    mark_send, mark_recv, local_sem,
):
    side, place, half, rank = plane_place()
    mine = place // 2
    core = place + 1 - 2 * half
    other = lax.rem(place + 2, 4)
    me = plane_index(side, place)
    extra = 80
    fetch_columns((w_query, w_key, w_value), w_qkv, local_sem.at[0])
    loads = [
        pltpu.make_async_copy(
            w_sout.at[span(me, 32), :], kept.at[me, pl.ds(80 * rank, 32), :], local_sem.at[1]
        ),
        pltpu.make_async_copy(
            w_out.at[span(me, 32), :], kept.at[me, pl.ds(80 * rank + 48, 32), :], local_sem.at[3]
        ),
        pltpu.make_async_copy(begin.at[span(me, 16), :], begin_rows, local_sem.at[2]),
    ]
    for one in loads:
        one.start()
    barrier = pltpu.get_barrier_semaphore()
    greeted = [{"tensor": lax.rem(rank + step, 4)} for step in (1, 2, 3)]
    seats = [lax.rem(place + step, 4) for step in (1, 2, 3)]
    greeted += [{"seq": one} for one in seats] + [{"dp": 1 - side}]
    for target in greeted:
        pl.semaphore_signal(barrier, inc=1, device_id=target, device_id_type=MESH_ID)
    gain = vecs[3:4, :]

    def normed(which):
        centered, scale = norm_parts(tokens[which].astype(jnp.float32))
        return to_low(centered * scale * gain)

    def moved(block_id, origin, sem, target):
        view = rows_all.at[block_id, span(origin, 128), :]
        return pltpu.make_async_remote_copy(
            src_ref=view,
            dst_ref=view,
            send_sem=sem,
            recv_sem=recv_sem.at[block_id, origin],
            device_id=target,
            device_id_type=MESH_ID,
        )

    stage[...] = normed(1 - mine)
    marks[place] = marks_own[...]
    pl.semaphore_wait(barrier, 7)
    aside = pltpu.make_async_remote_copy(
        src_ref=stage,
        dst_ref=rows_all.at[place, span(rank, 128), :],
        send_sem=send_sem.at[0, 0, 3],
        recv_sem=recv_sem.at[place, rank],
        device_id={"seq": other},
        device_id_type=MESH_ID,
    )
    aside.start()

    def mark_move(slot, origin, target):
        return pltpu.make_async_remote_copy(
            src_ref=marks.at[origin],
            dst_ref=marks.at[origin],
            send_sem=mark_send.at[slot],
            recv_sem=mark_recv.at[origin],
            device_id={"seq": target},
            device_id_type=MESH_ID,
        )

    def piece_move(slot, origin, target):
        view = kept.at[me, span(origin, extra), :]
        return pltpu.make_async_remote_copy(
            src_ref=view,
            dst_ref=view,
            send_sem=piece_send.at[slot],
            recv_sem=piece_recv.at[origin],
            device_id=target,
            device_id_type=MESH_ID,
        )

    for one in loads:
        one.wait()
    kept[me, pl.ds(pl.multiple_of(80 * rank + 32, 16), 16), :] = to_low(begin_rows[...])
    for slot in range(3):
        piece_move(slot, rank, greeted[slot]).start()
    for slot, target in enumerate(seats):
        mark_move(slot, place, target).start()
    rows_all[place, span(rank, 128), :] = normed(mine)
    right, left = {"tensor": lax.rem(rank + 1, 4)}, {"tensor": lax.rem(rank + 3, 4)}
    blocks = (place, other)

    def pass_on(which, distance):
        block_id = blocks[which]

        @pl.when((rank < 3) & (rank >= distance))
        def _():
            moved(block_id, jnp.maximum(rank - distance, 0), send_sem.at[which, distance, 0], right).start()

        @pl.when((rank > 0) & (rank + distance <= 3))
        def _():
            moved(block_id, jnp.minimum(rank + distance, 3), send_sem.at[which, distance, 1], left).start()

    def pass_done(which, distance):
        block_id = blocks[which]

        @pl.when((rank < 3) & (rank >= distance))
        def _():
            moved(block_id, jnp.maximum(rank - distance, 0), send_sem.at[which, distance, 0], right).wait_send()

        @pl.when((rank > 0) & (rank + distance <= 3))
        def _():
            moved(block_id, jnp.minimum(rank + distance, 3), send_sem.at[which, distance, 1], left).wait_send()

    def project(block_id, origin):
        view = span(origin, 128)
        qkv[block_id, view, :] = to_low(dot_nn(rows_all[block_id, view, :], w_qkv[...]))

    def rows_steps():
        pass_on(0, 0)
        fetched(w_qkv, local_sem.at[0])
        moved(place, rank, core_sem.at[0, rank], {"seq": core}).start()
        project(place, rank)
        moved(other, rank, send_sem.at[0, 0, 3], {"seq": other}).wait_recv()
        pass_on(1, 0)
        moved(other, rank, core_sem.at[1, rank], {"seq": core}).start()
        project(other, rank)
        yield
        for distance in (1, 2, 3):
            for which in (0, 1):
                block_id = blocks[which]
                for way, ok, origin in (
                    (0, rank >= distance, jnp.maximum(rank - distance, 0)),
                    (1, rank + distance <= 3, jnp.minimum(rank + distance, 3)),
                ):

                    @pl.when(ok)
                    def _():
                        moved(block_id, origin, send_sem.at[which, distance, way], right).wait_recv()
                        if distance < 3:
                            if way == 0:

                                @pl.when(rank < 3)
                                def _():
                                    moved(
                                        block_id, origin, send_sem.at[which, distance, 0], right
                                    ).start()

                            else:

                                @pl.when(rank > 0)
                                def _():
                                    moved(
                                        block_id, origin, send_sem.at[which, distance, 1], left
                                    ).start()

                        moved(block_id, origin, core_sem.at[which, origin], {"seq": core}).start()
                        project(block_id, origin)

                yield
        for which, block_id in enumerate((core, lax.rem(core + 2, 4))):
            for origin in range(4):
                moved(block_id, origin, core_sem.at[which, origin], {"seq": core}).wait_recv()
                project(block_id, origin)
        for which in (0, 1):
            for distance in (0, 1, 2):
                pass_done(which, distance)
            for origin in range(4):
                moved(blocks[which], origin, core_sem.at[which, origin], {"seq": core}).wait_send()

    def piece_steps():
        for slot in range(3):
            piece_move(slot, lax.rem(rank + slot + 1, 4), greeted[slot]).wait_recv()
        for _ in plane_gather(row_halves(kept, 4 * extra), ring_send, ring_recv):
            yield
        for slot in range(3):
            piece_move(slot, rank, greeted[slot]).wait_send()

    def bias_steps():
        lane = lax.broadcasted_iota(jnp.int32, (8, WIDE), 1)
        bucket_ids = bucket_of(jnp.where(lane >= WIDE - BLOCK, lane - WIDE - BLOCK, lane - BLOCK))
        first = jnp.zeros((8, WIDE), jnp.float32)
        for bucket_id in range(BUCKETS):
            value = jnp.where(
                half == 0,
                vecs[4:5, bucket_id : bucket_id + 1],
                vecs[4:5, BUCKETS + bucket_id : BUCKETS + bucket_id + 1],
            )
            first = jnp.where(bucket_ids == bucket_id, value, first)
        row = lax.broadcasted_iota(jnp.int32, (8, WIDE), 0)
        for step in (1, 2, 4):
            first = jnp.where(row // step % 2 == 1, pltpu.roll(first, step, 1), first)
        bias_rows[...] = first
        yield

        def one(group, _):
            table[span(group, 8), :] = pltpu.roll(bias_rows[...], 8 * group, 1)[:, 0 : 2 * BLOCK]
            return 0

        for part in range(4):
            lax.fori_loop(16 * part, 16 * part + 16, one, 0)
            yield

    run_all(rows_steps(), piece_steps(), bias_steps())
    aside.wait_send()
    for slot, target in enumerate(seats):
        mark_move(slot, place, target).wait_send()
        mark_move(slot, target, target).wait_recv()


def opening(tokens, w_query, w_key, w_value, w_sout, w_out, begin, vecs, marks):
    low, wide = jnp.bfloat16, jnp.float32
    shapes = (
        ((4, BLOCK, D), low),
        ((4, BLOCK, 384), low),
        ((8, 4 * 80, D), low),
        ((BLOCK, 2 * BLOCK), wide),
        ((4, 8, 128), jnp.int32),
        ((D, 384), low),
    )
    dma = pltpu.SemaphoreType.DMA
    outs = pl.pallas_call(
        opening_kernel,
        out_shape=[jax.ShapeDtypeStruct(*one) for one in shapes],
        in_specs=vmem_specs(1)
        + any_specs(6)
        + vmem_specs(2),
        out_specs=vmem_specs(6),
        scratch_shapes=[
            pltpu.VMEM((16, D), wide),
            pltpu.VMEM((8, WIDE), wide),
            pltpu.VMEM((128, D), low),
            dma((2, 4, 4)),
            dma((2, 4)),
            dma((4, 4)),
            dma((3,)),
            dma((4,)),
            dma((14,)),
            dma((8, 2)),
            dma((3,)),
            dma((4,)),
            dma((4,)),
        ],
        compiler_params=pltpu.CompilerParams(
            collective_id=5, has_side_effects=True, vmem_limit_bytes=VMEM_LIMIT
        ),
        cost_estimate=pl.CostEstimate(
            flops=30000000000, bytes_accessed=30000000, transcendentals=0
        ),
        name="opening",
    )(tokens, w_query, w_key, w_value, w_sout, w_out, begin, vecs, marks)
    rows_all, qkv, kept, table, marks, w_qkv = outs
    return rows_all, qkv, kept.reshape(8, 4, 80, D), table, marks, w_qkv


def pair_sum(part, near_got, far_got, result, rows, send_sem, recv_sem):
    side, place, half, rank = plane_place()
    mine = place // 2
    across, beside = 1 - side, 1 - mine
    me = 2 * side + mine
    at_x, at_y, at_d = 2 * across + mine, 2 * side + beside, 2 * across + beside
    to_x, to_y = {"dp": across}, {"seq": lax.rem(place + 2, 4)}
    size = rows // 2
    views = (pl.ds(0, size), pl.ds(size, size))

    def moved(source, target_ref, slot, target):
        return pltpu.make_async_remote_copy(
            src_ref=source,
            dst_ref=target_ref,
            send_sem=send_sem.at[slot],
            recv_sem=recv_sem.at[slot],
            device_id=target,
            device_id_type=MESH_ID,
        )

    def add_into(owner, view, other):
        part[owner, view, :] = to_low(
            part[owner, view, :].astype(jnp.float32) + other.astype(jnp.float32)
        )

    near = [
        moved(part.at[at_d, views[0], :], near_got.at[0], 0, to_x),
        moved(part.at[at_d, views[1], :], near_got.at[1], 1, to_y),
        moved(part.at[at_x, views[0], :], near_got.at[2], 2, to_x),
        moved(part.at[at_y, views[1], :], near_got.at[3], 3, to_y),
    ]
    for one in near:
        one.start()
    yield
    near[0].wait_recv()
    add_into(at_y, views[0], near_got[0])
    far = [
        moved(part.at[at_y, views[0], :], far_got.at[0], 4, to_y),
        moved(part.at[at_x, views[1], :], far_got.at[1], 5, to_x),
    ]
    far[0].start()
    near[1].wait_recv()
    add_into(at_x, views[1], near_got[1])
    far[1].start()
    yield
    near[2].wait_recv()
    add_into(me, views[0], near_got[2])
    near[3].wait_recv()
    add_into(me, views[1], near_got[3])
    for slot, view in enumerate(views):
        far[slot].wait_recv()
        result[me, view, :] = to_low(
            part[me, view, :].astype(jnp.float32) + far_got[slot].astype(jnp.float32)
        )

    def given(owner, which, slot, target):
        view = result.at[owner, views[which], :]
        return moved(view, view, slot, target)

    own = [
        given(me, 0, 6, to_x),
        given(me, 1, 7, to_y),
        given(me, 1, 8, to_x),
        given(me, 0, 9, to_y),
    ]
    for one in own:
        one.start()
    yield
    given(at_x, 0, 6, to_x).wait_recv()
    last = [given(at_x, 0, 10, to_y), given(at_y, 1, 11, to_x)]
    last[0].start()
    given(at_y, 1, 7, to_y).wait_recv()
    last[1].start()
    yield
    given(at_x, 1, 8, to_x).wait_recv()
    given(at_y, 0, 9, to_y).wait_recv()
    given(at_d, 0, 10, to_y).wait_recv()
    given(at_d, 1, 11, to_x).wait_recv()
    for one in near + far + own + last:
        one.wait_send()


PAIR_ROWS = 640


def closing_kernel(
    partial, pair_grads, tokens, d_hidden, vecs, d_start, mlp_sums, state_sums, out_part,
    sout_part,
    inputs_grad, pair_out, sout_out, small_out,
    sums, got, final, cross, cross_got,
    pair_part, pair_near, pair_far,
    z_part, z_got,
    small_z, small_p,
    line_send, line_recv, way_send, way_recv, pair_send, pair_recv, core_sem,
    zs_send, zs_recv, gather_send, gather_recv, small_send, small_recv, local_sem,
):
    loads = [
        pltpu.make_async_copy(source, target, local_sem.at[slot])
        for slot, (source, target) in enumerate(
            (
                (partial, sums),
            )
        )
    ]
    for one in loads:
        one.start()
    side, place, half, rank = plane_place()
    mine = place // 2
    core = place + 1 - 2 * half
    other = lax.rem(place + 2, 4)
    me = plane_index(side, place)
    ranks = [lax.rem(rank + step, 4) for step in (1, 2, 3)]
    spots_of = [lax.rem(me + step, 8) for step in range(1, 8)]
    barrier = pltpu.get_barrier_semaphore()
    for target in ranks:
        pl.semaphore_signal(barrier, inc=1, device_id={"tensor": target}, device_id_type=MESH_ID)
    for target in spots_of:
        pl.semaphore_signal(
            barrier,
            inc=1,
            device_id={"dp": target // 4, "seq": lax.rem(target, 4)},
            device_id_type=MESH_ID,
        )
    gain = vecs[3:4, :]
    right, left = {"tensor": lax.rem(rank + 1, 4)}, {"tensor": lax.rem(rank + 3, 4)}

    def moved(source, target_ref, send, recv, target):
        return pltpu.make_async_remote_copy(
            src_ref=source,
            dst_ref=target_ref,
            send_sem=send,
            recv_sem=recv,
            device_id=target,
            device_id_type=MESH_ID,
        )

    def crossing():
        return moved(cross, cross_got, line_send.at[0], line_recv.at[0], {"seq": other})

    near = rank // 2
    at_end = (rank == 0) | (rank == 3)

    def hop(way, which, target):
        return moved(
            sums.at[which, target],
            got.at[way, which, target],
            way_send.at[which, target],
            way_recv.at[way, which, target],
            {"tensor": lax.rem(rank + 5 - 2 * way, 4)},
        )

    def target_of(way, distance):
        return (1 - way) * (3 - distance) + way * distance

    def pass_first(which):
        @pl.when(at_end)
        def _():
            for distance in range(3):
                hop(near, which, target_of(near, distance)).start()

    def pass_on(way, which, distance):
        @pl.when(jnp.logical_not(at_end))
        def _():
            target = target_of(way, distance)
            hop(way, which, target).wait_recv()
            sums[which, target] = to_low(
                sums[which, target].astype(jnp.float32)
                + got[way, which, target].astype(jnp.float32)
            )
            hop(way, which, target).start()

    def finish(which):
        final[which] = sums[which, rank].astype(jnp.float32)

        @pl.when(rank > 0)
        def _():
            hop(0, which, rank).wait_recv()
            final[which] += got[0, which, rank].astype(jnp.float32)

        @pl.when(rank < 3)
        def _():
            hop(1, which, rank).wait_recv()
            final[which] += got[1, which, rank].astype(jnp.float32)

    def small_over_z(slot, sender, target):
        return moved(
            small_z.at[sender], small_z.at[sender], small_send.at[slot], small_recv.at[sender],
            {"tensor": target},
        )

    def small_over_plane(slot, sender, target):
        return moved(
            small_p.at[sender], small_p.at[sender], small_send.at[3 + slot],
            small_recv.at[4 + sender],
            {"dp": target // 4, "seq": lax.rem(target, 4)},
        )

    def line_steps():
        loads[0].wait()
        for which in (0, 1):
            pass_first(which)
        yield
        for which in (0, 1):
            pass_on(near, which, 0)
            yield
            pass_on(near, which, 1)
            pass_on(1 - near, which, 0)
            yield
            finish(which)
            if which == 0:
                cross[...] = to_low(final[0])
                crossing().start()
            yield
        crossing().wait_recv()
        final[0] = cross_got[...].astype(jnp.float32)
        small_z[rank] = jnp.zeros((8, D), jnp.float32)
        for row, source in enumerate(
            (state_sums[1:2, :], mlp_sums[0:1, :], state_sums[0:1, :], state_sums[2:3, :])
        ):
            small_z[rank, row + 1 : row + 2, :] = source
        for which, row_set in ((1, mine), (0, 1 - mine)):
            grad = final[which]
            centered, scale = norm_parts(tokens[row_set].astype(jnp.float32))
            normed = centered * scale
            small_z[rank, 0:1, :] += jnp.sum(grad * normed, axis=0, keepdims=True)
            lifted = grad * gain
            inputs_grad[row_set] = d_hidden[row_set] + scale * (
                lifted
                - jnp.mean(lifted, axis=-1, keepdims=True)
                - normed * jnp.mean(lifted * normed, axis=-1, keepdims=True)
            )
        for slot, target in enumerate(ranks):
            small_over_z(slot, rank, target).start()
        crossing().wait_send()
        yield
        for slot, target in enumerate(ranks):
            small_over_z(slot, target, target).wait_recv()
        small_p[me] = small_z[0] + small_z[1] + small_z[2] + small_z[3]
        for slot, target in enumerate(spots_of):
            small_over_plane(slot, me, target).start()
        yield
        for slot, target in enumerate(spots_of):
            small_over_plane(slot, target, target).wait_recv()
        acc = small_p[0]
        for target in range(1, 8):
            acc = acc + small_p[target]
        small_out[...] = acc
        for slot, target in enumerate(ranks):
            small_over_z(slot, rank, target).wait_send()
        for slot, target in enumerate(spots_of):
            small_over_plane(slot, me, target).wait_send()
        for which in (0, 1):
            for target in range(4):

                @pl.when(rank != target)
                def _():
                    hop(0, which, target).wait_send()

    def pair_steps():
        for owner in range(3):
            pair_part[owner] = pair_grads[160 * owner : 160 * owner + 160, :]
        pair_part[3, 0:32, :] = pair_grads[480:512, :]
        pair_part[3, 32:96, :] = to_low(d_start[...])
        pair_part[3, 96:160, :] = jnp.zeros((64, D), jnp.bfloat16)
        for _ in pair_sum(
            pair_part, pair_near, pair_far, pair_out.at[half], 160, pair_send, pair_recv
        ):
            yield
        full = moved(
            pair_out.at[half], pair_out.at[half], core_sem.at[0], core_sem.at[1], {"seq": core}
        )
        full.start()
        yield
        moved(
            pair_out.at[1 - half], pair_out.at[1 - half], core_sem.at[0], core_sem.at[1],
            {"seq": core},
        ).wait_recv()
        full.wait_send()

    def sout_steps():
        z_part[:, 0:32, :] = sout_part[...].reshape(4, 32, D)
        z_part[:, 32:64, :] = out_part[...].reshape(4, 32, D)
        out = [
            moved(
                z_part.at[target], z_got.at[rank], zs_send.at[slot], zs_recv.at[rank],
                {"tensor": target},
            )
            for slot, target in enumerate(ranks)
        ]
        for one in out:
            one.start()
        z_got[rank] = z_part[rank]
        yield
        for slot, target in enumerate(ranks):
            moved(
                z_part.at[target], z_got.at[target], zs_send.at[slot], zs_recv.at[target],
                {"tensor": target},
            ).wait_recv()
        acc = z_got[0].astype(jnp.float32)
        for target in range(1, 4):
            acc = acc + z_got[target].astype(jnp.float32)
        sout_out[me] = to_low(acc)
        for _ in plane_gather(row_halves(sout_out, 64), gather_send, gather_recv):
            yield
        for one in out:
            one.wait_send()

    pl.semaphore_wait(barrier, 10)
    run_all(sout_steps(), pair_steps(), line_steps())


def closing(
    partial, pair_grads, tokens, d_hidden, vecs, d_start, mlp_sums, state_sums, out_part, sout_part,
):
    low, wide = jnp.bfloat16, jnp.float32
    shapes = (
        ((2, 128, D), wide),
        ((2, 4, PAIR_ROWS // 4, D), low),
        ((8, 64, D), low),
        ((8, D), wide),
    )
    dma = pltpu.SemaphoreType.DMA
    return pl.pallas_call(
        closing_kernel,
        out_shape=[jax.ShapeDtypeStruct(*one) for one in shapes],
        in_specs=any_specs(1)
        + vmem_specs(9),
        out_specs=vmem_specs(4),
        scratch_shapes=[
            pltpu.VMEM((2, 4, 128, D), low),
            pltpu.VMEM((2, 2, 4, 128, D), low),
            pltpu.VMEM((2, 128, D), wide),
            pltpu.VMEM((128, D), low),
            pltpu.VMEM((128, D), low),
            pltpu.VMEM((4, PAIR_ROWS // 4, D), low),
            pltpu.VMEM((4, PAIR_ROWS // 8, D), low),
            pltpu.VMEM((2, PAIR_ROWS // 8, D), low),
            pltpu.VMEM((4, 64, D), low),
            pltpu.VMEM((4, 64, D), low),
            pltpu.VMEM((4, 8, D), wide),
            pltpu.VMEM((8, 8, D), wide),
            dma((1,)), dma((1,)), dma((2, 4)), dma((2, 2, 4)), dma((12,)), dma((12,)), dma((2,)),
            dma((3,)), dma((4,)), dma((16,)), dma((8, 2)), dma((10,)),
            dma((12,)), dma((1,)),
        ],
        compiler_params=pltpu.CompilerParams(
            collective_id=6, has_side_effects=True, vmem_limit_bytes=VMEM_LIMIT
        ),
        cost_estimate=pl.CostEstimate(
            flops=30000000000, bytes_accessed=30000000, transcendentals=0
        ),
        name="closing",
    )(
        partial, pair_grads, tokens, d_hidden, vecs, d_start, mlp_sums, state_sums, out_part,
        sout_part,
    )


def finish_kernel(
    pair, pair_tail, two, ff,
    query, key, value, squery, out, sout, up, down, state,
):
    step = pl.program_id(0)
    wide = jnp.float32
    up[...] = ff[0, 0].astype(wide).T
    down[...] = ff[0, 1].astype(wide)
    sout[...] = two[0, 0:32].astype(wide)
    out[...] = two[0, 32:64].astype(wide)
    for which, target in enumerate((query, key, value, squery)):

        @pl.when(step // 2 == which)
        def _():
            target[...] = pair[0].astype(wide).T

    @pl.when(step == 0)
    def _():
        state[...] = pair_tail[...].reshape(128, D).astype(wide)


def finish_grads(pair, two, ff):
    wide = jnp.float32
    turned = [
        pl.BlockSpec((D, 128), lambda i, w=which: (0, jnp.clip(i - 2 * w, 0, 1)))
        for which in range(4)
    ]
    square = jax.ShapeDtypeStruct((D, 256), wide)
    rows = jax.ShapeDtypeStruct((256, D), wide)
    whole = jax.ShapeDtypeStruct((D, D), wide)
    return pl.pallas_call(
        finish_kernel,
        grid=(8,),
        out_shape=[square] * 4 + [rows] * 2 + [whole] * 2 + [jax.ShapeDtypeStruct((128, D), wide)],
        in_specs=[
            pl.BlockSpec((1, 128, D), lambda i: (i % 2, i // 2, 0)),
            pl.BlockSpec((2, 64, D), lambda i: (0, 8, 0)),
            pl.BlockSpec((1, 64, D), lambda i: (i, 0, 0)),
            pl.BlockSpec((1, 2, 128, D), lambda i: (i, 0, 0, 0)),
        ],
        out_specs=turned
        + [pl.BlockSpec((32, D), lambda i: (i, 0))] * 2
        + [pl.BlockSpec((D, 128), lambda i: (0, i)), pl.BlockSpec((128, D), lambda i: (i, 0))]
        + [pl.BlockSpec((128, D), lambda i: (0, 0))],
        compiler_params=pltpu.CompilerParams(vmem_limit_bytes=VMEM_LIMIT),
        name="finish_grads",
    )(pair, pair, two, ff)


def swap_seq(value):
    return lax.all_to_all(value, "seq", 0, 0, tiled=False)


def line_body(
    inputs,
    seg_starts,
    lengths,
    init_state,
    attn_gain,
    state_gain,
    mlp_gain,
    w_query,
    w_key,
    w_value,
    w_out,
    w_squery,
    w_sout,
    w_up,
    w_down,
    rel_bias,
    gate_bias,
    out_cot,
    state_cot,
):
    low, wide = jnp.bfloat16, jnp.float32
    place = lax.axis_index("seq")
    half = lax.rem(place, 2)
    mine = place // 2
    plane = ("dp", "seq")
    spot = 4 * lax.axis_index("dp") + place
    gate_value = jax.nn.sigmoid(gate_bias)
    vecs = jnp.stack(
        [
            state_gain,
            gate_value,
            mlp_gain,
            attn_gain,
            jnp.pad(jnp.concatenate([rel_bias[:, 0], rel_bias[:, 1]]), (0, D - 2 * BUCKETS)),
        ]
        + [jnp.zeros_like(gate_value)] * 3
    )
    marks = jnp.concatenate([seg_starts[:, 0], lengths, jnp.zeros((4,), jnp.int32)])
    marks = jnp.broadcast_to(marks[:, None], (8, 128))
    cot_used = lax.all_gather(out_cot.reshape(256, D), plane, axis=0, tiled=True)
    rows_all, qkv, kept, bias, marks, w_qkv = opening(
        inputs, w_query, w_key, w_value, w_sout, w_out, init_state, vecs, marks
    )

    ff_own = w_up.shape[1] // 8
    piece_of = lambda weight: lax.dynamic_slice_in_dim(weight, spot * 32, 32, 1).T
    back_own = jnp.stack(
        [
            piece_of(w_squery),
            piece_of(w_key),
            piece_of(w_value),
        ]
    )
    pieces = jnp.concatenate(
        [
            lax.dynamic_slice_in_dim(w_up, spot * ff_own, ff_own, 1).T,
            lax.dynamic_slice_in_dim(w_down, spot * ff_own, ff_own, 0),
        ],
        axis=0,
    )
    qkv, pieces, cot_used, back_own = lax.optimization_barrier(
        (qkv, pieces, cot_used, back_own)
    )
    spread = lax.all_gather(pieces, "tensor", axis=0, tiled=True).reshape(4, 2 * ff_own, D)
    mixed, lse_tok, state_rows, state_low, qkvst, lse_st, os_rows, cots, back = forward_chain(
        marks, qkv, kept, w_squery, w_qkv, vecs, bias, state_cot.reshape(4, 64, D), back_own
    )
    hidden_in, grad_hidden, d_mixed, mlp_sums, extra, ff_grads = middle(
        mixed, inputs, kept, spread, cot_used.reshape(8, 256, D), vecs
    )
    d_mixed, ff_grads = lax.optimization_barrier((d_mixed, ff_grads))
    ff_sum = lax.psum_scatter(
        ff_grads.reshape(ff_grads.shape[2] * 8, D), "tensor", scatter_dimension=0, tiled=True
    )
    (
        _, d_start, sums, state_out, tokens_out, out_part, partial, pair_grads, sout_part,
    ) = backward_chain(
        marks, qkv, d_mixed, lse_tok, qkvst, lse_st, state_rows, init_state, cots,
        back, kept, vecs, bias, extra, hidden_in, rows_all, state_low, w_qkv,
        os_rows.reshape(256, D),
    )
    partial, ff_sum = lax.optimization_barrier((partial, ff_sum))
    ff_total = lax.all_gather(ff_sum, plane, axis=0, tiled=True).reshape(8, 2, ff_own, D)
    inputs_grad, pair, two_grads, small = closing(
        partial, pair_grads, inputs, grad_hidden, vecs, d_start, mlp_sums, sums, out_part,
        sout_part,
    )
    pair = pair.reshape(2, PAIR_ROWS, D)
    (
        query_grad, key_grad, value_grad, squery_grad, out_grad, sout_grad, up_grad, down_grad,
        state_grad,
    ) = finish_grads(pair, two_grads, ff_total)
    bias_grad = lax.dynamic_slice_in_dim(
        small[4, : LINE * BUCKETS].reshape(4, 2, BUCKETS), lax.axis_index("tensor"), 1, 0
    )[0].T
    return (
        tokens_out,
        state_out[:, None],
        inputs_grad,
        state_grad,
        small[0],
        small[1],
        small[2],
        query_grad,
        key_grad,
        value_grad,
        out_grad,
        squery_grad,
        sout_grad,
        up_grad,
        down_grad,
        bias_grad,
        small[3],
    )


def solution(mesh):
    return jax.shard_map(
        chosen_body(mesh),
        mesh=mesh,
        in_specs=(
            P("dp", ("seq", "tensor"), None),
            P("dp", "seq"),
            P("dp"),
            P("tensor", None),
            P(),
            P(),
            P(),
            P(None, "tensor"),
            P(None, "tensor"),
            P(None, "tensor"),
            P("tensor", None),
            P(None, "tensor"),
            P("tensor", None),
            P(None, "tensor"),
            P("tensor", None),
            P(None, "tensor"),
            P(),
            P("dp", ("seq", "tensor"), None),
            P("dp", "seq", "tensor", None),
        ),
        out_specs=(
            P("dp", ("seq", "tensor"), None),
            P("dp", "seq", "tensor", None),
            P("dp", ("seq", "tensor"), None),
            P("tensor", None),
            P(),
            P(),
            P(),
            P(None, "tensor"),
            P(None, "tensor"),
            P(None, "tensor"),
            P("tensor", None),
            P(None, "tensor"),
            P("tensor", None),
            P(None, "tensor"),
            P("tensor", None),
            P(None, "tensor"),
            P(),
        ),
        check_vma=False,
    )
```

```python
import jax
import jax.numpy as jnp
from jax import lax
from jax.experimental import pallas as pl
from jax.experimental.pallas import tpu as pltpu
from jax.sharding import PartitionSpec as P

D = 1024
HEAD_DIM = 128
STATES = 512
BLOCK = 512
SEG = 256
BUCKETS = 32


norm_eps = 1e-06
masked_score = -1e30
bucket_edges = (12, 16, 23, 32, 46, 64, 91)


def passed_along(value, axis, steps):
    count = lax.axis_size(axis)
    leading, last = (max(0, -steps), min(count, count - steps))
    return lax.ppermute(value, axis, [(source, source + steps) for source in range(leading, last)])


def bucket_of(relative):
    distance = jnp.abs(relative)
    far_bucket = 8 + sum(((distance >= boundary).astype(jnp.int32) for boundary in bucket_edges))
    near_far = jnp.where(distance < 8, distance, far_bucket)
    return near_far + 16 * (relative > 0).astype(jnp.int32)


def token_mask(seg_start, seq_length, block_index):
    positions = jnp.arange(BLOCK)
    offset = block_index * BLOCK
    prev_valid = (block_index > 0) & (offset - BLOCK + positions < seq_length)
    cur_valid = offset + positions < seq_length
    inside = (positions >= seg_start) & (positions < seg_start + SEG)
    prev_mask = (positions[None, :] > positions[:, None]) & prev_valid[None, :]
    cur_mask = (
        (positions[None, :] <= positions[:, None]) | inside[None, :] & inside[:, None]
    ) & cur_valid[None, :]
    state_mask = jnp.ones((BLOCK, STATES), jnp.bool_)
    return jnp.concatenate([prev_mask, cur_mask, state_mask], axis=1)


def state_mask_of(valid_blk):
    batch_count = valid_blk.shape[0]
    block_part = jnp.broadcast_to(valid_blk[:, None, :], (batch_count, STATES, BLOCK))
    return jnp.concatenate([block_part, jnp.ones((batch_count, STATES, STATES), jnp.bool_)], axis=2)


def layer_norm(values, gain_vec):
    centered = values - jnp.mean(values, axis=-1, keepdims=True)
    spread = jnp.mean(centered * centered, axis=-1, keepdims=True)
    return centered * lax.rsqrt(spread + norm_eps) * gain_vec


def norm_back(values, gain_vec, grad_out):
    _, pullback = jax.vjp(layer_norm, values, gain_vec)
    return pullback(grad_out)


def gelu_back(pre_act, grad_out):
    _, pullback = jax.vjp(jax.nn.gelu, pre_act)
    return pullback(grad_out)[0]


def to_low(array_in):
    return array_in.astype(jnp.bfloat16)


def matmul(left, right):
    return jnp.einsum("...k,kn->...n", left, right, preferred_element_type=jnp.float32)


def matmul_t(left, right):
    return jnp.einsum("...n,kn->...k", left, right, preferred_element_type=jnp.float32)


def outer_sum(left, right):
    left_flat = left.reshape(-1, left.shape[-1])
    right_flat = right.reshape(-1, right.shape[-1])
    return lax.dot_general(
        left_flat, right_flat, (((0,), (0,)), ((), ())), preferred_element_type=jnp.float32
    )


def gather_rows(values):
    return lax.all_gather(values, "tensor", axis=1, tiled=True)


def sum_rows(terms):
    return lax.psum_scatter(
        terms.astype(jnp.bfloat16), "tensor", scatter_dimension=1, tiled=True
    ).astype(jnp.float32)


def pass_state(rows_now):
    return passed_along(rows_now.astype(jnp.bfloat16), "seq", 1).astype(rows_now.dtype)


def pass_back(grad_now):
    return passed_along(grad_now.astype(jnp.bfloat16), "seq", -1).astype(grad_now.dtype)


def split_heads(rows_in):
    return rows_in.reshape(rows_in.shape[0], rows_in.shape[1] // HEAD_DIM, HEAD_DIM)


def score_block(query_rows, key_all, bias_all, allowed):
    scores = (
        jnp.einsum(
            "qhd,khd->hqk",
            split_heads(query_rows),
            split_heads(key_all),
            preferred_element_type=jnp.float32,
        )
        * HEAD_DIM ** (-0.5)
        + bias_all
    )
    return jnp.where(allowed[None], scores, masked_score)


def attend_forward(query_rows, key_all, value_all, bias_all, allowed):
    scores = score_block(query_rows, key_all, bias_all, allowed)
    row_max = jnp.max(scores, axis=-1, keepdims=True)
    exp_scores = jnp.exp(scores - row_max)
    row_total = jnp.sum(exp_scores, axis=-1, keepdims=True)
    weight_all = to_low(exp_scores / row_total)
    mixed_out = jnp.einsum(
        "hqk,khd->qhd", weight_all, split_heads(value_all), preferred_element_type=jnp.float32
    )
    return (
        to_low(mixed_out.reshape(query_rows.shape[0], -1)),
        (row_max + jnp.log(row_total))[..., 0],
    )


def attend_back(query_rows, key_all, value_all, bias_all, allowed, log_total, grad_mixed):
    scores = score_block(query_rows, key_all, bias_all, allowed)
    weight_all = jnp.where(allowed[None], jnp.exp(scores - log_total[..., None]), 0.0)
    grad_heads = split_heads(grad_mixed)
    grad_weight = jnp.einsum(
        "qhd,khd->hqk", grad_heads, split_heads(value_all), preferred_element_type=jnp.float32
    )
    row_inner = jnp.sum(weight_all * grad_weight, axis=-1, keepdims=True)
    grad_scores = to_low(weight_all * (grad_weight - row_inner))
    grad_query = jnp.einsum(
        "hqk,khd->qhd", grad_scores, split_heads(key_all), preferred_element_type=jnp.float32
    ) * HEAD_DIM ** (-0.5)
    grad_keys = jnp.einsum(
        "hqk,qhd->khd", grad_scores, split_heads(query_rows), preferred_element_type=jnp.float32
    ) * HEAD_DIM ** (-0.5)
    grad_values = jnp.einsum(
        "hqk,qhd->khd", to_low(weight_all), grad_heads, preferred_element_type=jnp.float32
    )
    return (
        grad_query.reshape(query_rows.shape[0], -1),
        grad_keys.reshape(key_all.shape[0], -1),
        grad_values.reshape(key_all.shape[0], -1),
        grad_scores,
    )


def bias_lookup(rel_bias, rel_table):
    table_heads = jnp.zeros((rel_bias.shape[1],) + rel_table.shape, jnp.float32)
    for bucket_id in range(BUCKETS):
        table_heads = table_heads + jnp.where(
            rel_table[None] == bucket_id, rel_bias[bucket_id][:, None, None], 0.0
        )
    return table_heads


def bias_sums(score_grad, rel_table):
    grad_wide = score_grad.astype(jnp.float32)
    columns = []
    for bucket_id in range(BUCKETS):
        columns.append(
            jnp.sum(jnp.where(rel_table[None, None] == bucket_id, grad_wide, 0.0), axis=(0, 2, 3))
        )
    return jnp.stack(columns, axis=0)


def body(
    inputs,
    seg_starts,
    lengths,
    init_state,
    attn_gain,
    state_gain,
    mlp_gain,
    w_query,
    w_key,
    w_value,
    w_out,
    w_squery,
    w_sout,
    w_up,
    w_down,
    rel_bias,
    gate_bias,
    out_cot,
    state_cot,
):
    seq_count = inputs.shape[0]
    chain_length = lax.axis_size("seq")
    block_index = lax.axis_index("seq")
    is_first = block_index == 0
    width_local = w_query.shape[1]
    head_count = width_local // HEAD_DIM
    gate_value = jax.nn.sigmoid(gate_bias)
    positions = jnp.arange(BLOCK)
    inputs_wide = inputs.astype(jnp.float32)
    tokens_low = gather_rows(to_low(layer_norm(inputs_wide, attn_gain)))
    query_tok = to_low(matmul(tokens_low, w_query))
    key_tok = to_low(matmul(tokens_low, w_key))
    value_tok = to_low(matmul(tokens_low, w_value))
    key_prev, value_prev = passed_along((key_tok, value_tok), "seq", 1)
    valid_keys = (block_index * BLOCK + positions)[None, :] < lengths[:, None]
    batched_attend = jax.vmap(attend_forward, in_axes=(0, 0, 0, None, 0))
    batched_back = jax.vmap(attend_back, in_axes=(0, 0, 0, None, 0, 0, 0))

    def state_forward(state_rows, key_blk, value_blk, valid_blk):
        state_low = lax.all_gather(
            to_low(layer_norm(state_rows, state_gain)), "tensor", axis=1, tiled=True
        )
        query_st = to_low(matmul(state_low, w_squery))
        key_st = to_low(matmul(state_low, w_key))
        value_st = to_low(matmul(state_low, w_value))
        key_all = jnp.concatenate([key_blk, key_st], axis=1)
        value_all = jnp.concatenate([value_blk, value_st], axis=1)
        mixed_st, lse_st = batched_attend(
            query_st, key_all, value_all, 0.0, state_mask_of(valid_blk)
        )
        update = lax.psum_scatter(
            matmul(mixed_st, w_sout).astype(jnp.bfloat16), "tensor", scatter_dimension=1, tiled=True
        ).astype(jnp.float32)
        state_next = gate_value * state_rows + (1.0 - gate_value) * update
        return (state_next, (state_low, query_st, key_st, value_st, mixed_st, lse_st, update))

    def state_backward(
        grad_out, state_rows, kept_one, key_blk, value_blk, valid_blk, extra_key, extra_value
    ):
        state_low, query_st, key_st, value_st, mixed_st, lse_st, update = kept_one
        gate_part = (
            jnp.sum(grad_out * (state_rows - update), axis=(0, 1)) * gate_value * (1.0 - gate_value)
        )
        grad_update = lax.all_gather(
            to_low((1.0 - gate_value) * grad_out), "tensor", axis=1, tiled=True
        )
        grad_mixed_st = to_low(matmul_t(grad_update, w_sout))
        sout_part = outer_sum(mixed_st, grad_update)
        key_all = jnp.concatenate([key_blk, key_st], axis=1)
        value_all = jnp.concatenate([value_blk, value_st], axis=1)
        grad_query_st, grad_keys_st, grad_values_st, _ = batched_back(
            query_st, key_all, value_all, 0.0, state_mask_of(valid_blk), lse_st, grad_mixed_st
        )
        query_low = to_low(grad_query_st)
        key_low = to_low(grad_keys_st[:, BLOCK:] + extra_key)
        value_low = to_low(grad_values_st[:, BLOCK:] + extra_value)
        squery_part = outer_sum(state_low, query_low)
        key_part = outer_sum(state_low, key_low)
        value_part = outer_sum(state_low, value_low)
        terms = (
            matmul_t(query_low, w_squery) + matmul_t(key_low, w_key) + matmul_t(value_low, w_value)
        )
        grad_normed = lax.psum_scatter(
            terms.astype(jnp.bfloat16), "tensor", scatter_dimension=1, tiled=True
        ).astype(jnp.float32)
        grad_rows_norm, gain_part = norm_back(state_rows, state_gain, grad_normed)
        grad_in = gate_value * grad_out + grad_rows_norm
        block_grads = (grad_keys_st[:, :BLOCK], grad_values_st[:, :BLOCK])
        return (
            grad_in,
            block_grads,
            (squery_part, key_part, value_part, sout_part, gain_part, gate_part),
        )

    zeros_rows = jnp.zeros((seq_count,) + init_state.shape, jnp.float32)
    narrow_zero = jnp.zeros((seq_count, STATES, width_local), jnp.bfloat16)
    stored_start = (
        zeros_rows,
        zeros_rows,
        jnp.zeros((seq_count, STATES, D), jnp.bfloat16),
        narrow_zero,
        narrow_zero,
        narrow_zero,
        narrow_zero,
        jnp.zeros((seq_count, head_count, STATES), jnp.float32),
        zeros_rows,
    )

    def forward_turn(turn_index, carry):
        incoming, stored_now = carry
        order_index = turn_index - block_index
        is_live = (order_index >= 0) & (order_index < seq_count)
        picked = jnp.clip(order_index, 0, seq_count - 1)
        rows_now = jnp.where(is_first, init_state[None], incoming)
        key_one = lax.dynamic_slice_in_dim(key_tok, picked, 1, 0)
        value_one = lax.dynamic_slice_in_dim(value_tok, picked, 1, 0)
        valid_one = lax.dynamic_slice_in_dim(valid_keys, picked, 1, 0)
        rows_next, kept_one = state_forward(rows_now, key_one, value_one, valid_one)
        fresh = (rows_now, rows_next) + kept_one
        stored_now = tuple(
            (
                jnp.where(
                    is_live,
                    lax.dynamic_update_slice_in_dim(whole_array, fresh_part, picked, 0),
                    whole_array,
                )
                for whole_array, fresh_part in zip(stored_now, fresh)
            )
        )
        return (pass_state(rows_next), stored_now)

    incoming_start = jnp.zeros((1,) + init_state.shape, jnp.float32)
    _, stored_all = lax.fori_loop(
        0, chain_length + seq_count - 1, forward_turn, (incoming_start, stored_start)
    )
    state_in = stored_all[0]
    state_out = stored_all[1]
    kept = stored_all[2:]
    key_all_tok = jnp.concatenate([key_prev, key_tok, kept[2]], axis=1)
    value_all_tok = jnp.concatenate([value_prev, value_tok, kept[3]], axis=1)
    allowed_tok = jax.vmap(token_mask, in_axes=(0, 0, None))(seg_starts[:, 0], lengths, block_index)
    rel_table = bucket_of((jnp.arange(2 * BLOCK) - BLOCK)[None, :] - positions[:, None])
    full_bias = jnp.concatenate(
        [bias_lookup(rel_bias, rel_table), jnp.zeros((head_count, BLOCK, STATES), jnp.float32)],
        axis=2,
    )
    mixed_tok, lse_tok = batched_attend(
        query_tok, key_all_tok, value_all_tok, full_bias, allowed_tok
    )
    hidden_in = inputs_wide + sum_rows(matmul(mixed_tok, w_out))
    mid_low = gather_rows(to_low(layer_norm(hidden_in, mlp_gain)))
    pre_act = matmul(mid_low, w_up)
    hidden_low = to_low(jax.nn.gelu(pre_act))
    mlp_rows = sum_rows(matmul(hidden_low, w_down))
    tokens_out = (hidden_in + mlp_rows).astype(jnp.bfloat16)
    cot_wide = out_cot.astype(jnp.float32)
    cot_used = gather_rows(out_cot)
    grad_hidden_act = matmul_t(cot_used, w_down)
    down_grad = outer_sum(hidden_low, cot_used)
    grad_pre = to_low(gelu_back(pre_act, grad_hidden_act))
    up_grad = outer_sum(mid_low, grad_pre)
    grad_normed_mid = sum_rows(matmul_t(grad_pre, w_up))
    grad_mid_in, mlp_gain_grad = norm_back(hidden_in, mlp_gain, grad_normed_mid)
    grad_hidden = cot_wide + grad_mid_in
    grad_attn_low = gather_rows(to_low(grad_hidden))
    grad_mixed = to_low(matmul_t(grad_attn_low, w_out))
    out_grad = outer_sum(mixed_tok, grad_attn_low)
    grad_query_tok, grad_keys_tok, grad_values_tok, grad_scores = batched_back(
        query_tok, key_all_tok, value_all_tok, full_bias, allowed_tok, lse_tok, grad_mixed
    )
    bias_grad = bias_sums(grad_scores[..., : 2 * BLOCK], rel_table)
    grad_key_next, grad_value_next = (
        passed_along(grad_keys_tok[:, :BLOCK].astype(jnp.bfloat16), "seq", -1).astype(jnp.float32),
        passed_along(grad_values_tok[:, :BLOCK].astype(jnp.bfloat16), "seq", -1).astype(
            jnp.float32
        ),
    )
    grad_key_own = grad_keys_tok[:, BLOCK : 2 * BLOCK] + grad_key_next
    grad_value_own = grad_values_tok[:, BLOCK : 2 * BLOCK] + grad_value_next
    grad_key_st_tok = grad_keys_tok[:, 2 * BLOCK :]
    grad_value_st_tok = grad_values_tok[:, 2 * BLOCK :]
    cot_rows = state_cot[:, 0].astype(jnp.float32)
    wide_zero = jnp.zeros((seq_count, BLOCK, width_local), jnp.float32)
    stored_back = (zeros_rows, wide_zero, wide_zero)
    totals_start = (
        jnp.zeros((D, width_local), jnp.float32),
        jnp.zeros((D, width_local), jnp.float32),
        jnp.zeros((D, width_local), jnp.float32),
        jnp.zeros((width_local, D), jnp.float32),
        jnp.zeros((D,), jnp.float32),
        jnp.zeros((D,), jnp.float32),
    )

    def backward_turn(turn_index, carry):
        incoming, stored_now, totals_now = carry
        order_index = turn_index - (chain_length - 1 - block_index)
        is_live = (order_index >= 0) & (order_index < seq_count)
        picked = jnp.clip(order_index, 0, seq_count - 1)

        def slice_one(whole_array):
            return lax.dynamic_slice_in_dim(whole_array, picked, 1, 0)

        grad_out = slice_one(cot_rows) + incoming
        kept_one = tuple((slice_one(kept_array) for kept_array in kept))
        grad_in, block_one, parts_one = state_backward(
            grad_out,
            slice_one(state_in),
            kept_one,
            slice_one(key_tok),
            slice_one(value_tok),
            slice_one(valid_keys),
            slice_one(grad_key_st_tok),
            slice_one(grad_value_st_tok),
        )
        fresh = (grad_in,) + block_one
        stored_now = tuple(
            (
                jnp.where(
                    is_live,
                    lax.dynamic_update_slice_in_dim(whole_array, fresh_part, picked, 0),
                    whole_array,
                )
                for whole_array, fresh_part in zip(stored_now, fresh)
            )
        )
        totals_now = tuple(
            (
                total_now + jnp.where(is_live, part_now, 0.0)
                for total_now, part_now in zip(totals_now, parts_one)
            )
        )
        return (pass_back(grad_in), stored_now, totals_now)

    incoming_start = jnp.zeros((1,) + init_state.shape, jnp.float32)
    _, stored_done, weight_parts = lax.fori_loop(
        0, chain_length + seq_count - 1, backward_turn, (incoming_start, stored_back, totals_start)
    )
    grad_in_all, grad_key_blk, grad_value_blk = stored_done
    query_low = to_low(grad_query_tok)
    key_low = to_low(grad_key_own + grad_key_blk)
    value_low = to_low(grad_value_own + grad_value_blk)
    query_grad = outer_sum(tokens_low, query_low)
    key_grad = outer_sum(tokens_low, key_low) + weight_parts[1]
    value_grad = outer_sum(tokens_low, value_low) + weight_parts[2]
    grad_tokens = sum_rows(
        matmul_t(query_low, w_query) + matmul_t(key_low, w_key) + matmul_t(value_low, w_value)
    )
    grad_in_norm, attn_gain_grad = norm_back(inputs_wide, attn_gain, grad_tokens)
    inputs_grad = grad_hidden + grad_in_norm
    state_part = jnp.where(is_first, jnp.sum(grad_in_all, axis=0), 0.0)
    gains = lax.psum(
        jnp.stack([attn_gain_grad, weight_parts[4], mlp_gain_grad, weight_parts[5]]), "tensor"
    )
    totals = (
        lax.psum(query_grad.astype(jnp.bfloat16), ("dp", "seq")).astype(jnp.float32),
        lax.psum(key_grad.astype(jnp.bfloat16), ("dp", "seq")).astype(jnp.float32),
        lax.psum(value_grad.astype(jnp.bfloat16), ("dp", "seq")).astype(jnp.float32),
        lax.psum(out_grad.astype(jnp.bfloat16), ("dp", "seq")).astype(jnp.float32),
        lax.psum(weight_parts[0].astype(jnp.bfloat16), ("dp", "seq")).astype(jnp.float32),
        lax.psum(weight_parts[3].astype(jnp.bfloat16), ("dp", "seq")).astype(jnp.float32),
        lax.psum(up_grad.astype(jnp.bfloat16), ("dp", "seq")).astype(jnp.float32),
        lax.psum(down_grad.astype(jnp.bfloat16), ("dp", "seq")).astype(jnp.float32),
        lax.psum(bias_grad.astype(jnp.bfloat16), ("dp", "seq")).astype(jnp.float32),
        lax.psum(state_part.astype(jnp.bfloat16), ("dp", "seq")).astype(jnp.float32),
        lax.psum(gains.astype(jnp.bfloat16), ("dp", "seq")).astype(jnp.float32),
    )
    gain_total = totals[10]
    return (
        tokens_out,
        state_out[:, None],
        inputs_grad,
        totals[9],
        gain_total[0],
        gain_total[1],
        gain_total[2],
        totals[0],
        totals[1],
        totals[2],
        totals[3],
        totals[4],
        totals[5],
        totals[6],
        totals[7],
        totals[8],
        gain_total[3],
    )


def chosen_body(mesh):
    if mesh.shape["seq"] == 4 and mesh.shape["tensor"] == 4:
        return line_body
    return body


MESH_ID = pl.DeviceIdType.MESH
ROWS = 128
CHUNKS = BLOCK // ROWS
LINE = 8
SCALE = HEAD_DIM ** (-0.5)
VMEM_LIMIT = 60 * 1024 * 1024


def dot_nn(left, right):
    return lax.dot_general(left, right, (((1,), (0,)), ((), ())), preferred_element_type=jnp.float32)


def dot_nt(left, right):
    return lax.dot_general(left, right, (((1,), (1,)), ((), ())), preferred_element_type=jnp.float32)


def dot_tn(left, right):
    return lax.dot_general(left, right, (((0,), (0,)), ((), ())), preferred_element_type=jnp.float32)


def line_place():
    place = lax.axis_index("seq")
    half = lax.rem(place, 2)
    rank = lax.axis_index("tensor")
    return place, half, rank


def span(index, size):
    return pl.ds(pl.multiple_of(index * size, size), size)


def fetch_pieces(kept, first, rows, target, sem):
    for owner in range(8):
        pltpu.make_async_copy(
            kept.at[owner, :, pl.ds(first, rows), :], target.at[:, owner], sem
        ).start()


def fetch_columns(weights, target, sem):
    half = lax.rem(lax.axis_index("seq"), 2)
    for index, weight in enumerate(weights):
        pltpu.make_async_copy(
            weight.at[:, span(half, 128)], target.at[:, pl.ds(128 * index, 128)], sem
        ).start()


def fetched(target, sem):
    pltpu.make_async_copy(target, target, sem).wait()


def norm_parts(rows):
    centered = rows - jnp.mean(rows, axis=-1, keepdims=True)
    spread = jnp.mean(centered * centered, axis=-1, keepdims=True)
    return centered, lax.rsqrt(spread + norm_eps)


def mark(marks, block_id, row):
    return marks[block_id, pl.ds(row, 1), 0:1]


def sequence_marks(marks, block_id):
    mine = lax.axis_index("seq") // 2
    return mark(marks, block_id, mine), mark(marks, 0, 2 + mine)


def token_masks(marks, block_id, first_row):
    start, length = sequence_marks(marks, block_id)
    row = lax.broadcasted_iota(jnp.int32, (ROWS, BLOCK), 0) + first_row
    col = lax.broadcasted_iota(jnp.int32, (ROWS, BLOCK), 1)
    prev_limit = jnp.where(block_id > 0, length - (block_id - 1) * BLOCK, 0)
    prev_ok = (col > row) & (col < prev_limit)
    row_in = (row >= start) & (row < start + SEG)
    col_in = (col >= start) & (col < start + SEG)
    cur_ok = ((col <= row) | (row_in & col_in)) & (col < length - block_id * BLOCK)
    return prev_ok, cur_ok


def state_block_mask(marks, block_id):
    _, length = sequence_marks(marks, block_id)
    col = lax.broadcasted_iota(jnp.int32, (ROWS, BLOCK), 1)
    return col < length - block_id * BLOCK


def softmax_of(score_parts):
    top = jnp.max(score_parts[0], axis=-1, keepdims=True)
    for part in score_parts[1:]:
        top = jnp.maximum(top, jnp.max(part, axis=-1, keepdims=True))
    raised = [jnp.exp(part - top) for part in score_parts]
    total = jnp.sum(raised[0], axis=-1, keepdims=True)
    for part in raised[1:]:
        total = total + jnp.sum(part, axis=-1, keepdims=True)
    inverse = 1.0 / total
    return [to_low(part * inverse) for part in raised], top + jnp.log(total)


def token_scores(scal, qkv, qkvst, bias, block_id, chunk):
    rows = span(chunk, ROWS)
    prev_id = jnp.maximum(block_id - 1, 0)
    query = qkv[block_id, rows, 0:128]
    prev_ok, cur_ok = token_masks(scal, block_id, chunk * ROWS)
    prev = dot_nt(query, qkv[prev_id, :, 128:256]) * SCALE + bias[rows, 0:BLOCK]
    cur = dot_nt(query, qkv[block_id, :, 128:256]) * SCALE + bias[rows, BLOCK : 2 * BLOCK]
    stt = dot_nt(query, qkvst[block_id, :, 128:256]) * SCALE
    prev = jnp.where(prev_ok, prev, masked_score)
    cur = jnp.where(cur_ok, cur, masked_score)
    return query, (prev, cur, stt)


def state_scores(scal, qkv, qkvst, block_id, chunk):
    query = qkvst[block_id, span(chunk, ROWS), 0:128]
    tok = dot_nt(query, qkv[block_id, :, 128:256]) * SCALE
    tok = jnp.where(state_block_mask(scal, block_id), tok, masked_score)
    stt = dot_nt(query, qkvst[block_id, :, 128:256]) * SCALE
    return query, (tok, stt)


HALVES = 2
HALF_ROWS = STATES // HALVES
HALF_CHUNKS = HALF_ROWS // ROWS


def forward_kernel(
    marks, qkv, kept, w_squery, w_qkv, vecs, bias, state_cot, back_own,
    o_out, lse_out, state_rows, low_out, qkvst, lse_st, os_rows, cots, back,
    held, os_all, state_low, w_sout, start, w_state,
    way_send, core_send, recv_sem, local_sem, low_sem, cot_send, cot_recv,
    piece_send, piece_recv, ring_send, ring_recv,
):
    side, place, half, rank = plane_place()
    me = plane_index(side, place)
    partner = place + 1 - 2 * half
    head = 2 * rank + half
    fetch_pieces(kept, 32, 16, start, local_sem.at[0])
    fetch_columns((w_squery,), w_state, local_sem.at[2])
    fetch_pieces(kept, 0, 32, w_sout, local_sem.at[1])
    own_cot = pltpu.make_async_copy(state_cot.at[place], cots.at[place], local_sem.at[4])
    own_cot.start()
    own_piece = pltpu.make_async_copy(back_own, back.at[me, rank], local_sem.at[3])
    own_piece.start()
    ranks = [lax.rem(rank + step, 4) for step in (1, 2, 3)]
    seats = [lax.rem(place + step, 4) for step in (1, 2, 3)]
    barrier = pltpu.get_barrier_semaphore()
    for target in [{"tensor": one} for one in ranks] + [{"seq": one} for one in seats] + [
        {"dp": 1 - side}
    ]:
        pl.semaphore_signal(barrier, inc=1, device_id=target, device_id_type=MESH_ID)
    fetched(start, local_sem.at[0])
    held[...] = start[...].reshape(STATES, D).astype(jnp.float32)
    gain = vecs[0:1, :]
    gate = vecs[1:2, :]
    fetched(w_state, local_sem.at[2])

    def project(block_id, part):
        def one(chunk, _):
            rows = span(chunk, ROWS)
            centered, scale = norm_parts(held[rows, :])
            low = to_low(centered * scale * gain)
            state_low[block_id, rows, :] = low
            qkvst[block_id, rows, 0:128] = to_low(dot_nn(low, w_state[...]))
            qkvst[block_id, rows, 128:384] = to_low(dot_nn(low, w_qkv[:, 128:384]))
            return 0

        lax.fori_loop(HALF_CHUNKS * part, HALF_CHUNKS * (part + 1), one, 0)

    pl.semaphore_wait(barrier, 7)

    def piece_move(origin, part, slot, target):
        return pltpu.make_async_remote_copy(
            src_ref=back_own.at[part],
            dst_ref=back.at[me, origin, part],
            send_sem=piece_send.at[part, slot],
            recv_sem=piece_recv.at[part, origin],
            device_id={"tensor": target},
            device_id_type=MESH_ID,
        )

    def send_piece(part):
        for slot, target in enumerate(ranks):
            piece_move(rank, part, slot, target).start()

    gather = plane_gather(
        lambda owner, part: back.at[owner, pl.ds(2 * part, 2)], ring_send, ring_recv
    )
    next(gather)
    send_piece(0)
    for part in range(HALVES):
        project(0, part)
    right, left = {"tensor": lax.rem(rank + 1, 4)}, {"tensor": lax.rem(rank + 3, 4)}

    def moved(block_id, part, which, sem, target):
        view = os_all.at[block_id, pl.ds(HALF_ROWS * part, HALF_ROWS), span(which, 128)]
        return pltpu.make_async_remote_copy(
            src_ref=view,
            dst_ref=view,
            send_sem=sem,
            recv_sem=recv_sem.at[block_id, part, which],
            device_id=target,
            device_id_type=MESH_ID,
        )

    def cot_move(index, origin, slot, target):
        return pltpu.make_async_remote_copy(
            src_ref=state_cot.at[index],
            dst_ref=cots.at[origin],
            send_sem=cot_send.at[slot],
            recv_sem=cot_recv.at[origin],
            device_id={"seq": target},
            device_id_type=MESH_ID,
        )

    for slot, target in enumerate(seats):
        cot_move(target, place, slot, target).start()
    fetched(w_sout, local_sem.at[1])

    def origin_of(way, distance):
        if way == 0:
            return jnp.maximum(rank - distance, 0)
        return jnp.minimum(rank + distance, 3)

    def ways(distance):
        return (
            (0, rank >= distance, (rank >= distance) & (rank < 3), right),
            (1, rank + distance <= 3, (rank + distance <= 3) & (rank > 0), left),
        )

    def relay(block_id, part, distance, waiting):
        for way, comes, goes, target in ways(distance):
            which = 2 * origin_of(way, distance) + half
            sem = way_send.at[block_id, part, min(distance, 2), way]
            core_sem = core_send.at[block_id, part, which // 2]
            if distance > 0:

                @pl.when(comes)
                def _():
                    to_core = moved(block_id, part, which, core_sem, {"seq": partner})
                    if waiting:
                        moved(block_id, part, which, sem, target).wait_recv()
                        to_core.start()
                    else:
                        to_core.wait_send()

            if distance < 3:

                @pl.when(goes)
                def _():
                    one = moved(block_id, part, which, sem, target)
                    if waiting:
                        one.start()
                    else:
                        one.wait_send()

        if distance == 0:
            mine = moved(
                block_id, part, head, core_send.at[block_id, part, rank], {"seq": partner}
            )
            if waiting:
                mine.start()
            else:
                mine.wait_send()

    def one_block(block_id, _):
        def attend_state(chunk, _):
            rows = span(chunk, ROWS)
            _, parts = state_scores(marks, qkv, qkvst, block_id, chunk)
            (w_tok, w_stt), total = softmax_of(parts)
            mixed = dot_nn(w_tok, qkv[block_id, :, 256:384]) + dot_nn(
                w_stt, qkvst[block_id, :, 256:384]
            )
            os_all[block_id, rows, span(head, 128)] = to_low(mixed)
            lse_st[block_id, rows, :] = total
            return 0

        def attend_token(chunk, _):
            rows = span(chunk, ROWS)
            _, parts = token_scores(marks, qkv, qkvst, bias, block_id, chunk)
            weights, total = softmax_of(parts)
            prev_id = jnp.maximum(block_id - 1, 0)
            mixed = (
                dot_nn(weights[0], qkv[prev_id, :, 256:384])
                + dot_nn(weights[1], qkv[block_id, :, 256:384])
                + dot_nn(weights[2], qkvst[block_id, :, 256:384])
            )
            o_out[block_id, rows, :] = to_low(mixed)
            lse_out[block_id, rows, :] = total
            return 0

        def attend_both(part, _):
            lax.fori_loop(HALF_CHUNKS * part, HALF_CHUNKS * (part + 1), attend_state, 0)
            for value in range(HALVES):

                @pl.when(part == value)
                def _():
                    relay(block_id, value, 0, True)

            return 0

        lax.fori_loop(0, HALVES, attend_both, 0)
        pltpu.make_async_copy(
            state_low.at[block_id], low_out.at[block_id], low_sem.at[block_id]
        ).start()

        @pl.when(block_id == 2)
        def _():
            own_piece.wait()
            for part in range(3):
                for slot, target in enumerate(ranks):
                    piece_move(target, part, slot, target).wait_recv()
            next(gather)

        @pl.when(block_id == 3)
        def _():
            next(gather)
            next(gather)

        def between(step, _):
            for value, (distance, part) in enumerate(((1, 0), (1, 1), (2, 0), (2, 1))):

                @pl.when(step == value)
                def _():
                    relay(block_id, part, distance, True)

            return attend_token(step, 0)

        lax.fori_loop(0, 4, between, 0)

        def settle(part, _):
            for value in range(HALVES):

                @pl.when(part == value)
                def _():
                    relay(block_id, value, 3, True)
                    for origin in range(4):
                        moved(
                            block_id, value, 2 * origin + 1 - half,
                            core_send.at[block_id, value, origin], {"seq": partner},
                        ).wait_recv()

                    if value == HALVES - 1:
                        for turn in (0, 1):

                            @pl.when(block_id == turn)
                            def _():
                                send_piece(turn + 1)

            def update(chunk, _):
                rows = span(chunk, ROWS)
                change = dot_nn(os_all[block_id, rows, :], w_sout[...].reshape(D, D))
                held[rows, :] = gate * held[rows, :] + (1.0 - gate) * change
                return 0

            lax.fori_loop(HALF_CHUNKS * part, HALF_CHUNKS * (part + 1), update, 0)

            @pl.when(block_id < 3)
            def _():
                project(block_id + 1, part)

            return 0

        lax.fori_loop(0, HALVES, settle, 0)
        state_rows[block_id] = held[span(rank, 128), :]
        os_rows[block_id] = os_all[block_id, span(head, 64), :]
        return 0

    lax.fori_loop(0, 4, one_block, 0)

    def drain(block_id, _):
        for part in range(HALVES):
            for distance in range(4):
                relay(block_id, part, distance, False)
        pltpu.make_async_copy(
            state_low.at[block_id], low_out.at[block_id], low_sem.at[block_id]
        ).wait()
        return 0

    lax.fori_loop(0, 4, drain, 0)
    own_cot.wait()
    for part in range(3):
        for slot, target in enumerate(ranks):
            piece_move(rank, part, slot, target).wait_send()
    for _ in gather:
        pass
    for slot, target in enumerate(seats):
        cot_move(target, place, slot, target).wait_send()
        cot_move(place, target, slot, target).wait_recv()


def any_specs(count):
    return [pl.BlockSpec(memory_space=pl.ANY)] * count


def vmem_specs(count):
    return [pl.BlockSpec(memory_space=pltpu.VMEM)] * count


def forward_chain(
    marks, qkv, kept, w_squery, w_qkv, vecs, bias, state_cot, back_own
):
    low, wide = jnp.bfloat16, jnp.float32
    shapes = (
        ((4, BLOCK, 128), low),
        ((4, BLOCK, 1), wide),
        ((4, 128, D), wide),
        ((4, STATES, D), low),
        ((4, STATES, 384), low),
        ((4, STATES, 1), wide),
        ((4, 64, D), low),
        ((4, 64, D), low),
        ((8, 4, 3, 32, D), low),
    )
    dma = pltpu.SemaphoreType.DMA
    return pl.pallas_call(
        forward_kernel,
        out_shape=[jax.ShapeDtypeStruct(*one) for one in shapes],
        in_specs=vmem_specs(2) + any_specs(2) + vmem_specs(3) + any_specs(2),
        out_specs=vmem_specs(3) + any_specs(1) + vmem_specs(3) + any_specs(2),
        scratch_shapes=[
            pltpu.VMEM((STATES, D), wide),
            pltpu.VMEM((4, STATES, D), low),
            pltpu.VMEM((4, STATES, D), low),
            pltpu.VMEM((4, 8, 32, D), low),
            pltpu.VMEM((4, 8, 16, D), low),
            pltpu.VMEM((D, 128), low),
            dma((4, HALVES, 3, 2)),
            dma((4, HALVES, 4)),
            dma((4, HALVES, 8)),
            dma((5,)),
            dma((4,)),
            dma((3,)),
            dma((4,)),
            dma((3, 3)),
            dma((3, 4)),
            dma((14,)),
            dma((8, 2)),
        ],
        compiler_params=pltpu.CompilerParams(
            collective_id=1, has_side_effects=True, vmem_limit_bytes=VMEM_LIMIT
        ),
        cost_estimate=pl.CostEstimate(
            flops=60000000000, bytes_accessed=60000000, transcendentals=0
        ),
        name="forward_chain",
    )(marks, qkv, kept, w_squery, w_qkv, vecs, bias, state_cot, back_own)


def backward_kernel(
    scal, qkv, d_o, lse_tok, qkvst, lse_st, state_rows, begin, cots, back, kept, vecs, bias,
    extra, hidden, rows_hbm, low_hbm, w_qkv, os_rows,
    du_rows, d_start, sums, state_out, tokens_out, out_part, partial, pair_grads, sout_part,
    dz_sum, diag, d_qkv, d_qkvst, rows_buf, low_buf, leave, came, grad_acc,
    key_acc, value_acc, st_key, st_value, dos_rows, dos_got, d_got, grad_in,
    states, w_back, w_sout, work, core_got, near_got, far_got, total,
    send_sem, recv_sem, local_sem, side_sem, ring_send, ring_recv, buf_sem, core_sem, came_sem,
    near_two, far_two, two_send, two_recv,
):
    place, half, rank = line_place()
    own_rows = pl.ds(pl.multiple_of(half * 64, 64), 64)
    loads = [
        pltpu.make_async_copy(
            state_rows.at[:, own_rows, :], states.at[pl.ds(1, 4)], local_sem.at[0]
        ),
        pltpu.make_async_copy(
            state_rows.at[place], state_out.at[place // 2], local_sem.at[3]
        ),
        pltpu.make_async_copy(extra, work, local_sem.at[4]),
    ]
    for one in loads:
        one.start()
    fetch_pieces(kept, 0, 32, w_sout, local_sem.at[1])
    for owner in range(8):
        pltpu.make_async_copy(
            back.at[owner], w_back.at[:, owner // 4, :, owner % 4], local_sem.at[2]
        ).start()
    states[0] = to_low(begin[own_rows, :]).astype(jnp.float32)

    def block_loads(block_id):
        slot = lax.rem(block_id, 2)
        return [
            pltpu.make_async_copy(
                source.at[block_id], target.at[slot], buf_sem.at[index, slot]
            )
            for index, (source, target) in enumerate(((rows_hbm, rows_buf), (low_hbm, low_buf)))
        ]

    for one in block_loads(3):
        one.start()
    head = 2 * rank + half
    peers = []
    for step in (4, 3, 5, 2, 6, 1, 7):
        other = lax.rem(head + step, LINE)
        peers.append((other, place - half + lax.rem(other, 2), other // 2))
    barrier = pltpu.get_barrier_semaphore()
    for _, seq_to, rank_to in peers:
        pl.semaphore_signal(
            barrier, inc=1, device_id={"seq": seq_to, "tensor": rank_to}, device_id_type=MESH_ID
        )
    beside = lax.rem(place + 2, 4)
    pl.semaphore_signal(barrier, inc=1, device_id={"seq": beside}, device_id_type=MESH_ID)
    pl.semaphore_signal(
        barrier, inc=1, device_id={"dp": 1 - lax.axis_index("dp")}, device_id_type=MESH_ID
    )
    plane_steps = plane_scatter(
        work, core_got, near_got, far_got, total, 384, ring_send, ring_recv
    )
    next(plane_steps)
    short = pl.ds(0, 128)
    sout_steps = plane_scatter(
        work.at[:, short, :], core_got.at[:, short, :], near_two, far_two, total.at[short, :],
        128, two_send, two_recv,
    )
    next(sout_steps)

    def sout_products():
        def one(index, _):
            part = to_low(
                dot_tn(os_rows[:, span(index, 128)], du_rows[...].reshape(256, D))
            )
            for block in range(4):
                work[4 * lax.rem(index, 2) + block, span(index // 2, 32), :] = part[
                    32 * block : 32 * block + 32, :
                ]
            return 0

        lax.fori_loop(0, LINE, one, 0)

    def plane_results():
        for which in range(2):
            rows = pl.ds(128 * which, 128)
            tokens_out[which] = to_low(hidden[which] + total[rows, :])
        out_part[...] = to_low(total[256:384, :])


    def aside(block_id, row_set):
        return pltpu.make_async_remote_copy(
            src_ref=state_rows.at[block_id],
            dst_ref=state_out.at[row_set],
            send_sem=side_sem.at[0],
            recv_sem=side_sem.at[1],
            device_id={"seq": beside},
            device_id_type=MESH_ID,
        )

    gain = vecs[0:1, :]
    gate = vecs[1:2, :]
    key_acc[...] = jnp.zeros_like(key_acc)
    value_acc[...] = jnp.zeros_like(value_acc)
    dz_sum[...] = jnp.zeros_like(dz_sum)
    sums[...] = jnp.zeros_like(sums)
    grad_in[...] = jnp.zeros_like(grad_in)
    grad_acc[...] = jnp.zeros_like(grad_acc)
    core = place + 1 - 2 * half

    def place_in(block_id, owner):
        return jnp.where(block_id == owner, 1, 0)

    def leaving(slot):
        return pltpu.make_async_remote_copy(
            src_ref=leave.at[slot],
            dst_ref=came.at[slot],
            send_sem=core_sem.at[slot],
            recv_sem=came_sem.at[slot],
            device_id={"seq": core},
            device_id_type=MESH_ID,
        )

    def add_came(slot):
        leaving(slot).wait_recv()

        def one(chunk, _):
            partial[slot, chunk] = to_low(
                partial[slot, chunk].astype(jnp.float32)
                + came[slot, span(chunk, 128), :].astype(jnp.float32)
            )
            return 0

        lax.fori_loop(0, 4, one, 0)

    def bucket_sums():
        diag[...] = jnp.zeros_like(diag)

        def one(group, _):
            rows = dz_sum[span(group, 8), :]
            wide = jnp.concatenate([rows, jnp.zeros((8, WIDE - 2 * BLOCK), jnp.float32)], axis=1)
            diag[...] += pltpu.roll(wide, lax.rem(WIDE - 8 * group, WIDE), 1)
            return 0

        lax.fori_loop(0, BLOCK // 8, one, 0)
        line = diag[...]
        row = lax.broadcasted_iota(jnp.int32, (8, WIDE), 0)
        for step in (1, 2, 4):
            line = jnp.where(row // step % 2 == 1, pltpu.roll(line, WIDE - step, 1), line)
        lane = lax.broadcasted_iota(jnp.int32, (8, WIDE), 1)
        bucket_ids = bucket_of(jnp.where(lane >= WIDE - BLOCK, lane - WIDE - BLOCK, lane - BLOCK))
        spot = lax.broadcasted_iota(jnp.int32, (1, 256), 1) - BUCKETS * head
        placed = jnp.zeros((1, 256), jnp.float32)
        for bucket_id in range(BUCKETS):
            chosen = jnp.where(bucket_ids == bucket_id, line, 0.0)
            value = jnp.sum(jnp.sum(chosen, axis=0, keepdims=True), axis=1, keepdims=True)
            placed = jnp.where(spot == bucket_id, value, placed)
        sums[2:3, 0:256] = placed

    def block_products(block_id):
        slot = lax.rem(block_id, 2)
        for one in block_loads(block_id):
            one.wait()

        @pl.when(block_id > 0)
        def _():
            for one in block_loads(jnp.maximum(block_id - 1, 0)):
                one.start()

        def one_part(part, _):
            rows = span(part, 128)

            @pl.when(part < 3)
            def _():
                grad_acc[rows, :] += dot_tn(
                    d_qkv[block_id, :, span(jnp.minimum(part, 2), 128)], rows_buf[slot]
                )

            @pl.when(part > 0)
            def _():
                grad_acc[rows, :] += dot_tn(
                    d_qkvst[block_id, :, span(lax.rem(part, 3), 128)], low_buf[slot]
                )

            return 0

        lax.fori_loop(0, 4, one_part, 0)
        kept_here = lax.rem(block_id, 2) == half
        mine_slot, core_slot = place_in(block_id, place), place_in(block_id, core)

        def one_chunk(chunk, _):
            rows = span(chunk, 128)
            value = to_low(dot_nt(d_qkv[block_id, rows, :], w_qkv[...]))

            @pl.when(kept_here)
            def _():
                partial[mine_slot, chunk] = value

            @pl.when(jnp.logical_not(kept_here))
            def _():
                leave[core_slot, rows, :] = value

            return 0

        lax.fori_loop(0, 4, one_chunk, 0)

        @pl.when(jnp.logical_not(kept_here))
        def _():
            leaving(core_slot).start()

    def back_parts(parts, total, grad, values):
        weights = [jnp.exp(part - total) for part in parts]
        d_weights = [dot_nt(grad, value) for value in values]
        inner = jnp.sum(weights[0] * d_weights[0], axis=-1, keepdims=True)
        for one, other in zip(weights[1:], d_weights[1:]):
            inner = inner + jnp.sum(one * other, axis=-1, keepdims=True)
        d_scores = [to_low(one * (other - inner)) for one, other in zip(weights, d_weights)]
        return [to_low(one) for one in weights], d_scores

    def token_back(block_id):
        prev_id = jnp.maximum(block_id - 1, 0)
        st_key[...] = jnp.zeros_like(st_key)
        st_value[...] = jnp.zeros_like(st_value)

        def one_chunk(chunk, _):
            rows = span(chunk, ROWS)
            query, parts = token_scores(scal, qkv, qkvst, bias, block_id, chunk)
            grad = d_o[block_id, rows, :]
            keys = (qkv[prev_id, :, 128:256], qkv[block_id, :, 128:256], qkvst[block_id, :, 128:256])
            values = (
                qkv[prev_id, :, 256:384], qkv[block_id, :, 256:384], qkvst[block_id, :, 256:384]
            )
            weights, d_scores = back_parts(parts, lse_tok[block_id, rows, :], grad, values)
            d_query = dot_nn(d_scores[0], keys[0])
            d_query = d_query + dot_nn(d_scores[1], keys[1]) + dot_nn(d_scores[2], keys[2])
            d_qkv[block_id, rows, 0:128] = to_low(d_query * SCALE)
            key_acc[prev_id] += dot_tn(d_scores[0], query) * SCALE
            value_acc[prev_id] += dot_tn(weights[0], grad)
            key_acc[block_id] += dot_tn(d_scores[1], query) * SCALE
            value_acc[block_id] += dot_tn(weights[1], grad)
            st_key[...] += dot_tn(d_scores[2], query) * SCALE
            st_value[...] += dot_tn(weights[2], grad)
            dz_sum[rows, 0:BLOCK] += d_scores[0].astype(jnp.float32)
            dz_sum[rows, BLOCK : 2 * BLOCK] += d_scores[1].astype(jnp.float32)
            return 0

        lax.fori_loop(0, CHUNKS, one_chunk, 0)

    token_back(3)
    pl.semaphore_wait(barrier, LINE + 1)
    aside(beside, place // 2).start()
    loads[2].wait()
    loads[0].wait()
    fetched(w_sout, local_sem.at[1])
    fetched(w_back, local_sem.at[2])

    def mixed_copy(block_id, slot, sender, other, seq_to, rank_to):
        return pltpu.make_async_remote_copy(
            src_ref=dos_rows.at[block_id, :, span(other, 128)],
            dst_ref=dos_got.at[block_id, span(sender, 64), :],
            send_sem=send_sem.at[0, block_id, slot],
            recv_sem=recv_sem.at[0, block_id, sender],
            device_id={"seq": seq_to, "tensor": rank_to},
            device_id_type=MESH_ID,
        )

    def grads_copy(block_id, slot, sender, other, seq_to, rank_to):
        return pltpu.make_async_remote_copy(
            src_ref=d_qkvst.at[block_id, span(other, 64), :],
            dst_ref=d_got.at[block_id, sender],
            send_sem=send_sem.at[1, block_id, slot],
            recv_sem=recv_sem.at[1, block_id, sender],
            device_id={"seq": seq_to, "tensor": rank_to},
            device_id_type=MESH_ID,
        )

    def one_block(turn, _):
        block_id = 3 - turn
        grad_out = grad_in[...] + cots[block_id].astype(jnp.float32)
        sums[0:1, :] += jnp.sum(
            grad_out * (states[block_id] - states[block_id + 1]), axis=0, keepdims=True
        ) * gate
        change = to_low((1.0 - gate) * grad_out)
        du_rows[block_id] = change
        dos_rows[block_id] = to_low(dot_nt(change, w_sout[...].reshape(D, D)))
        for slot, (other, seq_to, rank_to) in enumerate(peers):
            mixed_copy(block_id, slot, head, other, seq_to, rank_to).start()
        dos_got[block_id, span(head, 64), :] = dos_rows[block_id, :, span(head, 128)]

        @pl.when(turn > 0)
        def _():
            block_products(block_id + 1)

        @pl.when(turn == 3)
        def _():
            sout_products()

        for slot, (other, seq_to, rank_to) in enumerate(peers):
            mixed_copy(block_id, slot, other, other, seq_to, rank_to).wait_recv()

        def one_chunk(chunk, _):
            rows = span(chunk, ROWS)
            query, parts = state_scores(scal, qkv, qkvst, block_id, chunk)
            grad = dos_got[block_id, rows, :]
            keys = (qkv[block_id, :, 128:256], qkvst[block_id, :, 128:256])
            values = (qkv[block_id, :, 256:384], qkvst[block_id, :, 256:384])
            weights, d_scores = back_parts(parts, lse_st[block_id, rows, :], grad, values)
            d_query = dot_nn(d_scores[0], keys[0]) + dot_nn(d_scores[1], keys[1])
            d_qkvst[block_id, rows, 0:128] = to_low(d_query * SCALE)
            key_acc[block_id] += dot_tn(d_scores[0], query) * SCALE
            value_acc[block_id] += dot_tn(weights[0], grad)
            st_key[...] += dot_tn(d_scores[1], query) * SCALE
            st_value[...] += dot_tn(weights[1], grad)
            return 0

        lax.fori_loop(0, CHUNKS, one_chunk, 0)
        d_qkvst[block_id, :, 128:256] = to_low(st_key[...])
        d_qkvst[block_id, :, 256:384] = to_low(st_value[...])
        for slot, (other, seq_to, rank_to) in enumerate(peers):
            grads_copy(block_id, slot, head, other, seq_to, rank_to).start()
        d_got[block_id, head] = d_qkvst[block_id, span(head, 64), :]

        for step in range(3):

            @pl.when(turn == step)
            def _():
                next(plane_steps)
                if step == 2:
                    next(plane_steps, None)
                    plane_results()

        @pl.when(turn == 3)
        def _():
            next(sout_steps)
            add_came(place_in(2 + half, place))
            bucket_sums()
            next(sout_steps)

        @pl.when(turn < 3)
        def _():
            token_back(block_id - 1)

        d_qkv[block_id, :, 128:256] = to_low(key_acc[block_id])
        d_qkv[block_id, :, 256:384] = to_low(value_acc[block_id])
        @pl.when(turn == 3)
        def _():
            block_products(0)
            next(sout_steps)

        for slot, (other, seq_to, rank_to) in enumerate(peers):
            grads_copy(block_id, slot, other, other, seq_to, rank_to).wait_recv()
        d_low = dot_nn(d_got[block_id, 0], w_back[0, 0].reshape(384, D))
        for other in range(1, LINE):
            d_low = d_low + dot_nn(
                d_got[block_id, other], w_back[other // 2, other % 2].reshape(384, D)
            )
        centered, scale = norm_parts(states[block_id])
        normed = centered * scale
        sums[1:2, :] += jnp.sum(d_low * normed, axis=0, keepdims=True)
        lifted = d_low * gain
        grad_in[...] = gate * grad_out + scale * (
            lifted
            - jnp.mean(lifted, axis=-1, keepdims=True)
            - normed * jnp.mean(lifted * normed, axis=-1, keepdims=True)
        )
        return 0

    lax.fori_loop(0, 4, one_block, 0)
    d_start[...] = grad_in[...]

    def drain(block_id, _):
        for slot, (other, seq_to, rank_to) in enumerate(peers):
            mixed_copy(block_id, slot, head, other, seq_to, rank_to).wait_send()
            grads_copy(block_id, slot, head, other, seq_to, rank_to).wait_send()
        return 0

    lax.fori_loop(0, 4, drain, 0)
    pair_grads[...] = to_low(grad_acc[...])
    for _ in sout_steps:
        pass
    sout_part[...] = to_low(total[0:128, :])
    add_came(place_in(half, place))
    for slot in range(2):
        leaving(slot).wait_send()
    loads[1].wait()
    aside(beside, place // 2).wait_send()
    aside(place, 1 - place // 2).wait_recv()


def backward_chain(
    scal, qkv, d_o, lse_tok, qkvst, lse_st, state_rows, begin, cots, back, kept, vecs, bias,
    extra, hidden, rows_all, state_low, w_qkv, os_rows,
):
    low, wide = jnp.bfloat16, jnp.float32
    shapes = (
        ((4, 64, D), low),
        ((64, D), wide),
        ((8, D), wide),
        ((2, 128, D), wide),
        ((2, 128, D), low),
        ((128, D), low),
        ((2, 4, 128, D), low),
        ((512, D), low),
        ((128, D), low),
    )
    return pl.pallas_call(
        backward_kernel,
        out_shape=[jax.ShapeDtypeStruct(*one) for one in shapes],
        in_specs=vmem_specs(6)
        + any_specs(1)
        + vmem_specs(2)
        + any_specs(2)
        + vmem_specs(2)
        + any_specs(1)
        + vmem_specs(1)
        + any_specs(2)
        + vmem_specs(2),
        out_specs=vmem_specs(3) + any_specs(1) + vmem_specs(5),
        scratch_shapes=[
            pltpu.VMEM((BLOCK, 2 * BLOCK), wide),
            pltpu.VMEM((8, WIDE), wide),
            pltpu.VMEM((4, BLOCK, 384), low),
            pltpu.VMEM((4, STATES, 384), low),
            pltpu.VMEM((2, BLOCK, D), low),
            pltpu.VMEM((2, STATES, D), low),
            pltpu.VMEM((2, BLOCK, D), low),
            pltpu.VMEM((2, BLOCK, D), low),
            pltpu.VMEM((512, D), wide),
            pltpu.VMEM((4, BLOCK, 128), wide),
            pltpu.VMEM((4, BLOCK, 128), wide),
            pltpu.VMEM((STATES, 128), wide),
            pltpu.VMEM((STATES, 128), wide),
            pltpu.VMEM((4, 64, D), low),
            pltpu.VMEM((4, STATES, 128), low),
            pltpu.VMEM((4, LINE, 64, 384), low),
            pltpu.VMEM((64, D), wide),
            pltpu.VMEM((5, 64, D), wide),
            pltpu.VMEM((4, 2, 3, 4, 32, D), low),
            pltpu.VMEM((4, 8, 32, D), low),
            pltpu.VMEM((8, 384, D), low),
            pltpu.VMEM((4, 384, D), low),
            pltpu.VMEM((4, 192, D), low),
            pltpu.VMEM((2, 192, D), low),
            pltpu.VMEM((384, D), wide),
            pltpu.SemaphoreType.DMA((2, 4, LINE - 1)),
            pltpu.SemaphoreType.DMA((2, 4, LINE)),
            pltpu.SemaphoreType.DMA((5,)),
            pltpu.SemaphoreType.DMA((2,)),
            pltpu.SemaphoreType.DMA((10,)),
            pltpu.SemaphoreType.DMA((10,)),
            pltpu.SemaphoreType.DMA((2, 2)),
            pltpu.SemaphoreType.DMA((2,)),
            pltpu.SemaphoreType.DMA((2,)),
            pltpu.VMEM((4, 64, D), low),
            pltpu.VMEM((2, 64, D), low),
            pltpu.SemaphoreType.DMA((10,)),
            pltpu.SemaphoreType.DMA((10,)),
        ],
        compiler_params=pltpu.CompilerParams(
            collective_id=2, has_side_effects=True, vmem_limit_bytes=63 * 1024 * 1024
        ),
        cost_estimate=pl.CostEstimate(flops=40000000000, bytes_accessed=40000000, transcendentals=0),
        name="backward_chain",
    )(
        scal, qkv, d_o, lse_tok, qkvst, lse_st, state_rows, begin, cots, back, kept, vecs, bias,
        extra, hidden, rows_all, state_low, w_qkv, os_rows,
    )


def plane_place():
    place, half, rank = line_place()
    side = lax.axis_index("dp")
    return side, place, half, rank


def plane_index(side, place):
    return 4 * side + place


def row_halves(buf, rows):
    size = rows // 2
    return lambda owner, part: buf.at[owner, pl.ds(part * size, size), :]


def plane_gather(view, send_sem, recv_sem):
    side, place, half, rank = plane_place()
    across, beside = 1 - side, lax.rem(place + 2, 4)
    core = place + 1 - 2 * half
    me = plane_index(side, place)
    at_x, at_y = plane_index(across, place), plane_index(side, beside)
    at_d = plane_index(across, beside)
    to_x, to_y, to_c = {"dp": across}, {"seq": beside}, {"seq": core}

    def piece(owner, part, slot, target):
        one = view(owner, part)
        return pltpu.make_async_remote_copy(
            src_ref=one,
            dst_ref=one,
            send_sem=send_sem.at[slot],
            recv_sem=recv_sem.at[owner, part],
            device_id=target,
            device_id_type=MESH_ID,
        )

    own = [
        piece(me, 0, 0, to_x), piece(me, 1, 1, to_y), piece(me, 1, 2, to_x), piece(me, 0, 3, to_y),
        piece(me, 0, 4, to_c), piece(me, 1, 5, to_c),
    ]
    on_x0, on_y1 = piece(at_x, 0, 6, to_y), piece(at_y, 1, 7, to_x)
    came = [
        (piece(owner, part, 0, to_c), piece(owner, part, slot, to_c))
        for owner, part, slot in (
            (at_x, 0, 8), (at_y, 1, 9), (at_x, 1, 10), (at_y, 0, 11), (at_d, 0, 12), (at_d, 1, 13)
        )
    ]
    core_came = [
        piece(owner, part, 0, to_c)
        for owner in (
            plane_index(side, core),
            plane_index(across, core),
            plane_index(side, lax.rem(core + 2, 4)),
            plane_index(across, lax.rem(core + 2, 4)),
        )
        for part in (0, 1)
    ]
    yield
    for one in own:
        one.start()
    yield
    came[0][0].wait_recv()
    on_x0.start()
    came[1][0].wait_recv()
    on_y1.start()
    came[0][1].start()
    came[1][1].start()
    yield
    for index in (2, 3):
        came[index][0].wait_recv()
        came[index][1].start()
    yield
    for index in (4, 5):
        came[index][0].wait_recv()
        came[index][1].start()
    yield
    for one in core_came:
        one.wait_recv()
    for one in own + [on_x0, on_y1] + [two for _, two in came]:
        one.wait_send()


def run_all(*steps):
    waiting = list(steps)
    while waiting:
        for one in list(waiting):
            try:
                next(one)
            except StopIteration:
                waiting.remove(one)


def plane_scatter(part, core_got, near_got, far_got, total, rows, send_sem, recv_sem):
    side, place, half, rank = plane_place()
    across, beside = 1 - side, lax.rem(place + 2, 4)
    core = place + 1 - 2 * half
    me = plane_index(side, place)
    at_x, at_y = plane_index(across, place), plane_index(side, beside)
    at_d = plane_index(across, beside)
    size = rows // 2
    halves = (pl.ds(0, size), pl.ds(size, size))

    def moved(source, target_ref, slot, target):
        return pltpu.make_async_remote_copy(
            src_ref=source,
            dst_ref=target_ref,
            send_sem=send_sem.at[slot],
            recv_sem=recv_sem.at[slot],
            device_id=target,
            device_id_type=MESH_ID,
        )

    order = (at_d, at_x, at_y, me)
    swapped = (
        plane_index(across, lax.rem(core + 2, 4)),
        plane_index(across, core),
        plane_index(side, lax.rem(core + 2, 4)),
        plane_index(side, core),
    )
    def add_into(owner, view, other):
        part[owner, view, :] = to_low(
            part[owner, view, :].astype(jnp.float32) + other.astype(jnp.float32)
        )

    near = [
        moved(part.at[at_d, halves[0], :], near_got.at[0], 4, {"dp": across}),
        moved(part.at[at_d, halves[1], :], near_got.at[1], 5, {"seq": beside}),
        moved(part.at[at_x, halves[0], :], near_got.at[2], 6, {"dp": across}),
        moved(part.at[at_y, halves[1], :], near_got.at[3], 7, {"seq": beside}),
    ]
    first = [
        moved(part.at[owner], core_got.at[slot], slot, {"seq": core})
        for slot, owner in enumerate(swapped)
    ]
    far = [
        moved(part.at[at_y, halves[0], :], far_got.at[0], 8, {"seq": beside}),
        moved(part.at[at_x, halves[1], :], far_got.at[1], 9, {"dp": across}),
    ]
    yield
    for one in first:
        one.start()
    for slot, owner in enumerate(order):
        first[slot].wait_recv()
        for view in halves:
            add_into(owner, view, core_got[slot, view, :])
        if slot == 0:
            near[0].start()
            near[1].start()
        if slot == 1:
            near[2].start()
        if slot == 2:
            near[3].start()
    yield
    near[0].wait_recv()
    add_into(at_y, halves[0], near_got[0])
    far[0].start()
    near[1].wait_recv()
    add_into(at_x, halves[1], near_got[1])
    far[1].start()
    yield
    near[2].wait_recv()
    add_into(me, halves[0], near_got[2])
    near[3].wait_recv()
    add_into(me, halves[1], near_got[3])
    yield
    for slot, view in enumerate(halves):
        far[slot].wait_recv()
        total[view, :] = part[me, view, :].astype(jnp.float32) + far_got[slot].astype(jnp.float32)
    for one in first + near + far:
        one.wait_send()


def group_peers():
    place, half, rank = line_place()
    here = 4 * place + rank
    peers = []
    for step in range(1, 16):
        other = lax.rem(here + step, 16)
        peers.append((other, other // 4, lax.rem(other, 4)))
    return here, peers


def greet(peers):
    side = lax.axis_index("dp")
    barrier = pltpu.get_barrier_semaphore()
    for _, seq_to, rank_to in peers:
        pl.semaphore_signal(
            barrier, inc=1, device_id={"seq": seq_to, "tensor": rank_to}, device_id_type=MESH_ID
        )
    pl.semaphore_signal(barrier, inc=1, device_id={"dp": 1 - side}, device_id_type=MESH_ID)
    pl.semaphore_wait(barrier, len(peers) + 1)


def middle_kernel(
    mixed, tokens, kept, spread, cot_hbm, vecs,
    hidden, d_hidden, d_line, sums, extra, ff_grads,
    mixed_rows, mid_all, gl_all, dpre_all, work, core_got, near_got, far_got, total, d_rows,
    d_low, w_out, up, down, cot_all,
    send_sem, recv_sem, ring_send, ring_recv, sum_send, sum_recv, back_send, back_recv, local_sem,
):
    low, wide = jnp.bfloat16, jnp.float32
    side, place, half, rank = plane_place()
    mine = place // 2
    head = 2 * rank + half
    across, beside = 1 - side, lax.rem(place + 2, 4)
    core = place + 1 - 2 * half
    core_beside = lax.rem(core + 2, 4)
    me = plane_index(side, place)
    at_x, at_y = plane_index(across, place), plane_index(side, beside)
    at_d = plane_index(across, beside)
    me_c, x_c = plane_index(side, core), plane_index(across, core)
    y_c, d_c = plane_index(side, core_beside), plane_index(across, core_beside)
    to_x, to_y, to_c = {"dp": across}, {"seq": beside}, {"seq": core}
    here, peers = group_peers()
    fetch_pieces(kept, 48, 32, w_out, local_sem.at[0])
    ff_own = up.shape[1]
    first = spread.shape[1] - 2 * ff_own
    loads = [
        pltpu.make_async_copy(spread.at[:, pl.ds(first, ff_own), :], up, local_sem.at[1]),
        pltpu.make_async_copy(spread.at[:, pl.ds(first + ff_own, ff_own), :], down, local_sem.at[2]),
        pltpu.make_async_copy(cot_hbm, cot_all, local_sem.at[3]),
    ]
    for one in loads:
        one.start()
    greet(peers)

    def rows_copy(slot, sender, seq_from, rank_from, seq_to, rank_to):
        return pltpu.make_async_remote_copy(
            src_ref=mixed.at[seq_to, span(rank_to, 128), :],
            dst_ref=mixed_rows.at[
                seq_from // 2, :, span(2 * rank_from + lax.rem(seq_from, 2), 128)
            ],
            send_sem=send_sem.at[slot],
            recv_sem=recv_sem.at[sender],
            device_id={"seq": seq_to, "tensor": rank_to},
            device_id_type=MESH_ID,
        )

    for slot, (_, seq_to, rank_to) in enumerate(peers):
        rows_copy(slot, here, place, rank, seq_to, rank_to).start()
    mixed_rows[mine, :, span(head, 128)] = mixed[place, span(rank, 128), :]
    fetched(w_out, local_sem.at[0])
    for slot, (other, seq_to, rank_to) in enumerate(peers):
        rows_copy(slot, other, seq_to, rank_to, seq_to, rank_to).wait_recv()
    gain = vecs[2:3, :]

    def project(which, _):
        added = dot_nn(mixed_rows[which], w_out[...].reshape(D, D)) + tokens[which].astype(wide)
        hidden[which] = added
        centered, scale = norm_parts(added)
        mid_all[me, span(which, 128), :] = to_low(centered * scale * gain)
        return 0

    lax.fori_loop(0, 2, project, 0)

    def piece(owner, part, slot, target):
        view = mid_all.at[owner, pl.ds(part * 128, 128), :]
        return pltpu.make_async_remote_copy(
            src_ref=view,
            dst_ref=view,
            send_sem=ring_send.at[slot],
            recv_sem=ring_recv.at[owner, part],
            device_id=target,
            device_id_type=MESH_ID,
        )

    own = [
        piece(me, 0, 0, to_x), piece(me, 1, 1, to_y), piece(me, 1, 2, to_x), piece(me, 0, 3, to_y),
        piece(me, 0, 4, to_c), piece(me, 1, 5, to_c),
    ]
    on_x0, on_y1 = piece(at_x, 0, 6, to_y), piece(at_y, 1, 7, to_x)
    to_core = [
        piece(at_x, 0, 8, to_c), piece(at_y, 1, 9, to_c), piece(at_x, 1, 10, to_c),
        piece(at_y, 0, 11, to_c), piece(at_d, 0, 12, to_c), piece(at_d, 1, 13, to_c),
    ]
    wait_of = {
        (name, part): piece(owner, part, 0, to_c)
        for name, owner in (
            ("x", at_x), ("y", at_y), ("d", at_d), ("mc", me_c), ("xc", x_c), ("yc", y_c), ("dc", d_c)
        )
        for part in (0, 1)
    }

    def moved(source, target_ref, slot, target):
        return pltpu.make_async_remote_copy(
            src_ref=source,
            dst_ref=target_ref,
            send_sem=sum_send.at[slot],
            recv_sem=sum_recv.at[slot],
            device_id=target,
            device_id_type=MESH_ID,
        )

    views = (pl.ds(0, 128), pl.ds(128, 128))
    swap = [
        moved(work.at[owner], core_got.at[slot], slot, to_c)
        for slot, owner in enumerate((d_c, x_c, y_c, me_c))
    ]
    near = [
        moved(work.at[at_d, views[0], :], near_got.at[0], 4, to_x),
        moved(work.at[at_d, views[1], :], near_got.at[1], 5, to_y),
        moved(work.at[at_x, views[0], :], near_got.at[2], 6, to_x),
        moved(work.at[at_y, views[1], :], near_got.at[3], 7, to_y),
    ]
    far = [
        moved(work.at[at_y, views[0], :], far_got.at[0], 8, to_y),
        moved(work.at[at_x, views[1], :], far_got.at[1], 9, to_x),
    ]

    def add_into(owner, view, other):
        work[owner, view, :] = to_low(work[owner, view, :].astype(wide) + other.astype(wide))

    def add_core(slot, owner):
        swap[slot].wait_recv()
        for view in views:
            add_into(owner, view, core_got[slot, view, :])

    for one in own:
        one.start()
    loads[0].wait()
    loads[1].wait()
    loads[2].wait()
    order = (
        (me, 0), (me, 1), (me_c, 0), (me_c, 1), (at_x, 0), (at_y, 1), (x_c, 0), (y_c, 1),
        (at_x, 1), (at_y, 0), (x_c, 1), (y_c, 0), (at_d, 0), (at_d, 1), (d_c, 0), (d_c, 1),
    )

    def before_four():
        swap[3].start()
        wait_of["x", 0].wait_recv()
        on_x0.start()
        to_core[0].start()
        wait_of["y", 1].wait_recv()
        on_y1.start()
        to_core[1].start()

    def before_eight():
        wait_of["x", 1].wait_recv()
        to_core[2].start()
        wait_of["y", 0].wait_recv()
        to_core[3].start()

    def before_eleven():
        swap[1].start()
        wait_of["yc", 0].wait_recv()

    def before_twelve():
        swap[2].start()
        wait_of["d", 0].wait_recv()
        to_core[4].start()
        wait_of["d", 1].wait_recv()
        to_core[5].start()

    def before_fourteen():
        add_core(1, at_x)
        near[2].start()
        add_core(2, at_y)
        near[3].start()
        wait_of["dc", 0].wait_recv()

    ahead = {
        2: wait_of["mc", 0].wait_recv,
        3: wait_of["mc", 1].wait_recv,
        4: before_four,
        6: wait_of["xc", 0].wait_recv,
        7: wait_of["yc", 1].wait_recv,
        8: before_eight,
        10: wait_of["xc", 1].wait_recv,
        11: before_eleven,
        12: before_twelve,
        14: before_fourteen,
        15: wait_of["dc", 1].wait_recv,
    }

    def one_chunk(turn, _):
        for value, action in ahead.items():

            @pl.when(turn == value)
            def _():
                action()

        owner, which = order[15]
        for index in range(15):
            owner = jnp.where(turn == index, order[index][0], owner)
            which = jnp.where(turn == index, order[index][1], which)
        up_rows = up[...].reshape(4 * ff_own, D)
        down_rows = down[...].reshape(4 * ff_own, D)
        rows = span(which, 128)
        pre = dot_nt(mid_all[owner, rows, :], up_rows)
        square = pre * pre
        bend = jnp.tanh(GELU_SCALE * (pre + 0.044715 * (pre * square)))
        gl_all[owner, rows, :] = to_low(0.5 * pre * (1.0 + bend))
        slope = 0.5 * (1.0 + bend) + 0.5 * pre * (1.0 - bend * bend) * (
            GELU_SCALE * (1.0 + 3.0 * 0.044715 * square)
        )
        grad = to_low(dot_nt(cot_all[owner, rows, :], down_rows) * slope)
        dpre_all[owner, rows, :] = grad
        work[owner, rows, :] = to_low(dot_nn(grad, up_rows))
        return 0

    lax.fori_loop(0, 16, one_chunk, 0)
    swap[0].start()
    add_core(0, at_d)
    near[0].start()
    near[1].start()
    add_core(3, me)

    def grads(index, _):
        quarter, kind = index // 2, lax.rem(index, 2)
        columns = span(quarter, 128)

        @pl.when(kind == 0)
        def _():
            def add(owner, acc):
                return acc + dot_tn(dpre_all[owner, :, columns], mid_all[owner])

            ff_grads[quarter, 0] = to_low(lax.fori_loop(0, 8, add, jnp.zeros((128, D), wide)))

        @pl.when(kind == 1)
        def _():
            def add(owner, acc):
                return acc + dot_tn(gl_all[owner, :, columns], cot_all[owner])

            ff_grads[quarter, 1] = to_low(lax.fori_loop(0, 8, add, jnp.zeros((128, D), wide)))

        return 0

    lax.fori_loop(0, NEAR_GRADS, grads, 0)
    near[0].wait_recv()
    add_into(at_y, views[0], near_got[0])
    far[0].start()
    near[1].wait_recv()
    add_into(at_x, views[1], near_got[1])
    far[1].start()
    near[2].wait_recv()
    add_into(me, views[0], near_got[2])
    near[3].wait_recv()
    add_into(me, views[1], near_got[3])

    def outward(owner, _):
        down_rows = down[...].reshape(4 * ff_own, D)
        for which in range(2):
            rows = pl.ds(128 * which, 128)
            extra[owner, rows, :] = to_low(dot_nn(gl_all[owner, rows, :], down_rows))
        return 0

    lax.fori_loop(0, 8, outward, 0)
    lax.fori_loop(NEAR_GRADS, FAR_GRADS, grads, 0)
    for slot, view in enumerate(views):
        far[slot].wait_recv()
        total[view, :] = work[me, view, :].astype(wide) + far_got[slot].astype(wide)
    sums[...] = jnp.zeros_like(sums)

    def back(which, _):
        rows = span(which, 128)
        grad = total[rows, :]
        centered, scale = norm_parts(hidden[which])
        normed = centered * scale
        sums[0:1, :] += jnp.sum(grad * normed, axis=0, keepdims=True)
        lifted = grad * gain
        row_grad = cot_all[me, rows, :].astype(wide) + scale * (
            lifted
            - jnp.mean(lifted, axis=-1, keepdims=True)
            - normed * jnp.mean(lifted * normed, axis=-1, keepdims=True)
        )
        d_hidden[which] = row_grad
        d_low[which] = to_low(row_grad)
        d_rows[which] = to_low(dot_nt(to_low(row_grad), w_out[...].reshape(D, D)))
        return 0

    lax.fori_loop(0, 2, back, 0)

    def line_copy(slot, sender, seq_from, rank_from, seq_to, rank_to):
        return pltpu.make_async_remote_copy(
            src_ref=d_rows.at[seq_to // 2, :, span(2 * rank_to + lax.rem(seq_to, 2), 128)],
            dst_ref=d_line.at[seq_from, span(rank_from, 128), :],
            send_sem=back_send.at[slot],
            recv_sem=back_recv.at[sender],
            device_id={"seq": seq_to, "tensor": rank_to},
            device_id_type=MESH_ID,
        )

    for slot, (_, seq_to, rank_to) in enumerate(peers):
        line_copy(slot, here, place, rank, seq_to, rank_to).start()
    d_line[place, span(rank, 128), :] = d_rows[mine, :, span(head, 128)]
    lax.fori_loop(FAR_GRADS, 8, grads, 0)
    for index in range(LINE):
        columns = pl.ds(128 * index, 128)
        part = dot_tn(mixed_rows[0, :, columns], d_low[0]) + dot_tn(
            mixed_rows[1, :, columns], d_low[1]
        )
        part = to_low(part)
        for block in range(4):
            extra[
                4 * (index % 2) + block, 256 + 32 * (index // 2) : 288 + 32 * (index // 2), :
            ] = part[32 * block : 32 * block + 32, :]
    for slot, (other, seq_to, rank_to) in enumerate(peers):
        line_copy(slot, other, seq_to, rank_to, seq_to, rank_to).wait_recv()
    for slot, (_, seq_to, rank_to) in enumerate(peers):
        rows_copy(slot, here, place, rank, seq_to, rank_to).wait_send()
        line_copy(slot, here, place, rank, seq_to, rank_to).wait_send()
    for one in own + [on_x0, on_y1] + to_core + swap + near + far:
        one.wait_send()


GELU_SCALE = 0.7978845608028654
NEAR_GRADS = 3
FAR_GRADS = 4


def middle(mixed, tokens, kept, spread, cot_all, vecs):
    low, wide = jnp.bfloat16, jnp.float32
    ff_own = (spread.shape[1] - SPREAD_FIRST) // 2
    shapes = (
        ((2, 128, D), wide),
        ((2, 128, D), wide),
        ((4, BLOCK, 128), low),
        ((8, D), wide),
        ((8, 384, D), low),
        ((4, 2, ff_own, D), low),
    )
    dma = pltpu.SemaphoreType.DMA
    return pl.pallas_call(
        middle_kernel,
        out_shape=[jax.ShapeDtypeStruct(*one) for one in shapes],
        in_specs=vmem_specs(2) + any_specs(3) + vmem_specs(1),
        out_specs=vmem_specs(6),
        scratch_shapes=[
            pltpu.VMEM((2, 128, D), low),
            pltpu.VMEM((8, 256, D), low),
            pltpu.VMEM((8, 256, 4 * ff_own), low),
            pltpu.VMEM((8, 256, 4 * ff_own), low),
            pltpu.VMEM((8, 256, D), low),
            pltpu.VMEM((4, 256, D), low),
            pltpu.VMEM((4, 128, D), low),
            pltpu.VMEM((2, 128, D), low),
            pltpu.VMEM((256, D), wide),
            pltpu.VMEM((2, 128, D), low),
            pltpu.VMEM((2, 128, D), low),
            pltpu.VMEM((4, 8, 32, D), low),
            pltpu.VMEM((4, ff_own, D), low),
            pltpu.VMEM((4, ff_own, D), low),
            pltpu.VMEM((8, 256, D), low),
            dma((15,)), dma((16,)), dma((14,)), dma((8, 2)), dma((10,)), dma((10,)), dma((15,)),
            dma((16,)), dma((4,)),
        ],
        compiler_params=pltpu.CompilerParams(
            collective_id=3, has_side_effects=True, vmem_limit_bytes=VMEM_LIMIT
        ),
        cost_estimate=pl.CostEstimate(
            flops=60000000000, bytes_accessed=60000000, transcendentals=0
        ),
        name="middle",
    )(mixed, tokens, kept, spread, cot_all, vecs)


SPREAD_FIRST = 0


WIDE = 2048


def opening_kernel(
    tokens, w_query, w_key, w_value, w_sout, w_out, begin, vecs, marks_own,
    rows_all, qkv, kept, table, marks, w_qkv,
    begin_rows, bias_rows, stage, send_sem, core_sem, recv_sem, piece_send, piece_recv, ring_send, ring_recv,
    mark_send, mark_recv, local_sem,
):
    side, place, half, rank = plane_place()
    mine = place // 2
    core = place + 1 - 2 * half
    other = lax.rem(place + 2, 4)
    me = plane_index(side, place)
    extra = 80
    fetch_columns((w_query, w_key, w_value), w_qkv, local_sem.at[0])
    loads = [
        pltpu.make_async_copy(
            w_sout.at[span(me, 32), :], kept.at[me, pl.ds(80 * rank, 32), :], local_sem.at[1]
        ),
        pltpu.make_async_copy(
            w_out.at[span(me, 32), :], kept.at[me, pl.ds(80 * rank + 48, 32), :], local_sem.at[3]
        ),
        pltpu.make_async_copy(begin.at[span(me, 16), :], begin_rows, local_sem.at[2]),
    ]
    for one in loads:
        one.start()
    barrier = pltpu.get_barrier_semaphore()
    greeted = [{"tensor": lax.rem(rank + step, 4)} for step in (1, 2, 3)]
    seats = [lax.rem(place + step, 4) for step in (1, 2, 3)]
    greeted += [{"seq": one} for one in seats] + [{"dp": 1 - side}]
    for target in greeted:
        pl.semaphore_signal(barrier, inc=1, device_id=target, device_id_type=MESH_ID)
    gain = vecs[3:4, :]

    def normed(which):
        centered, scale = norm_parts(tokens[which].astype(jnp.float32))
        return to_low(centered * scale * gain)

    def moved(block_id, origin, sem, target):
        view = rows_all.at[block_id, span(origin, 128), :]
        return pltpu.make_async_remote_copy(
            src_ref=view,
            dst_ref=view,
            send_sem=sem,
            recv_sem=recv_sem.at[block_id, origin],
            device_id=target,
            device_id_type=MESH_ID,
        )

    stage[...] = normed(1 - mine)
    marks[place] = marks_own[...]
    pl.semaphore_wait(barrier, 7)
    aside = pltpu.make_async_remote_copy(
        src_ref=stage,
        dst_ref=rows_all.at[place, span(rank, 128), :],
        send_sem=send_sem.at[0, 0, 3],
        recv_sem=recv_sem.at[place, rank],
        device_id={"seq": other},
        device_id_type=MESH_ID,
    )
    aside.start()

    def mark_move(slot, origin, target):
        return pltpu.make_async_remote_copy(
            src_ref=marks.at[origin],
            dst_ref=marks.at[origin],
            send_sem=mark_send.at[slot],
            recv_sem=mark_recv.at[origin],
            device_id={"seq": target},
            device_id_type=MESH_ID,
        )

    def piece_move(slot, origin, target):
        view = kept.at[me, span(origin, extra), :]
        return pltpu.make_async_remote_copy(
            src_ref=view,
            dst_ref=view,
            send_sem=piece_send.at[slot],
            recv_sem=piece_recv.at[origin],
            device_id=target,
            device_id_type=MESH_ID,
        )

    for one in loads:
        one.wait()
    kept[me, pl.ds(pl.multiple_of(80 * rank + 32, 16), 16), :] = to_low(begin_rows[...])
    for slot in range(3):
        piece_move(slot, rank, greeted[slot]).start()
    for slot, target in enumerate(seats):
        mark_move(slot, place, target).start()
    rows_all[place, span(rank, 128), :] = normed(mine)
    right, left = {"tensor": lax.rem(rank + 1, 4)}, {"tensor": lax.rem(rank + 3, 4)}
    blocks = (place, other)

    def pass_on(which, distance):
        block_id = blocks[which]

        @pl.when((rank < 3) & (rank >= distance))
        def _():
            moved(block_id, jnp.maximum(rank - distance, 0), send_sem.at[which, distance, 0], right).start()

        @pl.when((rank > 0) & (rank + distance <= 3))
        def _():
            moved(block_id, jnp.minimum(rank + distance, 3), send_sem.at[which, distance, 1], left).start()

    def pass_done(which, distance):
        block_id = blocks[which]

        @pl.when((rank < 3) & (rank >= distance))
        def _():
            moved(block_id, jnp.maximum(rank - distance, 0), send_sem.at[which, distance, 0], right).wait_send()

        @pl.when((rank > 0) & (rank + distance <= 3))
        def _():
            moved(block_id, jnp.minimum(rank + distance, 3), send_sem.at[which, distance, 1], left).wait_send()

    def project(block_id, origin):
        view = span(origin, 128)
        qkv[block_id, view, :] = to_low(dot_nn(rows_all[block_id, view, :], w_qkv[...]))

    def rows_steps():
        pass_on(0, 0)
        fetched(w_qkv, local_sem.at[0])
        moved(place, rank, core_sem.at[0, rank], {"seq": core}).start()
        project(place, rank)
        moved(other, rank, send_sem.at[0, 0, 3], {"seq": other}).wait_recv()
        pass_on(1, 0)
        moved(other, rank, core_sem.at[1, rank], {"seq": core}).start()
        project(other, rank)
        yield
        for distance in (1, 2, 3):
            for which in (0, 1):
                block_id = blocks[which]
                for way, ok, origin in (
                    (0, rank >= distance, jnp.maximum(rank - distance, 0)),
                    (1, rank + distance <= 3, jnp.minimum(rank + distance, 3)),
                ):

                    @pl.when(ok)
                    def _():
                        moved(block_id, origin, send_sem.at[which, distance, way], right).wait_recv()
                        if distance < 3:
                            if way == 0:

                                @pl.when(rank < 3)
                                def _():
                                    moved(
                                        block_id, origin, send_sem.at[which, distance, 0], right
                                    ).start()

                            else:

                                @pl.when(rank > 0)
                                def _():
                                    moved(
                                        block_id, origin, send_sem.at[which, distance, 1], left
                                    ).start()

                        moved(block_id, origin, core_sem.at[which, origin], {"seq": core}).start()
                        project(block_id, origin)

                yield
        for which, block_id in enumerate((core, lax.rem(core + 2, 4))):
            for origin in range(4):
                moved(block_id, origin, core_sem.at[which, origin], {"seq": core}).wait_recv()
                project(block_id, origin)
        for which in (0, 1):
            for distance in (0, 1, 2):
                pass_done(which, distance)
            for origin in range(4):
                moved(blocks[which], origin, core_sem.at[which, origin], {"seq": core}).wait_send()

    def piece_steps():
        for slot in range(3):
            piece_move(slot, lax.rem(rank + slot + 1, 4), greeted[slot]).wait_recv()
        for _ in plane_gather(row_halves(kept, 4 * extra), ring_send, ring_recv):
            yield
        for slot in range(3):
            piece_move(slot, rank, greeted[slot]).wait_send()

    def bias_steps():
        lane = lax.broadcasted_iota(jnp.int32, (8, WIDE), 1)
        bucket_ids = bucket_of(jnp.where(lane >= WIDE - BLOCK, lane - WIDE - BLOCK, lane - BLOCK))
        first = jnp.zeros((8, WIDE), jnp.float32)
        for bucket_id in range(BUCKETS):
            value = jnp.where(
                half == 0,
                vecs[4:5, bucket_id : bucket_id + 1],
                vecs[4:5, BUCKETS + bucket_id : BUCKETS + bucket_id + 1],
            )
            first = jnp.where(bucket_ids == bucket_id, value, first)
        row = lax.broadcasted_iota(jnp.int32, (8, WIDE), 0)
        for step in (1, 2, 4):
            first = jnp.where(row // step % 2 == 1, pltpu.roll(first, step, 1), first)
        bias_rows[...] = first
        yield

        def one(group, _):
            table[span(group, 8), :] = pltpu.roll(bias_rows[...], 8 * group, 1)[:, 0 : 2 * BLOCK]
            return 0

        for part in range(4):
            lax.fori_loop(16 * part, 16 * part + 16, one, 0)
            yield

    run_all(rows_steps(), piece_steps(), bias_steps())
    aside.wait_send()
    for slot, target in enumerate(seats):
        mark_move(slot, place, target).wait_send()
        mark_move(slot, target, target).wait_recv()


def opening(tokens, w_query, w_key, w_value, w_sout, w_out, begin, vecs, marks):
    low, wide = jnp.bfloat16, jnp.float32
    shapes = (
        ((4, BLOCK, D), low),
        ((4, BLOCK, 384), low),
        ((8, 4 * 80, D), low),
        ((BLOCK, 2 * BLOCK), wide),
        ((4, 8, 128), jnp.int32),
        ((D, 384), low),
    )
    dma = pltpu.SemaphoreType.DMA
    outs = pl.pallas_call(
        opening_kernel,
        out_shape=[jax.ShapeDtypeStruct(*one) for one in shapes],
        in_specs=vmem_specs(1)
        + any_specs(6)
        + vmem_specs(2),
        out_specs=vmem_specs(6),
        scratch_shapes=[
            pltpu.VMEM((16, D), wide),
            pltpu.VMEM((8, WIDE), wide),
            pltpu.VMEM((128, D), low),
            dma((2, 4, 4)),
            dma((2, 4)),
            dma((4, 4)),
            dma((3,)),
            dma((4,)),
            dma((14,)),
            dma((8, 2)),
            dma((3,)),
            dma((4,)),
            dma((4,)),
        ],
        compiler_params=pltpu.CompilerParams(
            collective_id=5, has_side_effects=True, vmem_limit_bytes=VMEM_LIMIT
        ),
        cost_estimate=pl.CostEstimate(
            flops=30000000000, bytes_accessed=30000000, transcendentals=0
        ),
        name="opening",
    )(tokens, w_query, w_key, w_value, w_sout, w_out, begin, vecs, marks)
    rows_all, qkv, kept, table, marks, w_qkv = outs
    return rows_all, qkv, kept.reshape(8, 4, 80, D), table, marks, w_qkv


def pair_sum(part, near_got, far_got, result, rows, send_sem, recv_sem):
    side, place, half, rank = plane_place()
    mine = place // 2
    across, beside = 1 - side, 1 - mine
    me = 2 * side + mine
    at_x, at_y, at_d = 2 * across + mine, 2 * side + beside, 2 * across + beside
    to_x, to_y = {"dp": across}, {"seq": lax.rem(place + 2, 4)}
    size = rows // 2
    views = (pl.ds(0, size), pl.ds(size, size))

    def moved(source, target_ref, slot, target):
        return pltpu.make_async_remote_copy(
            src_ref=source,
            dst_ref=target_ref,
            send_sem=send_sem.at[slot],
            recv_sem=recv_sem.at[slot],
            device_id=target,
            device_id_type=MESH_ID,
        )

    def add_into(owner, view, other):
        part[owner, view, :] = to_low(
            part[owner, view, :].astype(jnp.float32) + other.astype(jnp.float32)
        )

    near = [
        moved(part.at[at_d, views[0], :], near_got.at[0], 0, to_x),
        moved(part.at[at_d, views[1], :], near_got.at[1], 1, to_y),
        moved(part.at[at_x, views[0], :], near_got.at[2], 2, to_x),
        moved(part.at[at_y, views[1], :], near_got.at[3], 3, to_y),
    ]
    for one in near:
        one.start()
    yield
    near[0].wait_recv()
    add_into(at_y, views[0], near_got[0])
    far = [
        moved(part.at[at_y, views[0], :], far_got.at[0], 4, to_y),
        moved(part.at[at_x, views[1], :], far_got.at[1], 5, to_x),
    ]
    far[0].start()
    near[1].wait_recv()
    add_into(at_x, views[1], near_got[1])
    far[1].start()
    yield
    near[2].wait_recv()
    add_into(me, views[0], near_got[2])
    near[3].wait_recv()
    add_into(me, views[1], near_got[3])
    for slot, view in enumerate(views):
        far[slot].wait_recv()
        result[me, view, :] = to_low(
            part[me, view, :].astype(jnp.float32) + far_got[slot].astype(jnp.float32)
        )

    def given(owner, which, slot, target):
        view = result.at[owner, views[which], :]
        return moved(view, view, slot, target)

    own = [
        given(me, 0, 6, to_x),
        given(me, 1, 7, to_y),
        given(me, 1, 8, to_x),
        given(me, 0, 9, to_y),
    ]
    for one in own:
        one.start()
    yield
    given(at_x, 0, 6, to_x).wait_recv()
    last = [given(at_x, 0, 10, to_y), given(at_y, 1, 11, to_x)]
    last[0].start()
    given(at_y, 1, 7, to_y).wait_recv()
    last[1].start()
    yield
    given(at_x, 1, 8, to_x).wait_recv()
    given(at_y, 0, 9, to_y).wait_recv()
    given(at_d, 0, 10, to_y).wait_recv()
    given(at_d, 1, 11, to_x).wait_recv()
    for one in near + far + own + last:
        one.wait_send()


PAIR_ROWS = 640


def closing_kernel(
    partial, pair_grads, tokens, d_hidden, vecs, d_start, mlp_sums, state_sums, out_part,
    sout_part,
    inputs_grad, pair_out, sout_out, small_out,
    sums, got, final, cross, cross_got,
    pair_part, pair_near, pair_far,
    z_part, z_got,
    small_z, small_p,
    line_send, line_recv, way_send, way_recv, pair_send, pair_recv, core_sem,
    zs_send, zs_recv, gather_send, gather_recv, small_send, small_recv, local_sem,
):
    loads = [
        pltpu.make_async_copy(source, target, local_sem.at[slot])
        for slot, (source, target) in enumerate(
            (
                (partial, sums),
            )
        )
    ]
    for one in loads:
        one.start()
    side, place, half, rank = plane_place()
    mine = place // 2
    core = place + 1 - 2 * half
    other = lax.rem(place + 2, 4)
    me = plane_index(side, place)
    ranks = [lax.rem(rank + step, 4) for step in (1, 2, 3)]
    spots_of = [lax.rem(me + step, 8) for step in range(1, 8)]
    barrier = pltpu.get_barrier_semaphore()
    for target in ranks:
        pl.semaphore_signal(barrier, inc=1, device_id={"tensor": target}, device_id_type=MESH_ID)
    for target in spots_of:
        pl.semaphore_signal(
            barrier,
            inc=1,
            device_id={"dp": target // 4, "seq": lax.rem(target, 4)},
            device_id_type=MESH_ID,
        )
    gain = vecs[3:4, :]
    right, left = {"tensor": lax.rem(rank + 1, 4)}, {"tensor": lax.rem(rank + 3, 4)}

    def moved(source, target_ref, send, recv, target):
        return pltpu.make_async_remote_copy(
            src_ref=source,
            dst_ref=target_ref,
            send_sem=send,
            recv_sem=recv,
            device_id=target,
            device_id_type=MESH_ID,
        )

    def crossing():
        return moved(cross, cross_got, line_send.at[0], line_recv.at[0], {"seq": other})

    near = rank // 2
    at_end = (rank == 0) | (rank == 3)

    def hop(way, which, target):
        return moved(
            sums.at[which, target],
            got.at[way, which, target],
            way_send.at[which, target],
            way_recv.at[way, which, target],
            {"tensor": lax.rem(rank + 5 - 2 * way, 4)},
        )

    def target_of(way, distance):
        return (1 - way) * (3 - distance) + way * distance

    def pass_first(which):
        @pl.when(at_end)
        def _():
            for distance in range(3):
                hop(near, which, target_of(near, distance)).start()

    def pass_on(way, which, distance):
        @pl.when(jnp.logical_not(at_end))
        def _():
            target = target_of(way, distance)
            hop(way, which, target).wait_recv()
            sums[which, target] = to_low(
                sums[which, target].astype(jnp.float32)
                + got[way, which, target].astype(jnp.float32)
            )
            hop(way, which, target).start()

    def finish(which):
        final[which] = sums[which, rank].astype(jnp.float32)

        @pl.when(rank > 0)
        def _():
            hop(0, which, rank).wait_recv()
            final[which] += got[0, which, rank].astype(jnp.float32)

        @pl.when(rank < 3)
        def _():
            hop(1, which, rank).wait_recv()
            final[which] += got[1, which, rank].astype(jnp.float32)

    def small_over_z(slot, sender, target):
        return moved(
            small_z.at[sender], small_z.at[sender], small_send.at[slot], small_recv.at[sender],
            {"tensor": target},
        )

    def small_over_plane(slot, sender, target):
        return moved(
            small_p.at[sender], small_p.at[sender], small_send.at[3 + slot],
            small_recv.at[4 + sender],
            {"dp": target // 4, "seq": lax.rem(target, 4)},
        )

    def line_steps():
        loads[0].wait()
        for which in (0, 1):
            pass_first(which)
        yield
        for which in (0, 1):
            pass_on(near, which, 0)
            yield
            pass_on(near, which, 1)
            pass_on(1 - near, which, 0)
            yield
            finish(which)
            if which == 0:
                cross[...] = to_low(final[0])
                crossing().start()
            yield
        crossing().wait_recv()
        final[0] = cross_got[...].astype(jnp.float32)
        small_z[rank] = jnp.zeros((8, D), jnp.float32)
        for row, source in enumerate(
            (state_sums[1:2, :], mlp_sums[0:1, :], state_sums[0:1, :], state_sums[2:3, :])
        ):
            small_z[rank, row + 1 : row + 2, :] = source
        for which, row_set in ((1, mine), (0, 1 - mine)):
            grad = final[which]
            centered, scale = norm_parts(tokens[row_set].astype(jnp.float32))
            normed = centered * scale
            small_z[rank, 0:1, :] += jnp.sum(grad * normed, axis=0, keepdims=True)
            lifted = grad * gain
            inputs_grad[row_set] = d_hidden[row_set] + scale * (
                lifted
                - jnp.mean(lifted, axis=-1, keepdims=True)
                - normed * jnp.mean(lifted * normed, axis=-1, keepdims=True)
            )
        for slot, target in enumerate(ranks):
            small_over_z(slot, rank, target).start()
        crossing().wait_send()
        yield
        for slot, target in enumerate(ranks):
            small_over_z(slot, target, target).wait_recv()
        small_p[me] = small_z[0] + small_z[1] + small_z[2] + small_z[3]
        for slot, target in enumerate(spots_of):
            small_over_plane(slot, me, target).start()
        yield
        for slot, target in enumerate(spots_of):
            small_over_plane(slot, target, target).wait_recv()
        acc = small_p[0]
        for target in range(1, 8):
            acc = acc + small_p[target]
        small_out[...] = acc
        for slot, target in enumerate(ranks):
            small_over_z(slot, rank, target).wait_send()
        for slot, target in enumerate(spots_of):
            small_over_plane(slot, me, target).wait_send()
        for which in (0, 1):
            for target in range(4):

                @pl.when(rank != target)
                def _():
                    hop(0, which, target).wait_send()

    def pair_steps():
        for owner in range(3):
            pair_part[owner] = pair_grads[160 * owner : 160 * owner + 160, :]
        pair_part[3, 0:32, :] = pair_grads[480:512, :]
        pair_part[3, 32:96, :] = to_low(d_start[...])
        pair_part[3, 96:160, :] = jnp.zeros((64, D), jnp.bfloat16)
        for _ in pair_sum(
            pair_part, pair_near, pair_far, pair_out.at[half], 160, pair_send, pair_recv
        ):
            yield
        full = moved(
            pair_out.at[half], pair_out.at[half], core_sem.at[0], core_sem.at[1], {"seq": core}
        )
        full.start()
        yield
        moved(
            pair_out.at[1 - half], pair_out.at[1 - half], core_sem.at[0], core_sem.at[1],
            {"seq": core},
        ).wait_recv()
        full.wait_send()

    def sout_steps():
        z_part[:, 0:32, :] = sout_part[...].reshape(4, 32, D)
        z_part[:, 32:64, :] = out_part[...].reshape(4, 32, D)
        out = [
            moved(
                z_part.at[target], z_got.at[rank], zs_send.at[slot], zs_recv.at[rank],
                {"tensor": target},
            )
            for slot, target in enumerate(ranks)
        ]
        for one in out:
            one.start()
        z_got[rank] = z_part[rank]
        yield
        for slot, target in enumerate(ranks):
            moved(
                z_part.at[target], z_got.at[target], zs_send.at[slot], zs_recv.at[target],
                {"tensor": target},
            ).wait_recv()
        acc = z_got[0].astype(jnp.float32)
        for target in range(1, 4):
            acc = acc + z_got[target].astype(jnp.float32)
        sout_out[me] = to_low(acc)
        for _ in plane_gather(row_halves(sout_out, 64), gather_send, gather_recv):
            yield
        for one in out:
            one.wait_send()

    pl.semaphore_wait(barrier, 10)
    run_all(sout_steps(), pair_steps(), line_steps())


def closing(
    partial, pair_grads, tokens, d_hidden, vecs, d_start, mlp_sums, state_sums, out_part, sout_part,
):
    low, wide = jnp.bfloat16, jnp.float32
    shapes = (
        ((2, 128, D), wide),
        ((2, 4, PAIR_ROWS // 4, D), low),
        ((8, 64, D), low),
        ((8, D), wide),
    )
    dma = pltpu.SemaphoreType.DMA
    return pl.pallas_call(
        closing_kernel,
        out_shape=[jax.ShapeDtypeStruct(*one) for one in shapes],
        in_specs=any_specs(1)
        + vmem_specs(9),
        out_specs=vmem_specs(4),
        scratch_shapes=[
            pltpu.VMEM((2, 4, 128, D), low),
            pltpu.VMEM((2, 2, 4, 128, D), low),
            pltpu.VMEM((2, 128, D), wide),
            pltpu.VMEM((128, D), low),
            pltpu.VMEM((128, D), low),
            pltpu.VMEM((4, PAIR_ROWS // 4, D), low),
            pltpu.VMEM((4, PAIR_ROWS // 8, D), low),
            pltpu.VMEM((2, PAIR_ROWS // 8, D), low),
            pltpu.VMEM((4, 64, D), low),
            pltpu.VMEM((4, 64, D), low),
            pltpu.VMEM((4, 8, D), wide),
            pltpu.VMEM((8, 8, D), wide),
            dma((1,)), dma((1,)), dma((2, 4)), dma((2, 2, 4)), dma((12,)), dma((12,)), dma((2,)),
            dma((3,)), dma((4,)), dma((16,)), dma((8, 2)), dma((10,)),
            dma((12,)), dma((1,)),
        ],
        compiler_params=pltpu.CompilerParams(
            collective_id=6, has_side_effects=True, vmem_limit_bytes=VMEM_LIMIT
        ),
        cost_estimate=pl.CostEstimate(
            flops=30000000000, bytes_accessed=30000000, transcendentals=0
        ),
        name="closing",
    )(
        partial, pair_grads, tokens, d_hidden, vecs, d_start, mlp_sums, state_sums, out_part,
        sout_part,
    )


def finish_kernel(
    pair, pair_tail, two, ff, small,
    query, key, value, squery, out, sout, up, down, state, gain_0, gain_1, gain_2, gain_3, biases,
):
    step = pl.program_id(0)
    wide = jnp.float32
    up[...] = ff[0, 0].astype(wide).T
    down[...] = ff[0, 1].astype(wide)
    sout[...] = two[0, 0:32].astype(wide)
    out[...] = two[0, 32:64].astype(wide)
    for which, target in enumerate((query, key, value, squery)):

        @pl.when(step // 2 == which)
        def _():
            target[...] = pair[0].astype(wide).T

    @pl.when(step == 0)
    def _():
        state[...] = pair_tail[...].reshape(128, D).astype(wide)
        for row, target in enumerate((gain_0, gain_1, gain_2, gain_3)):
            target[...] = small[row, :]
        turned = jnp.broadcast_to(small[4:5, 0 : LINE * BUCKETS], (8, LINE * BUCKETS)).T
        rank = lax.axis_index("tensor")
        column = lax.broadcasted_iota(jnp.int32, (BUCKETS, 2), 1)
        found = jnp.zeros((BUCKETS, 2), wide)
        for head in range(LINE):
            part = turned[BUCKETS * head : BUCKETS * head + BUCKETS, 0:2]
            found = jnp.where(column + 2 * rank == head, part, found)
        biases[...] = found


def finish_grads(pair, two, ff, small):
    wide = jnp.float32
    turned = [
        pl.BlockSpec((D, 128), lambda i, w=which: (0, jnp.clip(i - 2 * w, 0, 1)))
        for which in range(4)
    ]
    square = jax.ShapeDtypeStruct((D, 256), wide)
    rows = jax.ShapeDtypeStruct((256, D), wide)
    whole = jax.ShapeDtypeStruct((D, D), wide)
    return pl.pallas_call(
        finish_kernel,
        grid=(8,),
        out_shape=[square] * 4 + [rows] * 2 + [whole] * 2
        + [jax.ShapeDtypeStruct((128, D), wide)]
        + [jax.ShapeDtypeStruct((D,), wide)] * 4
        + [jax.ShapeDtypeStruct((BUCKETS, 2), wide)],
        in_specs=[
            pl.BlockSpec((1, 128, D), lambda i: (i % 2, i // 2, 0)),
            pl.BlockSpec((2, 64, D), lambda i: (0, 8, 0)),
            pl.BlockSpec((1, 64, D), lambda i: (i, 0, 0)),
            pl.BlockSpec((1, 2, 128, D), lambda i: (i, 0, 0, 0)),
            pl.BlockSpec((8, D), lambda i: (0, 0)),
        ],
        out_specs=turned
        + [pl.BlockSpec((32, D), lambda i: (i, 0))] * 2
        + [pl.BlockSpec((D, 128), lambda i: (0, i)), pl.BlockSpec((128, D), lambda i: (i, 0))]
        + [pl.BlockSpec((128, D), lambda i: (0, 0))]
        + [pl.BlockSpec((D,), lambda i: (0,))] * 4
        + [pl.BlockSpec((BUCKETS, 2), lambda i: (0, 0))],
        compiler_params=pltpu.CompilerParams(vmem_limit_bytes=VMEM_LIMIT),
        name="finish_grads",
    )(pair, pair, two, ff, small)


def swap_seq(value):
    return lax.all_to_all(value, "seq", 0, 0, tiled=False)


def line_body(
    inputs,
    seg_starts,
    lengths,
    init_state,
    attn_gain,
    state_gain,
    mlp_gain,
    w_query,
    w_key,
    w_value,
    w_out,
    w_squery,
    w_sout,
    w_up,
    w_down,
    rel_bias,
    gate_bias,
    out_cot,
    state_cot,
):
    low, wide = jnp.bfloat16, jnp.float32
    place = lax.axis_index("seq")
    half = lax.rem(place, 2)
    mine = place // 2
    plane = ("dp", "seq")
    spot = 4 * lax.axis_index("dp") + place
    gate_value = jax.nn.sigmoid(gate_bias)
    vecs = jnp.stack(
        [
            state_gain,
            gate_value,
            mlp_gain,
            attn_gain,
            jnp.pad(jnp.concatenate([rel_bias[:, 0], rel_bias[:, 1]]), (0, D - 2 * BUCKETS)),
        ]
        + [jnp.zeros_like(gate_value)] * 3
    )
    marks = jnp.concatenate([seg_starts[:, 0], lengths, jnp.zeros((4,), jnp.int32)])
    marks = jnp.broadcast_to(marks[:, None], (8, 128))
    cot_used = lax.all_gather(out_cot.reshape(256, D), plane, axis=0, tiled=True)
    rows_all, qkv, kept, bias, marks, w_qkv = opening(
        inputs, w_query, w_key, w_value, w_sout, w_out, init_state, vecs, marks
    )

    ff_own = w_up.shape[1] // 8
    piece_of = lambda weight: lax.dynamic_slice_in_dim(weight, spot * 32, 32, 1).T
    back_own = jnp.stack(
        [
            piece_of(w_squery),
            piece_of(w_key),
            piece_of(w_value),
        ]
    )
    pieces = jnp.concatenate(
        [
            lax.dynamic_slice_in_dim(w_up, spot * ff_own, ff_own, 1).T,
            lax.dynamic_slice_in_dim(w_down, spot * ff_own, ff_own, 0),
        ],
        axis=0,
    )
    qkv, pieces, cot_used, back_own = lax.optimization_barrier(
        (qkv, pieces, cot_used, back_own)
    )
    spread = lax.all_gather(pieces, "tensor", axis=0, tiled=True).reshape(4, 2 * ff_own, D)
    mixed, lse_tok, state_rows, state_low, qkvst, lse_st, os_rows, cots, back = forward_chain(
        marks, qkv, kept, w_squery, w_qkv, vecs, bias, state_cot.reshape(4, 64, D), back_own
    )
    hidden_in, grad_hidden, d_mixed, mlp_sums, extra, ff_grads = middle(
        mixed, inputs, kept, spread, cot_used.reshape(8, 256, D), vecs
    )
    d_mixed, ff_grads = lax.optimization_barrier((d_mixed, ff_grads))
    ff_sum = lax.psum_scatter(
        ff_grads.reshape(ff_grads.shape[2] * 8, D), "tensor", scatter_dimension=0, tiled=True
    )
    (
        _, d_start, sums, state_out, tokens_out, out_part, partial, pair_grads, sout_part,
    ) = backward_chain(
        marks, qkv, d_mixed, lse_tok, qkvst, lse_st, state_rows, init_state, cots,
        back, kept, vecs, bias, extra, hidden_in, rows_all, state_low, w_qkv,
        os_rows.reshape(256, D),
    )
    partial, ff_sum = lax.optimization_barrier((partial, ff_sum))
    ff_total = lax.all_gather(ff_sum, plane, axis=0, tiled=True).reshape(8, 2, ff_own, D)
    inputs_grad, pair, two_grads, small = closing(
        partial, pair_grads, inputs, grad_hidden, vecs, d_start, mlp_sums, sums, out_part,
        sout_part,
    )
    pair = pair.reshape(2, PAIR_ROWS, D)
    (
        query_grad, key_grad, value_grad, squery_grad, out_grad, sout_grad, up_grad, down_grad,
        state_grad, attn_gain_grad, state_gain_grad, mlp_gain_grad, gate_grad, bias_grad,
    ) = finish_grads(pair, two_grads, ff_total, small)
    return (
        tokens_out,
        state_out[:, None],
        inputs_grad,
        state_grad,
        attn_gain_grad,
        state_gain_grad,
        mlp_gain_grad,
        query_grad,
        key_grad,
        value_grad,
        out_grad,
        squery_grad,
        sout_grad,
        up_grad,
        down_grad,
        bias_grad,
        gate_grad,
    )


def solution(mesh):
    return jax.shard_map(
        chosen_body(mesh),
        mesh=mesh,
        in_specs=(
            P("dp", ("seq", "tensor"), None),
            P("dp", "seq"),
            P("dp"),
            P("tensor", None),
            P(),
            P(),
            P(),
            P(None, "tensor"),
            P(None, "tensor"),
            P(None, "tensor"),
            P("tensor", None),
            P(None, "tensor"),
            P("tensor", None),
            P(None, "tensor"),
            P("tensor", None),
            P(None, "tensor"),
            P(),
            P("dp", ("seq", "tensor"), None),
            P("dp", "seq", "tensor", None),
        ),
        out_specs=(
            P("dp", ("seq", "tensor"), None),
            P("dp", "seq", "tensor", None),
            P("dp", ("seq", "tensor"), None),
            P("tensor", None),
            P(),
            P(),
            P(),
            P(None, "tensor"),
            P(None, "tensor"),
            P(None, "tensor"),
            P("tensor", None),
            P(None, "tensor"),
            P("tensor", None),
            P(None, "tensor"),
            P("tensor", None),
            P(None, "tensor"),
            P(),
        ),
        check_vma=False,
    )
```

```python
import jax
import jax.numpy as jnp
from jax import lax
from jax.experimental import pallas as pl
from jax.experimental.pallas import tpu as pltpu
from jax.sharding import PartitionSpec as P

D = 1024
HEAD_DIM = 128
STATES = 512
BLOCK = 512
SEG = 256
BUCKETS = 32


norm_eps = 1e-06
masked_score = -1e30
bucket_edges = (12, 16, 23, 32, 46, 64, 91)


def passed_along(value, axis, steps):
    count = lax.axis_size(axis)
    leading, last = (max(0, -steps), min(count, count - steps))
    return lax.ppermute(value, axis, [(source, source + steps) for source in range(leading, last)])


def bucket_of(relative):
    distance = jnp.abs(relative)
    far_bucket = 8 + sum(((distance >= boundary).astype(jnp.int32) for boundary in bucket_edges))
    near_far = jnp.where(distance < 8, distance, far_bucket)
    return near_far + 16 * (relative > 0).astype(jnp.int32)


def token_mask(seg_start, seq_length, block_index):
    positions = jnp.arange(BLOCK)
    offset = block_index * BLOCK
    prev_valid = (block_index > 0) & (offset - BLOCK + positions < seq_length)
    cur_valid = offset + positions < seq_length
    inside = (positions >= seg_start) & (positions < seg_start + SEG)
    prev_mask = (positions[None, :] > positions[:, None]) & prev_valid[None, :]
    cur_mask = (
        (positions[None, :] <= positions[:, None]) | inside[None, :] & inside[:, None]
    ) & cur_valid[None, :]
    state_mask = jnp.ones((BLOCK, STATES), jnp.bool_)
    return jnp.concatenate([prev_mask, cur_mask, state_mask], axis=1)


def state_mask_of(valid_blk):
    batch_count = valid_blk.shape[0]
    block_part = jnp.broadcast_to(valid_blk[:, None, :], (batch_count, STATES, BLOCK))
    return jnp.concatenate([block_part, jnp.ones((batch_count, STATES, STATES), jnp.bool_)], axis=2)


def layer_norm(values, gain_vec):
    centered = values - jnp.mean(values, axis=-1, keepdims=True)
    spread = jnp.mean(centered * centered, axis=-1, keepdims=True)
    return centered * lax.rsqrt(spread + norm_eps) * gain_vec


def norm_back(values, gain_vec, grad_out):
    _, pullback = jax.vjp(layer_norm, values, gain_vec)
    return pullback(grad_out)


def gelu_back(pre_act, grad_out):
    _, pullback = jax.vjp(jax.nn.gelu, pre_act)
    return pullback(grad_out)[0]


def to_low(array_in):
    return array_in.astype(jnp.bfloat16)


def matmul(left, right):
    return jnp.einsum("...k,kn->...n", left, right, preferred_element_type=jnp.float32)


def matmul_t(left, right):
    return jnp.einsum("...n,kn->...k", left, right, preferred_element_type=jnp.float32)


def outer_sum(left, right):
    left_flat = left.reshape(-1, left.shape[-1])
    right_flat = right.reshape(-1, right.shape[-1])
    return lax.dot_general(
        left_flat, right_flat, (((0,), (0,)), ((), ())), preferred_element_type=jnp.float32
    )


def gather_rows(values):
    return lax.all_gather(values, "tensor", axis=1, tiled=True)


def sum_rows(terms):
    return lax.psum_scatter(
        terms.astype(jnp.bfloat16), "tensor", scatter_dimension=1, tiled=True
    ).astype(jnp.float32)


def pass_state(rows_now):
    return passed_along(rows_now.astype(jnp.bfloat16), "seq", 1).astype(rows_now.dtype)


def pass_back(grad_now):
    return passed_along(grad_now.astype(jnp.bfloat16), "seq", -1).astype(grad_now.dtype)


def split_heads(rows_in):
    return rows_in.reshape(rows_in.shape[0], rows_in.shape[1] // HEAD_DIM, HEAD_DIM)


def score_block(query_rows, key_all, bias_all, allowed):
    scores = (
        jnp.einsum(
            "qhd,khd->hqk",
            split_heads(query_rows),
            split_heads(key_all),
            preferred_element_type=jnp.float32,
        )
        * HEAD_DIM ** (-0.5)
        + bias_all
    )
    return jnp.where(allowed[None], scores, masked_score)


def attend_forward(query_rows, key_all, value_all, bias_all, allowed):
    scores = score_block(query_rows, key_all, bias_all, allowed)
    row_max = jnp.max(scores, axis=-1, keepdims=True)
    exp_scores = jnp.exp(scores - row_max)
    row_total = jnp.sum(exp_scores, axis=-1, keepdims=True)
    weight_all = to_low(exp_scores / row_total)
    mixed_out = jnp.einsum(
        "hqk,khd->qhd", weight_all, split_heads(value_all), preferred_element_type=jnp.float32
    )
    return (
        to_low(mixed_out.reshape(query_rows.shape[0], -1)),
        (row_max + jnp.log(row_total))[..., 0],
    )


def attend_back(query_rows, key_all, value_all, bias_all, allowed, log_total, grad_mixed):
    scores = score_block(query_rows, key_all, bias_all, allowed)
    weight_all = jnp.where(allowed[None], jnp.exp(scores - log_total[..., None]), 0.0)
    grad_heads = split_heads(grad_mixed)
    grad_weight = jnp.einsum(
        "qhd,khd->hqk", grad_heads, split_heads(value_all), preferred_element_type=jnp.float32
    )
    row_inner = jnp.sum(weight_all * grad_weight, axis=-1, keepdims=True)
    grad_scores = to_low(weight_all * (grad_weight - row_inner))
    grad_query = jnp.einsum(
        "hqk,khd->qhd", grad_scores, split_heads(key_all), preferred_element_type=jnp.float32
    ) * HEAD_DIM ** (-0.5)
    grad_keys = jnp.einsum(
        "hqk,qhd->khd", grad_scores, split_heads(query_rows), preferred_element_type=jnp.float32
    ) * HEAD_DIM ** (-0.5)
    grad_values = jnp.einsum(
        "hqk,qhd->khd", to_low(weight_all), grad_heads, preferred_element_type=jnp.float32
    )
    return (
        grad_query.reshape(query_rows.shape[0], -1),
        grad_keys.reshape(key_all.shape[0], -1),
        grad_values.reshape(key_all.shape[0], -1),
        grad_scores,
    )


def bias_lookup(rel_bias, rel_table):
    table_heads = jnp.zeros((rel_bias.shape[1],) + rel_table.shape, jnp.float32)
    for bucket_id in range(BUCKETS):
        table_heads = table_heads + jnp.where(
            rel_table[None] == bucket_id, rel_bias[bucket_id][:, None, None], 0.0
        )
    return table_heads


def bias_sums(score_grad, rel_table):
    grad_wide = score_grad.astype(jnp.float32)
    columns = []
    for bucket_id in range(BUCKETS):
        columns.append(
            jnp.sum(jnp.where(rel_table[None, None] == bucket_id, grad_wide, 0.0), axis=(0, 2, 3))
        )
    return jnp.stack(columns, axis=0)


def body(
    inputs,
    seg_starts,
    lengths,
    init_state,
    attn_gain,
    state_gain,
    mlp_gain,
    w_query,
    w_key,
    w_value,
    w_out,
    w_squery,
    w_sout,
    w_up,
    w_down,
    rel_bias,
    gate_bias,
    out_cot,
    state_cot,
):
    seq_count = inputs.shape[0]
    chain_length = lax.axis_size("seq")
    block_index = lax.axis_index("seq")
    is_first = block_index == 0
    width_local = w_query.shape[1]
    head_count = width_local // HEAD_DIM
    gate_value = jax.nn.sigmoid(gate_bias)
    positions = jnp.arange(BLOCK)
    inputs_wide = inputs.astype(jnp.float32)
    tokens_low = gather_rows(to_low(layer_norm(inputs_wide, attn_gain)))
    query_tok = to_low(matmul(tokens_low, w_query))
    key_tok = to_low(matmul(tokens_low, w_key))
    value_tok = to_low(matmul(tokens_low, w_value))
    key_prev, value_prev = passed_along((key_tok, value_tok), "seq", 1)
    valid_keys = (block_index * BLOCK + positions)[None, :] < lengths[:, None]
    batched_attend = jax.vmap(attend_forward, in_axes=(0, 0, 0, None, 0))
    batched_back = jax.vmap(attend_back, in_axes=(0, 0, 0, None, 0, 0, 0))

    def state_forward(state_rows, key_blk, value_blk, valid_blk):
        state_low = lax.all_gather(
            to_low(layer_norm(state_rows, state_gain)), "tensor", axis=1, tiled=True
        )
        query_st = to_low(matmul(state_low, w_squery))
        key_st = to_low(matmul(state_low, w_key))
        value_st = to_low(matmul(state_low, w_value))
        key_all = jnp.concatenate([key_blk, key_st], axis=1)
        value_all = jnp.concatenate([value_blk, value_st], axis=1)
        mixed_st, lse_st = batched_attend(
            query_st, key_all, value_all, 0.0, state_mask_of(valid_blk)
        )
        update = lax.psum_scatter(
            matmul(mixed_st, w_sout).astype(jnp.bfloat16), "tensor", scatter_dimension=1, tiled=True
        ).astype(jnp.float32)
        state_next = gate_value * state_rows + (1.0 - gate_value) * update
        return (state_next, (state_low, query_st, key_st, value_st, mixed_st, lse_st, update))

    def state_backward(
        grad_out, state_rows, kept_one, key_blk, value_blk, valid_blk, extra_key, extra_value
    ):
        state_low, query_st, key_st, value_st, mixed_st, lse_st, update = kept_one
        gate_part = (
            jnp.sum(grad_out * (state_rows - update), axis=(0, 1)) * gate_value * (1.0 - gate_value)
        )
        grad_update = lax.all_gather(
            to_low((1.0 - gate_value) * grad_out), "tensor", axis=1, tiled=True
        )
        grad_mixed_st = to_low(matmul_t(grad_update, w_sout))
        sout_part = outer_sum(mixed_st, grad_update)
        key_all = jnp.concatenate([key_blk, key_st], axis=1)
        value_all = jnp.concatenate([value_blk, value_st], axis=1)
        grad_query_st, grad_keys_st, grad_values_st, _ = batched_back(
            query_st, key_all, value_all, 0.0, state_mask_of(valid_blk), lse_st, grad_mixed_st
        )
        query_low = to_low(grad_query_st)
        key_low = to_low(grad_keys_st[:, BLOCK:] + extra_key)
        value_low = to_low(grad_values_st[:, BLOCK:] + extra_value)
        squery_part = outer_sum(state_low, query_low)
        key_part = outer_sum(state_low, key_low)
        value_part = outer_sum(state_low, value_low)
        terms = (
            matmul_t(query_low, w_squery) + matmul_t(key_low, w_key) + matmul_t(value_low, w_value)
        )
        grad_normed = lax.psum_scatter(
            terms.astype(jnp.bfloat16), "tensor", scatter_dimension=1, tiled=True
        ).astype(jnp.float32)
        grad_rows_norm, gain_part = norm_back(state_rows, state_gain, grad_normed)
        grad_in = gate_value * grad_out + grad_rows_norm
        block_grads = (grad_keys_st[:, :BLOCK], grad_values_st[:, :BLOCK])
        return (
            grad_in,
            block_grads,
            (squery_part, key_part, value_part, sout_part, gain_part, gate_part),
        )

    zeros_rows = jnp.zeros((seq_count,) + init_state.shape, jnp.float32)
    narrow_zero = jnp.zeros((seq_count, STATES, width_local), jnp.bfloat16)
    stored_start = (
        zeros_rows,
        zeros_rows,
        jnp.zeros((seq_count, STATES, D), jnp.bfloat16),
        narrow_zero,
        narrow_zero,
        narrow_zero,
        narrow_zero,
        jnp.zeros((seq_count, head_count, STATES), jnp.float32),
        zeros_rows,
    )

    def forward_turn(turn_index, carry):
        incoming, stored_now = carry
        order_index = turn_index - block_index
        is_live = (order_index >= 0) & (order_index < seq_count)
        picked = jnp.clip(order_index, 0, seq_count - 1)
        rows_now = jnp.where(is_first, init_state[None], incoming)
        key_one = lax.dynamic_slice_in_dim(key_tok, picked, 1, 0)
        value_one = lax.dynamic_slice_in_dim(value_tok, picked, 1, 0)
        valid_one = lax.dynamic_slice_in_dim(valid_keys, picked, 1, 0)
        rows_next, kept_one = state_forward(rows_now, key_one, value_one, valid_one)
        fresh = (rows_now, rows_next) + kept_one
        stored_now = tuple(
            (
                jnp.where(
                    is_live,
                    lax.dynamic_update_slice_in_dim(whole_array, fresh_part, picked, 0),
                    whole_array,
                )
                for whole_array, fresh_part in zip(stored_now, fresh)
            )
        )
        return (pass_state(rows_next), stored_now)

    incoming_start = jnp.zeros((1,) + init_state.shape, jnp.float32)
    _, stored_all = lax.fori_loop(
        0, chain_length + seq_count - 1, forward_turn, (incoming_start, stored_start)
    )
    state_in = stored_all[0]
    state_out = stored_all[1]
    kept = stored_all[2:]
    key_all_tok = jnp.concatenate([key_prev, key_tok, kept[2]], axis=1)
    value_all_tok = jnp.concatenate([value_prev, value_tok, kept[3]], axis=1)
    allowed_tok = jax.vmap(token_mask, in_axes=(0, 0, None))(seg_starts[:, 0], lengths, block_index)
    rel_table = bucket_of((jnp.arange(2 * BLOCK) - BLOCK)[None, :] - positions[:, None])
    full_bias = jnp.concatenate(
        [bias_lookup(rel_bias, rel_table), jnp.zeros((head_count, BLOCK, STATES), jnp.float32)],
        axis=2,
    )
    mixed_tok, lse_tok = batched_attend(
        query_tok, key_all_tok, value_all_tok, full_bias, allowed_tok
    )
    hidden_in = inputs_wide + sum_rows(matmul(mixed_tok, w_out))
    mid_low = gather_rows(to_low(layer_norm(hidden_in, mlp_gain)))
    pre_act = matmul(mid_low, w_up)
    hidden_low = to_low(jax.nn.gelu(pre_act))
    mlp_rows = sum_rows(matmul(hidden_low, w_down))
    tokens_out = (hidden_in + mlp_rows).astype(jnp.bfloat16)
    cot_wide = out_cot.astype(jnp.float32)
    cot_used = gather_rows(out_cot)
    grad_hidden_act = matmul_t(cot_used, w_down)
    down_grad = outer_sum(hidden_low, cot_used)
    grad_pre = to_low(gelu_back(pre_act, grad_hidden_act))
    up_grad = outer_sum(mid_low, grad_pre)
    grad_normed_mid = sum_rows(matmul_t(grad_pre, w_up))
    grad_mid_in, mlp_gain_grad = norm_back(hidden_in, mlp_gain, grad_normed_mid)
    grad_hidden = cot_wide + grad_mid_in
    grad_attn_low = gather_rows(to_low(grad_hidden))
    grad_mixed = to_low(matmul_t(grad_attn_low, w_out))
    out_grad = outer_sum(mixed_tok, grad_attn_low)
    grad_query_tok, grad_keys_tok, grad_values_tok, grad_scores = batched_back(
        query_tok, key_all_tok, value_all_tok, full_bias, allowed_tok, lse_tok, grad_mixed
    )
    bias_grad = bias_sums(grad_scores[..., : 2 * BLOCK], rel_table)
    grad_key_next, grad_value_next = (
        passed_along(grad_keys_tok[:, :BLOCK].astype(jnp.bfloat16), "seq", -1).astype(jnp.float32),
        passed_along(grad_values_tok[:, :BLOCK].astype(jnp.bfloat16), "seq", -1).astype(
            jnp.float32
        ),
    )
    grad_key_own = grad_keys_tok[:, BLOCK : 2 * BLOCK] + grad_key_next
    grad_value_own = grad_values_tok[:, BLOCK : 2 * BLOCK] + grad_value_next
    grad_key_st_tok = grad_keys_tok[:, 2 * BLOCK :]
    grad_value_st_tok = grad_values_tok[:, 2 * BLOCK :]
    cot_rows = state_cot[:, 0].astype(jnp.float32)
    wide_zero = jnp.zeros((seq_count, BLOCK, width_local), jnp.float32)
    stored_back = (zeros_rows, wide_zero, wide_zero)
    totals_start = (
        jnp.zeros((D, width_local), jnp.float32),
        jnp.zeros((D, width_local), jnp.float32),
        jnp.zeros((D, width_local), jnp.float32),
        jnp.zeros((width_local, D), jnp.float32),
        jnp.zeros((D,), jnp.float32),
        jnp.zeros((D,), jnp.float32),
    )

    def backward_turn(turn_index, carry):
        incoming, stored_now, totals_now = carry
        order_index = turn_index - (chain_length - 1 - block_index)
        is_live = (order_index >= 0) & (order_index < seq_count)
        picked = jnp.clip(order_index, 0, seq_count - 1)

        def slice_one(whole_array):
            return lax.dynamic_slice_in_dim(whole_array, picked, 1, 0)

        grad_out = slice_one(cot_rows) + incoming
        kept_one = tuple((slice_one(kept_array) for kept_array in kept))
        grad_in, block_one, parts_one = state_backward(
            grad_out,
            slice_one(state_in),
            kept_one,
            slice_one(key_tok),
            slice_one(value_tok),
            slice_one(valid_keys),
            slice_one(grad_key_st_tok),
            slice_one(grad_value_st_tok),
        )
        fresh = (grad_in,) + block_one
        stored_now = tuple(
            (
                jnp.where(
                    is_live,
                    lax.dynamic_update_slice_in_dim(whole_array, fresh_part, picked, 0),
                    whole_array,
                )
                for whole_array, fresh_part in zip(stored_now, fresh)
            )
        )
        totals_now = tuple(
            (
                total_now + jnp.where(is_live, part_now, 0.0)
                for total_now, part_now in zip(totals_now, parts_one)
            )
        )
        return (pass_back(grad_in), stored_now, totals_now)

    incoming_start = jnp.zeros((1,) + init_state.shape, jnp.float32)
    _, stored_done, weight_parts = lax.fori_loop(
        0, chain_length + seq_count - 1, backward_turn, (incoming_start, stored_back, totals_start)
    )
    grad_in_all, grad_key_blk, grad_value_blk = stored_done
    query_low = to_low(grad_query_tok)
    key_low = to_low(grad_key_own + grad_key_blk)
    value_low = to_low(grad_value_own + grad_value_blk)
    query_grad = outer_sum(tokens_low, query_low)
    key_grad = outer_sum(tokens_low, key_low) + weight_parts[1]
    value_grad = outer_sum(tokens_low, value_low) + weight_parts[2]
    grad_tokens = sum_rows(
        matmul_t(query_low, w_query) + matmul_t(key_low, w_key) + matmul_t(value_low, w_value)
    )
    grad_in_norm, attn_gain_grad = norm_back(inputs_wide, attn_gain, grad_tokens)
    inputs_grad = grad_hidden + grad_in_norm
    state_part = jnp.where(is_first, jnp.sum(grad_in_all, axis=0), 0.0)
    gains = lax.psum(
        jnp.stack([attn_gain_grad, weight_parts[4], mlp_gain_grad, weight_parts[5]]), "tensor"
    )
    totals = (
        lax.psum(query_grad.astype(jnp.bfloat16), ("dp", "seq")).astype(jnp.float32),
        lax.psum(key_grad.astype(jnp.bfloat16), ("dp", "seq")).astype(jnp.float32),
        lax.psum(value_grad.astype(jnp.bfloat16), ("dp", "seq")).astype(jnp.float32),
        lax.psum(out_grad.astype(jnp.bfloat16), ("dp", "seq")).astype(jnp.float32),
        lax.psum(weight_parts[0].astype(jnp.bfloat16), ("dp", "seq")).astype(jnp.float32),
        lax.psum(weight_parts[3].astype(jnp.bfloat16), ("dp", "seq")).astype(jnp.float32),
        lax.psum(up_grad.astype(jnp.bfloat16), ("dp", "seq")).astype(jnp.float32),
        lax.psum(down_grad.astype(jnp.bfloat16), ("dp", "seq")).astype(jnp.float32),
        lax.psum(bias_grad.astype(jnp.bfloat16), ("dp", "seq")).astype(jnp.float32),
        lax.psum(state_part.astype(jnp.bfloat16), ("dp", "seq")).astype(jnp.float32),
        lax.psum(gains.astype(jnp.bfloat16), ("dp", "seq")).astype(jnp.float32),
    )
    gain_total = totals[10]
    return (
        tokens_out,
        state_out[:, None],
        inputs_grad,
        totals[9],
        gain_total[0],
        gain_total[1],
        gain_total[2],
        totals[0],
        totals[1],
        totals[2],
        totals[3],
        totals[4],
        totals[5],
        totals[6],
        totals[7],
        totals[8],
        gain_total[3],
    )


def chosen_body(mesh):
    if mesh.shape["seq"] == 4 and mesh.shape["tensor"] == 4:
        return line_body
    return body


MESH_ID = pl.DeviceIdType.MESH
ROWS = 128
CHUNKS = BLOCK // ROWS
LINE = 8
SCALE = HEAD_DIM ** (-0.5)
VMEM_LIMIT = 60 * 1024 * 1024


def dot_nn(left, right):
    return lax.dot_general(left, right, (((1,), (0,)), ((), ())), preferred_element_type=jnp.float32)


def dot_nt(left, right):
    return lax.dot_general(left, right, (((1,), (1,)), ((), ())), preferred_element_type=jnp.float32)


def dot_tn(left, right):
    return lax.dot_general(left, right, (((0,), (0,)), ((), ())), preferred_element_type=jnp.float32)


def line_place():
    place = lax.axis_index("seq")
    half = lax.rem(place, 2)
    rank = lax.axis_index("tensor")
    return place, half, rank


def span(index, size):
    return pl.ds(pl.multiple_of(index * size, size), size)


def fetch_pieces(kept, first, rows, target, sem):
    for owner in range(8):
        pltpu.make_async_copy(
            kept.at[owner, :, pl.ds(first, rows), :], target.at[:, owner], sem
        ).start()


def fetch_columns(weights, target, sem):
    half = lax.rem(lax.axis_index("seq"), 2)
    for index, weight in enumerate(weights):
        pltpu.make_async_copy(
            weight.at[:, span(half, 128)], target.at[:, pl.ds(128 * index, 128)], sem
        ).start()


def fetched(target, sem):
    pltpu.make_async_copy(target, target, sem).wait()


def norm_parts(rows):
    centered = rows - jnp.mean(rows, axis=-1, keepdims=True)
    spread = jnp.mean(centered * centered, axis=-1, keepdims=True)
    return centered, lax.rsqrt(spread + norm_eps)


def mark(marks, block_id, row):
    return marks[block_id, pl.ds(row, 1), 0:1]


def sequence_marks(marks, block_id):
    mine = lax.axis_index("seq") // 2
    return mark(marks, block_id, mine), mark(marks, 0, 2 + mine)


def token_masks(marks, block_id, first_row):
    start, length = sequence_marks(marks, block_id)
    row = lax.broadcasted_iota(jnp.int32, (ROWS, BLOCK), 0) + first_row
    col = lax.broadcasted_iota(jnp.int32, (ROWS, BLOCK), 1)
    prev_limit = jnp.where(block_id > 0, length - (block_id - 1) * BLOCK, 0)
    prev_ok = (col > row) & (col < prev_limit)
    row_in = (row >= start) & (row < start + SEG)
    col_in = (col >= start) & (col < start + SEG)
    cur_ok = ((col <= row) | (row_in & col_in)) & (col < length - block_id * BLOCK)
    return prev_ok, cur_ok


def state_block_mask(marks, block_id):
    _, length = sequence_marks(marks, block_id)
    col = lax.broadcasted_iota(jnp.int32, (ROWS, BLOCK), 1)
    return col < length - block_id * BLOCK


def softmax_of(score_parts):
    top = jnp.max(score_parts[0], axis=-1, keepdims=True)
    for part in score_parts[1:]:
        top = jnp.maximum(top, jnp.max(part, axis=-1, keepdims=True))
    raised = [jnp.exp(part - top) for part in score_parts]
    total = jnp.sum(raised[0], axis=-1, keepdims=True)
    for part in raised[1:]:
        total = total + jnp.sum(part, axis=-1, keepdims=True)
    inverse = 1.0 / total
    return [to_low(part * inverse) for part in raised], top + jnp.log(total)


def token_scores(scal, qkv, qkvst, bias, block_id, chunk):
    rows = span(chunk, ROWS)
    prev_id = jnp.maximum(block_id - 1, 0)
    query = qkv[block_id, rows, 0:128]
    prev_ok, cur_ok = token_masks(scal, block_id, chunk * ROWS)
    prev = dot_nt(query, qkv[prev_id, :, 128:256]) * SCALE + bias[rows, 0:BLOCK]
    cur = dot_nt(query, qkv[block_id, :, 128:256]) * SCALE + bias[rows, BLOCK : 2 * BLOCK]
    stt = dot_nt(query, qkvst[block_id, :, 128:256]) * SCALE
    prev = jnp.where(prev_ok, prev, masked_score)
    cur = jnp.where(cur_ok, cur, masked_score)
    return query, (prev, cur, stt)


def state_scores(scal, qkv, qkvst, block_id, chunk):
    query = qkvst[block_id, span(chunk, ROWS), 0:128]
    tok = dot_nt(query, qkv[block_id, :, 128:256]) * SCALE
    tok = jnp.where(state_block_mask(scal, block_id), tok, masked_score)
    stt = dot_nt(query, qkvst[block_id, :, 128:256]) * SCALE
    return query, (tok, stt)


HALVES = 2
HALF_ROWS = STATES // HALVES
HALF_CHUNKS = HALF_ROWS // ROWS


def forward_kernel(
    marks, qkv, kept, w_squery, w_qkv, vecs, bias, state_cot, back_own,
    o_out, lse_out, state_rows, low_out, qkvst, lse_st, os_rows, cots, back,
    held, os_all, state_low, w_sout, start, w_state,
    way_send, core_send, recv_sem, local_sem, low_sem, cot_send, cot_recv,
    piece_send, piece_recv, ring_send, ring_recv,
):
    side, place, half, rank = plane_place()
    me = plane_index(side, place)
    partner = place + 1 - 2 * half
    head = 2 * rank + half
    fetch_pieces(kept, 32, 16, start, local_sem.at[0])
    fetch_columns((w_squery,), w_state, local_sem.at[2])
    fetch_pieces(kept, 0, 32, w_sout, local_sem.at[1])
    own_cot = pltpu.make_async_copy(state_cot.at[place], cots.at[place], local_sem.at[4])
    own_cot.start()
    own_piece = pltpu.make_async_copy(back_own, back.at[me, rank], local_sem.at[3])
    own_piece.start()
    ranks = [lax.rem(rank + step, 4) for step in (1, 2, 3)]
    seats = [lax.rem(place + step, 4) for step in (1, 2, 3)]
    barrier = pltpu.get_barrier_semaphore()
    for target in [{"tensor": one} for one in ranks] + [{"seq": one} for one in seats] + [
        {"dp": 1 - side}
    ]:
        pl.semaphore_signal(barrier, inc=1, device_id=target, device_id_type=MESH_ID)
    fetched(start, local_sem.at[0])
    held[...] = start[...].reshape(STATES, D).astype(jnp.float32)
    gain = vecs[0:1, :]
    gate = vecs[1:2, :]
    fetched(w_state, local_sem.at[2])

    def project(block_id, part):
        def one(chunk, _):
            rows = span(chunk, ROWS)
            centered, scale = norm_parts(held[rows, :])
            low = to_low(centered * scale * gain)
            state_low[block_id, rows, :] = low
            qkvst[block_id, rows, 0:128] = to_low(dot_nn(low, w_state[...]))
            qkvst[block_id, rows, 128:384] = to_low(dot_nn(low, w_qkv[:, 128:384]))
            return 0

        lax.fori_loop(HALF_CHUNKS * part, HALF_CHUNKS * (part + 1), one, 0)

    pl.semaphore_wait(barrier, 7)

    def piece_move(origin, part, slot, target):
        return pltpu.make_async_remote_copy(
            src_ref=back_own.at[part],
            dst_ref=back.at[me, origin, part],
            send_sem=piece_send.at[part, slot],
            recv_sem=piece_recv.at[part, origin],
            device_id={"tensor": target},
            device_id_type=MESH_ID,
        )

    def send_piece(part):
        for slot, target in enumerate(ranks):
            piece_move(rank, part, slot, target).start()

    gather = plane_gather(
        lambda owner, part: back.at[owner, pl.ds(2 * part, 2)], ring_send, ring_recv
    )
    next(gather)
    send_piece(0)
    for part in range(HALVES):
        project(0, part)
    right, left = {"tensor": lax.rem(rank + 1, 4)}, {"tensor": lax.rem(rank + 3, 4)}

    def moved(block_id, part, which, sem, target):
        view = os_all.at[block_id, pl.ds(HALF_ROWS * part, HALF_ROWS), span(which, 128)]
        return pltpu.make_async_remote_copy(
            src_ref=view,
            dst_ref=view,
            send_sem=sem,
            recv_sem=recv_sem.at[block_id, part, which],
            device_id=target,
            device_id_type=MESH_ID,
        )

    def cot_move(index, origin, slot, target):
        return pltpu.make_async_remote_copy(
            src_ref=state_cot.at[index],
            dst_ref=cots.at[origin],
            send_sem=cot_send.at[slot],
            recv_sem=cot_recv.at[origin],
            device_id={"seq": target},
            device_id_type=MESH_ID,
        )

    for slot, target in enumerate(seats):
        cot_move(target, place, slot, target).start()
    fetched(w_sout, local_sem.at[1])

    def origin_of(way, distance):
        if way == 0:
            return jnp.maximum(rank - distance, 0)
        return jnp.minimum(rank + distance, 3)

    def ways(distance):
        return (
            (0, rank >= distance, (rank >= distance) & (rank < 3), right),
            (1, rank + distance <= 3, (rank + distance <= 3) & (rank > 0), left),
        )

    def relay(block_id, part, distance, waiting):
        for way, comes, goes, target in ways(distance):
            which = 2 * origin_of(way, distance) + half
            sem = way_send.at[block_id, part, min(distance, 2), way]
            core_sem = core_send.at[block_id, part, which // 2]
            if distance > 0:

                @pl.when(comes)
                def _():
                    to_core = moved(block_id, part, which, core_sem, {"seq": partner})
                    if waiting:
                        moved(block_id, part, which, sem, target).wait_recv()
                        to_core.start()
                    else:
                        to_core.wait_send()

            if distance < 3:

                @pl.when(goes)
                def _():
                    one = moved(block_id, part, which, sem, target)
                    if waiting:
                        one.start()
                    else:
                        one.wait_send()

        if distance == 0:
            mine = moved(
                block_id, part, head, core_send.at[block_id, part, rank], {"seq": partner}
            )
            if waiting:
                mine.start()
            else:
                mine.wait_send()

    def one_block(block_id, _):
        def attend_state(chunk, _):
            rows = span(chunk, ROWS)
            _, parts = state_scores(marks, qkv, qkvst, block_id, chunk)
            (w_tok, w_stt), total = softmax_of(parts)
            mixed = dot_nn(w_tok, qkv[block_id, :, 256:384]) + dot_nn(
                w_stt, qkvst[block_id, :, 256:384]
            )
            os_all[block_id, rows, span(head, 128)] = to_low(mixed)
            lse_st[block_id, rows, :] = total
            return 0

        def attend_token(chunk, _):
            rows = span(chunk, ROWS)
            _, parts = token_scores(marks, qkv, qkvst, bias, block_id, chunk)
            weights, total = softmax_of(parts)
            prev_id = jnp.maximum(block_id - 1, 0)
            mixed = (
                dot_nn(weights[0], qkv[prev_id, :, 256:384])
                + dot_nn(weights[1], qkv[block_id, :, 256:384])
                + dot_nn(weights[2], qkvst[block_id, :, 256:384])
            )
            o_out[block_id, rows, :] = to_low(mixed)
            lse_out[block_id, rows, :] = total
            return 0

        def attend_both(part, _):
            lax.fori_loop(HALF_CHUNKS * part, HALF_CHUNKS * (part + 1), attend_state, 0)
            for value in range(HALVES):

                @pl.when(part == value)
                def _():
                    relay(block_id, value, 0, True)

            return 0

        lax.fori_loop(0, HALVES, attend_both, 0)
        pltpu.make_async_copy(
            state_low.at[block_id], low_out.at[block_id], low_sem.at[block_id]
        ).start()

        @pl.when(block_id == 2)
        def _():
            own_piece.wait()
            for part in range(3):
                for slot, target in enumerate(ranks):
                    piece_move(target, part, slot, target).wait_recv()
            next(gather)

        @pl.when(block_id == 3)
        def _():
            next(gather)
            next(gather)

        def between(step, _):
            for value, (distance, part) in enumerate(((1, 0), (1, 1), (2, 0), (2, 1))):

                @pl.when(step == value)
                def _():
                    relay(block_id, part, distance, True)

            return attend_token(step, 0)

        lax.fori_loop(0, 4, between, 0)

        def settle(part, _):
            for value in range(HALVES):

                @pl.when(part == value)
                def _():
                    relay(block_id, value, 3, True)
                    for origin in range(4):
                        moved(
                            block_id, value, 2 * origin + 1 - half,
                            core_send.at[block_id, value, origin], {"seq": partner},
                        ).wait_recv()

                    if value == HALVES - 1:
                        for turn in (0, 1):

                            @pl.when(block_id == turn)
                            def _():
                                send_piece(turn + 1)

            def update(chunk, _):
                rows = span(chunk, ROWS)
                change = dot_nn(os_all[block_id, rows, :], w_sout[...].reshape(D, D))
                held[rows, :] = gate * held[rows, :] + (1.0 - gate) * change
                return 0

            lax.fori_loop(HALF_CHUNKS * part, HALF_CHUNKS * (part + 1), update, 0)

            @pl.when(block_id < 3)
            def _():
                project(block_id + 1, part)

            return 0

        lax.fori_loop(0, HALVES, settle, 0)
        state_rows[block_id] = held[span(rank, 128), :]
        os_rows[block_id] = os_all[block_id, span(head, 64), :]
        return 0

    lax.fori_loop(0, 4, one_block, 0)

    def drain(block_id, _):
        for part in range(HALVES):
            for distance in range(4):
                relay(block_id, part, distance, False)
        pltpu.make_async_copy(
            state_low.at[block_id], low_out.at[block_id], low_sem.at[block_id]
        ).wait()
        return 0

    lax.fori_loop(0, 4, drain, 0)
    own_cot.wait()
    for part in range(3):
        for slot, target in enumerate(ranks):
            piece_move(rank, part, slot, target).wait_send()
    for _ in gather:
        pass
    for slot, target in enumerate(seats):
        cot_move(target, place, slot, target).wait_send()
        cot_move(place, target, slot, target).wait_recv()


def any_specs(count):
    return [pl.BlockSpec(memory_space=pl.ANY)] * count


def vmem_specs(count):
    return [pl.BlockSpec(memory_space=pltpu.VMEM)] * count


def forward_chain(
    marks, qkv, kept, w_squery, w_qkv, vecs, bias, state_cot, back_own
):
    low, wide = jnp.bfloat16, jnp.float32
    shapes = (
        ((4, BLOCK, 128), low),
        ((4, BLOCK, 1), wide),
        ((4, 128, D), wide),
        ((4, STATES, D), low),
        ((4, STATES, 384), low),
        ((4, STATES, 1), wide),
        ((4, 64, D), low),
        ((4, 64, D), low),
        ((8, 4, 3, 32, D), low),
    )
    dma = pltpu.SemaphoreType.DMA
    return pl.pallas_call(
        forward_kernel,
        out_shape=[jax.ShapeDtypeStruct(*one) for one in shapes],
        in_specs=vmem_specs(2) + any_specs(2) + vmem_specs(3) + any_specs(2),
        out_specs=vmem_specs(3) + any_specs(1) + vmem_specs(3) + any_specs(2),
        scratch_shapes=[
            pltpu.VMEM((STATES, D), wide),
            pltpu.VMEM((4, STATES, D), low),
            pltpu.VMEM((4, STATES, D), low),
            pltpu.VMEM((4, 8, 32, D), low),
            pltpu.VMEM((4, 8, 16, D), low),
            pltpu.VMEM((D, 128), low),
            dma((4, HALVES, 3, 2)),
            dma((4, HALVES, 4)),
            dma((4, HALVES, 8)),
            dma((5,)),
            dma((4,)),
            dma((3,)),
            dma((4,)),
            dma((3, 3)),
            dma((3, 4)),
            dma((14,)),
            dma((8, 2)),
        ],
        compiler_params=pltpu.CompilerParams(
            collective_id=1, has_side_effects=True, vmem_limit_bytes=VMEM_LIMIT
        ),
        cost_estimate=pl.CostEstimate(
            flops=60000000000, bytes_accessed=60000000, transcendentals=0
        ),
        name="forward_chain",
    )(marks, qkv, kept, w_squery, w_qkv, vecs, bias, state_cot, back_own)


def backward_kernel(
    scal, qkv, d_o, lse_tok, qkvst, lse_st, state_rows, begin, cots, back, kept, vecs, bias,
    extra, hidden, rows_hbm, low_hbm, w_qkv, os_rows,
    du_rows, d_start, sums, state_out, tokens_out, out_part, partial, pair_grads, sout_part,
    dz_sum, diag, d_qkv, d_qkvst, rows_buf, low_buf, leave, came, grad_acc,
    key_acc, value_acc, st_key, st_value, dos_rows, dos_got, d_got, grad_in,
    states, w_back, w_sout, work, core_got, near_got, far_got, total,
    send_sem, recv_sem, local_sem, side_sem, ring_send, ring_recv, buf_sem, core_sem, came_sem,
    near_two, far_two, two_send, two_recv,
):
    place, half, rank = line_place()
    own_rows = pl.ds(pl.multiple_of(half * 64, 64), 64)
    loads = [
        pltpu.make_async_copy(
            state_rows.at[:, own_rows, :], states.at[pl.ds(1, 4)], local_sem.at[0]
        ),
        pltpu.make_async_copy(
            state_rows.at[place], state_out.at[place // 2], local_sem.at[3]
        ),
        pltpu.make_async_copy(extra, work, local_sem.at[4]),
    ]
    for one in loads:
        one.start()
    fetch_pieces(kept, 0, 32, w_sout, local_sem.at[1])
    for owner in range(8):
        pltpu.make_async_copy(
            back.at[owner], w_back.at[:, owner // 4, :, owner % 4], local_sem.at[2]
        ).start()
    states[0] = to_low(begin[own_rows, :]).astype(jnp.float32)

    def block_loads(block_id):
        slot = lax.rem(block_id, 2)
        return [
            pltpu.make_async_copy(
                source.at[block_id], target.at[slot], buf_sem.at[index, slot]
            )
            for index, (source, target) in enumerate(((rows_hbm, rows_buf), (low_hbm, low_buf)))
        ]

    for one in block_loads(3):
        one.start()
    head = 2 * rank + half
    peers = []
    for step in (4, 3, 5, 2, 6, 1, 7):
        other = lax.rem(head + step, LINE)
        peers.append((other, place - half + lax.rem(other, 2), other // 2))
    barrier = pltpu.get_barrier_semaphore()
    for _, seq_to, rank_to in peers:
        pl.semaphore_signal(
            barrier, inc=1, device_id={"seq": seq_to, "tensor": rank_to}, device_id_type=MESH_ID
        )
    beside = lax.rem(place + 2, 4)
    pl.semaphore_signal(barrier, inc=1, device_id={"seq": beside}, device_id_type=MESH_ID)
    pl.semaphore_signal(
        barrier, inc=1, device_id={"dp": 1 - lax.axis_index("dp")}, device_id_type=MESH_ID
    )
    plane_steps = plane_scatter(
        work, core_got, near_got, far_got, total, 384, ring_send, ring_recv
    )
    next(plane_steps)
    short = pl.ds(0, 128)
    sout_steps = plane_scatter(
        work.at[:, short, :], core_got.at[:, short, :], near_two, far_two, total.at[short, :],
        128, two_send, two_recv,
    )
    next(sout_steps)

    def sout_products():
        def one(index, _):
            part = to_low(
                dot_tn(os_rows[:, span(index, 128)], du_rows[...].reshape(256, D))
            )
            for block in range(4):
                work[4 * lax.rem(index, 2) + block, span(index // 2, 32), :] = part[
                    32 * block : 32 * block + 32, :
                ]
            return 0

        lax.fori_loop(0, LINE, one, 0)

    def plane_results():
        for which in range(2):
            rows = pl.ds(128 * which, 128)
            tokens_out[which] = to_low(hidden[which] + total[rows, :])
        out_part[...] = to_low(total[256:384, :])


    def aside(block_id, row_set):
        return pltpu.make_async_remote_copy(
            src_ref=state_rows.at[block_id],
            dst_ref=state_out.at[row_set],
            send_sem=side_sem.at[0],
            recv_sem=side_sem.at[1],
            device_id={"seq": beside},
            device_id_type=MESH_ID,
        )

    gain = vecs[0:1, :]
    gate = vecs[1:2, :]
    key_acc[...] = jnp.zeros_like(key_acc)
    value_acc[...] = jnp.zeros_like(value_acc)
    dz_sum[...] = jnp.zeros_like(dz_sum)
    sums[...] = jnp.zeros_like(sums)
    grad_in[...] = jnp.zeros_like(grad_in)
    grad_acc[...] = jnp.zeros_like(grad_acc)
    core = place + 1 - 2 * half

    def place_in(block_id, owner):
        return jnp.where(block_id == owner, 1, 0)

    def leaving(slot):
        return pltpu.make_async_remote_copy(
            src_ref=leave.at[slot],
            dst_ref=came.at[slot],
            send_sem=core_sem.at[slot],
            recv_sem=came_sem.at[slot],
            device_id={"seq": core},
            device_id_type=MESH_ID,
        )

    def add_came(slot):
        leaving(slot).wait_recv()

        def one(chunk, _):
            partial[slot, chunk] = to_low(
                partial[slot, chunk].astype(jnp.float32)
                + came[slot, span(chunk, 128), :].astype(jnp.float32)
            )
            return 0

        lax.fori_loop(0, 4, one, 0)

    def bucket_sums():
        diag[...] = jnp.zeros_like(diag)

        def one(group, _):
            rows = dz_sum[span(group, 8), :]
            wide = jnp.concatenate([rows, jnp.zeros((8, WIDE - 2 * BLOCK), jnp.float32)], axis=1)
            diag[...] += pltpu.roll(wide, lax.rem(WIDE - 8 * group, WIDE), 1)
            return 0

        lax.fori_loop(0, BLOCK // 8, one, 0)
        line = diag[...]
        row = lax.broadcasted_iota(jnp.int32, (8, WIDE), 0)
        for step in (1, 2, 4):
            line = jnp.where(row // step % 2 == 1, pltpu.roll(line, WIDE - step, 1), line)
        lane = lax.broadcasted_iota(jnp.int32, (8, WIDE), 1)
        bucket_ids = bucket_of(jnp.where(lane >= WIDE - BLOCK, lane - WIDE - BLOCK, lane - BLOCK))
        spot = lax.broadcasted_iota(jnp.int32, (1, 256), 1) - BUCKETS * head
        placed = jnp.zeros((1, 256), jnp.float32)
        for bucket_id in range(BUCKETS):
            chosen = jnp.where(bucket_ids == bucket_id, line, 0.0)
            value = jnp.sum(jnp.sum(chosen, axis=0, keepdims=True), axis=1, keepdims=True)
            placed = jnp.where(spot == bucket_id, value, placed)
        sums[2:3, 0:256] = placed

    def block_products(block_id):
        slot = lax.rem(block_id, 2)
        for one in block_loads(block_id):
            one.wait()

        @pl.when(block_id > 0)
        def _():
            for one in block_loads(jnp.maximum(block_id - 1, 0)):
                one.start()

        def one_part(part, _):
            rows = span(part, 128)

            @pl.when(part < 3)
            def _():
                grad_acc[rows, :] += dot_tn(
                    d_qkv[block_id, :, span(jnp.minimum(part, 2), 128)], rows_buf[slot]
                )

            @pl.when(part > 0)
            def _():
                grad_acc[rows, :] += dot_tn(
                    d_qkvst[block_id, :, span(lax.rem(part, 3), 128)], low_buf[slot]
                )

            return 0

        lax.fori_loop(0, 4, one_part, 0)
        kept_here = lax.rem(block_id, 2) == half
        mine_slot, core_slot = place_in(block_id, place), place_in(block_id, core)

        def one_chunk(chunk, _):
            rows = span(chunk, 128)
            value = to_low(dot_nt(d_qkv[block_id, rows, :], w_qkv[...]))

            @pl.when(kept_here)
            def _():
                partial[mine_slot, chunk] = value

            @pl.when(jnp.logical_not(kept_here))
            def _():
                leave[core_slot, rows, :] = value

            return 0

        lax.fori_loop(0, 4, one_chunk, 0)

        @pl.when(jnp.logical_not(kept_here))
        def _():
            leaving(core_slot).start()

    def back_parts(parts, total, grad, values):
        weights = [jnp.exp(part - total) for part in parts]
        d_weights = [dot_nt(grad, value) for value in values]
        inner = jnp.sum(weights[0] * d_weights[0], axis=-1, keepdims=True)
        for one, other in zip(weights[1:], d_weights[1:]):
            inner = inner + jnp.sum(one * other, axis=-1, keepdims=True)
        d_scores = [to_low(one * (other - inner)) for one, other in zip(weights, d_weights)]
        return [to_low(one) for one in weights], d_scores

    def token_back(block_id):
        prev_id = jnp.maximum(block_id - 1, 0)
        st_key[...] = jnp.zeros_like(st_key)
        st_value[...] = jnp.zeros_like(st_value)

        def one_chunk(chunk, _):
            rows = span(chunk, ROWS)
            query, parts = token_scores(scal, qkv, qkvst, bias, block_id, chunk)
            grad = d_o[block_id, rows, :]
            keys = (qkv[prev_id, :, 128:256], qkv[block_id, :, 128:256], qkvst[block_id, :, 128:256])
            values = (
                qkv[prev_id, :, 256:384], qkv[block_id, :, 256:384], qkvst[block_id, :, 256:384]
            )
            weights, d_scores = back_parts(parts, lse_tok[block_id, rows, :], grad, values)
            d_query = dot_nn(d_scores[0], keys[0])
            d_query = d_query + dot_nn(d_scores[1], keys[1]) + dot_nn(d_scores[2], keys[2])
            d_qkv[block_id, rows, 0:128] = to_low(d_query * SCALE)
            key_acc[prev_id] += dot_tn(d_scores[0], query) * SCALE
            value_acc[prev_id] += dot_tn(weights[0], grad)
            key_acc[block_id] += dot_tn(d_scores[1], query) * SCALE
            value_acc[block_id] += dot_tn(weights[1], grad)
            st_key[...] += dot_tn(d_scores[2], query) * SCALE
            st_value[...] += dot_tn(weights[2], grad)
            dz_sum[rows, 0:BLOCK] += d_scores[0].astype(jnp.float32)
            dz_sum[rows, BLOCK : 2 * BLOCK] += d_scores[1].astype(jnp.float32)
            return 0

        lax.fori_loop(0, CHUNKS, one_chunk, 0)

    token_back(3)
    pl.semaphore_wait(barrier, LINE + 1)
    aside(beside, place // 2).start()
    loads[2].wait()
    loads[0].wait()
    fetched(w_sout, local_sem.at[1])
    fetched(w_back, local_sem.at[2])

    def mixed_copy(block_id, slot, sender, other, seq_to, rank_to):
        return pltpu.make_async_remote_copy(
            src_ref=dos_rows.at[block_id, :, span(other, 128)],
            dst_ref=dos_got.at[block_id, span(sender, 64), :],
            send_sem=send_sem.at[0, block_id, slot],
            recv_sem=recv_sem.at[0, block_id, sender],
            device_id={"seq": seq_to, "tensor": rank_to},
            device_id_type=MESH_ID,
        )

    def grads_copy(block_id, slot, sender, other, seq_to, rank_to):
        return pltpu.make_async_remote_copy(
            src_ref=d_qkvst.at[block_id, span(other, 64), :],
            dst_ref=d_got.at[block_id, sender],
            send_sem=send_sem.at[1, block_id, slot],
            recv_sem=recv_sem.at[1, block_id, sender],
            device_id={"seq": seq_to, "tensor": rank_to},
            device_id_type=MESH_ID,
        )

    def one_block(turn, _):
        block_id = 3 - turn
        grad_out = grad_in[...] + cots[block_id].astype(jnp.float32)
        sums[0:1, :] += jnp.sum(
            grad_out * (states[block_id] - states[block_id + 1]), axis=0, keepdims=True
        ) * gate
        change = to_low((1.0 - gate) * grad_out)
        du_rows[block_id] = change
        dos_rows[block_id] = to_low(dot_nt(change, w_sout[...].reshape(D, D)))
        for slot, (other, seq_to, rank_to) in enumerate(peers):
            mixed_copy(block_id, slot, head, other, seq_to, rank_to).start()
        dos_got[block_id, span(head, 64), :] = dos_rows[block_id, :, span(head, 128)]

        @pl.when(turn > 0)
        def _():
            block_products(block_id + 1)

        @pl.when(turn == 3)
        def _():
            sout_products()

        for slot, (other, seq_to, rank_to) in enumerate(peers):
            mixed_copy(block_id, slot, other, other, seq_to, rank_to).wait_recv()

        def one_chunk(chunk, _):
            rows = span(chunk, ROWS)
            query, parts = state_scores(scal, qkv, qkvst, block_id, chunk)
            grad = dos_got[block_id, rows, :]
            keys = (qkv[block_id, :, 128:256], qkvst[block_id, :, 128:256])
            values = (qkv[block_id, :, 256:384], qkvst[block_id, :, 256:384])
            weights, d_scores = back_parts(parts, lse_st[block_id, rows, :], grad, values)
            d_query = dot_nn(d_scores[0], keys[0]) + dot_nn(d_scores[1], keys[1])
            d_qkvst[block_id, rows, 0:128] = to_low(d_query * SCALE)
            key_acc[block_id] += dot_tn(d_scores[0], query) * SCALE
            value_acc[block_id] += dot_tn(weights[0], grad)
            st_key[...] += dot_tn(d_scores[1], query) * SCALE
            st_value[...] += dot_tn(weights[1], grad)
            return 0

        lax.fori_loop(0, CHUNKS, one_chunk, 0)
        d_qkvst[block_id, :, 128:256] = to_low(st_key[...])
        d_qkvst[block_id, :, 256:384] = to_low(st_value[...])
        for slot, (other, seq_to, rank_to) in enumerate(peers):
            grads_copy(block_id, slot, head, other, seq_to, rank_to).start()
        d_got[block_id, head] = d_qkvst[block_id, span(head, 64), :]

        for step in range(3):

            @pl.when(turn == step)
            def _():
                next(plane_steps)
                if step == 2:
                    next(plane_steps, None)
                    plane_results()

        @pl.when(turn == 3)
        def _():
            next(sout_steps)
            add_came(place_in(2 + half, place))
            bucket_sums()
            next(sout_steps)

        @pl.when(turn < 3)
        def _():
            token_back(block_id - 1)

        d_qkv[block_id, :, 128:256] = to_low(key_acc[block_id])
        d_qkv[block_id, :, 256:384] = to_low(value_acc[block_id])
        @pl.when(turn == 3)
        def _():
            block_products(0)
            next(sout_steps)

        for slot, (other, seq_to, rank_to) in enumerate(peers):
            grads_copy(block_id, slot, other, other, seq_to, rank_to).wait_recv()
        d_low = dot_nn(d_got[block_id, 0], w_back[0, 0].reshape(384, D))
        for other in range(1, LINE):
            d_low = d_low + dot_nn(
                d_got[block_id, other], w_back[other // 2, other % 2].reshape(384, D)
            )
        centered, scale = norm_parts(states[block_id])
        normed = centered * scale
        sums[1:2, :] += jnp.sum(d_low * normed, axis=0, keepdims=True)
        lifted = d_low * gain
        grad_in[...] = gate * grad_out + scale * (
            lifted
            - jnp.mean(lifted, axis=-1, keepdims=True)
            - normed * jnp.mean(lifted * normed, axis=-1, keepdims=True)
        )
        return 0

    lax.fori_loop(0, 4, one_block, 0)
    d_start[...] = grad_in[...]

    def drain(block_id, _):
        for slot, (other, seq_to, rank_to) in enumerate(peers):
            mixed_copy(block_id, slot, head, other, seq_to, rank_to).wait_send()
            grads_copy(block_id, slot, head, other, seq_to, rank_to).wait_send()
        return 0

    lax.fori_loop(0, 4, drain, 0)
    pair_grads[...] = to_low(grad_acc[...])
    for _ in sout_steps:
        pass
    sout_part[...] = to_low(total[0:128, :])
    add_came(place_in(half, place))
    for slot in range(2):
        leaving(slot).wait_send()
    loads[1].wait()
    aside(beside, place // 2).wait_send()
    aside(place, 1 - place // 2).wait_recv()


def backward_chain(
    scal, qkv, d_o, lse_tok, qkvst, lse_st, state_rows, begin, cots, back, kept, vecs, bias,
    extra, hidden, rows_all, state_low, w_qkv, os_rows,
):
    low, wide = jnp.bfloat16, jnp.float32
    shapes = (
        ((4, 64, D), low),
        ((64, D), wide),
        ((8, D), wide),
        ((2, 128, D), wide),
        ((2, 128, D), low),
        ((128, D), low),
        ((2, 4, 128, D), low),
        ((512, D), low),
        ((128, D), low),
    )
    return pl.pallas_call(
        backward_kernel,
        out_shape=[jax.ShapeDtypeStruct(*one) for one in shapes],
        in_specs=vmem_specs(6)
        + any_specs(1)
        + vmem_specs(2)
        + any_specs(2)
        + vmem_specs(2)
        + any_specs(1)
        + vmem_specs(1)
        + any_specs(2)
        + vmem_specs(2),
        out_specs=vmem_specs(3) + any_specs(1) + vmem_specs(5),
        scratch_shapes=[
            pltpu.VMEM((BLOCK, 2 * BLOCK), wide),
            pltpu.VMEM((8, WIDE), wide),
            pltpu.VMEM((4, BLOCK, 384), low),
            pltpu.VMEM((4, STATES, 384), low),
            pltpu.VMEM((2, BLOCK, D), low),
            pltpu.VMEM((2, STATES, D), low),
            pltpu.VMEM((2, BLOCK, D), low),
            pltpu.VMEM((2, BLOCK, D), low),
            pltpu.VMEM((512, D), wide),
            pltpu.VMEM((4, BLOCK, 128), wide),
            pltpu.VMEM((4, BLOCK, 128), wide),
            pltpu.VMEM((STATES, 128), wide),
            pltpu.VMEM((STATES, 128), wide),
            pltpu.VMEM((4, 64, D), low),
            pltpu.VMEM((4, STATES, 128), low),
            pltpu.VMEM((4, LINE, 64, 384), low),
            pltpu.VMEM((64, D), wide),
            pltpu.VMEM((5, 64, D), wide),
            pltpu.VMEM((4, 2, 3, 4, 32, D), low),
            pltpu.VMEM((4, 8, 32, D), low),
            pltpu.VMEM((8, 384, D), low),
            pltpu.VMEM((4, 384, D), low),
            pltpu.VMEM((4, 192, D), low),
            pltpu.VMEM((2, 192, D), low),
            pltpu.VMEM((384, D), wide),
            pltpu.SemaphoreType.DMA((2, 4, LINE - 1)),
            pltpu.SemaphoreType.DMA((2, 4, LINE)),
            pltpu.SemaphoreType.DMA((5,)),
            pltpu.SemaphoreType.DMA((2,)),
            pltpu.SemaphoreType.DMA((10,)),
            pltpu.SemaphoreType.DMA((10,)),
            pltpu.SemaphoreType.DMA((2, 2)),
            pltpu.SemaphoreType.DMA((2,)),
            pltpu.SemaphoreType.DMA((2,)),
            pltpu.VMEM((4, 64, D), low),
            pltpu.VMEM((2, 64, D), low),
            pltpu.SemaphoreType.DMA((10,)),
            pltpu.SemaphoreType.DMA((10,)),
        ],
        compiler_params=pltpu.CompilerParams(
            collective_id=2, has_side_effects=True, vmem_limit_bytes=63 * 1024 * 1024
        ),
        cost_estimate=pl.CostEstimate(flops=40000000000, bytes_accessed=40000000, transcendentals=0),
        name="backward_chain",
    )(
        scal, qkv, d_o, lse_tok, qkvst, lse_st, state_rows, begin, cots, back, kept, vecs, bias,
        extra, hidden, rows_all, state_low, w_qkv, os_rows,
    )


def plane_place():
    place, half, rank = line_place()
    side = lax.axis_index("dp")
    return side, place, half, rank


def plane_index(side, place):
    return 4 * side + place


def row_halves(buf, rows):
    size = rows // 2
    return lambda owner, part: buf.at[owner, pl.ds(part * size, size), :]


def plane_gather(view, send_sem, recv_sem):
    side, place, half, rank = plane_place()
    across, beside = 1 - side, lax.rem(place + 2, 4)
    core = place + 1 - 2 * half
    me = plane_index(side, place)
    at_x, at_y = plane_index(across, place), plane_index(side, beside)
    at_d = plane_index(across, beside)
    to_x, to_y, to_c = {"dp": across}, {"seq": beside}, {"seq": core}

    def piece(owner, part, slot, target):
        one = view(owner, part)
        return pltpu.make_async_remote_copy(
            src_ref=one,
            dst_ref=one,
            send_sem=send_sem.at[slot],
            recv_sem=recv_sem.at[owner, part],
            device_id=target,
            device_id_type=MESH_ID,
        )

    own = [
        piece(me, 0, 0, to_x), piece(me, 1, 1, to_y), piece(me, 1, 2, to_x), piece(me, 0, 3, to_y),
        piece(me, 0, 4, to_c), piece(me, 1, 5, to_c),
    ]
    on_x0, on_y1 = piece(at_x, 0, 6, to_y), piece(at_y, 1, 7, to_x)
    came = [
        (piece(owner, part, 0, to_c), piece(owner, part, slot, to_c))
        for owner, part, slot in (
            (at_x, 0, 8), (at_y, 1, 9), (at_x, 1, 10), (at_y, 0, 11), (at_d, 0, 12), (at_d, 1, 13)
        )
    ]
    core_came = [
        piece(owner, part, 0, to_c)
        for owner in (
            plane_index(side, core),
            plane_index(across, core),
            plane_index(side, lax.rem(core + 2, 4)),
            plane_index(across, lax.rem(core + 2, 4)),
        )
        for part in (0, 1)
    ]
    yield
    for one in own:
        one.start()
    yield
    came[0][0].wait_recv()
    on_x0.start()
    came[1][0].wait_recv()
    on_y1.start()
    came[0][1].start()
    came[1][1].start()
    yield
    for index in (2, 3):
        came[index][0].wait_recv()
        came[index][1].start()
    yield
    for index in (4, 5):
        came[index][0].wait_recv()
        came[index][1].start()
    yield
    for one in core_came:
        one.wait_recv()
    for one in own + [on_x0, on_y1] + [two for _, two in came]:
        one.wait_send()


def run_all(*steps):
    waiting = list(steps)
    while waiting:
        for one in list(waiting):
            try:
                next(one)
            except StopIteration:
                waiting.remove(one)


def plane_scatter(part, core_got, near_got, far_got, total, rows, send_sem, recv_sem):
    side, place, half, rank = plane_place()
    across, beside = 1 - side, lax.rem(place + 2, 4)
    core = place + 1 - 2 * half
    me = plane_index(side, place)
    at_x, at_y = plane_index(across, place), plane_index(side, beside)
    at_d = plane_index(across, beside)
    size = rows // 2
    halves = (pl.ds(0, size), pl.ds(size, size))

    def moved(source, target_ref, slot, target):
        return pltpu.make_async_remote_copy(
            src_ref=source,
            dst_ref=target_ref,
            send_sem=send_sem.at[slot],
            recv_sem=recv_sem.at[slot],
            device_id=target,
            device_id_type=MESH_ID,
        )

    order = (at_d, at_x, at_y, me)
    swapped = (
        plane_index(across, lax.rem(core + 2, 4)),
        plane_index(across, core),
        plane_index(side, lax.rem(core + 2, 4)),
        plane_index(side, core),
    )
    def add_into(owner, view, other):
        part[owner, view, :] = to_low(
            part[owner, view, :].astype(jnp.float32) + other.astype(jnp.float32)
        )

    near = [
        moved(part.at[at_d, halves[0], :], near_got.at[0], 4, {"dp": across}),
        moved(part.at[at_d, halves[1], :], near_got.at[1], 5, {"seq": beside}),
        moved(part.at[at_x, halves[0], :], near_got.at[2], 6, {"dp": across}),
        moved(part.at[at_y, halves[1], :], near_got.at[3], 7, {"seq": beside}),
    ]
    first = [
        moved(part.at[owner], core_got.at[slot], slot, {"seq": core})
        for slot, owner in enumerate(swapped)
    ]
    far = [
        moved(part.at[at_y, halves[0], :], far_got.at[0], 8, {"seq": beside}),
        moved(part.at[at_x, halves[1], :], far_got.at[1], 9, {"dp": across}),
    ]
    yield
    for one in first:
        one.start()
    for slot, owner in enumerate(order):
        first[slot].wait_recv()
        for view in halves:
            add_into(owner, view, core_got[slot, view, :])
        if slot == 0:
            near[0].start()
            near[1].start()
        if slot == 1:
            near[2].start()
        if slot == 2:
            near[3].start()
    yield
    near[0].wait_recv()
    add_into(at_y, halves[0], near_got[0])
    far[0].start()
    near[1].wait_recv()
    add_into(at_x, halves[1], near_got[1])
    far[1].start()
    yield
    near[2].wait_recv()
    add_into(me, halves[0], near_got[2])
    near[3].wait_recv()
    add_into(me, halves[1], near_got[3])
    yield
    for slot, view in enumerate(halves):
        far[slot].wait_recv()
        total[view, :] = part[me, view, :].astype(jnp.float32) + far_got[slot].astype(jnp.float32)
    for one in first + near + far:
        one.wait_send()


def group_peers():
    place, half, rank = line_place()
    here = 4 * place + rank
    peers = []
    for step in range(1, 16):
        other = lax.rem(here + step, 16)
        peers.append((other, other // 4, lax.rem(other, 4)))
    return here, peers


def greet(peers):
    side = lax.axis_index("dp")
    barrier = pltpu.get_barrier_semaphore()
    for _, seq_to, rank_to in peers:
        pl.semaphore_signal(
            barrier, inc=1, device_id={"seq": seq_to, "tensor": rank_to}, device_id_type=MESH_ID
        )
    pl.semaphore_signal(barrier, inc=1, device_id={"dp": 1 - side}, device_id_type=MESH_ID)
    pl.semaphore_wait(barrier, len(peers) + 1)


def middle_kernel(
    mixed, tokens, kept, spread, cot_hbm, vecs,
    hidden, d_hidden, d_line, sums, extra, ff_grads,
    mixed_rows, mid_all, gl_all, dpre_all, work, core_got, near_got, far_got, total, d_rows,
    d_low, w_out, up, down, cot_all,
    send_sem, recv_sem, ring_send, ring_recv, sum_send, sum_recv, back_send, back_recv, local_sem,
):
    low, wide = jnp.bfloat16, jnp.float32
    side, place, half, rank = plane_place()
    mine = place // 2
    head = 2 * rank + half
    across, beside = 1 - side, lax.rem(place + 2, 4)
    core = place + 1 - 2 * half
    core_beside = lax.rem(core + 2, 4)
    me = plane_index(side, place)
    at_x, at_y = plane_index(across, place), plane_index(side, beside)
    at_d = plane_index(across, beside)
    me_c, x_c = plane_index(side, core), plane_index(across, core)
    y_c, d_c = plane_index(side, core_beside), plane_index(across, core_beside)
    to_x, to_y, to_c = {"dp": across}, {"seq": beside}, {"seq": core}
    here, peers = group_peers()
    fetch_pieces(kept, 48, 32, w_out, local_sem.at[0])
    ff_own = up.shape[1]
    first = spread.shape[1] - 2 * ff_own
    loads = [
        pltpu.make_async_copy(spread.at[:, pl.ds(first, ff_own), :], up, local_sem.at[1]),
        pltpu.make_async_copy(spread.at[:, pl.ds(first + ff_own, ff_own), :], down, local_sem.at[2]),
        pltpu.make_async_copy(cot_hbm, cot_all, local_sem.at[3]),
    ]
    for one in loads:
        one.start()
    greet(peers)

    def rows_copy(slot, sender, seq_from, rank_from, seq_to, rank_to):
        return pltpu.make_async_remote_copy(
            src_ref=mixed.at[seq_to, span(rank_to, 128), :],
            dst_ref=mixed_rows.at[
                seq_from // 2, :, span(2 * rank_from + lax.rem(seq_from, 2), 128)
            ],
            send_sem=send_sem.at[slot],
            recv_sem=recv_sem.at[sender],
            device_id={"seq": seq_to, "tensor": rank_to},
            device_id_type=MESH_ID,
        )

    for slot, (_, seq_to, rank_to) in enumerate(peers):
        rows_copy(slot, here, place, rank, seq_to, rank_to).start()
    mixed_rows[mine, :, span(head, 128)] = mixed[place, span(rank, 128), :]
    fetched(w_out, local_sem.at[0])
    for slot, (other, seq_to, rank_to) in enumerate(peers):
        rows_copy(slot, other, seq_to, rank_to, seq_to, rank_to).wait_recv()
    gain = vecs[2:3, :]

    def project(which, _):
        added = dot_nn(mixed_rows[which], w_out[...].reshape(D, D)) + tokens[which].astype(wide)
        hidden[which] = added
        centered, scale = norm_parts(added)
        mid_all[me, span(which, 128), :] = to_low(centered * scale * gain)
        return 0

    lax.fori_loop(0, 2, project, 0)

    def piece(owner, part, slot, target):
        view = mid_all.at[owner, pl.ds(part * 128, 128), :]
        return pltpu.make_async_remote_copy(
            src_ref=view,
            dst_ref=view,
            send_sem=ring_send.at[slot],
            recv_sem=ring_recv.at[owner, part],
            device_id=target,
            device_id_type=MESH_ID,
        )

    own = [
        piece(me, 0, 0, to_x), piece(me, 1, 1, to_y), piece(me, 1, 2, to_x), piece(me, 0, 3, to_y),
        piece(me, 0, 4, to_c), piece(me, 1, 5, to_c),
    ]
    on_x0, on_y1 = piece(at_x, 0, 6, to_y), piece(at_y, 1, 7, to_x)
    to_core = [
        piece(at_x, 0, 8, to_c), piece(at_y, 1, 9, to_c), piece(at_x, 1, 10, to_c),
        piece(at_y, 0, 11, to_c), piece(at_d, 0, 12, to_c), piece(at_d, 1, 13, to_c),
    ]
    wait_of = {
        (name, part): piece(owner, part, 0, to_c)
        for name, owner in (
            ("x", at_x), ("y", at_y), ("d", at_d), ("mc", me_c), ("xc", x_c), ("yc", y_c), ("dc", d_c)
        )
        for part in (0, 1)
    }

    def moved(source, target_ref, slot, target):
        return pltpu.make_async_remote_copy(
            src_ref=source,
            dst_ref=target_ref,
            send_sem=sum_send.at[slot],
            recv_sem=sum_recv.at[slot],
            device_id=target,
            device_id_type=MESH_ID,
        )

    views = (pl.ds(0, 128), pl.ds(128, 128))
    swap = [
        moved(work.at[owner], core_got.at[slot], slot, to_c)
        for slot, owner in enumerate((d_c, x_c, y_c, me_c))
    ]
    near = [
        moved(work.at[at_d, views[0], :], near_got.at[0], 4, to_x),
        moved(work.at[at_d, views[1], :], near_got.at[1], 5, to_y),
        moved(work.at[at_x, views[0], :], near_got.at[2], 6, to_x),
        moved(work.at[at_y, views[1], :], near_got.at[3], 7, to_y),
    ]
    far = [
        moved(work.at[at_y, views[0], :], far_got.at[0], 8, to_y),
        moved(work.at[at_x, views[1], :], far_got.at[1], 9, to_x),
    ]

    def add_into(owner, view, other):
        work[owner, view, :] = to_low(work[owner, view, :].astype(wide) + other.astype(wide))

    def add_core(slot, owner):
        swap[slot].wait_recv()
        for view in views:
            add_into(owner, view, core_got[slot, view, :])

    for one in own:
        one.start()
    loads[0].wait()
    loads[1].wait()
    loads[2].wait()
    order = (
        (me, 0), (me, 1), (me_c, 0), (me_c, 1), (at_x, 0), (at_y, 1), (x_c, 0), (y_c, 1),
        (at_x, 1), (at_y, 0), (x_c, 1), (y_c, 0), (at_d, 0), (at_d, 1), (d_c, 0), (d_c, 1),
    )

    def before_four():
        swap[3].start()
        wait_of["x", 0].wait_recv()
        on_x0.start()
        to_core[0].start()
        wait_of["y", 1].wait_recv()
        on_y1.start()
        to_core[1].start()

    def before_eight():
        wait_of["x", 1].wait_recv()
        to_core[2].start()
        wait_of["y", 0].wait_recv()
        to_core[3].start()

    def before_eleven():
        swap[1].start()
        wait_of["yc", 0].wait_recv()

    def before_twelve():
        swap[2].start()
        wait_of["d", 0].wait_recv()
        to_core[4].start()
        wait_of["d", 1].wait_recv()
        to_core[5].start()

    def before_fourteen():
        add_core(1, at_x)
        near[2].start()
        add_core(2, at_y)
        near[3].start()
        wait_of["dc", 0].wait_recv()

    ahead = {
        2: wait_of["mc", 0].wait_recv,
        3: wait_of["mc", 1].wait_recv,
        4: before_four,
        6: wait_of["xc", 0].wait_recv,
        7: wait_of["yc", 1].wait_recv,
        8: before_eight,
        10: wait_of["xc", 1].wait_recv,
        11: before_eleven,
        12: before_twelve,
        14: before_fourteen,
        15: wait_of["dc", 1].wait_recv,
    }

    def one_chunk(turn, _):
        for value, action in ahead.items():

            @pl.when(turn == value)
            def _():
                action()

        owner, which = order[15]
        for index in range(15):
            owner = jnp.where(turn == index, order[index][0], owner)
            which = jnp.where(turn == index, order[index][1], which)
        up_rows = up[...].reshape(4 * ff_own, D)
        down_rows = down[...].reshape(4 * ff_own, D)
        rows = span(which, 128)
        pre = dot_nt(mid_all[owner, rows, :], up_rows)
        square = pre * pre
        bend = jnp.tanh(GELU_SCALE * (pre + 0.044715 * (pre * square)))
        gl_all[owner, rows, :] = to_low(0.5 * pre * (1.0 + bend))
        slope = 0.5 * (1.0 + bend) + 0.5 * pre * (1.0 - bend * bend) * (
            GELU_SCALE * (1.0 + 3.0 * 0.044715 * square)
        )
        grad = to_low(dot_nt(cot_all[owner, rows, :], down_rows) * slope)
        dpre_all[owner, rows, :] = grad
        work[owner, rows, :] = to_low(dot_nn(grad, up_rows))
        return 0

    lax.fori_loop(0, 16, one_chunk, 0)
    swap[0].start()
    add_core(0, at_d)
    near[0].start()
    near[1].start()
    add_core(3, me)

    def grads(index, _):
        quarter, kind = index // 2, lax.rem(index, 2)
        columns = span(quarter, 128)

        @pl.when(kind == 0)
        def _():
            def add(owner, acc):
                return acc + dot_tn(dpre_all[owner, :, columns], mid_all[owner])

            ff_grads[quarter, 0] = to_low(lax.fori_loop(0, 8, add, jnp.zeros((128, D), wide)))

        @pl.when(kind == 1)
        def _():
            def add(owner, acc):
                return acc + dot_tn(gl_all[owner, :, columns], cot_all[owner])

            ff_grads[quarter, 1] = to_low(lax.fori_loop(0, 8, add, jnp.zeros((128, D), wide)))

        return 0

    lax.fori_loop(0, NEAR_GRADS, grads, 0)
    near[0].wait_recv()
    add_into(at_y, views[0], near_got[0])
    far[0].start()
    near[1].wait_recv()
    add_into(at_x, views[1], near_got[1])
    far[1].start()
    near[2].wait_recv()
    add_into(me, views[0], near_got[2])
    near[3].wait_recv()
    add_into(me, views[1], near_got[3])

    def outward(owner, _):
        down_rows = down[...].reshape(4 * ff_own, D)
        for which in range(2):
            rows = pl.ds(128 * which, 128)
            extra[owner, rows, :] = to_low(dot_nn(gl_all[owner, rows, :], down_rows))
        return 0

    lax.fori_loop(0, 8, outward, 0)
    lax.fori_loop(NEAR_GRADS, FAR_GRADS, grads, 0)
    for slot, view in enumerate(views):
        far[slot].wait_recv()
        total[view, :] = work[me, view, :].astype(wide) + far_got[slot].astype(wide)
    sums[...] = jnp.zeros_like(sums)

    def back(which, _):
        rows = span(which, 128)
        grad = total[rows, :]
        centered, scale = norm_parts(hidden[which])
        normed = centered * scale
        sums[0:1, :] += jnp.sum(grad * normed, axis=0, keepdims=True)
        lifted = grad * gain
        row_grad = cot_all[me, rows, :].astype(wide) + scale * (
            lifted
            - jnp.mean(lifted, axis=-1, keepdims=True)
            - normed * jnp.mean(lifted * normed, axis=-1, keepdims=True)
        )
        d_hidden[which] = row_grad
        d_low[which] = to_low(row_grad)
        d_rows[which] = to_low(dot_nt(to_low(row_grad), w_out[...].reshape(D, D)))
        return 0

    lax.fori_loop(0, 2, back, 0)

    def line_copy(slot, sender, seq_from, rank_from, seq_to, rank_to):
        return pltpu.make_async_remote_copy(
            src_ref=d_rows.at[seq_to // 2, :, span(2 * rank_to + lax.rem(seq_to, 2), 128)],
            dst_ref=d_line.at[seq_from, span(rank_from, 128), :],
            send_sem=back_send.at[slot],
            recv_sem=back_recv.at[sender],
            device_id={"seq": seq_to, "tensor": rank_to},
            device_id_type=MESH_ID,
        )

    for slot, (_, seq_to, rank_to) in enumerate(peers):
        line_copy(slot, here, place, rank, seq_to, rank_to).start()
    d_line[place, span(rank, 128), :] = d_rows[mine, :, span(head, 128)]
    lax.fori_loop(FAR_GRADS, 8, grads, 0)
    for index in range(LINE):
        columns = pl.ds(128 * index, 128)
        part = dot_tn(mixed_rows[0, :, columns], d_low[0]) + dot_tn(
            mixed_rows[1, :, columns], d_low[1]
        )
        part = to_low(part)
        for block in range(4):
            extra[
                4 * (index % 2) + block, 256 + 32 * (index // 2) : 288 + 32 * (index // 2), :
            ] = part[32 * block : 32 * block + 32, :]
    for slot, (other, seq_to, rank_to) in enumerate(peers):
        line_copy(slot, other, seq_to, rank_to, seq_to, rank_to).wait_recv()
    for slot, (_, seq_to, rank_to) in enumerate(peers):
        rows_copy(slot, here, place, rank, seq_to, rank_to).wait_send()
        line_copy(slot, here, place, rank, seq_to, rank_to).wait_send()
    for one in own + [on_x0, on_y1] + to_core + swap + near + far:
        one.wait_send()


GELU_SCALE = 0.7978845608028654
NEAR_GRADS = 3
FAR_GRADS = 4


def middle(mixed, tokens, kept, spread, cot_all, vecs):
    low, wide = jnp.bfloat16, jnp.float32
    ff_own = (spread.shape[1] - SPREAD_FIRST) // 2
    shapes = (
        ((2, 128, D), wide),
        ((2, 128, D), wide),
        ((4, BLOCK, 128), low),
        ((8, D), wide),
        ((8, 384, D), low),
        ((4, 2, ff_own, D), low),
    )
    dma = pltpu.SemaphoreType.DMA
    return pl.pallas_call(
        middle_kernel,
        out_shape=[jax.ShapeDtypeStruct(*one) for one in shapes],
        in_specs=vmem_specs(2) + any_specs(3) + vmem_specs(1),
        out_specs=vmem_specs(6),
        scratch_shapes=[
            pltpu.VMEM((2, 128, D), low),
            pltpu.VMEM((8, 256, D), low),
            pltpu.VMEM((8, 256, 4 * ff_own), low),
            pltpu.VMEM((8, 256, 4 * ff_own), low),
            pltpu.VMEM((8, 256, D), low),
            pltpu.VMEM((4, 256, D), low),
            pltpu.VMEM((4, 128, D), low),
            pltpu.VMEM((2, 128, D), low),
            pltpu.VMEM((256, D), wide),
            pltpu.VMEM((2, 128, D), low),
            pltpu.VMEM((2, 128, D), low),
            pltpu.VMEM((4, 8, 32, D), low),
            pltpu.VMEM((4, ff_own, D), low),
            pltpu.VMEM((4, ff_own, D), low),
            pltpu.VMEM((8, 256, D), low),
            dma((15,)), dma((16,)), dma((14,)), dma((8, 2)), dma((10,)), dma((10,)), dma((15,)),
            dma((16,)), dma((4,)),
        ],
        compiler_params=pltpu.CompilerParams(
            collective_id=3, has_side_effects=True, vmem_limit_bytes=VMEM_LIMIT
        ),
        cost_estimate=pl.CostEstimate(
            flops=60000000000, bytes_accessed=60000000, transcendentals=0
        ),
        name="middle",
    )(mixed, tokens, kept, spread, cot_all, vecs)


SPREAD_FIRST = 0


WIDE = 2048


def opening_kernel(
    tokens, w_query, w_key, w_value, w_sout, w_out, begin, vecs, marks_own,
    rows_all, qkv, kept, table, marks, w_qkv,
    begin_rows, bias_rows, stage, send_sem, core_sem, recv_sem, piece_send, piece_recv, ring_send, ring_recv,
    mark_send, mark_recv, local_sem,
):
    side, place, half, rank = plane_place()
    mine = place // 2
    core = place + 1 - 2 * half
    other = lax.rem(place + 2, 4)
    me = plane_index(side, place)
    extra = 80
    fetch_columns((w_query, w_key, w_value), w_qkv, local_sem.at[0])
    loads = [
        pltpu.make_async_copy(
            w_sout.at[span(me, 32), :], kept.at[me, pl.ds(80 * rank, 32), :], local_sem.at[1]
        ),
        pltpu.make_async_copy(
            w_out.at[span(me, 32), :], kept.at[me, pl.ds(80 * rank + 48, 32), :], local_sem.at[3]
        ),
        pltpu.make_async_copy(begin.at[span(me, 16), :], begin_rows, local_sem.at[2]),
    ]
    for one in loads:
        one.start()
    barrier = pltpu.get_barrier_semaphore()
    greeted = [{"tensor": lax.rem(rank + step, 4)} for step in (1, 2, 3)]
    seats = [lax.rem(place + step, 4) for step in (1, 2, 3)]
    greeted += [{"seq": one} for one in seats] + [{"dp": 1 - side}]
    for target in greeted:
        pl.semaphore_signal(barrier, inc=1, device_id=target, device_id_type=MESH_ID)
    gain = vecs[3:4, :]

    def normed(which):
        centered, scale = norm_parts(tokens[which].astype(jnp.float32))
        return to_low(centered * scale * gain)

    def moved(block_id, origin, sem, target):
        view = rows_all.at[block_id, span(origin, 128), :]
        return pltpu.make_async_remote_copy(
            src_ref=view,
            dst_ref=view,
            send_sem=sem,
            recv_sem=recv_sem.at[block_id, origin],
            device_id=target,
            device_id_type=MESH_ID,
        )

    stage[...] = normed(1 - mine)
    marks[place] = marks_own[...]
    pl.semaphore_wait(barrier, 7)
    aside = pltpu.make_async_remote_copy(
        src_ref=stage,
        dst_ref=rows_all.at[place, span(rank, 128), :],
        send_sem=send_sem.at[0, 0, 3],
        recv_sem=recv_sem.at[place, rank],
        device_id={"seq": other},
        device_id_type=MESH_ID,
    )
    aside.start()

    def mark_move(slot, origin, target):
        return pltpu.make_async_remote_copy(
            src_ref=marks.at[origin],
            dst_ref=marks.at[origin],
            send_sem=mark_send.at[slot],
            recv_sem=mark_recv.at[origin],
            device_id={"seq": target},
            device_id_type=MESH_ID,
        )

    def piece_move(slot, origin, target):
        view = kept.at[me, span(origin, extra), :]
        return pltpu.make_async_remote_copy(
            src_ref=view,
            dst_ref=view,
            send_sem=piece_send.at[slot],
            recv_sem=piece_recv.at[origin],
            device_id=target,
            device_id_type=MESH_ID,
        )

    for one in loads:
        one.wait()
    kept[me, pl.ds(pl.multiple_of(80 * rank + 32, 16), 16), :] = to_low(begin_rows[...])
    for slot in range(3):
        piece_move(slot, rank, greeted[slot]).start()
    for slot, target in enumerate(seats):
        mark_move(slot, place, target).start()
    rows_all[place, span(rank, 128), :] = normed(mine)
    right, left = {"tensor": lax.rem(rank + 1, 4)}, {"tensor": lax.rem(rank + 3, 4)}
    blocks = (place, other)

    def pass_on(which, distance):
        block_id = blocks[which]

        @pl.when((rank < 3) & (rank >= distance))
        def _():
            moved(block_id, jnp.maximum(rank - distance, 0), send_sem.at[which, distance, 0], right).start()

        @pl.when((rank > 0) & (rank + distance <= 3))
        def _():
            moved(block_id, jnp.minimum(rank + distance, 3), send_sem.at[which, distance, 1], left).start()

    def pass_done(which, distance):
        block_id = blocks[which]

        @pl.when((rank < 3) & (rank >= distance))
        def _():
            moved(block_id, jnp.maximum(rank - distance, 0), send_sem.at[which, distance, 0], right).wait_send()

        @pl.when((rank > 0) & (rank + distance <= 3))
        def _():
            moved(block_id, jnp.minimum(rank + distance, 3), send_sem.at[which, distance, 1], left).wait_send()

    def project(block_id, origin):
        view = span(origin, 128)
        qkv[block_id, view, :] = to_low(dot_nn(rows_all[block_id, view, :], w_qkv[...]))

    def rows_steps():
        pass_on(0, 0)
        fetched(w_qkv, local_sem.at[0])
        moved(place, rank, core_sem.at[0, rank], {"seq": core}).start()
        project(place, rank)
        moved(other, rank, send_sem.at[0, 0, 3], {"seq": other}).wait_recv()
        pass_on(1, 0)
        moved(other, rank, core_sem.at[1, rank], {"seq": core}).start()
        project(other, rank)
        yield
        for distance in (1, 2, 3):
            for which in (0, 1):
                block_id = blocks[which]
                for way, ok, origin in (
                    (0, rank >= distance, jnp.maximum(rank - distance, 0)),
                    (1, rank + distance <= 3, jnp.minimum(rank + distance, 3)),
                ):

                    @pl.when(ok)
                    def _():
                        moved(block_id, origin, send_sem.at[which, distance, way], right).wait_recv()
                        if distance < 3:
                            if way == 0:

                                @pl.when(rank < 3)
                                def _():
                                    moved(
                                        block_id, origin, send_sem.at[which, distance, 0], right
                                    ).start()

                            else:

                                @pl.when(rank > 0)
                                def _():
                                    moved(
                                        block_id, origin, send_sem.at[which, distance, 1], left
                                    ).start()

                        moved(block_id, origin, core_sem.at[which, origin], {"seq": core}).start()
                        project(block_id, origin)

                yield
        for which, block_id in enumerate((core, lax.rem(core + 2, 4))):
            for origin in range(4):
                moved(block_id, origin, core_sem.at[which, origin], {"seq": core}).wait_recv()
                project(block_id, origin)
        for which in (0, 1):
            for distance in (0, 1, 2):
                pass_done(which, distance)
            for origin in range(4):
                moved(blocks[which], origin, core_sem.at[which, origin], {"seq": core}).wait_send()

    def piece_steps():
        for slot in range(3):
            piece_move(slot, lax.rem(rank + slot + 1, 4), greeted[slot]).wait_recv()
        for _ in plane_gather(row_halves(kept, 4 * extra), ring_send, ring_recv):
            yield
        for slot in range(3):
            piece_move(slot, rank, greeted[slot]).wait_send()

    def bias_steps():
        lane = lax.broadcasted_iota(jnp.int32, (8, WIDE), 1)
        bucket_ids = bucket_of(jnp.where(lane >= WIDE - BLOCK, lane - WIDE - BLOCK, lane - BLOCK))
        first = jnp.zeros((8, WIDE), jnp.float32)
        for bucket_id in range(BUCKETS):
            value = jnp.where(
                half == 0,
                vecs[4:5, bucket_id : bucket_id + 1],
                vecs[4:5, BUCKETS + bucket_id : BUCKETS + bucket_id + 1],
            )
            first = jnp.where(bucket_ids == bucket_id, value, first)
        row = lax.broadcasted_iota(jnp.int32, (8, WIDE), 0)
        for step in (1, 2, 4):
            first = jnp.where(row // step % 2 == 1, pltpu.roll(first, step, 1), first)
        bias_rows[...] = first
        yield

        def one(group, _):
            table[span(group, 8), :] = pltpu.roll(bias_rows[...], 8 * group, 1)[:, 0 : 2 * BLOCK]
            return 0

        for part in range(4):
            lax.fori_loop(16 * part, 16 * part + 16, one, 0)
            yield

    run_all(rows_steps(), piece_steps(), bias_steps())
    aside.wait_send()
    for slot, target in enumerate(seats):
        mark_move(slot, place, target).wait_send()
        mark_move(slot, target, target).wait_recv()


def opening(tokens, w_query, w_key, w_value, w_sout, w_out, begin, vecs, marks):
    low, wide = jnp.bfloat16, jnp.float32
    shapes = (
        ((4, BLOCK, D), low),
        ((4, BLOCK, 384), low),
        ((8, 4 * 80, D), low),
        ((BLOCK, 2 * BLOCK), wide),
        ((4, 8, 128), jnp.int32),
        ((D, 384), low),
    )
    dma = pltpu.SemaphoreType.DMA
    outs = pl.pallas_call(
        opening_kernel,
        out_shape=[jax.ShapeDtypeStruct(*one) for one in shapes],
        in_specs=vmem_specs(1)
        + any_specs(6)
        + vmem_specs(2),
        out_specs=vmem_specs(6),
        scratch_shapes=[
            pltpu.VMEM((16, D), wide),
            pltpu.VMEM((8, WIDE), wide),
            pltpu.VMEM((128, D), low),
            dma((2, 4, 4)),
            dma((2, 4)),
            dma((4, 4)),
            dma((3,)),
            dma((4,)),
            dma((14,)),
            dma((8, 2)),
            dma((3,)),
            dma((4,)),
            dma((4,)),
        ],
        compiler_params=pltpu.CompilerParams(
            collective_id=5, has_side_effects=True, vmem_limit_bytes=VMEM_LIMIT
        ),
        cost_estimate=pl.CostEstimate(
            flops=30000000000, bytes_accessed=30000000, transcendentals=0
        ),
        name="opening",
    )(tokens, w_query, w_key, w_value, w_sout, w_out, begin, vecs, marks)
    rows_all, qkv, kept, table, marks, w_qkv = outs
    return rows_all, qkv, kept.reshape(8, 4, 80, D), table, marks, w_qkv


def pair_sum(part, near_got, far_got, result, rows, send_sem, recv_sem):
    side, place, half, rank = plane_place()
    mine = place // 2
    across, beside = 1 - side, 1 - mine
    me = 2 * side + mine
    at_x, at_y, at_d = 2 * across + mine, 2 * side + beside, 2 * across + beside
    to_x, to_y = {"dp": across}, {"seq": lax.rem(place + 2, 4)}
    size = rows // 2
    views = (pl.ds(0, size), pl.ds(size, size))

    def moved(source, target_ref, slot, target):
        return pltpu.make_async_remote_copy(
            src_ref=source,
            dst_ref=target_ref,
            send_sem=send_sem.at[slot],
            recv_sem=recv_sem.at[slot],
            device_id=target,
            device_id_type=MESH_ID,
        )

    def add_into(owner, view, other):
        part[owner, view, :] = to_low(
            part[owner, view, :].astype(jnp.float32) + other.astype(jnp.float32)
        )

    near = [
        moved(part.at[at_d, views[0], :], near_got.at[0], 0, to_x),
        moved(part.at[at_d, views[1], :], near_got.at[1], 1, to_y),
        moved(part.at[at_x, views[0], :], near_got.at[2], 2, to_x),
        moved(part.at[at_y, views[1], :], near_got.at[3], 3, to_y),
    ]
    for one in near:
        one.start()
    yield
    near[0].wait_recv()
    add_into(at_y, views[0], near_got[0])
    far = [
        moved(part.at[at_y, views[0], :], far_got.at[0], 4, to_y),
        moved(part.at[at_x, views[1], :], far_got.at[1], 5, to_x),
    ]
    far[0].start()
    near[1].wait_recv()
    add_into(at_x, views[1], near_got[1])
    far[1].start()
    yield
    near[2].wait_recv()
    add_into(me, views[0], near_got[2])
    near[3].wait_recv()
    add_into(me, views[1], near_got[3])
    for slot, view in enumerate(views):
        far[slot].wait_recv()
        result[me, view, :] = to_low(
            part[me, view, :].astype(jnp.float32) + far_got[slot].astype(jnp.float32)
        )

    def given(owner, which, slot, target):
        view = result.at[owner, views[which], :]
        return moved(view, view, slot, target)

    own = [
        given(me, 0, 6, to_x),
        given(me, 1, 7, to_y),
        given(me, 1, 8, to_x),
        given(me, 0, 9, to_y),
    ]
    for one in own:
        one.start()
    yield
    given(at_x, 0, 6, to_x).wait_recv()
    last = [given(at_x, 0, 10, to_y), given(at_y, 1, 11, to_x)]
    last[0].start()
    given(at_y, 1, 7, to_y).wait_recv()
    last[1].start()
    yield
    given(at_x, 1, 8, to_x).wait_recv()
    given(at_y, 0, 9, to_y).wait_recv()
    given(at_d, 0, 10, to_y).wait_recv()
    given(at_d, 1, 11, to_x).wait_recv()
    for one in near + far + own + last:
        one.wait_send()


PAIR_ROWS = 640


def closing_kernel(
    partial, pair_grads, tokens, d_hidden, vecs, d_start, mlp_sums, state_sums, out_part,
    sout_part,
    inputs_grad, pair_out, sout_out, small_out,
    sums, got, final, cross, cross_got,
    pair_part, pair_near, pair_far,
    z_part, z_got,
    small_z, small_p,
    line_send, line_recv, way_send, way_recv, pair_send, pair_recv, core_sem,
    zs_send, zs_recv, gather_send, gather_recv, small_send, small_recv, local_sem,
):
    loads = [
        pltpu.make_async_copy(source, target, local_sem.at[slot])
        for slot, (source, target) in enumerate(
            (
                (partial, sums),
            )
        )
    ]
    for one in loads:
        one.start()
    side, place, half, rank = plane_place()
    mine = place // 2
    core = place + 1 - 2 * half
    other = lax.rem(place + 2, 4)
    me = plane_index(side, place)
    ranks = [lax.rem(rank + step, 4) for step in (1, 2, 3)]
    spots_of = [lax.rem(me + step, 8) for step in range(1, 8)]
    barrier = pltpu.get_barrier_semaphore()
    for target in ranks:
        pl.semaphore_signal(barrier, inc=1, device_id={"tensor": target}, device_id_type=MESH_ID)
    for target in spots_of:
        pl.semaphore_signal(
            barrier,
            inc=1,
            device_id={"dp": target // 4, "seq": lax.rem(target, 4)},
            device_id_type=MESH_ID,
        )
    gain = vecs[3:4, :]
    right, left = {"tensor": lax.rem(rank + 1, 4)}, {"tensor": lax.rem(rank + 3, 4)}

    def moved(source, target_ref, send, recv, target):
        return pltpu.make_async_remote_copy(
            src_ref=source,
            dst_ref=target_ref,
            send_sem=send,
            recv_sem=recv,
            device_id=target,
            device_id_type=MESH_ID,
        )

    def crossing():
        return moved(cross, cross_got, line_send.at[0], line_recv.at[0], {"seq": other})

    near = rank // 2
    at_end = (rank == 0) | (rank == 3)

    def hop(way, which, target):
        return moved(
            sums.at[which, target],
            got.at[way, which, target],
            way_send.at[which, target],
            way_recv.at[way, which, target],
            {"tensor": lax.rem(rank + 5 - 2 * way, 4)},
        )

    def target_of(way, distance):
        return (1 - way) * (3 - distance) + way * distance

    def pass_first(which):
        @pl.when(at_end)
        def _():
            for distance in range(3):
                hop(near, which, target_of(near, distance)).start()

    def pass_on(way, which, distance):
        @pl.when(jnp.logical_not(at_end))
        def _():
            target = target_of(way, distance)
            hop(way, which, target).wait_recv()
            sums[which, target] = to_low(
                sums[which, target].astype(jnp.float32)
                + got[way, which, target].astype(jnp.float32)
            )
            hop(way, which, target).start()

    def finish(which):
        final[which] = sums[which, rank].astype(jnp.float32)

        @pl.when(rank > 0)
        def _():
            hop(0, which, rank).wait_recv()
            final[which] += got[0, which, rank].astype(jnp.float32)

        @pl.when(rank < 3)
        def _():
            hop(1, which, rank).wait_recv()
            final[which] += got[1, which, rank].astype(jnp.float32)

    def small_over_z(slot, sender, target):
        return moved(
            small_z.at[sender], small_z.at[sender], small_send.at[slot], small_recv.at[sender],
            {"tensor": target},
        )

    def small_over_plane(slot, sender, target):
        return moved(
            small_p.at[sender], small_p.at[sender], small_send.at[3 + slot],
            small_recv.at[4 + sender],
            {"dp": target // 4, "seq": lax.rem(target, 4)},
        )

    def line_steps():
        loads[0].wait()
        for which in (0, 1):
            pass_first(which)
        yield
        for which in (0, 1):
            pass_on(near, which, 0)
            yield
            pass_on(near, which, 1)
            pass_on(1 - near, which, 0)
            yield
            finish(which)
            if which == 0:
                cross[...] = to_low(final[0])
                crossing().start()
            yield
        crossing().wait_recv()
        final[0] = cross_got[...].astype(jnp.float32)
        small_z[rank] = jnp.zeros((8, D), jnp.float32)
        for row, source in enumerate(
            (state_sums[1:2, :], mlp_sums[0:1, :], state_sums[0:1, :], state_sums[2:3, :])
        ):
            small_z[rank, row + 1 : row + 2, :] = source
        for which, row_set in ((1, mine), (0, 1 - mine)):
            grad = final[which]
            centered, scale = norm_parts(tokens[row_set].astype(jnp.float32))
            normed = centered * scale
            small_z[rank, 0:1, :] += jnp.sum(grad * normed, axis=0, keepdims=True)
            lifted = grad * gain
            inputs_grad[row_set] = d_hidden[row_set] + scale * (
                lifted
                - jnp.mean(lifted, axis=-1, keepdims=True)
                - normed * jnp.mean(lifted * normed, axis=-1, keepdims=True)
            )
        for slot, target in enumerate(ranks):
            small_over_z(slot, rank, target).start()
        crossing().wait_send()
        yield
        for slot, target in enumerate(ranks):
            small_over_z(slot, target, target).wait_recv()
        small_p[me] = small_z[0] + small_z[1] + small_z[2] + small_z[3]
        for slot, target in enumerate(spots_of):
            small_over_plane(slot, me, target).start()
        yield
        for slot, target in enumerate(spots_of):
            small_over_plane(slot, target, target).wait_recv()
        acc = small_p[0]
        for target in range(1, 8):
            acc = acc + small_p[target]
        small_out[...] = acc
        for slot, target in enumerate(ranks):
            small_over_z(slot, rank, target).wait_send()
        for slot, target in enumerate(spots_of):
            small_over_plane(slot, me, target).wait_send()
        for which in (0, 1):
            for target in range(4):

                @pl.when(rank != target)
                def _():
                    hop(0, which, target).wait_send()

    def pair_steps():
        for owner in range(3):
            pair_part[owner] = pair_grads[160 * owner : 160 * owner + 160, :]
        pair_part[3, 0:32, :] = pair_grads[480:512, :]
        pair_part[3, 32:96, :] = to_low(d_start[...])
        pair_part[3, 96:160, :] = jnp.zeros((64, D), jnp.bfloat16)
        for _ in pair_sum(
            pair_part, pair_near, pair_far, pair_out.at[half], 160, pair_send, pair_recv
        ):
            yield
        full = moved(
            pair_out.at[half], pair_out.at[half], core_sem.at[0], core_sem.at[1], {"seq": core}
        )
        full.start()
        yield
        moved(
            pair_out.at[1 - half], pair_out.at[1 - half], core_sem.at[0], core_sem.at[1],
            {"seq": core},
        ).wait_recv()
        full.wait_send()

    def sout_steps():
        z_part[:, 0:32, :] = sout_part[...].reshape(4, 32, D)
        z_part[:, 32:64, :] = out_part[...].reshape(4, 32, D)
        out = [
            moved(
                z_part.at[target], z_got.at[rank], zs_send.at[slot], zs_recv.at[rank],
                {"tensor": target},
            )
            for slot, target in enumerate(ranks)
        ]
        for one in out:
            one.start()
        z_got[rank] = z_part[rank]
        yield
        for slot, target in enumerate(ranks):
            moved(
                z_part.at[target], z_got.at[target], zs_send.at[slot], zs_recv.at[target],
                {"tensor": target},
            ).wait_recv()
        acc = z_got[0].astype(jnp.float32)
        for target in range(1, 4):
            acc = acc + z_got[target].astype(jnp.float32)
        sout_out[me] = to_low(acc)
        for _ in plane_gather(row_halves(sout_out, 64), gather_send, gather_recv):
            yield
        for one in out:
            one.wait_send()

    pl.semaphore_wait(barrier, 10)
    run_all(sout_steps(), pair_steps(), line_steps())


def closing(
    partial, pair_grads, tokens, d_hidden, vecs, d_start, mlp_sums, state_sums, out_part, sout_part,
):
    low, wide = jnp.bfloat16, jnp.float32
    shapes = (
        ((2, 128, D), wide),
        ((2, 4, PAIR_ROWS // 4, D), low),
        ((8, 64, D), low),
        ((8, D), wide),
    )
    dma = pltpu.SemaphoreType.DMA
    return pl.pallas_call(
        closing_kernel,
        out_shape=[jax.ShapeDtypeStruct(*one) for one in shapes],
        in_specs=any_specs(1)
        + vmem_specs(9),
        out_specs=vmem_specs(4),
        scratch_shapes=[
            pltpu.VMEM((2, 4, 128, D), low),
            pltpu.VMEM((2, 2, 4, 128, D), low),
            pltpu.VMEM((2, 128, D), wide),
            pltpu.VMEM((128, D), low),
            pltpu.VMEM((128, D), low),
            pltpu.VMEM((4, PAIR_ROWS // 4, D), low),
            pltpu.VMEM((4, PAIR_ROWS // 8, D), low),
            pltpu.VMEM((2, PAIR_ROWS // 8, D), low),
            pltpu.VMEM((4, 64, D), low),
            pltpu.VMEM((4, 64, D), low),
            pltpu.VMEM((4, 8, D), wide),
            pltpu.VMEM((8, 8, D), wide),
            dma((1,)), dma((1,)), dma((2, 4)), dma((2, 2, 4)), dma((12,)), dma((12,)), dma((2,)),
            dma((3,)), dma((4,)), dma((16,)), dma((8, 2)), dma((10,)),
            dma((12,)), dma((1,)),
        ],
        compiler_params=pltpu.CompilerParams(
            collective_id=6, has_side_effects=True, vmem_limit_bytes=VMEM_LIMIT
        ),
        cost_estimate=pl.CostEstimate(
            flops=30000000000, bytes_accessed=30000000, transcendentals=0
        ),
        name="closing",
    )(
        partial, pair_grads, tokens, d_hidden, vecs, d_start, mlp_sums, state_sums, out_part,
        sout_part,
    )


def finish_kernel(
    pair, pair_tail, two, ff, small,
    query, key, value, squery, out, sout, up, down, state, gain_0, gain_1, gain_2, gain_3, biases,
):
    step = pl.program_id(0)
    wide = jnp.float32
    up[...] = ff[0, 0].astype(wide).T
    down[...] = ff[0, 1].astype(wide)
    sout[...] = two[0, 0:32].astype(wide)
    out[...] = two[0, 32:64].astype(wide)
    for which, target in enumerate((query, key, value, squery)):

        @pl.when(step // 2 == which)
        def _():
            target[...] = pair[0].astype(wide).T

    @pl.when(step == 0)
    def _():
        state[...] = pair_tail[...].reshape(128, D).astype(wide)
        for row, target in enumerate((gain_0, gain_1, gain_2, gain_3)):
            target[...] = small[row, :]
        rank = lax.axis_index("tensor")
        row = lax.broadcasted_iota(jnp.int32, (2, BUCKETS), 0)
        found = jnp.zeros((2, BUCKETS), wide)
        for head in range(LINE):
            part = small[4:5, BUCKETS * head : BUCKETS * head + BUCKETS]
            found = jnp.where(row + 2 * rank == head, part, found)
        biases[...] = found


def finish_grads(pair, two, ff, small):
    wide = jnp.float32
    turned = [
        pl.BlockSpec((D, 128), lambda i, w=which: (0, jnp.clip(i - 2 * w, 0, 1)))
        for which in range(4)
    ]
    square = jax.ShapeDtypeStruct((D, 256), wide)
    rows = jax.ShapeDtypeStruct((256, D), wide)
    whole = jax.ShapeDtypeStruct((D, D), wide)
    return pl.pallas_call(
        finish_kernel,
        grid=(8,),
        out_shape=[square] * 4 + [rows] * 2 + [whole] * 2
        + [jax.ShapeDtypeStruct((128, D), wide)]
        + [jax.ShapeDtypeStruct((D,), wide)] * 4
        + [jax.ShapeDtypeStruct((2, BUCKETS), wide)],
        in_specs=[
            pl.BlockSpec((1, 128, D), lambda i: (i % 2, i // 2, 0)),
            pl.BlockSpec((2, 64, D), lambda i: (0, 8, 0)),
            pl.BlockSpec((1, 64, D), lambda i: (i, 0, 0)),
            pl.BlockSpec((1, 2, 128, D), lambda i: (i, 0, 0, 0)),
            pl.BlockSpec((8, D), lambda i: (0, 0)),
        ],
        out_specs=turned
        + [pl.BlockSpec((32, D), lambda i: (i, 0))] * 2
        + [pl.BlockSpec((D, 128), lambda i: (0, i)), pl.BlockSpec((128, D), lambda i: (i, 0))]
        + [pl.BlockSpec((128, D), lambda i: (0, 0))]
        + [pl.BlockSpec((D,), lambda i: (0,))] * 4
        + [pl.BlockSpec((2, BUCKETS), lambda i: (0, 0))],
        compiler_params=pltpu.CompilerParams(vmem_limit_bytes=VMEM_LIMIT),
        name="finish_grads",
    )(pair, pair, two, ff, small)


def swap_seq(value):
    return lax.all_to_all(value, "seq", 0, 0, tiled=False)


def line_body(
    inputs,
    seg_starts,
    lengths,
    init_state,
    attn_gain,
    state_gain,
    mlp_gain,
    w_query,
    w_key,
    w_value,
    w_out,
    w_squery,
    w_sout,
    w_up,
    w_down,
    rel_bias,
    gate_bias,
    out_cot,
    state_cot,
):
    low, wide = jnp.bfloat16, jnp.float32
    place = lax.axis_index("seq")
    half = lax.rem(place, 2)
    mine = place // 2
    plane = ("dp", "seq")
    spot = 4 * lax.axis_index("dp") + place
    gate_value = jax.nn.sigmoid(gate_bias)
    vecs = jnp.stack(
        [
            state_gain,
            gate_value,
            mlp_gain,
            attn_gain,
            jnp.pad(jnp.concatenate([rel_bias[:, 0], rel_bias[:, 1]]), (0, D - 2 * BUCKETS)),
        ]
        + [jnp.zeros_like(gate_value)] * 3
    )
    marks = jnp.concatenate([seg_starts[:, 0], lengths, jnp.zeros((4,), jnp.int32)])
    marks = jnp.broadcast_to(marks[:, None], (8, 128))
    cot_used = lax.all_gather(out_cot.reshape(256, D), plane, axis=0, tiled=True)
    rows_all, qkv, kept, bias, marks, w_qkv = opening(
        inputs, w_query, w_key, w_value, w_sout, w_out, init_state, vecs, marks
    )

    ff_own = w_up.shape[1] // 8
    piece_of = lambda weight: lax.dynamic_slice_in_dim(weight, spot * 32, 32, 1).T
    back_own = jnp.stack(
        [
            piece_of(w_squery),
            piece_of(w_key),
            piece_of(w_value),
        ]
    )
    pieces = jnp.concatenate(
        [
            lax.dynamic_slice_in_dim(w_up, spot * ff_own, ff_own, 1).T,
            lax.dynamic_slice_in_dim(w_down, spot * ff_own, ff_own, 0),
        ],
        axis=0,
    )
    qkv, pieces, cot_used, back_own = lax.optimization_barrier(
        (qkv, pieces, cot_used, back_own)
    )
    spread = lax.all_gather(pieces, "tensor", axis=0, tiled=True).reshape(4, 2 * ff_own, D)
    mixed, lse_tok, state_rows, state_low, qkvst, lse_st, os_rows, cots, back = forward_chain(
        marks, qkv, kept, w_squery, w_qkv, vecs, bias, state_cot.reshape(4, 64, D), back_own
    )
    hidden_in, grad_hidden, d_mixed, mlp_sums, extra, ff_grads = middle(
        mixed, inputs, kept, spread, cot_used.reshape(8, 256, D), vecs
    )
    d_mixed, ff_grads = lax.optimization_barrier((d_mixed, ff_grads))
    ff_sum = lax.psum_scatter(
        ff_grads.reshape(ff_grads.shape[2] * 8, D), "tensor", scatter_dimension=0, tiled=True
    )
    (
        _, d_start, sums, state_out, tokens_out, out_part, partial, pair_grads, sout_part,
    ) = backward_chain(
        marks, qkv, d_mixed, lse_tok, qkvst, lse_st, state_rows, init_state, cots,
        back, kept, vecs, bias, extra, hidden_in, rows_all, state_low, w_qkv,
        os_rows.reshape(256, D),
    )
    partial, ff_sum = lax.optimization_barrier((partial, ff_sum))
    ff_total = lax.all_gather(ff_sum, plane, axis=0, tiled=True).reshape(8, 2, ff_own, D)
    inputs_grad, pair, two_grads, small = closing(
        partial, pair_grads, inputs, grad_hidden, vecs, d_start, mlp_sums, sums, out_part,
        sout_part,
    )
    pair = pair.reshape(2, PAIR_ROWS, D)
    (
        query_grad, key_grad, value_grad, squery_grad, out_grad, sout_grad, up_grad, down_grad,
        state_grad, attn_gain_grad, state_gain_grad, mlp_gain_grad, gate_grad, bias_grad,
    ) = finish_grads(pair, two_grads, ff_total, small)
    return (
        tokens_out,
        state_out[:, None],
        inputs_grad,
        state_grad,
        attn_gain_grad,
        state_gain_grad,
        mlp_gain_grad,
        query_grad,
        key_grad,
        value_grad,
        out_grad,
        squery_grad,
        sout_grad,
        up_grad,
        down_grad,
        bias_grad.T,
        gate_grad,
    )


def solution(mesh):
    return jax.shard_map(
        chosen_body(mesh),
        mesh=mesh,
        in_specs=(
            P("dp", ("seq", "tensor"), None),
            P("dp", "seq"),
            P("dp"),
            P("tensor", None),
            P(),
            P(),
            P(),
            P(None, "tensor"),
            P(None, "tensor"),
            P(None, "tensor"),
            P("tensor", None),
            P(None, "tensor"),
            P("tensor", None),
            P(None, "tensor"),
            P("tensor", None),
            P(None, "tensor"),
            P(),
            P("dp", ("seq", "tensor"), None),
            P("dp", "seq", "tensor", None),
        ),
        out_specs=(
            P("dp", ("seq", "tensor"), None),
            P("dp", "seq", "tensor", None),
            P("dp", ("seq", "tensor"), None),
            P("tensor", None),
            P(),
            P(),
            P(),
            P(None, "tensor"),
            P(None, "tensor"),
            P(None, "tensor"),
            P("tensor", None),
            P(None, "tensor"),
            P("tensor", None),
            P(None, "tensor"),
            P("tensor", None),
            P(None, "tensor"),
            P(),
        ),
        check_vma=False,
    )
```
